32 devices in a mesh: clip: 8 (over z, x), frame: 2 (over y), head: 2 (over core).
Axes of the slice: x: 2, y: 2, z: 4, core: 2. Of those that a mesh axis runs over, the one named last changes fastest.
Arguments:
- clips_in: bfloat16 [40, 392, 768], P('clip', 'frame'), may hold values from -6 to 6
- cached_kv: bfloat16 [40, 392, 2, 768], P('clip', 'frame', None, 'head'), may hold values from -6 to 6
- old_memory: bfloat16 [40, 98, 2, 768], P('clip', 'frame', None, 'head'), may hold values from -6 to 6
- stride_group: int32 [40], P('clip'), may hold values from 0 to 2
- memory_place: int32 [40, 4], P('clip'), may hold values from 1 to 120
- norm_gain: float32 [2, 768], replicated, may hold values from 0.5 to 1.5
- norm_shift: float32 [2, 768], replicated, may hold values from -2 to 2
- qkv_weight: bfloat16 [768, 3, 768], P(('clip', 'frame'), None, 'head'), may hold values from -0.21875 to 0.21875
- qkv_shift: float32 [3, 768], P(None, 'head'), may hold values from -2 to 2
- pool_kernel: float32 [3, 27, 96], replicated, may hold values from -1.25 to 1.25
- pool_gain: float32 [3, 96], replicated, may hold values from 0.5 to 1.5
- pool_shift: float32 [3, 96], replicated, may hold values from -2 to 2
- squeeze_kernel: float32 [2, 4, 96], replicated, may hold values from -3 to 3
- time_table: float32 [233, 96], replicated, may hold values from -0.6 to 0.6
- space_tables: float32 [2, 13, 96], replicated, may hold values from -0.6 to 0.6
- proj_weight: bfloat16 [768, 768], P('head', ('clip', 'frame')), may hold values from -0.21875 to 0.21875
- out_shift: float32 [2, 768], replicated, may hold values from -2 to 2
- up_weight: bfloat16 [768, 3072], P(('clip', 'frame'), 'head'), may hold values from -0.21875 to 0.21875
- up_shift: float32 [3072], P('head'), may hold values from -2 to 2
- down_weight: bfloat16 [3072, 768], P('head', ('clip', 'frame')), may hold values from -0.109375 to 0.109375
- cotangent: bfloat16 [40, 392, 768], P('clip', 'frame'), may hold values from -6 to 6
Outputs:
- block_out: bfloat16 [40, 392, 768], P('clip', 'frame')
- grad_in: bfloat16 [40, 392, 768], P('clip', 'frame')
- grad_norm_gain: float32 [2, 768], replicated
- grad_norm_shift: float32 [2, 768], replicated
- grad_qkv_weight: float32 [768, 3, 768], P(('clip', 'frame'), None, 'head')
- grad_qkv_shift: float32 [3, 768], P(None, 'head')
- grad_pool_kernel: float32 [3, 27, 96], replicated
- grad_pool_gain: float32 [3, 96], replicated
- grad_pool_shift: float32 [3, 96], replicated
- grad_squeeze_kernel: float32 [2, 4, 96], replicated
- grad_time_table: float32 [233, 96], replicated
- grad_space_tables: float32 [2, 13, 96], replicated
- grad_proj_weight: float32 [768, 768], P('head', ('clip', 'frame'))
- grad_out_shift: float32 [2, 768], replicated
- grad_up_weight: float32 [768, 3072], P(('clip', 'frame'), 'head')
- grad_up_shift: float32 [3072], P('head')
- grad_down_weight: float32 [3072, 768], P('head', ('clip', 'frame'))
The draws below stay inside these ranges and needn't reach their ends.
Inputs may be any that keep to these rules, and one draw needn't show every extreme that they name: `stride_group`: the stride group g of each clip: its frames lie 2 ** (g + 1) raw frames apart. `memory_place`: for each clip, distances back in raw frames of its memory frames: first the 2 old_memory frames, then the 2 squeezed frames.
All inputs are finite; a program needn't handle non-finite values.
Results may differ from the reference program's by a relative error of at most 0.015.
Values may be sent and summed in bfloat16 or wider, within the bound.
A program may use at most 512 MiB of HBM per device.

```python
import jax
import jax.numpy as jnp
from jax import lax

D = 768
HEADS = 8
HD = 96
FF = 3072
FRAMES = 8
SIDE = 7
MEMF = 2
MAXBACK = 120
CLIPS = 40
SPOT = 49
TOK = 392
REL_T = 233


def set_ends(array, own_key, low, top_value):
    extent = array.shape
    index_at = [jax.random.randint(jax.random.fold_in(own_key, axis), (), 0, extent[axis]) for axis in range(len(extent))]
    array = array.at[tuple(index_at)].set(low)
    longest = extent.index(max(extent))
    index_at[longest] = (index_at[longest] + 1) % extent[longest]
    return array.at[tuple(index_at)].set(top_value)


def block_levels(rng, shape, cuts, low, top_value):
    level, own = 1.0, jax.random.fold_in(rng, 6)
    for position, blocks in cuts:
        heights = jnp.exp(jax.random.uniform(jax.random.fold_in(own, position), (blocks,), jnp.float32, low / len(cuts), top_value / len(cuts)))
        level = level * jnp.repeat(heights, shape[position] // blocks).reshape([-1 if axis == position else 1 for axis in range(len(shape))])
    return level


def gaussian(own_key, dims, scale, limit, shards=(), held_as=jnp.bfloat16):
    level = block_levels(own_key, dims, shards, -0.22, 0.18) if shards else 1.0
    values = jax.random.normal(own_key, dims, jnp.float32) * scale * level
    return jnp.minimum(jnp.maximum(values, -limit), limit).astype(held_as)


def setup_inputs(seed: int = 0) -> dict:
    seeds = jax.random.split(jax.random.key(seed), 22)
    return {
        "clips_in": gaussian(seeds[0], (CLIPS, TOK, D), 1.0, 6.0, ((0, 8), (1, 2))),
        "cached_kv": gaussian(seeds[1], (CLIPS, TOK, 2, HEADS * HD), 1.0, 6.0, ((0, 8), (1, 2), (3, 2))),
        "old_memory": gaussian(seeds[2], (CLIPS, MEMF * SPOT, 2, HEADS * HD), 1.0, 6.0, ((0, 8), (1, 2), (3, 2))),
        "stride_group": set_ends(jax.random.randint(seeds[3], (CLIPS,), 0, 3), jax.random.fold_in(seeds[3], 1), 0, 2).astype(jnp.int32),
        "memory_place": set_ends(jax.random.randint(seeds[4], (CLIPS, 2 * MEMF), 1, MAXBACK + 1), jax.random.fold_in(seeds[4], 1), 1, MAXBACK).astype(jnp.int32),
        "norm_gain": jnp.clip(1.0 + 0.1 * jax.random.normal(seeds[5], (2, D), jnp.float32), 0.5, 1.5),
        "norm_shift": gaussian(seeds[6], (2, D), 0.3, 2.0, (), jnp.float32),
        "qkv_weight": gaussian(seeds[7], (D, 3, HEADS * HD), D ** -0.5, 0.21875, ((0, 16), (2, 2))),
        "qkv_shift": gaussian(seeds[8], (3, HEADS * HD), 0.3, 2.0, ((1, 2),), jnp.float32),
        "pool_kernel": gaussian(seeds[9], (3, 27, HD), 27 ** -0.5, 1.25, (), jnp.float32),
        "pool_gain": jnp.clip(1.0 + 0.1 * jax.random.normal(seeds[10], (3, HD), jnp.float32), 0.5, 1.5),
        "pool_shift": gaussian(seeds[11], (3, HD), 0.3, 2.0, (), jnp.float32),
        "squeeze_kernel": gaussian(seeds[12], (2, FRAMES // MEMF, HD), (FRAMES // MEMF) ** -0.5, 3.0, (), jnp.float32),
        "time_table": gaussian(seeds[13], (REL_T, HD), 0.1, 0.6, (), jnp.float32),
        "space_tables": gaussian(seeds[14], (2, 2 * SIDE - 1, HD), 0.1, 0.6, (), jnp.float32),
        "proj_weight": gaussian(seeds[15], (HEADS * HD, D), (HEADS * HD) ** -0.5, 0.21875, ((0, 2), (1, 16))),
        "out_shift": gaussian(seeds[16], (2, D), 0.3, 2.0, (), jnp.float32),
        "up_weight": gaussian(seeds[17], (D, FF), D ** -0.5, 0.21875, ((0, 16), (1, 2))),
        "up_shift": gaussian(seeds[18], (FF,), 0.3, 2.0, ((0, 2),), jnp.float32),
        "down_weight": gaussian(seeds[19], (FF, D), FF ** -0.5, 0.109375, ((0, 2), (1, 16))),
        "cotangent": gaussian(seeds[20], (CLIPS, TOK, D), 1.0, 6.0, ((0, 8), (1, 2))),
    }


PRECISE_DOT = lax.Precision.HIGHEST

@jax.custom_vjp
def low(v):
    return lax.optimization_barrier(v.astype(jnp.bfloat16)).astype(jnp.float32)

@jax.custom_vjp
def low_back(v):
    return v

def low_keep(v):
    return (low(v), None)

def low_pass(kept, grad):
    return (grad,)

def back_keep(v):
    return (v, None)

def back_low(kept, grad):
    return (low(grad),)
low.defvjp(low_keep, low_pass)
low_back.defvjp(back_keep, back_low)

def layer_norm(values, gain_row, shift_row):
    average = lax.optimization_barrier(jnp.mean(values, axis=-1, keepdims=True))
    centred = values - average
    variance = lax.optimization_barrier(jnp.mean(centred * centred, axis=-1, keepdims=True))
    return centred * lax.rsqrt(variance + 1e-06) * gain_row + shift_row

def depth_pool(fields, kernel_rows, gain_rows, shift_rows):
    spaced = jnp.pad(fields, ((1, 1), (1, 1), (1, 1), (0, 0), (0, 0), (0, 0)))
    summed = jnp.zeros(fields.shape, jnp.float32)
    for shift_frame in range(3):
        for shift_height in range(3):
            for shift_width in range(3):
                window = spaced[shift_frame:shift_frame + FRAMES, shift_height:shift_height + SIDE, shift_width:shift_width + SIDE]
                summed = summed + window * kernel_rows[:, shift_frame * 9 + shift_height * 3 + shift_width][:, None, :]
    return layer_norm(summed, gain_rows[:, None, :], shift_rows[:, None, :])

def relative_bias(queries, time_rows, space_rows, time_hot):
    time_proj = jnp.einsum('thwnd,rd->thwnr', queries, time_rows, precision=PRECISE_DOT)
    time_part = jnp.einsum('thwnr,tkr->thwnk', time_proj, time_hot, precision=PRECISE_DOT)
    places = jnp.arange(SIDE, dtype=jnp.int32)
    offsets = places[:, None] - places[None, :] + SIDE - 1
    space_hot = (offsets[:, :, None] == jnp.arange(2 * SIDE - 1, dtype=jnp.int32)[None, None, :]).astype(jnp.float32)
    height_proj = jnp.einsum('thwnd,rd->thwnr', queries, space_rows[0], precision=PRECISE_DOT)
    height_part = jnp.einsum('thwnr,hkr->thwnk', height_proj, space_hot, precision=PRECISE_DOT)
    width_proj = jnp.einsum('thwnd,rd->thwnr', queries, space_rows[1], precision=PRECISE_DOT)
    width_part = jnp.einsum('thwnr,wkr->thwnk', width_proj, space_hot, precision=PRECISE_DOT)
    return time_part[..., :, None, None] + height_part[..., None, :, None] + width_part[..., None, None, :]

def time_table_hot(group_id, place_row):
    stride = jnp.left_shift(jnp.int32(2), group_id)
    offset = 8 * (FRAMES - 1)
    frame_ids = jnp.arange(FRAMES, dtype=jnp.int32)
    current = stride * (frame_ids[:, None] - frame_ids[None, :]) + offset
    newer = stride * frame_ids[:, None] + place_row[MEMF:][None, :] + offset
    older = stride * frame_ids[:, None] + place_row[:MEMF][None, :] + offset
    chosen = jnp.concatenate([current, newer, older], axis=1)
    return (chosen[:, :, None] == jnp.arange(REL_T, dtype=jnp.int32)[None, None, :]).astype(jnp.float32)

def clip_forward(params, clip_in, cached, older, group_id, place_row):
    norm_gain, norm_shift, qkv_weight, qkv_shift, pool_kernel, pool_gain, pool_shift, squeeze_kernel, time_table, space_tables, proj_weight, out_shift, up_weight, up_shift, down_weight = params
    normed = layer_norm(clip_in, norm_gain[0], norm_shift[0])
    joined = jnp.dot(low(normed), qkv_weight.reshape(D, 3 * HEADS * HD), precision=PRECISE_DOT) + qkv_shift.reshape(-1)
    joined = low(low_back(joined))
    fields = joined.reshape(FRAMES, SIDE, SIDE, 3, HEADS, HD)
    pooled = depth_pool(fields, pool_kernel, pool_gain, pool_shift)
    queries = low(pooled[:, :, :, 0])
    keys_now = low(pooled[:, :, :, 1])
    values_now = low(pooled[:, :, :, 2])
    stacked = cached.reshape(MEMF, FRAMES // MEMF, SIDE, SIDE, 2, HEADS, HD)
    squeezed = low(jnp.einsum('mjhwxnd,xjd->mhwxnd', stacked, squeeze_kernel, precision=PRECISE_DOT))
    old_frames = older.reshape(MEMF, SIDE, SIDE, 2, HEADS, HD)
    key_rows = jnp.concatenate([keys_now, squeezed[:, :, :, 0], old_frames[:, :, :, 0]], axis=0)
    value_rows = jnp.concatenate([values_now, squeezed[:, :, :, 1], old_frames[:, :, :, 1]], axis=0)
    key_count = (FRAMES + 2 * MEMF) * SPOT
    key_rows = key_rows.reshape(key_count, HEADS, HD)
    value_rows = value_rows.reshape(key_count, HEADS, HD)
    time_hot = time_table_hot(group_id, place_row)
    position_bias = relative_bias(queries, time_table, space_tables, time_hot).reshape(TOK, HEADS, key_count)
    query_rows = queries.reshape(TOK, HEADS, HD)
    scores = jnp.einsum('qnd,knd->qnk', query_rows, key_rows, precision=PRECISE_DOT) * HD ** (-0.5) + position_bias
    scores = low_back(scores)
    attention = low(jax.nn.softmax(scores, axis=-1))
    mixture = jnp.einsum('qnk,knd->qnd', attention, value_rows, precision=PRECISE_DOT) + query_rows
    attended = low(low_back(mixture.reshape(TOK, HEADS * HD)))
    branch = low_back(jnp.dot(attended, proj_weight, precision=PRECISE_DOT)) + out_shift[0]
    middle = clip_in + branch
    normed_two = layer_norm(middle, norm_gain[1], norm_shift[1])
    hidden = low_back(jnp.dot(low(normed_two), up_weight, precision=PRECISE_DOT) + up_shift)
    activated = low(jax.nn.gelu(hidden, approximate=False))
    return middle + jnp.dot(activated, down_weight, precision=PRECISE_DOT) + out_shift[1]

def reference(clips_in, cached_kv, old_memory, stride_group, memory_place, norm_gain, norm_shift, qkv_weight, qkv_shift, pool_kernel, pool_gain, pool_shift, squeeze_kernel, time_table, space_tables, proj_weight, out_shift, up_weight, up_shift, down_weight, cotangent):
    params = (norm_gain, norm_shift, qkv_weight.astype(jnp.float32), qkv_shift, pool_kernel, pool_gain, pool_shift, squeeze_kernel, time_table, space_tables, proj_weight.astype(jnp.float32), out_shift, up_weight.astype(jnp.float32), up_shift, down_weight.astype(jnp.float32))

    def one_clip(totals, items):
        clip_in, cached, older, group_id, place_row, cotan = items

        def forward(params_now, input_now):
            return clip_forward(params_now, input_now, cached.astype(jnp.float32), older.astype(jnp.float32), group_id, place_row)
        result, pullback = jax.vjp(forward, params, clip_in.astype(jnp.float32))
        grad_params, grad_input = pullback(cotan.astype(jnp.float32))
        totals = jax.tree.map(jnp.add, totals, grad_params)
        return (totals, (result.astype(jnp.bfloat16), grad_input.astype(jnp.bfloat16)))
    zeros = jax.tree.map(jnp.zeros_like, params)
    totals, (outputs, grads) = lax.scan(one_clip, zeros, (clips_in, cached_kv, old_memory, stride_group, memory_place, cotangent))
    return (outputs, grads, totals[0], totals[1], totals[2], totals[3], totals[4], totals[5], totals[6], totals[7], totals[8], totals[9], totals[10], totals[11], totals[12], totals[13], totals[14])
```

```python
from functools import partial

import jax
import jax.numpy as jnp
import numpy as np
from jax import lax
from jax.experimental import pallas as pl
from jax.experimental.pallas import tpu as pltpu
from jax.sharding import PartitionSpec as P

FRAMES = 8
MEMF = 2
SIDE = 7
CELLS = SIDE * SIDE
LANES = 128
HALF = 208
QROWS = 2 * HALF
GRID_ROWS = FRAMES * SIDE * 8
MEM_AT = QROWS
MEM_PAD = 112
KROWS = 640
BIAS_COLS = 256
SPACE_AT = 128
PAD_LANE = 127
BF = jnp.bfloat16
F32 = jnp.float32
VMEM_LIMIT = 60 * 1024 * 1024


def dot_f32(a, b, dims):
    return lax.dot_general(a, b, (dims, ((), ())), preferred_element_type=F32)


def frame_order(first, own):
    rest = [t for t in range(FRAMES) if not first * own <= t < (first + 1) * own]
    return list(range(first * own, (first + 1) * own)) + rest


def placement(frame_count):
    own = FRAMES // frame_count
    into = np.zeros((frame_count, GRID_ROWS, QROWS), np.float32)
    for first in range(frame_count):
        for slot, frame in enumerate(frame_order(first, own)):
            base = (slot // own) * HALF + (slot % own) * CELLS
            for high in range(SIDE):
                for wide in range(SIDE):
                    row = (frame * SIDE + high) * 8 + wide
                    into[first, row, base + high * SIDE + wide] = 1.0
    return into, np.ascontiguousarray(into.transpose(0, 2, 1))


def bias_constants(frame_count):
    own = FRAMES // frame_count
    frames_all = FRAMES + 2 * MEMF
    keys = np.zeros((BIAS_COLS, KROWS), np.float32)
    valid = np.zeros((KROWS,), bool)

    def mark(col, slot, high, wide):
        valid[col] = True
        for query in range(FRAMES):
            keys[query * frames_all + slot, col] = 1.0
        for place in range(SIDE):
            keys[SPACE_AT + place * SIDE + high, col] = 1.0
            keys[SPACE_AT + CELLS + place * SIDE + wide, col] = 1.0

    mask = np.zeros((QROWS, BIAS_COLS), np.float32)
    for slot in range(FRAMES):
        base = (slot // own) * HALF + (slot % own) * CELLS
        for high in range(SIDE):
            for wide in range(SIDE):
                row = base + high * SIDE + wide
                mark(row, slot, high, wide)
                mask[row, slot * frames_all : (slot + 1) * frames_all] = 1.0
                mask[row, SPACE_AT + high * SIDE : SPACE_AT + (high + 1) * SIDE] = 1.0
                low = SPACE_AT + CELLS + wide * SIDE
                mask[row, low : low + SIDE] = 1.0
    for group in range(2):
        for inner in range(MEMF):
            slot = FRAMES + group * MEMF + inner
            for high in range(SIDE):
                for wide in range(SIDE):
                    col = MEM_AT + group * MEM_PAD + inner * CELLS + high * SIDE + wide
                    mark(col, slot, high, wide)
    keys[PAD_LANE, ~valid] = -1e9
    pad_row = np.zeros((1, BIAS_COLS), np.float32)
    pad_row[0, PAD_LANE] = 1.0
    return keys, mask, pad_row


def spread_heads(source, target, rows_at, units, unit, first=0):
    count = source.shape[1]
    for index in range(units):
        at = (first + index) * unit
        target[rows_at : rows_at + count, index * LANES : index * LANES + unit] = source[
            0, :, at : at + unit
        ]


def load_shifted(field, shifted):
    grid = field.reshape(FRAMES, SIDE, 8, field.shape[-1])
    flat = field.reshape(FRAMES * SIDE, 8, field.shape[-1])
    shifted[1, 1 : FRAMES + 1, 1 : SIDE + 1] = grid
    shifted[0, 1 : FRAMES + 1, 1 : SIDE + 1] = pltpu.roll(flat, 1, 1).reshape(grid.shape)
    shifted[2, 1 : FRAMES + 1, 1 : SIDE + 1] = pltpu.roll(flat, 7, 1).reshape(grid.shape)


def convolve(shifted, taps, target, flip):
    tiles = target.shape[-1] // LANES

    def step(index, carry):
        frame = index // tiles
        lanes = pl.ds(pl.multiple_of((index % tiles) * LANES, LANES), LANES)
        total = jnp.zeros((SIDE, 8, LANES), F32)
        for i in range(3):
            for k in range(3):
                rows = shifted[k, frame + i, :, :, lanes]
                for j in range(3):
                    if flip:
                        tap = (2 - i) * 9 + (2 - j) * 3 + (2 - k)
                    else:
                        tap = i * 9 + j * 3 + k
                    total = total + rows[j : j + SIDE] * taps[tap, :, lanes][None]
        target[frame, :, :, lanes] = total
        return carry

    lax.fori_loop(0, FRAMES * tiles, step, 0)


def tap_grads(shifted, grads, target):
    tiles = target.shape[-1] // LANES
    for i in range(3):

        def step(index, carry, i=i):
            lanes = pl.ds(pl.multiple_of(index * LANES, LANES), LANES)

            def inner(frame, sums):
                centre = grads[frame + 1, :, :, lanes]
                new = []
                for j in range(3):
                    for k in range(3):
                        rows = shifted[k, frame + i, j : j + SIDE, :, lanes]
                        new.append(sums[j * 3 + k] + jnp.sum(rows * centre[1 : SIDE + 1], axis=0))
                return tuple(new)

            start = tuple(jnp.zeros((8, LANES), F32) for _ in range(9))
            sums = lax.fori_loop(0, FRAMES, inner, start)
            for tap in range(9):
                target[i * 9 + tap, :, lanes] += sums[tap]
            return carry

        lax.fori_loop(0, tiles, step, 0)


def head_stats(values, unit):
    average = jnp.sum(values, axis=-1, keepdims=True) * (1.0 / unit)
    lane = lax.broadcasted_iota(jnp.int32, values.shape, 1)
    centred = jnp.where(lane < unit, values - average, 0.0)
    variance = jnp.sum(centred * centred, axis=-1, keepdims=True) * (1.0 / unit)
    return centred, lax.rsqrt(variance + 1e-06)


def forward_kernel(
    which, own_ref, peer_ref, mem_own_ref, mem_peer_ref, into_ref, outof_ref, taps_ref, gain_ref,
    shift_ref, bias_ref, keyhot_ref, mask_ref, pad_ref,
    out_own, out_peer, q_out, k_out, v_out, p_out, c_out,
    packed, shifted, taps, *, heads, unit, scale,
):
    units = 3 * heads
    own_rows = own_ref.shape[1]

    @pl.when(pl.program_id(0) == 0)
    def _():
        packed[...] = jnp.zeros_like(packed)
        shifted[...] = jnp.zeros_like(shifted)
        for tap in range(27):
            taps[tap] = jnp.broadcast_to(taps_ref[tap : tap + 1], taps.shape[1:])

    spread_heads(own_ref, packed, 0, units, unit)
    spread_heads(peer_ref, packed, HALF, units, unit)
    field = dot_f32(into_ref[0], packed[...], ((1,), (0,)))
    load_shifted(field, shifted)
    conv = c_out.at[0]
    convolve(shifted, taps, conv, False)
    k_out[0, MEM_AT:, :] = jnp.zeros((KROWS - MEM_AT, heads * LANES), BF)
    v_out[0, MEM_AT:, :] = jnp.zeros((KROWS - MEM_AT, heads * LANES), BF)
    spread_heads(mem_own_ref, k_out.at[0], MEM_AT, heads, unit, 0 * heads)
    spread_heads(mem_own_ref, v_out.at[0], MEM_AT, heads, unit, 1 * heads)
    spread_heads(mem_peer_ref, k_out.at[0], MEM_AT + MEM_PAD, heads, unit, 0 * heads)
    spread_heads(mem_peer_ref, v_out.at[0], MEM_AT + MEM_PAD, heads, unit, 1 * heads)
    for index in range(units):
        lanes = slice(index * LANES, (index + 1) * LANES)
        block = conv[:, :, :, lanes].reshape(GRID_ROWS, LANES)
        centred, rate = head_stats(block, unit)
        normal = centred * rate * gain_ref[:, lanes] + shift_ref[:, lanes]
        rows = dot_f32(outof_ref[0], normal.astype(BF), ((1,), (0,))).astype(BF)
        target = (q_out, k_out, v_out)[index // heads]
        local = slice((index % heads) * LANES, (index % heads + 1) * LANES)
        target[0, 0:QROWS, local] = rows

    bias = bias_ref[0]
    bias_high = bias.astype(BF)
    bias_low = (bias - bias_high.astype(F32)).astype(BF)
    for head in range(heads):
        lanes = slice(head * LANES, (head + 1) * LANES)
        keys = k_out[0, :, lanes]
        values = v_out[0, :, lanes]
        for half in range(2):
            rows = slice(half * HALF, (half + 1) * HALF)
            query = q_out[0, rows, lanes]
            table = dot_f32(query, bias_high, ((1,), (1,))) + dot_f32(query, bias_low, ((1,), (1,)))
            table = table * mask_ref[rows, :] + pad_ref[...]
            table_high = table.astype(BF)
            table_low = (table - table_high.astype(F32)).astype(BF)
            scores = dot_f32(query, keys, ((1,), (1,)))
            scores = scores + dot_f32(table_high, keyhot_ref[...], ((1,), (0,)))
            scores = scores + dot_f32(table_low, keyhot_ref[...], ((1,), (0,)))
            top = jnp.max(scores, axis=-1, keepdims=True)
            weights = jnp.exp((scores - top) * scale)
            total = jnp.sum(weights, axis=-1, keepdims=True)
            probs = (weights * (1.0 / total)).astype(BF)
            p_out[0, head, rows, :] = probs
            mixed = dot_f32(probs, values, ((1,), (0,))) + query.astype(F32)
            target = (out_own, out_peer)[half]
            target[0, :, head * unit : (head + 1) * unit] = mixed[:own_rows, :unit].astype(BF)


def backward_kernel(
    which, own_ref, peer_ref, grad_own_ref, grad_peer_ref, into_ref, outof_ref, taps_ref, gain_ref,
    bias_ref, keyhot_ref, mask_ref, q_ref, k_ref, v_ref, p_ref, c_ref,
    out_own, out_peer, mem_own, mem_peer, taps_out, gain_out, shift_out, bias_out,
    packed, shifted, taps, grads, spread, pooled, *, heads, unit, scale,
):
    units = 3 * heads
    own_rows = own_ref.shape[1]

    @pl.when(pl.program_id(0) == 0)
    def _():
        packed[...] = jnp.zeros_like(packed)
        shifted[...] = jnp.zeros_like(shifted)
        grads[...] = jnp.zeros_like(grads)
        spread[...] = jnp.zeros_like(spread)
        taps_out[...] = jnp.zeros_like(taps_out)
        gain_out[...] = jnp.zeros_like(gain_out)
        shift_out[...] = jnp.zeros_like(shift_out)
        for tap in range(27):
            taps[tap] = jnp.broadcast_to(taps_ref[tap : tap + 1], taps.shape[1:])

    spread_heads(own_ref, packed, 0, units, unit)
    spread_heads(peer_ref, packed, HALF, units, unit)
    load_shifted(dot_f32(into_ref[0], packed[...], ((1,), (0,))), shifted)
    spread_heads(grad_own_ref, spread, 0, heads, unit)
    spread_heads(grad_peer_ref, spread, HALF, heads, unit)
    bias_low = bias_ref[0].astype(BF)
    bias_sum = jnp.zeros((BIAS_COLS, LANES), F32)
    for head in range(heads):
        lanes = slice(head * LANES, (head + 1) * LANES)
        keys = k_ref[0, :, lanes]
        values = v_ref[0, :, lanes]
        keys_grad = jnp.zeros((KROWS, LANES), F32)
        values_grad = jnp.zeros((KROWS, LANES), F32)
        for half in range(2):
            rows = slice(half * HALF, (half + 1) * HALF)
            query = q_ref[0, rows, lanes]
            out_grad = spread[rows, lanes]
            probs = p_ref[0, head, rows, :]
            wide = probs.astype(F32)
            probs_grad = dot_f32(out_grad, values, ((1,), (1,)))
            weighted = wide * probs_grad
            shared = jnp.sum(weighted, axis=-1, keepdims=True)
            score_grad = (weighted - wide * shared).astype(BF)
            values_grad = values_grad + dot_f32(probs, out_grad, ((0,), (0,)))
            keys_grad = keys_grad + dot_f32(score_grad, query, ((0,), (0,)))
            table_grad = dot_f32(score_grad, keyhot_ref[...], ((1,), (1,))) * mask_ref[rows, :]
            table_low = table_grad.astype(BF)
            query_grad = dot_f32(score_grad, keys, ((1,), (0,)))
            query_grad = query_grad + dot_f32(table_low, bias_low, ((1,), (0,)))
            query_grad = query_grad * scale + out_grad.astype(F32)
            pooled[rows, lanes] = query_grad.astype(BF)
            bias_sum = bias_sum + dot_f32(table_low, query, ((0,), (0,)))
        keys_grad = (keys_grad * scale).astype(BF)
        values_grad = values_grad.astype(BF)
        for member, part in enumerate((keys_grad, values_grad)):
            at = ((member + 1) * heads + head) * LANES
            pooled[:, at : at + LANES] = part[:QROWS]
            at = (member * heads + head) * LANES
            mem_own[0, :, at : at + LANES] = part[MEM_AT : MEM_AT + MEM_PAD]
            mem_peer[0, :, at : at + LANES] = part[MEM_AT + MEM_PAD : MEM_AT + 2 * MEM_PAD]
    bias_out[0] = bias_sum

    for index in range(units):
        lanes = slice(index * LANES, (index + 1) * LANES)
        incoming = dot_f32(into_ref[0], pooled[:, lanes], ((1,), (0,)))
        block = c_ref[0, :, :, :, lanes].reshape(GRID_ROWS, LANES)
        centred, rate = head_stats(block, unit)
        normal = centred * rate
        product = incoming * normal
        gain_out[:, lanes] += jnp.sum(product, axis=0, keepdims=True)
        shift_out[:, lanes] += jnp.sum(incoming, axis=0, keepdims=True)
        inner = incoming * gain_ref[:, lanes]
        mean_inner = jnp.sum(inner, axis=-1, keepdims=True) * (1.0 / unit)
        mean_both = jnp.sum(inner * normal, axis=-1, keepdims=True) * (1.0 / unit)
        lane = lax.broadcasted_iota(jnp.int32, block.shape, 1)
        result = rate * (inner - mean_inner - normal * mean_both)
        result = jnp.where(lane < unit, result, 0.0)
        flat = result.reshape(FRAMES * SIDE, 8, LANES)
        shape = (FRAMES, SIDE, 8, LANES)
        grads[1, 1 : FRAMES + 1, 1 : SIDE + 1, :, lanes] = flat.reshape(shape)
        grads[0, 1 : FRAMES + 1, 1 : SIDE + 1, :, lanes] = pltpu.roll(flat, 1, 1).reshape(shape)
        grads[2, 1 : FRAMES + 1, 1 : SIDE + 1, :, lanes] = pltpu.roll(flat, 7, 1).reshape(shape)

    tap_grads(shifted, grads.at[1], taps_out)
    conv = shifted.at[1, 1 : FRAMES + 1, 1 : SIDE + 1]
    convolve(grads, taps, conv, True)
    for index in range(units):
        lanes = slice(index * LANES, (index + 1) * LANES)
        block = shifted[1, 1 : FRAMES + 1, 1 : SIDE + 1, :, lanes].reshape(GRID_ROWS, LANES)
        rows = dot_f32(outof_ref[0], block.astype(BF), ((1,), (0,))).astype(BF)
        local = slice(index * unit, (index + 1) * unit)
        out_own[0, :, local] = rows[:own_rows, :unit]
        out_peer[0, :, local] = rows[HALF : HALF + own_rows, :unit]


def whole_spec(shape):
    return pl.BlockSpec(shape, lambda clip, which: (0,) * len(shape))


def clip_spec(shape):
    return pl.BlockSpec((1,) + shape, lambda clip, which: (clip,) + (0,) * len(shape))


def frame_spec(shape):
    return pl.BlockSpec((1,) + shape, lambda clip, which: (which[0],) + (0,) * len(shape))


def attention_forward(
    which, own, peer, mem_own, mem_peer, consts, taps, gains, shifts, bias, scale, unit
):
    clips, rows, width = own.shape
    heads = width // (3 * unit)
    into, outof, keyhot, mask, pad_row = consts
    wide = 3 * heads * LANES
    mem_shape = mem_own.shape[1:]
    out = jax.ShapeDtypeStruct
    return pl.pallas_call(
        partial(forward_kernel, heads=heads, unit=unit, scale=scale),
        grid_spec=pltpu.PrefetchScalarGridSpec(
            num_scalar_prefetch=1,
            grid=(clips,),
            in_specs=[
                clip_spec((rows, width)),
                clip_spec((rows, width)),
                clip_spec(mem_shape),
                clip_spec(mem_shape),
                frame_spec((GRID_ROWS, QROWS)),
                frame_spec((QROWS, GRID_ROWS)),
                whole_spec((27, wide)),
                whole_spec((1, wide)),
                whole_spec((1, wide)),
                clip_spec((BIAS_COLS, LANES)),
                whole_spec((BIAS_COLS, KROWS)),
                whole_spec((QROWS, BIAS_COLS)),
                whole_spec((1, BIAS_COLS)),
            ],
            out_specs=[
                clip_spec((rows, heads * unit)),
                clip_spec((rows, heads * unit)),
                clip_spec((QROWS, heads * LANES)),
                clip_spec((KROWS, heads * LANES)),
                clip_spec((KROWS, heads * LANES)),
                clip_spec((heads, QROWS, KROWS)),
                clip_spec((FRAMES, SIDE, 8, wide)),
            ],
            scratch_shapes=[
                pltpu.VMEM((QROWS, wide), BF),
                pltpu.VMEM((3, FRAMES + 2, SIDE + 2, 8, wide), F32),
                pltpu.VMEM((27, 8, wide), F32),
            ],
        ),
        out_shape=[
            out((clips, rows, heads * unit), BF),
            out((clips, rows, heads * unit), BF),
            out((clips, QROWS, heads * LANES), BF),
            out((clips, KROWS, heads * LANES), BF),
            out((clips, KROWS, heads * LANES), BF),
            out((clips, heads, QROWS, KROWS), BF),
            out((clips, FRAMES, SIDE, 8, wide), F32),
        ],
        compiler_params=pltpu.CompilerParams(vmem_limit_bytes=VMEM_LIMIT),
        name="pooled_attention_forward",
    )(which, own, peer, mem_own, mem_peer, into, outof, taps, gains, shifts, bias, keyhot, mask, pad_row)


def attention_backward(
    which, own, peer, grad_own, grad_peer, consts, taps, gains, bias, saved, scale, unit
):
    clips, rows, width = own.shape
    heads = width // (3 * unit)
    into, outof, keyhot, mask, pad_row = consts
    wide = 3 * heads * LANES
    out = jax.ShapeDtypeStruct
    return pl.pallas_call(
        partial(backward_kernel, heads=heads, unit=unit, scale=scale),
        grid_spec=pltpu.PrefetchScalarGridSpec(
            num_scalar_prefetch=1,
            grid=(clips,),
            in_specs=[
                clip_spec((rows, width)),
                clip_spec((rows, width)),
                clip_spec((rows, heads * unit)),
                clip_spec((rows, heads * unit)),
                frame_spec((GRID_ROWS, QROWS)),
                frame_spec((QROWS, GRID_ROWS)),
                whole_spec((27, wide)),
                whole_spec((1, wide)),
                clip_spec((BIAS_COLS, LANES)),
                whole_spec((BIAS_COLS, KROWS)),
                whole_spec((QROWS, BIAS_COLS)),
                clip_spec((QROWS, heads * LANES)),
                clip_spec((KROWS, heads * LANES)),
                clip_spec((KROWS, heads * LANES)),
                clip_spec((heads, QROWS, KROWS)),
                clip_spec((FRAMES, SIDE, 8, wide)),
            ],
            out_specs=[
                clip_spec((rows, width)),
                clip_spec((rows, width)),
                clip_spec((MEM_PAD, 2 * heads * LANES)),
                clip_spec((MEM_PAD, 2 * heads * LANES)),
                whole_spec((27, 8, wide)),
                whole_spec((1, wide)),
                whole_spec((1, wide)),
                clip_spec((BIAS_COLS, LANES)),
            ],
            scratch_shapes=[
                pltpu.VMEM((QROWS, wide), BF),
                pltpu.VMEM((3, FRAMES + 2, SIDE + 2, 8, wide), F32),
                pltpu.VMEM((27, 8, wide), F32),
                pltpu.VMEM((3, FRAMES + 2, SIDE + 2, 8, wide), F32),
                pltpu.VMEM((QROWS, heads * LANES), BF),
                pltpu.VMEM((QROWS, wide), BF),
            ],
        ),
        out_shape=[
            out((clips, rows, width), BF),
            out((clips, rows, width), BF),
            out((clips, MEM_PAD, 2 * heads * LANES), BF),
            out((clips, MEM_PAD, 2 * heads * LANES), BF),
            out((27, 8, wide), F32),
            out((1, wide), F32),
            out((1, wide), F32),
            out((clips, BIAS_COLS, LANES), F32),
        ],
        compiler_params=pltpu.CompilerParams(vmem_limit_bytes=VMEM_LIMIT),
        name="pooled_attention_backward",
    )(which, own, peer, grad_own, grad_peer, into, outof, taps, gains, bias, keyhot, mask, *saved)


def layer_norm(values, gain_row, shift_row):
    average = jnp.mean(values, axis=-1, keepdims=True)
    centred = values - average
    variance = jnp.mean(centred * centred, axis=-1, keepdims=True)
    return centred * lax.rsqrt(variance + 1e-06) * gain_row + shift_row


def exact_gelu(values):
    return jax.nn.gelu(values, approximate=False)


def swap(value, axis):
    return lax.ppermute(value, axis, [(0, 1), (1, 0)])


def head_total(portion):
    low = portion.astype(BF)
    return low.astype(F32) + swap(low, "head").astype(F32)


def precise(pattern, *operands):
    return jnp.einsum(pattern, *operands, precision=lax.Precision.HIGHEST)


def split_groups(value, which, axis):
    half = value.shape[axis] // 2
    low = lax.slice_in_dim(value, 0, half, axis=axis)
    high = lax.slice_in_dim(value, half, None, axis=axis)
    first = which == 0
    return jnp.where(first, low, high), jnp.where(first, high, low)


def join_groups(own, peer, which, axis):
    first = which == 0
    return jnp.concatenate([jnp.where(first, own, peer), jnp.where(first, peer, own)], axis=axis)


def time_choices(stride_group, memory_place, which, own, table_rows):
    local = jnp.arange(own, dtype=jnp.int32)
    times = jnp.concatenate([which * own + local, (1 - which) * own + local])
    stride = jnp.left_shift(jnp.int32(2), stride_group)[:, None, None]
    offset = 8 * (FRAMES - 1)
    current = stride * (times[None, :, None] - times[None, None, :]) + offset
    first = memory_place[:, np.array([2, 0, 3, 1])]
    second = memory_place[:, np.array([3, 1, 2, 0])]
    places = jnp.where(which == 0, first, second)
    memory = stride * times[None, :, None] + places[:, None, :] + offset
    chosen = jnp.concatenate([current, memory], axis=2)
    return (chosen[..., None] == jnp.arange(table_rows, dtype=jnp.int32)).astype(F32)


def space_choices():
    places = np.arange(SIDE)
    offsets = places[:, None] - places[None, :] + SIDE - 1
    hot = offsets.reshape(-1)[:, None] == np.arange(2 * SIDE - 1)[None, :]
    return jnp.asarray(hot.astype(np.float32))


def wide_rows(rows, heads):
    count, members, unit = rows.shape
    padded = jnp.pad(rows, ((0, 0), (0, 0), (0, LANES - unit)))
    spread = jnp.broadcast_to(padded[:, :, None], (count, members, heads, LANES))
    return spread.reshape(count, members * heads * LANES)


def local(
    clips_in,
    cached_kv,
    old_memory,
    stride_group,
    memory_place,
    norm_gain,
    norm_shift,
    qkv_weight,
    qkv_shift,
    pool_kernel,
    pool_gain,
    pool_shift,
    squeeze_kernel,
    time_table,
    space_tables,
    proj_weight,
    out_shift,
    up_weight,
    up_shift,
    down_weight,
    cotangent,
):
    clip_count, rows_clip, model_width = clips_in.shape
    head_width = qkv_weight.shape[2]
    unit = pool_gain.shape[1]
    head_count = head_width // unit
    frame_count = lax.axis_size("frame")
    heads = head_count // frame_count
    own_frames = rows_clip // CELLS
    row_total = clip_count * rows_clip
    hidden_width = up_weight.shape[1]
    group_width = heads * unit
    group_span = FRAMES // MEMF
    scale = unit ** (-0.5)
    both = ("clip", "frame")
    which = lax.axis_index("frame")
    which_row = which.astype(jnp.int32).reshape(1)
    into_np, outof_np = placement(frame_count)
    keys_np, mask_np, pad_np = bias_constants(frame_count)
    consts = (
        jnp.asarray(into_np, BF),
        jnp.asarray(outof_np, BF),
        jnp.asarray(keys_np, BF),
        jnp.asarray(mask_np),
        jnp.asarray(pad_np),
    )

    attn_full = lax.all_gather(qkv_weight, both, axis=0, tiled=True)
    shards = jnp.concatenate([proj_weight.T, up_weight, down_weight.T], axis=1)
    rest_full = lax.all_gather(shards, both, axis=0, tiled=True)
    proj_full = rest_full[:, :head_width]
    up_full = rest_full[:, head_width : head_width + hidden_width]
    down_full = rest_full[:, head_width + hidden_width :]

    cached_wide = cached_kv.astype(F32).reshape(
        clip_count, group_span, CELLS, 2, head_count, unit
    )
    squeezed = precise("cjsxnd,xjd->csxnd", cached_wide, squeeze_kernel).astype(BF)
    memory_rows = jnp.concatenate(
        [squeezed.reshape(clip_count, CELLS, 2, head_width), old_memory], axis=1
    )
    mem_own, mem_send = split_groups(memory_rows, which, 3)
    mem_own = mem_own.reshape(clip_count, -1, 2 * group_width)
    mem_send = mem_send.reshape(clip_count, -1, 2 * group_width)
    mem_peer = swap(mem_send, "frame")

    time_hot = time_choices(stride_group, memory_place, which, own_frames, time_table.shape[0])
    time_rows = precise("ctkr,rd->ctkd", time_hot, time_table).reshape(clip_count, -1, unit)
    space_hot = space_choices()
    space_rows = precise("pr,xrd->xpd", space_hot, space_tables).reshape(2 * CELLS, unit)
    bias = jnp.zeros((clip_count, BIAS_COLS, LANES), F32)
    bias = bias.at[:, : time_rows.shape[1], :unit].set(time_rows)
    bias = bias.at[:, SPACE_AT : SPACE_AT + 2 * CELLS, :unit].set(space_rows[None])
    bias = bias * (1.0 / scale)
    taps = wide_rows(pool_kernel.transpose(1, 0, 2), heads)
    gains = wide_rows(pool_gain[None], heads)
    shifts = wide_rows(pool_shift[None], heads)

    inputs_wide = clips_in.reshape(row_total, model_width).astype(F32)
    normed_one, norm_one_back = jax.vjp(layer_norm, inputs_wide, norm_gain[0], norm_shift[0])
    rounded_one = normed_one.astype(BF)
    attn_own, attn_send = split_groups(attn_full, which, 2)
    shift_own, shift_send = split_groups(qkv_shift, which, 1)

    def project(weight, shift):
        flat = weight.reshape(model_width, 3 * group_width)
        result = jnp.dot(rounded_one, flat, preferred_element_type=F32) + shift.reshape(-1)
        return result.astype(BF).reshape(clip_count, rows_clip, 3 * group_width)

    joined_peer = swap(project(attn_send, shift_send), "frame")
    joined_own = project(attn_own, shift_own)
    forward = attention_forward(
        which_row, joined_own, joined_peer, mem_own, mem_peer, consts, taps, gains, shifts, bias,
        scale, unit,
    )
    attended_own, attended_send = forward[:2]
    saved = forward[2:]
    attended_peer = swap(attended_send, "frame")
    attended = join_groups(attended_own, attended_peer, which, 2).reshape(row_total, head_width)
    branch = head_total(dot_f32(attended, proj_full, ((1,), (1,)))) + out_shift[0]
    middle = inputs_wide + branch
    normed_two, norm_two_back = jax.vjp(layer_norm, middle, norm_gain[1], norm_shift[1])
    rounded_two = normed_two.astype(BF)
    hidden = jnp.dot(rounded_two, up_full, preferred_element_type=F32) + up_shift
    activated, gelu_back = jax.vjp(exact_gelu, hidden)
    activated_low = activated.astype(BF)
    block_out = (
        middle + head_total(dot_f32(activated_low, down_full, ((1,), (1,)))) + out_shift[1]
    )
    block_out = block_out.astype(BF).reshape(clip_count, rows_clip, model_width)

    cotan_low = cotangent.reshape(row_total, model_width)
    cotan_wide = cotan_low.astype(F32)
    active_grad = jnp.dot(cotan_low, down_full, preferred_element_type=F32)
    hidden_grad = gelu_back(active_grad)[0].astype(BF)
    grad_up_bias = jnp.sum(hidden_grad.astype(F32), axis=0)
    normed_two_grad = head_total(dot_f32(hidden_grad, up_full, ((1,), (1,))))
    middle_norm_grad, gain_two_grad, shift_two_grad = norm_two_back(normed_two_grad)
    middle_grad = cotan_wide + middle_norm_grad
    branch_grad = middle_grad.astype(BF)
    attended_grad = jnp.dot(branch_grad, proj_full, preferred_element_type=F32).astype(BF)
    attended_grad = attended_grad.reshape(clip_count, rows_clip, head_width)
    attended_grad_own, attended_grad_send = split_groups(attended_grad, which, 2)
    attended_grad_peer = swap(attended_grad_send, "frame")
    backward = attention_backward(
        which_row, joined_own, joined_peer, attended_grad_own, attended_grad_peer, consts, taps,
        gains, bias, saved, scale, unit,
    )
    grad_own, grad_send, mem_grad_own, mem_grad_send = backward[:4]
    taps_grad, pool_gain_grad, pool_shift_grad, bias_grad = backward[4:]
    grad_peer = swap(grad_send, "frame")
    mem_grad_peer = swap(mem_grad_send[:, :CELLS], "frame")

    grad_rest = jnp.concatenate(
        [
            dot_f32(branch_grad, attended, ((0,), (0,))).astype(BF),
            dot_f32(rounded_two, hidden_grad, ((0,), (0,))).astype(BF),
            dot_f32(cotan_low, activated_low, ((0,), (0,))).astype(BF),
        ],
        axis=1,
    )
    rest_shard = lax.psum_scatter(grad_rest, both, scatter_dimension=0, tiled=True).astype(F32)

    def lanes_back(rows, lead):
        return rows.reshape(lead + (-1, heads, LANES))[..., :unit]

    mem_grads = [
        part.reshape(clip_count, CELLS, 2, heads, LANES)[..., :unit]
        for part in (mem_grad_own[:, :CELLS], mem_grad_peer)
    ]
    squeezed_grads = join_groups(mem_grads[0], mem_grads[1], which, 3).astype(F32)
    grad_squeeze = precise("cjsxnd,csxnd->xjd", cached_wide, squeezed_grads)
    time_count = time_rows.shape[1]
    time_grad_rows = bias_grad[:, :time_count, :unit]
    grad_time = precise(
        "ckr,ckd->rd", time_hot.reshape(clip_count, time_count, -1), time_grad_rows
    )
    space_grad_rows = jnp.sum(bias_grad[:, SPACE_AT : SPACE_AT + 2 * CELLS, :unit], axis=0)
    grad_space = precise("pr,xpd->xrd", space_hot, space_grad_rows.reshape(2, CELLS, unit))
    grad_kernel = jnp.sum(lanes_back(jnp.sum(taps_grad, axis=1), (27,)), axis=2).transpose(1, 0, 2)
    grad_pool_gain = jnp.sum(lanes_back(pool_gain_grad, ()), axis=1)
    grad_pool_shift = jnp.sum(lanes_back(pool_shift_grad, ()), axis=1)

    parts = [
        part.reshape(row_total, 3, group_width)
        for part in (grad_own, grad_peer)
    ]
    joined_grad = join_groups(parts[0], parts[1], which, 2).reshape(row_total, 3 * head_width)
    grad_qkv_bias = jnp.sum(joined_grad.astype(F32), axis=0)
    grad_qkv = dot_f32(rounded_one, joined_grad, ((0,), (0,))).astype(BF)
    qkv_shard = lax.psum_scatter(grad_qkv, both, scatter_dimension=0, tiled=True).astype(F32)
    attn_flat = attn_full.reshape(model_width, 3 * head_width)
    normed_one_grad = head_total(dot_f32(joined_grad, attn_flat, ((1,), (1,))))
    input_norm_grad, gain_one_grad, shift_one_grad = norm_one_back(normed_one_grad)
    grad_in = (
        (middle_grad + input_norm_grad).astype(BF).reshape(clip_count, rows_clip, model_width)
    )

    head_index = lax.axis_index("head")
    head_axis = lax.axis_size("head")
    once = (head_index == 0).astype(F32)
    slot = (jnp.arange(head_axis) == head_index).astype(F32)[:, None]
    pieces = [
        jnp.stack([gain_one_grad, gain_two_grad]) * once,
        jnp.stack([shift_one_grad, shift_two_grad]) * once,
        jnp.stack([jnp.sum(middle_grad, axis=0), jnp.sum(cotan_wide, axis=0)]) * once,
        slot * grad_qkv_bias[None],
        slot * grad_up_bias[None],
        grad_kernel,
        grad_pool_gain,
        grad_pool_shift,
        grad_squeeze,
        grad_time,
        grad_space,
    ]
    flat = jnp.concatenate([piece.reshape(-1) for piece in pieces])
    flat = lax.psum(flat, ("clip", "frame", "head"))
    sums = []
    at = 0
    for piece in pieces:
        sums.append(flat[at : at + piece.size].reshape(piece.shape))
        at += piece.size
    gain_sums, shift_sums, out_sums, qkv_bias_sum, up_bias_sum = sums[:5]
    kernel_sum, pool_gain_sum, pool_shift_sum, squeeze_sum, time_sum, space_sum = sums[5:]
    qkv_bias_sum = lax.dynamic_index_in_dim(qkv_bias_sum, head_index, 0, keepdims=False)
    up_bias_sum = lax.dynamic_index_in_dim(up_bias_sum, head_index, 0, keepdims=False)
    return (
        block_out,
        grad_in,
        gain_sums,
        shift_sums,
        qkv_shard.reshape(-1, 3, head_width),
        qkv_bias_sum.reshape(3, head_width),
        kernel_sum,
        pool_gain_sum,
        pool_shift_sum,
        squeeze_sum,
        time_sum,
        space_sum,
        rest_shard[:, :head_width].T,
        out_sums,
        rest_shard[:, head_width : head_width + hidden_width],
        up_bias_sum,
        rest_shard[:, head_width + hidden_width :].T,
    )


def solution(mesh):
    return jax.shard_map(
        local,
        mesh=mesh,
        in_specs=(
            P("clip", "frame", None),
            P("clip", "frame", None, "head"),
            P("clip", "frame", None, "head"),
            P("clip"),
            P("clip", None),
            P(),
            P(),
            P(("clip", "frame"), None, "head"),
            P(None, "head"),
            P(),
            P(),
            P(),
            P(),
            P(),
            P(),
            P("head", ("clip", "frame")),
            P(),
            P(("clip", "frame"), "head"),
            P("head"),
            P("head", ("clip", "frame")),
            P("clip", "frame", None),
        ),
        out_specs=(
            P("clip", "frame", None),
            P("clip", "frame", None),
            P(),
            P(),
            P(("clip", "frame"), None, "head"),
            P(None, "head"),
            P(),
            P(),
            P(),
            P(),
            P(),
            P(),
            P("head", ("clip", "frame")),
            P(),
            P(("clip", "frame"), "head"),
            P("head"),
            P("head", ("clip", "frame")),
        ),
        check_vma=False,
    )
```

```python
from functools import partial

import jax
import jax.numpy as jnp
import numpy as np
from jax import lax
from jax.experimental import pallas as pl
from jax.experimental.pallas import tpu as pltpu
from jax.sharding import PartitionSpec as P

FRAMES = 8
MEMF = 2
SIDE = 7
CELLS = SIDE * SIDE
LANES = 128
HALF = 208
QROWS = 2 * HALF
GRID_ROWS = FRAMES * SIDE * 8
MEM_AT = QROWS
MEM_PAD = 112
KROWS = 640
BIAS_COLS = 256
SPACE_AT = 128
PAD_LANE = 127
BF = jnp.bfloat16
F32 = jnp.float32
VMEM_LIMIT = 60 * 1024 * 1024
MESH_ID = pl.DeviceIdType.MESH


def dot_f32(a, b, dims):
    return lax.dot_general(a, b, (dims, ((), ())), preferred_element_type=F32)


def frame_order(first, own):
    rest = [t for t in range(FRAMES) if not first * own <= t < (first + 1) * own]
    return list(range(first * own, (first + 1) * own)) + rest


def placement(frame_count):
    own = FRAMES // frame_count
    into = np.zeros((frame_count, GRID_ROWS, QROWS), np.float32)
    for first in range(frame_count):
        for slot, frame in enumerate(frame_order(first, own)):
            base = (slot // own) * HALF + (slot % own) * CELLS
            for high in range(SIDE):
                for wide in range(SIDE):
                    row = (frame * SIDE + high) * 8 + wide
                    into[first, row, base + high * SIDE + wide] = 1.0
    return into, np.ascontiguousarray(into.transpose(0, 2, 1))


def bias_constants(frame_count):
    own = FRAMES // frame_count
    frames_all = FRAMES + 2 * MEMF
    keys = np.zeros((BIAS_COLS, KROWS), np.float32)
    valid = np.zeros((KROWS,), bool)

    def mark(col, slot, high, wide):
        valid[col] = True
        for query in range(FRAMES):
            keys[query * frames_all + slot, col] = 1.0
        for place in range(SIDE):
            keys[SPACE_AT + place * SIDE + high, col] = 1.0
            keys[SPACE_AT + CELLS + place * SIDE + wide, col] = 1.0

    mask = np.zeros((QROWS, BIAS_COLS), np.float32)
    for slot in range(FRAMES):
        base = (slot // own) * HALF + (slot % own) * CELLS
        for high in range(SIDE):
            for wide in range(SIDE):
                row = base + high * SIDE + wide
                mark(row, slot, high, wide)
                mask[row, slot * frames_all : (slot + 1) * frames_all] = 1.0
                mask[row, SPACE_AT + high * SIDE : SPACE_AT + (high + 1) * SIDE] = 1.0
                low = SPACE_AT + CELLS + wide * SIDE
                mask[row, low : low + SIDE] = 1.0
    for group in range(2):
        for inner in range(MEMF):
            slot = FRAMES + group * MEMF + inner
            for high in range(SIDE):
                for wide in range(SIDE):
                    col = MEM_AT + group * MEM_PAD + inner * CELLS + high * SIDE + wide
                    mark(col, slot, high, wide)
    keys[PAD_LANE, ~valid] = -1e9
    pad_row = np.zeros((1, BIAS_COLS), np.float32)
    pad_row[0, PAD_LANE] = 1.0
    return keys, mask, pad_row


def spread_heads(source, target, rows_at, units, unit, first=0):
    count = source.shape[1]
    for index in range(units):
        at = (first + index) * unit
        target[rows_at : rows_at + count, index * LANES : index * LANES + unit] = source[
            0, :, at : at + unit
        ]


def load_shifted(field, shifted):
    grid = field.reshape(FRAMES, SIDE, 8, field.shape[-1])
    flat = field.reshape(FRAMES * SIDE, 8, field.shape[-1])
    shifted[1, 1 : FRAMES + 1, 1 : SIDE + 1] = grid
    shifted[0, 1 : FRAMES + 1, 1 : SIDE + 1] = pltpu.roll(flat, 1, 1).reshape(grid.shape)
    shifted[2, 1 : FRAMES + 1, 1 : SIDE + 1] = pltpu.roll(flat, 7, 1).reshape(grid.shape)


def convolve(shifted, taps, target, flip):
    tiles = target.shape[-1] // LANES

    def step(index, carry):
        frame = index // tiles
        lanes = pl.ds(pl.multiple_of((index % tiles) * LANES, LANES), LANES)
        total = jnp.zeros((SIDE, 8, LANES), F32)
        for i in range(3):
            for k in range(3):
                rows = shifted[k, frame + i, :, :, lanes]
                for j in range(3):
                    if flip:
                        tap = (2 - i) * 9 + (2 - j) * 3 + (2 - k)
                    else:
                        tap = i * 9 + j * 3 + k
                    total = total + rows[j : j + SIDE] * taps[tap, :, lanes][None]
        target[frame, :, :, lanes] = total
        return carry

    lax.fori_loop(0, FRAMES * tiles, step, 0)


def tap_grads(shifted, grads, target):
    tiles = target.shape[-1] // LANES
    for i in range(3):

        def step(index, carry, i=i):
            lanes = pl.ds(pl.multiple_of(index * LANES, LANES), LANES)

            def inner(frame, sums):
                centre = grads[frame + 1, :, :, lanes]
                new = []
                for j in range(3):
                    for k in range(3):
                        rows = shifted[k, frame + i, j : j + SIDE, :, lanes]
                        new.append(sums[j * 3 + k] + jnp.sum(rows * centre[1 : SIDE + 1], axis=0))
                return tuple(new)

            start = tuple(jnp.zeros((8, LANES), F32) for _ in range(9))
            sums = lax.fori_loop(0, FRAMES, inner, start)
            for tap in range(9):
                target[i * 9 + tap, :, lanes] += sums[tap]
            return carry

        lax.fori_loop(0, tiles, step, 0)


def head_stats(values, unit):
    average = jnp.sum(values, axis=-1, keepdims=True) * (1.0 / unit)
    lane = lax.broadcasted_iota(jnp.int32, values.shape, 1)
    centred = jnp.where(lane < unit, values - average, 0.0)
    variance = jnp.sum(centred * centred, axis=-1, keepdims=True) * (1.0 / unit)
    return centred, lax.rsqrt(variance + 1e-06)


def forward_kernel(
    which, own_ref, peer_ref, mem_own_ref, mem_peer_ref, into_ref, outof_ref, taps_ref, gain_ref,
    shift_ref, bias_ref, keyhot_ref, mask_ref, pad_ref,
    out_own, out_peer, q_out, k_out, v_out, p_out, c_out,
    packed, shifted, taps, *, heads, unit, scale,
):
    units = 3 * heads
    own_rows = own_ref.shape[1]

    @pl.when(pl.program_id(0) == 0)
    def _():
        packed[...] = jnp.zeros_like(packed)
        shifted[...] = jnp.zeros_like(shifted)
        for tap in range(27):
            taps[tap] = jnp.broadcast_to(taps_ref[tap : tap + 1], taps.shape[1:])

    spread_heads(own_ref, packed, 0, units, unit)
    spread_heads(peer_ref, packed, HALF, units, unit)
    field = dot_f32(into_ref[0], packed[...], ((1,), (0,)))
    load_shifted(field, shifted)
    conv = c_out.at[0]
    convolve(shifted, taps, conv, False)
    k_out[0, MEM_AT:, :] = jnp.zeros((KROWS - MEM_AT, heads * LANES), BF)
    v_out[0, MEM_AT:, :] = jnp.zeros((KROWS - MEM_AT, heads * LANES), BF)
    spread_heads(mem_own_ref, k_out.at[0], MEM_AT, heads, unit, 0 * heads)
    spread_heads(mem_own_ref, v_out.at[0], MEM_AT, heads, unit, 1 * heads)
    spread_heads(mem_peer_ref, k_out.at[0], MEM_AT + MEM_PAD, heads, unit, 0 * heads)
    spread_heads(mem_peer_ref, v_out.at[0], MEM_AT + MEM_PAD, heads, unit, 1 * heads)
    for index in range(units):
        lanes = slice(index * LANES, (index + 1) * LANES)
        block = conv[:, :, :, lanes].reshape(GRID_ROWS, LANES)
        centred, rate = head_stats(block, unit)
        normal = centred * rate * gain_ref[:, lanes] + shift_ref[:, lanes]
        rows = dot_f32(outof_ref[0], normal.astype(BF), ((1,), (0,))).astype(BF)
        target = (q_out, k_out, v_out)[index // heads]
        local = slice((index % heads) * LANES, (index % heads + 1) * LANES)
        target[0, 0:QROWS, local] = rows

    bias = bias_ref[0]
    bias_high = bias.astype(BF)
    bias_low = (bias - bias_high.astype(F32)).astype(BF)
    for head in range(heads):
        lanes = slice(head * LANES, (head + 1) * LANES)
        keys = k_out[0, :, lanes]
        values = v_out[0, :, lanes]
        for half in range(2):
            rows = slice(half * HALF, (half + 1) * HALF)
            query = q_out[0, rows, lanes]
            table = dot_f32(query, bias_high, ((1,), (1,))) + dot_f32(query, bias_low, ((1,), (1,)))
            table = table * mask_ref[rows, :] + pad_ref[...]
            table_high = table.astype(BF)
            table_low = (table - table_high.astype(F32)).astype(BF)
            scores = dot_f32(query, keys, ((1,), (1,)))
            scores = scores + dot_f32(table_high, keyhot_ref[...], ((1,), (0,)))
            scores = scores + dot_f32(table_low, keyhot_ref[...], ((1,), (0,)))
            top = jnp.max(scores, axis=-1, keepdims=True)
            weights = jnp.exp((scores - top) * scale)
            total = jnp.sum(weights, axis=-1, keepdims=True)
            probs = (weights * (1.0 / total)).astype(BF)
            p_out[0, head, rows, :] = probs
            mixed = dot_f32(probs, values, ((1,), (0,))) + query.astype(F32)
            target = (out_own, out_peer)[half]
            target[0, :, head * unit : (head + 1) * unit] = mixed[:own_rows, :unit].astype(BF)


def backward_kernel(
    which, own_ref, peer_ref, grad_own_ref, grad_peer_ref, into_ref, outof_ref, taps_ref, gain_ref,
    bias_ref, keyhot_ref, mask_ref, q_ref, k_ref, v_ref, p_ref, c_ref,
    out_own, out_peer, mem_own, mem_peer, taps_out, gain_out, shift_out, bias_out,
    packed, shifted, taps, grads, spread, pooled, *, heads, unit, scale,
):
    units = 3 * heads
    own_rows = own_ref.shape[1]

    @pl.when(pl.program_id(0) == 0)
    def _():
        packed[...] = jnp.zeros_like(packed)
        shifted[...] = jnp.zeros_like(shifted)
        grads[...] = jnp.zeros_like(grads)
        spread[...] = jnp.zeros_like(spread)
        taps_out[...] = jnp.zeros_like(taps_out)
        gain_out[...] = jnp.zeros_like(gain_out)
        shift_out[...] = jnp.zeros_like(shift_out)
        for tap in range(27):
            taps[tap] = jnp.broadcast_to(taps_ref[tap : tap + 1], taps.shape[1:])

    spread_heads(own_ref, packed, 0, units, unit)
    spread_heads(peer_ref, packed, HALF, units, unit)
    load_shifted(dot_f32(into_ref[0], packed[...], ((1,), (0,))), shifted)
    spread_heads(grad_own_ref, spread, 0, heads, unit)
    spread_heads(grad_peer_ref, spread, HALF, heads, unit)
    bias_low = bias_ref[0].astype(BF)
    bias_sum = jnp.zeros((BIAS_COLS, LANES), F32)
    for head in range(heads):
        lanes = slice(head * LANES, (head + 1) * LANES)
        keys = k_ref[0, :, lanes]
        values = v_ref[0, :, lanes]
        keys_grad = jnp.zeros((KROWS, LANES), F32)
        values_grad = jnp.zeros((KROWS, LANES), F32)
        for half in range(2):
            rows = slice(half * HALF, (half + 1) * HALF)
            query = q_ref[0, rows, lanes]
            out_grad = spread[rows, lanes]
            probs = p_ref[0, head, rows, :]
            wide = probs.astype(F32)
            probs_grad = dot_f32(out_grad, values, ((1,), (1,)))
            weighted = wide * probs_grad
            shared = jnp.sum(weighted, axis=-1, keepdims=True)
            score_grad = (weighted - wide * shared).astype(BF)
            values_grad = values_grad + dot_f32(probs, out_grad, ((0,), (0,)))
            keys_grad = keys_grad + dot_f32(score_grad, query, ((0,), (0,)))
            table_grad = dot_f32(score_grad, keyhot_ref[...], ((1,), (1,))) * mask_ref[rows, :]
            table_low = table_grad.astype(BF)
            query_grad = dot_f32(score_grad, keys, ((1,), (0,)))
            query_grad = query_grad + dot_f32(table_low, bias_low, ((1,), (0,)))
            query_grad = query_grad * scale + out_grad.astype(F32)
            pooled[rows, lanes] = query_grad.astype(BF)
            bias_sum = bias_sum + dot_f32(table_low, query, ((0,), (0,)))
        keys_grad = (keys_grad * scale).astype(BF)
        values_grad = values_grad.astype(BF)
        for member, part in enumerate((keys_grad, values_grad)):
            at = ((member + 1) * heads + head) * LANES
            pooled[:, at : at + LANES] = part[:QROWS]
            at = (member * heads + head) * LANES
            mem_own[0, :, at : at + LANES] = part[MEM_AT : MEM_AT + MEM_PAD]
            mem_peer[0, :, at : at + LANES] = part[MEM_AT + MEM_PAD : MEM_AT + 2 * MEM_PAD]
    bias_out[0] = bias_sum

    for index in range(units):
        lanes = slice(index * LANES, (index + 1) * LANES)
        incoming = dot_f32(into_ref[0], pooled[:, lanes], ((1,), (0,)))
        block = c_ref[0, :, :, :, lanes].reshape(GRID_ROWS, LANES)
        centred, rate = head_stats(block, unit)
        normal = centred * rate
        product = incoming * normal
        gain_out[:, lanes] += jnp.sum(product, axis=0, keepdims=True)
        shift_out[:, lanes] += jnp.sum(incoming, axis=0, keepdims=True)
        inner = incoming * gain_ref[:, lanes]
        mean_inner = jnp.sum(inner, axis=-1, keepdims=True) * (1.0 / unit)
        mean_both = jnp.sum(inner * normal, axis=-1, keepdims=True) * (1.0 / unit)
        lane = lax.broadcasted_iota(jnp.int32, block.shape, 1)
        result = rate * (inner - mean_inner - normal * mean_both)
        result = jnp.where(lane < unit, result, 0.0)
        flat = result.reshape(FRAMES * SIDE, 8, LANES)
        shape = (FRAMES, SIDE, 8, LANES)
        grads[1, 1 : FRAMES + 1, 1 : SIDE + 1, :, lanes] = flat.reshape(shape)
        grads[0, 1 : FRAMES + 1, 1 : SIDE + 1, :, lanes] = pltpu.roll(flat, 1, 1).reshape(shape)
        grads[2, 1 : FRAMES + 1, 1 : SIDE + 1, :, lanes] = pltpu.roll(flat, 7, 1).reshape(shape)

    tap_grads(shifted, grads.at[1], taps_out)
    conv = shifted.at[1, 1 : FRAMES + 1, 1 : SIDE + 1]
    convolve(grads, taps, conv, True)
    for index in range(units):
        lanes = slice(index * LANES, (index + 1) * LANES)
        block = shifted[1, 1 : FRAMES + 1, 1 : SIDE + 1, :, lanes].reshape(GRID_ROWS, LANES)
        rows = dot_f32(outof_ref[0], block.astype(BF), ((1,), (0,))).astype(BF)
        local = slice(index * unit, (index + 1) * unit)
        out_own[0, :, local] = rows[:own_rows, :unit]
        out_peer[0, :, local] = rows[HALF : HALF + own_rows, :unit]


def whole_spec(shape):
    return pl.BlockSpec(shape, lambda clip, which: (0,) * len(shape))


def clip_spec(shape):
    return pl.BlockSpec((1,) + shape, lambda clip, which: (clip,) + (0,) * len(shape))


def frame_spec(shape):
    return pl.BlockSpec((1,) + shape, lambda clip, which: (which[0],) + (0,) * len(shape))


def attention_forward(
    which, own, peer, mem_own, mem_peer, consts, taps, gains, shifts, bias, scale, unit
):
    clips, rows, width = own.shape
    heads = width // (3 * unit)
    into, outof, keyhot, mask, pad_row = consts
    wide = 3 * heads * LANES
    mem_shape = mem_own.shape[1:]
    out = jax.ShapeDtypeStruct
    return pl.pallas_call(
        partial(forward_kernel, heads=heads, unit=unit, scale=scale),
        grid_spec=pltpu.PrefetchScalarGridSpec(
            num_scalar_prefetch=1,
            grid=(clips,),
            in_specs=[
                clip_spec((rows, width)),
                clip_spec((rows, width)),
                clip_spec(mem_shape),
                clip_spec(mem_shape),
                frame_spec((GRID_ROWS, QROWS)),
                frame_spec((QROWS, GRID_ROWS)),
                whole_spec((27, wide)),
                whole_spec((1, wide)),
                whole_spec((1, wide)),
                clip_spec((BIAS_COLS, LANES)),
                whole_spec((BIAS_COLS, KROWS)),
                whole_spec((QROWS, BIAS_COLS)),
                whole_spec((1, BIAS_COLS)),
            ],
            out_specs=[
                clip_spec((rows, heads * unit)),
                clip_spec((rows, heads * unit)),
                clip_spec((QROWS, heads * LANES)),
                clip_spec((KROWS, heads * LANES)),
                clip_spec((KROWS, heads * LANES)),
                clip_spec((heads, QROWS, KROWS)),
                clip_spec((FRAMES, SIDE, 8, wide)),
            ],
            scratch_shapes=[
                pltpu.VMEM((QROWS, wide), BF),
                pltpu.VMEM((3, FRAMES + 2, SIDE + 2, 8, wide), F32),
                pltpu.VMEM((27, 8, wide), F32),
            ],
        ),
        out_shape=[
            out((clips, rows, heads * unit), BF),
            out((clips, rows, heads * unit), BF),
            out((clips, QROWS, heads * LANES), BF),
            out((clips, KROWS, heads * LANES), BF),
            out((clips, KROWS, heads * LANES), BF),
            out((clips, heads, QROWS, KROWS), BF),
            out((clips, FRAMES, SIDE, 8, wide), F32),
        ],
        compiler_params=pltpu.CompilerParams(vmem_limit_bytes=VMEM_LIMIT),
        name="pooled_attention_forward",
    )(which, own, peer, mem_own, mem_peer, into, outof, taps, gains, shifts, bias, keyhot, mask, pad_row)


def attention_backward(
    which, own, peer, grad_own, grad_peer, consts, taps, gains, bias, saved, scale, unit
):
    clips, rows, width = own.shape
    heads = width // (3 * unit)
    into, outof, keyhot, mask, pad_row = consts
    wide = 3 * heads * LANES
    out = jax.ShapeDtypeStruct
    return pl.pallas_call(
        partial(backward_kernel, heads=heads, unit=unit, scale=scale),
        grid_spec=pltpu.PrefetchScalarGridSpec(
            num_scalar_prefetch=1,
            grid=(clips,),
            in_specs=[
                clip_spec((rows, width)),
                clip_spec((rows, width)),
                clip_spec((rows, heads * unit)),
                clip_spec((rows, heads * unit)),
                frame_spec((GRID_ROWS, QROWS)),
                frame_spec((QROWS, GRID_ROWS)),
                whole_spec((27, wide)),
                whole_spec((1, wide)),
                clip_spec((BIAS_COLS, LANES)),
                whole_spec((BIAS_COLS, KROWS)),
                whole_spec((QROWS, BIAS_COLS)),
                clip_spec((QROWS, heads * LANES)),
                clip_spec((KROWS, heads * LANES)),
                clip_spec((KROWS, heads * LANES)),
                clip_spec((heads, QROWS, KROWS)),
                clip_spec((FRAMES, SIDE, 8, wide)),
            ],
            out_specs=[
                clip_spec((rows, width)),
                clip_spec((rows, width)),
                clip_spec((MEM_PAD, 2 * heads * LANES)),
                clip_spec((MEM_PAD, 2 * heads * LANES)),
                whole_spec((27, 8, wide)),
                whole_spec((1, wide)),
                whole_spec((1, wide)),
                clip_spec((BIAS_COLS, LANES)),
            ],
            scratch_shapes=[
                pltpu.VMEM((QROWS, wide), BF),
                pltpu.VMEM((3, FRAMES + 2, SIDE + 2, 8, wide), F32),
                pltpu.VMEM((27, 8, wide), F32),
                pltpu.VMEM((3, FRAMES + 2, SIDE + 2, 8, wide), F32),
                pltpu.VMEM((QROWS, heads * LANES), BF),
                pltpu.VMEM((QROWS, wide), BF),
            ],
        ),
        out_shape=[
            out((clips, rows, width), BF),
            out((clips, rows, width), BF),
            out((clips, MEM_PAD, 2 * heads * LANES), BF),
            out((clips, MEM_PAD, 2 * heads * LANES), BF),
            out((27, 8, wide), F32),
            out((1, wide), F32),
            out((1, wide), F32),
            out((clips, BIAS_COLS, LANES), F32),
        ],
        compiler_params=pltpu.CompilerParams(vmem_limit_bytes=VMEM_LIMIT),
        name="pooled_attention_backward",
    )(which, own, peer, grad_own, grad_peer, into, outof, taps, gains, bias, keyhot, mask, *saved)


def device_of(outer, inner, frame, head):
    return (outer * 2 + inner, frame, head)


def plane_peer(inner, frame, step):
    return (inner + step // 2) % 2, (frame + step % 2) % 2


def finish_kernel(
    grads, small, out, small_out, near, part, far, small_in,
    near_send, near_recv, far_send, far_recv, first_send, first_recv, second_send, second_recv,
):
    outers, shard_rows, width = part.shape[1], part.shape[2], grads.shape[3]
    chunks = part.shape[0]
    cols = width // chunks
    devices = small.shape[0]
    clip = lax.axis_index("clip")
    frame = lax.axis_index("frame")
    head = lax.axis_index("head")
    outer, inner = clip // 2, clip % 2
    place = inner * 2 + frame
    mine = (clip * 2 + frame) * 2 + head

    def device(index):
        return (index // 4, (index // 2) % 2, index % 2)

    barrier = pltpu.get_barrier_semaphore()

    def greet(step, carry):
        pl.semaphore_signal(
            barrier, inc=1, device_id=device((mine + step) % devices), device_id_type=MESH_ID
        )
        return carry

    lax.fori_loop(1, devices, greet, 0)
    pl.semaphore_wait(barrier, devices - 1)

    def first(step):
        other = (mine + step) % devices
        return pltpu.make_async_remote_copy(
            src_ref=small.at[other], dst_ref=small_in.at[step],
            send_sem=first_send.at[step], recv_sem=first_recv.at[step],
            device_id=device(other), device_id_type=MESH_ID,
        )

    def second(step):
        return pltpu.make_async_remote_copy(
            src_ref=small_out.at[mine], dst_ref=small_out.at[mine],
            send_sem=second_send.at[step], recv_sem=second_recv.at[step],
            device_id=device((mine + step) % devices), device_id_type=MESH_ID,
        )

    def second_in(step):
        other = (mine + devices - step) % devices
        return pltpu.make_async_remote_copy(
            src_ref=small_out.at[other], dst_ref=small_out.at[other],
            send_sem=second_send.at[step], recv_sem=second_recv.at[step],
            device_id=device((mine + step) % devices), device_id_type=MESH_ID,
        )

    def near_copy(chunk, step):
        there_inner, there_frame = plane_peer(inner, frame, step)
        return pltpu.make_async_remote_copy(
            src_ref=grads.at[:, there_inner * 2 + there_frame, :, pl.ds(chunk * cols, cols)],
            dst_ref=near.at[chunk, step - 1],
            send_sem=near_send.at[chunk, step - 1], recv_sem=near_recv.at[chunk, step - 1],
            device_id=device_of(outer, there_inner, there_frame, head), device_id_type=MESH_ID,
        )

    def far_copy(chunk, step):
        there = (outer + step) % outers
        return pltpu.make_async_remote_copy(
            src_ref=part.at[chunk, there], dst_ref=far.at[chunk, step],
            send_sem=far_send.at[chunk, step], recv_sem=far_recv.at[chunk, step],
            device_id=device_of(there, inner, frame, head), device_id_type=MESH_ID,
        )

    def each(low, high, act):
        def body(step, carry):
            act(step)
            return carry

        lax.fori_loop(low, high, body, 0)

    each(1, devices, lambda step: first(step).start())
    for chunk in range(chunks):
        for step in range(1, 4):
            near_copy(chunk, step).start()

    each(1, devices, lambda step: first(step).wait_recv())
    total = lax.fori_loop(
        1, devices, lambda step, total: total + small_in[step], small[mine]
    )
    small_out[mine] = total
    each(1, devices, lambda step: second(step).start())

    for chunk in range(chunks):
        lanes = slice(chunk * cols, (chunk + 1) * cols)
        for step in range(1, 4):
            near_copy(chunk, step).wait_recv()

        def gathered(index):
            value = grads[index, place, :, lanes].astype(F32)
            for step in range(3):
                value = value + near[chunk, step, index].astype(F32)
            return value

        def send(step):
            there = (outer + step) % outers
            part[chunk, there] = gathered(there).astype(BF)
            far_copy(chunk, step).start()

        each(1, outers, send)
        out[:, lanes] = gathered(outer)
    for chunk in range(chunks):
        lanes = slice(chunk * cols, (chunk + 1) * cols)
        each(1, outers, lambda step: far_copy(chunk, step).wait_recv())
        out[:, lanes] = lax.fori_loop(
            1, outers, lambda step, total: total + far[chunk, step].astype(F32), out[:, lanes]
        )
    each(1, devices, lambda step: second_in(step).wait_recv())
    each(1, devices, lambda step: first(step).wait_send())
    each(1, devices, lambda step: second(step).wait_send())
    for chunk in range(chunks):
        for step in range(1, 4):
            near_copy(chunk, step).wait_send()
        each(1, outers, lambda step: far_copy(chunk, step).wait_send())


def finish(grads, small, clip_count, devices):
    outers = clip_count // 2
    shard_rows = grads.shape[0] // (4 * outers)
    width = grads.shape[1]
    chunks = 3
    cols = width // chunks
    out = jax.ShapeDtypeStruct
    dma = pltpu.SemaphoreType.DMA
    vmem = pl.BlockSpec(memory_space=pltpu.VMEM)
    return pl.pallas_call(
        finish_kernel,
        in_specs=[vmem, vmem],
        out_specs=[vmem, vmem],
        out_shape=[out((shard_rows, width), F32), out(small.shape, F32)],
        scratch_shapes=[
            pltpu.VMEM((chunks, 3, outers, shard_rows, cols), BF),
            pltpu.VMEM((chunks, outers, shard_rows, cols), BF),
            pltpu.VMEM((chunks, outers, shard_rows, cols), BF),
            pltpu.VMEM(small.shape, F32),
            dma((chunks, 3)),
            dma((chunks, 3)),
            dma((chunks, outers)),
            dma((chunks, outers)),
            dma((devices,)),
            dma((devices,)),
            dma((devices,)),
            dma((devices,)),
        ],
        compiler_params=pltpu.CompilerParams(
            collective_id=0, has_side_effects=True, vmem_limit_bytes=VMEM_LIMIT
        ),
        name="finish_reductions",
    )(grads.reshape(outers, 4, shard_rows, width), small)


def layer_norm(values, gain_row, shift_row):
    average = jnp.mean(values, axis=-1, keepdims=True)
    centred = values - average
    variance = jnp.mean(centred * centred, axis=-1, keepdims=True)
    return centred * lax.rsqrt(variance + 1e-06) * gain_row + shift_row


def exact_gelu(values):
    return jax.nn.gelu(values, approximate=False)


def swap(value, axis):
    return lax.ppermute(value, axis, [(0, 1), (1, 0)])


def head_total(portion):
    low = portion.astype(BF)
    return low.astype(F32) + swap(low, "head").astype(F32)


def precise(pattern, *operands):
    return jnp.einsum(pattern, *operands, precision=lax.Precision.HIGHEST)


def split_groups(value, which, axis):
    half = value.shape[axis] // 2
    low = lax.slice_in_dim(value, 0, half, axis=axis)
    high = lax.slice_in_dim(value, half, None, axis=axis)
    first = which == 0
    return jnp.where(first, low, high), jnp.where(first, high, low)


def join_groups(own, peer, which, axis):
    first = which == 0
    return jnp.concatenate([jnp.where(first, own, peer), jnp.where(first, peer, own)], axis=axis)


def time_choices(stride_group, memory_place, which, own, table_rows):
    local = jnp.arange(own, dtype=jnp.int32)
    times = jnp.concatenate([which * own + local, (1 - which) * own + local])
    stride = jnp.left_shift(jnp.int32(2), stride_group)[:, None, None]
    offset = 8 * (FRAMES - 1)
    current = stride * (times[None, :, None] - times[None, None, :]) + offset
    first = memory_place[:, np.array([2, 0, 3, 1])]
    second = memory_place[:, np.array([3, 1, 2, 0])]
    places = jnp.where(which == 0, first, second)
    memory = stride * times[None, :, None] + places[:, None, :] + offset
    chosen = jnp.concatenate([current, memory], axis=2)
    return (chosen[..., None] == jnp.arange(table_rows, dtype=jnp.int32)).astype(F32)


def space_choices():
    places = np.arange(SIDE)
    offsets = places[:, None] - places[None, :] + SIDE - 1
    hot = offsets.reshape(-1)[:, None] == np.arange(2 * SIDE - 1)[None, :]
    return jnp.asarray(hot.astype(np.float32))


def wide_rows(rows, heads):
    count, members, unit = rows.shape
    padded = jnp.pad(rows, ((0, 0), (0, 0), (0, LANES - unit)))
    spread = jnp.broadcast_to(padded[:, :, None], (count, members, heads, LANES))
    return spread.reshape(count, members * heads * LANES)


def local(
    clips_in,
    cached_kv,
    old_memory,
    stride_group,
    memory_place,
    norm_gain,
    norm_shift,
    qkv_weight,
    qkv_shift,
    pool_kernel,
    pool_gain,
    pool_shift,
    squeeze_kernel,
    time_table,
    space_tables,
    proj_weight,
    out_shift,
    up_weight,
    up_shift,
    down_weight,
    cotangent,
):
    clip_count, rows_clip, model_width = clips_in.shape
    head_width = qkv_weight.shape[2]
    unit = pool_gain.shape[1]
    head_count = head_width // unit
    frame_count = lax.axis_size("frame")
    heads = head_count // frame_count
    own_frames = rows_clip // CELLS
    row_total = clip_count * rows_clip
    hidden_width = up_weight.shape[1]
    group_width = heads * unit
    group_span = FRAMES // MEMF
    scale = unit ** (-0.5)
    both = ("clip", "frame")
    which = lax.axis_index("frame")
    which_row = which.astype(jnp.int32).reshape(1)
    into_np, outof_np = placement(frame_count)
    keys_np, mask_np, pad_np = bias_constants(frame_count)
    consts = (
        jnp.asarray(into_np, BF),
        jnp.asarray(outof_np, BF),
        jnp.asarray(keys_np, BF),
        jnp.asarray(mask_np),
        jnp.asarray(pad_np),
    )

    attn_full = lax.all_gather(qkv_weight, both, axis=0, tiled=True)
    shards = jnp.concatenate([proj_weight.T, up_weight, down_weight.T], axis=1)
    rest_full = lax.all_gather(shards, both, axis=0, tiled=True)
    proj_full = rest_full[:, :head_width]
    up_full = rest_full[:, head_width : head_width + hidden_width]
    down_full = rest_full[:, head_width + hidden_width :]

    cached_wide = cached_kv.astype(F32).reshape(
        clip_count, group_span, CELLS, 2, head_count, unit
    )
    squeezed = precise("cjsxnd,xjd->csxnd", cached_wide, squeeze_kernel).astype(BF)
    memory_rows = jnp.concatenate(
        [squeezed.reshape(clip_count, CELLS, 2, head_width), old_memory], axis=1
    )
    mem_own, mem_send = split_groups(memory_rows, which, 3)
    mem_own = mem_own.reshape(clip_count, -1, 2 * group_width)
    mem_send = mem_send.reshape(clip_count, -1, 2 * group_width)
    mem_peer = swap(mem_send, "frame")

    time_hot = time_choices(stride_group, memory_place, which, own_frames, time_table.shape[0])
    time_rows = precise("ctkr,rd->ctkd", time_hot, time_table).reshape(clip_count, -1, unit)
    space_hot = space_choices()
    space_rows = precise("pr,xrd->xpd", space_hot, space_tables).reshape(2 * CELLS, unit)
    bias = jnp.zeros((clip_count, BIAS_COLS, LANES), F32)
    bias = bias.at[:, : time_rows.shape[1], :unit].set(time_rows)
    bias = bias.at[:, SPACE_AT : SPACE_AT + 2 * CELLS, :unit].set(space_rows[None])
    bias = bias * (1.0 / scale)
    taps = wide_rows(pool_kernel.transpose(1, 0, 2), heads)
    gains = wide_rows(pool_gain[None], heads)
    shifts = wide_rows(pool_shift[None], heads)

    inputs_wide = clips_in.reshape(row_total, model_width).astype(F32)
    normed_one, norm_one_back = jax.vjp(layer_norm, inputs_wide, norm_gain[0], norm_shift[0])
    rounded_one = normed_one.astype(BF)
    attn_own, attn_send = split_groups(attn_full, which, 2)
    shift_own, shift_send = split_groups(qkv_shift, which, 1)

    def project(weight, shift):
        flat = weight.reshape(model_width, 3 * group_width)
        result = jnp.dot(rounded_one, flat, preferred_element_type=F32) + shift.reshape(-1)
        return result.astype(BF).reshape(clip_count, rows_clip, 3 * group_width)

    joined_peer = swap(project(attn_send, shift_send), "frame")
    joined_own = project(attn_own, shift_own)
    forward = attention_forward(
        which_row, joined_own, joined_peer, mem_own, mem_peer, consts, taps, gains, shifts, bias,
        scale, unit,
    )
    attended_own, attended_send = forward[:2]
    saved = forward[2:]
    attended_peer = swap(attended_send, "frame")
    attended = join_groups(attended_own, attended_peer, which, 2).reshape(row_total, head_width)
    branch = head_total(dot_f32(attended, proj_full, ((1,), (1,)))) + out_shift[0]
    middle = inputs_wide + branch
    normed_two, norm_two_back = jax.vjp(layer_norm, middle, norm_gain[1], norm_shift[1])
    rounded_two = normed_two.astype(BF)
    hidden = jnp.dot(rounded_two, up_full, preferred_element_type=F32) + up_shift
    activated, gelu_back = jax.vjp(exact_gelu, hidden)
    activated_low = activated.astype(BF)
    block_out = (
        middle + head_total(dot_f32(activated_low, down_full, ((1,), (1,)))) + out_shift[1]
    )
    block_out = block_out.astype(BF).reshape(clip_count, rows_clip, model_width)

    cotan_low = cotangent.reshape(row_total, model_width)
    cotan_wide = cotan_low.astype(F32)
    active_grad = jnp.dot(cotan_low, down_full, preferred_element_type=F32)
    hidden_grad = gelu_back(active_grad)[0].astype(BF)
    grad_up_bias = jnp.sum(hidden_grad.astype(F32), axis=0)
    normed_two_grad = head_total(dot_f32(hidden_grad, up_full, ((1,), (1,))))
    middle_norm_grad, gain_two_grad, shift_two_grad = norm_two_back(normed_two_grad)
    middle_grad = cotan_wide + middle_norm_grad
    branch_grad = middle_grad.astype(BF)
    attended_grad = jnp.dot(branch_grad, proj_full, preferred_element_type=F32).astype(BF)
    attended_grad = attended_grad.reshape(clip_count, rows_clip, head_width)
    grad_rest = jnp.concatenate(
        [
            dot_f32(branch_grad, attended, ((0,), (0,))).astype(BF),
            dot_f32(rounded_two, hidden_grad, ((0,), (0,))).astype(BF),
            dot_f32(cotan_low, activated_low, ((0,), (0,))).astype(BF),
        ],
        axis=1,
    )
    grad_rest, attended_grad = lax.optimization_barrier((grad_rest, attended_grad))
    rest_shard = lax.psum_scatter(grad_rest, both, scatter_dimension=0, tiled=True).astype(F32)

    attended_grad_own, attended_grad_send = split_groups(attended_grad, which, 2)
    attended_grad_peer = swap(attended_grad_send, "frame")
    backward = attention_backward(
        which_row, joined_own, joined_peer, attended_grad_own, attended_grad_peer, consts, taps,
        gains, bias, saved, scale, unit,
    )
    grad_own, grad_send, mem_grad_own, mem_grad_send = backward[:4]
    taps_grad, pool_gain_grad, pool_shift_grad, bias_grad = backward[4:]
    grad_peer = swap(grad_send, "frame")
    mem_grad_peer = swap(mem_grad_send[:, :CELLS], "frame")

    def lanes_back(rows, lead):
        return rows.reshape(lead + (-1, heads, LANES))[..., :unit]

    mem_grads = [
        part.reshape(clip_count, CELLS, 2, heads, LANES)[..., :unit]
        for part in (mem_grad_own[:, :CELLS], mem_grad_peer)
    ]
    squeezed_grads = join_groups(mem_grads[0], mem_grads[1], which, 3).astype(F32)
    grad_squeeze = precise("cjsxnd,csxnd->xjd", cached_wide, squeezed_grads)
    time_count = time_rows.shape[1]
    time_grad_rows = bias_grad[:, :time_count, :unit]
    grad_time = precise(
        "ckr,ckd->rd", time_hot.reshape(clip_count, time_count, -1), time_grad_rows
    )
    space_grad_rows = jnp.sum(bias_grad[:, SPACE_AT : SPACE_AT + 2 * CELLS, :unit], axis=0)
    grad_space = precise("pr,xpd->xrd", space_hot, space_grad_rows.reshape(2, CELLS, unit))
    grad_kernel = jnp.sum(lanes_back(jnp.sum(taps_grad, axis=1), (27,)), axis=2).transpose(1, 0, 2)
    grad_pool_gain = jnp.sum(lanes_back(pool_gain_grad, ()), axis=1)
    grad_pool_shift = jnp.sum(lanes_back(pool_shift_grad, ()), axis=1)

    parts = [
        part.reshape(row_total, 3, group_width)
        for part in (grad_own, grad_peer)
    ]
    joined_grad = join_groups(parts[0], parts[1], which, 2).reshape(row_total, 3 * head_width)
    grad_qkv_bias = jnp.sum(joined_grad.astype(F32), axis=0)
    grad_qkv = dot_f32(rounded_one, joined_grad, ((0,), (0,))).astype(BF)
    attn_flat = attn_full.reshape(model_width, 3 * head_width)
    normed_one_grad = head_total(dot_f32(joined_grad, attn_flat, ((1,), (1,))))
    input_norm_grad, gain_one_grad, shift_one_grad = norm_one_back(normed_one_grad)
    grad_in = (
        (middle_grad + input_norm_grad).astype(BF).reshape(clip_count, rows_clip, model_width)
    )

    head_index = lax.axis_index("head")
    head_axis = lax.axis_size("head")
    once = (head_index == 0).astype(F32)
    slot = (jnp.arange(head_axis) == head_index).astype(F32)[:, None]
    pieces = [
        jnp.stack([gain_one_grad, gain_two_grad]) * once,
        jnp.stack([shift_one_grad, shift_two_grad]) * once,
        jnp.stack([jnp.sum(middle_grad, axis=0), jnp.sum(cotan_wide, axis=0)]) * once,
        slot * grad_qkv_bias[None],
        slot * grad_up_bias[None],
        grad_kernel,
        grad_pool_gain,
        grad_pool_shift,
        grad_squeeze,
        grad_time,
        grad_space,
    ]
    flat = jnp.concatenate([piece.reshape(-1) for piece in pieces])
    devices = lax.axis_size("clip") * frame_count * head_axis
    block = -(-flat.size // (devices * 8 * LANES)) * 8
    flat = jnp.pad(flat, (0, devices * block * LANES - flat.size))
    qkv_shard, flat = finish(
        grad_qkv, flat.reshape(devices, block, LANES), lax.axis_size("clip"), devices
    )
    flat = flat.reshape(-1)
    sums = []
    at = 0
    for piece in pieces:
        sums.append(flat[at : at + piece.size].reshape(piece.shape))
        at += piece.size
    gain_sums, shift_sums, out_sums, qkv_bias_sum, up_bias_sum = sums[:5]
    kernel_sum, pool_gain_sum, pool_shift_sum, squeeze_sum, time_sum, space_sum = sums[5:]
    qkv_bias_sum = lax.dynamic_index_in_dim(qkv_bias_sum, head_index, 0, keepdims=False)
    up_bias_sum = lax.dynamic_index_in_dim(up_bias_sum, head_index, 0, keepdims=False)
    return (
        block_out,
        grad_in,
        gain_sums,
        shift_sums,
        qkv_shard.reshape(-1, 3, head_width),
        qkv_bias_sum.reshape(3, head_width),
        kernel_sum,
        pool_gain_sum,
        pool_shift_sum,
        squeeze_sum,
        time_sum,
        space_sum,
        rest_shard[:, :head_width].T,
        out_sums,
        rest_shard[:, head_width : head_width + hidden_width],
        up_bias_sum,
        rest_shard[:, head_width + hidden_width :].T,
    )


def solution(mesh):
    return jax.shard_map(
        local,
        mesh=mesh,
        in_specs=(
            P("clip", "frame", None),
            P("clip", "frame", None, "head"),
            P("clip", "frame", None, "head"),
            P("clip"),
            P("clip", None),
            P(),
            P(),
            P(("clip", "frame"), None, "head"),
            P(None, "head"),
            P(),
            P(),
            P(),
            P(),
            P(),
            P(),
            P("head", ("clip", "frame")),
            P(),
            P(("clip", "frame"), "head"),
            P("head"),
            P("head", ("clip", "frame")),
            P("clip", "frame", None),
        ),
        out_specs=(
            P("clip", "frame", None),
            P("clip", "frame", None),
            P(),
            P(),
            P(("clip", "frame"), None, "head"),
            P(None, "head"),
            P(),
            P(),
            P(),
            P(),
            P(),
            P(),
            P("head", ("clip", "frame")),
            P(),
            P(("clip", "frame"), "head"),
            P("head"),
            P("head", ("clip", "frame")),
        ),
        check_vma=False,
    )
```

```python
from functools import partial

import jax
import jax.numpy as jnp
import numpy as np
from jax import lax
from jax.experimental import pallas as pl
from jax.experimental.pallas import tpu as pltpu
from jax.sharding import PartitionSpec as P

FRAMES = 8
MEMF = 2
SIDE = 7
CELLS = SIDE * SIDE
LANES = 128
HALF = 208
QROWS = 2 * HALF
GRID_ROWS = FRAMES * SIDE * 8
MEM_AT = QROWS
MEM_PAD = 112
MEM_BACK = 64
KROWS = 640
BIAS_COLS = 256
SPACE_AT = 128
PAD_LANE = 127
BF = jnp.bfloat16
F32 = jnp.float32
VMEM_LIMIT = 60 * 1024 * 1024
MESH_ID = pl.DeviceIdType.MESH


def dot_f32(a, b, dims):
    return lax.dot_general(a, b, (dims, ((), ())), preferred_element_type=F32)


def frame_order(first, own):
    rest = [t for t in range(FRAMES) if not first * own <= t < (first + 1) * own]
    return list(range(first * own, (first + 1) * own)) + rest


def placement(frame_count):
    own = FRAMES // frame_count
    into = np.zeros((frame_count, GRID_ROWS, QROWS), np.float32)
    for first in range(frame_count):
        for slot, frame in enumerate(frame_order(first, own)):
            base = (slot // own) * HALF + (slot % own) * CELLS
            for high in range(SIDE):
                for wide in range(SIDE):
                    row = (frame * SIDE + high) * 8 + wide
                    into[first, row, base + high * SIDE + wide] = 1.0
    return into, np.ascontiguousarray(into.transpose(0, 2, 1))


def bias_constants(frame_count):
    own = FRAMES // frame_count
    frames_all = FRAMES + 2 * MEMF
    keys = np.zeros((BIAS_COLS, KROWS), np.float32)
    valid = np.zeros((KROWS,), bool)

    def mark(col, slot, high, wide):
        valid[col] = True
        for query in range(FRAMES):
            keys[query * frames_all + slot, col] = 1.0
        for place in range(SIDE):
            keys[SPACE_AT + place * SIDE + high, col] = 1.0
            keys[SPACE_AT + CELLS + place * SIDE + wide, col] = 1.0

    mask = np.zeros((QROWS, BIAS_COLS), np.float32)
    for slot in range(FRAMES):
        base = (slot // own) * HALF + (slot % own) * CELLS
        for high in range(SIDE):
            for wide in range(SIDE):
                row = base + high * SIDE + wide
                mark(row, slot, high, wide)
                mask[row, slot * frames_all : (slot + 1) * frames_all] = 1.0
                mask[row, SPACE_AT + high * SIDE : SPACE_AT + (high + 1) * SIDE] = 1.0
                low = SPACE_AT + CELLS + wide * SIDE
                mask[row, low : low + SIDE] = 1.0
    for group in range(2):
        for inner in range(MEMF):
            slot = FRAMES + group * MEMF + inner
            for high in range(SIDE):
                for wide in range(SIDE):
                    col = MEM_AT + group * MEM_PAD + inner * CELLS + high * SIDE + wide
                    mark(col, slot, high, wide)
    keys[PAD_LANE, ~valid] = -1e9
    pad_row = np.zeros((1, BIAS_COLS), np.float32)
    pad_row[0, PAD_LANE] = 1.0
    return keys, mask, pad_row


def spread_heads(source, target, rows_at, units, unit, first=0):
    count = source.shape[0]
    for index in range(units):
        at = (first + index) * unit
        target[rows_at : rows_at + count, index * LANES : index * LANES + unit] = source[
            :, at : at + unit
        ]


def load_shifted(field, shifted):
    grid = field.reshape(FRAMES, SIDE, 8, field.shape[-1])
    flat = field.reshape(FRAMES * SIDE, 8, field.shape[-1])
    shifted[1, 1 : FRAMES + 1, 1 : SIDE + 1] = grid
    shifted[0, 1 : FRAMES + 1, 1 : SIDE + 1] = pltpu.roll(flat, 1, 1).reshape(grid.shape)
    shifted[2, 1 : FRAMES + 1, 1 : SIDE + 1] = pltpu.roll(flat, 7, 1).reshape(grid.shape)


def convolve(shifted, taps, target, flip):
    tiles = target.shape[-1] // LANES

    def step(index, carry):
        frame = index // tiles
        lanes = pl.ds(pl.multiple_of((index % tiles) * LANES, LANES), LANES)
        total = jnp.zeros((SIDE, 8, LANES), F32)
        for i in range(3):
            for k in range(3):
                rows = shifted[k, frame + i, :, :, lanes]
                for j in range(3):
                    if flip:
                        tap = (2 - i) * 9 + (2 - j) * 3 + (2 - k)
                    else:
                        tap = i * 9 + j * 3 + k
                    total = total + rows[j : j + SIDE] * taps[tap, :, lanes][None]
        target[frame, :, :, lanes] = total
        return carry

    lax.fori_loop(0, FRAMES * tiles, step, 0)


def tap_grads(shifted, grads, target):
    tiles = target.shape[-1] // LANES
    for i in range(3):

        def step(index, carry, i=i):
            lanes = pl.ds(pl.multiple_of(index * LANES, LANES), LANES)

            def inner(frame, sums):
                centre = grads[frame + 1, :, :, lanes]
                new = []
                for j in range(3):
                    for k in range(3):
                        rows = shifted[k, frame + i, j : j + SIDE, :, lanes]
                        new.append(sums[j * 3 + k] + jnp.sum(rows * centre[1 : SIDE + 1], axis=0))
                return tuple(new)

            start = tuple(jnp.zeros((8, LANES), F32) for _ in range(9))
            sums = lax.fori_loop(0, FRAMES, inner, start)
            for tap in range(9):
                target[i * 9 + tap, :, lanes] += sums[tap]
            return carry

        lax.fori_loop(0, tiles, step, 0)


def head_stats(values, unit):
    average = jnp.sum(values, axis=-1, keepdims=True) * (1.0 / unit)
    lane = lax.broadcasted_iota(jnp.int32, values.shape, 1)
    centred = jnp.where(lane < unit, values - average, 0.0)
    variance = jnp.sum(centred * centred, axis=-1, keepdims=True) * (1.0 / unit)
    return centred, lax.rsqrt(variance + 1e-06)


def frame_partner():
    return (lax.axis_index("clip"), 1 - lax.axis_index("frame"), lax.axis_index("head"))


def partner_copy(source, target, send_sem, recv_sem):
    return pltpu.make_async_remote_copy(
        src_ref=source, dst_ref=target, send_sem=send_sem, recv_sem=recv_sem,
        device_id=frame_partner(), device_id_type=MESH_ID,
    )


def greet_partner():
    barrier = pltpu.get_barrier_semaphore()
    pl.semaphore_signal(barrier, inc=1, device_id=frame_partner(), device_id_type=MESH_ID)
    pl.semaphore_wait(barrier, 1)


def forward_kernel(
    own_ref, send_ref, mem_own_ref, mem_send_ref, into_ref, outof_ref, taps_ref, gain_ref,
    shift_ref, bias_ref, keyhot_ref, mask_ref, pad_ref,
    out_own, out_recv, packed_out, q_out, k_out, v_out, p_out, c_out,
    shifted, taps, peer, mem_peer, out_send, joined_sems, mem_sems, out_sems,
    *, heads, unit, scale,
):
    units = 3 * heads
    own_rows = own_ref.shape[1]
    clip = pl.program_id(0)
    clips = peer.shape[0]

    def joined_copy(index):
        return partner_copy(
            send_ref.at[index], peer.at[index], joined_sems.at[0, index], joined_sems.at[1, index]
        )

    def out_copy(index):
        return partner_copy(
            out_send.at[index], out_recv.at[index], out_sems.at[0, index], out_sems.at[1, index]
        )

    mem_copy = partner_copy(mem_send_ref, mem_peer, mem_sems.at[0], mem_sems.at[1])

    @pl.when(clip == 0)
    def _():
        greet_partner()
        for index in range(clips):
            joined_copy(index).start()
            if index == 0:
                mem_copy.start()
        shifted[...] = jnp.zeros_like(shifted)
        for tap in range(27):
            taps[tap] = jnp.broadcast_to(taps_ref[tap : tap + 1], taps.shape[1:])

    packed = packed_out.at[0]
    packed[...] = jnp.zeros(packed.shape, BF)
    spread_heads(own_ref.at[0], packed, 0, units, unit)
    joined_copy(clip).wait_recv()
    spread_heads(peer.at[clip], packed, HALF, units, unit)
    field = dot_f32(into_ref[...], packed[...], ((1,), (0,)))
    load_shifted(field, shifted)
    conv = c_out.at[0]
    convolve(shifted, taps, conv, False)

    @pl.when(clip == 0)
    def _():
        mem_copy.wait_recv()

    k_out[0, MEM_AT:, :] = jnp.zeros((KROWS - MEM_AT, heads * LANES), BF)
    v_out[0, MEM_AT:, :] = jnp.zeros((KROWS - MEM_AT, heads * LANES), BF)
    spread_heads(mem_own_ref.at[0], k_out.at[0], MEM_AT, heads, unit, 0 * heads)
    spread_heads(mem_own_ref.at[0], v_out.at[0], MEM_AT, heads, unit, 1 * heads)
    spread_heads(mem_peer.at[clip], k_out.at[0], MEM_AT + MEM_PAD, heads, unit, 0 * heads)
    spread_heads(mem_peer.at[clip], v_out.at[0], MEM_AT + MEM_PAD, heads, unit, 1 * heads)
    for index in range(units):
        lanes = slice(index * LANES, (index + 1) * LANES)
        block = conv[:, :, :, lanes].reshape(GRID_ROWS, LANES)
        centred, rate = head_stats(block, unit)
        normal = centred * rate * gain_ref[:, lanes] + shift_ref[:, lanes]
        rows = dot_f32(outof_ref[...], normal.astype(BF), ((1,), (0,))).astype(BF)
        target = (q_out, k_out, v_out)[index // heads]
        local = slice((index % heads) * LANES, (index % heads + 1) * LANES)
        target[0, 0:QROWS, local] = rows

    bias = bias_ref[0]
    bias_high = bias.astype(BF)
    bias_low = (bias - bias_high.astype(F32)).astype(BF)
    for head in range(heads):
        lanes = slice(head * LANES, (head + 1) * LANES)
        keys = k_out[0, :, lanes]
        values = v_out[0, :, lanes]
        for half in range(2):
            rows = slice(half * HALF, (half + 1) * HALF)
            query = q_out[0, rows, lanes]
            table = dot_f32(query, bias_high, ((1,), (1,))) + dot_f32(query, bias_low, ((1,), (1,)))
            table = table * mask_ref[rows, :] + pad_ref[...]
            table_high = table.astype(BF)
            table_low = (table - table_high.astype(F32)).astype(BF)
            scores = dot_f32(query, keys, ((1,), (1,)))
            scores = scores + dot_f32(table_high, keyhot_ref[...], ((1,), (0,)))
            scores = scores + dot_f32(table_low, keyhot_ref[...], ((1,), (0,)))
            top = jnp.max(scores, axis=-1, keepdims=True)
            weights = jnp.exp((scores - top) * scale)
            total = jnp.sum(weights, axis=-1, keepdims=True)
            probs = (weights * (1.0 / total)).astype(BF)
            p_out[0, head, rows, :] = probs
            mixed = dot_f32(probs, values, ((1,), (0,))) + query.astype(F32)
            target = (out_own.at[0], out_send.at[clip])[half]
            target[:, head * unit : (head + 1) * unit] = mixed[:own_rows, :unit].astype(BF)

    out_copy(clip).start()

    @pl.when(clip == clips - 1)
    def _():
        mem_copy.wait_send()
        for index in range(clips):
            joined_copy(index).wait_send()
            out_copy(index).wait()


def backward_kernel(
    packed_ref, grad_own_ref, grad_send_ref, into_ref, outof_ref, taps_ref, gain_ref,
    bias_ref, keyhot_ref, mask_ref, q_ref, k_ref, v_ref, p_ref, c_ref,
    out_own, out_recv, mem_own, mem_recv, taps_out, gain_out, shift_out, bias_out,
    shifted, taps, grads, spread, pooled, peer, out_send, mem_send, grad_sems, out_sems, mem_sems,
    *, heads, unit, scale,
):
    units = 3 * heads
    own_rows = grad_own_ref.shape[1]
    clip = pl.program_id(0)
    clips = peer.shape[0]

    def grad_copy(index):
        return partner_copy(
            grad_send_ref.at[index], peer.at[index], grad_sems.at[0, index], grad_sems.at[1, index]
        )

    def out_copy(index):
        return partner_copy(
            out_send.at[index], out_recv.at[index], out_sems.at[0, index], out_sems.at[1, index]
        )

    def mem_copy(index):
        return partner_copy(
            mem_send.at[index], mem_recv.at[index], mem_sems.at[0, index], mem_sems.at[1, index]
        )

    @pl.when(clip == 0)
    def _():
        greet_partner()
        for index in range(clips):
            grad_copy(index).start()
        shifted[...] = jnp.zeros_like(shifted)
        grads[...] = jnp.zeros_like(grads)
        spread[...] = jnp.zeros_like(spread)
        taps_out[...] = jnp.zeros_like(taps_out)
        gain_out[...] = jnp.zeros_like(gain_out)
        shift_out[...] = jnp.zeros_like(shift_out)
        for tap in range(27):
            taps[tap] = jnp.broadcast_to(taps_ref[tap : tap + 1], taps.shape[1:])

    load_shifted(dot_f32(into_ref[...], packed_ref[0], ((1,), (0,))), shifted)
    spread_heads(grad_own_ref.at[0], spread, 0, heads, unit)
    grad_copy(clip).wait_recv()
    spread_heads(peer.at[clip], spread, HALF, heads, unit)
    bias_low = bias_ref[0].astype(BF)
    bias_sum = jnp.zeros((BIAS_COLS, LANES), F32)
    for head in range(heads):
        lanes = slice(head * LANES, (head + 1) * LANES)
        keys = k_ref[0, :, lanes]
        values = v_ref[0, :, lanes]
        keys_grad = jnp.zeros((KROWS, LANES), F32)
        values_grad = jnp.zeros((KROWS, LANES), F32)
        for half in range(2):
            rows = slice(half * HALF, (half + 1) * HALF)
            query = q_ref[0, rows, lanes]
            out_grad = spread[rows, lanes]
            probs = p_ref[0, head, rows, :]
            wide = probs.astype(F32)
            probs_grad = dot_f32(out_grad, values, ((1,), (1,)))
            weighted = wide * probs_grad
            shared = jnp.sum(weighted, axis=-1, keepdims=True)
            score_grad = (weighted - wide * shared).astype(BF)
            values_grad = values_grad + dot_f32(probs, out_grad, ((0,), (0,)))
            keys_grad = keys_grad + dot_f32(score_grad, query, ((0,), (0,)))
            table_grad = dot_f32(score_grad, keyhot_ref[...], ((1,), (1,))) * mask_ref[rows, :]
            table_low = table_grad.astype(BF)
            query_grad = dot_f32(score_grad, keys, ((1,), (0,)))
            query_grad = query_grad + dot_f32(table_low, bias_low, ((1,), (0,)))
            query_grad = query_grad * scale + out_grad.astype(F32)
            pooled[rows, lanes] = query_grad.astype(BF)
            bias_sum = bias_sum + dot_f32(table_low, query, ((0,), (0,)))
        keys_grad = (keys_grad * scale).astype(BF)
        values_grad = values_grad.astype(BF)
        for member, part in enumerate((keys_grad, values_grad)):
            at = ((member + 1) * heads + head) * LANES
            pooled[:, at : at + LANES] = part[:QROWS]
            at = (member * heads + head) * LANES
            low = MEM_AT + MEM_PAD
            mem_own[0, :, at : at + LANES] = part[MEM_AT : MEM_AT + MEM_BACK]
            mem_send[clip, :, at : at + LANES] = part[low : low + MEM_BACK]
    bias_out[0] = bias_sum
    mem_copy(clip).start()

    for index in range(units):
        lanes = slice(index * LANES, (index + 1) * LANES)
        incoming = dot_f32(into_ref[...], pooled[:, lanes], ((1,), (0,)))
        block = c_ref[0, :, :, :, lanes].reshape(GRID_ROWS, LANES)
        centred, rate = head_stats(block, unit)
        normal = centred * rate
        product = incoming * normal
        gain_out[:, lanes] += jnp.sum(product, axis=0, keepdims=True)
        shift_out[:, lanes] += jnp.sum(incoming, axis=0, keepdims=True)
        inner = incoming * gain_ref[:, lanes]
        mean_inner = jnp.sum(inner, axis=-1, keepdims=True) * (1.0 / unit)
        mean_both = jnp.sum(inner * normal, axis=-1, keepdims=True) * (1.0 / unit)
        lane = lax.broadcasted_iota(jnp.int32, block.shape, 1)
        result = rate * (inner - mean_inner - normal * mean_both)
        result = jnp.where(lane < unit, result, 0.0)
        flat = result.reshape(FRAMES * SIDE, 8, LANES)
        shape = (FRAMES, SIDE, 8, LANES)
        grads[1, 1 : FRAMES + 1, 1 : SIDE + 1, :, lanes] = flat.reshape(shape)
        grads[0, 1 : FRAMES + 1, 1 : SIDE + 1, :, lanes] = pltpu.roll(flat, 1, 1).reshape(shape)
        grads[2, 1 : FRAMES + 1, 1 : SIDE + 1, :, lanes] = pltpu.roll(flat, 7, 1).reshape(shape)

    tap_grads(shifted, grads.at[1], taps_out)
    conv = shifted.at[1, 1 : FRAMES + 1, 1 : SIDE + 1]
    convolve(grads, taps, conv, True)
    for index in range(units):
        lanes = slice(index * LANES, (index + 1) * LANES)
        block = shifted[1, 1 : FRAMES + 1, 1 : SIDE + 1, :, lanes].reshape(GRID_ROWS, LANES)
        rows = dot_f32(outof_ref[...], block.astype(BF), ((1,), (0,))).astype(BF)
        local = slice(index * unit, (index + 1) * unit)
        out_own[0, :, local] = rows[:own_rows, :unit]
        out_send[clip, :, local] = rows[HALF : HALF + own_rows, :unit]
    out_copy(clip).start()

    @pl.when(clip == clips - 1)
    def _():
        for index in range(clips):
            grad_copy(index).wait_send()
            mem_copy(index).wait()
            out_copy(index).wait()


def whole_spec(shape):
    return pl.BlockSpec(shape, lambda clip: (0,) * len(shape))


def clip_spec(shape):
    return pl.BlockSpec((1,) + shape, lambda clip: (clip,) + (0,) * len(shape))


def any_spec():
    return pl.BlockSpec(memory_space=pl.ANY)


def attention_forward(own, send, mem_own, mem_send, consts, taps, gains, shifts, bias, scale, unit):
    clips, rows, width = own.shape
    heads = width // (3 * unit)
    into, outof, keyhot, mask, pad_row = consts
    wide = 3 * heads * LANES
    mem_shape = mem_own.shape[1:]
    out = jax.ShapeDtypeStruct
    dma = pltpu.SemaphoreType.DMA
    return pl.pallas_call(
        partial(forward_kernel, heads=heads, unit=unit, scale=scale),
        grid=(clips,),
        in_specs=[
            clip_spec((rows, width)),
            any_spec(),
            clip_spec(mem_shape),
            any_spec(),
            whole_spec((GRID_ROWS, QROWS)),
            whole_spec((QROWS, GRID_ROWS)),
            whole_spec((27, wide)),
            whole_spec((1, wide)),
            whole_spec((1, wide)),
            clip_spec((BIAS_COLS, LANES)),
            whole_spec((BIAS_COLS, KROWS)),
            whole_spec((QROWS, BIAS_COLS)),
            whole_spec((1, BIAS_COLS)),
        ],
        out_specs=[
            clip_spec((rows, heads * unit)),
            any_spec(),
            clip_spec((QROWS, wide)),
            clip_spec((QROWS, heads * LANES)),
            clip_spec((KROWS, heads * LANES)),
            clip_spec((KROWS, heads * LANES)),
            clip_spec((heads, QROWS, KROWS)),
            clip_spec((FRAMES, SIDE, 8, wide)),
        ],
        scratch_shapes=[
            pltpu.VMEM((3, FRAMES + 2, SIDE + 2, 8, wide), F32),
            pltpu.VMEM((27, 8, wide), F32),
            pltpu.VMEM((clips, rows, width), BF),
            pltpu.VMEM((clips,) + mem_shape, BF),
            pltpu.VMEM((clips, rows, heads * unit), BF),
            dma((2, clips)),
            dma((2,)),
            dma((2, clips)),
        ],
        out_shape=[
            out((clips, rows, heads * unit), BF),
            out((clips, rows, heads * unit), BF),
            out((clips, QROWS, wide), BF),
            out((clips, QROWS, heads * LANES), BF),
            out((clips, KROWS, heads * LANES), BF),
            out((clips, KROWS, heads * LANES), BF),
            out((clips, heads, QROWS, KROWS), BF),
            out((clips, FRAMES, SIDE, 8, wide), F32),
        ],
        compiler_params=pltpu.CompilerParams(
            collective_id=1, has_side_effects=True, vmem_limit_bytes=VMEM_LIMIT
        ),
        name="pooled_attention_forward",
    )(own, send, mem_own, mem_send, into, outof, taps, gains, shifts, bias, keyhot, mask, pad_row)


def attention_backward(grad_own, grad_send, consts, taps, gains, bias, saved, scale, unit):
    clips, rows, width = grad_own.shape
    heads = width // unit
    into, outof, keyhot, mask, pad_row = consts
    wide = 3 * heads * LANES
    joined_width = 3 * heads * unit
    out = jax.ShapeDtypeStruct
    dma = pltpu.SemaphoreType.DMA
    return pl.pallas_call(
        partial(backward_kernel, heads=heads, unit=unit, scale=scale),
        grid=(clips,),
        in_specs=[
            clip_spec((QROWS, wide)),
            clip_spec((rows, width)),
            any_spec(),
            whole_spec((GRID_ROWS, QROWS)),
            whole_spec((QROWS, GRID_ROWS)),
            whole_spec((27, wide)),
            whole_spec((1, wide)),
            clip_spec((BIAS_COLS, LANES)),
            whole_spec((BIAS_COLS, KROWS)),
            whole_spec((QROWS, BIAS_COLS)),
            clip_spec((QROWS, heads * LANES)),
            clip_spec((KROWS, heads * LANES)),
            clip_spec((KROWS, heads * LANES)),
            clip_spec((heads, QROWS, KROWS)),
            clip_spec((FRAMES, SIDE, 8, wide)),
        ],
        out_specs=[
            clip_spec((rows, joined_width)),
            any_spec(),
            clip_spec((MEM_BACK, 2 * heads * LANES)),
            any_spec(),
            whole_spec((27, 8, wide)),
            whole_spec((1, wide)),
            whole_spec((1, wide)),
            clip_spec((BIAS_COLS, LANES)),
        ],
        scratch_shapes=[
            pltpu.VMEM((3, FRAMES + 2, SIDE + 2, 8, wide), F32),
            pltpu.VMEM((27, 8, wide), F32),
            pltpu.VMEM((3, FRAMES + 2, SIDE + 2, 8, wide), F32),
            pltpu.VMEM((QROWS, heads * LANES), BF),
            pltpu.VMEM((QROWS, wide), BF),
            pltpu.VMEM((clips, rows, width), BF),
            pltpu.VMEM((clips, rows, joined_width), BF),
            pltpu.VMEM((clips, MEM_BACK, 2 * heads * LANES), BF),
            dma((2, clips)),
            dma((2, clips)),
            dma((2, clips)),
        ],
        out_shape=[
            out((clips, rows, joined_width), BF),
            out((clips, rows, joined_width), BF),
            out((clips, MEM_BACK, 2 * heads * LANES), BF),
            out((clips, MEM_BACK, 2 * heads * LANES), BF),
            out((27, 8, wide), F32),
            out((1, wide), F32),
            out((1, wide), F32),
            out((clips, BIAS_COLS, LANES), F32),
        ],
        compiler_params=pltpu.CompilerParams(
            collective_id=2, has_side_effects=True, vmem_limit_bytes=VMEM_LIMIT
        ),
        name="pooled_attention_backward",
    )(saved[0], grad_own, grad_send, into, outof, taps, gains, bias, keyhot, mask, *saved[1:])


def row_stats(values):
    width = values.shape[-1]
    centred = values - jnp.sum(values, axis=-1, keepdims=True) * (1.0 / width)
    variance = jnp.sum(centred * centred, axis=-1, keepdims=True) * (1.0 / width)
    return centred, lax.rsqrt(variance + 1e-06)


def each(low, high, act):
    def body(step, carry):
        act(step)
        return carry

    lax.fori_loop(low, high, body, 0)


def project_rows(x, gain, shift, normed):
    def step(clip):
        centred, rate = row_stats(x[clip].astype(F32))
        normed[clip] = (centred * rate * gain[...] + shift[...]).astype(BF)

    each(0, x.shape[0], step)


def project_out(normed, weight, bias, own, send):
    model = normed.shape[2]
    group = own.shape[2] // 3
    first = lax.axis_index("frame") == 0

    def step(clip):
        rows = dot_f32(normed[clip], weight, ((1,), (0,))) + bias[...]
        rows = rows.astype(BF)

        def store(low, high):
            for member in range(3):
                at = 2 * member * group
                local = slice(member * group, (member + 1) * group)
                low[clip, :, local] = rows[:, at : at + group]
                high[clip, :, local] = rows[:, at + group : at + 2 * group]

        @pl.when(first)
        def _():
            store(own, send)

        @pl.when(jnp.logical_not(first))
        def _():
            store(send, own)

    each(0, own.shape[0], step)


def project_kernel(
    x, shard, gain, shift, bias, full, own, send, normed, far_send, far_recv, near_send, near_recv
):
    outers, _, shard_rows, width = full.shape
    clip = lax.axis_index("clip")
    frame = lax.axis_index("frame")
    head = lax.axis_index("head")
    outer, inner = clip // 2, clip % 2
    place = inner * 2 + frame
    barrier = pltpu.get_barrier_semaphore()

    def far_device(step):
        return device_of((outer + step) % outers, inner, frame, head)

    def near_device(step):
        there_inner, there_frame = plane_peer(inner, frame, step)
        return device_of(outer, there_inner, there_frame, head)

    def greet(device):
        pl.semaphore_signal(barrier, inc=1, device_id=device, device_id_type=MESH_ID)

    each(1, outers, lambda step: greet(far_device(step)))
    for step in range(1, 4):
        greet(near_device(step))
    pl.semaphore_wait(barrier, outers - 1 + 3)

    def far_copy(step, at):
        return pltpu.make_async_remote_copy(
            src_ref=shard, dst_ref=full.at[at, place],
            send_sem=far_send.at[step], recv_sem=far_recv.at[step],
            device_id=far_device(step), device_id_type=MESH_ID,
        )

    def near_copy(index, step, source, at):
        return pltpu.make_async_remote_copy(
            src_ref=source, dst_ref=full.at[at, place],
            send_sem=near_send.at[index, step - 1], recv_sem=near_recv.at[index, step - 1],
            device_id=near_device(step), device_id_type=MESH_ID,
        )

    def near_arrival(index, step, at):
        there_inner, there_frame = plane_peer(inner, frame, step)
        return pltpu.make_async_remote_copy(
            src_ref=shard, dst_ref=full.at[at, there_inner * 2 + there_frame],
            send_sem=near_send.at[index, step - 1], recv_sem=near_recv.at[index, step - 1],
            device_id=near_device(step), device_id_type=MESH_ID,
        )

    def origin(step):
        return (outer + outers - step) % outers

    each(1, outers, lambda step: far_copy(step, outer).start())
    for step in range(1, 4):
        near_copy(0, step, shard, outer).start()
    full[outer, place] = shard[...]
    project_rows(x, gain, shift, normed)

    def forward(index):
        far_copy(index, origin(index)).wait_recv()
        for step in range(1, 4):
            near_copy(index, step, full.at[origin(index), place], origin(index)).start()

    each(1, outers, forward)

    def arrive(index):
        for step in range(1, 4):
            near_arrival(index, step, origin(index)).wait_recv()

    each(0, outers, arrive)
    project_out(normed, full[...].reshape(outers * 4 * shard_rows, width), bias, own, send)
    each(1, outers, lambda step: far_copy(step, outer).wait_send())
    for step in range(1, 4):
        near_copy(0, step, shard, outer).wait_send()

    def sent(index):
        for step in range(1, 4):
            near_copy(index, step, full.at[origin(index), place], origin(index)).wait_send()

    each(1, outers, sent)


def project_local_kernel(x, weight, gain, shift, bias, own, send, normed):
    project_rows(x, gain, shift, normed)
    project_out(normed, weight[...], bias, own, send)


def project(x, shard, gain, shift, bias, clip_count):
    clips, rows, model = x.shape
    width = shard.shape[1]
    outers = clip_count // 2
    half = width // 2
    out = jax.ShapeDtypeStruct
    dma = pltpu.SemaphoreType.DMA
    vmem = pl.BlockSpec(memory_space=pltpu.VMEM)
    halves = [out((clips, rows, half), BF)] * 2
    normed = pltpu.VMEM((clips, rows, model), BF)
    if shard.shape[0] % 16:
        full = lax.all_gather(shard, ("clip", "frame"), axis=0, tiled=True)
        own, send = pl.pallas_call(
            project_local_kernel,
            in_specs=[vmem] * 5,
            out_specs=[vmem] * 2,
            out_shape=halves,
            scratch_shapes=[normed],
            compiler_params=pltpu.CompilerParams(vmem_limit_bytes=VMEM_LIMIT),
            name="project_local",
        )(x, full, gain, shift, bias)
        return full, own, send
    full, own, send = pl.pallas_call(
        project_kernel,
        in_specs=[vmem] * 5,
        out_specs=[vmem] * 3,
        out_shape=[out((outers, 4) + shard.shape, BF)] + halves,
        scratch_shapes=[
            normed,
            dma((outers,)),
            dma((outers,)),
            dma((outers, 3)),
            dma((outers, 3)),
        ],
        compiler_params=pltpu.CompilerParams(
            collective_id=3, has_side_effects=True, vmem_limit_bytes=VMEM_LIMIT
        ),
        name="gather_and_project",
    )(x, shard, gain, shift, bias)
    return full.reshape(model, width), own, send


def device_of(outer, inner, frame, head):
    return (outer * 2 + inner, frame, head)


def plane_peer(inner, frame, step):
    return (inner + step // 2) % 2, (frame + step % 2) % 2


def row_piece(value, row):
    return value[:, row * LANES : (row + 1) * LANES]


def tail_kernel(
    own, recv, x, middle_grad, weight, gain, shift, taps, pool_gain, pool_shift, bias_grad, hot,
    space_hot, squeeze, vectors, up_bias,
    grad_in, out, gain_out, shift_out, rows_out, joined_out, up_out, taps_out, pool_gain_out,
    pool_shift_out, squeeze_out, time_out, space_out,
    joined, normed, grads, near, part, far, small, small_in, small_out, cross_send, cross_recv,
    cross_sems, near_sems, far_sems, first_sems, second_sems,
    *, unit, plan,
):
    chunks, outers, shard_rows, cols = part.shape
    clips, rows, model = x.shape
    group = own.shape[2] // 3
    span = joined.shape[0] // clips
    devices = small.shape[0]
    clip = lax.axis_index("clip")
    frame = lax.axis_index("frame")
    head = lax.axis_index("head")
    outer, inner = clip // 2, clip % 2
    place = inner * 2 + frame
    mine = (clip * 2 + frame) * 2 + head

    def device(index):
        return (index // 4, (index // 2) % 2, index % 2)

    barrier = pltpu.get_barrier_semaphore()
    each(
        1,
        devices,
        lambda step: pl.semaphore_signal(
            barrier, inc=1, device_id=device((mine + step) % devices), device_id_type=MESH_ID
        ),
    )

    def first(step):
        other = (mine + step) % devices
        return pltpu.make_async_remote_copy(
            src_ref=small.at[other], dst_ref=small_in.at[step],
            send_sem=first_sems.at[0, step], recv_sem=first_sems.at[1, step],
            device_id=device(other), device_id_type=MESH_ID,
        )

    def second(step, block):
        return pltpu.make_async_remote_copy(
            src_ref=small_out.at[block], dst_ref=small_out.at[block],
            send_sem=second_sems.at[0, step], recv_sem=second_sems.at[1, step],
            device_id=device((mine + step) % devices), device_id_type=MESH_ID,
        )

    def near_copy(chunk, step):
        there_inner, there_frame = plane_peer(inner, frame, step)
        return pltpu.make_async_remote_copy(
            src_ref=grads.at[chunk, :, there_inner * 2 + there_frame],
            dst_ref=near.at[chunk, step - 1],
            send_sem=near_sems.at[0, chunk, step - 1], recv_sem=near_sems.at[1, chunk, step - 1],
            device_id=device_of(outer, there_inner, there_frame, head), device_id_type=MESH_ID,
        )

    def far_copy(chunk, step):
        there = (outer + step) % outers
        return pltpu.make_async_remote_copy(
            src_ref=part.at[chunk, there], dst_ref=far.at[chunk, step],
            send_sem=far_sems.at[0, chunk, step], recv_sem=far_sems.at[1, chunk, step],
            device_id=device_of(there, inner, frame, head), device_id_type=MESH_ID,
        )

    def cross_copy(index):
        return pltpu.make_async_remote_copy(
            src_ref=cross_send.at[index], dst_ref=cross_recv.at[index],
            send_sem=cross_sems.at[0, index], recv_sem=cross_sems.at[1, index],
            device_id=(clip, frame, 1 - head), device_id_type=MESH_ID,
        )

    joined[...] = jnp.zeros_like(joined)
    normed[...] = jnp.zeros_like(normed)
    small[...] = jnp.zeros_like(small)

    def assemble(low, high):
        for index in range(clips):
            at = slice(index * span, index * span + rows)
            for member in range(3):
                source = slice(member * group, (member + 1) * group)
                left = 2 * member * group
                joined[at, left : left + group] = low[index, :, source]
                joined[at, left + group : left + 2 * group] = high[index, :, source]

    @pl.when(frame == 0)
    def _():
        assemble(own, recv)

    @pl.when(frame == 1)
    def _():
        assemble(recv, own)

    pl.semaphore_wait(barrier, devices - 1)
    for index in range(clips):
        block = joined[index * span : (index + 1) * span]
        partial_rows = dot_f32(block, weight[...], ((1,), (1,)))
        cross_send[index] = partial_rows[:rows].astype(BF)
        cross_copy(index).start()
    for index in range(clips):
        centred, rate = row_stats(x[index].astype(F32))
        value = centred * rate * gain[...] + shift[...]
        normed[index * span : index * span + rows] = value.astype(BF)
    for chunk in range(chunks):
        value = dot_f32(normed[...], joined[:, chunk * cols : (chunk + 1) * cols], ((0,), (0,)))
        value = value.astype(BF)
        if shard_rows % 16 == 0:
            grads[chunk] = value.reshape(outers, 4, shard_rows, cols)
        else:
            for block in range(outers * 4):
                low = block * shard_rows
                grads[chunk, block // 4, block % 4] = value[low : low + shard_rows]
        for step in range(1, 4):
            near_copy(chunk, step).start()

    gain_sum = jnp.zeros((1, model), F32)
    shift_sum = jnp.zeros((1, model), F32)
    for index in range(clips):
        cross_copy(index).wait_recv()
        incoming = cross_send[index].astype(F32) + cross_recv[index].astype(F32)
        centred, rate = row_stats(x[index].astype(F32))
        normal = centred * rate
        product = incoming * normal
        gain_sum = gain_sum + jnp.sum(product, axis=0, keepdims=True)
        shift_sum = shift_sum + jnp.sum(incoming, axis=0, keepdims=True)
        scaled = incoming * gain[...]
        mean_scaled = jnp.sum(scaled, axis=-1, keepdims=True) * (1.0 / model)
        mean_both = jnp.sum(scaled * normal, axis=-1, keepdims=True) * (1.0 / model)
        result = rate * (scaled - mean_scaled - normal * mean_both) + middle_grad[index]
        grad_in[index] = result.astype(BF)

    rows_small = small.shape[1]

    def put(row, value):
        count = value.shape[0]
        done = 0
        while done < count:
            block, offset = divmod(row + done, rows_small)
            size = min(count - done, rows_small - offset)
            small[block, offset : offset + size, : value.shape[1]] = value[done : done + size]
            done += size

    def take(row, target):
        count = target.shape[0]
        done = 0
        while done < count:
            block, offset = divmod(row + done, rows_small)
            size = min(count - done, rows_small - offset)
            target[done : done + size] = small_out[
                block, offset : offset + size, : target.shape[1]
            ]
            done += size

    def put_wide(row, value):
        for index in range(value.shape[1] // LANES):
            put(row + index, row_piece(value, index))

    def take_wide(row, target, at):
        for index in range(target.shape[1] // LANES):
            block, offset = divmod(row + index, rows_small)
            target[at : at + 1, index * LANES : (index + 1) * LANES] = small_out[
                block, offset : offset + 1
            ]

    wide_rows_count = model // LANES

    @pl.when(head == 0)
    def _():
        put_wide(plan["gain"], gain_sum)
        put_wide(plan["gain"] + wide_rows_count, vectors[0:1])
        put_wide(plan["shift"], shift_sum)
        put_wide(plan["shift"] + wide_rows_count, vectors[1:2])
        put_wide(plan["rows"], vectors[2:3])
        put_wide(plan["rows"] + wide_rows_count, vectors[3:4])

    joined_sum = jnp.sum(joined[...].astype(F32), axis=0, keepdims=True)
    joined_rows = joined.shape[1] // LANES
    up_rows = up_bias.shape[1] // LANES
    for which in range(2):

        @pl.when(head == which)
        def _():
            put_wide(plan["joined"] + which * joined_rows, joined_sum)
            put_wide(plan["up"] + which * up_rows, up_bias[...])

    heads = taps.shape[2] // (3 * LANES)
    tap_sum = jnp.sum(taps[...], axis=1)
    for member in range(3):
        totals = []
        for value in (tap_sum, pool_gain[...], pool_shift[...]):
            total = row_piece(value, member * heads)
            for index in range(1, heads):
                total = total + row_piece(value, member * heads + index)
            totals.append(total)
        put(plan["taps"] + member * 27, totals[0])
        put(plan["pool_gain"] + member, totals[1])
        put(plan["pool_shift"] + member, totals[2])
    put(plan["squeeze"], squeeze[...])
    time_sum = jnp.zeros((hot.shape[2], LANES), F32)
    bias_sum = jnp.zeros((BIAS_COLS, LANES), F32)
    for index in range(clips):
        value = bias_grad[index]
        bias_sum = bias_sum + value
        value = value[: hot.shape[1]]
        high = value.astype(BF)
        low = (value - high.astype(F32)).astype(BF)
        time_sum = time_sum + dot_f32(hot[index], high, ((0,), (0,)))
        time_sum = time_sum + dot_f32(hot[index], low, ((0,), (0,)))
    put(plan["time"], time_sum[: time_out.shape[0]])
    high = bias_sum.astype(BF)
    low = (bias_sum - high.astype(F32)).astype(BF)
    space_sum = dot_f32(space_hot[...], high, ((1,), (0,)))
    space_sum = space_sum + dot_f32(space_hot[...], low, ((1,), (0,)))
    put(plan["space"], space_sum[: space_out.shape[0]])

    each(1, devices, lambda step: first(step).start())

    def reduce_near(chunk):
        lanes = slice(chunk * cols, (chunk + 1) * cols)
        for step in range(1, 4):
            near_copy(chunk, step).wait_recv()

        def gathered(index):
            value = grads[chunk, index, place].astype(F32)
            for step in range(3):
                value = value + near[chunk, step, index].astype(F32)
            return value

        def send(step):
            there = (outer + step) % outers
            part[chunk, there] = gathered(there).astype(BF)
            far_copy(chunk, step).start()

        each(1, outers, send)
        out[:, lanes] = gathered(outer)

    reduce_near(0)
    each(1, devices, lambda step: first(step).wait_recv())
    total = lax.fori_loop(1, devices, lambda step, sums: sums + small_in[step], small[mine])
    small_out[mine] = total
    each(1, devices, lambda step: second(step, mine).start())
    for chunk in range(1, chunks):
        reduce_near(chunk)
    for chunk in range(chunks):
        lanes = slice(chunk * cols, (chunk + 1) * cols)
        each(1, outers, lambda step: far_copy(chunk, step).wait_recv())
        out[:, lanes] = lax.fori_loop(
            1, outers, lambda step, sums: sums + far[chunk, step].astype(F32), out[:, lanes]
        )
    each(1, devices, lambda step: second(step, (mine + devices - step) % devices).wait_recv())
    for index in range(2):
        take_wide(plan["gain"] + index * wide_rows_count, gain_out, index)
        take_wide(plan["shift"] + index * wide_rows_count, shift_out, index)
        take_wide(plan["rows"] + index * wide_rows_count, rows_out, index)
    for which in range(2):

        @pl.when(head == which)
        def _():
            for member in range(3):
                row = plan["joined"] + which * joined_rows + member * (joined_rows // 3)
                take_wide(row, joined_out, member)
            take_wide(plan["up"] + which * up_rows, up_out, 0)

    for member in range(3):
        take(plan["taps"] + member * 27, taps_out.at[member])
    take(plan["pool_gain"], pool_gain_out)
    take(plan["pool_shift"], pool_shift_out)
    take(plan["squeeze"], squeeze_out)
    take(plan["time"], time_out)
    take(plan["space"], space_out)
    each(1, devices, lambda step: first(step).wait_send())
    each(1, devices, lambda step: second(step, mine).wait_send())
    for index in range(clips):
        cross_copy(index).wait_send()
    for chunk in range(chunks):
        for step in range(1, 4):
            near_copy(chunk, step).wait_send()
        each(1, outers, lambda step: far_copy(chunk, step).wait_send())


def tail(
    own, recv, x, middle_grad, weight, gain, shift, taps, pool_gain, pool_shift, bias_grad, hot,
    space_hot, squeeze, vectors, up_bias, clip_count, devices, unit, table_rows,
):
    clips, rows, model = x.shape
    width = weight.shape[1]
    outers = clip_count // 2
    shard_rows = model // (4 * outers)
    chunks = 3
    cols = width // chunks
    span = -(-rows // 16) * 16
    plan = {}
    at = 0
    for name, count in (
        ("gain", 2 * model // LANES),
        ("shift", 2 * model // LANES),
        ("rows", 2 * model // LANES),
        ("joined", 2 * width // LANES),
        ("up", 2 * up_bias.shape[1] // LANES),
        ("taps", 81),
        ("pool_gain", 3),
        ("pool_shift", 3),
        ("squeeze", squeeze.shape[0]),
        ("time", table_rows),
        ("space", 2 * (2 * SIDE - 1)),
    ):
        plan[name] = at
        at += count
    block = -(-at // (devices * 8)) * 8
    out = jax.ShapeDtypeStruct
    dma = pltpu.SemaphoreType.DMA
    vmem = pl.BlockSpec(memory_space=pltpu.VMEM)
    shapes = [
        out((clips, rows, model), BF),
        out((shard_rows, width), F32),
        out((2, model), F32),
        out((2, model), F32),
        out((2, model), F32),
        out((3, width // 3), F32),
        out((1, up_bias.shape[1]), F32),
        out((3, 27, unit), F32),
        out((3, unit), F32),
        out((3, unit), F32),
        out(squeeze.shape, F32),
        out((table_rows, unit), F32),
        out((2 * (2 * SIDE - 1), unit), F32),
    ]
    return pl.pallas_call(
        partial(tail_kernel, unit=unit, plan=plan),
        in_specs=[vmem] * 16,
        out_specs=[vmem] * len(shapes),
        out_shape=shapes,
        scratch_shapes=[
            pltpu.VMEM((clips * span, width), BF),
            pltpu.VMEM((clips * span, model), BF),
            pltpu.VMEM((chunks, outers, 4, shard_rows, cols), BF),
            pltpu.VMEM((chunks, 3, outers, shard_rows, cols), BF),
            pltpu.VMEM((chunks, outers, shard_rows, cols), BF),
            pltpu.VMEM((chunks, outers, shard_rows, cols), BF),
            pltpu.VMEM((devices, block, LANES), F32),
            pltpu.VMEM((devices, block, LANES), F32),
            pltpu.VMEM((devices, block, LANES), F32),
            pltpu.VMEM((clips, rows, model), BF),
            pltpu.VMEM((clips, rows, model), BF),
            dma((2, clips)),
            dma((2, chunks, 3)),
            dma((2, chunks, outers)),
            dma((2, devices)),
            dma((2, devices)),
        ],
        compiler_params=pltpu.CompilerParams(
            collective_id=0, has_side_effects=True, vmem_limit_bytes=VMEM_LIMIT
        ),
        name="tail_gradients",
    )(
        own, recv, x, middle_grad, weight, gain, shift, taps, pool_gain, pool_shift, bias_grad,
        hot, space_hot, squeeze, vectors, up_bias,
    )


def layer_norm(values, gain_row, shift_row):
    average = jnp.mean(values, axis=-1, keepdims=True)
    centred = values - average
    variance = jnp.mean(centred * centred, axis=-1, keepdims=True)
    return centred * lax.rsqrt(variance + 1e-06) * gain_row + shift_row


def exact_gelu(values):
    return jax.nn.gelu(values, approximate=False)


def swap(value, axis):
    return lax.ppermute(value, axis, [(0, 1), (1, 0)])


def head_total(portion):
    low = portion.astype(BF)
    return low.astype(F32) + swap(low, "head").astype(F32)


def precise(pattern, *operands):
    return jnp.einsum(pattern, *operands, precision=lax.Precision.HIGHEST)


def split_groups(value, which, axis):
    half = value.shape[axis] // 2
    low = lax.slice_in_dim(value, 0, half, axis=axis)
    high = lax.slice_in_dim(value, half, None, axis=axis)
    first = which == 0
    return jnp.where(first, low, high), jnp.where(first, high, low)


def join_groups(own, peer, which, axis):
    first = which == 0
    return jnp.concatenate([jnp.where(first, own, peer), jnp.where(first, peer, own)], axis=axis)


def time_choices(stride_group, memory_place, which, own, table_rows):
    local = jnp.arange(own, dtype=jnp.int32)
    times = jnp.concatenate([which * own + local, (1 - which) * own + local])
    stride = jnp.left_shift(jnp.int32(2), stride_group)[:, None, None]
    offset = 8 * (FRAMES - 1)
    current = stride * (times[None, :, None] - times[None, None, :]) + offset
    first = memory_place[:, np.array([2, 0, 3, 1])]
    second = memory_place[:, np.array([3, 1, 2, 0])]
    places = jnp.where(which == 0, first, second)
    memory = stride * times[None, :, None] + places[:, None, :] + offset
    chosen = jnp.concatenate([current, memory], axis=2)
    return (chosen[..., None] == jnp.arange(table_rows, dtype=jnp.int32)).astype(F32)


def space_choices():
    places = np.arange(SIDE)
    offsets = places[:, None] - places[None, :] + SIDE - 1
    hot = offsets.reshape(-1)[:, None] == np.arange(2 * SIDE - 1)[None, :]
    return jnp.asarray(hot.astype(np.float32))


def space_sums():
    spans = 2 * SIDE - 1
    hot = np.zeros((32, BIAS_COLS), np.float32)
    for axis in range(2):
        for query in range(SIDE):
            for key in range(SIDE):
                col = SPACE_AT + axis * CELLS + query * SIDE + key
                hot[axis * spans + query - key + SIDE - 1, col] = 1.0
    return hot


def wide_rows(rows, heads):
    count, members, unit = rows.shape
    padded = jnp.pad(rows, ((0, 0), (0, 0), (0, LANES - unit)))
    spread = jnp.broadcast_to(padded[:, :, None], (count, members, heads, LANES))
    return spread.reshape(count, members * heads * LANES)


def local(
    clips_in,
    cached_kv,
    old_memory,
    stride_group,
    memory_place,
    norm_gain,
    norm_shift,
    qkv_weight,
    qkv_shift,
    pool_kernel,
    pool_gain,
    pool_shift,
    squeeze_kernel,
    time_table,
    space_tables,
    proj_weight,
    out_shift,
    up_weight,
    up_shift,
    down_weight,
    cotangent,
):
    clip_count, rows_clip, model_width = clips_in.shape
    head_width = qkv_weight.shape[2]
    unit = pool_gain.shape[1]
    head_count = head_width // unit
    frame_count = lax.axis_size("frame")
    heads = head_count // frame_count
    own_frames = rows_clip // CELLS
    row_total = clip_count * rows_clip
    hidden_width = up_weight.shape[1]
    group_width = heads * unit
    group_span = FRAMES // MEMF
    scale = unit ** (-0.5)
    both = ("clip", "frame")
    which = lax.axis_index("frame")
    into_np, outof_np = placement(frame_count)
    keys_np, mask_np, pad_np = bias_constants(frame_count)
    consts = (
        jnp.where(which == 0, jnp.asarray(into_np[0], BF), jnp.asarray(into_np[1], BF)),
        jnp.where(which == 0, jnp.asarray(outof_np[0], BF), jnp.asarray(outof_np[1], BF)),
        jnp.asarray(keys_np, BF),
        jnp.asarray(mask_np),
        jnp.asarray(pad_np),
    )

    attn_flat, joined_own, joined_send = project(
        clips_in, qkv_weight.reshape(-1, 3 * head_width), norm_gain[:1], norm_shift[:1],
        qkv_shift.reshape(1, -1), lax.axis_size("clip"),
    )
    shards = jnp.concatenate([proj_weight.T, up_weight, down_weight.T], axis=1)
    rest_full = lax.all_gather(shards, both, axis=0, tiled=True)
    proj_full = rest_full[:, :head_width]
    up_full = rest_full[:, head_width : head_width + hidden_width]
    down_full = rest_full[:, head_width + hidden_width :]

    cached_wide = cached_kv.astype(F32).reshape(
        clip_count, group_span, CELLS, 2, head_count, unit
    )
    squeezed = precise("cjsxnd,xjd->csxnd", cached_wide, squeeze_kernel).astype(BF)
    memory_rows = jnp.concatenate(
        [squeezed.reshape(clip_count, CELLS, 2, head_width), old_memory], axis=1
    )
    mem_own, mem_send = split_groups(memory_rows, which, 3)
    mem_own = mem_own.reshape(clip_count, -1, 2 * group_width)
    mem_send = mem_send.reshape(clip_count, -1, 2 * group_width)

    time_hot = time_choices(stride_group, memory_place, which, own_frames, time_table.shape[0])
    time_rows = precise("ctkr,rd->ctkd", time_hot, time_table).reshape(clip_count, -1, unit)
    space_hot = space_choices()
    space_rows = precise("pr,xrd->xpd", space_hot, space_tables).reshape(2 * CELLS, unit)
    bias = jnp.zeros((clip_count, BIAS_COLS, LANES), F32)
    bias = bias.at[:, : time_rows.shape[1], :unit].set(time_rows)
    bias = bias.at[:, SPACE_AT : SPACE_AT + 2 * CELLS, :unit].set(space_rows[None])
    bias = bias * (1.0 / scale)
    taps = wide_rows(pool_kernel.transpose(1, 0, 2), heads)
    gains = wide_rows(pool_gain[None], heads)
    shifts = wide_rows(pool_shift[None], heads)

    inputs_wide = clips_in.reshape(row_total, model_width).astype(F32)
    normed_one, norm_one_back = jax.vjp(layer_norm, inputs_wide, norm_gain[0], norm_shift[0])
    rounded_one = normed_one.astype(BF)
    forward = attention_forward(
        joined_own, joined_send, mem_own, mem_send, consts, taps, gains, shifts, bias, scale, unit
    )
    attended_own, attended_peer = forward[:2]
    saved = forward[2:]
    attended = join_groups(attended_own, attended_peer, which, 2).reshape(row_total, head_width)
    branch = head_total(dot_f32(attended, proj_full, ((1,), (1,)))) + out_shift[0]
    middle = inputs_wide + branch
    normed_two, norm_two_back = jax.vjp(layer_norm, middle, norm_gain[1], norm_shift[1])
    rounded_two = normed_two.astype(BF)
    hidden = jnp.dot(rounded_two, up_full, preferred_element_type=F32) + up_shift
    activated, gelu_back = jax.vjp(exact_gelu, hidden)
    activated_low = activated.astype(BF)
    block_out = (
        middle + head_total(dot_f32(activated_low, down_full, ((1,), (1,)))) + out_shift[1]
    )
    block_out = block_out.astype(BF).reshape(clip_count, rows_clip, model_width)

    cotan_low = cotangent.reshape(row_total, model_width)
    cotan_wide = cotan_low.astype(F32)
    active_grad = jnp.dot(cotan_low, down_full, preferred_element_type=F32)
    hidden_grad = gelu_back(active_grad)[0].astype(BF)
    grad_up_bias = jnp.sum(hidden_grad.astype(F32), axis=0)
    normed_two_grad = head_total(dot_f32(hidden_grad, up_full, ((1,), (1,))))
    middle_norm_grad, gain_two_grad, shift_two_grad = norm_two_back(normed_two_grad)
    middle_grad = cotan_wide + middle_norm_grad
    branch_grad = middle_grad.astype(BF)
    attended_grad = jnp.dot(branch_grad, proj_full, preferred_element_type=F32).astype(BF)
    attended_grad = attended_grad.reshape(clip_count, rows_clip, head_width)
    grad_rest = jnp.concatenate(
        [
            dot_f32(branch_grad, attended, ((0,), (0,))).astype(BF),
            dot_f32(rounded_two, hidden_grad, ((0,), (0,))).astype(BF),
            dot_f32(cotan_low, activated_low, ((0,), (0,))).astype(BF),
        ],
        axis=1,
    )
    grad_rest, attended_grad = lax.optimization_barrier((grad_rest, attended_grad))
    rest_shard = lax.psum_scatter(grad_rest, both, scatter_dimension=0, tiled=True).astype(F32)

    attended_grad_own, attended_grad_send = split_groups(attended_grad, which, 2)
    backward = attention_backward(
        attended_grad_own, attended_grad_send, consts, taps, gains, bias, saved, scale, unit
    )
    grad_own, grad_peer, mem_grad_own, mem_grad_peer = backward[:4]
    taps_grad, pool_gain_grad, pool_shift_grad, bias_grad = backward[4:]

    mem_grads = [
        part[:, :CELLS].reshape(clip_count, CELLS, 2, heads, LANES)[..., :unit]
        for part in (mem_grad_own, mem_grad_peer)
    ]
    squeezed_grads = join_groups(mem_grads[0], mem_grads[1], which, 3).astype(F32)
    grad_squeeze = precise("cjsxnd,csxnd->xjd", cached_wide, squeezed_grads)
    time_count = time_rows.shape[1]
    hot = time_hot.reshape(clip_count, time_count, -1).astype(BF)
    hot = jnp.pad(hot, ((0, 0), (0, 0), (0, -hot.shape[2] % LANES)))
    vectors = jnp.stack(
        [gain_two_grad, shift_two_grad, jnp.sum(middle_grad, axis=0), jnp.sum(cotan_wide, axis=0)]
    )
    devices = lax.axis_size("clip") * frame_count * lax.axis_size("head")
    (
        grad_in, qkv_shard, gain_sums, shift_sums, out_sums, qkv_bias_sum, up_bias_sum, kernel_sum,
        pool_gain_sum, pool_shift_sum, squeeze_sum, time_sum, space_sum,
    ) = tail(
        grad_own, grad_peer, clips_in, middle_grad.reshape(clips_in.shape), attn_flat,
        norm_gain[:1], norm_shift[:1], taps_grad, pool_gain_grad, pool_shift_grad, bias_grad, hot,
        jnp.asarray(space_sums(), BF), grad_squeeze.reshape(-1, unit), vectors,
        grad_up_bias.reshape(1, -1), lax.axis_size("clip"), devices, unit, time_table.shape[0],
    )
    return (
        block_out,
        grad_in,
        gain_sums,
        shift_sums,
        qkv_shard.reshape(-1, 3, head_width),
        qkv_bias_sum,
        kernel_sum,
        pool_gain_sum,
        pool_shift_sum,
        squeeze_sum.reshape(squeeze_kernel.shape),
        time_sum,
        space_sum.reshape(space_tables.shape),
        rest_shard[:, :head_width].T,
        out_sums,
        rest_shard[:, head_width : head_width + hidden_width],
        up_bias_sum.reshape(-1),
        rest_shard[:, head_width + hidden_width :].T,
    )


def solution(mesh):
    return jax.shard_map(
        local,
        mesh=mesh,
        in_specs=(
            P("clip", "frame", None),
            P("clip", "frame", None, "head"),
            P("clip", "frame", None, "head"),
            P("clip"),
            P("clip", None),
            P(),
            P(),
            P(("clip", "frame"), None, "head"),
            P(None, "head"),
            P(),
            P(),
            P(),
            P(),
            P(),
            P(),
            P("head", ("clip", "frame")),
            P(),
            P(("clip", "frame"), "head"),
            P("head"),
            P("head", ("clip", "frame")),
            P("clip", "frame", None),
        ),
        out_specs=(
            P("clip", "frame", None),
            P("clip", "frame", None),
            P(),
            P(),
            P(("clip", "frame"), None, "head"),
            P(None, "head"),
            P(),
            P(),
            P(),
            P(),
            P(),
            P(),
            P("head", ("clip", "frame")),
            P(),
            P(("clip", "frame"), "head"),
            P("head"),
            P("head", ("clip", "frame")),
        ),
        check_vma=False,
    )
```

```python
from functools import partial

import jax
import jax.numpy as jnp
import numpy as np
from jax import lax
from jax.experimental import pallas as pl
from jax.experimental.pallas import tpu as pltpu
from jax.sharding import PartitionSpec as P

FRAMES = 8
MEMF = 2
SIDE = 7
CELLS = SIDE * SIDE
LANES = 128
HALF = 208
QROWS = 2 * HALF
GRID_ROWS = FRAMES * SIDE * 8
MEM_AT = QROWS
MEM_PAD = 112
MEM_BACK = 64
KROWS = 640
BIAS_COLS = 256
SPACE_AT = 128
PAD_LANE = 127
BF = jnp.bfloat16
F32 = jnp.float32
VMEM_LIMIT = 60 * 1024 * 1024
MESH_ID = pl.DeviceIdType.MESH


def dot_f32(a, b, dims):
    return lax.dot_general(a, b, (dims, ((), ())), preferred_element_type=F32)


def frame_order(first, own):
    rest = [t for t in range(FRAMES) if not first * own <= t < (first + 1) * own]
    return list(range(first * own, (first + 1) * own)) + rest


def placement(frame_count):
    own = FRAMES // frame_count
    into = np.zeros((frame_count, GRID_ROWS, QROWS), np.float32)
    for first in range(frame_count):
        for slot, frame in enumerate(frame_order(first, own)):
            base = (slot // own) * HALF + (slot % own) * CELLS
            for high in range(SIDE):
                for wide in range(SIDE):
                    row = (frame * SIDE + high) * 8 + wide
                    into[first, row, base + high * SIDE + wide] = 1.0
    return into, np.ascontiguousarray(into.transpose(0, 2, 1))


def bias_constants(frame_count):
    own = FRAMES // frame_count
    frames_all = FRAMES + 2 * MEMF
    keys = np.zeros((BIAS_COLS, KROWS), np.float32)
    valid = np.zeros((KROWS,), bool)

    def mark(col, slot, high, wide):
        valid[col] = True
        for query in range(FRAMES):
            keys[query * frames_all + slot, col] = 1.0
        for place in range(SIDE):
            keys[SPACE_AT + place * SIDE + high, col] = 1.0
            keys[SPACE_AT + CELLS + place * SIDE + wide, col] = 1.0

    mask = np.zeros((QROWS, BIAS_COLS), np.float32)
    for slot in range(FRAMES):
        base = (slot // own) * HALF + (slot % own) * CELLS
        for high in range(SIDE):
            for wide in range(SIDE):
                row = base + high * SIDE + wide
                mark(row, slot, high, wide)
                mask[row, slot * frames_all : (slot + 1) * frames_all] = 1.0
                mask[row, SPACE_AT + high * SIDE : SPACE_AT + (high + 1) * SIDE] = 1.0
                low = SPACE_AT + CELLS + wide * SIDE
                mask[row, low : low + SIDE] = 1.0
    for group in range(2):
        for inner in range(MEMF):
            slot = FRAMES + group * MEMF + inner
            for high in range(SIDE):
                for wide in range(SIDE):
                    col = MEM_AT + group * MEM_PAD + inner * CELLS + high * SIDE + wide
                    mark(col, slot, high, wide)
    keys[PAD_LANE, ~valid] = -1e9
    pad_row = np.zeros((1, BIAS_COLS), np.float32)
    pad_row[0, PAD_LANE] = 1.0
    return keys, mask, pad_row


def spread_heads(source, target, rows_at, units, unit, first=0):
    count = source.shape[0]
    for index in range(units):
        at = (first + index) * unit
        target[rows_at : rows_at + count, index * LANES : index * LANES + unit] = source[
            :, at : at + unit
        ]


def load_shifted(field, shifted):
    grid = field.reshape(FRAMES, SIDE, 8, field.shape[-1])
    flat = field.reshape(FRAMES * SIDE, 8, field.shape[-1])
    shifted[1, 1 : FRAMES + 1, 1 : SIDE + 1] = grid
    shifted[0, 1 : FRAMES + 1, 1 : SIDE + 1] = pltpu.roll(flat, 1, 1).reshape(grid.shape)
    shifted[2, 1 : FRAMES + 1, 1 : SIDE + 1] = pltpu.roll(flat, 7, 1).reshape(grid.shape)


def convolve(shifted, taps, target, flip):
    tiles = target.shape[-1] // LANES

    def step(index, carry):
        frame = index // tiles
        lanes = pl.ds(pl.multiple_of((index % tiles) * LANES, LANES), LANES)
        total = jnp.zeros((SIDE, 8, LANES), F32)
        for i in range(3):
            for k in range(3):
                rows = shifted[k, frame + i, :, :, lanes]
                for j in range(3):
                    if flip:
                        tap = (2 - i) * 9 + (2 - j) * 3 + (2 - k)
                    else:
                        tap = i * 9 + j * 3 + k
                    total = total + rows[j : j + SIDE] * taps[tap, :, lanes][None]
        target[frame, :, :, lanes] = total
        return carry

    lax.fori_loop(0, FRAMES * tiles, step, 0)


def tap_grads(shifted, grads, target):
    tiles = target.shape[-1] // LANES
    for i in range(3):

        def step(index, carry, i=i):
            lanes = pl.ds(pl.multiple_of(index * LANES, LANES), LANES)

            def inner(frame, sums):
                centre = grads[frame + 1, :, :, lanes]
                new = []
                for j in range(3):
                    for k in range(3):
                        rows = shifted[k, frame + i, j : j + SIDE, :, lanes]
                        new.append(sums[j * 3 + k] + jnp.sum(rows * centre[1 : SIDE + 1], axis=0))
                return tuple(new)

            start = tuple(jnp.zeros((8, LANES), F32) for _ in range(9))
            sums = lax.fori_loop(0, FRAMES, inner, start)
            for tap in range(9):
                target[i * 9 + tap, :, lanes] += sums[tap]
            return carry

        lax.fori_loop(0, tiles, step, 0)


def head_stats(values, unit):
    average = jnp.sum(values, axis=-1, keepdims=True) * (1.0 / unit)
    lane = lax.broadcasted_iota(jnp.int32, values.shape, 1)
    centred = jnp.where(lane < unit, values - average, 0.0)
    variance = jnp.sum(centred * centred, axis=-1, keepdims=True) * (1.0 / unit)
    return centred, lax.rsqrt(variance + 1e-06)


def frame_partner():
    return (lax.axis_index("clip"), 1 - lax.axis_index("frame"), lax.axis_index("head"))


def partner_copy(source, target, send_sem, recv_sem):
    return pltpu.make_async_remote_copy(
        src_ref=source, dst_ref=target, send_sem=send_sem, recv_sem=recv_sem,
        device_id=frame_partner(), device_id_type=MESH_ID,
    )


def side_partner():
    clip = lax.axis_index("clip")
    across = (clip // 2) * 2 + 1 - clip % 2
    return (across, lax.axis_index("frame"), lax.axis_index("head"))


def side_copy(source, target, send_sem, recv_sem):
    return pltpu.make_async_remote_copy(
        src_ref=source, dst_ref=target, send_sem=send_sem, recv_sem=recv_sem,
        device_id=side_partner(), device_id_type=MESH_ID,
    )


def greet_partner():
    barrier = pltpu.get_barrier_semaphore()
    pl.semaphore_signal(barrier, inc=1, device_id=frame_partner(), device_id_type=MESH_ID)
    pl.semaphore_wait(barrier, 1)


def forward_kernel(
    own_ref, send_ref, mem_own_ref, mem_send_ref, into_ref, outof_ref, taps_ref, gain_ref,
    shift_ref, bias_ref, keyhot_ref, mask_ref, pad_ref,
    out_own, out_recv, packed_out, q_out, k_out, v_out, p_out, c_out,
    shifted, taps, peer, mem_peer, out_send, joined_sems, mem_sems, out_sems,
    *, heads, unit, scale,
):
    units = 3 * heads
    own_rows = own_ref.shape[1]
    clip = pl.program_id(0)
    clips = peer.shape[0]

    def joined_copy(index):
        return partner_copy(
            send_ref.at[index], peer.at[index], joined_sems.at[0, index], joined_sems.at[1, index]
        )

    def out_copy(index):
        return partner_copy(
            out_send.at[index], out_recv.at[index], out_sems.at[0, index], out_sems.at[1, index]
        )

    mem_copy = partner_copy(mem_send_ref, mem_peer, mem_sems.at[0], mem_sems.at[1])

    @pl.when(clip == 0)
    def _():
        greet_partner()
        for index in range(clips):
            joined_copy(index).start()
            if index == 0:
                mem_copy.start()
        shifted[...] = jnp.zeros_like(shifted)
        for tap in range(27):
            taps[tap] = jnp.broadcast_to(taps_ref[tap : tap + 1], taps.shape[1:])

    packed = packed_out.at[0]
    packed[...] = jnp.zeros(packed.shape, BF)
    spread_heads(own_ref.at[0], packed, 0, units, unit)
    joined_copy(clip).wait_recv()
    spread_heads(peer.at[clip], packed, HALF, units, unit)
    field = dot_f32(into_ref[...], packed[...], ((1,), (0,)))
    load_shifted(field, shifted)
    conv = c_out.at[0]
    convolve(shifted, taps, conv, False)

    @pl.when(clip == 0)
    def _():
        mem_copy.wait_recv()

    k_out[0, MEM_AT:, :] = jnp.zeros((KROWS - MEM_AT, heads * LANES), BF)
    v_out[0, MEM_AT:, :] = jnp.zeros((KROWS - MEM_AT, heads * LANES), BF)
    spread_heads(mem_own_ref.at[0], k_out.at[0], MEM_AT, heads, unit, 0 * heads)
    spread_heads(mem_own_ref.at[0], v_out.at[0], MEM_AT, heads, unit, 1 * heads)
    spread_heads(mem_peer.at[clip], k_out.at[0], MEM_AT + MEM_PAD, heads, unit, 0 * heads)
    spread_heads(mem_peer.at[clip], v_out.at[0], MEM_AT + MEM_PAD, heads, unit, 1 * heads)
    for index in range(units):
        lanes = slice(index * LANES, (index + 1) * LANES)
        block = conv[:, :, :, lanes].reshape(GRID_ROWS, LANES)
        centred, rate = head_stats(block, unit)
        normal = centred * rate * gain_ref[:, lanes] + shift_ref[:, lanes]
        rows = dot_f32(outof_ref[...], normal.astype(BF), ((1,), (0,))).astype(BF)
        target = (q_out, k_out, v_out)[index // heads]
        local = slice((index % heads) * LANES, (index % heads + 1) * LANES)
        target[0, 0:QROWS, local] = rows

    bias = bias_ref[0]
    bias_high = bias.astype(BF)
    bias_low = (bias - bias_high.astype(F32)).astype(BF)
    for head in range(heads):
        lanes = slice(head * LANES, (head + 1) * LANES)
        keys = k_out[0, :, lanes]
        values = v_out[0, :, lanes]
        for half in range(2):
            rows = slice(half * HALF, (half + 1) * HALF)
            query = q_out[0, rows, lanes]
            table = dot_f32(query, bias_high, ((1,), (1,))) + dot_f32(query, bias_low, ((1,), (1,)))
            table = table * mask_ref[rows, :] + pad_ref[...]
            table_high = table.astype(BF)
            table_low = (table - table_high.astype(F32)).astype(BF)
            scores = dot_f32(query, keys, ((1,), (1,)))
            scores = scores + dot_f32(table_high, keyhot_ref[...], ((1,), (0,)))
            scores = scores + dot_f32(table_low, keyhot_ref[...], ((1,), (0,)))
            top = jnp.max(scores, axis=-1, keepdims=True)
            weights = jnp.exp((scores - top) * scale)
            total = jnp.sum(weights, axis=-1, keepdims=True)
            probs = (weights * (1.0 / total)).astype(BF)
            p_out[0, head, rows, :] = probs
            mixed = dot_f32(probs, values, ((1,), (0,))) + query.astype(F32)
            target = (out_own.at[0], out_send.at[clip])[half]
            target[:, head * unit : (head + 1) * unit] = mixed[:own_rows, :unit].astype(BF)

    out_copy(clip).start()

    @pl.when(clip == clips - 1)
    def _():
        mem_copy.wait_send()
        for index in range(clips):
            joined_copy(index).wait_send()
            out_copy(index).wait()


def backward_kernel(
    packed_ref, grad_own_ref, grad_send_ref, rest_ref, into_ref, outof_ref, taps_ref, gain_ref,
    bias_ref, keyhot_ref, mask_ref, q_ref, k_ref, v_ref, p_ref, c_ref,
    out_own, out_recv, mem_own, mem_recv, taps_out, gain_out, shift_out, bias_out, rest_out,
    shifted, taps, grads, spread, pooled, peer, out_send, mem_send, rest_own, rest_side, rest_send,
    rest_peer, grad_sems, out_sems, mem_sems, own_sems, side_sems, rest_sems,
    *, heads, unit, scale,
):
    units = 3 * heads
    own_rows = grad_own_ref.shape[1]
    clip = pl.program_id(0)
    clips = peer.shape[0]

    def grad_copy(index):
        return partner_copy(
            grad_send_ref.at[index], peer.at[index], grad_sems.at[0, index], grad_sems.at[1, index]
        )

    def out_copy(index):
        return partner_copy(
            out_send.at[index], out_recv.at[index], out_sems.at[0, index], out_sems.at[1, index]
        )

    def mem_copy(index):
        return partner_copy(
            mem_send.at[index], mem_recv.at[index], mem_sems.at[0, index], mem_sems.at[1, index]
        )

    chunks, outers, _, _, cols = rest_own.shape
    side_at = lax.axis_index("clip") % 2
    frame = lax.axis_index("frame")

    def rest_at(side, chunk):
        return rest_ref.at[:, pl.ds(side * 2, 2), :, pl.ds(chunk * cols, cols)]

    def own_copy(chunk):
        return pltpu.make_async_copy(
            rest_at(side_at, chunk), rest_own.at[chunk], own_sems.at[chunk]
        )

    def over_copy(chunk):
        return side_copy(
            rest_at(1 - side_at, chunk), rest_side.at[chunk], side_sems.at[0, chunk],
            side_sems.at[1, chunk],
        )

    def rest_copy(chunk):
        return partner_copy(
            rest_send.at[chunk], rest_peer.at[chunk], rest_sems.at[0, chunk],
            rest_sems.at[1, chunk],
        )

    def pass_on(chunk):
        own_copy(chunk).wait()
        over_copy(chunk).wait_recv()

        def add(index):
            def total(part):
                first = rest_own[chunk, index, part].astype(F32)
                return (first + rest_side[chunk, index, part].astype(F32)).astype(BF)

            rest_send[chunk, index] = total(1 - frame)
            rest_out[index, :, chunk * cols : (chunk + 1) * cols] = total(frame)

        each(0, outers, add)
        rest_copy(chunk).start()

    @pl.when(clip == 0)
    def _():
        barrier = pltpu.get_barrier_semaphore()
        for device in (frame_partner(), side_partner()):
            pl.semaphore_signal(barrier, inc=1, device_id=device, device_id_type=MESH_ID)
        pl.semaphore_wait(barrier, 2)
        for index in range(clips):
            grad_copy(index).start()
        for chunk in range(chunks):
            over_copy(chunk).start()
            own_copy(chunk).start()
        shifted[...] = jnp.zeros_like(shifted)
        grads[...] = jnp.zeros_like(grads)
        spread[...] = jnp.zeros_like(spread)
        taps_out[...] = jnp.zeros_like(taps_out)
        gain_out[...] = jnp.zeros_like(gain_out)
        shift_out[...] = jnp.zeros_like(shift_out)
        for tap in range(27):
            taps[tap] = jnp.broadcast_to(taps_ref[tap : tap + 1], taps.shape[1:])

    for chunk in range(chunks):

        @pl.when(clip == jnp.minimum(chunk + 2, clips - 1))
        def _():
            pass_on(chunk)

    load_shifted(dot_f32(into_ref[...], packed_ref[0], ((1,), (0,))), shifted)
    spread_heads(grad_own_ref.at[0], spread, 0, heads, unit)
    grad_copy(clip).wait_recv()
    spread_heads(peer.at[clip], spread, HALF, heads, unit)
    bias_low = bias_ref[0].astype(BF)
    bias_sum = jnp.zeros((BIAS_COLS, LANES), F32)
    for head in range(heads):
        lanes = slice(head * LANES, (head + 1) * LANES)
        keys = k_ref[0, :, lanes]
        values = v_ref[0, :, lanes]
        keys_grad = jnp.zeros((KROWS, LANES), F32)
        values_grad = jnp.zeros((KROWS, LANES), F32)
        for half in range(2):
            rows = slice(half * HALF, (half + 1) * HALF)
            query = q_ref[0, rows, lanes]
            out_grad = spread[rows, lanes]
            probs = p_ref[0, head, rows, :]
            wide = probs.astype(F32)
            probs_grad = dot_f32(out_grad, values, ((1,), (1,)))
            weighted = wide * probs_grad
            shared = jnp.sum(weighted, axis=-1, keepdims=True)
            score_grad = (weighted - wide * shared).astype(BF)
            values_grad = values_grad + dot_f32(probs, out_grad, ((0,), (0,)))
            keys_grad = keys_grad + dot_f32(score_grad, query, ((0,), (0,)))
            table_grad = dot_f32(score_grad, keyhot_ref[...], ((1,), (1,))) * mask_ref[rows, :]
            table_low = table_grad.astype(BF)
            query_grad = dot_f32(score_grad, keys, ((1,), (0,)))
            query_grad = query_grad + dot_f32(table_low, bias_low, ((1,), (0,)))
            query_grad = query_grad * scale + out_grad.astype(F32)
            pooled[rows, lanes] = query_grad.astype(BF)
            bias_sum = bias_sum + dot_f32(table_low, query, ((0,), (0,)))
        keys_grad = (keys_grad * scale).astype(BF)
        values_grad = values_grad.astype(BF)
        for member, part in enumerate((keys_grad, values_grad)):
            at = ((member + 1) * heads + head) * LANES
            pooled[:, at : at + LANES] = part[:QROWS]
            at = (member * heads + head) * LANES
            low = MEM_AT + MEM_PAD
            mem_own[0, :, at : at + LANES] = part[MEM_AT : MEM_AT + MEM_BACK]
            mem_send[clip, :, at : at + LANES] = part[low : low + MEM_BACK]
    bias_out[0] = bias_sum
    mem_copy(clip).start()

    for index in range(units):
        lanes = slice(index * LANES, (index + 1) * LANES)
        incoming = dot_f32(into_ref[...], pooled[:, lanes], ((1,), (0,)))
        block = c_ref[0, :, :, :, lanes].reshape(GRID_ROWS, LANES)
        centred, rate = head_stats(block, unit)
        normal = centred * rate
        product = incoming * normal
        gain_out[:, lanes] += jnp.sum(product, axis=0, keepdims=True)
        shift_out[:, lanes] += jnp.sum(incoming, axis=0, keepdims=True)
        inner = incoming * gain_ref[:, lanes]
        mean_inner = jnp.sum(inner, axis=-1, keepdims=True) * (1.0 / unit)
        mean_both = jnp.sum(inner * normal, axis=-1, keepdims=True) * (1.0 / unit)
        lane = lax.broadcasted_iota(jnp.int32, block.shape, 1)
        result = rate * (inner - mean_inner - normal * mean_both)
        result = jnp.where(lane < unit, result, 0.0)
        flat = result.reshape(FRAMES * SIDE, 8, LANES)
        shape = (FRAMES, SIDE, 8, LANES)
        grads[1, 1 : FRAMES + 1, 1 : SIDE + 1, :, lanes] = flat.reshape(shape)
        grads[0, 1 : FRAMES + 1, 1 : SIDE + 1, :, lanes] = pltpu.roll(flat, 1, 1).reshape(shape)
        grads[2, 1 : FRAMES + 1, 1 : SIDE + 1, :, lanes] = pltpu.roll(flat, 7, 1).reshape(shape)

    tap_grads(shifted, grads.at[1], taps_out)
    conv = shifted.at[1, 1 : FRAMES + 1, 1 : SIDE + 1]
    convolve(grads, taps, conv, True)
    for index in range(units):
        lanes = slice(index * LANES, (index + 1) * LANES)
        block = shifted[1, 1 : FRAMES + 1, 1 : SIDE + 1, :, lanes].reshape(GRID_ROWS, LANES)
        rows = dot_f32(outof_ref[...], block.astype(BF), ((1,), (0,))).astype(BF)
        local = slice(index * unit, (index + 1) * unit)
        out_own[0, :, local] = rows[:own_rows, :unit]
        out_send[clip, :, local] = rows[HALF : HALF + own_rows, :unit]
    out_copy(clip).start()

    @pl.when(clip == clips - 1)
    def _():
        for index in range(clips):
            grad_copy(index).wait_send()
            mem_copy(index).wait()
            out_copy(index).wait()
        for chunk in range(chunks):
            over_copy(chunk).wait_send()
            rest_copy(chunk).wait()

            def add(index):
                lanes = slice(chunk * cols, (chunk + 1) * cols)
                total = rest_out[index, :, lanes].astype(F32)
                total = total + rest_peer[chunk, index].astype(F32)
                rest_out[index, :, lanes] = total.astype(BF)

            each(0, outers, add)


def whole_spec(shape):
    return pl.BlockSpec(shape, lambda clip: (0,) * len(shape))


def clip_spec(shape):
    return pl.BlockSpec((1,) + shape, lambda clip: (clip,) + (0,) * len(shape))


def any_spec():
    return pl.BlockSpec(memory_space=pl.ANY)


def attention_forward(own, send, mem_own, mem_send, consts, taps, gains, shifts, bias, scale, unit):
    clips, rows, width = own.shape
    heads = width // (3 * unit)
    into, outof, keyhot, mask, pad_row = consts
    wide = 3 * heads * LANES
    mem_shape = mem_own.shape[1:]
    out = jax.ShapeDtypeStruct
    dma = pltpu.SemaphoreType.DMA
    return pl.pallas_call(
        partial(forward_kernel, heads=heads, unit=unit, scale=scale),
        grid=(clips,),
        in_specs=[
            clip_spec((rows, width)),
            any_spec(),
            clip_spec(mem_shape),
            any_spec(),
            whole_spec((GRID_ROWS, QROWS)),
            whole_spec((QROWS, GRID_ROWS)),
            whole_spec((27, wide)),
            whole_spec((1, wide)),
            whole_spec((1, wide)),
            clip_spec((BIAS_COLS, LANES)),
            whole_spec((BIAS_COLS, KROWS)),
            whole_spec((QROWS, BIAS_COLS)),
            whole_spec((1, BIAS_COLS)),
        ],
        out_specs=[
            clip_spec((rows, heads * unit)),
            any_spec(),
            clip_spec((QROWS, wide)),
            clip_spec((QROWS, heads * LANES)),
            clip_spec((KROWS, heads * LANES)),
            clip_spec((KROWS, heads * LANES)),
            clip_spec((heads, QROWS, KROWS)),
            clip_spec((FRAMES, SIDE, 8, wide)),
        ],
        scratch_shapes=[
            pltpu.VMEM((3, FRAMES + 2, SIDE + 2, 8, wide), F32),
            pltpu.VMEM((27, 8, wide), F32),
            pltpu.VMEM((clips, rows, width), BF),
            pltpu.VMEM((clips,) + mem_shape, BF),
            pltpu.VMEM((clips, rows, heads * unit), BF),
            dma((2, clips)),
            dma((2,)),
            dma((2, clips)),
        ],
        out_shape=[
            out((clips, rows, heads * unit), BF),
            out((clips, rows, heads * unit), BF),
            out((clips, QROWS, wide), BF),
            out((clips, QROWS, heads * LANES), BF),
            out((clips, KROWS, heads * LANES), BF),
            out((clips, KROWS, heads * LANES), BF),
            out((clips, heads, QROWS, KROWS), BF),
            out((clips, FRAMES, SIDE, 8, wide), F32),
        ],
        compiler_params=pltpu.CompilerParams(
            collective_id=1, has_side_effects=True, vmem_limit_bytes=VMEM_LIMIT
        ),
        name="pooled_attention_forward",
    )(own, send, mem_own, mem_send, into, outof, taps, gains, shifts, bias, keyhot, mask, pad_row)


def attention_backward(grad_own, grad_send, rest, consts, taps, gains, bias, saved, scale, unit):
    clips, rows, width = grad_own.shape
    heads = width // unit
    into, outof, keyhot, mask, pad_row = consts
    wide = 3 * heads * LANES
    joined_width = 3 * heads * unit
    outers, _, shard_rows, rest_width = rest.shape
    chunks = 3
    cols = rest_width // chunks
    out = jax.ShapeDtypeStruct
    dma = pltpu.SemaphoreType.DMA
    return pl.pallas_call(
        partial(backward_kernel, heads=heads, unit=unit, scale=scale),
        grid=(clips,),
        in_specs=[
            clip_spec((QROWS, wide)),
            clip_spec((rows, width)),
            any_spec(),
            any_spec(),
            whole_spec((GRID_ROWS, QROWS)),
            whole_spec((QROWS, GRID_ROWS)),
            whole_spec((27, wide)),
            whole_spec((1, wide)),
            clip_spec((BIAS_COLS, LANES)),
            whole_spec((BIAS_COLS, KROWS)),
            whole_spec((QROWS, BIAS_COLS)),
            clip_spec((QROWS, heads * LANES)),
            clip_spec((KROWS, heads * LANES)),
            clip_spec((KROWS, heads * LANES)),
            clip_spec((heads, QROWS, KROWS)),
            clip_spec((FRAMES, SIDE, 8, wide)),
        ],
        out_specs=[
            clip_spec((rows, joined_width)),
            any_spec(),
            clip_spec((MEM_BACK, 2 * heads * LANES)),
            any_spec(),
            whole_spec((27, 8, wide)),
            whole_spec((1, wide)),
            whole_spec((1, wide)),
            clip_spec((BIAS_COLS, LANES)),
            whole_spec((outers, shard_rows, rest_width)),
        ],
        scratch_shapes=[
            pltpu.VMEM((3, FRAMES + 2, SIDE + 2, 8, wide), F32),
            pltpu.VMEM((27, 8, wide), F32),
            pltpu.VMEM((3, FRAMES + 2, SIDE + 2, 8, wide), F32),
            pltpu.VMEM((QROWS, heads * LANES), BF),
            pltpu.VMEM((QROWS, wide), BF),
            pltpu.VMEM((clips, rows, width), BF),
            pltpu.VMEM((clips, rows, joined_width), BF),
            pltpu.VMEM((clips, MEM_BACK, 2 * heads * LANES), BF),
            pltpu.VMEM((chunks, outers, 2, shard_rows, cols), BF),
            pltpu.VMEM((chunks, outers, 2, shard_rows, cols), BF),
            pltpu.VMEM((chunks, outers, shard_rows, cols), BF),
            pltpu.VMEM((chunks, outers, shard_rows, cols), BF),
            dma((2, clips)),
            dma((2, clips)),
            dma((2, clips)),
            dma((chunks,)),
            dma((2, chunks)),
            dma((2, chunks)),
        ],
        out_shape=[
            out((clips, rows, joined_width), BF),
            out((clips, rows, joined_width), BF),
            out((clips, MEM_BACK, 2 * heads * LANES), BF),
            out((clips, MEM_BACK, 2 * heads * LANES), BF),
            out((27, 8, wide), F32),
            out((1, wide), F32),
            out((1, wide), F32),
            out((clips, BIAS_COLS, LANES), F32),
            out((outers, shard_rows, rest_width), BF),
        ],
        compiler_params=pltpu.CompilerParams(
            collective_id=2, has_side_effects=True, vmem_limit_bytes=VMEM_LIMIT
        ),
        name="pooled_attention_backward",
    )(saved[0], grad_own, grad_send, rest, into, outof, taps, gains, bias, keyhot, mask, *saved[1:])


def row_stats(values):
    width = values.shape[-1]
    centred = values - jnp.sum(values, axis=-1, keepdims=True) * (1.0 / width)
    variance = jnp.sum(centred * centred, axis=-1, keepdims=True) * (1.0 / width)
    return centred, lax.rsqrt(variance + 1e-06)


def each(low, high, act):
    def body(step, carry):
        act(step)
        return carry

    lax.fori_loop(low, high, body, 0)


def project_rows(x, gain, shift, normed):
    def step(clip):
        centred, rate = row_stats(x[clip].astype(F32))
        normed[clip] = (centred * rate * gain[...] + shift[...]).astype(BF)

    each(0, x.shape[0], step)


def project_out(normed, weight, bias, own, send):
    model = normed.shape[2]
    group = own.shape[2] // 3
    first = lax.axis_index("frame") == 0

    def step(clip):
        rows = dot_f32(normed[clip], weight, ((1,), (0,))) + bias[...]
        rows = rows.astype(BF)

        def store(low, high):
            for member in range(3):
                at = 2 * member * group
                local = slice(member * group, (member + 1) * group)
                low[clip, :, local] = rows[:, at : at + group]
                high[clip, :, local] = rows[:, at + group : at + 2 * group]

        @pl.when(first)
        def _():
            store(own, send)

        @pl.when(jnp.logical_not(first))
        def _():
            store(send, own)

    each(0, own.shape[0], step)


def project_kernel(
    x, shard, gain, shift, bias, full, own, send, normed, far_send, far_recv, near_send, near_recv
):
    outers, _, shard_rows, width = full.shape
    clip = lax.axis_index("clip")
    frame = lax.axis_index("frame")
    head = lax.axis_index("head")
    outer, inner = clip // 2, clip % 2
    place = inner * 2 + frame
    barrier = pltpu.get_barrier_semaphore()

    def far_device(step):
        return device_of((outer + step) % outers, inner, frame, head)

    def near_device(step):
        there_inner, there_frame = plane_peer(inner, frame, step)
        return device_of(outer, there_inner, there_frame, head)

    def greet(device):
        pl.semaphore_signal(barrier, inc=1, device_id=device, device_id_type=MESH_ID)

    each(1, outers, lambda step: greet(far_device(step)))
    for step in range(1, 4):
        greet(near_device(step))
    pl.semaphore_wait(barrier, outers - 1 + 3)

    def far_copy(step, at):
        return pltpu.make_async_remote_copy(
            src_ref=shard, dst_ref=full.at[at, place],
            send_sem=far_send.at[step], recv_sem=far_recv.at[step],
            device_id=far_device(step), device_id_type=MESH_ID,
        )

    def near_copy(index, step, source, at):
        return pltpu.make_async_remote_copy(
            src_ref=source, dst_ref=full.at[at, place],
            send_sem=near_send.at[index, step - 1], recv_sem=near_recv.at[index, step - 1],
            device_id=near_device(step), device_id_type=MESH_ID,
        )

    def near_arrival(index, step, at):
        there_inner, there_frame = plane_peer(inner, frame, step)
        return pltpu.make_async_remote_copy(
            src_ref=shard, dst_ref=full.at[at, there_inner * 2 + there_frame],
            send_sem=near_send.at[index, step - 1], recv_sem=near_recv.at[index, step - 1],
            device_id=near_device(step), device_id_type=MESH_ID,
        )

    def origin(step):
        return (outer + outers - step) % outers

    each(1, outers, lambda step: far_copy(step, outer).start())
    for step in range(1, 4):
        near_copy(0, step, shard, outer).start()
    full[outer, place] = shard[...]
    project_rows(x, gain, shift, normed)

    def forward(index):
        far_copy(index, origin(index)).wait_recv()
        for step in range(1, 4):
            near_copy(index, step, full.at[origin(index), place], origin(index)).start()

    each(1, outers, forward)

    def arrive(index):
        for step in range(1, 4):
            near_arrival(index, step, origin(index)).wait_recv()

    each(0, outers, arrive)
    project_out(normed, full[...].reshape(outers * 4 * shard_rows, width), bias, own, send)
    each(1, outers, lambda step: far_copy(step, outer).wait_send())
    for step in range(1, 4):
        near_copy(0, step, shard, outer).wait_send()

    def sent(index):
        for step in range(1, 4):
            near_copy(index, step, full.at[origin(index), place], origin(index)).wait_send()

    each(1, outers, sent)


def project_local_kernel(x, weight, gain, shift, bias, own, send, normed):
    project_rows(x, gain, shift, normed)
    project_out(normed, weight[...], bias, own, send)


def project(x, shard, gain, shift, bias, clip_count):
    clips, rows, model = x.shape
    width = shard.shape[1]
    outers = clip_count // 2
    half = width // 2
    out = jax.ShapeDtypeStruct
    dma = pltpu.SemaphoreType.DMA
    vmem = pl.BlockSpec(memory_space=pltpu.VMEM)
    halves = [out((clips, rows, half), BF)] * 2
    normed = pltpu.VMEM((clips, rows, model), BF)
    if shard.shape[0] % 16:
        full = lax.all_gather(shard, ("clip", "frame"), axis=0, tiled=True)
        own, send = pl.pallas_call(
            project_local_kernel,
            in_specs=[vmem] * 5,
            out_specs=[vmem] * 2,
            out_shape=halves,
            scratch_shapes=[normed],
            compiler_params=pltpu.CompilerParams(vmem_limit_bytes=VMEM_LIMIT),
            name="project_local",
        )(x, full, gain, shift, bias)
        return full, own, send
    full, own, send = pl.pallas_call(
        project_kernel,
        in_specs=[vmem] * 5,
        out_specs=[vmem] * 3,
        out_shape=[out((outers, 4) + shard.shape, BF)] + halves,
        scratch_shapes=[
            normed,
            dma((outers,)),
            dma((outers,)),
            dma((outers, 3)),
            dma((outers, 3)),
        ],
        compiler_params=pltpu.CompilerParams(
            collective_id=3, has_side_effects=True, vmem_limit_bytes=VMEM_LIMIT
        ),
        name="gather_and_project",
    )(x, shard, gain, shift, bias)
    return full.reshape(model, width), own, send


def device_of(outer, inner, frame, head):
    return (outer * 2 + inner, frame, head)


def plane_peer(inner, frame, step):
    return (inner + step // 2) % 2, (frame + step % 2) % 2


def row_piece(value, row):
    return value[:, row * LANES : (row + 1) * LANES]


def tail_kernel(
    own, recv, x, middle_grad, weight, gain, shift, taps, pool_gain, pool_shift, bias_grad, hot,
    space_hot, squeeze, vectors, up_bias, rest,
    grad_in, out, proj_out, up_grad_out, down_out, gain_out, shift_out, rows_out, joined_out, up_out, taps_out, pool_gain_out,
    pool_shift_out, squeeze_out, time_out, space_out,
    joined, normed, grads, near, part, far, small, small_in, small_out, cross_send, cross_recv,
    rest_in, cross_sems, near_sems, far_sems, first_sems, second_sems, rest_sems,
    *, unit, plan,
):
    chunks, outers, shard_rows, cols = part.shape
    clips, rows, model = x.shape
    group = own.shape[2] // 3
    span = joined.shape[0] // clips
    devices = small.shape[0]
    clip = lax.axis_index("clip")
    frame = lax.axis_index("frame")
    head = lax.axis_index("head")
    outer, inner = clip // 2, clip % 2
    place = inner * 2 + frame
    mine = (clip * 2 + frame) * 2 + head

    def device(index):
        return (index // 4, (index // 2) % 2, index % 2)

    barrier = pltpu.get_barrier_semaphore()
    each(
        1,
        devices,
        lambda step: pl.semaphore_signal(
            barrier, inc=1, device_id=device((mine + step) % devices), device_id_type=MESH_ID
        ),
    )

    def first(step):
        other = (mine + step) % devices
        return pltpu.make_async_remote_copy(
            src_ref=small.at[other], dst_ref=small_in.at[step],
            send_sem=first_sems.at[0, step], recv_sem=first_sems.at[1, step],
            device_id=device(other), device_id_type=MESH_ID,
        )

    def second(step, block):
        return pltpu.make_async_remote_copy(
            src_ref=small_out.at[block], dst_ref=small_out.at[block],
            send_sem=second_sems.at[0, step], recv_sem=second_sems.at[1, step],
            device_id=device((mine + step) % devices), device_id_type=MESH_ID,
        )

    def near_copy(chunk, step):
        there_inner, there_frame = plane_peer(inner, frame, step)
        return pltpu.make_async_remote_copy(
            src_ref=grads.at[chunk, :, there_inner * 2 + there_frame],
            dst_ref=near.at[chunk, step - 1],
            send_sem=near_sems.at[0, chunk, step - 1], recv_sem=near_sems.at[1, chunk, step - 1],
            device_id=device_of(outer, there_inner, there_frame, head), device_id_type=MESH_ID,
        )

    def far_copy(chunk, step):
        there = (outer + step) % outers
        return pltpu.make_async_remote_copy(
            src_ref=part.at[chunk, there], dst_ref=far.at[chunk, step],
            send_sem=far_sems.at[0, chunk, step], recv_sem=far_sems.at[1, chunk, step],
            device_id=device_of(there, inner, frame, head), device_id_type=MESH_ID,
        )

    def cross_copy(index):
        return pltpu.make_async_remote_copy(
            src_ref=cross_send.at[index], dst_ref=cross_recv.at[index],
            send_sem=cross_sems.at[0, index], recv_sem=cross_sems.at[1, index],
            device_id=(clip, frame, 1 - head), device_id_type=MESH_ID,
        )

    def rest_copy(step):
        there = (outer + step) % outers
        return pltpu.make_async_remote_copy(
            src_ref=rest.at[there], dst_ref=rest_in.at[step],
            send_sem=rest_sems.at[0, step], recv_sem=rest_sems.at[1, step],
            device_id=device_of(there, inner, frame, head), device_id_type=MESH_ID,
        )

    joined[...] = jnp.zeros_like(joined)
    normed[...] = jnp.zeros_like(normed)
    small[...] = jnp.zeros_like(small)

    def assemble(low, high):
        for index in range(clips):
            at = slice(index * span, index * span + rows)
            for member in range(3):
                source = slice(member * group, (member + 1) * group)
                left = 2 * member * group
                joined[at, left : left + group] = low[index, :, source]
                joined[at, left + group : left + 2 * group] = high[index, :, source]

    @pl.when(frame == 0)
    def _():
        assemble(own, recv)

    @pl.when(frame == 1)
    def _():
        assemble(recv, own)

    pl.semaphore_wait(barrier, devices - 1)
    each(1, outers, lambda step: rest_copy(step).start())
    for index in range(clips):
        block = joined[index * span : (index + 1) * span]
        partial_rows = dot_f32(block, weight[...], ((1,), (1,)))
        cross_send[index] = partial_rows[:rows].astype(BF)
        cross_copy(index).start()
    for index in range(clips):
        centred, rate = row_stats(x[index].astype(F32))
        value = centred * rate * gain[...] + shift[...]
        normed[index * span : index * span + rows] = value.astype(BF)
    for chunk in range(chunks):
        value = dot_f32(normed[...], joined[:, chunk * cols : (chunk + 1) * cols], ((0,), (0,)))
        value = value.astype(BF)
        if shard_rows % 16 == 0:
            grads[chunk] = value.reshape(outers, 4, shard_rows, cols)
        else:
            for block in range(outers * 4):
                low = block * shard_rows
                grads[chunk, block // 4, block % 4] = value[low : low + shard_rows]
        for step in range(1, 4):
            near_copy(chunk, step).start()

    gain_sum = jnp.zeros((1, model), F32)
    shift_sum = jnp.zeros((1, model), F32)
    for index in range(clips):
        cross_copy(index).wait_recv()
        incoming = cross_send[index].astype(F32) + cross_recv[index].astype(F32)
        centred, rate = row_stats(x[index].astype(F32))
        normal = centred * rate
        product = incoming * normal
        gain_sum = gain_sum + jnp.sum(product, axis=0, keepdims=True)
        shift_sum = shift_sum + jnp.sum(incoming, axis=0, keepdims=True)
        scaled = incoming * gain[...]
        mean_scaled = jnp.sum(scaled, axis=-1, keepdims=True) * (1.0 / model)
        mean_both = jnp.sum(scaled * normal, axis=-1, keepdims=True) * (1.0 / model)
        result = rate * (scaled - mean_scaled - normal * mean_both) + middle_grad[index]
        grad_in[index] = result.astype(BF)

    rows_small = small.shape[1]

    def put(row, value):
        count = value.shape[0]
        done = 0
        while done < count:
            block, offset = divmod(row + done, rows_small)
            size = min(count - done, rows_small - offset)
            small[block, offset : offset + size, : value.shape[1]] = value[done : done + size]
            done += size

    def take(row, target):
        count = target.shape[0]
        done = 0
        while done < count:
            block, offset = divmod(row + done, rows_small)
            size = min(count - done, rows_small - offset)
            target[done : done + size] = small_out[
                block, offset : offset + size, : target.shape[1]
            ]
            done += size

    def put_wide(row, value):
        for index in range(value.shape[1] // LANES):
            put(row + index, row_piece(value, index))

    def take_wide(row, target, at):
        for index in range(target.shape[1] // LANES):
            block, offset = divmod(row + index, rows_small)
            target[at : at + 1, index * LANES : (index + 1) * LANES] = small_out[
                block, offset : offset + 1
            ]

    wide_rows_count = model // LANES

    @pl.when(head == 0)
    def _():
        put_wide(plan["gain"], gain_sum)
        put_wide(plan["gain"] + wide_rows_count, vectors[0:1])
        put_wide(plan["shift"], shift_sum)
        put_wide(plan["shift"] + wide_rows_count, vectors[1:2])
        put_wide(plan["rows"], vectors[2:3])
        put_wide(plan["rows"] + wide_rows_count, vectors[3:4])

    joined_sum = jnp.sum(joined[...].astype(F32), axis=0, keepdims=True)
    joined_rows = joined.shape[1] // LANES
    up_rows = up_bias.shape[1] // LANES
    for which in range(2):

        @pl.when(head == which)
        def _():
            put_wide(plan["joined"] + which * joined_rows, joined_sum)
            put_wide(plan["up"] + which * up_rows, up_bias[...])

    heads = taps.shape[2] // (3 * LANES)
    tap_sum = jnp.sum(taps[...], axis=1)
    for member in range(3):
        totals = []
        for value in (tap_sum, pool_gain[...], pool_shift[...]):
            total = row_piece(value, member * heads)
            for index in range(1, heads):
                total = total + row_piece(value, member * heads + index)
            totals.append(total)
        put(plan["taps"] + member * 27, totals[0])
        put(plan["pool_gain"] + member, totals[1])
        put(plan["pool_shift"] + member, totals[2])
    put(plan["squeeze"], squeeze[...])
    time_sum = jnp.zeros((hot.shape[2], LANES), F32)
    bias_sum = jnp.zeros((BIAS_COLS, LANES), F32)
    for index in range(clips):
        value = bias_grad[index]
        bias_sum = bias_sum + value
        value = value[: hot.shape[1]]
        high = value.astype(BF)
        low = (value - high.astype(F32)).astype(BF)
        time_sum = time_sum + dot_f32(hot[index], high, ((0,), (0,)))
        time_sum = time_sum + dot_f32(hot[index], low, ((0,), (0,)))
    put(plan["time"], time_sum[: time_out.shape[0]])
    high = bias_sum.astype(BF)
    low = (bias_sum - high.astype(F32)).astype(BF)
    space_sum = dot_f32(space_hot[...], high, ((1,), (0,)))
    space_sum = space_sum + dot_f32(space_hot[...], low, ((1,), (0,)))
    put(plan["space"], space_sum[: space_out.shape[0]])

    each(1, devices, lambda step: first(step).start())

    def reduce_near(chunk):
        lanes = slice(chunk * cols, (chunk + 1) * cols)
        for step in range(1, 4):
            near_copy(chunk, step).wait_recv()

        def gathered(index):
            value = grads[chunk, index, place].astype(F32)
            for step in range(3):
                value = value + near[chunk, step, index].astype(F32)
            return value

        def send(step):
            there = (outer + step) % outers
            part[chunk, there] = gathered(there).astype(BF)
            far_copy(chunk, step).start()

        each(1, outers, send)
        out[:, lanes] = gathered(outer)

    reduce_near(0)
    each(1, devices, lambda step: first(step).wait_recv())
    total = lax.fori_loop(1, devices, lambda step, sums: sums + small_in[step], small[mine])
    small_out[mine] = total
    each(1, devices, lambda step: second(step, mine).start())
    for chunk in range(1, chunks):
        reduce_near(chunk)
    each(1, outers, lambda step: rest_copy(step).wait_recv())
    at = 0
    for target in (proj_out, up_grad_out, down_out):
        lanes = slice(at, at + target.shape[1])
        target[...] = lax.fori_loop(
            1,
            outers,
            lambda step, sums: sums + rest_in[step, :, lanes].astype(F32),
            rest[outer, :, lanes].astype(F32),
        )
        at += target.shape[1]
    for chunk in range(chunks):
        lanes = slice(chunk * cols, (chunk + 1) * cols)
        each(1, outers, lambda step: far_copy(chunk, step).wait_recv())
        out[:, lanes] = lax.fori_loop(
            1, outers, lambda step, sums: sums + far[chunk, step].astype(F32), out[:, lanes]
        )
    each(1, devices, lambda step: second(step, (mine + devices - step) % devices).wait_recv())
    for index in range(2):
        take_wide(plan["gain"] + index * wide_rows_count, gain_out, index)
        take_wide(plan["shift"] + index * wide_rows_count, shift_out, index)
        take_wide(plan["rows"] + index * wide_rows_count, rows_out, index)
    for which in range(2):

        @pl.when(head == which)
        def _():
            for member in range(3):
                row = plan["joined"] + which * joined_rows + member * (joined_rows // 3)
                take_wide(row, joined_out, member)
            take_wide(plan["up"] + which * up_rows, up_out, 0)

    for member in range(3):
        take(plan["taps"] + member * 27, taps_out.at[member])
    take(plan["pool_gain"], pool_gain_out)
    take(plan["pool_shift"], pool_shift_out)
    take(plan["squeeze"], squeeze_out)
    take(plan["time"], time_out)
    take(plan["space"], space_out)
    each(1, devices, lambda step: first(step).wait_send())
    each(1, devices, lambda step: second(step, mine).wait_send())
    each(1, outers, lambda step: rest_copy(step).wait_send())
    for index in range(clips):
        cross_copy(index).wait_send()
    for chunk in range(chunks):
        for step in range(1, 4):
            near_copy(chunk, step).wait_send()
        each(1, outers, lambda step: far_copy(chunk, step).wait_send())


def tail(
    own, recv, x, middle_grad, weight, gain, shift, taps, pool_gain, pool_shift, bias_grad, hot,
    space_hot, squeeze, vectors, up_bias, rest, clip_count, devices, unit, table_rows,
):
    clips, rows, model = x.shape
    width = weight.shape[1]
    outers = clip_count // 2
    shard_rows = model // (4 * outers)
    chunks = 3
    cols = width // chunks
    span = -(-rows // 16) * 16
    plan = {}
    at = 0
    for name, count in (
        ("gain", 2 * model // LANES),
        ("shift", 2 * model // LANES),
        ("rows", 2 * model // LANES),
        ("joined", 2 * width // LANES),
        ("up", 2 * up_bias.shape[1] // LANES),
        ("taps", 81),
        ("pool_gain", 3),
        ("pool_shift", 3),
        ("squeeze", squeeze.shape[0]),
        ("time", table_rows),
        ("space", 2 * (2 * SIDE - 1)),
    ):
        plan[name] = at
        at += count
    block = -(-at // (devices * 8)) * 8
    out = jax.ShapeDtypeStruct
    dma = pltpu.SemaphoreType.DMA
    vmem = pl.BlockSpec(memory_space=pltpu.VMEM)
    shapes = [
        out((clips, rows, model), BF),
        out((shard_rows, width), F32),
        out((shard_rows, rest.shape[2] - 2 * up_bias.shape[1]), F32),
        out((shard_rows, up_bias.shape[1]), F32),
        out((shard_rows, up_bias.shape[1]), F32),
        out((2, model), F32),
        out((2, model), F32),
        out((2, model), F32),
        out((3, width // 3), F32),
        out((1, up_bias.shape[1]), F32),
        out((3, 27, unit), F32),
        out((3, unit), F32),
        out((3, unit), F32),
        out(squeeze.shape, F32),
        out((table_rows, unit), F32),
        out((2 * (2 * SIDE - 1), unit), F32),
    ]
    return pl.pallas_call(
        partial(tail_kernel, unit=unit, plan=plan),
        in_specs=[vmem] * 17,
        out_specs=[vmem] * len(shapes),
        out_shape=shapes,
        scratch_shapes=[
            pltpu.VMEM((clips * span, width), BF),
            pltpu.VMEM((clips * span, model), BF),
            pltpu.VMEM((chunks, outers, 4, shard_rows, cols), BF),
            pltpu.VMEM((chunks, 3, outers, shard_rows, cols), BF),
            pltpu.VMEM((chunks, outers, shard_rows, cols), BF),
            pltpu.VMEM((chunks, outers, shard_rows, cols), BF),
            pltpu.VMEM((devices, block, LANES), F32),
            pltpu.VMEM((devices, block, LANES), F32),
            pltpu.VMEM((devices, block, LANES), F32),
            pltpu.VMEM((clips, rows, model), BF),
            pltpu.VMEM((clips, rows, model), BF),
            pltpu.VMEM(rest.shape, BF),
            dma((2, clips)),
            dma((2, chunks, 3)),
            dma((2, chunks, outers)),
            dma((2, devices)),
            dma((2, devices)),
            dma((2, outers)),
        ],
        compiler_params=pltpu.CompilerParams(
            collective_id=0, has_side_effects=True, vmem_limit_bytes=VMEM_LIMIT
        ),
        name="tail_gradients",
    )(
        own, recv, x, middle_grad, weight, gain, shift, taps, pool_gain, pool_shift, bias_grad,
        hot, space_hot, squeeze, vectors, up_bias, rest,
    )


def feed_kernel(
    att_own, att_recv, x, cot, weights, gain, shift, out_shift, up_shift,
    block_out, middle_grad, grad_own, grad_send, grad_rest, vectors, up_bias,
    attended, normed, cots, active, hidden_low, branch, middle, send, recv, sems,
):
    clips, rows, model = x.shape
    span = attended.shape[0] // clips
    group = att_own.shape[2]
    head_width = 2 * group
    hidden_width = up_shift.shape[1]
    tiles = 4
    tile = hidden_width // tiles
    clip_at = lax.axis_index("clip")
    frame = lax.axis_index("frame")
    head = lax.axis_index("head")
    partner = (clip_at, frame, 1 - head)

    def cross(kind, index):
        return pltpu.make_async_remote_copy(
            src_ref=send.at[kind, index], dst_ref=recv.at[kind, index],
            send_sem=sems.at[0, kind, index], recv_sem=sems.at[1, kind, index],
            device_id=partner, device_id_type=MESH_ID,
        )

    barrier = pltpu.get_barrier_semaphore()
    pl.semaphore_signal(barrier, inc=1, device_id=partner, device_id_type=MESH_ID)
    for ref in (attended, normed, cots, branch):
        ref[...] = jnp.zeros_like(ref)

    def assemble(low, high):
        for index in range(clips):
            at = slice(index * span, index * span + rows)
            attended[at, :group] = low[index]
            attended[at, group:] = high[index]

    @pl.when(frame == 0)
    def _():
        assemble(att_own, att_recv)

    @pl.when(frame == 1)
    def _():
        assemble(att_recv, att_own)

    for index in range(clips):
        cots[index * span : index * span + rows] = cot[index]
    pl.semaphore_wait(barrier, 1)

    def block_rows(index):
        return pl.ds(pl.multiple_of(index * span, 16), span)

    def project(index):
        part = dot_f32(attended[block_rows(index)], weights[:, :head_width], ((1,), (1,)))
        send[0, index] = part[:rows].astype(BF)
        cross(0, index).start()

    each(0, clips, project)

    def feed(index, bias_sum):
        cross(0, index).wait_recv()
        branch_rows = send[0, index].astype(F32) + recv[0, index].astype(F32)
        value = x[index].astype(F32) + branch_rows + out_shift[0:1]
        middle[index] = value
        centred, rate = row_stats(value)
        low = (centred * rate * gain[...] + shift[...]).astype(BF)
        at = pl.multiple_of(index * span, 16)
        normed[pl.ds(at, rows)] = low
        low = normed[block_rows(index)]
        cot_rows = cots[block_rows(index)]
        out_part = jnp.zeros((span, model), F32)
        norm_part = jnp.zeros((span, model), F32)
        sums = []
        for step in range(tiles):
            lanes = slice(step * tile, (step + 1) * tile)
            up = weights[:, head_width + step * tile : head_width + (step + 1) * tile]
            at = head_width + hidden_width + step * tile
            down = weights[:, at : at + tile]
            hidden = dot_f32(low, up, ((1,), (0,))) + up_shift[:, lanes]
            incoming = dot_f32(cot_rows, down, ((1,), (0,)))
            normal = 0.5 * (1.0 + lax.erf(hidden * (0.5**0.5)))
            density = jnp.exp(hidden * hidden * -0.5) * ((2.0 * np.pi) ** -0.5)
            acted = (hidden * normal).astype(BF)
            back = (incoming * (normal + hidden * density)).astype(BF)
            active[block_rows(index), lanes] = acted
            hidden_low[block_rows(index), lanes] = back
            sums.append(jnp.sum(back.astype(F32), axis=0, keepdims=True))
            out_part = out_part + dot_f32(acted, down, ((1,), (1,)))
            norm_part = norm_part + dot_f32(back, up, ((1,), (1,)))
        send[1, index] = norm_part[:rows].astype(BF)
        cross(1, index).start()
        send[2, index] = out_part[:rows].astype(BF)
        cross(2, index).start()
        return bias_sum + jnp.concatenate(sums, axis=1)

    up_bias[...] = lax.fori_loop(0, clips, feed, jnp.zeros((1, hidden_width), F32))

    for step in range(tiles):
        lanes = slice(step * tile, (step + 1) * tile)
        value = dot_f32(normed[...], hidden_low[:, lanes], ((0,), (0,)))
        at = head_width + step * tile
        grad_rest[:, at : at + tile] = value.astype(BF)
        value = dot_f32(cots[...], active[:, lanes], ((0,), (0,)))
        at = head_width + hidden_width + step * tile
        grad_rest[:, at : at + tile] = value.astype(BF)

    def back(index, sums):
        gain_sum, shift_sum, first_sum, second_sum = sums
        cross(1, index).wait_recv()
        incoming = send[1, index].astype(F32) + recv[1, index].astype(F32)
        centred, rate = row_stats(middle[index])
        normal = centred * rate
        scaled = incoming * gain[...]
        mean_scaled = jnp.sum(scaled, axis=-1, keepdims=True) * (1.0 / model)
        mean_both = jnp.sum(scaled * normal, axis=-1, keepdims=True) * (1.0 / model)
        cot_rows = cot[index].astype(F32)
        value = cot_rows + rate * (scaled - mean_scaled - normal * mean_both)
        middle_grad[index] = value
        at = pl.multiple_of(index * span, 16)
        branch[pl.ds(at, rows)] = value.astype(BF)
        part = dot_f32(branch[block_rows(index)], weights[:, :head_width], ((1,), (0,)))
        part = part[:rows].astype(BF)

        @pl.when(frame == 0)
        def _():
            grad_own[index] = part[:, :group]
            grad_send[index] = part[:, group:]

        @pl.when(frame == 1)
        def _():
            grad_send[index] = part[:, :group]
            grad_own[index] = part[:, group:]

        cross(2, index).wait_recv()
        out_rows = send[2, index].astype(F32) + recv[2, index].astype(F32)
        block_out[index] = (middle[index] + out_rows + out_shift[1:2]).astype(BF)

        def column(rows_here):
            return jnp.sum(rows_here, axis=0, keepdims=True)

        return (
            gain_sum + column(incoming * normal),
            shift_sum + column(incoming),
            first_sum + column(value),
            second_sum + column(cot_rows),
        )

    start = tuple(jnp.zeros((1, model), F32) for _ in range(4))
    sums = lax.fori_loop(0, clips, back, start)
    for row in range(4):
        vectors[row : row + 1] = sums[row]
    value = dot_f32(branch[...], attended[...], ((0,), (0,)))
    grad_rest[:, :head_width] = value.astype(BF)
    for kind in range(3):
        each(0, clips, lambda index: cross(kind, index).wait_send())


def feed(att_own, att_recv, x, cot, weights, gain, shift, out_shift, up_shift):
    clips, rows, model = x.shape
    group = att_own.shape[2]
    hidden_width = up_shift.shape[1]
    span = -(-rows // 16) * 16
    out = jax.ShapeDtypeStruct
    vmem = pl.BlockSpec(memory_space=pltpu.VMEM)
    shapes = [
        out((clips, rows, model), BF),
        out((clips, rows, model), F32),
        out((clips, rows, group), BF),
        out((clips, rows, group), BF),
        out(weights.shape, BF),
        out((4, model), F32),
        out((1, hidden_width), F32),
    ]
    return pl.pallas_call(
        feed_kernel,
        in_specs=[vmem] * 9,
        out_specs=[vmem] * len(shapes),
        out_shape=shapes,
        scratch_shapes=[
            pltpu.VMEM((clips * span, 2 * group), BF),
            pltpu.VMEM((clips * span, model), BF),
            pltpu.VMEM((clips * span, model), BF),
            pltpu.VMEM((clips * span, hidden_width), BF),
            pltpu.VMEM((clips * span, hidden_width), BF),
            pltpu.VMEM((clips * span, model), BF),
            pltpu.VMEM((clips, rows, model), F32),
            pltpu.VMEM((3, clips, rows, model), BF),
            pltpu.VMEM((3, clips, rows, model), BF),
            pltpu.SemaphoreType.DMA((2, 3, clips)),
        ],
        compiler_params=pltpu.CompilerParams(
            collective_id=4, has_side_effects=True, vmem_limit_bytes=VMEM_LIMIT
        ),
        name="feed_forward_both_ways",
    )(att_own, att_recv, x, cot, weights, gain, shift, out_shift, up_shift)


def precise(pattern, *operands):
    return jnp.einsum(pattern, *operands, precision=lax.Precision.HIGHEST)


def split_groups(value, which, axis):
    half = value.shape[axis] // 2
    low = lax.slice_in_dim(value, 0, half, axis=axis)
    high = lax.slice_in_dim(value, half, None, axis=axis)
    first = which == 0
    return jnp.where(first, low, high), jnp.where(first, high, low)


def join_groups(own, peer, which, axis):
    first = which == 0
    return jnp.concatenate([jnp.where(first, own, peer), jnp.where(first, peer, own)], axis=axis)


def time_choices(stride_group, memory_place, which, own, table_rows):
    local = jnp.arange(own, dtype=jnp.int32)
    times = jnp.concatenate([which * own + local, (1 - which) * own + local])
    stride = jnp.left_shift(jnp.int32(2), stride_group)[:, None, None]
    offset = 8 * (FRAMES - 1)
    current = stride * (times[None, :, None] - times[None, None, :]) + offset
    first = memory_place[:, np.array([2, 0, 3, 1])]
    second = memory_place[:, np.array([3, 1, 2, 0])]
    places = jnp.where(which == 0, first, second)
    memory = stride * times[None, :, None] + places[:, None, :] + offset
    chosen = jnp.concatenate([current, memory], axis=2)
    return (chosen[..., None] == jnp.arange(table_rows, dtype=jnp.int32)).astype(F32)


def space_choices():
    places = np.arange(SIDE)
    offsets = places[:, None] - places[None, :] + SIDE - 1
    hot = offsets.reshape(-1)[:, None] == np.arange(2 * SIDE - 1)[None, :]
    return jnp.asarray(hot.astype(np.float32))


def space_sums():
    spans = 2 * SIDE - 1
    hot = np.zeros((32, BIAS_COLS), np.float32)
    for axis in range(2):
        for query in range(SIDE):
            for key in range(SIDE):
                col = SPACE_AT + axis * CELLS + query * SIDE + key
                hot[axis * spans + query - key + SIDE - 1, col] = 1.0
    return hot


def wide_rows(rows, heads):
    count, members, unit = rows.shape
    padded = jnp.pad(rows, ((0, 0), (0, 0), (0, LANES - unit)))
    spread = jnp.broadcast_to(padded[:, :, None], (count, members, heads, LANES))
    return spread.reshape(count, members * heads * LANES)


def local(
    clips_in,
    cached_kv,
    old_memory,
    stride_group,
    memory_place,
    norm_gain,
    norm_shift,
    qkv_weight,
    qkv_shift,
    pool_kernel,
    pool_gain,
    pool_shift,
    squeeze_kernel,
    time_table,
    space_tables,
    proj_weight,
    out_shift,
    up_weight,
    up_shift,
    down_weight,
    cotangent,
):
    clip_count, rows_clip, model_width = clips_in.shape
    head_width = qkv_weight.shape[2]
    unit = pool_gain.shape[1]
    head_count = head_width // unit
    frame_count = lax.axis_size("frame")
    heads = head_count // frame_count
    own_frames = rows_clip // CELLS
    group_width = heads * unit
    group_span = FRAMES // MEMF
    scale = unit ** (-0.5)
    both = ("clip", "frame")
    which = lax.axis_index("frame")
    into_np, outof_np = placement(frame_count)
    keys_np, mask_np, pad_np = bias_constants(frame_count)
    consts = (
        jnp.where(which == 0, jnp.asarray(into_np[0], BF), jnp.asarray(into_np[1], BF)),
        jnp.where(which == 0, jnp.asarray(outof_np[0], BF), jnp.asarray(outof_np[1], BF)),
        jnp.asarray(keys_np, BF),
        jnp.asarray(mask_np),
        jnp.asarray(pad_np),
    )

    attn_flat, joined_own, joined_send = project(
        clips_in, qkv_weight.reshape(-1, 3 * head_width), norm_gain[:1], norm_shift[:1],
        qkv_shift.reshape(1, -1), lax.axis_size("clip"),
    )
    shards = jnp.concatenate([proj_weight.T, up_weight, down_weight.T], axis=1)
    rest_full = lax.all_gather(shards, both, axis=0, tiled=True)

    cached_wide = cached_kv.astype(F32).reshape(
        clip_count, group_span, CELLS, 2, head_count, unit
    )
    squeezed = precise("cjsxnd,xjd->csxnd", cached_wide, squeeze_kernel).astype(BF)
    memory_rows = jnp.concatenate(
        [squeezed.reshape(clip_count, CELLS, 2, head_width), old_memory], axis=1
    )
    mem_own, mem_send = split_groups(memory_rows, which, 3)
    mem_own = mem_own.reshape(clip_count, -1, 2 * group_width)
    mem_send = mem_send.reshape(clip_count, -1, 2 * group_width)

    time_hot = time_choices(stride_group, memory_place, which, own_frames, time_table.shape[0])
    time_rows = precise("ctkr,rd->ctkd", time_hot, time_table).reshape(clip_count, -1, unit)
    space_hot = space_choices()
    space_rows = precise("pr,xrd->xpd", space_hot, space_tables).reshape(2 * CELLS, unit)
    bias = jnp.zeros((clip_count, BIAS_COLS, LANES), F32)
    bias = bias.at[:, : time_rows.shape[1], :unit].set(time_rows)
    bias = bias.at[:, SPACE_AT : SPACE_AT + 2 * CELLS, :unit].set(space_rows[None])
    bias = bias * (1.0 / scale)
    taps = wide_rows(pool_kernel.transpose(1, 0, 2), heads)
    gains = wide_rows(pool_gain[None], heads)
    shifts = wide_rows(pool_shift[None], heads)

    forward = attention_forward(
        joined_own, joined_send, mem_own, mem_send, consts, taps, gains, shifts, bias, scale, unit
    )
    attended_own, attended_peer = forward[:2]
    saved = forward[2:]
    block_out, middle_grad, attended_grad_own, attended_grad_send, grad_rest, vectors, up_grads = (
        feed(
            attended_own, attended_peer, clips_in, cotangent, rest_full, norm_gain[1:],
            norm_shift[1:], out_shift, up_shift.reshape(1, -1),
        )
    )
    outers = lax.axis_size("clip") // 2
    grad_rest = grad_rest.reshape(outers, 4, -1, grad_rest.shape[1])
    backward = attention_backward(
        attended_grad_own, attended_grad_send, grad_rest, consts, taps, gains, bias, saved, scale, unit
    )
    grad_own, grad_peer, mem_grad_own, mem_grad_peer = backward[:4]
    taps_grad, pool_gain_grad, pool_shift_grad, bias_grad, rest_part = backward[4:]

    mem_grads = [
        part[:, :CELLS].reshape(clip_count, CELLS, 2, heads, LANES)[..., :unit]
        for part in (mem_grad_own, mem_grad_peer)
    ]
    squeezed_grads = join_groups(mem_grads[0], mem_grads[1], which, 3).astype(F32)
    grad_squeeze = precise("cjsxnd,csxnd->xjd", cached_wide, squeezed_grads)
    time_count = time_rows.shape[1]
    hot = time_hot.reshape(clip_count, time_count, -1).astype(BF)
    hot = jnp.pad(hot, ((0, 0), (0, 0), (0, -hot.shape[2] % LANES)))
    devices = lax.axis_size("clip") * frame_count * lax.axis_size("head")
    (
        grad_in, qkv_shard, proj_shard, up_shard, down_shard, gain_sums, shift_sums, out_sums, qkv_bias_sum, up_bias_sum, kernel_sum,
        pool_gain_sum, pool_shift_sum, squeeze_sum, time_sum, space_sum,
    ) = tail(
        grad_own, grad_peer, clips_in, middle_grad, attn_flat,
        norm_gain[:1], norm_shift[:1], taps_grad, pool_gain_grad, pool_shift_grad, bias_grad, hot,
        jnp.asarray(space_sums(), BF), grad_squeeze.reshape(-1, unit), vectors,
        up_grads, rest_part, lax.axis_size("clip"), devices, unit, time_table.shape[0],
    )
    return (
        block_out,
        grad_in,
        gain_sums,
        shift_sums,
        qkv_shard.reshape(-1, 3, head_width),
        qkv_bias_sum,
        kernel_sum,
        pool_gain_sum,
        pool_shift_sum,
        squeeze_sum.reshape(squeeze_kernel.shape),
        time_sum,
        space_sum.reshape(space_tables.shape),
        proj_shard.T,
        out_sums,
        up_shard,
        up_bias_sum.reshape(-1),
        down_shard.T,
    )


def solution(mesh):
    return jax.shard_map(
        local,
        mesh=mesh,
        in_specs=(
            P("clip", "frame", None),
            P("clip", "frame", None, "head"),
            P("clip", "frame", None, "head"),
            P("clip"),
            P("clip", None),
            P(),
            P(),
            P(("clip", "frame"), None, "head"),
            P(None, "head"),
            P(),
            P(),
            P(),
            P(),
            P(),
            P(),
            P("head", ("clip", "frame")),
            P(),
            P(("clip", "frame"), "head"),
            P("head"),
            P("head", ("clip", "frame")),
            P("clip", "frame", None),
        ),
        out_specs=(
            P("clip", "frame", None),
            P("clip", "frame", None),
            P(),
            P(),
            P(("clip", "frame"), None, "head"),
            P(None, "head"),
            P(),
            P(),
            P(),
            P(),
            P(),
            P(),
            P("head", ("clip", "frame")),
            P(),
            P(("clip", "frame"), "head"),
            P("head"),
            P("head", ("clip", "frame")),
        ),
        check_vma=False,
    )
```

```python
from functools import partial

import jax
import jax.numpy as jnp
import numpy as np
from jax import lax
from jax.experimental import pallas as pl
from jax.experimental.pallas import tpu as pltpu
from jax.sharding import PartitionSpec as P

FRAMES = 8
MEMF = 2
SIDE = 7
CELLS = SIDE * SIDE
LANES = 128
HALF = 208
QROWS = 2 * HALF
GRID_ROWS = FRAMES * SIDE * 8
MEM_AT = QROWS
MEM_PAD = 112
MEM_BACK = 64
TURN_STEP = 3
KROWS = 640
BIAS_COLS = 256
SPACE_AT = 128
PAD_LANE = 127
BF = jnp.bfloat16
F32 = jnp.float32
VMEM_LIMIT = 60 * 1024 * 1024
MESH_ID = pl.DeviceIdType.MESH


def dot_f32(a, b, dims):
    return lax.dot_general(a, b, (dims, ((), ())), preferred_element_type=F32)


def frame_order(first, own):
    rest = [t for t in range(FRAMES) if not first * own <= t < (first + 1) * own]
    return list(range(first * own, (first + 1) * own)) + rest


def placement(frame_count):
    own = FRAMES // frame_count
    into = np.zeros((frame_count, GRID_ROWS, QROWS), np.float32)
    for first in range(frame_count):
        for slot, frame in enumerate(frame_order(first, own)):
            base = (slot // own) * HALF + (slot % own) * CELLS
            for high in range(SIDE):
                for wide in range(SIDE):
                    row = (frame * SIDE + high) * 8 + wide
                    into[first, row, base + high * SIDE + wide] = 1.0
    return into, np.ascontiguousarray(into.transpose(0, 2, 1))


def bias_constants(frame_count):
    own = FRAMES // frame_count
    frames_all = FRAMES + 2 * MEMF
    keys = np.zeros((BIAS_COLS, KROWS), np.float32)
    valid = np.zeros((KROWS,), bool)

    def mark(col, slot, high, wide):
        valid[col] = True
        for query in range(FRAMES):
            keys[query * frames_all + slot, col] = 1.0
        for place in range(SIDE):
            keys[SPACE_AT + place * SIDE + high, col] = 1.0
            keys[SPACE_AT + CELLS + place * SIDE + wide, col] = 1.0

    mask = np.zeros((QROWS, BIAS_COLS), np.float32)
    for slot in range(FRAMES):
        base = (slot // own) * HALF + (slot % own) * CELLS
        for high in range(SIDE):
            for wide in range(SIDE):
                row = base + high * SIDE + wide
                mark(row, slot, high, wide)
                mask[row, slot * frames_all : (slot + 1) * frames_all] = 1.0
                mask[row, SPACE_AT + high * SIDE : SPACE_AT + (high + 1) * SIDE] = 1.0
                low = SPACE_AT + CELLS + wide * SIDE
                mask[row, low : low + SIDE] = 1.0
    for group in range(2):
        for inner in range(MEMF):
            slot = FRAMES + group * MEMF + inner
            for high in range(SIDE):
                for wide in range(SIDE):
                    col = MEM_AT + group * MEM_PAD + inner * CELLS + high * SIDE + wide
                    mark(col, slot, high, wide)
    keys[PAD_LANE, ~valid] = -1e9
    pad_row = np.zeros((1, BIAS_COLS), np.float32)
    pad_row[0, PAD_LANE] = 1.0
    return keys, mask, pad_row


def spread_heads(source, target, rows_at, units, unit, first=0):
    count = source.shape[0]
    for index in range(units):
        at = (first + index) * unit
        target[rows_at : rows_at + count, index * LANES : index * LANES + unit] = source[
            :, at : at + unit
        ]


def load_shifted(field, shifted):
    grid = field.reshape(FRAMES, SIDE, 8, field.shape[-1])
    flat = field.reshape(FRAMES * SIDE, 8, field.shape[-1])
    shifted[1, 1 : FRAMES + 1, 1 : SIDE + 1] = grid
    shifted[0, 1 : FRAMES + 1, 1 : SIDE + 1] = pltpu.roll(flat, 1, 1).reshape(grid.shape)
    shifted[2, 1 : FRAMES + 1, 1 : SIDE + 1] = pltpu.roll(flat, 7, 1).reshape(grid.shape)


def convolve(shifted, taps, target, flip):
    tiles = target.shape[-1] // LANES

    def step(pair, carry):
        for sub in range(2):
            frame = pair * 2 + sub
            for tile in range(tiles):
                lanes = slice(tile * LANES, (tile + 1) * LANES)
                total = None
                for i in range(3):
                    for k in range(3):
                        rows = shifted[k, frame + i, :, :, lanes]
                        for j in range(3):
                            if flip:
                                tap = (2 - i) * 9 + (2 - j) * 3 + (2 - k)
                            else:
                                tap = i * 9 + j * 3 + k
                            value = rows[j : j + SIDE] * taps[tap, :, lanes][None]
                            total = value if total is None else total + value
                target[frame, :, :, lanes] = total
        return carry

    lax.fori_loop(0, FRAMES // 2, step, 0)


def tap_grads(shifted, grads, target):
    tiles = target.shape[-1] // LANES

    def step(index, carry):
        lanes = pl.ds(pl.multiple_of(index * LANES, LANES), LANES)

        def inner(frame, sums):
            centre = grads[frame + 1, 1 : SIDE + 1, :, lanes]
            new = []
            for i in range(3):
                for k in range(3):
                    rows = shifted[k, frame + i, :, :, lanes]
                    for j in range(3):
                        parts = [rows[j + high] * centre[high] for high in range(SIDE)]
                        parts.append(sums[len(new)])
                        while len(parts) > 1:
                            pairs = zip(parts[::2], parts[1::2])
                            parts = [left + right for left, right in pairs]
                        new.append(parts[0])
            return tuple(new)

        start = tuple(jnp.zeros((8, LANES), F32) for _ in range(27))
        sums = lax.fori_loop(0, FRAMES, inner, start, unroll=4)
        for i in range(3):
            for k in range(3):
                for j in range(3):
                    target[i * 9 + j * 3 + k, :, lanes] += sums[(i * 3 + k) * 3 + j]
        return carry

    lax.fori_loop(0, tiles, step, 0)


def head_stats(values, unit):
    average = jnp.sum(values, axis=-1, keepdims=True) * (1.0 / unit)
    lane = lax.broadcasted_iota(jnp.int32, values.shape, 1)
    centred = jnp.where(lane < unit, values - average, 0.0)
    variance = jnp.sum(centred * centred, axis=-1, keepdims=True) * (1.0 / unit)
    return centred, lax.rsqrt(variance + 1e-06)


def frame_partner():
    return (lax.axis_index("clip"), 1 - lax.axis_index("frame"), lax.axis_index("head"))


def partner_copy(source, target, send_sem, recv_sem):
    return pltpu.make_async_remote_copy(
        src_ref=source, dst_ref=target, send_sem=send_sem, recv_sem=recv_sem,
        device_id=frame_partner(), device_id_type=MESH_ID,
    )


def side_partner():
    clip = lax.axis_index("clip")
    across = (clip // 2) * 2 + 1 - clip % 2
    return (across, lax.axis_index("frame"), lax.axis_index("head"))


def side_copy(source, target, send_sem, recv_sem):
    return pltpu.make_async_remote_copy(
        src_ref=source, dst_ref=target, send_sem=send_sem, recv_sem=recv_sem,
        device_id=side_partner(), device_id_type=MESH_ID,
    )


def greet_partner():
    barrier = pltpu.get_barrier_semaphore()
    pl.semaphore_signal(barrier, inc=1, device_id=frame_partner(), device_id_type=MESH_ID)
    pl.semaphore_wait(barrier, 1)


def forward_kernel(
    packed_ref, mem_own_ref, mem_peer_ref, column_ref, into_ref, outof_ref, taps_ref, gain_ref,
    shift_ref, bias_ref, keyhot_ref, mask_ref, pad_ref,
    out_own, out_recv, rest_full, q_out, k_out, v_out, p_out, c_out,
    shifted, taps, out_send, out_sems, side_sems, pair_sems, turn_sems, own_sem,
    *, heads, unit, scale,
):
    units = 3 * heads
    own_rows = out_own.shape[1]
    clip = pl.program_id(0)
    clips = out_send.shape[0]

    def out_copy(index):
        return partner_copy(
            out_send.at[index], out_recv.at[index], out_sems.at[0, index], out_sems.at[1, index]
        )

    outers = column_ref.shape[0]
    split = outers // 2
    inner = lax.axis_index("clip") % 2
    frame = lax.axis_index("frame")
    place = inner * 2 + frame
    side_place = (1 - inner) * 2 + frame
    pair_place = inner * 2 + 1 - frame
    turn_place = (1 - inner) * 2 + 1 - frame
    own_copy = pltpu.make_async_copy(column_ref, rest_full.at[:, place], own_sem)

    def side_move(at, source, target):
        return side_copy(source, target, side_sems.at[0, at], side_sems.at[1, at])

    def pair_move(at, source, target):
        return partner_copy(source, target, pair_sems.at[0, at], pair_sems.at[1, at])

    def to_side(at):
        return side_move(at, column_ref.at[at], rest_full.at[at, place])

    def to_pair(at):
        return pair_move(at, column_ref.at[at], rest_full.at[at, place])

    def turn_side(at):
        block = rest_full.at[at, pair_place]
        return side_copy(block, block, turn_sems.at[0, at], turn_sems.at[1, at])

    def turn_pair(at):
        block = rest_full.at[at, side_place]
        return partner_copy(block, block, turn_sems.at[0, at], turn_sems.at[1, at])

    def turned(at):
        block = rest_full.at[at, turn_place]
        return side_copy(block, block, turn_sems.at[0, at], turn_sems.at[1, at])

    def side_arrival(at):
        block = rest_full.at[at, side_place]
        return side_move(at, block, block)

    def pair_arrival(at):
        block = rest_full.at[at, pair_place]
        return pair_move(at, block, block)

    @pl.when(clip == 0)
    def _():
        barrier = pltpu.get_barrier_semaphore()
        for device in (frame_partner(), side_partner()):
            pl.semaphore_signal(barrier, inc=1, device_id=device, device_id_type=MESH_ID)
        pl.semaphore_wait(barrier, 2)
        each(0, outers, lambda at: to_side(outers - 1 - at).start())
        each(0, outers, lambda at: to_pair(at).start())
        own_copy.start()
        shifted[...] = jnp.zeros_like(shifted)
        for tap in range(27):
            taps[tap] = jnp.broadcast_to(taps_ref[tap : tap + 1], taps.shape[1:])

    @pl.when(clip == jnp.minimum(TURN_STEP, clips - 1))
    def _():
        def turn_low(at):
            pair_arrival(at).wait_recv()
            turn_side(at).start()

        def turn_high(at):
            side_arrival(at).wait_recv()
            turn_pair(at).start()

        each(0, split, turn_low)
        each(split, outers, turn_high)

    load_shifted(dot_f32(into_ref[...], packed_ref[0], ((1,), (0,))), shifted)
    conv = c_out.at[0]
    convolve(shifted, taps, conv, False)
    k_out[0, MEM_AT:, :] = jnp.zeros((KROWS - MEM_AT, heads * LANES), BF)
    v_out[0, MEM_AT:, :] = jnp.zeros((KROWS - MEM_AT, heads * LANES), BF)
    spread_heads(mem_own_ref.at[0], k_out.at[0], MEM_AT, heads, unit, 0 * heads)
    spread_heads(mem_own_ref.at[0], v_out.at[0], MEM_AT, heads, unit, 1 * heads)
    spread_heads(mem_peer_ref.at[0], k_out.at[0], MEM_AT + MEM_PAD, heads, unit, 0 * heads)
    spread_heads(mem_peer_ref.at[0], v_out.at[0], MEM_AT + MEM_PAD, heads, unit, 1 * heads)
    for index in range(units):
        lanes = slice(index * LANES, (index + 1) * LANES)
        block = conv[:, :, :, lanes].reshape(GRID_ROWS, LANES)
        centred, rate = head_stats(block, unit)
        normal = centred * rate * gain_ref[:, lanes] + shift_ref[:, lanes]
        rows = dot_f32(outof_ref[...], normal.astype(BF), ((1,), (0,))).astype(BF)
        target = (q_out, k_out, v_out)[index // heads]
        local = slice((index % heads) * LANES, (index % heads + 1) * LANES)
        target[0, 0:QROWS, local] = rows

    bias = bias_ref[0]
    bias_high = bias.astype(BF)
    bias_low = (bias - bias_high.astype(F32)).astype(BF)
    for head in range(heads):
        lanes = slice(head * LANES, (head + 1) * LANES)
        keys = k_out[0, :, lanes]
        values = v_out[0, :, lanes]
        for half in range(2):
            rows = slice(half * HALF, (half + 1) * HALF)
            query = q_out[0, rows, lanes]
            table = dot_f32(query, bias_high, ((1,), (1,))) + dot_f32(query, bias_low, ((1,), (1,)))
            table = table * mask_ref[rows, :] + pad_ref[...]
            table_high = table.astype(BF)
            table_low = (table - table_high.astype(F32)).astype(BF)
            scores = dot_f32(query, keys, ((1,), (1,)))
            scores = scores + dot_f32(table_high, keyhot_ref[...], ((1,), (0,)))
            scores = scores + dot_f32(table_low, keyhot_ref[...], ((1,), (0,)))
            top = jnp.max(scores, axis=-1, keepdims=True)
            weights = jnp.exp((scores - top) * scale)
            total = jnp.sum(weights, axis=-1, keepdims=True)
            probs = (weights * (1.0 / total)).astype(BF)
            p_out[0, head, rows, :] = probs
            mixed = dot_f32(probs, values, ((1,), (0,))) + query.astype(F32)
            target = (out_own.at[0], out_send.at[clip])[half]
            target[:, head * unit : (head + 1) * unit] = mixed[:own_rows, :unit].astype(BF)

    out_copy(clip).start()

    @pl.when(clip == clips - 1)
    def _():
        own_copy.wait()
        each(split, outers, lambda at: pair_arrival(at).wait_recv())
        each(0, split, lambda at: side_arrival(at).wait_recv())
        each(0, outers, lambda at: turned(at).wait_recv())
        each(0, split, lambda at: turn_side(at).wait_send())
        each(split, outers, lambda at: turn_pair(at).wait_send())
        each(0, outers, lambda at: to_side(at).wait_send())
        each(0, outers, lambda at: to_pair(at).wait_send())
        for index in range(clips):
            out_copy(index).wait()


def backward_kernel(
    packed_ref, normed_ref, weight_ref, grad_own_ref, grad_send_ref, rest_ref, into_ref, outof_ref,
    taps_ref, gain_ref, bias_ref, keyhot_ref, mask_ref, q_ref, k_ref, v_ref, p_ref, c_ref,
    row_own, row_recv, mem_own, mem_recv, taps_out, gain_out, shift_out, bias_out, weight_out,
    joined_out, rest_part, rest_out,
    shifted, taps, grads, spread, pooled, peer, mem_send, rest_own, rest_side, rest_send,
    rest_peer, rest_sum, rest_far, weight_sum, keep, cross_send, cross_recv, row_send,
    grad_sems, mem_sems, own_sems, side_sems, rest_sems, far_sems, cross_sems, row_sems,
    *, heads, unit, scale,
):
    units = 3 * heads
    own_rows = grad_own_ref.shape[1]
    clip = pl.program_id(0)
    clips = peer.shape[0]
    clip_at = lax.axis_index("clip")
    frame = lax.axis_index("frame")
    head_at = lax.axis_index("head")

    def grad_copy(index):
        return partner_copy(
            grad_send_ref.at[index], peer.at[index], grad_sems.at[0, index], grad_sems.at[1, index]
        )

    def mem_copy(index):
        return partner_copy(
            mem_send.at[index], mem_recv.at[index], mem_sems.at[0, index], mem_sems.at[1, index]
        )

    def row_copy(index):
        return partner_copy(
            row_send.at[index], row_recv.at[index], row_sems.at[0, index], row_sems.at[1, index]
        )

    def cross_copy(index):
        return pltpu.make_async_remote_copy(
            src_ref=cross_send.at[index], dst_ref=cross_recv.at[index],
            send_sem=cross_sems.at[0, index], recv_sem=cross_sems.at[1, index],
            device_id=(clip_at, frame, 1 - head_at), device_id_type=MESH_ID,
        )

    def finish_rows(index):
        cross_copy(index).wait_recv()
        total = (keep[index].astype(F32) + cross_recv[index].astype(F32)).astype(BF)
        row_own[index] = total[:own_rows]
        row_send[index] = total[HALF : HALF + own_rows]
        row_copy(index).start()

    chunks, outers, _, _, cols = rest_own.shape
    side_at = clip_at % 2
    outer = clip_at // 2
    early = rest_far.shape[0]

    def rest_at(side, chunk):
        return rest_ref.at[:, pl.ds(side * 2, 2), :, pl.ds(chunk * cols, cols)]

    def own_copy(chunk):
        return pltpu.make_async_copy(
            rest_at(side_at, chunk), rest_own.at[chunk], own_sems.at[chunk]
        )

    def over_copy(chunk):
        return side_copy(
            rest_at(1 - side_at, chunk), rest_side.at[chunk], side_sems.at[0, chunk],
            side_sems.at[1, chunk],
        )

    def rest_copy(chunk):
        return partner_copy(
            rest_send.at[chunk], rest_peer.at[chunk], rest_sems.at[0, chunk],
            rest_sems.at[1, chunk],
        )

    def pass_on(chunk):
        own_copy(chunk).wait()
        over_copy(chunk).wait_recv()

        def add(index):
            def total(part):
                first = rest_own[chunk, index, part].astype(F32)
                return (first + rest_side[chunk, index, part].astype(F32)).astype(BF)

            rest_send[chunk, index] = total(1 - frame)
            rest_sum[chunk, index] = total(frame)

        each(0, outers, add)
        rest_copy(chunk).start()

    def far_device(step):
        return (((outer + step) % outers) * 2 + side_at, frame, head_at)

    def far_copy(chunk, step):
        there = (outer + step) % outers
        return pltpu.make_async_remote_copy(
            src_ref=rest_sum.at[chunk, there], dst_ref=rest_far.at[chunk, step],
            send_sem=far_sems.at[0, chunk, step], recv_sem=far_sems.at[1, chunk, step],
            device_id=far_device(step), device_id_type=MESH_ID,
        )

    def settle(chunk):
        rest_copy(chunk).wait_recv()

        def add(index):
            total = rest_sum[chunk, index].astype(F32) + rest_peer[chunk, index].astype(F32)
            if chunk < early:
                rest_sum[chunk, index] = total.astype(BF)
            else:
                rest_part[index] = total.astype(BF)

        each(0, outers, add)
        if chunk < early:
            each(1, outers, lambda step: far_copy(chunk, step).start())

    @pl.when(clip == 0)
    def _():
        barrier = pltpu.get_barrier_semaphore()

        def greet(device):
            pl.semaphore_signal(barrier, inc=1, device_id=device, device_id_type=MESH_ID)

        for device in (frame_partner(), side_partner(), (clip_at, frame, 1 - head_at)):
            greet(device)
        each(1, outers, lambda step: greet(far_device(step)))
        pl.semaphore_wait(barrier, 3 + outers - 1)
        for index in range(clips):
            grad_copy(index).start()
        over_copy(0).start()
        own_copy(0).start()
        shifted[...] = jnp.zeros_like(shifted)
        grads[...] = jnp.zeros_like(grads)
        spread[...] = jnp.zeros_like(spread)
        taps_out[...] = jnp.zeros_like(taps_out)
        gain_out[...] = jnp.zeros_like(gain_out)
        shift_out[...] = jnp.zeros_like(shift_out)
        weight_sum[...] = jnp.zeros_like(weight_sum)
        joined_out[...] = jnp.zeros_like(joined_out)
        for tap in range(27):
            taps[tap] = jnp.broadcast_to(taps_ref[tap : tap + 1], taps.shape[1:])

    def pump(odd):
        for chunk in range(chunks):
            point = min(chunk + 1, 2 * clips - 1)
            if point % 2 == odd:

                @pl.when(clip == point // 2)
                def _():
                    if chunk + 1 < chunks:
                        over_copy(chunk + 1).start()
                        own_copy(chunk + 1).start()
                    pass_on(chunk)
                    if chunk:
                        settle(chunk - 1)

    pump(0)
    load_shifted(dot_f32(into_ref[...], packed_ref[0], ((1,), (0,))), shifted)
    spread_heads(grad_own_ref.at[0], spread, 0, heads, unit)
    grad_copy(clip).wait_recv()
    spread_heads(peer.at[clip], spread, HALF, heads, unit)
    bias_low = bias_ref[0].astype(BF)
    bias_sum = jnp.zeros((BIAS_COLS, LANES), F32)
    for head in range(heads):
        lanes = slice(head * LANES, (head + 1) * LANES)
        keys = k_ref[0, :, lanes]
        values = v_ref[0, :, lanes]
        keys_grad = jnp.zeros((KROWS, LANES), F32)
        values_grad = jnp.zeros((KROWS, LANES), F32)
        for half in range(2):
            rows = slice(half * HALF, (half + 1) * HALF)
            query = q_ref[0, rows, lanes]
            out_grad = spread[rows, lanes]
            probs = p_ref[0, head, rows, :]
            wide = probs.astype(F32)
            probs_grad = dot_f32(out_grad, values, ((1,), (1,)))
            weighted = wide * probs_grad
            shared = jnp.sum(weighted, axis=-1, keepdims=True)
            score_grad = (weighted - wide * shared).astype(BF)
            values_grad = values_grad + dot_f32(probs, out_grad, ((0,), (0,)))
            keys_grad = keys_grad + dot_f32(score_grad, query, ((0,), (0,)))
            table_grad = dot_f32(score_grad, keyhot_ref[...], ((1,), (1,))) * mask_ref[rows, :]
            table_low = table_grad.astype(BF)
            query_grad = dot_f32(score_grad, keys, ((1,), (0,)))
            query_grad = query_grad + dot_f32(table_low, bias_low, ((1,), (0,)))
            query_grad = query_grad * scale + out_grad.astype(F32)
            pooled[rows, lanes] = query_grad.astype(BF)
            bias_sum = bias_sum + dot_f32(table_low, query, ((0,), (0,)))
        keys_grad = (keys_grad * scale).astype(BF)
        values_grad = values_grad.astype(BF)
        for member, part in enumerate((keys_grad, values_grad)):
            at = ((member + 1) * heads + head) * LANES
            pooled[:, at : at + LANES] = part[:QROWS]
            at = (member * heads + head) * LANES
            low = MEM_AT + MEM_PAD
            mem_own[0, :, at : at + LANES] = part[MEM_AT : MEM_AT + MEM_BACK]
            mem_send[clip, :, at : at + LANES] = part[low : low + MEM_BACK]
    bias_out[0] = bias_sum
    mem_copy(clip).start()

    for index in range(units):
        lanes = slice(index * LANES, (index + 1) * LANES)
        incoming = dot_f32(into_ref[...], pooled[:, lanes], ((1,), (0,)))
        block = c_ref[0, :, :, :, lanes].reshape(GRID_ROWS, LANES)
        centred, rate = head_stats(block, unit)
        normal = centred * rate
        product = incoming * normal
        gain_out[:, lanes] += jnp.sum(product, axis=0, keepdims=True)
        shift_out[:, lanes] += jnp.sum(incoming, axis=0, keepdims=True)
        inner = incoming * gain_ref[:, lanes]
        mean_inner = jnp.sum(inner, axis=-1, keepdims=True) * (1.0 / unit)
        mean_both = jnp.sum(inner * normal, axis=-1, keepdims=True) * (1.0 / unit)
        lane = lax.broadcasted_iota(jnp.int32, block.shape, 1)
        result = rate * (inner - mean_inner - normal * mean_both)
        result = jnp.where(lane < unit, result, 0.0)
        flat = result.reshape(FRAMES * SIDE, 8, LANES)
        shape = (FRAMES, SIDE, 8, LANES)
        grads[1, 1 : FRAMES + 1, 1 : SIDE + 1, :, lanes] = flat.reshape(shape)
        grads[0, 1 : FRAMES + 1, 1 : SIDE + 1, :, lanes] = pltpu.roll(flat, 1, 1).reshape(shape)
        grads[2, 1 : FRAMES + 1, 1 : SIDE + 1, :, lanes] = pltpu.roll(flat, 7, 1).reshape(shape)

    @pl.when(clip > 0)
    def _():
        finish_rows(clip - 1)

    pump(1)
    tap_grads(shifted, grads.at[1], taps_out)
    conv = shifted.at[1, 1 : FRAMES + 1, 1 : SIDE + 1]
    convolve(grads, taps, conv, True)
    for index in range(units):
        lanes = slice(index * LANES, (index + 1) * LANES)
        block = shifted[1, 1 : FRAMES + 1, 1 : SIDE + 1, :, lanes].reshape(GRID_ROWS, LANES)
        rows = dot_f32(outof_ref[...], block.astype(BF), ((1,), (0,))).astype(BF)
        pooled[:, lanes] = rows
        joined_out[:, lanes] += jnp.sum(rows.astype(F32), axis=0, keepdims=True)
    weight_sum[...] += dot_f32(normed_ref[0], pooled[...], ((0,), (0,)))
    result = dot_f32(pooled[...], weight_ref[...], ((1,), (1,))).astype(BF)
    cut = result.shape[1] // 2

    @pl.when(head_at == 0)
    def _():
        keep[clip] = result[:, :cut]
        cross_send[clip] = result[:, cut:]

    @pl.when(head_at == 1)
    def _():
        keep[clip] = result[:, cut:]
        cross_send[clip] = result[:, :cut]

    cross_copy(clip).start()

    @pl.when(clip == clips - 1)
    def _():
        weight_out[...] = weight_sum[...].astype(BF)
        finish_rows(clip)
        settle(chunks - 1)
        for chunk in range(early):
            each(1, outers, lambda step: far_copy(chunk, step).wait_recv())
            rest_out[:, chunk * cols : (chunk + 1) * cols] = lax.fori_loop(
                1,
                outers,
                lambda step, sums: sums + rest_far[chunk, step].astype(F32),
                rest_sum[chunk, outer].astype(F32),
            )
        for index in range(clips):
            grad_copy(index).wait_send()
            cross_copy(index).wait_send()
            mem_copy(index).wait()
            row_copy(index).wait()
        for chunk in range(chunks):
            over_copy(chunk).wait_send()
            rest_copy(chunk).wait_send()
        for chunk in range(early):
            each(1, outers, lambda step: far_copy(chunk, step).wait_send())


def whole_spec(shape):
    return pl.BlockSpec(shape, lambda clip: (0,) * len(shape))


def clip_spec(shape):
    return pl.BlockSpec((1,) + shape, lambda clip: (clip,) + (0,) * len(shape))


def once_spec(shape):
    return pl.BlockSpec(
        shape, lambda clip: (0,) * len(shape), pipeline_mode=pl.Buffered(1)
    )


def any_spec():
    return pl.BlockSpec(memory_space=pl.ANY)


def attention_forward(
    packed, mem_own, mem_peer, column, consts, taps, gains, shifts, bias, scale, unit, rows
):
    clips = packed.shape[0]
    heads = packed.shape[2] // (3 * LANES)
    into, outof, keyhot, mask, pad_row = consts
    wide = 3 * heads * LANES
    mem_shape = mem_own.shape[1:]
    outers = column.shape[0]
    dma = pltpu.SemaphoreType.DMA
    out = jax.ShapeDtypeStruct
    return pl.pallas_call(
        partial(forward_kernel, heads=heads, unit=unit, scale=scale),
        grid=(clips,),
        in_specs=[
            clip_spec((QROWS, wide)),
            clip_spec(mem_shape),
            clip_spec(mem_shape),
            once_spec(column.shape),
            whole_spec((GRID_ROWS, QROWS)),
            whole_spec((QROWS, GRID_ROWS)),
            whole_spec((27, wide)),
            whole_spec((1, wide)),
            whole_spec((1, wide)),
            clip_spec((BIAS_COLS, LANES)),
            whole_spec((BIAS_COLS, KROWS)),
            whole_spec((QROWS, BIAS_COLS)),
            whole_spec((1, BIAS_COLS)),
        ],
        out_specs=[
            clip_spec((rows, heads * unit)),
            any_spec(),
            any_spec(),
            clip_spec((QROWS, heads * LANES)),
            clip_spec((KROWS, heads * LANES)),
            clip_spec((KROWS, heads * LANES)),
            clip_spec((heads, QROWS, KROWS)),
            clip_spec((FRAMES, SIDE, 8, wide)),
        ],
        scratch_shapes=[
            pltpu.VMEM((3, FRAMES + 2, SIDE + 2, 8, wide), F32),
            pltpu.VMEM((27, 8, wide), F32),
            pltpu.VMEM((clips, rows, heads * unit), BF),
            dma((2, clips)),
            dma((2, outers)),
            dma((2, outers)),
            dma((2, outers)),
            pltpu.SemaphoreType.DMA,
        ],
        out_shape=[
            out((clips, rows, heads * unit), BF),
            out((clips, rows, heads * unit), BF),
            out((outers, 4) + column.shape[1:], BF),
            out((clips, QROWS, heads * LANES), BF),
            out((clips, KROWS, heads * LANES), BF),
            out((clips, KROWS, heads * LANES), BF),
            out((clips, heads, QROWS, KROWS), BF),
            out((clips, FRAMES, SIDE, 8, wide), F32),
        ],
        compiler_params=pltpu.CompilerParams(
            collective_id=1, has_side_effects=True, vmem_limit_bytes=VMEM_LIMIT
        ),
        name="pooled_attention_forward",
    )(
        packed, mem_own, mem_peer, column, into, outof, taps, gains, shifts, bias, keyhot, mask,
        pad_row,
    )


def attention_backward(
    packed, normed, weight, grad_own, grad_send, rest, consts, taps, gains, bias, saved, scale, unit
):
    clips, rows, width = grad_own.shape
    heads = width // unit
    model = weight.shape[0]
    half = model // 2
    into, outof, keyhot, mask, pad_row = consts
    wide = 3 * heads * LANES
    outers, _, shard_rows, rest_width = rest.shape
    chunks = 9
    early = 8
    cols = rest_width // chunks
    out = jax.ShapeDtypeStruct
    dma = pltpu.SemaphoreType.DMA
    return pl.pallas_call(
        partial(backward_kernel, heads=heads, unit=unit, scale=scale),
        grid=(clips,),
        in_specs=[
            clip_spec((QROWS, wide)),
            clip_spec((QROWS, model)),
            once_spec((model, wide)),
            clip_spec((rows, width)),
            any_spec(),
            any_spec(),
            once_spec((GRID_ROWS, QROWS)),
            once_spec((QROWS, GRID_ROWS)),
            once_spec((27, wide)),
            once_spec((1, wide)),
            clip_spec((BIAS_COLS, LANES)),
            once_spec((BIAS_COLS, KROWS)),
            once_spec((QROWS, BIAS_COLS)),
            clip_spec((QROWS, heads * LANES)),
            clip_spec((KROWS, heads * LANES)),
            clip_spec((KROWS, heads * LANES)),
            clip_spec((heads, QROWS, KROWS)),
            clip_spec((FRAMES, SIDE, 8, wide)),
        ],
        out_specs=[
            whole_spec((clips, rows, half)),
            any_spec(),
            clip_spec((MEM_BACK, 2 * heads * LANES)),
            any_spec(),
            whole_spec((27, 8, wide)),
            whole_spec((1, wide)),
            whole_spec((1, wide)),
            clip_spec((BIAS_COLS, LANES)),
            whole_spec((model, wide)),
            whole_spec((1, wide)),
            whole_spec((outers, shard_rows, cols)),
            whole_spec((shard_rows, early * cols)),
        ],
        scratch_shapes=[
            pltpu.VMEM((3, FRAMES + 2, SIDE + 2, 8, wide), F32),
            pltpu.VMEM((27, 8, wide), F32),
            pltpu.VMEM((3, FRAMES + 2, SIDE + 2, 8, wide), F32),
            pltpu.VMEM((QROWS, heads * LANES), BF),
            pltpu.VMEM((QROWS, wide), BF),
            pltpu.VMEM((clips, rows, width), BF),
            pltpu.VMEM((clips, MEM_BACK, 2 * heads * LANES), BF),
            pltpu.VMEM((chunks, outers, 2, shard_rows, cols), BF),
            pltpu.VMEM((chunks, outers, 2, shard_rows, cols), BF),
            pltpu.VMEM((chunks, outers, shard_rows, cols), BF),
            pltpu.VMEM((chunks, outers, shard_rows, cols), BF),
            pltpu.VMEM((chunks, outers, shard_rows, cols), BF),
            pltpu.VMEM((early, outers, shard_rows, cols), BF),
            pltpu.VMEM((model, wide), F32),
            pltpu.VMEM((clips, QROWS, half), BF),
            pltpu.VMEM((clips, QROWS, half), BF),
            pltpu.VMEM((clips, QROWS, half), BF),
            pltpu.VMEM((clips, rows, half), BF),
            dma((2, clips)),
            dma((2, clips)),
            dma((chunks,)),
            dma((2, chunks)),
            dma((2, chunks)),
            dma((2, early, outers)),
            dma((2, clips)),
            dma((2, clips)),
        ],
        out_shape=[
            out((clips, rows, half), BF),
            out((clips, rows, half), BF),
            out((clips, MEM_BACK, 2 * heads * LANES), BF),
            out((clips, MEM_BACK, 2 * heads * LANES), BF),
            out((27, 8, wide), F32),
            out((1, wide), F32),
            out((1, wide), F32),
            out((clips, BIAS_COLS, LANES), F32),
            out((model, wide), BF),
            out((1, wide), F32),
            out((outers, shard_rows, cols), BF),
            out((shard_rows, early * cols), F32),
        ],
        compiler_params=pltpu.CompilerParams(
            collective_id=2, has_side_effects=True, vmem_limit_bytes=VMEM_LIMIT
        ),
        name="pooled_attention_backward",
    )(
        packed, normed, weight, grad_own, grad_send, rest, into, outof, taps, gains, bias, keyhot,
        mask, *saved,
    )


def row_stats(values):
    width = values.shape[-1]
    centred = values - jnp.sum(values, axis=-1, keepdims=True) * (1.0 / width)
    variance = jnp.sum(centred * centred, axis=-1, keepdims=True) * (1.0 / width)
    return centred, lax.rsqrt(variance + 1e-06)


def each(low, high, act):
    def body(step, carry):
        act(step)
        return carry

    lax.fori_loop(low, high, body, 0)


def norm_rows(source, index, gain, shift, target, at):
    rows = source.shape[1]
    centred, rate = row_stats(source[index].astype(F32))
    target[index, at : at + rows] = (centred * rate * gain[...] + shift[...]).astype(BF)


def project_rows(normed, weight, bias, packed):
    def step(index):
        packed[index] = (dot_f32(normed[index], weight, ((1,), (0,))) + bias[...]).astype(BF)

    each(0, packed.shape[0], step)


def project_kernel(
    x, shards, gain, shift, bias, mem_send, rest, full, packed, normed, mem_peer, rest_column,
    x_peer, columns, far_sems, near_sems, x_sems, cross_sems, mem_sems, rest_sems, own_sem,
):
    outers, _, shard_rows, width = full.shape
    clips, rows, model = x.shape
    clip = lax.axis_index("clip")
    frame = lax.axis_index("frame")
    head = lax.axis_index("head")
    outer, inner = clip // 2, clip % 2
    place = inner * 2 + frame
    half = model // 2
    lanes = pl.ds(pl.multiple_of(head * half, LANES), half)
    barrier = pltpu.get_barrier_semaphore()

    def far_device(step):
        return device_of((outer + step) % outers, inner, frame, head)

    def near_device(step):
        there_inner, there_frame = plane_peer(inner, frame, step)
        return device_of(outer, there_inner, there_frame, head)

    def greet(device):
        pl.semaphore_signal(barrier, inc=1, device_id=device, device_id_type=MESH_ID)

    each(1, outers, lambda step: greet(far_device(step)))
    for step in range(1, 4):
        greet(near_device(step))
    greet((clip, frame, 1 - head))
    pl.semaphore_wait(barrier, outers - 1 + 4)

    def far_copy(step, at):
        return pltpu.make_async_remote_copy(
            src_ref=shards, dst_ref=columns.at[at],
            send_sem=far_sems.at[0, step], recv_sem=far_sems.at[1, step],
            device_id=far_device(step), device_id_type=MESH_ID,
        )

    def near_copy(index, step, source, at):
        return pltpu.make_async_remote_copy(
            src_ref=source.at[(frame + step % 2) % 2], dst_ref=full.at[at, place],
            send_sem=near_sems.at[0, index, step - 1], recv_sem=near_sems.at[1, index, step - 1],
            device_id=near_device(step), device_id_type=MESH_ID,
        )

    def near_arrival(index, step, at):
        there_inner, there_frame = plane_peer(inner, frame, step)
        return pltpu.make_async_remote_copy(
            src_ref=shards.at[0], dst_ref=full.at[at, there_inner * 2 + there_frame],
            send_sem=near_sems.at[0, index, step - 1], recv_sem=near_sems.at[1, index, step - 1],
            device_id=near_device(step), device_id_type=MESH_ID,
        )

    def x_copy(index):
        return partner_copy(
            x.at[index, :, lanes], x_peer.at[index, :, lanes], x_sems.at[0, index],
            x_sems.at[1, index],
        )

    def cross_copy(index):
        return pltpu.make_async_remote_copy(
            src_ref=x_peer.at[index, :, lanes], dst_ref=x_peer.at[index, :, lanes],
            send_sem=cross_sems.at[0, index], recv_sem=cross_sems.at[1, index],
            device_id=(clip, frame, 1 - head), device_id_type=MESH_ID,
        )

    def cross_arrival(index):
        other = pl.ds(pl.multiple_of((1 - head) * half, LANES), half)
        return pltpu.make_async_remote_copy(
            src_ref=x_peer.at[index, :, other], dst_ref=x_peer.at[index, :, other],
            send_sem=cross_sems.at[0, index], recv_sem=cross_sems.at[1, index],
            device_id=(clip, frame, 1 - head), device_id_type=MESH_ID,
        )

    mem_copy = partner_copy(mem_send, mem_peer, mem_sems.at[0], mem_sems.at[1])

    def rest_copy(step, at):
        return pltpu.make_async_remote_copy(
            src_ref=rest, dst_ref=rest_column.at[at],
            send_sem=rest_sems.at[0, step], recv_sem=rest_sems.at[1, step],
            device_id=far_device(step), device_id_type=MESH_ID,
        )

    own_copy = pltpu.make_async_copy(rest, rest_column.at[outer], own_sem)

    def origin(step):
        return (outer + outers - step) % outers

    each(1, outers, lambda step: far_copy(step, outer).start())
    for step in range(1, 4):
        near_copy(0, step, shards, outer).start()
    each(0, clips, lambda index: x_copy(index).start())
    mem_copy.start()
    own_copy.start()
    full[outer, place] = shards[frame]
    normed[...] = jnp.zeros_like(normed)
    each(0, clips, lambda index: norm_rows(x, index, gain, shift, normed, 0))

    def forward(index):
        at = origin(index)
        far_copy(index, at).wait_recv()
        for step in range(1, 4):
            near_copy(index, step, columns.at[at], at).start()
        full[at, place] = columns[at, frame]

    each(1, outers, forward)
    each(1, outers, lambda step: rest_copy(step, outer).start())

    def relay(index):
        x_copy(index).wait_recv()
        cross_copy(index).start()

    each(0, clips, relay)

    def receive(index):
        cross_arrival(index).wait_recv()
        norm_rows(x_peer, index, gain, shift, normed, HALF)

    each(0, clips, receive)

    def arrive(index):
        for step in range(1, 4):
            near_arrival(index, step, origin(index)).wait_recv()

    each(0, outers, arrive)
    project_rows(normed, full[...].reshape(outers * 4 * shard_rows, width), bias, packed)
    mem_copy.wait()
    own_copy.wait()
    each(1, outers, lambda step: rest_copy(step, origin(step)).wait_recv())
    each(1, outers, lambda step: rest_copy(step, outer).wait_send())
    each(1, outers, lambda step: far_copy(step, outer).wait_send())
    for step in range(1, 4):
        near_copy(0, step, shards, outer).wait_send()

    def sent(index):
        for step in range(1, 4):
            near_copy(index, step, columns.at[origin(index)], origin(index)).wait_send()

    each(1, outers, sent)

    def x_sent(index):
        x_copy(index).wait_send()
        cross_copy(index).wait_send()

    each(0, clips, x_sent)


def project_local_kernel(x, x_peer, weight, gain, shift, bias, packed, normed):
    normed[...] = jnp.zeros_like(normed)
    each(0, x.shape[0], lambda index: norm_rows(x, index, gain, shift, normed, 0))
    each(0, x.shape[0], lambda index: norm_rows(x_peer, index, gain, shift, normed, HALF))
    project_rows(normed, weight[...], bias, packed)


def swap(value, axis):
    return lax.ppermute(value, axis, [(0, 1), (1, 0)])


def project(x, shards, gain, shift, bias, mem_send, rest, clip_count):
    clips, rows, model = x.shape
    _, shard_rows, width = shards.shape
    outers = clip_count // 2
    out = jax.ShapeDtypeStruct
    dma = pltpu.SemaphoreType.DMA
    vmem = pl.BlockSpec(memory_space=pltpu.VMEM)
    shapes = [out((clips, QROWS, width), BF), out((clips, QROWS, model), BF)]
    if shard_rows % 16:
        full = lax.all_gather(shards, ("clip", "frame"), axis=1, tiled=True)
        full = lax.dynamic_index_in_dim(full, lax.axis_index("frame"), 0, keepdims=False)
        packed, normed = pl.pallas_call(
            project_local_kernel,
            in_specs=[vmem] * 6,
            out_specs=[vmem] * 2,
            out_shape=shapes,
            compiler_params=pltpu.CompilerParams(vmem_limit_bytes=VMEM_LIMIT),
            name="project_local",
        )(x, swap(x, "frame"), full, gain, shift, bias)
        column = lax.all_gather(rest, ("clip", "frame"), axis=0, tiled=False)
        column = column.reshape((outers, 4) + rest.shape)
        place = lax.axis_index("clip") % 2 * 2 + lax.axis_index("frame")
        column = lax.dynamic_index_in_dim(column, place, 1, keepdims=False)
        return full, packed, normed, swap(mem_send, "frame"), column
    hbm = pl.BlockSpec(memory_space=pl.ANY)
    full, packed, normed, mem_peer, column = pl.pallas_call(
        project_kernel,
        in_specs=[vmem] * 6 + [hbm],
        out_specs=[vmem] * 5,
        out_shape=[out((outers, 4) + shards.shape[1:], BF)]
        + shapes
        + [out(mem_send.shape, BF), out((outers,) + rest.shape, BF)],
        scratch_shapes=[
            pltpu.VMEM((clips, rows, model), BF),
            pltpu.VMEM((outers,) + shards.shape, BF),
            dma((2, outers)),
            dma((2, outers, 3)),
            dma((2, clips)),
            dma((2, clips)),
            dma((2,)),
            dma((2, outers)),
            pltpu.SemaphoreType.DMA,
        ],
        compiler_params=pltpu.CompilerParams(
            collective_id=3, has_side_effects=True, vmem_limit_bytes=VMEM_LIMIT
        ),
        name="gather_and_project",
    )(x, shards, gain, shift, bias, mem_send, rest)
    return full.reshape(model, width), packed, normed, mem_peer, column


def device_of(outer, inner, frame, head):
    return (outer * 2 + inner, frame, head)


def plane_peer(inner, frame, step):
    return (inner + step // 2) % 2, (frame + step % 2) % 2


def row_piece(value, row):
    return value[:, row * LANES : (row + 1) * LANES]


def tail_kernel(
    row_own, row_recv, x, middle_grad, grads, joined_sum, gain, taps, pool_gain, pool_shift,
    bias_grad, hot, space_hot, squeeze, vectors, up_bias, rest,
    grad_in, out, rest_out, small_out,
    near, part, far, small, small_in, row_full, rest_in,
    cross_sems, near_sems, far_sems, first_sems, second_sems, rest_sems,
    *, unit, plan, table_rows,
):
    chunks, outers, _, shard_rows, cols = part.shape
    clips, rows, model = x.shape
    half = model // 2
    devices = small.shape[0]
    clip = lax.axis_index("clip")
    frame = lax.axis_index("frame")
    head = lax.axis_index("head")
    outer, inner = clip // 2, clip % 2
    place = inner * 2 + frame
    mine = (clip * 2 + frame) * 2 + head

    def device(index):
        return (index // 4, (index // 2) % 2, index % 2)

    barrier = pltpu.get_barrier_semaphore()
    each(
        1,
        devices,
        lambda step: pl.semaphore_signal(
            barrier, inc=1, device_id=device((mine + step) % devices), device_id_type=MESH_ID
        ),
    )

    def first(step):
        other = (mine + step) % devices
        return pltpu.make_async_remote_copy(
            src_ref=small.at[other], dst_ref=small_in.at[step],
            send_sem=first_sems.at[0, step], recv_sem=first_sems.at[1, step],
            device_id=device(other), device_id_type=MESH_ID,
        )

    def second(step, block):
        return pltpu.make_async_remote_copy(
            src_ref=small_out.at[block], dst_ref=small_out.at[block],
            send_sem=second_sems.at[0, step], recv_sem=second_sems.at[1, step],
            device_id=device((mine + step) % devices), device_id_type=MESH_ID,
        )

    def near_copy(chunk, step):
        there_inner, there_frame = plane_peer(inner, frame, step)
        return pltpu.make_async_remote_copy(
            src_ref=grads.at[:, there_inner * 2 + there_frame, :, pl.ds(chunk * cols, cols)],
            dst_ref=near.at[chunk, step - 1],
            send_sem=near_sems.at[0, chunk, step - 1], recv_sem=near_sems.at[1, chunk, step - 1],
            device_id=device_of(outer, there_inner, there_frame, head), device_id_type=MESH_ID,
        )

    def far_copy(chunk, step):
        there = (outer + step) % outers
        return pltpu.make_async_remote_copy(
            src_ref=part.at[chunk, there], dst_ref=far.at[chunk, step],
            send_sem=far_sems.at[0, chunk, step], recv_sem=far_sems.at[1, chunk, step],
            device_id=device_of(there, inner, frame, head), device_id_type=MESH_ID,
        )

    def cross_copy(index, side):
        lanes = pl.ds(pl.multiple_of(side * half, LANES), half)
        return pltpu.make_async_remote_copy(
            src_ref=row_full.at[index, :, lanes], dst_ref=row_full.at[index, :, lanes],
            send_sem=cross_sems.at[0, index], recv_sem=cross_sems.at[1, index],
            device_id=(clip, frame, 1 - head), device_id_type=MESH_ID,
        )

    def rest_copy(step):
        there = (outer + step) % outers
        return pltpu.make_async_remote_copy(
            src_ref=rest.at[there], dst_ref=rest_in.at[step],
            send_sem=rest_sems.at[0, step], recv_sem=rest_sems.at[1, step],
            device_id=device_of(there, inner, frame, head), device_id_type=MESH_ID,
        )

    small[...] = jnp.zeros_like(small)
    pl.semaphore_wait(barrier, devices - 1)
    for chunk in range(chunks):
        for step in range(1, 4):
            near_copy(chunk, step).start()
    lanes_here = pl.ds(pl.multiple_of(head * half, LANES), half)

    def join(index):
        total = row_own[index].astype(F32) + row_recv[index].astype(F32)
        row_full[index, :, lanes_here] = total.astype(BF)
        cross_copy(index, head).start()

    each(0, clips, join)
    each(1, outers, lambda step: rest_copy(step).start())

    gain_sum = jnp.zeros((1, model), F32)
    shift_sum = jnp.zeros((1, model), F32)
    for index in range(clips):
        cross_copy(index, 1 - head).wait_recv()
        incoming = row_full[index].astype(F32)
        centred, rate = row_stats(x[index].astype(F32))
        normal = centred * rate
        product = incoming * normal
        gain_sum = gain_sum + jnp.sum(product, axis=0, keepdims=True)
        shift_sum = shift_sum + jnp.sum(incoming, axis=0, keepdims=True)
        scaled = incoming * gain[...]
        mean_scaled = jnp.sum(scaled, axis=-1, keepdims=True) * (1.0 / model)
        mean_both = jnp.sum(scaled * normal, axis=-1, keepdims=True) * (1.0 / model)
        result = rate * (scaled - mean_scaled - normal * mean_both) + middle_grad[index]
        grad_in[index] = result.astype(BF)

    rows_small = small.shape[1]

    def put(row, value):
        count = value.shape[0]
        done = 0
        while done < count:
            block, offset = divmod(row + done, rows_small)
            size = min(count - done, rows_small - offset)
            small[block, offset : offset + size, : value.shape[1]] = value[done : done + size]
            done += size

    def put_wide(row, value):
        for index in range(value.shape[1] // LANES):
            put(row + index, row_piece(value, index))

    wide_rows_count = model // LANES

    @pl.when(head == 0)
    def _():
        put_wide(plan["gain"], gain_sum)
        put_wide(plan["gain"] + wide_rows_count, vectors[0:1])
        put_wide(plan["shift"], shift_sum)
        put_wide(plan["shift"] + wide_rows_count, vectors[1:2])
        put_wide(plan["rows"], vectors[2:3])
        put_wide(plan["rows"] + wide_rows_count, vectors[3:4])

    joined_rows = joined_sum.shape[1] // LANES
    up_rows = up_bias.shape[1] // LANES
    for which in range(2):

        @pl.when(head == which)
        def _():
            for side in range(2):

                @pl.when(frame == side)
                def _():
                    put_wide(plan["joined"] + (2 * which + side) * joined_rows, joined_sum[...])

            put_wide(plan["up"] + which * up_rows, up_bias[...])

    heads = taps.shape[2] // (3 * LANES)
    tap_sum = jnp.sum(taps[...], axis=1)
    for member in range(3):
        totals = []
        for value in (tap_sum, pool_gain[...], pool_shift[...]):
            total = row_piece(value, member * heads)
            for index in range(1, heads):
                total = total + row_piece(value, member * heads + index)
            totals.append(total)
        put(plan["taps"] + member * 27, totals[0])
        put(plan["pool_gain"] + member, totals[1])
        put(plan["pool_shift"] + member, totals[2])
    put(plan["squeeze"], squeeze[...])
    time_sum = jnp.zeros((hot.shape[2], LANES), F32)
    bias_sum = jnp.zeros((BIAS_COLS, LANES), F32)
    for index in range(clips):
        value = bias_grad[index]
        bias_sum = bias_sum + value
        value = value[: hot.shape[1]]
        high = value.astype(BF)
        low = (value - high.astype(F32)).astype(BF)
        time_sum = time_sum + dot_f32(hot[index], high, ((0,), (0,)))
        time_sum = time_sum + dot_f32(hot[index], low, ((0,), (0,)))
    put(plan["time"], time_sum[:table_rows])
    high = bias_sum.astype(BF)
    low = (bias_sum - high.astype(F32)).astype(BF)
    space_sum = dot_f32(space_hot[...], high, ((1,), (0,)))
    space_sum = space_sum + dot_f32(space_hot[...], low, ((1,), (0,)))
    put(plan["space"], space_sum[: 2 * (2 * SIDE - 1)])

    each(1, devices, lambda step: first(step).start())

    def reduce_near(chunk):
        lanes = slice(chunk * cols, (chunk + 1) * cols)
        for step in range(1, 4):
            near_copy(chunk, step).wait_recv()

        def gathered(index):
            own = grads[index, place, :, lanes].astype(F32)
            own = own + near[chunk, 1, index].astype(F32)
            other = near[chunk, 0, index].astype(F32) + near[chunk, 2, index].astype(F32)
            return own, other

        def send(step):
            there = (outer + step) % outers
            own, other = gathered(there)
            part[chunk, there, 0] = own.astype(BF)
            part[chunk, there, 1] = other.astype(BF)
            far_copy(chunk, step).start()

        each(1, outers, send)
        own, other = gathered(outer)
        far[chunk, 0, 0] = own.astype(BF)
        far[chunk, 0, 1] = other.astype(BF)

    reduce_near(0)
    each(1, devices, lambda step: first(step).wait_recv())
    total = lax.fori_loop(1, devices, lambda step, sums: sums + small_in[step], small[mine])
    small_out[mine] = total
    each(1, devices, lambda step: second(step, mine).start())
    for chunk in range(1, chunks):
        reduce_near(chunk)
    heads = cols // LANES
    group = heads * unit
    for chunk in range(chunks):
        each(1, outers, lambda step: far_copy(chunk, step).wait_recv())
        totals = []
        for side in range(2):
            totals.append(
                lax.fori_loop(
                    0,
                    outers,
                    lambda step, sums: sums + far[chunk, step, side].astype(F32),
                    jnp.zeros((shard_rows, cols), F32),
                )
            )

        def store(order):
            for spot, side in enumerate(order):
                for index in range(heads):
                    at = (2 * chunk + spot) * group + index * unit
                    value = totals[side][:, index * LANES : index * LANES + unit]
                    out[:, at : at + unit] = value

        @pl.when(frame == 0)
        def _():
            store((0, 1))

        @pl.when(frame == 1)
        def _():
            store((1, 0))

    each(1, outers, lambda step: rest_copy(step).wait_recv())
    rest_out[...] = lax.fori_loop(
        1,
        outers,
        lambda step, sums: sums + rest_in[step].astype(F32),
        rest[outer].astype(F32),
    )
    each(1, devices, lambda step: second(step, (mine + devices - step) % devices).wait_recv())
    each(1, devices, lambda step: first(step).wait_send())
    each(1, devices, lambda step: second(step, mine).wait_send())
    each(1, outers, lambda step: rest_copy(step).wait_send())
    for index in range(clips):
        cross_copy(index, head).wait_send()
    for chunk in range(chunks):
        for step in range(1, 4):
            near_copy(chunk, step).wait_send()
        each(1, outers, lambda step: far_copy(chunk, step).wait_send())


def unpack_kernel(
    small, qkv, early, late, grad_in, block_out,
    grad_in_out, block_out_out, gain_out, shift_out, rows_out, joined_out, up_out, taps_out,
    pool_gain_out, pool_shift_out, squeeze_out, time_out, space_out, qkv_out, proj_out,
    up_grad_out, down_out, *, plan, unit,
):
    for index in range(grad_in.shape[0]):
        grad_in_out[index] = grad_in[index]
        block_out_out[index] = block_out[index]
    head = lax.axis_index("head")
    rows_small = small.shape[1]

    def take(row, target):
        count = target.shape[0]
        done = 0
        while done < count:
            block, offset = divmod(row + done, rows_small)
            size = min(count - done, rows_small - offset)
            target[done : done + size] = small[block, offset : offset + size, : target.shape[1]]
            done += size

    def take_wide(row, target, at):
        for index in range(target.shape[1] // LANES):
            block, offset = divmod(row + index, rows_small)
            target[at : at + 1, index * LANES : (index + 1) * LANES] = small[
                block, offset : offset + 1
            ]

    per_row = gain_out.shape[1] // LANES
    for index in range(2):
        take_wide(plan["gain"] + index * per_row, gain_out, index)
        take_wide(plan["shift"] + index * per_row, shift_out, index)
        take_wide(plan["rows"] + index * per_row, rows_out, index)
    width = joined_out.shape[1]
    group = width // 2
    heads = group // unit
    joined_rows = 3 * heads
    up_rows = up_out.shape[1] // LANES
    for which in range(2):

        @pl.when(head == which)
        def _():
            for member in range(3):
                for side in range(2):
                    for index in range(heads):
                        row = plan["joined"] + (2 * which + side) * joined_rows
                        block, offset = divmod(row + member * heads + index, rows_small)
                        at = side * group + index * unit
                        joined_out[member : member + 1, at : at + unit] = small[
                            block, offset : offset + 1, :unit
                        ]
            take_wide(plan["up"] + which * up_rows, up_out, 0)

    for member in range(3):
        take(plan["taps"] + member * 27, taps_out.at[member])
        qkv_out[:, member, :] = qkv[:, member * width : (member + 1) * width]
    take(plan["pool_gain"], pool_gain_out)
    take(plan["pool_shift"], pool_shift_out)
    take(plan["time"], time_out)
    for index in range(2):
        count = squeeze_out.shape[1]
        take(plan["squeeze"] + index * count, squeeze_out.at[index])
        count = space_out.shape[1]
        take(plan["space"] + index * count, space_out.at[index])
    proj_width, up_width = proj_out.shape[0], up_grad_out.shape[1]
    proj_out[...] = early[:, :proj_width].T
    up_grad_out[...] = early[:, proj_width : proj_width + up_width]
    at = proj_width + up_width
    first = early.shape[1] - at
    down_out[:first] = early[:, at:].T
    down_out[first:] = late[...].T


def unpack(small, qkv, early, late, grad_in, block_out, plan, unit, hidden_width, table_rows):
    shard_rows, width = qkv.shape
    model = grad_in.shape[2]
    rest_width = early.shape[1] + late.shape[1]
    out = jax.ShapeDtypeStruct
    vmem = pl.BlockSpec(memory_space=pltpu.VMEM)
    shapes = [
        out(grad_in.shape, BF),
        out(block_out.shape, BF),
        out((2, model), F32),
        out((2, model), F32),
        out((2, model), F32),
        out((3, width // 3), F32),
        out((1, hidden_width), F32),
        out((3, 27, unit), F32),
        out((3, unit), F32),
        out((3, unit), F32),
        out((2, FRAMES // MEMF, unit), F32),
        out((table_rows, unit), F32),
        out((2, 2 * SIDE - 1, unit), F32),
        out((shard_rows, 3, width // 3), F32),
        out((rest_width - 2 * hidden_width, shard_rows), F32),
        out((shard_rows, hidden_width), F32),
        out((hidden_width, shard_rows), F32),
    ]
    return pl.pallas_call(
        partial(unpack_kernel, plan=plan, unit=unit),
        in_specs=[vmem] * 6,
        out_specs=[vmem] * len(shapes),
        out_shape=shapes,
        compiler_params=pltpu.CompilerParams(vmem_limit_bytes=VMEM_LIMIT),
        name="unpack_results",
    )(small, qkv, early, late, grad_in, block_out)


def tail(
    row_own, row_recv, x, middle_grad, grads, joined_sum, gain, taps, pool_gain, pool_shift,
    bias_grad, hot, space_hot, squeeze, vectors, up_bias, rest, clip_count, devices, unit,
    table_rows,
):
    clips, rows, model = x.shape
    wide = grads.shape[3]
    heads = wide // (3 * LANES)
    width = 3 * 2 * heads * unit
    outers = clip_count // 2
    shard_rows = model // (4 * outers)
    chunks = 3
    cols = wide // chunks
    plan = {}
    at = 0
    for name, count in (
        ("gain", 2 * model // LANES),
        ("shift", 2 * model // LANES),
        ("rows", 2 * model // LANES),
        ("joined", 4 * wide // LANES),
        ("up", 2 * up_bias.shape[1] // LANES),
        ("taps", 81),
        ("pool_gain", 3),
        ("pool_shift", 3),
        ("squeeze", squeeze.shape[0]),
        ("time", table_rows),
        ("space", 2 * (2 * SIDE - 1)),
    ):
        plan[name] = at
        at += count
    block = -(-at // (devices * 8)) * 8
    out = jax.ShapeDtypeStruct
    dma = pltpu.SemaphoreType.DMA
    vmem = pl.BlockSpec(memory_space=pltpu.VMEM)
    shapes = [
        out((clips, rows, model), BF),
        out((shard_rows, width), F32),
        out((shard_rows, rest.shape[2]), F32),
        out((devices, block, LANES), F32),
    ]
    results = pl.pallas_call(
        partial(tail_kernel, unit=unit, plan=plan, table_rows=table_rows),
        in_specs=[vmem] * 17,
        out_specs=[vmem] * len(shapes),
        out_shape=shapes,
        scratch_shapes=[
            pltpu.VMEM((chunks, 3, outers, shard_rows, cols), BF),
            pltpu.VMEM((chunks, outers, 2, shard_rows, cols), BF),
            pltpu.VMEM((chunks, outers, 2, shard_rows, cols), BF),
            pltpu.VMEM((devices, block, LANES), F32),
            pltpu.VMEM((devices, block, LANES), F32),
            pltpu.VMEM((clips, rows, model), BF),
            pltpu.VMEM(rest.shape, BF),
            dma((2, clips)),
            dma((2, chunks, 3)),
            dma((2, chunks, outers)),
            dma((2, devices)),
            dma((2, devices)),
            dma((2, outers)),
        ],
        compiler_params=pltpu.CompilerParams(
            collective_id=0, has_side_effects=True, vmem_limit_bytes=VMEM_LIMIT
        ),
        name="tail_gradients",
    )(
        row_own, row_recv, x, middle_grad, grads, joined_sum, gain, taps, pool_gain, pool_shift,
        bias_grad, hot, space_hot, squeeze, vectors, up_bias, rest,
    )
    return results, plan


def feed_kernel(
    att_own, att_recv, x, cot, weights, gain, shift, out_shift, up_shift,
    block_out, middle_grad, grad_own, grad_send, grad_rest, vectors, up_bias,
    attended, normed, cots, active, hidden_low, branch, middle, send, recv, sems,
):
    clips, rows, model = x.shape
    span = attended.shape[0] // clips
    group = att_own.shape[2]
    head_width = 2 * group
    hidden_width = up_shift.shape[1]
    tiles = 4
    tile = hidden_width // tiles
    clip_at = lax.axis_index("clip")
    frame = lax.axis_index("frame")
    head = lax.axis_index("head")
    partner = (clip_at, frame, 1 - head)

    def cross(kind, index):
        return pltpu.make_async_remote_copy(
            src_ref=send.at[kind, index], dst_ref=recv.at[kind, index],
            send_sem=sems.at[0, kind, index], recv_sem=sems.at[1, kind, index],
            device_id=partner, device_id_type=MESH_ID,
        )

    barrier = pltpu.get_barrier_semaphore()
    pl.semaphore_signal(barrier, inc=1, device_id=partner, device_id_type=MESH_ID)
    for ref in (attended, normed, cots, branch):
        ref[...] = jnp.zeros_like(ref)

    def assemble(low, high):
        for index in range(clips):
            at = slice(index * span, index * span + rows)
            attended[at, :group] = low[index]
            attended[at, group:] = high[index]

    @pl.when(frame == 0)
    def _():
        assemble(att_own, att_recv)

    @pl.when(frame == 1)
    def _():
        assemble(att_recv, att_own)

    for index in range(clips):
        cots[index * span : index * span + rows] = cot[index]
    pl.semaphore_wait(barrier, 1)

    def block_rows(index):
        return pl.ds(pl.multiple_of(index * span, 16), span)

    def project(index):
        part = dot_f32(attended[block_rows(index)], weights[:, :head_width], ((1,), (1,)))
        send[0, index] = part[:rows].astype(BF)
        cross(0, index).start()

    each(0, clips, project)

    def feed(index, bias_sum):
        cross(0, index).wait_recv()
        branch_rows = send[0, index].astype(F32) + recv[0, index].astype(F32)
        value = x[index].astype(F32) + branch_rows + out_shift[0:1]
        middle[index] = value
        centred, rate = row_stats(value)
        low = (centred * rate * gain[...] + shift[...]).astype(BF)
        at = pl.multiple_of(index * span, 16)
        normed[pl.ds(at, rows)] = low
        low = normed[block_rows(index)]
        cot_rows = cots[block_rows(index)]
        out_part = jnp.zeros((span, model), F32)
        norm_part = jnp.zeros((span, model), F32)
        sums = []
        for step in range(tiles):
            lanes = slice(step * tile, (step + 1) * tile)
            up = weights[:, head_width + step * tile : head_width + (step + 1) * tile]
            at = head_width + hidden_width + step * tile
            down = weights[:, at : at + tile]
            hidden = dot_f32(low, up, ((1,), (0,))) + up_shift[:, lanes]
            incoming = dot_f32(cot_rows, down, ((1,), (0,)))
            normal = 0.5 * (1.0 + lax.erf(hidden * (0.5**0.5)))
            density = jnp.exp(hidden * hidden * -0.5) * ((2.0 * np.pi) ** -0.5)
            acted = (hidden * normal).astype(BF)
            back = (incoming * (normal + hidden * density)).astype(BF)
            active[block_rows(index), lanes] = acted
            hidden_low[block_rows(index), lanes] = back
            sums.append(jnp.sum(back.astype(F32), axis=0, keepdims=True))
            out_part = out_part + dot_f32(acted, down, ((1,), (1,)))
            norm_part = norm_part + dot_f32(back, up, ((1,), (1,)))
        send[1, index] = norm_part[:rows].astype(BF)
        cross(1, index).start()
        send[2, index] = out_part[:rows].astype(BF)
        cross(2, index).start()
        return bias_sum + jnp.concatenate(sums, axis=1)

    up_bias[...] = lax.fori_loop(0, clips, feed, jnp.zeros((1, hidden_width), F32))

    for step in range(tiles):
        lanes = slice(step * tile, (step + 1) * tile)
        value = dot_f32(normed[...], hidden_low[:, lanes], ((0,), (0,)))
        at = head_width + step * tile
        grad_rest[:, at : at + tile] = value.astype(BF)
        value = dot_f32(cots[...], active[:, lanes], ((0,), (0,)))
        at = head_width + hidden_width + step * tile
        grad_rest[:, at : at + tile] = value.astype(BF)

    def back(index, sums):
        gain_sum, shift_sum, first_sum, second_sum = sums
        cross(1, index).wait_recv()
        incoming = send[1, index].astype(F32) + recv[1, index].astype(F32)
        centred, rate = row_stats(middle[index])
        normal = centred * rate
        scaled = incoming * gain[...]
        mean_scaled = jnp.sum(scaled, axis=-1, keepdims=True) * (1.0 / model)
        mean_both = jnp.sum(scaled * normal, axis=-1, keepdims=True) * (1.0 / model)
        cot_rows = cot[index].astype(F32)
        value = cot_rows + rate * (scaled - mean_scaled - normal * mean_both)
        middle_grad[index] = value
        at = pl.multiple_of(index * span, 16)
        branch[pl.ds(at, rows)] = value.astype(BF)
        part = dot_f32(branch[block_rows(index)], weights[:, :head_width], ((1,), (0,)))
        part = part[:rows].astype(BF)

        @pl.when(frame == 0)
        def _():
            grad_own[index] = part[:, :group]
            grad_send[index] = part[:, group:]

        @pl.when(frame == 1)
        def _():
            grad_send[index] = part[:, :group]
            grad_own[index] = part[:, group:]

        cross(2, index).wait_recv()
        out_rows = send[2, index].astype(F32) + recv[2, index].astype(F32)
        block_out[index] = (middle[index] + out_rows + out_shift[1:2]).astype(BF)

        def column(rows_here):
            return jnp.sum(rows_here, axis=0, keepdims=True)

        return (
            gain_sum + column(incoming * normal),
            shift_sum + column(incoming),
            first_sum + column(value),
            second_sum + column(cot_rows),
        )

    start = tuple(jnp.zeros((1, model), F32) for _ in range(4))
    sums = lax.fori_loop(0, clips, back, start)
    for row in range(4):
        vectors[row : row + 1] = sums[row]
    value = dot_f32(branch[...], attended[...], ((0,), (0,)))
    grad_rest[:, :head_width] = value.astype(BF)
    for kind in range(3):
        each(0, clips, lambda index: cross(kind, index).wait_send())


def feed(att_own, att_recv, x, cot, weights, gain, shift, out_shift, up_shift):
    clips, rows, model = x.shape
    group = att_own.shape[2]
    hidden_width = up_shift.shape[1]
    span = -(-rows // 16) * 16
    out = jax.ShapeDtypeStruct
    vmem = pl.BlockSpec(memory_space=pltpu.VMEM)
    shapes = [
        out((clips, rows, model), BF),
        out((clips, rows, model), F32),
        out((clips, rows, group), BF),
        out((clips, rows, group), BF),
        out(weights.shape, BF),
        out((4, model), F32),
        out((1, hidden_width), F32),
    ]
    return pl.pallas_call(
        feed_kernel,
        in_specs=[vmem] * 9,
        out_specs=[vmem] * len(shapes),
        out_shape=shapes,
        scratch_shapes=[
            pltpu.VMEM((clips * span, 2 * group), BF),
            pltpu.VMEM((clips * span, model), BF),
            pltpu.VMEM((clips * span, model), BF),
            pltpu.VMEM((clips * span, hidden_width), BF),
            pltpu.VMEM((clips * span, hidden_width), BF),
            pltpu.VMEM((clips * span, model), BF),
            pltpu.VMEM((clips, rows, model), F32),
            pltpu.VMEM((3, clips, rows, model), BF),
            pltpu.VMEM((3, clips, rows, model), BF),
            pltpu.SemaphoreType.DMA((2, 3, clips)),
        ],
        compiler_params=pltpu.CompilerParams(
            collective_id=4, has_side_effects=True, vmem_limit_bytes=VMEM_LIMIT
        ),
        name="feed_forward_both_ways",
    )(att_own, att_recv, x, cot, weights, gain, shift, out_shift, up_shift)


def precise(pattern, *operands):
    return jnp.einsum(pattern, *operands, precision=lax.Precision.HIGHEST)


def split_groups(value, which, axis):
    half = value.shape[axis] // 2
    low = lax.slice_in_dim(value, 0, half, axis=axis)
    high = lax.slice_in_dim(value, half, None, axis=axis)
    first = which == 0
    return jnp.where(first, low, high), jnp.where(first, high, low)


def join_groups(own, peer, which, axis):
    first = which == 0
    return jnp.concatenate([jnp.where(first, own, peer), jnp.where(first, peer, own)], axis=axis)


def time_choices(stride_group, memory_place, which, own, table_rows):
    local = jnp.arange(own, dtype=jnp.int32)
    times = jnp.concatenate([which * own + local, (1 - which) * own + local])
    stride = jnp.left_shift(jnp.int32(2), stride_group)[:, None, None]
    offset = 8 * (FRAMES - 1)
    current = stride * (times[None, :, None] - times[None, None, :]) + offset
    first = memory_place[:, np.array([2, 0, 3, 1])]
    second = memory_place[:, np.array([3, 1, 2, 0])]
    places = jnp.where(which == 0, first, second)
    memory = stride * times[None, :, None] + places[:, None, :] + offset
    chosen = jnp.concatenate([current, memory], axis=2)
    return (chosen[..., None] == jnp.arange(table_rows, dtype=jnp.int32)).astype(F32)


def space_choices():
    places = np.arange(SIDE)
    offsets = places[:, None] - places[None, :] + SIDE - 1
    hot = offsets.reshape(-1)[:, None] == np.arange(2 * SIDE - 1)[None, :]
    return jnp.asarray(hot.astype(np.float32))


def space_sums():
    spans = 2 * SIDE - 1
    hot = np.zeros((32, BIAS_COLS), np.float32)
    for axis in range(2):
        for query in range(SIDE):
            for key in range(SIDE):
                col = SPACE_AT + axis * CELLS + query * SIDE + key
                hot[axis * spans + query - key + SIDE - 1, col] = 1.0
    return hot


def wide_rows(rows, heads):
    count, members, unit = rows.shape
    padded = jnp.pad(rows, ((0, 0), (0, 0), (0, LANES - unit)))
    spread = jnp.broadcast_to(padded[:, :, None], (count, members, heads, LANES))
    return spread.reshape(count, members * heads * LANES)


def local(
    clips_in,
    cached_kv,
    old_memory,
    stride_group,
    memory_place,
    norm_gain,
    norm_shift,
    qkv_weight,
    qkv_shift,
    pool_kernel,
    pool_gain,
    pool_shift,
    squeeze_kernel,
    time_table,
    space_tables,
    proj_weight,
    out_shift,
    up_weight,
    up_shift,
    down_weight,
    cotangent,
):
    clip_count, rows_clip, model_width = clips_in.shape
    head_width = qkv_weight.shape[2]
    unit = pool_gain.shape[1]
    head_count = head_width // unit
    frame_count = lax.axis_size("frame")
    heads = head_count // frame_count
    own_frames = rows_clip // CELLS
    group_width = heads * unit
    group_span = FRAMES // MEMF
    scale = unit ** (-0.5)
    which = lax.axis_index("frame")
    into_np, outof_np = placement(frame_count)
    keys_np, mask_np, pad_np = bias_constants(frame_count)
    consts = (
        jnp.where(which == 0, jnp.asarray(into_np[0], BF), jnp.asarray(into_np[1], BF)),
        jnp.where(which == 0, jnp.asarray(outof_np[0], BF), jnp.asarray(outof_np[1], BF)),
        jnp.asarray(keys_np, BF),
        jnp.asarray(mask_np),
        jnp.asarray(pad_np),
    )

    shards = jnp.concatenate([proj_weight.T, up_weight, down_weight.T], axis=1)

    cached_wide = cached_kv.astype(F32).reshape(
        clip_count, group_span, CELLS, 2, head_count, unit
    )
    squeezed = precise("cjsxnd,xjd->csxnd", cached_wide, squeeze_kernel).astype(BF)
    memory_rows = jnp.concatenate(
        [squeezed.reshape(clip_count, CELLS, 2, head_width), old_memory], axis=1
    )
    mem_own, mem_send = split_groups(memory_rows, which, 3)
    mem_own = mem_own.reshape(clip_count, -1, 2 * group_width)
    mem_send = mem_send.reshape(clip_count, -1, 2 * group_width)

    def padded_heads(value):
        value = value.reshape(value.shape[0], 3, frame_count, heads, unit)
        value = jnp.pad(value, ((0, 0),) * 4 + ((0, LANES - unit),))
        return value.transpose(2, 0, 1, 3, 4).reshape(frame_count, -1, 3 * heads * LANES)

    bias_pair = padded_heads(qkv_shift[None])
    attn_group, packed, normed, mem_peer, column = project(
        clips_in, padded_heads(qkv_weight), norm_gain[:1], norm_shift[:1],
        jnp.where(which == 0, bias_pair[0], bias_pair[1]), mem_send, shards,
        lax.axis_size("clip"),
    )

    time_hot = time_choices(stride_group, memory_place, which, own_frames, time_table.shape[0])
    time_rows = precise("ctkr,rd->ctkd", time_hot, time_table).reshape(clip_count, -1, unit)
    space_hot = space_choices()
    space_rows = precise("pr,xrd->xpd", space_hot, space_tables).reshape(2 * CELLS, unit)
    bias = jnp.zeros((clip_count, BIAS_COLS, LANES), F32)
    bias = bias.at[:, : time_rows.shape[1], :unit].set(time_rows)
    bias = bias.at[:, SPACE_AT : SPACE_AT + 2 * CELLS, :unit].set(space_rows[None])
    bias = bias * (1.0 / scale)
    taps = wide_rows(pool_kernel.transpose(1, 0, 2), heads)
    gains = wide_rows(pool_gain[None], heads)
    shifts = wide_rows(pool_shift[None], heads)

    forward = attention_forward(
        packed, mem_own, mem_peer, column, consts, taps, gains, shifts, bias, scale, unit, rows_clip
    )
    attended_own, attended_peer, rest_full = forward[:3]
    rest_full = rest_full.reshape(model_width, -1)
    saved = forward[3:]
    block_out, middle_grad, attended_grad_own, attended_grad_send, grad_rest, vectors, up_grads = (
        feed(
            attended_own, attended_peer, clips_in, cotangent, rest_full, norm_gain[1:],
            norm_shift[1:], out_shift, up_shift.reshape(1, -1),
        )
    )
    outers = lax.axis_size("clip") // 2
    grad_rest = grad_rest.reshape(outers, 4, -1, grad_rest.shape[1])
    backward = attention_backward(
        packed, normed, attn_group, attended_grad_own, attended_grad_send, grad_rest, consts, taps,
        gains, bias, saved, scale, unit,
    )
    row_own, row_recv, mem_grad_own, mem_grad_peer = backward[:4]
    taps_grad, pool_gain_grad, pool_shift_grad, bias_grad = backward[4:8]
    attn_grad, joined_grad, rest_part, rest_early = backward[8:]

    mem_grads = [
        part[:, :CELLS].reshape(clip_count, CELLS, 2, heads, LANES)[..., :unit]
        for part in (mem_grad_own, mem_grad_peer)
    ]
    squeezed_grads = join_groups(mem_grads[0], mem_grads[1], which, 3).astype(F32)
    grad_squeeze = precise("cjsxnd,csxnd->xjd", cached_wide, squeezed_grads)
    time_count = time_rows.shape[1]
    hot = time_hot.reshape(clip_count, time_count, -1).astype(BF)
    hot = jnp.pad(hot, ((0, 0), (0, 0), (0, -hot.shape[2] % LANES)))
    devices = lax.axis_size("clip") * frame_count * lax.axis_size("head")
    (grad_in, qkv_shard, rest_late, small), plan = tail(
        row_own, row_recv, clips_in, middle_grad,
        attn_grad.reshape(outers, 4, -1, attn_grad.shape[1]), joined_grad, norm_gain[:1], taps_grad,
        pool_gain_grad, pool_shift_grad, bias_grad, hot,
        jnp.asarray(space_sums(), BF), grad_squeeze.reshape(-1, unit), vectors,
        up_grads, rest_part, lax.axis_size("clip"), devices, unit, time_table.shape[0],
    )
    (
        grad_in, block_out, gain_sums, shift_sums, out_sums, qkv_bias_sum, up_bias_sum, kernel_sum,
        pool_gain_sum, pool_shift_sum, squeeze_sum, time_sum, space_sum, qkv_shard, proj_shard,
        up_shard, down_shard,
    ) = unpack(
        small, qkv_shard, rest_early, rest_late, grad_in, block_out, plan, unit,
        up_weight.shape[1], time_table.shape[0],
    )
    return (
        block_out,
        grad_in,
        gain_sums,
        shift_sums,
        qkv_shard,
        qkv_bias_sum,
        kernel_sum,
        pool_gain_sum,
        pool_shift_sum,
        squeeze_sum,
        time_sum,
        space_sum,
        proj_shard,
        out_sums,
        up_shard,
        up_bias_sum.reshape(-1),
        down_shard,
    )


def solution(mesh):
    return jax.shard_map(
        local,
        mesh=mesh,
        in_specs=(
            P("clip", "frame", None),
            P("clip", "frame", None, "head"),
            P("clip", "frame", None, "head"),
            P("clip"),
            P("clip", None),
            P(),
            P(),
            P(("clip", "frame"), None, "head"),
            P(None, "head"),
            P(),
            P(),
            P(),
            P(),
            P(),
            P(),
            P("head", ("clip", "frame")),
            P(),
            P(("clip", "frame"), "head"),
            P("head"),
            P("head", ("clip", "frame")),
            P("clip", "frame", None),
        ),
        out_specs=(
            P("clip", "frame", None),
            P("clip", "frame", None),
            P(),
            P(),
            P(("clip", "frame"), None, "head"),
            P(None, "head"),
            P(),
            P(),
            P(),
            P(),
            P(),
            P(),
            P("head", ("clip", "frame")),
            P(),
            P(("clip", "frame"), "head"),
            P("head"),
            P("head", ("clip", "frame")),
        ),
        check_vma=False,
    )
```

```python
from functools import partial

import jax
import jax.numpy as jnp
import numpy as np
from jax import lax
from jax.experimental import pallas as pl
from jax.experimental.pallas import tpu as pltpu
from jax.sharding import PartitionSpec as P

FRAMES = 8
MEMF = 2
SIDE = 7
CELLS = SIDE * SIDE
LANES = 128
HALF = 208
QROWS = 2 * HALF
GRID_ROWS = FRAMES * SIDE * 8
MEM_AT = QROWS
MEM_PAD = 112
MEM_BACK = 64
MEM_STEP = 56
TURN_STEP = 3
KROWS = 640
BIAS_COLS = 256
SPACE_AT = 128
PAD_LANE = 127
BF = jnp.bfloat16
F32 = jnp.float32
VMEM_LIMIT = 60 * 1024 * 1024
MESH_ID = pl.DeviceIdType.MESH


def dot_f32(a, b, dims):
    return lax.dot_general(a, b, (dims, ((), ())), preferred_element_type=F32)


def frame_order(first, own):
    rest = [t for t in range(FRAMES) if not first * own <= t < (first + 1) * own]
    return list(range(first * own, (first + 1) * own)) + rest


def placement(frame_count):
    own = FRAMES // frame_count
    into = np.zeros((frame_count, GRID_ROWS, QROWS), np.float32)
    for first in range(frame_count):
        for slot, frame in enumerate(frame_order(first, own)):
            base = (slot // own) * HALF + (slot % own) * CELLS
            for high in range(SIDE):
                for wide in range(SIDE):
                    row = (frame * SIDE + high) * 8 + wide
                    into[first, row, base + high * SIDE + wide] = 1.0
    return into, np.ascontiguousarray(into.transpose(0, 2, 1))


def bias_constants(frame_count):
    own = FRAMES // frame_count
    frames_all = FRAMES + 2 * MEMF
    keys = np.zeros((BIAS_COLS, KROWS), np.float32)
    valid = np.zeros((KROWS,), bool)

    def mark(col, slot, high, wide):
        valid[col] = True
        for query in range(FRAMES):
            keys[query * frames_all + slot, col] = 1.0
        for place in range(SIDE):
            keys[SPACE_AT + place * SIDE + high, col] = 1.0
            keys[SPACE_AT + CELLS + place * SIDE + wide, col] = 1.0

    mask = np.zeros((QROWS, BIAS_COLS), np.float32)
    for slot in range(FRAMES):
        base = (slot // own) * HALF + (slot % own) * CELLS
        for high in range(SIDE):
            for wide in range(SIDE):
                row = base + high * SIDE + wide
                mark(row, slot, high, wide)
                mask[row, slot * frames_all : (slot + 1) * frames_all] = 1.0
                mask[row, SPACE_AT + high * SIDE : SPACE_AT + (high + 1) * SIDE] = 1.0
                low = SPACE_AT + CELLS + wide * SIDE
                mask[row, low : low + SIDE] = 1.0
    for group in range(2):
        for inner in range(MEMF):
            slot = FRAMES + group * MEMF + inner
            for high in range(SIDE):
                for wide in range(SIDE):
                    col = MEM_AT + group * MEM_PAD + inner * MEM_STEP + high * SIDE + wide
                    mark(col, slot, high, wide)
    keys[PAD_LANE, ~valid] = -1e9
    pad_row = np.zeros((1, BIAS_COLS), np.float32)
    pad_row[0, PAD_LANE] = 1.0
    return keys, mask, pad_row


def spread_heads(source, target, rows_at, units, unit, first=0):
    count = source.shape[0]
    for index in range(units):
        at = (first + index) * unit
        target[rows_at : rows_at + count, index * LANES : index * LANES + unit] = source[
            :, at : at + unit
        ]


def spread_tables(kernel_ref, taps, pairs, heads, unit):
    taps[...] = jnp.zeros_like(taps)
    for _, target in pairs:
        target[...] = jnp.zeros_like(target)
    for member in range(3):
        for index in range(heads):
            at = (member * heads + index) * LANES
            for tap in range(27):
                row = kernel_ref[member, tap : tap + 1]
                taps[tap, :, at : at + unit] = jnp.broadcast_to(row, (8, unit))
            for source, target in pairs:
                target[:, at : at + unit] = source[member : member + 1]


def load_shifted(field, shifted):
    grid = field.reshape(FRAMES, SIDE, 8, field.shape[-1])
    flat = field.reshape(FRAMES * SIDE, 8, field.shape[-1])
    shifted[1, 1 : FRAMES + 1, 1 : SIDE + 1] = grid
    shifted[0, 1 : FRAMES + 1, 1 : SIDE + 1] = pltpu.roll(flat, 1, 1).reshape(grid.shape)
    shifted[2, 1 : FRAMES + 1, 1 : SIDE + 1] = pltpu.roll(flat, 7, 1).reshape(grid.shape)


def convolve(shifted, taps, target, flip):
    tiles = target.shape[-1] // LANES

    def step(pair, carry):
        for sub in range(2):
            frame = pair * 2 + sub
            for tile in range(tiles):
                lanes = slice(tile * LANES, (tile + 1) * LANES)
                total = None
                for i in range(3):
                    for k in range(3):
                        rows = shifted[k, frame + i, :, :, lanes]
                        for j in range(3):
                            if flip:
                                tap = (2 - i) * 9 + (2 - j) * 3 + (2 - k)
                            else:
                                tap = i * 9 + j * 3 + k
                            value = rows[j : j + SIDE] * taps[tap, :, lanes][None]
                            total = value if total is None else total + value
                target[frame, :, :, lanes] = total
        return carry

    lax.fori_loop(0, FRAMES // 2, step, 0)


def tap_grads(shifted, grads, target):
    tiles = target.shape[-1] // LANES

    def step(index, carry):
        lanes = pl.ds(pl.multiple_of(index * LANES, LANES), LANES)

        def inner(frame, sums):
            centre = grads[frame + 1, 1 : SIDE + 1, :, lanes]
            new = []
            for i in range(3):
                for k in range(3):
                    rows = shifted[k, frame + i, :, :, lanes]
                    for j in range(3):
                        parts = [rows[j + high] * centre[high] for high in range(SIDE)]
                        parts.append(sums[len(new)])
                        while len(parts) > 1:
                            pairs = zip(parts[::2], parts[1::2])
                            parts = [left + right for left, right in pairs]
                        new.append(parts[0])
            return tuple(new)

        start = tuple(jnp.zeros((8, LANES), F32) for _ in range(27))
        sums = lax.fori_loop(0, FRAMES, inner, start, unroll=4)
        for i in range(3):
            for k in range(3):
                for j in range(3):
                    target[i * 9 + j * 3 + k, :, lanes] += sums[(i * 3 + k) * 3 + j]
        return carry

    lax.fori_loop(0, tiles, step, 0)


def head_stats(values, unit):
    average = jnp.sum(values, axis=-1, keepdims=True) * (1.0 / unit)
    lane = lax.broadcasted_iota(jnp.int32, values.shape, 1)
    centred = jnp.where(lane < unit, values - average, 0.0)
    variance = jnp.sum(centred * centred, axis=-1, keepdims=True) * (1.0 / unit)
    return centred, lax.rsqrt(variance + 1e-06)


def frame_partner():
    return (lax.axis_index("clip"), 1 - lax.axis_index("frame"), lax.axis_index("head"))


def partner_copy(source, target, send_sem, recv_sem):
    return pltpu.make_async_remote_copy(
        src_ref=source, dst_ref=target, send_sem=send_sem, recv_sem=recv_sem,
        device_id=frame_partner(), device_id_type=MESH_ID,
    )


def side_partner():
    clip = lax.axis_index("clip")
    across = (clip // 2) * 2 + 1 - clip % 2
    return (across, lax.axis_index("frame"), lax.axis_index("head"))


def side_copy(source, target, send_sem, recv_sem):
    return pltpu.make_async_remote_copy(
        src_ref=source, dst_ref=target, send_sem=send_sem, recv_sem=recv_sem,
        device_id=side_partner(), device_id_type=MESH_ID,
    )


def greet_partner():
    barrier = pltpu.get_barrier_semaphore()
    pl.semaphore_signal(barrier, inc=1, device_id=frame_partner(), device_id_type=MESH_ID)
    pl.semaphore_wait(barrier, 1)


def forward_kernel(
    packed_ref, mem_own_ref, mem_peer_ref, column_ref, into_ref, outof_ref, kernel_ref,
    pool_gain_ref, pool_shift_ref, bias_ref, keyhot_ref, mask_ref, pad_ref,
    out_own, out_recv, rest_full, q_out, k_out, v_out, p_out, c_out,
    shifted, taps, gain_ref, shift_ref, out_send, out_sems, side_sems, pair_sems, turn_sems,
    own_sem,
    *, heads, unit, scale,
):
    units = 3 * heads
    own_rows = out_own.shape[1]
    clip = pl.program_id(0)
    clips = out_send.shape[0]

    def out_copy(index):
        return partner_copy(
            out_send.at[index], out_recv.at[index], out_sems.at[0, index], out_sems.at[1, index]
        )

    outers = column_ref.shape[0]
    split = outers // 2
    inner = lax.axis_index("clip") % 2
    frame = lax.axis_index("frame")
    place = inner * 2 + frame
    side_place = (1 - inner) * 2 + frame
    pair_place = inner * 2 + 1 - frame
    turn_place = (1 - inner) * 2 + 1 - frame
    own_copy = pltpu.make_async_copy(column_ref, rest_full.at[:, place], own_sem)

    def side_move(at, source, target):
        return side_copy(source, target, side_sems.at[0, at], side_sems.at[1, at])

    def pair_move(at, source, target):
        return partner_copy(source, target, pair_sems.at[0, at], pair_sems.at[1, at])

    def to_side(at):
        return side_move(at, column_ref.at[at], rest_full.at[at, place])

    def to_pair(at):
        return pair_move(at, column_ref.at[at], rest_full.at[at, place])

    def turn_side(at):
        block = rest_full.at[at, pair_place]
        return side_copy(block, block, turn_sems.at[0, at], turn_sems.at[1, at])

    def turn_pair(at):
        block = rest_full.at[at, side_place]
        return partner_copy(block, block, turn_sems.at[0, at], turn_sems.at[1, at])

    def turned(at):
        block = rest_full.at[at, turn_place]
        return side_copy(block, block, turn_sems.at[0, at], turn_sems.at[1, at])

    def side_arrival(at):
        block = rest_full.at[at, side_place]
        return side_move(at, block, block)

    def pair_arrival(at):
        block = rest_full.at[at, pair_place]
        return pair_move(at, block, block)

    @pl.when(clip == 0)
    def _():
        barrier = pltpu.get_barrier_semaphore()
        for device in (frame_partner(), side_partner()):
            pl.semaphore_signal(barrier, inc=1, device_id=device, device_id_type=MESH_ID)
        pl.semaphore_wait(barrier, 2)
        each(0, outers, lambda at: to_side(outers - 1 - at).start())
        each(0, outers, lambda at: to_pair(at).start())
        own_copy.start()
        shifted[...] = jnp.zeros_like(shifted)
        pairs = ((pool_gain_ref, gain_ref), (pool_shift_ref, shift_ref))
        spread_tables(kernel_ref, taps, pairs, heads, unit)

    @pl.when(clip == jnp.minimum(TURN_STEP, clips - 1))
    def _():
        def turn_low(at):
            pair_arrival(at).wait_recv()
            turn_side(at).start()

        def turn_high(at):
            side_arrival(at).wait_recv()
            turn_pair(at).start()

        each(0, split, turn_low)
        each(split, outers, turn_high)

    load_shifted(dot_f32(into_ref[frame], packed_ref[0], ((1,), (0,))), shifted)
    conv = c_out.at[0]
    convolve(shifted, taps, conv, False)
    k_out[0, MEM_AT:, :] = jnp.zeros((KROWS - MEM_AT, heads * LANES), BF)
    v_out[0, MEM_AT:, :] = jnp.zeros((KROWS - MEM_AT, heads * LANES), BF)
    spread_heads(mem_own_ref.at[0], k_out.at[0], MEM_AT, heads, unit, 0 * heads)
    spread_heads(mem_own_ref.at[0], v_out.at[0], MEM_AT, heads, unit, 1 * heads)
    spread_heads(mem_peer_ref.at[0], k_out.at[0], MEM_AT + MEM_PAD, heads, unit, 0 * heads)
    spread_heads(mem_peer_ref.at[0], v_out.at[0], MEM_AT + MEM_PAD, heads, unit, 1 * heads)
    for index in range(units):
        lanes = slice(index * LANES, (index + 1) * LANES)
        block = conv[:, :, :, lanes].reshape(GRID_ROWS, LANES)
        centred, rate = head_stats(block, unit)
        normal = centred * rate * gain_ref[:, lanes] + shift_ref[:, lanes]
        rows = dot_f32(outof_ref[frame], normal.astype(BF), ((1,), (0,))).astype(BF)
        target = (q_out, k_out, v_out)[index // heads]
        local = slice((index % heads) * LANES, (index % heads + 1) * LANES)
        target[0, 0:QROWS, local] = rows

    bias = bias_ref[0]
    bias_high = bias.astype(BF)
    bias_low = (bias - bias_high.astype(F32)).astype(BF)
    for head in range(heads):
        lanes = slice(head * LANES, (head + 1) * LANES)
        keys = k_out[0, :, lanes]
        values = v_out[0, :, lanes]
        for half in range(2):
            rows = slice(half * HALF, (half + 1) * HALF)
            query = q_out[0, rows, lanes]
            table = dot_f32(query, bias_high, ((1,), (1,))) + dot_f32(query, bias_low, ((1,), (1,)))
            table = table * mask_ref[rows, :] + pad_ref[...]
            table_high = table.astype(BF)
            table_low = (table - table_high.astype(F32)).astype(BF)
            scores = dot_f32(query, keys, ((1,), (1,)))
            scores = scores + dot_f32(table_high, keyhot_ref[...], ((1,), (0,)))
            scores = scores + dot_f32(table_low, keyhot_ref[...], ((1,), (0,)))
            top = jnp.max(scores, axis=-1, keepdims=True)
            weights = jnp.exp((scores - top) * scale)
            total = jnp.sum(weights, axis=-1, keepdims=True)
            probs = (weights * (1.0 / total)).astype(BF)
            p_out[0, head, rows, :] = probs
            mixed = dot_f32(probs, values, ((1,), (0,))) + query.astype(F32)
            target = (out_own.at[0], out_send.at[clip])[half]
            target[:, head * unit : (head + 1) * unit] = mixed[:own_rows, :unit].astype(BF)

    out_copy(clip).start()

    @pl.when(clip == clips - 1)
    def _():
        own_copy.wait()
        each(split, outers, lambda at: pair_arrival(at).wait_recv())
        each(0, split, lambda at: side_arrival(at).wait_recv())
        each(0, outers, lambda at: turned(at).wait_recv())
        each(0, split, lambda at: turn_side(at).wait_send())
        each(split, outers, lambda at: turn_pair(at).wait_send())
        each(0, outers, lambda at: to_side(at).wait_send())
        each(0, outers, lambda at: to_pair(at).wait_send())
        for index in range(clips):
            out_copy(index).wait()


def backward_kernel(
    packed_ref, normed_ref, weight_ref, grad_own_ref, grad_send_ref, rest_ref, into_ref, outof_ref,
    kernel_ref, pool_gain_ref, bias_ref, keyhot_ref, mask_ref, q_ref, k_ref, v_ref, p_ref, c_ref,
    row_own, row_recv, mem_own, mem_recv, taps_out, gain_out, shift_out, bias_out, weight_out,
    joined_out, rest_part, rest_out,
    shifted, taps, gain_ref, grads, spread, pooled, peer, mem_send, rest_own, rest_side, rest_send,
    rest_peer, rest_sum, rest_far, weight_sum, keep, cross_send, cross_recv, row_send,
    grad_sems, mem_sems, own_sems, side_sems, rest_sems, far_sems, cross_sems, row_sems,
    *, heads, unit, scale,
):
    units = 3 * heads
    own_rows = grad_own_ref.shape[1]
    clip = pl.program_id(0)
    clips = peer.shape[0]
    clip_at = lax.axis_index("clip")
    frame = lax.axis_index("frame")
    head_at = lax.axis_index("head")

    def grad_copy(index):
        return partner_copy(
            grad_send_ref.at[index], peer.at[index], grad_sems.at[0, index], grad_sems.at[1, index]
        )

    def mem_copy(index):
        return partner_copy(
            mem_send.at[index], mem_recv.at[index], mem_sems.at[0, index], mem_sems.at[1, index]
        )

    def row_copy(index):
        return partner_copy(
            row_send.at[index], row_recv.at[index], row_sems.at[0, index], row_sems.at[1, index]
        )

    def cross_copy(index):
        return pltpu.make_async_remote_copy(
            src_ref=cross_send.at[index], dst_ref=cross_recv.at[index],
            send_sem=cross_sems.at[0, index], recv_sem=cross_sems.at[1, index],
            device_id=(clip_at, frame, 1 - head_at), device_id_type=MESH_ID,
        )

    def finish_rows(index):
        cross_copy(index).wait_recv()
        total = (keep[index].astype(F32) + cross_recv[index].astype(F32)).astype(BF)
        row_own[index] = total[:own_rows]
        row_send[index] = total[HALF : HALF + own_rows]
        row_copy(index).start()

    chunks, outers, _, _, cols = rest_own.shape
    side_at = clip_at % 2
    outer = clip_at // 2
    early = rest_far.shape[0]

    def rest_at(side, chunk):
        return rest_ref.at[:, pl.ds(side * 2, 2), :, pl.ds(chunk * cols, cols)]

    def own_copy(chunk):
        return pltpu.make_async_copy(
            rest_at(side_at, chunk), rest_own.at[chunk], own_sems.at[chunk]
        )

    def over_copy(chunk):
        return side_copy(
            rest_at(1 - side_at, chunk), rest_side.at[chunk], side_sems.at[0, chunk],
            side_sems.at[1, chunk],
        )

    def rest_copy(chunk):
        return partner_copy(
            rest_send.at[chunk], rest_peer.at[chunk], rest_sems.at[0, chunk],
            rest_sems.at[1, chunk],
        )

    def pass_on(chunk):
        own_copy(chunk).wait()
        over_copy(chunk).wait_recv()

        def add(index):
            def total(part):
                first = rest_own[chunk, index, part].astype(F32)
                return (first + rest_side[chunk, index, part].astype(F32)).astype(BF)

            rest_send[chunk, index] = total(1 - frame)
            rest_sum[chunk, index] = total(frame)

        each(0, outers, add)
        rest_copy(chunk).start()

    def far_device(step):
        return (((outer + step) % outers) * 2 + side_at, frame, head_at)

    def far_copy(chunk, step):
        there = (outer + step) % outers
        return pltpu.make_async_remote_copy(
            src_ref=rest_sum.at[chunk, there], dst_ref=rest_far.at[chunk, step],
            send_sem=far_sems.at[0, chunk, step], recv_sem=far_sems.at[1, chunk, step],
            device_id=far_device(step), device_id_type=MESH_ID,
        )

    def settle(chunk):
        rest_copy(chunk).wait_recv()

        def add(index):
            total = rest_sum[chunk, index].astype(F32) + rest_peer[chunk, index].astype(F32)
            if chunk < early:
                rest_sum[chunk, index] = total.astype(BF)
            else:
                rest_part[index] = total.astype(BF)

        each(0, outers, add)
        if chunk < early:
            each(1, outers, lambda step: far_copy(chunk, step).start())

    @pl.when(clip == 0)
    def _():
        barrier = pltpu.get_barrier_semaphore()

        def greet(device):
            pl.semaphore_signal(barrier, inc=1, device_id=device, device_id_type=MESH_ID)

        for device in (frame_partner(), side_partner(), (clip_at, frame, 1 - head_at)):
            greet(device)
        each(1, outers, lambda step: greet(far_device(step)))
        pl.semaphore_wait(barrier, 3 + outers - 1)
        for index in range(clips):
            grad_copy(index).start()
        over_copy(0).start()
        own_copy(0).start()
        shifted[...] = jnp.zeros_like(shifted)
        grads[...] = jnp.zeros_like(grads)
        spread[...] = jnp.zeros_like(spread)
        taps_out[...] = jnp.zeros_like(taps_out)
        gain_out[...] = jnp.zeros_like(gain_out)
        shift_out[...] = jnp.zeros_like(shift_out)
        weight_sum[...] = jnp.zeros_like(weight_sum)
        joined_out[...] = jnp.zeros_like(joined_out)
        spread_tables(kernel_ref, taps, ((pool_gain_ref, gain_ref),), heads, unit)

    def pump(odd):
        for chunk in range(chunks):
            point = min(chunk + 1, 2 * clips - 1)
            if point % 2 == odd:

                @pl.when(clip == point // 2)
                def _():
                    if chunk + 1 < chunks:
                        over_copy(chunk + 1).start()
                        own_copy(chunk + 1).start()
                    pass_on(chunk)
                    if chunk:
                        settle(chunk - 1)

    pump(0)
    load_shifted(dot_f32(into_ref[frame], packed_ref[0], ((1,), (0,))), shifted)
    spread_heads(grad_own_ref.at[0], spread, 0, heads, unit)
    grad_copy(clip).wait_recv()
    spread_heads(peer.at[clip], spread, HALF, heads, unit)
    bias_low = bias_ref[0].astype(BF)
    bias_sum = jnp.zeros((BIAS_COLS, LANES), F32)
    for head in range(heads):
        lanes = slice(head * LANES, (head + 1) * LANES)
        keys = k_ref[0, :, lanes]
        values = v_ref[0, :, lanes]
        keys_grad = jnp.zeros((KROWS, LANES), F32)
        values_grad = jnp.zeros((KROWS, LANES), F32)
        for half in range(2):
            rows = slice(half * HALF, (half + 1) * HALF)
            query = q_ref[0, rows, lanes]
            out_grad = spread[rows, lanes]
            probs = p_ref[0, head, rows, :]
            wide = probs.astype(F32)
            probs_grad = dot_f32(out_grad, values, ((1,), (1,)))
            weighted = wide * probs_grad
            shared = jnp.sum(weighted, axis=-1, keepdims=True)
            score_grad = (weighted - wide * shared).astype(BF)
            values_grad = values_grad + dot_f32(probs, out_grad, ((0,), (0,)))
            keys_grad = keys_grad + dot_f32(score_grad, query, ((0,), (0,)))
            table_grad = dot_f32(score_grad, keyhot_ref[...], ((1,), (1,))) * mask_ref[rows, :]
            table_low = table_grad.astype(BF)
            query_grad = dot_f32(score_grad, keys, ((1,), (0,)))
            query_grad = query_grad + dot_f32(table_low, bias_low, ((1,), (0,)))
            query_grad = query_grad * scale + out_grad.astype(F32)
            pooled[rows, lanes] = query_grad.astype(BF)
            bias_sum = bias_sum + dot_f32(table_low, query, ((0,), (0,)))
        keys_grad = (keys_grad * scale).astype(BF)
        values_grad = values_grad.astype(BF)
        for member, part in enumerate((keys_grad, values_grad)):
            at = ((member + 1) * heads + head) * LANES
            pooled[:, at : at + LANES] = part[:QROWS]
            at = (member * heads + head) * LANES
            low = MEM_AT + MEM_PAD
            mem_own[0, :, at : at + LANES] = part[MEM_AT : MEM_AT + MEM_BACK]
            mem_send[clip, :, at : at + LANES] = part[low : low + MEM_BACK]
    bias_out[0] = bias_sum
    mem_copy(clip).start()

    for index in range(units):
        lanes = slice(index * LANES, (index + 1) * LANES)
        incoming = dot_f32(into_ref[frame], pooled[:, lanes], ((1,), (0,)))
        block = c_ref[0, :, :, :, lanes].reshape(GRID_ROWS, LANES)
        centred, rate = head_stats(block, unit)
        normal = centred * rate
        product = incoming * normal
        gain_out[:, lanes] += jnp.sum(product, axis=0, keepdims=True)
        shift_out[:, lanes] += jnp.sum(incoming, axis=0, keepdims=True)
        inner = incoming * gain_ref[:, lanes]
        mean_inner = jnp.sum(inner, axis=-1, keepdims=True) * (1.0 / unit)
        mean_both = jnp.sum(inner * normal, axis=-1, keepdims=True) * (1.0 / unit)
        lane = lax.broadcasted_iota(jnp.int32, block.shape, 1)
        result = rate * (inner - mean_inner - normal * mean_both)
        result = jnp.where(lane < unit, result, 0.0)
        flat = result.reshape(FRAMES * SIDE, 8, LANES)
        shape = (FRAMES, SIDE, 8, LANES)
        grads[1, 1 : FRAMES + 1, 1 : SIDE + 1, :, lanes] = flat.reshape(shape)
        grads[0, 1 : FRAMES + 1, 1 : SIDE + 1, :, lanes] = pltpu.roll(flat, 1, 1).reshape(shape)
        grads[2, 1 : FRAMES + 1, 1 : SIDE + 1, :, lanes] = pltpu.roll(flat, 7, 1).reshape(shape)

    @pl.when(clip > 0)
    def _():
        finish_rows(clip - 1)

    pump(1)
    tap_grads(shifted, grads.at[1], taps_out)
    conv = shifted.at[1, 1 : FRAMES + 1, 1 : SIDE + 1]
    convolve(grads, taps, conv, True)
    for index in range(units):
        lanes = slice(index * LANES, (index + 1) * LANES)
        block = shifted[1, 1 : FRAMES + 1, 1 : SIDE + 1, :, lanes].reshape(GRID_ROWS, LANES)
        rows = dot_f32(outof_ref[frame], block.astype(BF), ((1,), (0,))).astype(BF)
        pooled[:, lanes] = rows
        joined_out[:, lanes] += jnp.sum(rows.astype(F32), axis=0, keepdims=True)
    weight_sum[...] += dot_f32(normed_ref[0], pooled[...], ((0,), (0,)))
    result = dot_f32(pooled[...], weight_ref[...], ((1,), (1,))).astype(BF)
    cut = result.shape[1] // 2

    @pl.when(head_at == 0)
    def _():
        keep[clip] = result[:, :cut]
        cross_send[clip] = result[:, cut:]

    @pl.when(head_at == 1)
    def _():
        keep[clip] = result[:, cut:]
        cross_send[clip] = result[:, :cut]

    cross_copy(clip).start()

    @pl.when(clip == clips - 1)
    def _():
        weight_out[...] = weight_sum[...].astype(BF)
        finish_rows(clip)
        settle(chunks - 1)
        for chunk in range(early):
            each(1, outers, lambda step: far_copy(chunk, step).wait_recv())
            rest_out[:, chunk * cols : (chunk + 1) * cols] = lax.fori_loop(
                1,
                outers,
                lambda step, sums: sums + rest_far[chunk, step].astype(F32),
                rest_sum[chunk, outer].astype(F32),
            )
        for index in range(clips):
            grad_copy(index).wait_send()
            cross_copy(index).wait_send()
            mem_copy(index).wait()
            row_copy(index).wait()
        for chunk in range(chunks):
            over_copy(chunk).wait_send()
            rest_copy(chunk).wait_send()
        for chunk in range(early):
            each(1, outers, lambda step: far_copy(chunk, step).wait_send())


def whole_spec(shape):
    return pl.BlockSpec(shape, lambda clip: (0,) * len(shape))


def clip_spec(shape):
    return pl.BlockSpec((1,) + shape, lambda clip: (clip,) + (0,) * len(shape))


def once_spec(shape):
    return pl.BlockSpec(
        shape, lambda clip: (0,) * len(shape), pipeline_mode=pl.Buffered(1)
    )


def any_spec():
    return pl.BlockSpec(memory_space=pl.ANY)


def attention_forward(
    packed, mem_own, mem_peer, column, consts, kernels, gains, shifts, bias, scale, unit, rows
):
    clips = packed.shape[0]
    heads = packed.shape[2] // (3 * LANES)
    into, outof, keyhot, mask, pad_row = consts
    wide = 3 * heads * LANES
    mem_shape = mem_own.shape[1:]
    outers = column.shape[0]
    dma = pltpu.SemaphoreType.DMA
    out = jax.ShapeDtypeStruct
    return pl.pallas_call(
        partial(forward_kernel, heads=heads, unit=unit, scale=scale),
        grid=(clips,),
        in_specs=[
            clip_spec((QROWS, wide)),
            clip_spec(mem_shape),
            clip_spec(mem_shape),
            once_spec(column.shape),
            once_spec(into.shape),
            once_spec(outof.shape),
            once_spec(kernels.shape),
            once_spec(gains.shape),
            once_spec(shifts.shape),
            clip_spec((BIAS_COLS, LANES)),
            once_spec((BIAS_COLS, KROWS)),
            once_spec((QROWS, BIAS_COLS)),
            once_spec((1, BIAS_COLS)),
        ],
        out_specs=[
            clip_spec((rows, heads * unit)),
            any_spec(),
            any_spec(),
            clip_spec((QROWS, heads * LANES)),
            clip_spec((KROWS, heads * LANES)),
            clip_spec((KROWS, heads * LANES)),
            clip_spec((heads, QROWS, KROWS)),
            clip_spec((FRAMES, SIDE, 8, wide)),
        ],
        scratch_shapes=[
            pltpu.VMEM((3, FRAMES + 2, SIDE + 2, 8, wide), F32),
            pltpu.VMEM((27, 8, wide), F32),
            pltpu.VMEM((1, wide), F32),
            pltpu.VMEM((1, wide), F32),
            pltpu.VMEM((clips, rows, heads * unit), BF),
            dma((2, clips)),
            dma((2, outers)),
            dma((2, outers)),
            dma((2, outers)),
            pltpu.SemaphoreType.DMA,
        ],
        out_shape=[
            out((clips, rows, heads * unit), BF),
            out((clips, rows, heads * unit), BF),
            out((outers, 4) + column.shape[1:], BF),
            out((clips, QROWS, heads * LANES), BF),
            out((clips, KROWS, heads * LANES), BF),
            out((clips, KROWS, heads * LANES), BF),
            out((clips, heads, QROWS, KROWS), BF),
            out((clips, FRAMES, SIDE, 8, wide), F32),
        ],
        compiler_params=pltpu.CompilerParams(
            collective_id=1, has_side_effects=True, vmem_limit_bytes=VMEM_LIMIT
        ),
        name="pooled_attention_forward",
    )(
        packed, mem_own, mem_peer, column, into, outof, kernels, gains, shifts, bias, keyhot, mask,
        pad_row,
    )


def attention_backward(
    packed, normed, weight, grad_own, grad_send, rest, consts, kernels, gains, bias, saved, scale,
    unit,
):
    clips, rows, width = grad_own.shape
    heads = width // unit
    model = weight.shape[0]
    half = model // 2
    into, outof, keyhot, mask, pad_row = consts
    wide = 3 * heads * LANES
    outers, _, shard_rows, rest_width = rest.shape
    chunks = 9
    early = 8
    cols = rest_width // chunks
    out = jax.ShapeDtypeStruct
    dma = pltpu.SemaphoreType.DMA
    return pl.pallas_call(
        partial(backward_kernel, heads=heads, unit=unit, scale=scale),
        grid=(clips,),
        in_specs=[
            clip_spec((QROWS, wide)),
            clip_spec((QROWS, model)),
            once_spec((model, wide)),
            clip_spec((rows, width)),
            any_spec(),
            any_spec(),
            once_spec(into.shape),
            once_spec(outof.shape),
            once_spec(kernels.shape),
            once_spec(gains.shape),
            clip_spec((BIAS_COLS, LANES)),
            once_spec((BIAS_COLS, KROWS)),
            once_spec((QROWS, BIAS_COLS)),
            clip_spec((QROWS, heads * LANES)),
            clip_spec((KROWS, heads * LANES)),
            clip_spec((KROWS, heads * LANES)),
            clip_spec((heads, QROWS, KROWS)),
            clip_spec((FRAMES, SIDE, 8, wide)),
        ],
        out_specs=[
            whole_spec((clips, rows, half)),
            any_spec(),
            clip_spec((MEM_BACK, 2 * heads * LANES)),
            any_spec(),
            whole_spec((27, 8, wide)),
            whole_spec((1, wide)),
            whole_spec((1, wide)),
            clip_spec((BIAS_COLS, LANES)),
            whole_spec((model, wide)),
            whole_spec((1, wide)),
            whole_spec((outers, shard_rows, cols)),
            whole_spec((shard_rows, early * cols)),
        ],
        scratch_shapes=[
            pltpu.VMEM((3, FRAMES + 2, SIDE + 2, 8, wide), F32),
            pltpu.VMEM((27, 8, wide), F32),
            pltpu.VMEM((1, wide), F32),
            pltpu.VMEM((3, FRAMES + 2, SIDE + 2, 8, wide), F32),
            pltpu.VMEM((QROWS, heads * LANES), BF),
            pltpu.VMEM((QROWS, wide), BF),
            pltpu.VMEM((clips, rows, width), BF),
            pltpu.VMEM((clips, MEM_BACK, 2 * heads * LANES), BF),
            pltpu.VMEM((chunks, outers, 2, shard_rows, cols), BF),
            pltpu.VMEM((chunks, outers, 2, shard_rows, cols), BF),
            pltpu.VMEM((chunks, outers, shard_rows, cols), BF),
            pltpu.VMEM((chunks, outers, shard_rows, cols), BF),
            pltpu.VMEM((chunks, outers, shard_rows, cols), BF),
            pltpu.VMEM((early, outers, shard_rows, cols), BF),
            pltpu.VMEM((model, wide), F32),
            pltpu.VMEM((clips, QROWS, half), BF),
            pltpu.VMEM((clips, QROWS, half), BF),
            pltpu.VMEM((clips, QROWS, half), BF),
            pltpu.VMEM((clips, rows, half), BF),
            dma((2, clips)),
            dma((2, clips)),
            dma((chunks,)),
            dma((2, chunks)),
            dma((2, chunks)),
            dma((2, early, outers)),
            dma((2, clips)),
            dma((2, clips)),
        ],
        out_shape=[
            out((clips, rows, half), BF),
            out((clips, rows, half), BF),
            out((clips, MEM_BACK, 2 * heads * LANES), BF),
            out((clips, MEM_BACK, 2 * heads * LANES), BF),
            out((27, 8, wide), F32),
            out((1, wide), F32),
            out((1, wide), F32),
            out((clips, BIAS_COLS, LANES), F32),
            out((model, wide), BF),
            out((1, wide), F32),
            out((outers, shard_rows, cols), BF),
            out((shard_rows, early * cols), F32),
        ],
        compiler_params=pltpu.CompilerParams(
            collective_id=2, has_side_effects=True, vmem_limit_bytes=VMEM_LIMIT
        ),
        name="pooled_attention_backward",
    )(
        packed, normed, weight, grad_own, grad_send, rest, into, outof, kernels, gains, bias, keyhot,
        mask, *saved,
    )


def row_stats(values):
    width = values.shape[-1]
    centred = values - jnp.sum(values, axis=-1, keepdims=True) * (1.0 / width)
    variance = jnp.sum(centred * centred, axis=-1, keepdims=True) * (1.0 / width)
    return centred, lax.rsqrt(variance + 1e-06)


def each(low, high, act):
    def body(step, carry):
        act(step)
        return carry

    lax.fori_loop(low, high, body, 0)


def norm_rows(source, index, gain, shift, target, at):
    rows = source.shape[1]
    centred, rate = row_stats(source[index].astype(F32))
    target[index, at : at + rows] = (centred * rate * gain[0:1] + shift[0:1]).astype(BF)


def project_rows(normed, weight, bias, packed):
    def step(index):
        packed[index] = (dot_f32(normed[index], weight, ((1,), (0,))) + bias[...]).astype(BF)

    each(0, packed.shape[0], step)


def project_kernel(
    x, attn, gain, shift, attn_shift, cached, old, squeeze, proj, up, down, full, packed, normed, mem_own, mem_peer,
    rest_column, shards, bias, rest, mem_send, squeeze_rows, x_peer, columns, far_sems, near_sems, x_sems, cross_sems, mem_sems, rest_sems, own_sem,
):
    outers, _, _, width = full.shape
    clips, rows, model = x.shape
    clip = lax.axis_index("clip")
    frame = lax.axis_index("frame")
    head = lax.axis_index("head")
    outer, inner = clip // 2, clip % 2
    place = inner * 2 + frame
    half = model // 2
    lanes = pl.ds(pl.multiple_of(head * half, LANES), half)
    barrier = pltpu.get_barrier_semaphore()

    def far_device(step):
        return device_of((outer + step) % outers, inner, frame, head)

    def near_device(step):
        there_inner, there_frame = plane_peer(inner, frame, step)
        return device_of(outer, there_inner, there_frame, head)

    def greet(device):
        pl.semaphore_signal(barrier, inc=1, device_id=device, device_id_type=MESH_ID)

    each(1, outers, lambda step: greet(far_device(step)))
    for step in range(1, 4):
        greet(near_device(step))
    greet((clip, frame, 1 - head))
    group = mem_own.shape[2] // 2
    heads = shards.shape[2] // (3 * LANES)
    unit = group // heads
    shards[...] = jnp.zeros_like(shards)
    bias[...] = jnp.zeros_like(bias)
    for member in range(3):
        for side in range(2):
            for index in range(heads):
                target = (member * heads + index) * LANES
                source = slice(side * group + index * unit, side * group + (index + 1) * unit)
                shards[side, :, target : target + unit] = attn[member, :, source]
    at = 0
    for part in (proj, up, down):
        rest[:, at : at + part.shape[1]] = part[...]
        at += part.shape[1]
    for side in range(2):

        @pl.when(frame == side)
        def _():
            for member in range(3):
                for index in range(heads):
                    target = (member * heads + index) * LANES
                    source = slice(side * group + index * unit, side * group + (index + 1) * unit)
                    bias[:, target : target + unit] = attn_shift[member : member + 1, source]

    for member in range(2):
        for index in range(2 * heads):
            at = (2 * member * heads + index) * unit
            squeeze_rows[:, at : at + unit] = squeeze[member]
    mem_own[...] = jnp.zeros_like(mem_own)
    mem_send[...] = jnp.zeros_like(mem_send)

    def squeeze_clip(index):
        total = jnp.zeros((CELLS, cached.shape[2]), F32)
        for step in range(squeeze_rows.shape[0]):
            rows_here = cached[index, step * CELLS : (step + 1) * CELLS].astype(F32)
            total = total + rows_here * squeeze_rows[step : step + 1]
        pieces = ((0, total.astype(BF)), (MEM_STEP, old[index]))
        for side in range(2):

            @pl.when(frame == side)
            def _():
                for at, value in pieces:
                    for member in range(2):
                        local = slice(member * group, (member + 1) * group)
                        low = (2 * member + side) * group
                        mem_own[index, at : at + CELLS, local] = value[:, low : low + group]
                        low = (2 * member + 1 - side) * group
                        mem_send[index, at : at + CELLS, local] = value[:, low : low + group]

    pl.semaphore_wait(barrier, outers - 1 + 4)

    def far_copy(step, at):
        return pltpu.make_async_remote_copy(
            src_ref=shards, dst_ref=columns.at[at],
            send_sem=far_sems.at[0, step], recv_sem=far_sems.at[1, step],
            device_id=far_device(step), device_id_type=MESH_ID,
        )

    def near_copy(index, step, source, at):
        return pltpu.make_async_remote_copy(
            src_ref=source.at[(frame + step % 2) % 2], dst_ref=full.at[at, place],
            send_sem=near_sems.at[0, index, step - 1], recv_sem=near_sems.at[1, index, step - 1],
            device_id=near_device(step), device_id_type=MESH_ID,
        )

    def near_arrival(index, step, at):
        there_inner, there_frame = plane_peer(inner, frame, step)
        return pltpu.make_async_remote_copy(
            src_ref=shards.at[0], dst_ref=full.at[at, there_inner * 2 + there_frame],
            send_sem=near_sems.at[0, index, step - 1], recv_sem=near_sems.at[1, index, step - 1],
            device_id=near_device(step), device_id_type=MESH_ID,
        )

    def x_copy(index):
        return partner_copy(
            x.at[index, :, lanes], x_peer.at[index, :, lanes], x_sems.at[0, index],
            x_sems.at[1, index],
        )

    def cross_copy(index):
        return pltpu.make_async_remote_copy(
            src_ref=x_peer.at[index, :, lanes], dst_ref=x_peer.at[index, :, lanes],
            send_sem=cross_sems.at[0, index], recv_sem=cross_sems.at[1, index],
            device_id=(clip, frame, 1 - head), device_id_type=MESH_ID,
        )

    def cross_arrival(index):
        other = pl.ds(pl.multiple_of((1 - head) * half, LANES), half)
        return pltpu.make_async_remote_copy(
            src_ref=x_peer.at[index, :, other], dst_ref=x_peer.at[index, :, other],
            send_sem=cross_sems.at[0, index], recv_sem=cross_sems.at[1, index],
            device_id=(clip, frame, 1 - head), device_id_type=MESH_ID,
        )

    mem_copy = partner_copy(mem_send, mem_peer, mem_sems.at[0], mem_sems.at[1])

    def rest_copy(step, at):
        return pltpu.make_async_remote_copy(
            src_ref=rest, dst_ref=rest_column.at[at],
            send_sem=rest_sems.at[0, step], recv_sem=rest_sems.at[1, step],
            device_id=far_device(step), device_id_type=MESH_ID,
        )

    own_copy = pltpu.make_async_copy(rest, rest_column.at[outer], own_sem)

    def origin(step):
        return (outer + outers - step) % outers

    each(1, outers, lambda step: far_copy(step, outer).start())
    for step in range(1, 4):
        near_copy(0, step, shards, outer).start()
    each(0, clips, lambda index: x_copy(index).start())
    each(0, clips, squeeze_clip)
    mem_copy.start()
    own_copy.start()
    full[outer, place] = shards[frame]
    normed[...] = jnp.zeros_like(normed)
    each(0, clips, lambda index: norm_rows(x, index, gain, shift, normed, 0))

    def forward(index):
        at = origin(index)
        far_copy(index, at).wait_recv()
        for step in range(1, 4):
            near_copy(index, step, columns.at[at], at).start()
        full[at, place] = columns[at, frame]

    each(1, outers, forward)
    each(1, outers, lambda step: rest_copy(step, outer).start())

    def relay(index):
        x_copy(index).wait_recv()
        cross_copy(index).start()

    each(0, clips, relay)

    def receive(index):
        cross_arrival(index).wait_recv()
        norm_rows(x_peer, index, gain, shift, normed, HALF)

    each(0, clips, receive)

    def arrive(index):
        for step in range(1, 4):
            near_arrival(index, step, origin(index)).wait_recv()

    each(0, outers, arrive)
    project_rows(normed, full[...].reshape(model, width), bias, packed)
    mem_copy.wait()
    own_copy.wait()
    each(1, outers, lambda step: rest_copy(step, origin(step)).wait_recv())
    each(1, outers, lambda step: rest_copy(step, outer).wait_send())
    each(1, outers, lambda step: far_copy(step, outer).wait_send())
    for step in range(1, 4):
        near_copy(0, step, shards, outer).wait_send()

    def sent(index):
        for step in range(1, 4):
            near_copy(index, step, columns.at[origin(index)], origin(index)).wait_send()

    each(1, outers, sent)

    def x_sent(index):
        x_copy(index).wait_send()
        cross_copy(index).wait_send()

    each(0, clips, x_sent)


def project_local_kernel(x, x_peer, weight, gain, shift, bias, packed, normed):
    normed[...] = jnp.zeros_like(normed)
    each(0, x.shape[0], lambda index: norm_rows(x, index, gain, shift, normed, 0))
    each(0, x.shape[0], lambda index: norm_rows(x_peer, index, gain, shift, normed, HALF))
    project_rows(normed, weight[...], bias, packed)


def swap(value, axis):
    return lax.ppermute(value, axis, [(0, 1), (1, 0)])


def padded_heads(value, unit):
    value = value.reshape(value.shape[0], 3, 2, -1, unit)
    value = jnp.pad(value, ((0, 0),) * 4 + ((0, LANES - unit),))
    return value.transpose(2, 0, 1, 3, 4).reshape(2, value.shape[0], -1)


def project(
    x, attn, gain, shift, attn_shift, cached, old, squeeze, proj, up, down, clip_count, unit
):
    clips, rows, model = x.shape
    _, shard_rows, head_width = attn.shape
    heads = head_width // (2 * unit)
    width = 3 * heads * LANES
    outers = clip_count // 2
    rest_shape = (shard_rows, proj.shape[1] + up.shape[1] + down.shape[1])
    out = jax.ShapeDtypeStruct
    dma = pltpu.SemaphoreType.DMA
    vmem = pl.BlockSpec(memory_space=pltpu.VMEM)
    shapes = [out((clips, QROWS, width), BF), out((clips, QROWS, model), BF)]
    if shard_rows % 16:
        frame = lax.axis_index("frame")
        shards = padded_heads(attn.transpose(1, 0, 2), unit)
        full = lax.all_gather(shards, ("clip", "frame"), axis=1, tiled=True)
        full = lax.dynamic_index_in_dim(full, frame, 0, keepdims=False)
        bias = padded_heads(attn_shift[None], unit)
        bias = lax.dynamic_index_in_dim(bias, frame, 0, keepdims=False)
        steps = squeeze.shape[1]
        wide = cached.astype(F32).reshape(clips, steps, CELLS, 2, head_width)
        tiled = jnp.tile(squeeze, (1, 1, 2 * heads))
        mem = sum(wide[:, step] * tiled[:, step] for step in range(steps)).astype(BF)
        mem = jnp.stack([mem, old.reshape(mem.shape)], axis=1)
        mem = jnp.pad(mem, ((0, 0), (0, 0), (0, MEM_STEP - CELLS), (0, 0), (0, 0)))
        pieces = mem.reshape(clips, 2 * MEM_STEP, 2, 2, heads * unit)
        mem_own = lax.dynamic_index_in_dim(pieces, frame, 3, keepdims=False)
        mem_send = lax.dynamic_index_in_dim(pieces, 1 - frame, 3, keepdims=False)
        mem_own = mem_own.reshape(clips, -1, head_width)
        mem_peer = swap(mem_send.reshape(clips, -1, head_width), "frame")
        packed, normed = pl.pallas_call(
            project_local_kernel,
            in_specs=[vmem] * 6,
            out_specs=[vmem] * 2,
            out_shape=shapes,
            compiler_params=pltpu.CompilerParams(vmem_limit_bytes=VMEM_LIMIT),
            name="project_local",
        )(x, swap(x, "frame"), full, gain, shift, bias)
        rest = jnp.concatenate([proj, up, down], axis=1)
        column = lax.all_gather(rest, ("clip", "frame"), axis=0, tiled=False)
        column = column.reshape((outers, 4) + rest.shape)
        place = lax.axis_index("clip") % 2 * 2 + frame
        column = lax.dynamic_index_in_dim(column, place, 1, keepdims=False)
        return full, packed, normed, mem_own, mem_peer, column
    mem_shape = (clips, MEM_PAD, head_width)
    full, packed, normed, mem_own, mem_peer, column = pl.pallas_call(
        project_kernel,
        in_specs=[vmem] * 11,
        out_specs=[vmem] * 6,
        out_shape=[out((outers, 4, shard_rows, width), BF)]
        + shapes
        + [out(mem_shape, BF), out(mem_shape, BF), out((outers,) + rest_shape, BF)],
        scratch_shapes=[
            pltpu.VMEM((2, shard_rows, width), BF),
            pltpu.VMEM((1, width), F32),
            pltpu.VMEM(rest_shape, BF),
            pltpu.VMEM(mem_shape, BF),
            pltpu.VMEM((squeeze.shape[1], cached.shape[2]), F32),
            pltpu.VMEM((clips, rows, model), BF),
            pltpu.VMEM((outers, 2, shard_rows, width), BF),
            dma((2, outers)),
            dma((2, outers, 3)),
            dma((2, clips)),
            dma((2, clips)),
            dma((2,)),
            dma((2, outers)),
            pltpu.SemaphoreType.DMA,
        ],
        compiler_params=pltpu.CompilerParams(
            collective_id=3, has_side_effects=True, vmem_limit_bytes=VMEM_LIMIT
        ),
        name="gather_and_project",
    )(x, attn, gain, shift, attn_shift, cached, old, squeeze, proj, up, down)
    return full.reshape(model, width), packed, normed, mem_own, mem_peer, column


def device_of(outer, inner, frame, head):
    return (outer * 2 + inner, frame, head)


def plane_peer(inner, frame, step):
    return (inner + step // 2) % 2, (frame + step % 2) % 2


def row_piece(value, row):
    return value[:, row * LANES : (row + 1) * LANES]


def tail_kernel(
    row_own, row_recv, x, middle_grad, grads, joined_sum, gain, taps, pool_gain, pool_shift,
    bias_grad, hot, space_hot, cached, mem_own, mem_recv, vectors, up_bias, rest,
    grad_in, out, rest_out, small_out,
    near, part, far, small, small_in, row_full, rest_in,
    cross_sems, near_sems, far_sems, first_sems, second_sems, rest_sems,
    *, unit, plan, table_rows,
):
    chunks, outers, _, shard_rows, cols = part.shape
    clips, rows, model = x.shape
    half = model // 2
    devices = small.shape[0]
    clip = lax.axis_index("clip")
    frame = lax.axis_index("frame")
    head = lax.axis_index("head")
    outer, inner = clip // 2, clip % 2
    place = inner * 2 + frame
    mine = (clip * 2 + frame) * 2 + head

    def device(index):
        return (index // 4, (index // 2) % 2, index % 2)

    barrier = pltpu.get_barrier_semaphore()
    each(
        1,
        devices,
        lambda step: pl.semaphore_signal(
            barrier, inc=1, device_id=device((mine + step) % devices), device_id_type=MESH_ID
        ),
    )

    def first(step):
        other = (mine + step) % devices
        return pltpu.make_async_remote_copy(
            src_ref=small.at[other], dst_ref=small_in.at[step],
            send_sem=first_sems.at[0, step], recv_sem=first_sems.at[1, step],
            device_id=device(other), device_id_type=MESH_ID,
        )

    def second(step, block):
        return pltpu.make_async_remote_copy(
            src_ref=small_out.at[block], dst_ref=small_out.at[block],
            send_sem=second_sems.at[0, step], recv_sem=second_sems.at[1, step],
            device_id=device((mine + step) % devices), device_id_type=MESH_ID,
        )

    def near_copy(chunk, step):
        there_inner, there_frame = plane_peer(inner, frame, step)
        return pltpu.make_async_remote_copy(
            src_ref=grads.at[:, there_inner * 2 + there_frame, :, pl.ds(chunk * cols, cols)],
            dst_ref=near.at[chunk, step - 1],
            send_sem=near_sems.at[0, chunk, step - 1], recv_sem=near_sems.at[1, chunk, step - 1],
            device_id=device_of(outer, there_inner, there_frame, head), device_id_type=MESH_ID,
        )

    def far_copy(chunk, step):
        there = (outer + step) % outers
        return pltpu.make_async_remote_copy(
            src_ref=part.at[chunk, there], dst_ref=far.at[chunk, step],
            send_sem=far_sems.at[0, chunk, step], recv_sem=far_sems.at[1, chunk, step],
            device_id=device_of(there, inner, frame, head), device_id_type=MESH_ID,
        )

    def cross_copy(index, side):
        lanes = pl.ds(pl.multiple_of(side * half, LANES), half)
        return pltpu.make_async_remote_copy(
            src_ref=row_full.at[index, :, lanes], dst_ref=row_full.at[index, :, lanes],
            send_sem=cross_sems.at[0, index], recv_sem=cross_sems.at[1, index],
            device_id=(clip, frame, 1 - head), device_id_type=MESH_ID,
        )

    def rest_copy(step):
        there = (outer + step) % outers
        return pltpu.make_async_remote_copy(
            src_ref=rest.at[there], dst_ref=rest_in.at[step],
            send_sem=rest_sems.at[0, step], recv_sem=rest_sems.at[1, step],
            device_id=device_of(there, inner, frame, head), device_id_type=MESH_ID,
        )

    small[...] = jnp.zeros_like(small)
    pl.semaphore_wait(barrier, devices - 1)
    for chunk in range(chunks):
        for step in range(1, 4):
            near_copy(chunk, step).start()
    lanes_here = pl.ds(pl.multiple_of(head * half, LANES), half)

    def join(index):
        total = row_own[index].astype(F32) + row_recv[index].astype(F32)
        row_full[index, :, lanes_here] = total.astype(BF)
        cross_copy(index, head).start()

    each(0, clips, join)
    each(1, outers, lambda step: rest_copy(step).start())

    gain_sum = jnp.zeros((1, model), F32)
    shift_sum = jnp.zeros((1, model), F32)
    for index in range(clips):
        cross_copy(index, 1 - head).wait_recv()
        incoming = row_full[index].astype(F32)
        centred, rate = row_stats(x[index].astype(F32))
        normal = centred * rate
        product = incoming * normal
        gain_sum = gain_sum + jnp.sum(product, axis=0, keepdims=True)
        shift_sum = shift_sum + jnp.sum(incoming, axis=0, keepdims=True)
        scaled = incoming * gain[0:1]
        mean_scaled = jnp.sum(scaled, axis=-1, keepdims=True) * (1.0 / model)
        mean_both = jnp.sum(scaled * normal, axis=-1, keepdims=True) * (1.0 / model)
        result = rate * (scaled - mean_scaled - normal * mean_both) + middle_grad[index]
        grad_in[index] = result.astype(BF)

    rows_small = small.shape[1]

    def put(row, value):
        count = value.shape[0]
        done = 0
        while done < count:
            block, offset = divmod(row + done, rows_small)
            size = min(count - done, rows_small - offset)
            small[block, offset : offset + size, : value.shape[1]] = value[done : done + size]
            done += size

    def put_wide(row, value):
        for index in range(value.shape[1] // LANES):
            put(row + index, row_piece(value, index))

    wide_rows_count = model // LANES

    @pl.when(head == 0)
    def _():
        put_wide(plan["gain"], gain_sum)
        put_wide(plan["gain"] + wide_rows_count, vectors[0:1])
        put_wide(plan["shift"], shift_sum)
        put_wide(plan["shift"] + wide_rows_count, vectors[1:2])
        put_wide(plan["rows"], vectors[2:3])
        put_wide(plan["rows"] + wide_rows_count, vectors[3:4])

    joined_rows = joined_sum.shape[1] // LANES
    up_rows = up_bias.shape[1] // LANES
    for which in range(2):

        @pl.when(head == which)
        def _():
            for side in range(2):

                @pl.when(frame == side)
                def _():
                    put_wide(plan["joined"] + (2 * which + side) * joined_rows, joined_sum[...])

            put_wide(plan["up"] + which * up_rows, up_bias[...])

    heads = taps.shape[2] // (3 * LANES)
    tap_sum = jnp.sum(taps[...], axis=1)
    for member in range(3):
        totals = []
        for value in (tap_sum, pool_gain[...], pool_shift[...]):
            total = row_piece(value, member * heads)
            for index in range(1, heads):
                total = total + row_piece(value, member * heads + index)
            totals.append(total)
        put(plan["taps"] + member * 27, totals[0])
        put(plan["pool_gain"] + member, totals[1])
        put(plan["pool_shift"] + member, totals[2])
    heads_here = joined_sum.shape[1] // (3 * LANES)
    for side in range(2):

        @pl.when(frame == side)
        def _():
            for member in range(2):
                totals = [jnp.zeros((1, unit), F32) for _ in range(FRAMES // MEMF)]
                for index in range(clips):
                    for which, part in ((side, mem_own), (1 - side, mem_recv)):
                        for spot in range(heads_here):
                            at = (member * heads_here + spot) * LANES
                            value = part[index, :CELLS, at : at + unit].astype(F32)
                            at = ((2 * member + which) * heads_here + spot) * unit
                            for step in range(len(totals)):
                                rows_here = cached[
                                    index, step * CELLS : (step + 1) * CELLS, at : at + unit
                                ]
                                product = rows_here.astype(F32) * value
                                totals[step] = totals[step] + jnp.sum(
                                    product, axis=0, keepdims=True
                                )
                for step in range(len(totals)):
                    put(plan["squeeze"] + member * len(totals) + step, totals[step])

    time_sum = jnp.zeros((hot.shape[2], LANES), F32)
    bias_sum = jnp.zeros((BIAS_COLS, LANES), F32)
    for index in range(clips):
        value = bias_grad[index]
        bias_sum = bias_sum + value
        value = value[: hot.shape[1]]
        high = value.astype(BF)
        low = (value - high.astype(F32)).astype(BF)
        time_sum = time_sum + dot_f32(hot[index], high, ((0,), (0,)))
        time_sum = time_sum + dot_f32(hot[index], low, ((0,), (0,)))
    put(plan["time"], time_sum[:table_rows])
    high = bias_sum.astype(BF)
    low = (bias_sum - high.astype(F32)).astype(BF)
    space_sum = dot_f32(space_hot[...], high, ((1,), (0,)))
    space_sum = space_sum + dot_f32(space_hot[...], low, ((1,), (0,)))
    put(plan["space"], space_sum[: 2 * (2 * SIDE - 1)])

    each(1, devices, lambda step: first(step).start())

    def reduce_near(chunk):
        lanes = slice(chunk * cols, (chunk + 1) * cols)
        for step in range(1, 4):
            near_copy(chunk, step).wait_recv()

        def gathered(index):
            own = grads[index, place, :, lanes].astype(F32)
            own = own + near[chunk, 1, index].astype(F32)
            other = near[chunk, 0, index].astype(F32) + near[chunk, 2, index].astype(F32)
            return own, other

        def send(step):
            there = (outer + step) % outers
            own, other = gathered(there)
            part[chunk, there, 0] = own.astype(BF)
            part[chunk, there, 1] = other.astype(BF)
            far_copy(chunk, step).start()

        each(1, outers, send)
        own, other = gathered(outer)
        far[chunk, 0, 0] = own.astype(BF)
        far[chunk, 0, 1] = other.astype(BF)

    reduce_near(0)
    each(1, devices, lambda step: first(step).wait_recv())
    total = lax.fori_loop(1, devices, lambda step, sums: sums + small_in[step], small[mine])
    small_out[mine] = total
    each(1, devices, lambda step: second(step, mine).start())
    for chunk in range(1, chunks):
        reduce_near(chunk)
    heads = cols // LANES
    group = heads * unit
    for chunk in range(chunks):
        each(1, outers, lambda step: far_copy(chunk, step).wait_recv())
        totals = []
        for side in range(2):
            totals.append(
                lax.fori_loop(
                    0,
                    outers,
                    lambda step, sums: sums + far[chunk, step, side].astype(F32),
                    jnp.zeros((shard_rows, cols), F32),
                )
            )

        def store(order):
            for spot, side in enumerate(order):
                for index in range(heads):
                    at = (2 * chunk + spot) * group + index * unit
                    value = totals[side][:, index * LANES : index * LANES + unit]
                    out[:, at : at + unit] = value

        @pl.when(frame == 0)
        def _():
            store((0, 1))

        @pl.when(frame == 1)
        def _():
            store((1, 0))

    each(1, outers, lambda step: rest_copy(step).wait_recv())
    rest_out[...] = lax.fori_loop(
        1,
        outers,
        lambda step, sums: sums + rest_in[step].astype(F32),
        rest[outer].astype(F32),
    )
    each(1, devices, lambda step: second(step, (mine + devices - step) % devices).wait_recv())
    each(1, devices, lambda step: first(step).wait_send())
    each(1, devices, lambda step: second(step, mine).wait_send())
    each(1, outers, lambda step: rest_copy(step).wait_send())
    for index in range(clips):
        cross_copy(index, head).wait_send()
    for chunk in range(chunks):
        for step in range(1, 4):
            near_copy(chunk, step).wait_send()
        each(1, outers, lambda step: far_copy(chunk, step).wait_send())


def unpack_kernel(
    small, qkv, early, late, grad_in, block_out,
    grad_in_out, block_out_out, gain_out, shift_out, rows_out, joined_out, up_out, taps_out,
    pool_gain_out, pool_shift_out, squeeze_out, time_out, space_out, qkv_out, proj_out,
    up_grad_out, down_out, time_rows, *, plan, unit,
):
    for index in range(grad_in.shape[0]):
        grad_in_out[index] = grad_in[index]
        block_out_out[index] = block_out[index]
    head = lax.axis_index("head")
    rows_small = small.shape[1]

    def take(row, target):
        count = target.shape[0]
        done = 0
        while done < count:
            block, offset = divmod(row + done, rows_small)
            size = min(count - done, rows_small - offset)
            target[done : done + size] = small[block, offset : offset + size, : target.shape[1]]
            done += size

    def take_wide(row, target, at):
        for index in range(target.shape[1] // LANES):
            block, offset = divmod(row + index, rows_small)
            target[at : at + 1, index * LANES : (index + 1) * LANES] = small[
                block, offset : offset + 1
            ]

    per_row = gain_out.shape[1] // LANES
    for index in range(2):
        take_wide(plan["gain"] + index * per_row, gain_out, index)
        take_wide(plan["shift"] + index * per_row, shift_out, index)
        take_wide(plan["rows"] + index * per_row, rows_out, index)
    width = joined_out.shape[1]
    group = width // 2
    heads = group // unit
    joined_rows = 3 * heads
    up_rows = up_out.shape[0]
    for which in range(2):

        @pl.when(head == which)
        def _():
            for member in range(3):
                for side in range(2):
                    for index in range(heads):
                        row = plan["joined"] + (2 * which + side) * joined_rows
                        block, offset = divmod(row + member * heads + index, rows_small)
                        at = side * group + index * unit
                        joined_out[member : member + 1, at : at + unit] = small[
                            block, offset : offset + 1, :unit
                        ]
            take(plan["up"] + which * up_rows, up_out)

    for member in range(3):
        take(plan["taps"] + member * 27, taps_out.at[member])
        qkv_out[member] = qkv[:, member * width : (member + 1) * width]
    take(plan["pool_gain"], pool_gain_out)
    take(plan["pool_shift"], pool_shift_out)
    take(plan["time"], time_rows)
    time_out[...] = time_rows[...].T
    for index in range(2):
        count = squeeze_out.shape[1]
        take(plan["squeeze"] + index * count, squeeze_out.at[index])
        for spot in range(space_out.shape[0]):
            block, offset = divmod(
                plan["space"] + index * space_out.shape[0] + spot, rows_small
            )
            space_out[spot, index : index + 1] = small[block, offset : offset + 1, :unit]
    proj_width, up_width = proj_out.shape[1], up_grad_out.shape[1]
    proj_out[...] = early[:, :proj_width]
    up_grad_out[...] = early[:, proj_width : proj_width + up_width]
    at = proj_width + up_width
    first = early.shape[1] - at
    down_out[:, :first] = early[:, at:]
    down_out[:, first:] = late[...]


def unpack(small, qkv, early, late, grad_in, block_out, plan, unit, hidden_width, table_rows):
    shard_rows, width = qkv.shape
    model = grad_in.shape[2]
    rest_width = early.shape[1] + late.shape[1]
    out = jax.ShapeDtypeStruct
    vmem = pl.BlockSpec(memory_space=pltpu.VMEM)
    shapes = [
        out(grad_in.shape, BF),
        out(block_out.shape, BF),
        out((2, model), F32),
        out((2, model), F32),
        out((2, model), F32),
        out((3, width // 3), F32),
        out((hidden_width // LANES, LANES), F32),
        out((3, 27, unit), F32),
        out((3, unit), F32),
        out((3, unit), F32),
        out((2, FRAMES // MEMF, unit), F32),
        out((unit, table_rows), F32),
        out((2 * SIDE - 1, 2, unit), F32),
        out((3, shard_rows, width // 3), F32),
        out((shard_rows, rest_width - 2 * hidden_width), F32),
        out((shard_rows, hidden_width), F32),
        out((shard_rows, hidden_width), F32),
    ]
    return pl.pallas_call(
        partial(unpack_kernel, plan=plan, unit=unit),
        in_specs=[vmem] * 6,
        out_specs=[vmem] * len(shapes),
        out_shape=shapes,
        scratch_shapes=[pltpu.VMEM((table_rows, unit), F32)],
        compiler_params=pltpu.CompilerParams(vmem_limit_bytes=VMEM_LIMIT),
        name="unpack_results",
    )(small, qkv, early, late, grad_in, block_out)


def tail(
    row_own, row_recv, x, middle_grad, grads, joined_sum, gain, taps, pool_gain, pool_shift,
    bias_grad, hot, space_hot, cached, mem_own, mem_recv, vectors, up_bias, rest, clip_count, devices,
    unit, table_rows,
):
    clips, rows, model = x.shape
    wide = grads.shape[3]
    heads = wide // (3 * LANES)
    width = 3 * 2 * heads * unit
    outers = clip_count // 2
    shard_rows = model // (4 * outers)
    chunks = 3
    cols = wide // chunks
    plan = {}
    at = 0
    for name, count in (
        ("gain", 2 * model // LANES),
        ("shift", 2 * model // LANES),
        ("rows", 2 * model // LANES),
        ("joined", 4 * wide // LANES),
        ("up", 2 * up_bias.shape[1] // LANES),
        ("taps", 81),
        ("pool_gain", 3),
        ("pool_shift", 3),
        ("squeeze", 2 * FRAMES // MEMF),
        ("time", table_rows),
        ("space", 2 * (2 * SIDE - 1)),
    ):
        plan[name] = at
        at += count
    block = -(-at // (devices * 8)) * 8
    out = jax.ShapeDtypeStruct
    dma = pltpu.SemaphoreType.DMA
    vmem = pl.BlockSpec(memory_space=pltpu.VMEM)
    shapes = [
        out((clips, rows, model), BF),
        out((shard_rows, width), F32),
        out((shard_rows, rest.shape[2]), F32),
        out((devices, block, LANES), F32),
    ]
    results = pl.pallas_call(
        partial(tail_kernel, unit=unit, plan=plan, table_rows=table_rows),
        in_specs=[vmem] * 19,
        out_specs=[vmem] * len(shapes),
        out_shape=shapes,
        scratch_shapes=[
            pltpu.VMEM((chunks, 3, outers, shard_rows, cols), BF),
            pltpu.VMEM((chunks, outers, 2, shard_rows, cols), BF),
            pltpu.VMEM((chunks, outers, 2, shard_rows, cols), BF),
            pltpu.VMEM((devices, block, LANES), F32),
            pltpu.VMEM((devices, block, LANES), F32),
            pltpu.VMEM((clips, rows, model), BF),
            pltpu.VMEM(rest.shape, BF),
            dma((2, clips)),
            dma((2, chunks, 3)),
            dma((2, chunks, outers)),
            dma((2, devices)),
            dma((2, devices)),
            dma((2, outers)),
        ],
        compiler_params=pltpu.CompilerParams(
            collective_id=0, has_side_effects=True, vmem_limit_bytes=VMEM_LIMIT
        ),
        name="tail_gradients",
    )(
        row_own, row_recv, x, middle_grad, grads, joined_sum, gain, taps, pool_gain, pool_shift,
        bias_grad, hot, space_hot, cached, mem_own, mem_recv, vectors, up_bias, rest,
    )
    return results, plan


def feed_kernel(
    att_own, att_recv, x, cot, weights, gain, shift, out_shift, up_shift,
    block_out, middle_grad, grad_own, grad_send, grad_rest, vectors, up_bias,
    attended, normed, cots, active, hidden_low, branch, middle, send, recv, sems,
):
    clips, rows, model = x.shape
    span = attended.shape[0] // clips
    group = att_own.shape[2]
    head_width = 2 * group
    hidden_width = up_shift.shape[1]
    tiles = 4
    tile = hidden_width // tiles
    clip_at = lax.axis_index("clip")
    frame = lax.axis_index("frame")
    head = lax.axis_index("head")
    partner = (clip_at, frame, 1 - head)

    def cross(kind, index):
        return pltpu.make_async_remote_copy(
            src_ref=send.at[kind, index], dst_ref=recv.at[kind, index],
            send_sem=sems.at[0, kind, index], recv_sem=sems.at[1, kind, index],
            device_id=partner, device_id_type=MESH_ID,
        )

    barrier = pltpu.get_barrier_semaphore()
    pl.semaphore_signal(barrier, inc=1, device_id=partner, device_id_type=MESH_ID)
    for ref in (attended, normed, cots, branch):
        ref[...] = jnp.zeros_like(ref)

    def assemble(low, high):
        for index in range(clips):
            at = slice(index * span, index * span + rows)
            attended[at, :group] = low[index]
            attended[at, group:] = high[index]

    @pl.when(frame == 0)
    def _():
        assemble(att_own, att_recv)

    @pl.when(frame == 1)
    def _():
        assemble(att_recv, att_own)

    for index in range(clips):
        cots[index * span : index * span + rows] = cot[index]
    pl.semaphore_wait(barrier, 1)

    def block_rows(index):
        return pl.ds(pl.multiple_of(index * span, 16), span)

    def project(index):
        part = dot_f32(attended[block_rows(index)], weights[:, :head_width], ((1,), (1,)))
        send[0, index] = part[:rows].astype(BF)
        cross(0, index).start()

    each(0, clips, project)

    def feed(index, bias_sum):
        cross(0, index).wait_recv()
        branch_rows = send[0, index].astype(F32) + recv[0, index].astype(F32)
        value = x[index].astype(F32) + branch_rows + out_shift[0:1]
        middle[index] = value
        centred, rate = row_stats(value)
        low = (centred * rate * gain[1:2] + shift[1:2]).astype(BF)
        at = pl.multiple_of(index * span, 16)
        normed[pl.ds(at, rows)] = low
        low = normed[block_rows(index)]
        cot_rows = cots[block_rows(index)]
        out_part = jnp.zeros((span, model), F32)
        norm_part = jnp.zeros((span, model), F32)
        sums = []
        for step in range(tiles):
            lanes = slice(step * tile, (step + 1) * tile)
            up = weights[:, head_width + step * tile : head_width + (step + 1) * tile]
            at = head_width + hidden_width + step * tile
            down = weights[:, at : at + tile]
            hidden = dot_f32(low, up, ((1,), (0,))) + up_shift[:, lanes]
            incoming = dot_f32(cot_rows, down, ((1,), (0,)))
            normal = 0.5 * (1.0 + lax.erf(hidden * (0.5**0.5)))
            density = jnp.exp(hidden * hidden * -0.5) * ((2.0 * np.pi) ** -0.5)
            acted = (hidden * normal).astype(BF)
            back = (incoming * (normal + hidden * density)).astype(BF)
            active[block_rows(index), lanes] = acted
            hidden_low[block_rows(index), lanes] = back
            sums.append(jnp.sum(back.astype(F32), axis=0, keepdims=True))
            out_part = out_part + dot_f32(acted, down, ((1,), (1,)))
            norm_part = norm_part + dot_f32(back, up, ((1,), (1,)))
        send[1, index] = norm_part[:rows].astype(BF)
        cross(1, index).start()
        send[2, index] = out_part[:rows].astype(BF)
        cross(2, index).start()
        return bias_sum + jnp.concatenate(sums, axis=1)

    up_bias[...] = lax.fori_loop(0, clips, feed, jnp.zeros((1, hidden_width), F32))

    for step in range(tiles):
        lanes = slice(step * tile, (step + 1) * tile)
        value = dot_f32(normed[...], hidden_low[:, lanes], ((0,), (0,)))
        at = head_width + step * tile
        grad_rest[:, at : at + tile] = value.astype(BF)
        value = dot_f32(cots[...], active[:, lanes], ((0,), (0,)))
        at = head_width + hidden_width + step * tile
        grad_rest[:, at : at + tile] = value.astype(BF)

    def back(index, sums):
        gain_sum, shift_sum, first_sum, second_sum = sums
        cross(1, index).wait_recv()
        incoming = send[1, index].astype(F32) + recv[1, index].astype(F32)
        centred, rate = row_stats(middle[index])
        normal = centred * rate
        scaled = incoming * gain[1:2]
        mean_scaled = jnp.sum(scaled, axis=-1, keepdims=True) * (1.0 / model)
        mean_both = jnp.sum(scaled * normal, axis=-1, keepdims=True) * (1.0 / model)
        cot_rows = cot[index].astype(F32)
        value = cot_rows + rate * (scaled - mean_scaled - normal * mean_both)
        middle_grad[index] = value
        at = pl.multiple_of(index * span, 16)
        branch[pl.ds(at, rows)] = value.astype(BF)
        part = dot_f32(branch[block_rows(index)], weights[:, :head_width], ((1,), (0,)))
        part = part[:rows].astype(BF)

        @pl.when(frame == 0)
        def _():
            grad_own[index] = part[:, :group]
            grad_send[index] = part[:, group:]

        @pl.when(frame == 1)
        def _():
            grad_send[index] = part[:, :group]
            grad_own[index] = part[:, group:]

        cross(2, index).wait_recv()
        out_rows = send[2, index].astype(F32) + recv[2, index].astype(F32)
        block_out[index] = (middle[index] + out_rows + out_shift[1:2]).astype(BF)

        def column(rows_here):
            return jnp.sum(rows_here, axis=0, keepdims=True)

        return (
            gain_sum + column(incoming * normal),
            shift_sum + column(incoming),
            first_sum + column(value),
            second_sum + column(cot_rows),
        )

    start = tuple(jnp.zeros((1, model), F32) for _ in range(4))
    sums = lax.fori_loop(0, clips, back, start)
    for row in range(4):
        vectors[row : row + 1] = sums[row]
    value = dot_f32(branch[...], attended[...], ((0,), (0,)))
    grad_rest[:, :head_width] = value.astype(BF)
    for kind in range(3):
        each(0, clips, lambda index: cross(kind, index).wait_send())


def feed(att_own, att_recv, x, cot, weights, gain, shift, out_shift, up_shift):
    clips, rows, model = x.shape
    group = att_own.shape[2]
    hidden_width = up_shift.shape[1]
    span = -(-rows // 16) * 16
    out = jax.ShapeDtypeStruct
    vmem = pl.BlockSpec(memory_space=pltpu.VMEM)
    shapes = [
        out((clips, rows, model), BF),
        out((clips, rows, model), F32),
        out((clips, rows, group), BF),
        out((clips, rows, group), BF),
        out(weights.shape, BF),
        out((4, model), F32),
        out((1, hidden_width), F32),
    ]
    return pl.pallas_call(
        feed_kernel,
        in_specs=[vmem] * 9,
        out_specs=[vmem] * len(shapes),
        out_shape=shapes,
        scratch_shapes=[
            pltpu.VMEM((clips * span, 2 * group), BF),
            pltpu.VMEM((clips * span, model), BF),
            pltpu.VMEM((clips * span, model), BF),
            pltpu.VMEM((clips * span, hidden_width), BF),
            pltpu.VMEM((clips * span, hidden_width), BF),
            pltpu.VMEM((clips * span, model), BF),
            pltpu.VMEM((clips, rows, model), F32),
            pltpu.VMEM((3, clips, rows, model), BF),
            pltpu.VMEM((3, clips, rows, model), BF),
            pltpu.SemaphoreType.DMA((2, 3, clips)),
        ],
        compiler_params=pltpu.CompilerParams(
            collective_id=4, has_side_effects=True, vmem_limit_bytes=VMEM_LIMIT
        ),
        name="feed_forward_both_ways",
    )(att_own, att_recv, x, cot, weights, gain, shift, out_shift, up_shift)


def precise(pattern, *operands):
    return jnp.einsum(pattern, *operands, precision=lax.Precision.HIGHEST)


def split_groups(value, which, axis):
    half = value.shape[axis] // 2
    low = lax.slice_in_dim(value, 0, half, axis=axis)
    high = lax.slice_in_dim(value, half, None, axis=axis)
    first = which == 0
    return jnp.where(first, low, high), jnp.where(first, high, low)


def join_groups(own, peer, which, axis):
    first = which == 0
    return jnp.concatenate([jnp.where(first, own, peer), jnp.where(first, peer, own)], axis=axis)


def time_choices(stride_group, memory_place, which, own, table_rows):
    local = jnp.arange(own, dtype=jnp.int32)
    times = jnp.concatenate([which * own + local, (1 - which) * own + local])
    stride = jnp.left_shift(jnp.int32(2), stride_group)[:, None, None]
    offset = 8 * (FRAMES - 1)
    current = stride * (times[None, :, None] - times[None, None, :]) + offset
    slots = [memory_place[:, index : index + 1] for index in range(4)]
    first = jnp.concatenate([slots[2], slots[0], slots[3], slots[1]], axis=1)
    second = jnp.concatenate([slots[3], slots[1], slots[2], slots[0]], axis=1)
    places = jnp.where(which == 0, first, second)
    memory = stride * times[None, :, None] + places[:, None, :] + offset
    chosen = jnp.concatenate([current, memory], axis=2)
    return (chosen[..., None] == jnp.arange(table_rows, dtype=jnp.int32)).astype(F32)


def space_choices():
    places = np.arange(SIDE)
    offsets = places[:, None] - places[None, :] + SIDE - 1
    hot = offsets.reshape(-1)[:, None] == np.arange(2 * SIDE - 1)[None, :]
    return jnp.asarray(hot.astype(np.float32))


def space_sums():
    spans = 2 * SIDE - 1
    hot = np.zeros((32, BIAS_COLS), np.float32)
    for axis in range(2):
        for query in range(SIDE):
            for key in range(SIDE):
                col = SPACE_AT + axis * CELLS + query * SIDE + key
                hot[axis * spans + query - key + SIDE - 1, col] = 1.0
    return hot


def wide_rows(rows, heads):
    count, members, unit = rows.shape
    padded = jnp.pad(rows, ((0, 0), (0, 0), (0, LANES - unit)))
    spread = jnp.broadcast_to(padded[:, :, None], (count, members, heads, LANES))
    return spread.reshape(count, members * heads * LANES)


def local(
    clips_in,
    cached_kv,
    old_memory,
    stride_group,
    memory_place,
    norm_gain,
    norm_shift,
    qkv_weight,
    qkv_shift,
    pool_kernel,
    pool_gain,
    pool_shift,
    squeeze_kernel,
    time_table,
    space_tables,
    proj_weight,
    out_shift,
    up_weight,
    up_shift,
    down_weight,
    cotangent,
):
    clip_count, rows_clip, model_width = clips_in.shape
    head_width = qkv_weight.shape[2]
    unit = pool_gain.shape[1]
    head_count = head_width // unit
    frame_count = lax.axis_size("frame")
    heads = head_count // frame_count
    own_frames = rows_clip // CELLS
    group_width = heads * unit
    group_span = FRAMES // MEMF
    scale = unit ** (-0.5)
    which = lax.axis_index("frame")
    into_np, outof_np = placement(frame_count)
    keys_np, mask_np, pad_np = bias_constants(frame_count)
    consts = (
        jnp.asarray(into_np, BF),
        jnp.asarray(outof_np, BF),
        jnp.asarray(keys_np, BF),
        jnp.asarray(mask_np),
        jnp.asarray(pad_np),
    )

    cached_flat = cached_kv.reshape(clip_count, rows_clip, 2 * head_width)
    attn_group, packed, normed, mem_own, mem_peer, column = project(
        clips_in, qkv_weight.transpose(1, 0, 2), norm_gain, norm_shift, qkv_shift,
        cached_flat, old_memory.reshape(clip_count, -1, 2 * head_width), squeeze_kernel,
        proj_weight.T, up_weight, down_weight.T, lax.axis_size("clip"), unit,
    )

    time_hot = time_choices(stride_group, memory_place, which, own_frames, time_table.shape[0])
    time_rows = precise("ctkr,rd->ctkd", time_hot, time_table).reshape(clip_count, -1, unit)
    space_hot = space_choices()
    space_rows = precise("pr,xrd->xpd", space_hot, space_tables).reshape(2 * CELLS, unit)
    space_rows = jnp.broadcast_to(space_rows[None], (clip_count,) + space_rows.shape)
    bias = jnp.concatenate(
        [
            jnp.pad(time_rows, ((0, 0), (0, SPACE_AT - time_rows.shape[1]), (0, LANES - unit))),
            jnp.pad(
                space_rows,
                ((0, 0), (0, BIAS_COLS - SPACE_AT - 2 * CELLS), (0, LANES - unit)),
            ),
        ],
        axis=1,
    )
    bias = bias * (1.0 / scale)
    forward = attention_forward(
        packed, mem_own, mem_peer, column, consts, pool_kernel, pool_gain, pool_shift, bias, scale, unit,
        rows_clip,
    )
    attended_own, attended_peer, rest_full = forward[:3]
    rest_full = rest_full.reshape(model_width, -1)
    saved = forward[3:]
    block_out, middle_grad, attended_grad_own, attended_grad_send, grad_rest, vectors, up_grads = (
        feed(
            attended_own, attended_peer, clips_in, cotangent, rest_full, norm_gain,
            norm_shift, out_shift, up_shift.reshape(1, -1),
        )
    )
    outers = lax.axis_size("clip") // 2
    grad_rest = grad_rest.reshape(outers, 4, -1, grad_rest.shape[1])
    backward = attention_backward(
        packed, normed, attn_group, attended_grad_own, attended_grad_send, grad_rest, consts,
        pool_kernel, pool_gain, bias, saved, scale, unit,
    )
    row_own, row_recv, mem_grad_own, mem_grad_peer = backward[:4]
    taps_grad, pool_gain_grad, pool_shift_grad, bias_grad = backward[4:8]
    attn_grad, joined_grad, rest_part, rest_early = backward[8:]

    time_count = time_rows.shape[1]
    hot = time_hot.reshape(clip_count, time_count, -1).astype(BF)
    hot = jnp.pad(hot, ((0, 0), (0, 0), (0, -hot.shape[2] % LANES)))
    devices = lax.axis_size("clip") * frame_count * lax.axis_size("head")
    (grad_in, qkv_shard, rest_late, small), plan = tail(
        row_own, row_recv, clips_in, middle_grad,
        attn_grad.reshape(outers, 4, -1, attn_grad.shape[1]), joined_grad, norm_gain, taps_grad,
        pool_gain_grad, pool_shift_grad, bias_grad, hot,
        jnp.asarray(space_sums(), BF), cached_flat, mem_grad_own, mem_grad_peer, vectors,
        up_grads, rest_part, lax.axis_size("clip"), devices, unit, time_table.shape[0],
    )
    (
        grad_in, block_out, gain_sums, shift_sums, out_sums, qkv_bias_sum, up_bias_sum, kernel_sum,
        pool_gain_sum, pool_shift_sum, squeeze_sum, time_sum, space_sum, qkv_shard, proj_shard,
        up_shard, down_shard,
    ) = unpack(
        small, qkv_shard, rest_early, rest_late, grad_in, block_out, plan, unit,
        up_weight.shape[1], time_table.shape[0],
    )
    return (
        block_out,
        grad_in,
        gain_sums,
        shift_sums,
        qkv_shard.transpose(1, 0, 2),
        qkv_bias_sum,
        kernel_sum,
        pool_gain_sum,
        pool_shift_sum,
        squeeze_sum,
        time_sum.T,
        space_sum.transpose(1, 0, 2),
        proj_shard.T,
        out_sums,
        up_shard,
        up_bias_sum.reshape(-1),
        down_shard.T,
    )


def solution(mesh):
    return jax.shard_map(
        local,
        mesh=mesh,
        in_specs=(
            P("clip", "frame", None),
            P("clip", "frame", None, "head"),
            P("clip", "frame", None, "head"),
            P("clip"),
            P("clip", None),
            P(),
            P(),
            P(("clip", "frame"), None, "head"),
            P(None, "head"),
            P(),
            P(),
            P(),
            P(),
            P(),
            P(),
            P("head", ("clip", "frame")),
            P(),
            P(("clip", "frame"), "head"),
            P("head"),
            P("head", ("clip", "frame")),
            P("clip", "frame", None),
        ),
        out_specs=(
            P("clip", "frame", None),
            P("clip", "frame", None),
            P(),
            P(),
            P(("clip", "frame"), None, "head"),
            P(None, "head"),
            P(),
            P(),
            P(),
            P(),
            P(),
            P(),
            P("head", ("clip", "frame")),
            P(),
            P(("clip", "frame"), "head"),
            P("head"),
            P("head", ("clip", "frame")),
        ),
        check_vma=False,
    )
```

```python
from functools import partial

import jax
import jax.numpy as jnp
import numpy as np
from jax import lax
from jax.experimental import pallas as pl
from jax.experimental.pallas import tpu as pltpu
from jax.sharding import PartitionSpec as P

FRAMES = 8
MEMF = 2
SIDE = 7
CELLS = SIDE * SIDE
LANES = 128
HALF = 208
QROWS = 2 * HALF
GRID_ROWS = FRAMES * SIDE * 8
MEM_AT = QROWS
MEM_PAD = 112
MEM_BACK = 64
MEM_STEP = 56
TURN_STEP = 3
TURN_PAIRS = 1
TURN_LAG = 5
KROWS = 640
BIAS_COLS = 256
SPACE_AT = 128
PAD_LANE = 127
BF = jnp.bfloat16
F32 = jnp.float32
VMEM_LIMIT = 60 * 1024 * 1024
MESH_ID = pl.DeviceIdType.MESH


def dot_f32(a, b, dims):
    return lax.dot_general(a, b, (dims, ((), ())), preferred_element_type=F32)


def frame_order(first, own):
    rest = [t for t in range(FRAMES) if not first * own <= t < (first + 1) * own]
    return list(range(first * own, (first + 1) * own)) + rest


def placement(frame_count):
    own = FRAMES // frame_count
    into = np.zeros((frame_count, GRID_ROWS, QROWS), np.float32)
    for first in range(frame_count):
        for slot, frame in enumerate(frame_order(first, own)):
            base = (slot // own) * HALF + (slot % own) * CELLS
            for high in range(SIDE):
                for wide in range(SIDE):
                    row = (frame * SIDE + high) * 8 + wide
                    into[first, row, base + high * SIDE + wide] = 1.0
    return into, np.ascontiguousarray(into.transpose(0, 2, 1))


def bias_constants(frame_count):
    own = FRAMES // frame_count
    frames_all = FRAMES + 2 * MEMF
    keys = np.zeros((BIAS_COLS, KROWS), np.float32)
    valid = np.zeros((KROWS,), bool)

    def mark(col, slot, high, wide):
        valid[col] = True
        for query in range(FRAMES):
            keys[query * frames_all + slot, col] = 1.0
        for place in range(SIDE):
            keys[SPACE_AT + place * SIDE + high, col] = 1.0
            keys[SPACE_AT + CELLS + place * SIDE + wide, col] = 1.0

    mask = np.zeros((QROWS, BIAS_COLS), np.float32)
    for slot in range(FRAMES):
        base = (slot // own) * HALF + (slot % own) * CELLS
        for high in range(SIDE):
            for wide in range(SIDE):
                row = base + high * SIDE + wide
                mark(row, slot, high, wide)
                mask[row, slot * frames_all : (slot + 1) * frames_all] = 1.0
                mask[row, SPACE_AT + high * SIDE : SPACE_AT + (high + 1) * SIDE] = 1.0
                low = SPACE_AT + CELLS + wide * SIDE
                mask[row, low : low + SIDE] = 1.0
    for group in range(2):
        for inner in range(MEMF):
            slot = FRAMES + group * MEMF + inner
            for high in range(SIDE):
                for wide in range(SIDE):
                    col = MEM_AT + group * MEM_PAD + inner * MEM_STEP + high * SIDE + wide
                    mark(col, slot, high, wide)
    keys[PAD_LANE, ~valid] = -1e9
    pad_row = np.zeros((1, BIAS_COLS), np.float32)
    pad_row[0, PAD_LANE] = 1.0
    return keys, mask, pad_row


def spread_heads(source, target, rows_at, units, unit, first=0):
    count = source.shape[0]
    for index in range(units):
        at = (first + index) * unit
        target[rows_at : rows_at + count, index * LANES : index * LANES + unit] = source[
            :, at : at + unit
        ]


def spread_tables(kernel_ref, taps, pairs, heads, unit):
    taps[...] = jnp.zeros_like(taps)
    for _, target in pairs:
        target[...] = jnp.zeros_like(target)
    for member in range(3):
        for index in range(heads):
            at = (member * heads + index) * LANES
            for tap in range(27):
                row = kernel_ref[member, tap : tap + 1]
                taps[tap, :, at : at + unit] = jnp.broadcast_to(row, (8, unit))
            for source, target in pairs:
                target[:, at : at + unit] = source[member : member + 1]


def load_shifted(field, shifted):
    grid = field.reshape(FRAMES, SIDE, 8, field.shape[-1])
    flat = field.reshape(FRAMES * SIDE, 8, field.shape[-1])
    shifted[1, 1 : FRAMES + 1, 1 : SIDE + 1] = grid
    shifted[0, 1 : FRAMES + 1, 1 : SIDE + 1] = pltpu.roll(flat, 1, 1).reshape(grid.shape)
    shifted[2, 1 : FRAMES + 1, 1 : SIDE + 1] = pltpu.roll(flat, 7, 1).reshape(grid.shape)


def convolve(shifted, taps, target, flip):
    tiles = target.shape[-1] // LANES

    def step(pair, carry):
        for sub in range(2):
            frame = pair * 2 + sub
            for tile in range(tiles):
                lanes = slice(tile * LANES, (tile + 1) * LANES)
                total = None
                for i in range(3):
                    for k in range(3):
                        rows = shifted[k, frame + i, :, :, lanes]
                        for j in range(3):
                            if flip:
                                tap = (2 - i) * 9 + (2 - j) * 3 + (2 - k)
                            else:
                                tap = i * 9 + j * 3 + k
                            value = rows[j : j + SIDE] * taps[tap, :, lanes][None]
                            total = value if total is None else total + value
                target[frame, :, :, lanes] = total
        return carry

    lax.fori_loop(0, FRAMES // 2, step, 0)


def tap_grads(shifted, grads, target):
    tiles = target.shape[-1] // LANES

    def step(index, carry):
        lanes = pl.ds(pl.multiple_of(index * LANES, LANES), LANES)

        def inner(frame, sums):
            centre = grads[frame + 1, 1 : SIDE + 1, :, lanes]
            new = []
            for i in range(3):
                for k in range(3):
                    rows = shifted[k, frame + i, :, :, lanes]
                    for j in range(3):
                        parts = [rows[j + high] * centre[high] for high in range(SIDE)]
                        parts.append(sums[len(new)])
                        while len(parts) > 1:
                            pairs = zip(parts[::2], parts[1::2])
                            parts = [left + right for left, right in pairs]
                        new.append(parts[0])
            return tuple(new)

        start = tuple(jnp.zeros((8, LANES), F32) for _ in range(27))
        sums = lax.fori_loop(0, FRAMES, inner, start, unroll=4)
        for i in range(3):
            for k in range(3):
                for j in range(3):
                    target[i * 9 + j * 3 + k, :, lanes] += sums[(i * 3 + k) * 3 + j]
        return carry

    lax.fori_loop(0, tiles, step, 0)


def head_stats(values, unit):
    average = jnp.sum(values, axis=-1, keepdims=True) * (1.0 / unit)
    lane = lax.broadcasted_iota(jnp.int32, values.shape, 1)
    centred = jnp.where(lane < unit, values - average, 0.0)
    variance = jnp.sum(centred * centred, axis=-1, keepdims=True) * (1.0 / unit)
    return centred, lax.rsqrt(variance + 1e-06)


def frame_partner():
    return (lax.axis_index("clip"), 1 - lax.axis_index("frame"), lax.axis_index("head"))


def partner_copy(source, target, send_sem, recv_sem):
    return pltpu.make_async_remote_copy(
        src_ref=source, dst_ref=target, send_sem=send_sem, recv_sem=recv_sem,
        device_id=frame_partner(), device_id_type=MESH_ID,
    )


def side_partner():
    clip = lax.axis_index("clip")
    across = (clip // 2) * 2 + 1 - clip % 2
    return (across, lax.axis_index("frame"), lax.axis_index("head"))


def side_copy(source, target, send_sem, recv_sem):
    return pltpu.make_async_remote_copy(
        src_ref=source, dst_ref=target, send_sem=send_sem, recv_sem=recv_sem,
        device_id=side_partner(), device_id_type=MESH_ID,
    )


def greet_partner():
    barrier = pltpu.get_barrier_semaphore()
    pl.semaphore_signal(barrier, inc=1, device_id=frame_partner(), device_id_type=MESH_ID)
    pl.semaphore_wait(barrier, 1)


def plane_stage(column_ref, rest_full, side_sems, pair_sems, turn_sems, own_sem):
    outers = column_ref.shape[0]
    split = min(TURN_PAIRS, outers)
    outer = lax.axis_index("clip") // 2
    inner = lax.axis_index("clip") % 2
    frame = lax.axis_index("frame")
    place = inner * 2 + frame
    side_place = (1 - inner) * 2 + frame
    pair_place = inner * 2 + 1 - frame
    turn_place = (1 - inner) * 2 + 1 - frame
    own_copy = pltpu.make_async_copy(column_ref, rest_full.at[:, place], own_sem)

    def side_move(at, source, target):
        return side_copy(source, target, side_sems.at[0, at], side_sems.at[1, at])

    def pair_move(at, source, target):
        return partner_copy(source, target, pair_sems.at[0, at], pair_sems.at[1, at])

    def to_side(at):
        return side_move(at, column_ref.at[at], rest_full.at[at, place])

    def to_pair(at):
        return pair_move(at, column_ref.at[at], rest_full.at[at, place])

    def turn_side(at):
        block = rest_full.at[at, pair_place]
        return side_copy(block, block, turn_sems.at[0, at], turn_sems.at[1, at])

    def turn_pair(at):
        block = rest_full.at[at, side_place]
        return partner_copy(block, block, turn_sems.at[0, at], turn_sems.at[1, at])

    def turned(at):
        block = rest_full.at[at, turn_place]
        return side_copy(block, block, turn_sems.at[0, at], turn_sems.at[1, at])

    def side_arrival(at):
        block = rest_full.at[at, side_place]
        return side_move(at, block, block)

    def pair_arrival(at):
        block = rest_full.at[at, pair_place]
        return pair_move(at, block, block)

    def send(at):
        to_side(at).start()
        to_pair(at).start()

    def spot(step):
        return (outer + step) % outers

    def turn(step):
        at = spot(step)
        if step < split:
            side_arrival(at).wait_recv()
            turn_pair(at).start()
        else:
            pair_arrival(at).wait_recv()
            turn_side(at).start()

    def finish():
        own_copy.wait()
        each(0, split, lambda step: pair_arrival(spot(step)).wait_recv())
        each(split, outers, lambda step: side_arrival(spot(step)).wait_recv())
        each(0, outers, lambda at: turned(at).wait_recv())
        each(0, split, lambda step: turn_pair(spot(step)).wait_send())
        each(split, outers, lambda step: turn_side(spot(step)).wait_send())
        each(0, outers, lambda at: to_side(at).wait_send())
        each(0, outers, lambda at: to_pair(at).wait_send())

    return own_copy, send, turn, finish


def attend_clip(
    packed, mem_own, mem_peer, frame, into_ref, outof_ref, gain_ref, shift_ref, bias_ref,
    keyhot_ref, mask_ref, pad_ref, out_own, out_peer, q_out, k_out, v_out, p_out, c_out, shifted,
    taps, heads, unit, scale, after_conv,
):
    units = 3 * heads
    own_rows = out_own.shape[0]
    load_shifted(dot_f32(into_ref[frame], packed[...], ((1,), (0,))), shifted)
    conv = c_out.at[0]
    convolve(shifted, taps, conv, False)
    after_conv()
    k_out[0, MEM_AT:, :] = jnp.zeros((KROWS - MEM_AT, heads * LANES), BF)
    v_out[0, MEM_AT:, :] = jnp.zeros((KROWS - MEM_AT, heads * LANES), BF)
    spread_heads(mem_own, k_out.at[0], MEM_AT, heads, unit, 0 * heads)
    spread_heads(mem_own, v_out.at[0], MEM_AT, heads, unit, 1 * heads)
    spread_heads(mem_peer, k_out.at[0], MEM_AT + MEM_PAD, heads, unit, 0 * heads)
    spread_heads(mem_peer, v_out.at[0], MEM_AT + MEM_PAD, heads, unit, 1 * heads)
    for index in range(units):
        lanes = slice(index * LANES, (index + 1) * LANES)
        block = conv[:, :, :, lanes].reshape(GRID_ROWS, LANES)
        centred, rate = head_stats(block, unit)
        normal = centred * rate * gain_ref[:, lanes] + shift_ref[:, lanes]
        rows = dot_f32(outof_ref[frame], normal.astype(BF), ((1,), (0,))).astype(BF)
        target = (q_out, k_out, v_out)[index // heads]
        local = slice((index % heads) * LANES, (index % heads + 1) * LANES)
        target[0, 0:QROWS, local] = rows

    bias = bias_ref[0]
    bias_high = bias.astype(BF)
    bias_low = (bias - bias_high.astype(F32)).astype(BF)
    for head in range(heads):
        lanes = slice(head * LANES, (head + 1) * LANES)
        keys = k_out[0, :, lanes]
        values = v_out[0, :, lanes]
        for half in range(2):
            rows = slice(half * HALF, (half + 1) * HALF)
            query = q_out[0, rows, lanes]
            table = dot_f32(query, bias_high, ((1,), (1,))) + dot_f32(query, bias_low, ((1,), (1,)))
            table = table * mask_ref[rows, :] + pad_ref[...]
            table_high = table.astype(BF)
            table_low = (table - table_high.astype(F32)).astype(BF)
            scores = dot_f32(query, keys, ((1,), (1,)))
            scores = scores + dot_f32(table_high, keyhot_ref[...], ((1,), (0,)))
            scores = scores + dot_f32(table_low, keyhot_ref[...], ((1,), (0,)))
            top = jnp.max(scores, axis=-1, keepdims=True)
            weights = jnp.exp((scores - top) * scale)
            total = jnp.sum(weights, axis=-1, keepdims=True)
            probs = (weights * (1.0 / total)).astype(BF)
            p_out[0, head, rows, :] = probs
            mixed = dot_f32(probs, values, ((1,), (0,))) + query.astype(F32)
            target = (out_own, out_peer)[half]
            target[:, head * unit : (head + 1) * unit] = mixed[:own_rows, :unit].astype(BF)


def forward_kernel(
    packed_ref, mem_own_ref, mem_peer_ref, column_ref, into_ref, outof_ref, kernel_ref,
    pool_gain_ref, pool_shift_ref, bias_ref, keyhot_ref, mask_ref, pad_ref,
    out_own, out_recv, rest_full, q_out, k_out, v_out, p_out, c_out,
    shifted, taps, gain_ref, shift_ref, out_send, out_sems, side_sems, pair_sems, turn_sems,
    own_sem,
    *, heads, unit, scale,
):
    clip = pl.program_id(0)
    clips = out_send.shape[0]
    frame = lax.axis_index("frame")

    def out_copy(index):
        return partner_copy(
            out_send.at[index], out_recv.at[index], out_sems.at[0, index], out_sems.at[1, index]
        )

    own_copy, send, turn, finish = plane_stage(
        column_ref, rest_full, side_sems, pair_sems, turn_sems, own_sem
    )

    @pl.when(clip == 0)
    def _():
        barrier = pltpu.get_barrier_semaphore()
        for device in (frame_partner(), side_partner()):
            pl.semaphore_signal(barrier, inc=1, device_id=device, device_id_type=MESH_ID)
        pl.semaphore_wait(barrier, 2)
        each(0, column_ref.shape[0], send)
        own_copy.start()
        shifted[...] = jnp.zeros_like(shifted)
        pairs = ((pool_gain_ref, gain_ref), (pool_shift_ref, shift_ref))
        spread_tables(kernel_ref, taps, pairs, heads, unit)

    @pl.when(clip == jnp.minimum(TURN_STEP, clips - 1))
    def _():
        for step in range(column_ref.shape[0]):
            turn(step)

    attend_clip(
        packed_ref.at[0], mem_own_ref.at[0], mem_peer_ref.at[0], frame, into_ref, outof_ref,
        gain_ref, shift_ref, bias_ref, keyhot_ref, mask_ref, pad_ref, out_own.at[0],
        out_send.at[clip], q_out, k_out, v_out, p_out, c_out, shifted, taps, heads, unit, scale,
        lambda: None,
    )
    out_copy(clip).start()

    @pl.when(clip == clips - 1)
    def _():
        finish()
        for index in range(clips):
            out_copy(index).wait()


def backward_kernel(
    packed_ref, normed_ref, weight_ref, grad_own_ref, grad_send_ref, rest_ref, into_ref, outof_ref,
    kernel_ref, pool_gain_ref, bias_ref, keyhot_ref, mask_ref, q_ref, k_ref, v_ref, p_ref, c_ref,
    row_own, row_recv, mem_own, mem_recv, taps_out, gain_out, shift_out, bias_out, weight_out,
    joined_out, rest_part, rest_out,
    shifted, taps, gain_ref, grads, spread, pooled, peer, mem_send, rest_own, rest_side, rest_send,
    rest_peer, rest_sum, rest_far, weight_sum, keep, cross_send, cross_recv, row_send,
    grad_sems, mem_sems, own_sems, side_sems, rest_sems, far_sems, cross_sems, row_sems,
    *, heads, unit, scale,
):
    units = 3 * heads
    own_rows = grad_own_ref.shape[1]
    clip = pl.program_id(0)
    clips = peer.shape[0]
    clip_at = lax.axis_index("clip")
    frame = lax.axis_index("frame")
    head_at = lax.axis_index("head")

    def grad_copy(index):
        return partner_copy(
            grad_send_ref.at[index], peer.at[index], grad_sems.at[0, index], grad_sems.at[1, index]
        )

    def mem_copy(index):
        return partner_copy(
            mem_send.at[index], mem_recv.at[index], mem_sems.at[0, index], mem_sems.at[1, index]
        )

    def row_copy(index):
        return partner_copy(
            row_send.at[index], row_recv.at[index], row_sems.at[0, index], row_sems.at[1, index]
        )

    def cross_copy(index):
        return pltpu.make_async_remote_copy(
            src_ref=cross_send.at[index], dst_ref=cross_recv.at[index],
            send_sem=cross_sems.at[0, index], recv_sem=cross_sems.at[1, index],
            device_id=(clip_at, frame, 1 - head_at), device_id_type=MESH_ID,
        )

    def finish_rows(index):
        cross_copy(index).wait_recv()
        total = (keep[index].astype(F32) + cross_recv[index].astype(F32)).astype(BF)
        row_own[index] = total[:own_rows]
        row_send[index] = total[HALF : HALF + own_rows]
        row_copy(index).start()

    chunks, outers, _, _, cols = rest_own.shape
    side_at = clip_at % 2
    outer = clip_at // 2
    early = rest_far.shape[0]

    def rest_at(side, chunk):
        return rest_ref.at[:, pl.ds(side * 2, 2), :, pl.ds(chunk * cols, cols)]

    def own_copy(chunk):
        return pltpu.make_async_copy(
            rest_at(side_at, chunk), rest_own.at[chunk], own_sems.at[chunk]
        )

    def over_copy(chunk):
        return side_copy(
            rest_at(1 - side_at, chunk), rest_side.at[chunk], side_sems.at[0, chunk],
            side_sems.at[1, chunk],
        )

    def rest_copy(chunk):
        return partner_copy(
            rest_send.at[chunk], rest_peer.at[chunk], rest_sems.at[0, chunk],
            rest_sems.at[1, chunk],
        )

    def pass_on(chunk):
        own_copy(chunk).wait()
        over_copy(chunk).wait_recv()

        def add(index):
            def total(part):
                first = rest_own[chunk, index, part].astype(F32)
                return (first + rest_side[chunk, index, part].astype(F32)).astype(BF)

            rest_send[chunk, index] = total(1 - frame)
            rest_sum[chunk, index] = total(frame)

        each(0, outers, add)
        rest_copy(chunk).start()

    def far_device(step):
        return (((outer + step) % outers) * 2 + side_at, frame, head_at)

    def far_copy(chunk, step):
        there = (outer + step) % outers
        return pltpu.make_async_remote_copy(
            src_ref=rest_sum.at[chunk, there], dst_ref=rest_far.at[chunk, step],
            send_sem=far_sems.at[0, chunk, step], recv_sem=far_sems.at[1, chunk, step],
            device_id=far_device(step), device_id_type=MESH_ID,
        )

    def settle(chunk):
        rest_copy(chunk).wait_recv()

        def add(index):
            total = rest_sum[chunk, index].astype(F32) + rest_peer[chunk, index].astype(F32)
            if chunk < early:
                rest_sum[chunk, index] = total.astype(BF)
            else:
                rest_part[index] = total.astype(BF)

        each(0, outers, add)
        if chunk < early:
            each(1, outers, lambda step: far_copy(chunk, step).start())

    @pl.when(clip == 0)
    def _():
        barrier = pltpu.get_barrier_semaphore()

        def greet(device):
            pl.semaphore_signal(barrier, inc=1, device_id=device, device_id_type=MESH_ID)

        for device in (frame_partner(), side_partner(), (clip_at, frame, 1 - head_at)):
            greet(device)
        each(1, outers, lambda step: greet(far_device(step)))
        pl.semaphore_wait(barrier, 3 + outers - 1)
        for index in range(clips):
            grad_copy(index).start()
        over_copy(0).start()
        own_copy(0).start()
        shifted[...] = jnp.zeros_like(shifted)
        grads[...] = jnp.zeros_like(grads)
        spread[...] = jnp.zeros_like(spread)
        taps_out[...] = jnp.zeros_like(taps_out)
        gain_out[...] = jnp.zeros_like(gain_out)
        shift_out[...] = jnp.zeros_like(shift_out)
        weight_sum[...] = jnp.zeros_like(weight_sum)
        joined_out[...] = jnp.zeros_like(joined_out)
        spread_tables(kernel_ref, taps, ((pool_gain_ref, gain_ref),), heads, unit)

    def pump(odd):
        for chunk in range(chunks):
            point = min(chunk + 1, 2 * clips - 1)
            if point % 2 == odd:

                @pl.when(clip == point // 2)
                def _():
                    if chunk + 1 < chunks:
                        over_copy(chunk + 1).start()
                        own_copy(chunk + 1).start()
                    pass_on(chunk)
                    if chunk:
                        settle(chunk - 1)

    pump(0)
    load_shifted(dot_f32(into_ref[frame], packed_ref[0], ((1,), (0,))), shifted)
    spread_heads(grad_own_ref.at[0], spread, 0, heads, unit)
    grad_copy(clip).wait_recv()
    spread_heads(peer.at[clip], spread, HALF, heads, unit)
    bias_low = bias_ref[0].astype(BF)
    bias_sum = jnp.zeros((BIAS_COLS, LANES), F32)
    for head in range(heads):
        lanes = slice(head * LANES, (head + 1) * LANES)
        keys = k_ref[0, :, lanes]
        values = v_ref[0, :, lanes]
        keys_grad = jnp.zeros((KROWS, LANES), F32)
        values_grad = jnp.zeros((KROWS, LANES), F32)
        for half in range(2):
            rows = slice(half * HALF, (half + 1) * HALF)
            query = q_ref[0, rows, lanes]
            out_grad = spread[rows, lanes]
            probs = p_ref[0, head, rows, :]
            wide = probs.astype(F32)
            probs_grad = dot_f32(out_grad, values, ((1,), (1,)))
            weighted = wide * probs_grad
            shared = jnp.sum(weighted, axis=-1, keepdims=True)
            score_grad = (weighted - wide * shared).astype(BF)
            values_grad = values_grad + dot_f32(probs, out_grad, ((0,), (0,)))
            keys_grad = keys_grad + dot_f32(score_grad, query, ((0,), (0,)))
            table_grad = dot_f32(score_grad, keyhot_ref[...], ((1,), (1,))) * mask_ref[rows, :]
            table_low = table_grad.astype(BF)
            query_grad = dot_f32(score_grad, keys, ((1,), (0,)))
            query_grad = query_grad + dot_f32(table_low, bias_low, ((1,), (0,)))
            query_grad = query_grad * scale + out_grad.astype(F32)
            pooled[rows, lanes] = query_grad.astype(BF)
            bias_sum = bias_sum + dot_f32(table_low, query, ((0,), (0,)))
        keys_grad = (keys_grad * scale).astype(BF)
        values_grad = values_grad.astype(BF)
        for member, part in enumerate((keys_grad, values_grad)):
            at = ((member + 1) * heads + head) * LANES
            pooled[:, at : at + LANES] = part[:QROWS]
            at = (member * heads + head) * LANES
            low = MEM_AT + MEM_PAD
            mem_own[0, :, at : at + LANES] = part[MEM_AT : MEM_AT + MEM_BACK]
            mem_send[clip, :, at : at + LANES] = part[low : low + MEM_BACK]
    bias_out[0] = bias_sum
    mem_copy(clip).start()

    for index in range(units):
        lanes = slice(index * LANES, (index + 1) * LANES)
        incoming = dot_f32(into_ref[frame], pooled[:, lanes], ((1,), (0,)))
        block = c_ref[0, :, :, :, lanes].reshape(GRID_ROWS, LANES)
        centred, rate = head_stats(block, unit)
        normal = centred * rate
        product = incoming * normal
        gain_out[:, lanes] += jnp.sum(product, axis=0, keepdims=True)
        shift_out[:, lanes] += jnp.sum(incoming, axis=0, keepdims=True)
        inner = incoming * gain_ref[:, lanes]
        mean_inner = jnp.sum(inner, axis=-1, keepdims=True) * (1.0 / unit)
        mean_both = jnp.sum(inner * normal, axis=-1, keepdims=True) * (1.0 / unit)
        lane = lax.broadcasted_iota(jnp.int32, block.shape, 1)
        result = rate * (inner - mean_inner - normal * mean_both)
        result = jnp.where(lane < unit, result, 0.0)
        flat = result.reshape(FRAMES * SIDE, 8, LANES)
        shape = (FRAMES, SIDE, 8, LANES)
        grads[1, 1 : FRAMES + 1, 1 : SIDE + 1, :, lanes] = flat.reshape(shape)
        grads[0, 1 : FRAMES + 1, 1 : SIDE + 1, :, lanes] = pltpu.roll(flat, 1, 1).reshape(shape)
        grads[2, 1 : FRAMES + 1, 1 : SIDE + 1, :, lanes] = pltpu.roll(flat, 7, 1).reshape(shape)

    @pl.when(clip > 0)
    def _():
        finish_rows(clip - 1)

    pump(1)
    tap_grads(shifted, grads.at[1], taps_out)
    conv = shifted.at[1, 1 : FRAMES + 1, 1 : SIDE + 1]
    convolve(grads, taps, conv, True)
    for index in range(units):
        lanes = slice(index * LANES, (index + 1) * LANES)
        block = shifted[1, 1 : FRAMES + 1, 1 : SIDE + 1, :, lanes].reshape(GRID_ROWS, LANES)
        rows = dot_f32(outof_ref[frame], block.astype(BF), ((1,), (0,))).astype(BF)
        pooled[:, lanes] = rows
        joined_out[:, lanes] += jnp.sum(rows.astype(F32), axis=0, keepdims=True)
    weight_sum[...] += dot_f32(normed_ref[0], pooled[...], ((0,), (0,)))
    result = dot_f32(pooled[...], weight_ref[...], ((1,), (1,))).astype(BF)
    cut = result.shape[1] // 2

    @pl.when(head_at == 0)
    def _():
        keep[clip] = result[:, :cut]
        cross_send[clip] = result[:, cut:]

    @pl.when(head_at == 1)
    def _():
        keep[clip] = result[:, cut:]
        cross_send[clip] = result[:, :cut]

    cross_copy(clip).start()

    @pl.when(clip == clips - 1)
    def _():
        weight_out[...] = weight_sum[...].astype(BF)
        finish_rows(clip)
        settle(chunks - 1)
        for chunk in range(early):
            each(1, outers, lambda step: far_copy(chunk, step).wait_recv())
            rest_out[:, chunk * cols : (chunk + 1) * cols] = lax.fori_loop(
                1,
                outers,
                lambda step, sums: sums + rest_far[chunk, step].astype(F32),
                rest_sum[chunk, outer].astype(F32),
            )
        for index in range(clips):
            grad_copy(index).wait_send()
            cross_copy(index).wait_send()
            mem_copy(index).wait()
            row_copy(index).wait()
        for chunk in range(chunks):
            over_copy(chunk).wait_send()
            rest_copy(chunk).wait_send()
        for chunk in range(early):
            each(1, outers, lambda step: far_copy(chunk, step).wait_send())


def whole_spec(shape):
    return pl.BlockSpec(shape, lambda clip: (0,) * len(shape))


def clip_spec(shape):
    return pl.BlockSpec((1,) + shape, lambda clip: (clip,) + (0,) * len(shape))


def once_spec(shape):
    return pl.BlockSpec(
        shape, lambda clip: (0,) * len(shape), pipeline_mode=pl.Buffered(1)
    )


def any_spec():
    return pl.BlockSpec(memory_space=pl.ANY)


def attention_forward(
    packed, mem_own, mem_peer, column, consts, kernels, gains, shifts, bias, scale, unit, rows
):
    clips = packed.shape[0]
    heads = packed.shape[2] // (3 * LANES)
    into, outof, keyhot, mask, pad_row = consts
    wide = 3 * heads * LANES
    mem_shape = mem_own.shape[1:]
    outers = column.shape[0]
    dma = pltpu.SemaphoreType.DMA
    out = jax.ShapeDtypeStruct
    return pl.pallas_call(
        partial(forward_kernel, heads=heads, unit=unit, scale=scale),
        grid=(clips,),
        in_specs=[
            clip_spec((QROWS, wide)),
            clip_spec(mem_shape),
            clip_spec(mem_shape),
            once_spec(column.shape),
            once_spec(into.shape),
            once_spec(outof.shape),
            once_spec(kernels.shape),
            once_spec(gains.shape),
            once_spec(shifts.shape),
            clip_spec((BIAS_COLS, LANES)),
            once_spec((BIAS_COLS, KROWS)),
            once_spec((QROWS, BIAS_COLS)),
            once_spec((1, BIAS_COLS)),
        ],
        out_specs=[
            clip_spec((rows, heads * unit)),
            any_spec(),
            any_spec(),
            clip_spec((QROWS, heads * LANES)),
            clip_spec((KROWS, heads * LANES)),
            clip_spec((KROWS, heads * LANES)),
            clip_spec((heads, QROWS, KROWS)),
            clip_spec((FRAMES, SIDE, 8, wide)),
        ],
        scratch_shapes=[
            pltpu.VMEM((3, FRAMES + 2, SIDE + 2, 8, wide), F32),
            pltpu.VMEM((27, 8, wide), F32),
            pltpu.VMEM((1, wide), F32),
            pltpu.VMEM((1, wide), F32),
            pltpu.VMEM((clips, rows, heads * unit), BF),
            dma((2, clips)),
            dma((2, outers)),
            dma((2, outers)),
            dma((2, outers)),
            pltpu.SemaphoreType.DMA,
        ],
        out_shape=[
            out((clips, rows, heads * unit), BF),
            out((clips, rows, heads * unit), BF),
            out((outers, 4) + column.shape[1:], BF),
            out((clips, QROWS, heads * LANES), BF),
            out((clips, KROWS, heads * LANES), BF),
            out((clips, KROWS, heads * LANES), BF),
            out((clips, heads, QROWS, KROWS), BF),
            out((clips, FRAMES, SIDE, 8, wide), F32),
        ],
        compiler_params=pltpu.CompilerParams(
            collective_id=1, has_side_effects=True, vmem_limit_bytes=VMEM_LIMIT
        ),
        name="pooled_attention_forward",
    )(
        packed, mem_own, mem_peer, column, into, outof, kernels, gains, shifts, bias, keyhot, mask,
        pad_row,
    )


def attention_backward(
    packed, normed, weight, grad_own, grad_send, rest, consts, kernels, gains, bias, saved, scale,
    unit,
):
    clips, rows, width = grad_own.shape
    heads = width // unit
    model = weight.shape[0]
    half = model // 2
    into, outof, keyhot, mask, pad_row = consts
    wide = 3 * heads * LANES
    outers, _, shard_rows, rest_width = rest.shape
    chunks = 9
    early = 8
    cols = rest_width // chunks
    out = jax.ShapeDtypeStruct
    dma = pltpu.SemaphoreType.DMA
    return pl.pallas_call(
        partial(backward_kernel, heads=heads, unit=unit, scale=scale),
        grid=(clips,),
        in_specs=[
            clip_spec((QROWS, wide)),
            clip_spec((QROWS, model)),
            once_spec((model, wide)),
            clip_spec((rows, width)),
            any_spec(),
            any_spec(),
            once_spec(into.shape),
            once_spec(outof.shape),
            once_spec(kernels.shape),
            once_spec(gains.shape),
            clip_spec((BIAS_COLS, LANES)),
            once_spec((BIAS_COLS, KROWS)),
            once_spec((QROWS, BIAS_COLS)),
            clip_spec((QROWS, heads * LANES)),
            clip_spec((KROWS, heads * LANES)),
            clip_spec((KROWS, heads * LANES)),
            clip_spec((heads, QROWS, KROWS)),
            clip_spec((FRAMES, SIDE, 8, wide)),
        ],
        out_specs=[
            whole_spec((clips, rows, half)),
            any_spec(),
            clip_spec((MEM_BACK, 2 * heads * LANES)),
            any_spec(),
            whole_spec((27, 8, wide)),
            whole_spec((1, wide)),
            whole_spec((1, wide)),
            clip_spec((BIAS_COLS, LANES)),
            whole_spec((model, wide)),
            whole_spec((1, wide)),
            whole_spec((outers, shard_rows, cols)),
            whole_spec((shard_rows, early * cols)),
        ],
        scratch_shapes=[
            pltpu.VMEM((3, FRAMES + 2, SIDE + 2, 8, wide), F32),
            pltpu.VMEM((27, 8, wide), F32),
            pltpu.VMEM((1, wide), F32),
            pltpu.VMEM((3, FRAMES + 2, SIDE + 2, 8, wide), F32),
            pltpu.VMEM((QROWS, heads * LANES), BF),
            pltpu.VMEM((QROWS, wide), BF),
            pltpu.VMEM((clips, rows, width), BF),
            pltpu.VMEM((clips, MEM_BACK, 2 * heads * LANES), BF),
            pltpu.VMEM((chunks, outers, 2, shard_rows, cols), BF),
            pltpu.VMEM((chunks, outers, 2, shard_rows, cols), BF),
            pltpu.VMEM((chunks, outers, shard_rows, cols), BF),
            pltpu.VMEM((chunks, outers, shard_rows, cols), BF),
            pltpu.VMEM((chunks, outers, shard_rows, cols), BF),
            pltpu.VMEM((early, outers, shard_rows, cols), BF),
            pltpu.VMEM((model, wide), F32),
            pltpu.VMEM((clips, QROWS, half), BF),
            pltpu.VMEM((clips, QROWS, half), BF),
            pltpu.VMEM((clips, QROWS, half), BF),
            pltpu.VMEM((clips, rows, half), BF),
            dma((2, clips)),
            dma((2, clips)),
            dma((chunks,)),
            dma((2, chunks)),
            dma((2, chunks)),
            dma((2, early, outers)),
            dma((2, clips)),
            dma((2, clips)),
        ],
        out_shape=[
            out((clips, rows, half), BF),
            out((clips, rows, half), BF),
            out((clips, MEM_BACK, 2 * heads * LANES), BF),
            out((clips, MEM_BACK, 2 * heads * LANES), BF),
            out((27, 8, wide), F32),
            out((1, wide), F32),
            out((1, wide), F32),
            out((clips, BIAS_COLS, LANES), F32),
            out((model, wide), BF),
            out((1, wide), F32),
            out((outers, shard_rows, cols), BF),
            out((shard_rows, early * cols), F32),
        ],
        compiler_params=pltpu.CompilerParams(
            collective_id=2, has_side_effects=True, vmem_limit_bytes=VMEM_LIMIT
        ),
        name="pooled_attention_backward",
    )(
        packed, normed, weight, grad_own, grad_send, rest, into, outof, kernels, gains, bias, keyhot,
        mask, *saved,
    )


def row_stats(values):
    width = values.shape[-1]
    centred = values - jnp.sum(values, axis=-1, keepdims=True) * (1.0 / width)
    variance = jnp.sum(centred * centred, axis=-1, keepdims=True) * (1.0 / width)
    return centred, lax.rsqrt(variance + 1e-06)


def each(low, high, act):
    def body(step, carry):
        act(step)
        return carry

    lax.fori_loop(low, high, body, 0)


def norm_rows(source, index, gain, shift, target, at):
    rows = source.shape[1]
    centred, rate = row_stats(source[index].astype(F32))
    target[index, at : at + rows] = (centred * rate * gain[0:1] + shift[0:1]).astype(BF)


def project_rows(normed, weight, bias, packed):
    def step(index):
        packed[index] = (dot_f32(normed[index], weight, ((1,), (0,))) + bias[...]).astype(BF)

    each(0, packed.shape[0], step)


def project_moves(
    x, attn, gain, shift, attn_shift, cached, old, squeeze, proj, up, down, full, normed, mem_own,
    mem_peer, rest_column, shards, bias, rest, mem_send, squeeze_rows, x_peer, columns, far_sems,
    near_sems, x_sems, cross_sems, mem_sems, rest_sems,
):
    outers = full.shape[0]
    clips, rows, model = x.shape
    clip = lax.axis_index("clip")
    frame = lax.axis_index("frame")
    head = lax.axis_index("head")
    outer, inner = clip // 2, clip % 2
    place = inner * 2 + frame
    half = model // 2
    lanes = pl.ds(pl.multiple_of(head * half, LANES), half)
    barrier = pltpu.get_barrier_semaphore()

    def far_device(step):
        return device_of((outer + step) % outers, inner, frame, head)

    def near_device(step):
        there_inner, there_frame = plane_peer(inner, frame, step)
        return device_of(outer, there_inner, there_frame, head)

    def greet(device):
        pl.semaphore_signal(barrier, inc=1, device_id=device, device_id_type=MESH_ID)

    group = mem_own.shape[2] // 2
    heads = shards.shape[2] // (3 * LANES)
    unit = group // heads

    def squeeze_clip(index):
        total = jnp.zeros((CELLS, cached.shape[2]), F32)
        for step in range(squeeze_rows.shape[0]):
            rows_here = cached[index, step * CELLS : (step + 1) * CELLS].astype(F32)
            total = total + rows_here * squeeze_rows[step : step + 1]
        pieces = ((0, total.astype(BF)), (MEM_STEP, old[index]))
        for side in range(2):

            @pl.when(frame == side)
            def _():
                for at, value in pieces:
                    for member in range(2):
                        local = slice(member * group, (member + 1) * group)
                        low = (2 * member + side) * group
                        mem_own[index, at : at + CELLS, local] = value[:, low : low + group]
                        low = (2 * member + 1 - side) * group
                        mem_send[index, at : at + CELLS, local] = value[:, low : low + group]

    def far_copy(step, at):
        return pltpu.make_async_remote_copy(
            src_ref=shards, dst_ref=columns.at[at],
            send_sem=far_sems.at[0, step], recv_sem=far_sems.at[1, step],
            device_id=far_device(step), device_id_type=MESH_ID,
        )

    def near_copy(index, step, source, at):
        return pltpu.make_async_remote_copy(
            src_ref=source.at[(frame + step % 2) % 2], dst_ref=full.at[at, place],
            send_sem=near_sems.at[0, index, step - 1], recv_sem=near_sems.at[1, index, step - 1],
            device_id=near_device(step), device_id_type=MESH_ID,
        )

    def near_arrival(index, step, at):
        there_inner, there_frame = plane_peer(inner, frame, step)
        return pltpu.make_async_remote_copy(
            src_ref=shards.at[0], dst_ref=full.at[at, there_inner * 2 + there_frame],
            send_sem=near_sems.at[0, index, step - 1], recv_sem=near_sems.at[1, index, step - 1],
            device_id=near_device(step), device_id_type=MESH_ID,
        )

    def x_copy(index):
        return partner_copy(
            x.at[index, :, lanes], x_peer.at[index, :, lanes], x_sems.at[0, index],
            x_sems.at[1, index],
        )

    def cross_copy(index):
        return pltpu.make_async_remote_copy(
            src_ref=x_peer.at[index, :, lanes], dst_ref=x_peer.at[index, :, lanes],
            send_sem=cross_sems.at[0, index], recv_sem=cross_sems.at[1, index],
            device_id=(clip, frame, 1 - head), device_id_type=MESH_ID,
        )

    def cross_arrival(index):
        other = pl.ds(pl.multiple_of((1 - head) * half, LANES), half)
        return pltpu.make_async_remote_copy(
            src_ref=x_peer.at[index, :, other], dst_ref=x_peer.at[index, :, other],
            send_sem=cross_sems.at[0, index], recv_sem=cross_sems.at[1, index],
            device_id=(clip, frame, 1 - head), device_id_type=MESH_ID,
        )

    mem_copy = partner_copy(mem_send, mem_peer, mem_sems.at[0], mem_sems.at[1])

    def rest_copy(step, at):
        return pltpu.make_async_remote_copy(
            src_ref=rest, dst_ref=rest_column.at[at],
            send_sem=rest_sems.at[0, step], recv_sem=rest_sems.at[1, step],
            device_id=far_device(step), device_id_type=MESH_ID,
        )

    def origin(step):
        return (outer + outers - step) % outers

    def prologue():
        each(1, outers, lambda step: greet(far_device(step)))
        for step in range(1, 4):
            greet(near_device(step))
        greet((clip, frame, 1 - head))
        shards[...] = jnp.zeros_like(shards)
        bias[...] = jnp.zeros_like(bias)
        for member in range(3):
            for side in range(2):
                for index in range(heads):
                    target = (member * heads + index) * LANES
                    source = slice(side * group + index * unit, side * group + (index + 1) * unit)
                    shards[side, :, target : target + unit] = attn[member, :, source]
        at = 0
        for part in (proj, up, down):
            rest[:, at : at + part.shape[1]] = part[...]
            at += part.shape[1]
        for side in range(2):

            @pl.when(frame == side)
            def _():
                for member in range(3):
                    for index in range(heads):
                        target = (member * heads + index) * LANES
                        source = slice(side * group + index * unit, side * group + (index + 1) * unit)
                        bias[:, target : target + unit] = attn_shift[member : member + 1, source]

        for member in range(2):
            for index in range(2 * heads):
                at = (2 * member * heads + index) * unit
                squeeze_rows[:, at : at + unit] = squeeze[member]
        mem_own[...] = jnp.zeros_like(mem_own)
        mem_send[...] = jnp.zeros_like(mem_send)

        pl.semaphore_wait(barrier, outers - 1 + 4)
        each(1, outers, lambda step: far_copy(step, outer).start())
        for step in range(1, 4):
            near_copy(0, step, shards, outer).start()
        each(0, clips, lambda index: x_copy(index).start())
        each(0, clips, squeeze_clip)
        rest_column[outer] = rest[...]
        full[outer, place] = shards[frame]
        normed[...] = jnp.zeros_like(normed)
        each(0, clips, lambda index: norm_rows(x, index, gain, shift, normed, 0))

        def forward(index):
            at = origin(index)
            far_copy(index, at).wait_recv()
            for step in range(1, 4):
                near_copy(index, step, columns.at[at], at).start()
            full[at, place] = columns[at, frame]

        each(1, outers, forward)
        each(1, outers, lambda step: rest_copy(step, outer).start())

        def relay(index):
            x_copy(index).wait_recv()
            cross_copy(index).start()

        each(0, clips, relay)
        mem_copy.start()

        def receive(index):
            cross_arrival(index).wait_recv()
            norm_rows(x_peer, index, gain, shift, normed, HALF)

        each(0, clips, receive)

        def arrive(index):
            for step in range(1, 4):
                near_arrival(index, step, origin(index)).wait_recv()

        each(0, outers, arrive)
    def rest_arrive():
        each(1, outers, lambda step: rest_copy(step, origin(step)).wait_recv())

    def finish():
        each(1, outers, lambda step: rest_copy(step, outer).wait_send())
        each(1, outers, lambda step: far_copy(step, outer).wait_send())
        for step in range(1, 4):
            near_copy(0, step, shards, outer).wait_send()

        def sent(index):
            for step in range(1, 4):
                near_copy(index, step, columns.at[origin(index)], origin(index)).wait_send()

        each(1, outers, sent)

        def x_sent(index):
            x_copy(index).wait_send()
            cross_copy(index).wait_send()

        each(0, clips, x_sent)

    return outer, prologue, mem_copy, rest_arrive, finish


def front_kernel(
    x, attn, gain, shift, attn_shift, cached, old, squeeze, proj, up, down, into_ref, outof_ref,
    kernel_ref, pool_gain_ref, pool_shift_ref, bias_ref, keyhot_ref, mask_ref, pad_ref,
    full_out, packed_out, normed_out, out_own, out_recv, rest_full, q_out, k_out, v_out, p_out,
    c_out, full, shards, attn_bias, rest, mem_send, mem_own, mem_peer, squeeze_rows, x_peer, columns, normed,
    rest_column, shifted, taps, gain_ref, shift_ref, out_send, far_sems, near_sems, x_sems,
    cross_sems, mem_sems, rest_sems, out_sems, side_sems, pair_sems, turn_sems, own_sem,
    *, heads, unit, scale,
):
    clip = pl.program_id(0)
    clips = out_send.shape[0]
    outers = full.shape[0]
    frame = lax.axis_index("frame")
    outer, prologue, mem_copy, rest_arrive, project_finish = project_moves(
        x, attn, gain, shift, attn_shift, cached, old, squeeze, proj, up, down, full, normed,
        mem_own, mem_peer, rest_column, shards, attn_bias, rest, mem_send, squeeze_rows, x_peer,
        columns, far_sems, near_sems, x_sems, cross_sems, mem_sems, rest_sems,
    )
    own_copy, send, turn, plane_finish = plane_stage(
        rest_column, rest_full, side_sems, pair_sems, turn_sems, own_sem
    )

    def out_copy(index):
        return partner_copy(
            out_send.at[index], out_recv.at[index], out_sems.at[0, index], out_sems.at[1, index]
        )

    @pl.when(clip == 0)
    def _():
        prologue()
        send(outer)
        shifted[...] = jnp.zeros_like(shifted)
        pairs = ((pool_gain_ref, gain_ref), (pool_shift_ref, shift_ref))
        spread_tables(kernel_ref, taps, pairs, heads, unit)

    def points(odd):
        for step in range(outers):
            point = min(step + TURN_LAG, 2 * clips - 1)
            if step and step % 2 == odd:

                @pl.when(clip == step // 2)
                def _():
                    send((outer + step) % outers)

            if point % 2 == odd:

                @pl.when(clip == point // 2)
                def _():
                    turn(step)

    def after_conv():
        @pl.when(clip == 0)
        def _():
            mem_copy.wait_recv()
            rest_arrive()
            own_copy.start()

        points(1)

    points(0)
    @pl.when(clip == clips - 1)
    def _():
        full_out[...] = full[...]

    normed_out[0] = normed[clip]
    weight = full[...].reshape(x.shape[2], full.shape[3])
    rows = dot_f32(normed[clip], weight, ((1,), (0,))) + attn_bias[...]
    packed_out[0] = rows.astype(BF)
    attend_clip(
        packed_out.at[0], mem_own.at[clip], mem_peer.at[clip], frame, into_ref, outof_ref, gain_ref,
        shift_ref, bias_ref, keyhot_ref, mask_ref, pad_ref, out_own.at[0], out_send.at[clip], q_out,
        k_out, v_out, p_out, c_out, shifted, taps, heads, unit, scale, after_conv,
    )
    out_copy(clip).start()

    @pl.when(clip == clips - 1)
    def _():
        mem_copy.wait_send()
        project_finish()
        plane_finish()
        for index in range(clips):
            out_copy(index).wait()


def front(
    x, attn, gain, shift, attn_shift, cached, old, squeeze, proj, up, down, consts, kernels, gains,
    shifts, bias, scale, clip_count, unit,
):
    clips, rows, model = x.shape
    _, shard_rows, head_width = attn.shape
    heads = head_width // (2 * unit)
    wide = 3 * heads * LANES
    outers = clip_count // 2
    into, outof, keyhot, mask, pad_row = consts
    rest_shape = (shard_rows, proj.shape[1] + up.shape[1] + down.shape[1])
    mem_shape = (clips, MEM_PAD, head_width)
    out = jax.ShapeDtypeStruct
    dma = pltpu.SemaphoreType.DMA
    operands = (
        x, attn, gain, shift, attn_shift, cached, old, squeeze, proj, up, down, into, outof,
        kernels, gains, shifts, bias, keyhot, mask, pad_row,
    )
    specs = [once_spec(value.shape) for value in operands]
    specs[16] = clip_spec((BIAS_COLS, LANES))
    results = pl.pallas_call(
        partial(front_kernel, heads=heads, unit=unit, scale=scale),
        grid=(clips,),
        in_specs=specs,
        out_specs=[
            whole_spec((outers, 4, shard_rows, wide)),
            clip_spec((QROWS, wide)),
            clip_spec((QROWS, model)),
            clip_spec((rows, heads * unit)),
            any_spec(),
            any_spec(),
            clip_spec((QROWS, heads * LANES)),
            clip_spec((KROWS, heads * LANES)),
            clip_spec((KROWS, heads * LANES)),
            clip_spec((heads, QROWS, KROWS)),
            clip_spec((FRAMES, SIDE, 8, wide)),
        ],
        out_shape=[
            out((outers, 4, shard_rows, wide), BF),
            out((clips, QROWS, wide), BF),
            out((clips, QROWS, model), BF),
            out((clips, rows, heads * unit), BF),
            out((clips, rows, heads * unit), BF),
            out((outers, 4) + rest_shape, BF),
            out((clips, QROWS, heads * LANES), BF),
            out((clips, KROWS, heads * LANES), BF),
            out((clips, KROWS, heads * LANES), BF),
            out((clips, heads, QROWS, KROWS), BF),
            out((clips, FRAMES, SIDE, 8, wide), F32),
        ],
        scratch_shapes=[
            pltpu.VMEM((outers, 4, shard_rows, wide), BF),
            pltpu.VMEM((2, shard_rows, wide), BF),
            pltpu.VMEM((1, wide), F32),
            pltpu.VMEM(rest_shape, BF),
            pltpu.VMEM(mem_shape, BF),
            pltpu.VMEM(mem_shape, BF),
            pltpu.VMEM(mem_shape, BF),
            pltpu.VMEM((squeeze.shape[1], cached.shape[2]), F32),
            pltpu.VMEM((clips, rows, model), BF),
            pltpu.VMEM((outers, 2, shard_rows, wide), BF),
            pltpu.VMEM((clips, QROWS, model), BF),
            pltpu.VMEM((outers,) + rest_shape, BF),
            pltpu.VMEM((3, FRAMES + 2, SIDE + 2, 8, wide), F32),
            pltpu.VMEM((27, 8, wide), F32),
            pltpu.VMEM((1, wide), F32),
            pltpu.VMEM((1, wide), F32),
            pltpu.VMEM((clips, rows, heads * unit), BF),
            dma((2, outers)),
            dma((2, outers, 3)),
            dma((2, clips)),
            dma((2, clips)),
            dma((2,)),
            dma((2, outers)),
            dma((2, clips)),
            dma((2, outers)),
            dma((2, outers)),
            dma((2, outers)),
            pltpu.SemaphoreType.DMA,
        ],
        compiler_params=pltpu.CompilerParams(
            collective_id=1, has_side_effects=True, vmem_limit_bytes=VMEM_LIMIT
        ),
        name="project_and_attend",
    )(*operands)
    return (results[0].reshape(model, wide),) + tuple(results[1:])


def project_local_kernel(x, x_peer, weight, gain, shift, bias, packed, normed):
    normed[...] = jnp.zeros_like(normed)
    each(0, x.shape[0], lambda index: norm_rows(x, index, gain, shift, normed, 0))
    each(0, x.shape[0], lambda index: norm_rows(x_peer, index, gain, shift, normed, HALF))
    project_rows(normed, weight[...], bias, packed)


def swap(value, axis):
    return lax.ppermute(value, axis, [(0, 1), (1, 0)])


def padded_heads(value, unit):
    value = value.reshape(value.shape[0], 3, 2, -1, unit)
    value = jnp.pad(value, ((0, 0),) * 4 + ((0, LANES - unit),))
    return value.transpose(2, 0, 1, 3, 4).reshape(2, value.shape[0], -1)


def project_plain(
    x, attn, gain, shift, attn_shift, cached, old, squeeze, proj, up, down, clip_count, unit
):
    clips, rows, model = x.shape
    _, shard_rows, head_width = attn.shape
    heads = head_width // (2 * unit)
    width = 3 * heads * LANES
    outers = clip_count // 2
    rest_shape = (shard_rows, proj.shape[1] + up.shape[1] + down.shape[1])
    out = jax.ShapeDtypeStruct
    dma = pltpu.SemaphoreType.DMA
    vmem = pl.BlockSpec(memory_space=pltpu.VMEM)
    shapes = [out((clips, QROWS, width), BF), out((clips, QROWS, model), BF)]
    frame = lax.axis_index("frame")
    shards = padded_heads(attn.transpose(1, 0, 2), unit)
    full = lax.all_gather(shards, ("clip", "frame"), axis=1, tiled=True)
    full = lax.dynamic_index_in_dim(full, frame, 0, keepdims=False)
    bias = padded_heads(attn_shift[None], unit)
    bias = lax.dynamic_index_in_dim(bias, frame, 0, keepdims=False)
    steps = squeeze.shape[1]
    wide = cached.astype(F32).reshape(clips, steps, CELLS, 2, head_width)
    tiled = jnp.tile(squeeze, (1, 1, 2 * heads))
    mem = sum(wide[:, step] * tiled[:, step] for step in range(steps)).astype(BF)
    mem = jnp.stack([mem, old.reshape(mem.shape)], axis=1)
    mem = jnp.pad(mem, ((0, 0), (0, 0), (0, MEM_STEP - CELLS), (0, 0), (0, 0)))
    pieces = mem.reshape(clips, 2 * MEM_STEP, 2, 2, heads * unit)
    mem_own = lax.dynamic_index_in_dim(pieces, frame, 3, keepdims=False)
    mem_send = lax.dynamic_index_in_dim(pieces, 1 - frame, 3, keepdims=False)
    mem_own = mem_own.reshape(clips, -1, head_width)
    mem_peer = swap(mem_send.reshape(clips, -1, head_width), "frame")
    packed, normed = pl.pallas_call(
        project_local_kernel,
        in_specs=[vmem] * 6,
        out_specs=[vmem] * 2,
        out_shape=shapes,
        compiler_params=pltpu.CompilerParams(vmem_limit_bytes=VMEM_LIMIT),
        name="project_local",
    )(x, swap(x, "frame"), full, gain, shift, bias)
    rest = jnp.concatenate([proj, up, down], axis=1)
    column = lax.all_gather(rest, ("clip", "frame"), axis=0, tiled=False)
    column = column.reshape((outers, 4) + rest.shape)
    place = lax.axis_index("clip") % 2 * 2 + frame
    column = lax.dynamic_index_in_dim(column, place, 1, keepdims=False)
    return full, packed, normed, mem_own, mem_peer, column


def device_of(outer, inner, frame, head):
    return (outer * 2 + inner, frame, head)


def plane_peer(inner, frame, step):
    return (inner + step // 2) % 2, (frame + step % 2) % 2


def row_piece(value, row):
    return value[:, row * LANES : (row + 1) * LANES]


def tail_kernel(
    row_own, row_recv, x, middle_grad, grads, joined_sum, gain, taps, pool_gain, pool_shift,
    bias_grad, hot, space_hot, cached, mem_own, mem_recv, vectors, up_bias, rest,
    grad_in, out, rest_out, small_out,
    near, part, far, small, small_in, row_full, rest_in,
    cross_sems, near_sems, far_sems, first_sems, second_sems, rest_sems,
    *, unit, plan, table_rows,
):
    chunks, outers, _, shard_rows, cols = part.shape
    clips, rows, model = x.shape
    half = model // 2
    devices = small.shape[0]
    clip = lax.axis_index("clip")
    frame = lax.axis_index("frame")
    head = lax.axis_index("head")
    outer, inner = clip // 2, clip % 2
    place = inner * 2 + frame
    mine = (clip * 2 + frame) * 2 + head

    def device(index):
        return (index // 4, (index // 2) % 2, index % 2)

    barrier = pltpu.get_barrier_semaphore()
    each(
        1,
        devices,
        lambda step: pl.semaphore_signal(
            barrier, inc=1, device_id=device((mine + step) % devices), device_id_type=MESH_ID
        ),
    )

    def first(step):
        other = (mine + step) % devices
        return pltpu.make_async_remote_copy(
            src_ref=small.at[other], dst_ref=small_in.at[step],
            send_sem=first_sems.at[0, step], recv_sem=first_sems.at[1, step],
            device_id=device(other), device_id_type=MESH_ID,
        )

    def second(step, block):
        return pltpu.make_async_remote_copy(
            src_ref=small_out.at[block], dst_ref=small_out.at[block],
            send_sem=second_sems.at[0, step], recv_sem=second_sems.at[1, step],
            device_id=device((mine + step) % devices), device_id_type=MESH_ID,
        )

    def near_copy(chunk, step):
        there_inner, there_frame = plane_peer(inner, frame, step)
        return pltpu.make_async_remote_copy(
            src_ref=grads.at[:, there_inner * 2 + there_frame, :, pl.ds(chunk * cols, cols)],
            dst_ref=near.at[chunk, step - 1],
            send_sem=near_sems.at[0, chunk, step - 1], recv_sem=near_sems.at[1, chunk, step - 1],
            device_id=device_of(outer, there_inner, there_frame, head), device_id_type=MESH_ID,
        )

    def far_copy(chunk, step):
        there = (outer + step) % outers
        return pltpu.make_async_remote_copy(
            src_ref=part.at[chunk, there], dst_ref=far.at[chunk, step],
            send_sem=far_sems.at[0, chunk, step], recv_sem=far_sems.at[1, chunk, step],
            device_id=device_of(there, inner, frame, head), device_id_type=MESH_ID,
        )

    def cross_copy(index, side):
        lanes = pl.ds(pl.multiple_of(side * half, LANES), half)
        return pltpu.make_async_remote_copy(
            src_ref=row_full.at[index, :, lanes], dst_ref=row_full.at[index, :, lanes],
            send_sem=cross_sems.at[0, index], recv_sem=cross_sems.at[1, index],
            device_id=(clip, frame, 1 - head), device_id_type=MESH_ID,
        )

    def rest_copy(step):
        there = (outer + step) % outers
        return pltpu.make_async_remote_copy(
            src_ref=rest.at[there], dst_ref=rest_in.at[step],
            send_sem=rest_sems.at[0, step], recv_sem=rest_sems.at[1, step],
            device_id=device_of(there, inner, frame, head), device_id_type=MESH_ID,
        )

    small[...] = jnp.zeros_like(small)
    pl.semaphore_wait(barrier, devices - 1)
    for chunk in range(chunks):
        for step in range(1, 4):
            near_copy(chunk, step).start()
    lanes_here = pl.ds(pl.multiple_of(head * half, LANES), half)

    def join(index):
        total = row_own[index].astype(F32) + row_recv[index].astype(F32)
        row_full[index, :, lanes_here] = total.astype(BF)
        cross_copy(index, head).start()

    each(0, clips, join)
    each(1, outers, lambda step: rest_copy(step).start())

    gain_sum = jnp.zeros((1, model), F32)
    shift_sum = jnp.zeros((1, model), F32)
    for index in range(clips):
        cross_copy(index, 1 - head).wait_recv()
        incoming = row_full[index].astype(F32)
        centred, rate = row_stats(x[index].astype(F32))
        normal = centred * rate
        product = incoming * normal
        gain_sum = gain_sum + jnp.sum(product, axis=0, keepdims=True)
        shift_sum = shift_sum + jnp.sum(incoming, axis=0, keepdims=True)
        scaled = incoming * gain[0:1]
        mean_scaled = jnp.sum(scaled, axis=-1, keepdims=True) * (1.0 / model)
        mean_both = jnp.sum(scaled * normal, axis=-1, keepdims=True) * (1.0 / model)
        result = rate * (scaled - mean_scaled - normal * mean_both) + middle_grad[index]
        grad_in[index] = result.astype(BF)

    rows_small = small.shape[1]

    def put(row, value):
        count = value.shape[0]
        done = 0
        while done < count:
            block, offset = divmod(row + done, rows_small)
            size = min(count - done, rows_small - offset)
            small[block, offset : offset + size, : value.shape[1]] = value[done : done + size]
            done += size

    def put_wide(row, value):
        for index in range(value.shape[1] // LANES):
            put(row + index, row_piece(value, index))

    wide_rows_count = model // LANES

    @pl.when(head == 0)
    def _():
        put_wide(plan["gain"], gain_sum)
        put_wide(plan["gain"] + wide_rows_count, vectors[0:1])
        put_wide(plan["shift"], shift_sum)
        put_wide(plan["shift"] + wide_rows_count, vectors[1:2])
        put_wide(plan["rows"], vectors[2:3])
        put_wide(plan["rows"] + wide_rows_count, vectors[3:4])

    joined_rows = joined_sum.shape[1] // LANES
    up_rows = up_bias.shape[1] // LANES
    for which in range(2):

        @pl.when(head == which)
        def _():
            for side in range(2):

                @pl.when(frame == side)
                def _():
                    put_wide(plan["joined"] + (2 * which + side) * joined_rows, joined_sum[...])

            put_wide(plan["up"] + which * up_rows, up_bias[...])

    heads = taps.shape[2] // (3 * LANES)
    tap_sum = jnp.sum(taps[...], axis=1)
    for member in range(3):
        totals = []
        for value in (tap_sum, pool_gain[...], pool_shift[...]):
            total = row_piece(value, member * heads)
            for index in range(1, heads):
                total = total + row_piece(value, member * heads + index)
            totals.append(total)
        put(plan["taps"] + member * 27, totals[0])
        put(plan["pool_gain"] + member, totals[1])
        put(plan["pool_shift"] + member, totals[2])
    heads_here = joined_sum.shape[1] // (3 * LANES)
    for side in range(2):

        @pl.when(frame == side)
        def _():
            for member in range(2):
                totals = [jnp.zeros((1, unit), F32) for _ in range(FRAMES // MEMF)]
                for index in range(clips):
                    for which, part in ((side, mem_own), (1 - side, mem_recv)):
                        for spot in range(heads_here):
                            at = (member * heads_here + spot) * LANES
                            value = part[index, :CELLS, at : at + unit].astype(F32)
                            at = ((2 * member + which) * heads_here + spot) * unit
                            for step in range(len(totals)):
                                rows_here = cached[
                                    index, step * CELLS : (step + 1) * CELLS, at : at + unit
                                ]
                                product = rows_here.astype(F32) * value
                                totals[step] = totals[step] + jnp.sum(
                                    product, axis=0, keepdims=True
                                )
                for step in range(len(totals)):
                    put(plan["squeeze"] + member * len(totals) + step, totals[step])

    time_sum = jnp.zeros((hot.shape[2], LANES), F32)
    bias_sum = jnp.zeros((BIAS_COLS, LANES), F32)
    for index in range(clips):
        value = bias_grad[index]
        bias_sum = bias_sum + value
        value = value[: hot.shape[1]]
        high = value.astype(BF)
        low = (value - high.astype(F32)).astype(BF)
        time_sum = time_sum + dot_f32(hot[index], high, ((0,), (0,)))
        time_sum = time_sum + dot_f32(hot[index], low, ((0,), (0,)))
    put(plan["time"], time_sum[:table_rows])
    high = bias_sum.astype(BF)
    low = (bias_sum - high.astype(F32)).astype(BF)
    space_sum = dot_f32(space_hot[...], high, ((1,), (0,)))
    space_sum = space_sum + dot_f32(space_hot[...], low, ((1,), (0,)))
    put(plan["space"], space_sum[: 2 * (2 * SIDE - 1)])

    each(1, devices, lambda step: first(step).start())

    def reduce_near(chunk):
        lanes = slice(chunk * cols, (chunk + 1) * cols)
        for step in range(1, 4):
            near_copy(chunk, step).wait_recv()

        def gathered(index):
            own = grads[index, place, :, lanes].astype(F32)
            own = own + near[chunk, 1, index].astype(F32)
            other = near[chunk, 0, index].astype(F32) + near[chunk, 2, index].astype(F32)
            return own, other

        def send(step):
            there = (outer + step) % outers
            own, other = gathered(there)
            part[chunk, there, 0] = own.astype(BF)
            part[chunk, there, 1] = other.astype(BF)
            far_copy(chunk, step).start()

        each(1, outers, send)
        own, other = gathered(outer)
        far[chunk, 0, 0] = own.astype(BF)
        far[chunk, 0, 1] = other.astype(BF)

    reduce_near(0)
    each(1, devices, lambda step: first(step).wait_recv())
    total = lax.fori_loop(1, devices, lambda step, sums: sums + small_in[step], small[mine])
    small_out[mine] = total
    each(1, devices, lambda step: second(step, mine).start())
    for chunk in range(1, chunks):
        reduce_near(chunk)
    heads = cols // LANES
    group = heads * unit
    for chunk in range(chunks):
        each(1, outers, lambda step: far_copy(chunk, step).wait_recv())
        totals = []
        for side in range(2):
            totals.append(
                lax.fori_loop(
                    0,
                    outers,
                    lambda step, sums: sums + far[chunk, step, side].astype(F32),
                    jnp.zeros((shard_rows, cols), F32),
                )
            )

        def store(order):
            for spot, side in enumerate(order):
                for index in range(heads):
                    at = (2 * chunk + spot) * group + index * unit
                    value = totals[side][:, index * LANES : index * LANES + unit]
                    out[:, at : at + unit] = value

        @pl.when(frame == 0)
        def _():
            store((0, 1))

        @pl.when(frame == 1)
        def _():
            store((1, 0))

    each(1, outers, lambda step: rest_copy(step).wait_recv())
    rest_out[...] = lax.fori_loop(
        1,
        outers,
        lambda step, sums: sums + rest_in[step].astype(F32),
        rest[outer].astype(F32),
    )
    each(1, devices, lambda step: second(step, (mine + devices - step) % devices).wait_recv())
    each(1, devices, lambda step: first(step).wait_send())
    each(1, devices, lambda step: second(step, mine).wait_send())
    each(1, outers, lambda step: rest_copy(step).wait_send())
    for index in range(clips):
        cross_copy(index, head).wait_send()
    for chunk in range(chunks):
        for step in range(1, 4):
            near_copy(chunk, step).wait_send()
        each(1, outers, lambda step: far_copy(chunk, step).wait_send())


def unpack_kernel(
    small, qkv, early, late, grad_in, block_out,
    grad_in_out, block_out_out, gain_out, shift_out, rows_out, joined_out, up_out, taps_out,
    pool_gain_out, pool_shift_out, squeeze_out, time_out, space_out, qkv_out, proj_out,
    up_grad_out, down_out, time_rows, *, plan, unit,
):
    for index in range(grad_in.shape[0]):
        grad_in_out[index] = grad_in[index]
        block_out_out[index] = block_out[index]
    head = lax.axis_index("head")
    rows_small = small.shape[1]

    def take(row, target):
        count = target.shape[0]
        done = 0
        while done < count:
            block, offset = divmod(row + done, rows_small)
            size = min(count - done, rows_small - offset)
            target[done : done + size] = small[block, offset : offset + size, : target.shape[1]]
            done += size

    def take_wide(row, target, at):
        for index in range(target.shape[1] // LANES):
            block, offset = divmod(row + index, rows_small)
            target[at : at + 1, index * LANES : (index + 1) * LANES] = small[
                block, offset : offset + 1
            ]

    per_row = gain_out.shape[1] // LANES
    for index in range(2):
        take_wide(plan["gain"] + index * per_row, gain_out, index)
        take_wide(plan["shift"] + index * per_row, shift_out, index)
        take_wide(plan["rows"] + index * per_row, rows_out, index)
    width = joined_out.shape[1]
    group = width // 2
    heads = group // unit
    joined_rows = 3 * heads
    up_rows = up_out.shape[0]
    for which in range(2):

        @pl.when(head == which)
        def _():
            for member in range(3):
                for side in range(2):
                    for index in range(heads):
                        row = plan["joined"] + (2 * which + side) * joined_rows
                        block, offset = divmod(row + member * heads + index, rows_small)
                        at = side * group + index * unit
                        joined_out[member : member + 1, at : at + unit] = small[
                            block, offset : offset + 1, :unit
                        ]
            take(plan["up"] + which * up_rows, up_out)

    for member in range(3):
        take(plan["taps"] + member * 27, taps_out.at[member])
        qkv_out[member] = qkv[:, member * width : (member + 1) * width]
    take(plan["pool_gain"], pool_gain_out)
    take(plan["pool_shift"], pool_shift_out)
    take(plan["time"], time_rows)
    time_out[...] = time_rows[...].T
    for index in range(2):
        count = squeeze_out.shape[1]
        take(plan["squeeze"] + index * count, squeeze_out.at[index])
        for spot in range(space_out.shape[0]):
            block, offset = divmod(
                plan["space"] + index * space_out.shape[0] + spot, rows_small
            )
            space_out[spot, index : index + 1] = small[block, offset : offset + 1, :unit]
    proj_width, up_width = proj_out.shape[1], up_grad_out.shape[1]
    proj_out[...] = early[:, :proj_width]
    up_grad_out[...] = early[:, proj_width : proj_width + up_width]
    at = proj_width + up_width
    first = early.shape[1] - at
    down_out[:, :first] = early[:, at:]
    down_out[:, first:] = late[...]


def unpack(small, qkv, early, late, grad_in, block_out, plan, unit, hidden_width, table_rows):
    shard_rows, width = qkv.shape
    model = grad_in.shape[2]
    rest_width = early.shape[1] + late.shape[1]
    out = jax.ShapeDtypeStruct
    vmem = pl.BlockSpec(memory_space=pltpu.VMEM)
    shapes = [
        out(grad_in.shape, BF),
        out(block_out.shape, BF),
        out((2, model), F32),
        out((2, model), F32),
        out((2, model), F32),
        out((3, width // 3), F32),
        out((hidden_width // LANES, LANES), F32),
        out((3, 27, unit), F32),
        out((3, unit), F32),
        out((3, unit), F32),
        out((2, FRAMES // MEMF, unit), F32),
        out((unit, table_rows), F32),
        out((2 * SIDE - 1, 2, unit), F32),
        out((3, shard_rows, width // 3), F32),
        out((shard_rows, rest_width - 2 * hidden_width), F32),
        out((shard_rows, hidden_width), F32),
        out((shard_rows, hidden_width), F32),
    ]
    return pl.pallas_call(
        partial(unpack_kernel, plan=plan, unit=unit),
        in_specs=[vmem] * 6,
        out_specs=[vmem] * len(shapes),
        out_shape=shapes,
        scratch_shapes=[pltpu.VMEM((table_rows, unit), F32)],
        compiler_params=pltpu.CompilerParams(vmem_limit_bytes=VMEM_LIMIT),
        name="unpack_results",
    )(small, qkv, early, late, grad_in, block_out)


def tail(
    row_own, row_recv, x, middle_grad, grads, joined_sum, gain, taps, pool_gain, pool_shift,
    bias_grad, hot, space_hot, cached, mem_own, mem_recv, vectors, up_bias, rest, clip_count, devices,
    unit, table_rows,
):
    clips, rows, model = x.shape
    wide = grads.shape[3]
    heads = wide // (3 * LANES)
    width = 3 * 2 * heads * unit
    outers = clip_count // 2
    shard_rows = model // (4 * outers)
    chunks = 3
    cols = wide // chunks
    plan = {}
    at = 0
    for name, count in (
        ("gain", 2 * model // LANES),
        ("shift", 2 * model // LANES),
        ("rows", 2 * model // LANES),
        ("joined", 4 * wide // LANES),
        ("up", 2 * up_bias.shape[1] // LANES),
        ("taps", 81),
        ("pool_gain", 3),
        ("pool_shift", 3),
        ("squeeze", 2 * FRAMES // MEMF),
        ("time", table_rows),
        ("space", 2 * (2 * SIDE - 1)),
    ):
        plan[name] = at
        at += count
    block = -(-at // (devices * 8)) * 8
    out = jax.ShapeDtypeStruct
    dma = pltpu.SemaphoreType.DMA
    vmem = pl.BlockSpec(memory_space=pltpu.VMEM)
    shapes = [
        out((clips, rows, model), BF),
        out((shard_rows, width), F32),
        out((shard_rows, rest.shape[2]), F32),
        out((devices, block, LANES), F32),
    ]
    results = pl.pallas_call(
        partial(tail_kernel, unit=unit, plan=plan, table_rows=table_rows),
        in_specs=[vmem] * 19,
        out_specs=[vmem] * len(shapes),
        out_shape=shapes,
        scratch_shapes=[
            pltpu.VMEM((chunks, 3, outers, shard_rows, cols), BF),
            pltpu.VMEM((chunks, outers, 2, shard_rows, cols), BF),
            pltpu.VMEM((chunks, outers, 2, shard_rows, cols), BF),
            pltpu.VMEM((devices, block, LANES), F32),
            pltpu.VMEM((devices, block, LANES), F32),
            pltpu.VMEM((clips, rows, model), BF),
            pltpu.VMEM(rest.shape, BF),
            dma((2, clips)),
            dma((2, chunks, 3)),
            dma((2, chunks, outers)),
            dma((2, devices)),
            dma((2, devices)),
            dma((2, outers)),
        ],
        compiler_params=pltpu.CompilerParams(
            collective_id=0, has_side_effects=True, vmem_limit_bytes=VMEM_LIMIT
        ),
        name="tail_gradients",
    )(
        row_own, row_recv, x, middle_grad, grads, joined_sum, gain, taps, pool_gain, pool_shift,
        bias_grad, hot, space_hot, cached, mem_own, mem_recv, vectors, up_bias, rest,
    )
    return results, plan


def feed_kernel(
    att_own, att_recv, x, cot, weights, gain, shift, out_shift, up_shift,
    block_out, middle_grad, grad_own, grad_send, grad_rest, vectors, up_bias,
    attended, normed, cots, active, hidden_low, branch, middle, send, recv, sems,
):
    clips, rows, model = x.shape
    span = attended.shape[0] // clips
    group = att_own.shape[2]
    head_width = 2 * group
    hidden_width = up_shift.shape[1]
    tiles = 4
    tile = hidden_width // tiles
    clip_at = lax.axis_index("clip")
    frame = lax.axis_index("frame")
    head = lax.axis_index("head")
    partner = (clip_at, frame, 1 - head)

    def cross(kind, index):
        return pltpu.make_async_remote_copy(
            src_ref=send.at[kind, index], dst_ref=recv.at[kind, index],
            send_sem=sems.at[0, kind, index], recv_sem=sems.at[1, kind, index],
            device_id=partner, device_id_type=MESH_ID,
        )

    barrier = pltpu.get_barrier_semaphore()
    pl.semaphore_signal(barrier, inc=1, device_id=partner, device_id_type=MESH_ID)
    for ref in (attended, normed, cots, branch):
        ref[...] = jnp.zeros_like(ref)

    def assemble(low, high):
        for index in range(clips):
            at = slice(index * span, index * span + rows)
            attended[at, :group] = low[index]
            attended[at, group:] = high[index]

    @pl.when(frame == 0)
    def _():
        assemble(att_own, att_recv)

    @pl.when(frame == 1)
    def _():
        assemble(att_recv, att_own)

    for index in range(clips):
        cots[index * span : index * span + rows] = cot[index]
    pl.semaphore_wait(barrier, 1)

    def block_rows(index):
        return pl.ds(pl.multiple_of(index * span, 16), span)

    def project(index):
        part = dot_f32(attended[block_rows(index)], weights[:, :head_width], ((1,), (1,)))
        send[0, index] = part[:rows].astype(BF)
        cross(0, index).start()

    each(0, clips, project)

    def feed(index, bias_sum):
        cross(0, index).wait_recv()
        branch_rows = send[0, index].astype(F32) + recv[0, index].astype(F32)
        value = x[index].astype(F32) + branch_rows + out_shift[0:1]
        middle[index] = value
        centred, rate = row_stats(value)
        low = (centred * rate * gain[1:2] + shift[1:2]).astype(BF)
        at = pl.multiple_of(index * span, 16)
        normed[pl.ds(at, rows)] = low
        low = normed[block_rows(index)]
        cot_rows = cots[block_rows(index)]
        out_part = jnp.zeros((span, model), F32)
        norm_part = jnp.zeros((span, model), F32)
        sums = []
        for step in range(tiles):
            lanes = slice(step * tile, (step + 1) * tile)
            up = weights[:, head_width + step * tile : head_width + (step + 1) * tile]
            at = head_width + hidden_width + step * tile
            down = weights[:, at : at + tile]
            hidden = dot_f32(low, up, ((1,), (0,))) + up_shift[:, lanes]
            incoming = dot_f32(cot_rows, down, ((1,), (0,)))
            normal = 0.5 * (1.0 + lax.erf(hidden * (0.5**0.5)))
            density = jnp.exp(hidden * hidden * -0.5) * ((2.0 * np.pi) ** -0.5)
            acted = (hidden * normal).astype(BF)
            back = (incoming * (normal + hidden * density)).astype(BF)
            active[block_rows(index), lanes] = acted
            hidden_low[block_rows(index), lanes] = back
            sums.append(jnp.sum(back.astype(F32), axis=0, keepdims=True))
            out_part = out_part + dot_f32(acted, down, ((1,), (1,)))
            norm_part = norm_part + dot_f32(back, up, ((1,), (1,)))
        send[1, index] = norm_part[:rows].astype(BF)
        cross(1, index).start()
        send[2, index] = out_part[:rows].astype(BF)
        cross(2, index).start()
        return bias_sum + jnp.concatenate(sums, axis=1)

    up_bias[...] = lax.fori_loop(0, clips, feed, jnp.zeros((1, hidden_width), F32))

    for step in range(tiles):
        lanes = slice(step * tile, (step + 1) * tile)
        value = dot_f32(normed[...], hidden_low[:, lanes], ((0,), (0,)))
        at = head_width + step * tile
        grad_rest[:, at : at + tile] = value.astype(BF)
        value = dot_f32(cots[...], active[:, lanes], ((0,), (0,)))
        at = head_width + hidden_width + step * tile
        grad_rest[:, at : at + tile] = value.astype(BF)

    def back(index, sums):
        gain_sum, shift_sum, first_sum, second_sum = sums
        cross(1, index).wait_recv()
        incoming = send[1, index].astype(F32) + recv[1, index].astype(F32)
        centred, rate = row_stats(middle[index])
        normal = centred * rate
        scaled = incoming * gain[1:2]
        mean_scaled = jnp.sum(scaled, axis=-1, keepdims=True) * (1.0 / model)
        mean_both = jnp.sum(scaled * normal, axis=-1, keepdims=True) * (1.0 / model)
        cot_rows = cot[index].astype(F32)
        value = cot_rows + rate * (scaled - mean_scaled - normal * mean_both)
        middle_grad[index] = value
        at = pl.multiple_of(index * span, 16)
        branch[pl.ds(at, rows)] = value.astype(BF)
        part = dot_f32(branch[block_rows(index)], weights[:, :head_width], ((1,), (0,)))
        part = part[:rows].astype(BF)

        @pl.when(frame == 0)
        def _():
            grad_own[index] = part[:, :group]
            grad_send[index] = part[:, group:]

        @pl.when(frame == 1)
        def _():
            grad_send[index] = part[:, :group]
            grad_own[index] = part[:, group:]

        cross(2, index).wait_recv()
        out_rows = send[2, index].astype(F32) + recv[2, index].astype(F32)
        block_out[index] = (middle[index] + out_rows + out_shift[1:2]).astype(BF)

        def column(rows_here):
            return jnp.sum(rows_here, axis=0, keepdims=True)

        return (
            gain_sum + column(incoming * normal),
            shift_sum + column(incoming),
            first_sum + column(value),
            second_sum + column(cot_rows),
        )

    start = tuple(jnp.zeros((1, model), F32) for _ in range(4))
    sums = lax.fori_loop(0, clips, back, start)
    for row in range(4):
        vectors[row : row + 1] = sums[row]
    value = dot_f32(branch[...], attended[...], ((0,), (0,)))
    grad_rest[:, :head_width] = value.astype(BF)
    for kind in range(3):
        each(0, clips, lambda index: cross(kind, index).wait_send())


def feed(att_own, att_recv, x, cot, weights, gain, shift, out_shift, up_shift):
    clips, rows, model = x.shape
    group = att_own.shape[2]
    hidden_width = up_shift.shape[1]
    span = -(-rows // 16) * 16
    out = jax.ShapeDtypeStruct
    vmem = pl.BlockSpec(memory_space=pltpu.VMEM)
    shapes = [
        out((clips, rows, model), BF),
        out((clips, rows, model), F32),
        out((clips, rows, group), BF),
        out((clips, rows, group), BF),
        out(weights.shape, BF),
        out((4, model), F32),
        out((1, hidden_width), F32),
    ]
    return pl.pallas_call(
        feed_kernel,
        in_specs=[vmem] * 9,
        out_specs=[vmem] * len(shapes),
        out_shape=shapes,
        scratch_shapes=[
            pltpu.VMEM((clips * span, 2 * group), BF),
            pltpu.VMEM((clips * span, model), BF),
            pltpu.VMEM((clips * span, model), BF),
            pltpu.VMEM((clips * span, hidden_width), BF),
            pltpu.VMEM((clips * span, hidden_width), BF),
            pltpu.VMEM((clips * span, model), BF),
            pltpu.VMEM((clips, rows, model), F32),
            pltpu.VMEM((3, clips, rows, model), BF),
            pltpu.VMEM((3, clips, rows, model), BF),
            pltpu.SemaphoreType.DMA((2, 3, clips)),
        ],
        compiler_params=pltpu.CompilerParams(
            collective_id=4, has_side_effects=True, vmem_limit_bytes=VMEM_LIMIT
        ),
        name="feed_forward_both_ways",
    )(att_own, att_recv, x, cot, weights, gain, shift, out_shift, up_shift)


def precise(pattern, *operands):
    return jnp.einsum(pattern, *operands, precision=lax.Precision.HIGHEST)


def split_groups(value, which, axis):
    half = value.shape[axis] // 2
    low = lax.slice_in_dim(value, 0, half, axis=axis)
    high = lax.slice_in_dim(value, half, None, axis=axis)
    first = which == 0
    return jnp.where(first, low, high), jnp.where(first, high, low)


def join_groups(own, peer, which, axis):
    first = which == 0
    return jnp.concatenate([jnp.where(first, own, peer), jnp.where(first, peer, own)], axis=axis)


def time_choices(stride_group, memory_place, which, own, table_rows):
    local = jnp.arange(own, dtype=jnp.int32)
    times = jnp.concatenate([which * own + local, (1 - which) * own + local])
    stride = jnp.left_shift(jnp.int32(2), stride_group)[:, None, None]
    offset = 8 * (FRAMES - 1)
    current = stride * (times[None, :, None] - times[None, None, :]) + offset
    slots = [memory_place[:, index : index + 1] for index in range(4)]
    first = jnp.concatenate([slots[2], slots[0], slots[3], slots[1]], axis=1)
    second = jnp.concatenate([slots[3], slots[1], slots[2], slots[0]], axis=1)
    places = jnp.where(which == 0, first, second)
    memory = stride * times[None, :, None] + places[:, None, :] + offset
    chosen = jnp.concatenate([current, memory], axis=2)
    return (chosen[..., None] == jnp.arange(table_rows, dtype=jnp.int32)).astype(F32)


def space_choices():
    places = np.arange(SIDE)
    offsets = places[:, None] - places[None, :] + SIDE - 1
    hot = offsets.reshape(-1)[:, None] == np.arange(2 * SIDE - 1)[None, :]
    return jnp.asarray(hot.astype(np.float32))


def space_sums():
    spans = 2 * SIDE - 1
    hot = np.zeros((32, BIAS_COLS), np.float32)
    for axis in range(2):
        for query in range(SIDE):
            for key in range(SIDE):
                col = SPACE_AT + axis * CELLS + query * SIDE + key
                hot[axis * spans + query - key + SIDE - 1, col] = 1.0
    return hot


def wide_rows(rows, heads):
    count, members, unit = rows.shape
    padded = jnp.pad(rows, ((0, 0), (0, 0), (0, LANES - unit)))
    spread = jnp.broadcast_to(padded[:, :, None], (count, members, heads, LANES))
    return spread.reshape(count, members * heads * LANES)


def local(
    clips_in,
    cached_kv,
    old_memory,
    stride_group,
    memory_place,
    norm_gain,
    norm_shift,
    qkv_weight,
    qkv_shift,
    pool_kernel,
    pool_gain,
    pool_shift,
    squeeze_kernel,
    time_table,
    space_tables,
    proj_weight,
    out_shift,
    up_weight,
    up_shift,
    down_weight,
    cotangent,
):
    clip_count, rows_clip, model_width = clips_in.shape
    head_width = qkv_weight.shape[2]
    unit = pool_gain.shape[1]
    head_count = head_width // unit
    frame_count = lax.axis_size("frame")
    heads = head_count // frame_count
    own_frames = rows_clip // CELLS
    group_width = heads * unit
    group_span = FRAMES // MEMF
    scale = unit ** (-0.5)
    which = lax.axis_index("frame")
    into_np, outof_np = placement(frame_count)
    keys_np, mask_np, pad_np = bias_constants(frame_count)
    consts = (
        jnp.asarray(into_np, BF),
        jnp.asarray(outof_np, BF),
        jnp.asarray(keys_np, BF),
        jnp.asarray(mask_np),
        jnp.asarray(pad_np),
    )

    cached_flat = cached_kv.reshape(clip_count, rows_clip, 2 * head_width)
    time_hot = time_choices(stride_group, memory_place, which, own_frames, time_table.shape[0])
    time_rows = precise("ctkr,rd->ctkd", time_hot, time_table).reshape(clip_count, -1, unit)
    space_hot = space_choices()
    space_rows = precise("pr,xrd->xpd", space_hot, space_tables).reshape(2 * CELLS, unit)
    space_rows = jnp.broadcast_to(space_rows[None], (clip_count,) + space_rows.shape)
    bias = jnp.concatenate(
        [
            jnp.pad(time_rows, ((0, 0), (0, SPACE_AT - time_rows.shape[1]), (0, LANES - unit))),
            jnp.pad(
                space_rows,
                ((0, 0), (0, BIAS_COLS - SPACE_AT - 2 * CELLS), (0, LANES - unit)),
            ),
        ],
        axis=1,
    )
    bias = bias * (1.0 / scale)
    inputs = (
        clips_in, qkv_weight.transpose(1, 0, 2), norm_gain, norm_shift, qkv_shift, cached_flat,
        old_memory.reshape(clip_count, -1, 2 * head_width), squeeze_kernel, proj_weight.T, up_weight,
        down_weight.T,
    )
    clip_axis = lax.axis_size("clip")
    if qkv_weight.shape[0] % 16:
        attn_group, packed, normed, mem_own, mem_peer, column = project_plain(
            *inputs, clip_axis, unit
        )
        forward = attention_forward(
            packed, mem_own, mem_peer, column, consts, pool_kernel, pool_gain, pool_shift, bias,
            scale, unit, rows_clip,
        )
    else:
        attn_group, packed, normed, *forward = front(
            *inputs, consts, pool_kernel, pool_gain, pool_shift, bias, scale, clip_axis, unit
        )
    attended_own, attended_peer, rest_full = forward[:3]
    rest_full = rest_full.reshape(model_width, -1)
    saved = forward[3:]
    block_out, middle_grad, attended_grad_own, attended_grad_send, grad_rest, vectors, up_grads = (
        feed(
            attended_own, attended_peer, clips_in, cotangent, rest_full, norm_gain,
            norm_shift, out_shift, up_shift.reshape(1, -1),
        )
    )
    outers = lax.axis_size("clip") // 2
    grad_rest = grad_rest.reshape(outers, 4, -1, grad_rest.shape[1])
    backward = attention_backward(
        packed, normed, attn_group, attended_grad_own, attended_grad_send, grad_rest, consts,
        pool_kernel, pool_gain, bias, saved, scale, unit,
    )
    row_own, row_recv, mem_grad_own, mem_grad_peer = backward[:4]
    taps_grad, pool_gain_grad, pool_shift_grad, bias_grad = backward[4:8]
    attn_grad, joined_grad, rest_part, rest_early = backward[8:]

    time_count = time_rows.shape[1]
    hot = time_hot.reshape(clip_count, time_count, -1).astype(BF)
    hot = jnp.pad(hot, ((0, 0), (0, 0), (0, -hot.shape[2] % LANES)))
    devices = lax.axis_size("clip") * frame_count * lax.axis_size("head")
    (grad_in, qkv_shard, rest_late, small), plan = tail(
        row_own, row_recv, clips_in, middle_grad,
        attn_grad.reshape(outers, 4, -1, attn_grad.shape[1]), joined_grad, norm_gain, taps_grad,
        pool_gain_grad, pool_shift_grad, bias_grad, hot,
        jnp.asarray(space_sums(), BF), cached_flat, mem_grad_own, mem_grad_peer, vectors,
        up_grads, rest_part, lax.axis_size("clip"), devices, unit, time_table.shape[0],
    )
    (
        grad_in, block_out, gain_sums, shift_sums, out_sums, qkv_bias_sum, up_bias_sum, kernel_sum,
        pool_gain_sum, pool_shift_sum, squeeze_sum, time_sum, space_sum, qkv_shard, proj_shard,
        up_shard, down_shard,
    ) = unpack(
        small, qkv_shard, rest_early, rest_late, grad_in, block_out, plan, unit,
        up_weight.shape[1], time_table.shape[0],
    )
    return (
        block_out,
        grad_in,
        gain_sums,
        shift_sums,
        qkv_shard.transpose(1, 0, 2),
        qkv_bias_sum,
        kernel_sum,
        pool_gain_sum,
        pool_shift_sum,
        squeeze_sum,
        time_sum.T,
        space_sum.transpose(1, 0, 2),
        proj_shard.T,
        out_sums,
        up_shard,
        up_bias_sum.reshape(-1),
        down_shard.T,
    )


def solution(mesh):
    return jax.shard_map(
        local,
        mesh=mesh,
        in_specs=(
            P("clip", "frame", None),
            P("clip", "frame", None, "head"),
            P("clip", "frame", None, "head"),
            P("clip"),
            P("clip", None),
            P(),
            P(),
            P(("clip", "frame"), None, "head"),
            P(None, "head"),
            P(),
            P(),
            P(),
            P(),
            P(),
            P(),
            P("head", ("clip", "frame")),
            P(),
            P(("clip", "frame"), "head"),
            P("head"),
            P("head", ("clip", "frame")),
            P("clip", "frame", None),
        ),
        out_specs=(
            P("clip", "frame", None),
            P("clip", "frame", None),
            P(),
            P(),
            P(("clip", "frame"), None, "head"),
            P(None, "head"),
            P(),
            P(),
            P(),
            P(),
            P(),
            P(),
            P("head", ("clip", "frame")),
            P(),
            P(("clip", "frame"), "head"),
            P("head"),
            P("head", ("clip", "frame")),
        ),
        check_vma=False,
    )
```

```python
from functools import partial

import jax
import jax.numpy as jnp
import numpy as np
from jax import lax
from jax.experimental import pallas as pl
from jax.experimental.pallas import tpu as pltpu
from jax.sharding import PartitionSpec as P

FRAMES = 8
MEMF = 2
SIDE = 7
CELLS = SIDE * SIDE
LANES = 128
HALF = 208
QROWS = 2 * HALF
GRID_ROWS = FRAMES * SIDE * 8
MEM_AT = QROWS
MEM_PAD = 112
MEM_BACK = 64
MEM_STEP = 56
TURN_STEP = 3
TURN_PAIRS = 1
TURN_LAG = 5
KROWS = 640
BIAS_COLS = 256
SPACE_AT = 128
PAD_LANE = 127
BF = jnp.bfloat16
F32 = jnp.float32
VMEM_LIMIT = 60 * 1024 * 1024
MESH_ID = pl.DeviceIdType.MESH


def dot_f32(a, b, dims):
    return lax.dot_general(a, b, (dims, ((), ())), preferred_element_type=F32)


def frame_order(first, own):
    rest = [t for t in range(FRAMES) if not first * own <= t < (first + 1) * own]
    return list(range(first * own, (first + 1) * own)) + rest


def placement(frame_count):
    own = FRAMES // frame_count
    into = np.zeros((frame_count, GRID_ROWS, QROWS), np.float32)
    for first in range(frame_count):
        for slot, frame in enumerate(frame_order(first, own)):
            base = (slot // own) * HALF + (slot % own) * CELLS
            for high in range(SIDE):
                for wide in range(SIDE):
                    row = (frame * SIDE + high) * 8 + wide
                    into[first, row, base + high * SIDE + wide] = 1.0
    return into, np.ascontiguousarray(into.transpose(0, 2, 1))


def bias_constants(frame_count):
    own = FRAMES // frame_count
    frames_all = FRAMES + 2 * MEMF
    keys = np.zeros((BIAS_COLS, KROWS), np.float32)
    valid = np.zeros((KROWS,), bool)

    def mark(col, slot, high, wide):
        valid[col] = True
        for query in range(FRAMES):
            keys[query * frames_all + slot, col] = 1.0
        for place in range(SIDE):
            keys[SPACE_AT + place * SIDE + high, col] = 1.0
            keys[SPACE_AT + CELLS + place * SIDE + wide, col] = 1.0

    mask = np.zeros((QROWS, BIAS_COLS), np.float32)
    for slot in range(FRAMES):
        base = (slot // own) * HALF + (slot % own) * CELLS
        for high in range(SIDE):
            for wide in range(SIDE):
                row = base + high * SIDE + wide
                mark(row, slot, high, wide)
                mask[row, slot * frames_all : (slot + 1) * frames_all] = 1.0
                mask[row, SPACE_AT + high * SIDE : SPACE_AT + (high + 1) * SIDE] = 1.0
                low = SPACE_AT + CELLS + wide * SIDE
                mask[row, low : low + SIDE] = 1.0
    for group in range(2):
        for inner in range(MEMF):
            slot = FRAMES + group * MEMF + inner
            for high in range(SIDE):
                for wide in range(SIDE):
                    col = MEM_AT + group * MEM_PAD + inner * MEM_STEP + high * SIDE + wide
                    mark(col, slot, high, wide)
    keys[PAD_LANE, ~valid] = -1e9
    pad_row = np.zeros((1, BIAS_COLS), np.float32)
    pad_row[0, PAD_LANE] = 1.0
    return keys, mask, pad_row


def spread_heads(source, target, rows_at, units, unit, first=0):
    count = source.shape[0]
    for index in range(units):
        at = (first + index) * unit
        target[rows_at : rows_at + count, index * LANES : index * LANES + unit] = source[
            :, at : at + unit
        ]


def spread_tables(kernel_ref, taps, pairs, heads, unit):
    taps[...] = jnp.zeros_like(taps)
    for _, target in pairs:
        target[...] = jnp.zeros_like(target)
    for member in range(3):
        for index in range(heads):
            at = (member * heads + index) * LANES
            for tap in range(27):
                row = kernel_ref[member, tap : tap + 1]
                taps[tap, :, at : at + unit] = jnp.broadcast_to(row, (8, unit))
            for source, target in pairs:
                target[:, at : at + unit] = source[member : member + 1]


def load_shifted(field, shifted):
    grid = field.reshape(FRAMES, SIDE, 8, field.shape[-1])
    flat = field.reshape(FRAMES * SIDE, 8, field.shape[-1])
    shifted[1, 1 : FRAMES + 1, 1 : SIDE + 1] = grid
    shifted[0, 1 : FRAMES + 1, 1 : SIDE + 1] = pltpu.roll(flat, 1, 1).reshape(grid.shape)
    shifted[2, 1 : FRAMES + 1, 1 : SIDE + 1] = pltpu.roll(flat, 7, 1).reshape(grid.shape)


def convolve(shifted, taps, target, flip):
    tiles = target.shape[-1] // LANES

    def step(pair, carry):
        for sub in range(2):
            frame = pair * 2 + sub
            for tile in range(tiles):
                lanes = slice(tile * LANES, (tile + 1) * LANES)
                total = None
                for i in range(3):
                    for k in range(3):
                        rows = shifted[k, frame + i, :, :, lanes]
                        for j in range(3):
                            if flip:
                                tap = (2 - i) * 9 + (2 - j) * 3 + (2 - k)
                            else:
                                tap = i * 9 + j * 3 + k
                            value = rows[j : j + SIDE] * taps[tap, :, lanes][None]
                            total = value if total is None else total + value
                target[frame, :, :, lanes] = total
        return carry

    lax.fori_loop(0, FRAMES // 2, step, 0)


def tap_grads(shifted, grads, target):
    tiles = target.shape[-1] // LANES

    def step(index, carry):
        lanes = pl.ds(pl.multiple_of(index * LANES, LANES), LANES)

        def inner(frame, sums):
            centre = grads[frame + 1, 1 : SIDE + 1, :, lanes]
            new = []
            for i in range(3):
                for k in range(3):
                    rows = shifted[k, frame + i, :, :, lanes]
                    for j in range(3):
                        parts = [rows[j + high] * centre[high] for high in range(SIDE)]
                        parts.append(sums[len(new)])
                        while len(parts) > 1:
                            pairs = zip(parts[::2], parts[1::2])
                            parts = [left + right for left, right in pairs]
                        new.append(parts[0])
            return tuple(new)

        start = tuple(jnp.zeros((8, LANES), F32) for _ in range(27))
        sums = lax.fori_loop(0, FRAMES, inner, start, unroll=4)
        for i in range(3):
            for k in range(3):
                for j in range(3):
                    target[i * 9 + j * 3 + k, :, lanes] += sums[(i * 3 + k) * 3 + j]
        return carry

    lax.fori_loop(0, tiles, step, 0)


def head_stats(values, unit):
    average = jnp.sum(values, axis=-1, keepdims=True) * (1.0 / unit)
    lane = lax.broadcasted_iota(jnp.int32, values.shape, 1)
    centred = jnp.where(lane < unit, values - average, 0.0)
    variance = jnp.sum(centred * centred, axis=-1, keepdims=True) * (1.0 / unit)
    return centred, lax.rsqrt(variance + 1e-06)


def frame_partner():
    return (lax.axis_index("clip"), 1 - lax.axis_index("frame"), lax.axis_index("head"))


def partner_copy(source, target, send_sem, recv_sem):
    return pltpu.make_async_remote_copy(
        src_ref=source, dst_ref=target, send_sem=send_sem, recv_sem=recv_sem,
        device_id=frame_partner(), device_id_type=MESH_ID,
    )


def side_partner():
    clip = lax.axis_index("clip")
    across = (clip // 2) * 2 + 1 - clip % 2
    return (across, lax.axis_index("frame"), lax.axis_index("head"))


def side_copy(source, target, send_sem, recv_sem):
    return pltpu.make_async_remote_copy(
        src_ref=source, dst_ref=target, send_sem=send_sem, recv_sem=recv_sem,
        device_id=side_partner(), device_id_type=MESH_ID,
    )


def greet_partner():
    barrier = pltpu.get_barrier_semaphore()
    pl.semaphore_signal(barrier, inc=1, device_id=frame_partner(), device_id_type=MESH_ID)
    pl.semaphore_wait(barrier, 1)


def plane_stage(column_ref, rest_full, side_sems, pair_sems, turn_sems, own_sem):
    outers = column_ref.shape[0]
    split = min(TURN_PAIRS, outers)
    outer = lax.axis_index("clip") // 2
    inner = lax.axis_index("clip") % 2
    frame = lax.axis_index("frame")
    place = inner * 2 + frame
    side_place = (1 - inner) * 2 + frame
    pair_place = inner * 2 + 1 - frame
    turn_place = (1 - inner) * 2 + 1 - frame
    own_copy = pltpu.make_async_copy(column_ref, rest_full.at[:, place], own_sem)

    def side_move(at, source, target):
        return side_copy(source, target, side_sems.at[0, at], side_sems.at[1, at])

    def pair_move(at, source, target):
        return partner_copy(source, target, pair_sems.at[0, at], pair_sems.at[1, at])

    def to_side(at):
        return side_move(at, column_ref.at[at], rest_full.at[at, place])

    def to_pair(at):
        return pair_move(at, column_ref.at[at], rest_full.at[at, place])

    def turn_side(at):
        block = rest_full.at[at, pair_place]
        return side_copy(block, block, turn_sems.at[0, at], turn_sems.at[1, at])

    def turn_pair(at):
        block = rest_full.at[at, side_place]
        return partner_copy(block, block, turn_sems.at[0, at], turn_sems.at[1, at])

    def turned(at):
        block = rest_full.at[at, turn_place]
        return side_copy(block, block, turn_sems.at[0, at], turn_sems.at[1, at])

    def side_arrival(at):
        block = rest_full.at[at, side_place]
        return side_move(at, block, block)

    def pair_arrival(at):
        block = rest_full.at[at, pair_place]
        return pair_move(at, block, block)

    def send(at):
        to_side(at).start()
        to_pair(at).start()

    def spot(step):
        return (outer + step) % outers

    def turn(step):
        at = spot(step)
        if step < split:
            side_arrival(at).wait_recv()
            turn_pair(at).start()
        else:
            pair_arrival(at).wait_recv()
            turn_side(at).start()

    def finish():
        own_copy.wait()
        each(0, split, lambda step: pair_arrival(spot(step)).wait_recv())
        each(split, outers, lambda step: side_arrival(spot(step)).wait_recv())
        each(0, outers, lambda at: turned(at).wait_recv())
        each(0, split, lambda step: turn_pair(spot(step)).wait_send())
        each(split, outers, lambda step: turn_side(spot(step)).wait_send())
        each(0, outers, lambda at: to_side(at).wait_send())
        each(0, outers, lambda at: to_pair(at).wait_send())

    return own_copy, send, turn, finish


def attend_clip(
    packed, mem_own, mem_peer, frame, into_ref, outof_ref, gain_ref, shift_ref, bias_ref,
    keyhot_ref, mask_ref, pad_ref, out_own, out_peer, q_out, k_out, v_out, p_out, c_out, shifted,
    taps, heads, unit, scale, after_conv,
):
    units = 3 * heads
    own_rows = out_own.shape[0]
    load_shifted(dot_f32(into_ref[frame], packed[...], ((1,), (0,))), shifted)
    conv = c_out.at[0]
    convolve(shifted, taps, conv, False)
    after_conv()
    k_out[0, MEM_AT:, :] = jnp.zeros((KROWS - MEM_AT, heads * LANES), BF)
    v_out[0, MEM_AT:, :] = jnp.zeros((KROWS - MEM_AT, heads * LANES), BF)
    spread_heads(mem_own, k_out.at[0], MEM_AT, heads, unit, 0 * heads)
    spread_heads(mem_own, v_out.at[0], MEM_AT, heads, unit, 1 * heads)
    spread_heads(mem_peer, k_out.at[0], MEM_AT + MEM_PAD, heads, unit, 0 * heads)
    spread_heads(mem_peer, v_out.at[0], MEM_AT + MEM_PAD, heads, unit, 1 * heads)
    for index in range(units):
        lanes = slice(index * LANES, (index + 1) * LANES)
        block = conv[:, :, :, lanes].reshape(GRID_ROWS, LANES)
        centred, rate = head_stats(block, unit)
        normal = centred * rate * gain_ref[:, lanes] + shift_ref[:, lanes]
        rows = dot_f32(outof_ref[frame], normal.astype(BF), ((1,), (0,))).astype(BF)
        target = (q_out, k_out, v_out)[index // heads]
        local = slice((index % heads) * LANES, (index % heads + 1) * LANES)
        target[0, 0:QROWS, local] = rows

    bias = bias_ref[0]
    bias_high = bias.astype(BF)
    bias_low = (bias - bias_high.astype(F32)).astype(BF)
    for head in range(heads):
        lanes = slice(head * LANES, (head + 1) * LANES)
        keys = k_out[0, :, lanes]
        values = v_out[0, :, lanes]
        for half in range(2):
            rows = slice(half * HALF, (half + 1) * HALF)
            query = q_out[0, rows, lanes]
            table = dot_f32(query, bias_high, ((1,), (1,))) + dot_f32(query, bias_low, ((1,), (1,)))
            table = table * mask_ref[rows, :] + pad_ref[...]
            table_high = table.astype(BF)
            table_low = (table - table_high.astype(F32)).astype(BF)
            scores = dot_f32(query, keys, ((1,), (1,)))
            scores = scores + dot_f32(table_high, keyhot_ref[...], ((1,), (0,)))
            scores = scores + dot_f32(table_low, keyhot_ref[...], ((1,), (0,)))
            top = jnp.max(scores, axis=-1, keepdims=True)
            weights = jnp.exp((scores - top) * scale)
            total = jnp.sum(weights, axis=-1, keepdims=True)
            probs = (weights * (1.0 / total)).astype(BF)
            p_out[0, head, rows, :] = probs
            mixed = dot_f32(probs, values, ((1,), (0,))) + query.astype(F32)
            target = (out_own, out_peer)[half]
            target[:, head * unit : (head + 1) * unit] = mixed[:own_rows, :unit].astype(BF)


def forward_kernel(
    packed_ref, mem_own_ref, mem_peer_ref, column_ref, into_ref, outof_ref, kernel_ref,
    pool_gain_ref, pool_shift_ref, bias_ref, keyhot_ref, mask_ref, pad_ref,
    out_own, out_recv, rest_full, q_out, k_out, v_out, p_out, c_out,
    shifted, taps, gain_ref, shift_ref, out_send, out_sems, side_sems, pair_sems, turn_sems,
    own_sem,
    *, heads, unit, scale,
):
    clip = pl.program_id(0)
    clips = out_send.shape[0]
    frame = lax.axis_index("frame")

    def out_copy(index):
        return partner_copy(
            out_send.at[index], out_recv.at[index], out_sems.at[0, index], out_sems.at[1, index]
        )

    own_copy, send, turn, finish = plane_stage(
        column_ref, rest_full, side_sems, pair_sems, turn_sems, own_sem
    )

    @pl.when(clip == 0)
    def _():
        barrier = pltpu.get_barrier_semaphore()
        for device in (frame_partner(), side_partner()):
            pl.semaphore_signal(barrier, inc=1, device_id=device, device_id_type=MESH_ID)
        pl.semaphore_wait(barrier, 2)
        each(0, column_ref.shape[0], send)
        own_copy.start()
        shifted[...] = jnp.zeros_like(shifted)
        pairs = ((pool_gain_ref, gain_ref), (pool_shift_ref, shift_ref))
        spread_tables(kernel_ref, taps, pairs, heads, unit)

    @pl.when(clip == jnp.minimum(TURN_STEP, clips - 1))
    def _():
        for step in range(column_ref.shape[0]):
            turn(step)

    attend_clip(
        packed_ref.at[0], mem_own_ref.at[0], mem_peer_ref.at[0], frame, into_ref, outof_ref,
        gain_ref, shift_ref, bias_ref, keyhot_ref, mask_ref, pad_ref, out_own.at[0],
        out_send.at[clip], q_out, k_out, v_out, p_out, c_out, shifted, taps, heads, unit, scale,
        lambda: None,
    )
    out_copy(clip).start()

    @pl.when(clip == clips - 1)
    def _():
        finish()
        for index in range(clips):
            out_copy(index).wait()


def backward_kernel(
    packed_ref, normed_ref, weight_ref, grad_own_ref, grad_send_ref, rest_ref, into_ref, outof_ref,
    kernel_ref, pool_gain_ref, bias_ref, keyhot_ref, mask_ref, q_ref, k_ref, v_ref, p_ref, c_ref,
    row_own, row_recv, mem_own, mem_recv, taps_out, gain_out, shift_out, bias_out, weight_out,
    joined_out, rest_part, rest_out,
    shifted, taps, gain_ref, grads, spread, pooled, peer, mem_send, rest_own, rest_side, rest_send,
    rest_peer, rest_sum, rest_far, weight_sum, keep, cross_send, cross_recv, row_send,
    grad_sems, mem_sems, own_sems, side_sems, rest_sems, far_sems, cross_sems, row_sems,
    *, heads, unit, scale,
):
    units = 3 * heads
    own_rows = grad_own_ref.shape[1]
    clip = pl.program_id(0)
    clips = peer.shape[0]
    clip_at = lax.axis_index("clip")
    frame = lax.axis_index("frame")
    head_at = lax.axis_index("head")

    def grad_copy(index):
        return partner_copy(
            grad_send_ref.at[index], peer.at[index], grad_sems.at[0, index], grad_sems.at[1, index]
        )

    def mem_copy(index):
        return partner_copy(
            mem_send.at[index], mem_recv.at[index], mem_sems.at[0, index], mem_sems.at[1, index]
        )

    def row_copy(index):
        return partner_copy(
            row_send.at[index], row_recv.at[index], row_sems.at[0, index], row_sems.at[1, index]
        )

    def cross_copy(index):
        return pltpu.make_async_remote_copy(
            src_ref=cross_send.at[index], dst_ref=cross_recv.at[index],
            send_sem=cross_sems.at[0, index], recv_sem=cross_sems.at[1, index],
            device_id=(clip_at, frame, 1 - head_at), device_id_type=MESH_ID,
        )

    def finish_rows(index):
        cross_copy(index).wait_recv()
        total = (keep[index].astype(F32) + cross_recv[index].astype(F32)).astype(BF)
        row_own[index] = total[:own_rows]
        row_send[index] = total[HALF : HALF + own_rows]
        row_copy(index).start()

    chunks, outers, _, _, cols = rest_own.shape
    side_at = clip_at % 2
    outer = clip_at // 2
    early = rest_far.shape[0]

    def rest_at(side, chunk):
        return rest_ref.at[:, pl.ds(side * 2, 2), :, pl.ds(chunk * cols, cols)]

    def own_copy(chunk):
        return pltpu.make_async_copy(
            rest_at(side_at, chunk), rest_own.at[chunk], own_sems.at[chunk]
        )

    def over_copy(chunk):
        return side_copy(
            rest_at(1 - side_at, chunk), rest_side.at[chunk], side_sems.at[0, chunk],
            side_sems.at[1, chunk],
        )

    def rest_copy(chunk):
        return partner_copy(
            rest_send.at[chunk], rest_peer.at[chunk], rest_sems.at[0, chunk],
            rest_sems.at[1, chunk],
        )

    def pass_on(chunk):
        own_copy(chunk).wait()
        over_copy(chunk).wait_recv()

        def add(index):
            def total(part):
                first = rest_own[chunk, index, part].astype(F32)
                return (first + rest_side[chunk, index, part].astype(F32)).astype(BF)

            rest_send[chunk, index] = total(1 - frame)
            rest_sum[chunk, index] = total(frame)

        each(0, outers, add)
        rest_copy(chunk).start()

    def far_device(step):
        return (((outer + step) % outers) * 2 + side_at, frame, head_at)

    def far_copy(chunk, step):
        there = (outer + step) % outers
        return pltpu.make_async_remote_copy(
            src_ref=rest_sum.at[chunk, there], dst_ref=rest_far.at[chunk, step],
            send_sem=far_sems.at[0, chunk, step], recv_sem=far_sems.at[1, chunk, step],
            device_id=far_device(step), device_id_type=MESH_ID,
        )

    def settle(chunk):
        rest_copy(chunk).wait_recv()

        def add(index):
            total = rest_sum[chunk, index].astype(F32) + rest_peer[chunk, index].astype(F32)
            if chunk < early:
                rest_sum[chunk, index] = total.astype(BF)
            else:
                rest_part[index] = total.astype(BF)

        each(0, outers, add)
        if chunk < early:
            each(1, outers, lambda step: far_copy(chunk, step).start())

    @pl.when(clip == 0)
    def _():
        barrier = pltpu.get_barrier_semaphore()

        def greet(device):
            pl.semaphore_signal(barrier, inc=1, device_id=device, device_id_type=MESH_ID)

        for device in (frame_partner(), side_partner(), (clip_at, frame, 1 - head_at)):
            greet(device)
        each(1, outers, lambda step: greet(far_device(step)))
        pl.semaphore_wait(barrier, 3 + outers - 1)
        for index in range(clips):
            grad_copy(index).start()
        over_copy(0).start()
        own_copy(0).start()
        shifted[...] = jnp.zeros_like(shifted)
        grads[...] = jnp.zeros_like(grads)
        spread[...] = jnp.zeros_like(spread)
        taps_out[...] = jnp.zeros_like(taps_out)
        gain_out[...] = jnp.zeros_like(gain_out)
        shift_out[...] = jnp.zeros_like(shift_out)
        weight_sum[...] = jnp.zeros_like(weight_sum)
        joined_out[...] = jnp.zeros_like(joined_out)
        spread_tables(kernel_ref, taps, ((pool_gain_ref, gain_ref),), heads, unit)

    def pump(odd):
        for chunk in range(chunks):
            point = min(chunk + 1, 2 * clips - 1)
            if point % 2 == odd:

                @pl.when(clip == point // 2)
                def _():
                    if chunk + 1 < chunks:
                        over_copy(chunk + 1).start()
                        own_copy(chunk + 1).start()
                    pass_on(chunk)
                    if chunk:
                        settle(chunk - 1)

    pump(0)
    load_shifted(dot_f32(into_ref[frame], packed_ref[0], ((1,), (0,))), shifted)
    spread_heads(grad_own_ref.at[0], spread, 0, heads, unit)
    grad_copy(clip).wait_recv()
    spread_heads(peer.at[clip], spread, HALF, heads, unit)
    bias_low = bias_ref[0].astype(BF)
    bias_sum = jnp.zeros((BIAS_COLS, LANES), F32)
    for head in range(heads):
        lanes = slice(head * LANES, (head + 1) * LANES)
        keys = k_ref[0, :, lanes]
        values = v_ref[0, :, lanes]
        keys_grad = jnp.zeros((KROWS, LANES), F32)
        values_grad = jnp.zeros((KROWS, LANES), F32)
        for half in range(2):
            rows = slice(half * HALF, (half + 1) * HALF)
            query = q_ref[0, rows, lanes]
            out_grad = spread[rows, lanes]
            probs = p_ref[0, head, rows, :]
            wide = probs.astype(F32)
            probs_grad = dot_f32(out_grad, values, ((1,), (1,)))
            weighted = wide * probs_grad
            shared = jnp.sum(weighted, axis=-1, keepdims=True)
            score_grad = (weighted - wide * shared).astype(BF)
            values_grad = values_grad + dot_f32(probs, out_grad, ((0,), (0,)))
            keys_grad = keys_grad + dot_f32(score_grad, query, ((0,), (0,)))
            table_grad = dot_f32(score_grad, keyhot_ref[...], ((1,), (1,))) * mask_ref[rows, :]
            table_low = table_grad.astype(BF)
            query_grad = dot_f32(score_grad, keys, ((1,), (0,)))
            query_grad = query_grad + dot_f32(table_low, bias_low, ((1,), (0,)))
            query_grad = query_grad * scale + out_grad.astype(F32)
            pooled[rows, lanes] = query_grad.astype(BF)
            bias_sum = bias_sum + dot_f32(table_low, query, ((0,), (0,)))
        keys_grad = (keys_grad * scale).astype(BF)
        values_grad = values_grad.astype(BF)
        for member, part in enumerate((keys_grad, values_grad)):
            at = ((member + 1) * heads + head) * LANES
            pooled[:, at : at + LANES] = part[:QROWS]
            at = (member * heads + head) * LANES
            low = MEM_AT + MEM_PAD
            mem_own[0, :, at : at + LANES] = part[MEM_AT : MEM_AT + MEM_BACK]
            mem_send[clip, :, at : at + LANES] = part[low : low + MEM_BACK]
    bias_out[0] = bias_sum
    mem_copy(clip).start()

    for index in range(units):
        lanes = slice(index * LANES, (index + 1) * LANES)
        incoming = dot_f32(into_ref[frame], pooled[:, lanes], ((1,), (0,)))
        block = c_ref[0, :, :, :, lanes].reshape(GRID_ROWS, LANES)
        centred, rate = head_stats(block, unit)
        normal = centred * rate
        product = incoming * normal
        gain_out[:, lanes] += jnp.sum(product, axis=0, keepdims=True)
        shift_out[:, lanes] += jnp.sum(incoming, axis=0, keepdims=True)
        inner = incoming * gain_ref[:, lanes]
        mean_inner = jnp.sum(inner, axis=-1, keepdims=True) * (1.0 / unit)
        mean_both = jnp.sum(inner * normal, axis=-1, keepdims=True) * (1.0 / unit)
        lane = lax.broadcasted_iota(jnp.int32, block.shape, 1)
        result = rate * (inner - mean_inner - normal * mean_both)
        result = jnp.where(lane < unit, result, 0.0)
        flat = result.reshape(FRAMES * SIDE, 8, LANES)
        shape = (FRAMES, SIDE, 8, LANES)
        grads[1, 1 : FRAMES + 1, 1 : SIDE + 1, :, lanes] = flat.reshape(shape)
        grads[0, 1 : FRAMES + 1, 1 : SIDE + 1, :, lanes] = pltpu.roll(flat, 1, 1).reshape(shape)
        grads[2, 1 : FRAMES + 1, 1 : SIDE + 1, :, lanes] = pltpu.roll(flat, 7, 1).reshape(shape)

    @pl.when(clip > 0)
    def _():
        finish_rows(clip - 1)

    pump(1)
    tap_grads(shifted, grads.at[1], taps_out)
    conv = shifted.at[1, 1 : FRAMES + 1, 1 : SIDE + 1]
    convolve(grads, taps, conv, True)
    for index in range(units):
        lanes = slice(index * LANES, (index + 1) * LANES)
        block = shifted[1, 1 : FRAMES + 1, 1 : SIDE + 1, :, lanes].reshape(GRID_ROWS, LANES)
        rows = dot_f32(outof_ref[frame], block.astype(BF), ((1,), (0,))).astype(BF)
        pooled[:, lanes] = rows
        joined_out[:, lanes] += jnp.sum(rows.astype(F32), axis=0, keepdims=True)
    weight_sum[...] += dot_f32(normed_ref[0], pooled[...], ((0,), (0,)))
    result = dot_f32(pooled[...], weight_ref[...], ((1,), (1,))).astype(BF)
    cut = result.shape[1] // 2

    @pl.when(head_at == 0)
    def _():
        keep[clip] = result[:, :cut]
        cross_send[clip] = result[:, cut:]

    @pl.when(head_at == 1)
    def _():
        keep[clip] = result[:, cut:]
        cross_send[clip] = result[:, :cut]

    cross_copy(clip).start()

    @pl.when(clip == clips - 1)
    def _():
        weight_out[...] = weight_sum[...].astype(BF)
        finish_rows(clip)
        settle(chunks - 1)
        for chunk in range(early):
            each(1, outers, lambda step: far_copy(chunk, step).wait_recv())
            rest_out[:, chunk * cols : (chunk + 1) * cols] = lax.fori_loop(
                1,
                outers,
                lambda step, sums: sums + rest_far[chunk, step].astype(F32),
                rest_sum[chunk, outer].astype(F32),
            )
        for index in range(clips):
            grad_copy(index).wait_send()
            cross_copy(index).wait_send()
            mem_copy(index).wait()
            row_copy(index).wait()
        for chunk in range(chunks):
            over_copy(chunk).wait_send()
            rest_copy(chunk).wait_send()
        for chunk in range(early):
            each(1, outers, lambda step: far_copy(chunk, step).wait_send())


def whole_spec(shape):
    return pl.BlockSpec(shape, lambda clip: (0,) * len(shape))


def clip_spec(shape):
    return pl.BlockSpec((1,) + shape, lambda clip: (clip,) + (0,) * len(shape))


def once_spec(shape):
    return pl.BlockSpec(
        shape, lambda clip: (0,) * len(shape), pipeline_mode=pl.Buffered(1)
    )


def any_spec():
    return pl.BlockSpec(memory_space=pl.ANY)


def attention_forward(
    packed, mem_own, mem_peer, column, consts, kernels, gains, shifts, bias, scale, unit, rows
):
    clips = packed.shape[0]
    heads = packed.shape[2] // (3 * LANES)
    into, outof, keyhot, mask, pad_row = consts
    wide = 3 * heads * LANES
    mem_shape = mem_own.shape[1:]
    outers = column.shape[0]
    dma = pltpu.SemaphoreType.DMA
    out = jax.ShapeDtypeStruct
    return pl.pallas_call(
        partial(forward_kernel, heads=heads, unit=unit, scale=scale),
        grid=(clips,),
        in_specs=[
            clip_spec((QROWS, wide)),
            clip_spec(mem_shape),
            clip_spec(mem_shape),
            once_spec(column.shape),
            once_spec(into.shape),
            once_spec(outof.shape),
            once_spec(kernels.shape),
            once_spec(gains.shape),
            once_spec(shifts.shape),
            clip_spec((BIAS_COLS, LANES)),
            once_spec((BIAS_COLS, KROWS)),
            once_spec((QROWS, BIAS_COLS)),
            once_spec((1, BIAS_COLS)),
        ],
        out_specs=[
            clip_spec((rows, heads * unit)),
            any_spec(),
            any_spec(),
            clip_spec((QROWS, heads * LANES)),
            clip_spec((KROWS, heads * LANES)),
            clip_spec((KROWS, heads * LANES)),
            clip_spec((heads, QROWS, KROWS)),
            clip_spec((FRAMES, SIDE, 8, wide)),
        ],
        scratch_shapes=[
            pltpu.VMEM((3, FRAMES + 2, SIDE + 2, 8, wide), F32),
            pltpu.VMEM((27, 8, wide), F32),
            pltpu.VMEM((1, wide), F32),
            pltpu.VMEM((1, wide), F32),
            pltpu.VMEM((clips, rows, heads * unit), BF),
            dma((2, clips)),
            dma((2, outers)),
            dma((2, outers)),
            dma((2, outers)),
            pltpu.SemaphoreType.DMA,
        ],
        out_shape=[
            out((clips, rows, heads * unit), BF),
            out((clips, rows, heads * unit), BF),
            out((outers, 4) + column.shape[1:], BF),
            out((clips, QROWS, heads * LANES), BF),
            out((clips, KROWS, heads * LANES), BF),
            out((clips, KROWS, heads * LANES), BF),
            out((clips, heads, QROWS, KROWS), BF),
            out((clips, FRAMES, SIDE, 8, wide), F32),
        ],
        compiler_params=pltpu.CompilerParams(
            collective_id=1, has_side_effects=True, vmem_limit_bytes=VMEM_LIMIT
        ),
        name="pooled_attention_forward",
    )(
        packed, mem_own, mem_peer, column, into, outof, kernels, gains, shifts, bias, keyhot, mask,
        pad_row,
    )


def attention_backward(
    packed, normed, weight, grad_own, grad_send, rest, consts, kernels, gains, bias, saved, scale,
    unit,
):
    clips, rows, width = grad_own.shape
    heads = width // unit
    model = weight.shape[0]
    half = model // 2
    into, outof, keyhot, mask, pad_row = consts
    wide = 3 * heads * LANES
    outers, _, shard_rows, rest_width = rest.shape
    chunks = 9
    early = 8
    cols = rest_width // chunks
    out = jax.ShapeDtypeStruct
    dma = pltpu.SemaphoreType.DMA
    return pl.pallas_call(
        partial(backward_kernel, heads=heads, unit=unit, scale=scale),
        grid=(clips,),
        in_specs=[
            clip_spec((QROWS, wide)),
            clip_spec((QROWS, model)),
            once_spec((model, wide)),
            clip_spec((rows, width)),
            any_spec(),
            any_spec(),
            once_spec(into.shape),
            once_spec(outof.shape),
            once_spec(kernels.shape),
            once_spec(gains.shape),
            clip_spec((BIAS_COLS, LANES)),
            once_spec((BIAS_COLS, KROWS)),
            once_spec((QROWS, BIAS_COLS)),
            clip_spec((QROWS, heads * LANES)),
            clip_spec((KROWS, heads * LANES)),
            clip_spec((KROWS, heads * LANES)),
            clip_spec((heads, QROWS, KROWS)),
            clip_spec((FRAMES, SIDE, 8, wide)),
        ],
        out_specs=[
            whole_spec((clips, rows, half)),
            any_spec(),
            clip_spec((MEM_BACK, 2 * heads * LANES)),
            any_spec(),
            whole_spec((27, 8, wide)),
            whole_spec((1, wide)),
            whole_spec((1, wide)),
            clip_spec((BIAS_COLS, LANES)),
            whole_spec((model, wide)),
            whole_spec((1, wide)),
            whole_spec((outers, shard_rows, cols)),
            whole_spec((shard_rows, early * cols)),
        ],
        scratch_shapes=[
            pltpu.VMEM((3, FRAMES + 2, SIDE + 2, 8, wide), F32),
            pltpu.VMEM((27, 8, wide), F32),
            pltpu.VMEM((1, wide), F32),
            pltpu.VMEM((3, FRAMES + 2, SIDE + 2, 8, wide), F32),
            pltpu.VMEM((QROWS, heads * LANES), BF),
            pltpu.VMEM((QROWS, wide), BF),
            pltpu.VMEM((clips, rows, width), BF),
            pltpu.VMEM((clips, MEM_BACK, 2 * heads * LANES), BF),
            pltpu.VMEM((chunks, outers, 2, shard_rows, cols), BF),
            pltpu.VMEM((chunks, outers, 2, shard_rows, cols), BF),
            pltpu.VMEM((chunks, outers, shard_rows, cols), BF),
            pltpu.VMEM((chunks, outers, shard_rows, cols), BF),
            pltpu.VMEM((chunks, outers, shard_rows, cols), BF),
            pltpu.VMEM((early, outers, shard_rows, cols), BF),
            pltpu.VMEM((model, wide), F32),
            pltpu.VMEM((clips, QROWS, half), BF),
            pltpu.VMEM((clips, QROWS, half), BF),
            pltpu.VMEM((clips, QROWS, half), BF),
            pltpu.VMEM((clips, rows, half), BF),
            dma((2, clips)),
            dma((2, clips)),
            dma((chunks,)),
            dma((2, chunks)),
            dma((2, chunks)),
            dma((2, early, outers)),
            dma((2, clips)),
            dma((2, clips)),
        ],
        out_shape=[
            out((clips, rows, half), BF),
            out((clips, rows, half), BF),
            out((clips, MEM_BACK, 2 * heads * LANES), BF),
            out((clips, MEM_BACK, 2 * heads * LANES), BF),
            out((27, 8, wide), F32),
            out((1, wide), F32),
            out((1, wide), F32),
            out((clips, BIAS_COLS, LANES), F32),
            out((model, wide), BF),
            out((1, wide), F32),
            out((outers, shard_rows, cols), BF),
            out((shard_rows, early * cols), F32),
        ],
        compiler_params=pltpu.CompilerParams(
            collective_id=2, has_side_effects=True, vmem_limit_bytes=VMEM_LIMIT
        ),
        name="pooled_attention_backward",
    )(
        packed, normed, weight, grad_own, grad_send, rest, into, outof, kernels, gains, bias, keyhot,
        mask, *saved,
    )


def row_stats(values):
    width = values.shape[-1]
    centred = values - jnp.sum(values, axis=-1, keepdims=True) * (1.0 / width)
    variance = jnp.sum(centred * centred, axis=-1, keepdims=True) * (1.0 / width)
    return centred, lax.rsqrt(variance + 1e-06)


def each(low, high, act):
    def body(step, carry):
        act(step)
        return carry

    lax.fori_loop(low, high, body, 0)


def norm_rows(source, index, gain, shift, target, at):
    rows = source.shape[1]
    centred, rate = row_stats(source[index].astype(F32))
    target[index, at : at + rows] = (centred * rate * gain[0:1] + shift[0:1]).astype(BF)


def project_rows(normed, weight, bias, packed):
    def step(index):
        packed[index] = (dot_f32(normed[index], weight, ((1,), (0,))) + bias[...]).astype(BF)

    each(0, packed.shape[0], step)


def project_moves(
    x, attn, gain, shift, attn_shift, cached, old, squeeze, proj, up, down, full, normed, mem_own,
    mem_peer, rest_column, shards, bias, rest, mem_send, squeeze_rows, x_peer, columns, far_sems,
    near_sems, x_sems, cross_sems, mem_sems, rest_sems,
):
    outers = full.shape[0]
    clips, rows, model = x.shape
    clip = lax.axis_index("clip")
    frame = lax.axis_index("frame")
    head = lax.axis_index("head")
    outer, inner = clip // 2, clip % 2
    place = inner * 2 + frame
    half = model // 2
    lanes = pl.ds(pl.multiple_of(head * half, LANES), half)
    barrier = pltpu.get_barrier_semaphore()

    def far_device(step):
        return device_of((outer + step) % outers, inner, frame, head)

    def near_device(step):
        there_inner, there_frame = plane_peer(inner, frame, step)
        return device_of(outer, there_inner, there_frame, head)

    def greet(device):
        pl.semaphore_signal(barrier, inc=1, device_id=device, device_id_type=MESH_ID)

    group = mem_own.shape[2] // 2
    heads = shards.shape[2] // (3 * LANES)
    unit = group // heads

    def squeeze_clip(index):
        total = jnp.zeros((CELLS, cached.shape[2]), F32)
        for step in range(squeeze_rows.shape[0]):
            rows_here = cached[index, step * CELLS : (step + 1) * CELLS].astype(F32)
            total = total + rows_here * squeeze_rows[step : step + 1]
        pieces = ((0, total.astype(BF)), (MEM_STEP, old[index]))
        for side in range(2):

            @pl.when(frame == side)
            def _():
                for at, value in pieces:
                    for member in range(2):
                        local = slice(member * group, (member + 1) * group)
                        low = (2 * member + side) * group
                        mem_own[index, at : at + CELLS, local] = value[:, low : low + group]
                        low = (2 * member + 1 - side) * group
                        mem_send[index, at : at + CELLS, local] = value[:, low : low + group]

    def far_copy(step, at):
        return pltpu.make_async_remote_copy(
            src_ref=shards, dst_ref=columns.at[at],
            send_sem=far_sems.at[0, step], recv_sem=far_sems.at[1, step],
            device_id=far_device(step), device_id_type=MESH_ID,
        )

    def near_copy(index, step, source, at):
        return pltpu.make_async_remote_copy(
            src_ref=source.at[(frame + step % 2) % 2], dst_ref=full.at[at, place],
            send_sem=near_sems.at[0, index, step - 1], recv_sem=near_sems.at[1, index, step - 1],
            device_id=near_device(step), device_id_type=MESH_ID,
        )

    def near_arrival(index, step, at):
        there_inner, there_frame = plane_peer(inner, frame, step)
        return pltpu.make_async_remote_copy(
            src_ref=shards.at[0], dst_ref=full.at[at, there_inner * 2 + there_frame],
            send_sem=near_sems.at[0, index, step - 1], recv_sem=near_sems.at[1, index, step - 1],
            device_id=near_device(step), device_id_type=MESH_ID,
        )

    def x_copy(index):
        return partner_copy(
            x.at[index, :, lanes], x_peer.at[index, :, lanes], x_sems.at[0, index],
            x_sems.at[1, index],
        )

    def cross_copy(index):
        return pltpu.make_async_remote_copy(
            src_ref=x_peer.at[index, :, lanes], dst_ref=x_peer.at[index, :, lanes],
            send_sem=cross_sems.at[0, index], recv_sem=cross_sems.at[1, index],
            device_id=(clip, frame, 1 - head), device_id_type=MESH_ID,
        )

    def cross_arrival(index):
        other = pl.ds(pl.multiple_of((1 - head) * half, LANES), half)
        return pltpu.make_async_remote_copy(
            src_ref=x_peer.at[index, :, other], dst_ref=x_peer.at[index, :, other],
            send_sem=cross_sems.at[0, index], recv_sem=cross_sems.at[1, index],
            device_id=(clip, frame, 1 - head), device_id_type=MESH_ID,
        )

    mem_copy = partner_copy(mem_send, mem_peer, mem_sems.at[0], mem_sems.at[1])

    def rest_copy(step, at):
        return pltpu.make_async_remote_copy(
            src_ref=rest, dst_ref=rest_column.at[at],
            send_sem=rest_sems.at[0, step], recv_sem=rest_sems.at[1, step],
            device_id=far_device(step), device_id_type=MESH_ID,
        )

    def origin(step):
        return (outer + outers - step) % outers

    def prologue():
        each(1, outers, lambda step: greet(far_device(step)))
        for step in range(1, 4):
            greet(near_device(step))
        greet((clip, frame, 1 - head))
        shards[...] = jnp.zeros_like(shards)
        bias[...] = jnp.zeros_like(bias)
        for member in range(3):
            for side in range(2):
                for index in range(heads):
                    target = (member * heads + index) * LANES
                    source = slice(side * group + index * unit, side * group + (index + 1) * unit)
                    shards[side, :, target : target + unit] = attn[member, :, source]
        at = 0
        for part in (proj, up, down):
            rest[:, at : at + part.shape[1]] = part[...]
            at += part.shape[1]
        for side in range(2):

            @pl.when(frame == side)
            def _():
                for member in range(3):
                    for index in range(heads):
                        target = (member * heads + index) * LANES
                        source = slice(side * group + index * unit, side * group + (index + 1) * unit)
                        bias[:, target : target + unit] = attn_shift[member : member + 1, source]

        for member in range(2):
            for index in range(2 * heads):
                at = (2 * member * heads + index) * unit
                squeeze_rows[:, at : at + unit] = squeeze[member]
        mem_own[...] = jnp.zeros_like(mem_own)
        mem_send[...] = jnp.zeros_like(mem_send)

        pl.semaphore_wait(barrier, outers - 1 + 4)
        each(1, outers, lambda step: far_copy(step, outer).start())
        for step in range(1, 4):
            near_copy(0, step, shards, outer).start()
        each(0, clips, lambda index: x_copy(index).start())
        each(0, clips, squeeze_clip)
        rest_column[outer] = rest[...]
        full[outer, place] = shards[frame]
        normed[...] = jnp.zeros_like(normed)
        each(0, clips, lambda index: norm_rows(x, index, gain, shift, normed, 0))

        def forward(index):
            at = origin(index)
            far_copy(index, at).wait_recv()
            for step in range(1, 4):
                near_copy(index, step, columns.at[at], at).start()
            full[at, place] = columns[at, frame]

        each(1, outers, forward)
        each(1, outers, lambda step: rest_copy(step, outer).start())

        def relay(index):
            x_copy(index).wait_recv()
            cross_copy(index).start()

        each(0, clips, relay)
        mem_copy.start()

        def receive(index):
            cross_arrival(index).wait_recv()
            norm_rows(x_peer, index, gain, shift, normed, HALF)

        each(0, clips, receive)

        def arrive(index):
            for step in range(1, 4):
                near_arrival(index, step, origin(index)).wait_recv()

        each(0, outers, arrive)
    def rest_arrive():
        each(1, outers, lambda step: rest_copy(step, origin(step)).wait_recv())

    def finish():
        each(1, outers, lambda step: rest_copy(step, outer).wait_send())
        each(1, outers, lambda step: far_copy(step, outer).wait_send())
        for step in range(1, 4):
            near_copy(0, step, shards, outer).wait_send()

        def sent(index):
            for step in range(1, 4):
                near_copy(index, step, columns.at[origin(index)], origin(index)).wait_send()

        each(1, outers, sent)

        def x_sent(index):
            x_copy(index).wait_send()
            cross_copy(index).wait_send()

        each(0, clips, x_sent)

    return outer, prologue, mem_copy, rest_arrive, finish


def front_kernel(
    x, attn, gain, shift, attn_shift, cached, old, squeeze, proj, up, down, into_ref, outof_ref,
    kernel_ref, pool_gain_ref, pool_shift_ref, bias_ref, keyhot_ref, mask_ref, pad_ref,
    full_out, packed_out, normed_out, out_own, out_recv, rest_full, q_out, k_out, v_out, p_out,
    c_out, full, shards, attn_bias, rest, mem_send, mem_own, mem_peer, squeeze_rows, x_peer, columns, normed,
    rest_column, shifted, taps, gain_ref, shift_ref, out_send, far_sems, near_sems, x_sems,
    cross_sems, mem_sems, rest_sems, out_sems, side_sems, pair_sems, turn_sems, own_sem,
    *, heads, unit, scale,
):
    clip = pl.program_id(0)
    clips = out_send.shape[0]
    outers = full.shape[0]
    frame = lax.axis_index("frame")
    outer, prologue, mem_copy, rest_arrive, project_finish = project_moves(
        x, attn, gain, shift, attn_shift, cached, old, squeeze, proj, up, down, full, normed,
        mem_own, mem_peer, rest_column, shards, attn_bias, rest, mem_send, squeeze_rows, x_peer,
        columns, far_sems, near_sems, x_sems, cross_sems, mem_sems, rest_sems,
    )
    own_copy, send, turn, plane_finish = plane_stage(
        rest_column, rest_full, side_sems, pair_sems, turn_sems, own_sem
    )

    def out_copy(index):
        return partner_copy(
            out_send.at[index], out_recv.at[index], out_sems.at[0, index], out_sems.at[1, index]
        )

    @pl.when(clip == 0)
    def _():
        prologue()
        send(outer)
        shifted[...] = jnp.zeros_like(shifted)
        pairs = ((pool_gain_ref, gain_ref), (pool_shift_ref, shift_ref))
        spread_tables(kernel_ref, taps, pairs, heads, unit)

    def points(odd):
        for step in range(outers):
            point = min(step + TURN_LAG, 2 * clips - 1)
            if step and step % 2 == odd:

                @pl.when(clip == step // 2)
                def _():
                    send((outer + step) % outers)

            if point % 2 == odd:

                @pl.when(clip == point // 2)
                def _():
                    turn(step)

    def after_conv():
        @pl.when(clip == 0)
        def _():
            mem_copy.wait_recv()
            rest_arrive()
            own_copy.start()

        points(1)

    points(0)
    @pl.when(clip == clips - 1)
    def _():
        full_out[...] = full[...]

    normed_out[0] = normed[clip]
    weight = full[...].reshape(x.shape[2], full.shape[3])
    rows = dot_f32(normed[clip], weight, ((1,), (0,))) + attn_bias[...]
    packed_out[0] = rows.astype(BF)
    attend_clip(
        packed_out.at[0], mem_own.at[clip], mem_peer.at[clip], frame, into_ref, outof_ref, gain_ref,
        shift_ref, bias_ref, keyhot_ref, mask_ref, pad_ref, out_own.at[0], out_send.at[clip], q_out,
        k_out, v_out, p_out, c_out, shifted, taps, heads, unit, scale, after_conv,
    )
    out_copy(clip).start()

    @pl.when(clip == clips - 1)
    def _():
        mem_copy.wait_send()
        project_finish()
        plane_finish()
        for index in range(clips):
            out_copy(index).wait()


def front(
    x, attn, gain, shift, attn_shift, cached, old, squeeze, proj, up, down, consts, kernels, gains,
    shifts, bias, scale, clip_count, unit,
):
    clips, rows, model = x.shape
    _, shard_rows, head_width = attn.shape
    heads = head_width // (2 * unit)
    wide = 3 * heads * LANES
    outers = clip_count // 2
    into, outof, keyhot, mask, pad_row = consts
    rest_shape = (shard_rows, proj.shape[1] + up.shape[1] + down.shape[1])
    mem_shape = (clips, MEM_PAD, head_width)
    out = jax.ShapeDtypeStruct
    dma = pltpu.SemaphoreType.DMA
    operands = (
        x, attn, gain, shift, attn_shift, cached, old, squeeze, proj, up, down, into, outof,
        kernels, gains, shifts, bias, keyhot, mask, pad_row,
    )
    specs = [once_spec(value.shape) for value in operands]
    specs[16] = clip_spec((BIAS_COLS, LANES))
    results = pl.pallas_call(
        partial(front_kernel, heads=heads, unit=unit, scale=scale),
        grid=(clips,),
        in_specs=specs,
        out_specs=[
            whole_spec((outers, 4, shard_rows, wide)),
            clip_spec((QROWS, wide)),
            clip_spec((QROWS, model)),
            clip_spec((rows, heads * unit)),
            any_spec(),
            any_spec(),
            clip_spec((QROWS, heads * LANES)),
            clip_spec((KROWS, heads * LANES)),
            clip_spec((KROWS, heads * LANES)),
            clip_spec((heads, QROWS, KROWS)),
            clip_spec((FRAMES, SIDE, 8, wide)),
        ],
        out_shape=[
            out((outers, 4, shard_rows, wide), BF),
            out((clips, QROWS, wide), BF),
            out((clips, QROWS, model), BF),
            out((clips, rows, heads * unit), BF),
            out((clips, rows, heads * unit), BF),
            out((outers, 4) + rest_shape, BF),
            out((clips, QROWS, heads * LANES), BF),
            out((clips, KROWS, heads * LANES), BF),
            out((clips, KROWS, heads * LANES), BF),
            out((clips, heads, QROWS, KROWS), BF),
            out((clips, FRAMES, SIDE, 8, wide), F32),
        ],
        scratch_shapes=[
            pltpu.VMEM((outers, 4, shard_rows, wide), BF),
            pltpu.VMEM((2, shard_rows, wide), BF),
            pltpu.VMEM((1, wide), F32),
            pltpu.VMEM(rest_shape, BF),
            pltpu.VMEM(mem_shape, BF),
            pltpu.VMEM(mem_shape, BF),
            pltpu.VMEM(mem_shape, BF),
            pltpu.VMEM((squeeze.shape[1], cached.shape[2]), F32),
            pltpu.VMEM((clips, rows, model), BF),
            pltpu.VMEM((outers, 2, shard_rows, wide), BF),
            pltpu.VMEM((clips, QROWS, model), BF),
            pltpu.VMEM((outers,) + rest_shape, BF),
            pltpu.VMEM((3, FRAMES + 2, SIDE + 2, 8, wide), F32),
            pltpu.VMEM((27, 8, wide), F32),
            pltpu.VMEM((1, wide), F32),
            pltpu.VMEM((1, wide), F32),
            pltpu.VMEM((clips, rows, heads * unit), BF),
            dma((2, outers)),
            dma((2, outers, 3)),
            dma((2, clips)),
            dma((2, clips)),
            dma((2,)),
            dma((2, outers)),
            dma((2, clips)),
            dma((2, outers)),
            dma((2, outers)),
            dma((2, outers)),
            pltpu.SemaphoreType.DMA,
        ],
        compiler_params=pltpu.CompilerParams(
            collective_id=1, has_side_effects=True, vmem_limit_bytes=VMEM_LIMIT
        ),
        name="project_and_attend",
    )(*operands)
    return (results[0].reshape(model, wide),) + tuple(results[1:])


def project_local_kernel(x, x_peer, weight, gain, shift, bias, packed, normed):
    normed[...] = jnp.zeros_like(normed)
    each(0, x.shape[0], lambda index: norm_rows(x, index, gain, shift, normed, 0))
    each(0, x.shape[0], lambda index: norm_rows(x_peer, index, gain, shift, normed, HALF))
    project_rows(normed, weight[...], bias, packed)


def swap(value, axis):
    return lax.ppermute(value, axis, [(0, 1), (1, 0)])


def padded_heads(value, unit):
    value = value.reshape(value.shape[0], 3, 2, -1, unit)
    value = jnp.pad(value, ((0, 0),) * 4 + ((0, LANES - unit),))
    return value.transpose(2, 0, 1, 3, 4).reshape(2, value.shape[0], -1)


def project_plain(
    x, attn, gain, shift, attn_shift, cached, old, squeeze, proj, up, down, clip_count, unit
):
    clips, rows, model = x.shape
    _, shard_rows, head_width = attn.shape
    heads = head_width // (2 * unit)
    width = 3 * heads * LANES
    outers = clip_count // 2
    rest_shape = (shard_rows, proj.shape[1] + up.shape[1] + down.shape[1])
    out = jax.ShapeDtypeStruct
    dma = pltpu.SemaphoreType.DMA
    vmem = pl.BlockSpec(memory_space=pltpu.VMEM)
    shapes = [out((clips, QROWS, width), BF), out((clips, QROWS, model), BF)]
    frame = lax.axis_index("frame")
    shards = padded_heads(attn.transpose(1, 0, 2), unit)
    full = lax.all_gather(shards, ("clip", "frame"), axis=1, tiled=True)
    full = lax.dynamic_index_in_dim(full, frame, 0, keepdims=False)
    bias = padded_heads(attn_shift[None], unit)
    bias = lax.dynamic_index_in_dim(bias, frame, 0, keepdims=False)
    steps = squeeze.shape[1]
    wide = cached.astype(F32).reshape(clips, steps, CELLS, 2, head_width)
    tiled = jnp.tile(squeeze, (1, 1, 2 * heads))
    mem = sum(wide[:, step] * tiled[:, step] for step in range(steps)).astype(BF)
    mem = jnp.stack([mem, old.reshape(mem.shape)], axis=1)
    mem = jnp.pad(mem, ((0, 0), (0, 0), (0, MEM_STEP - CELLS), (0, 0), (0, 0)))
    pieces = mem.reshape(clips, 2 * MEM_STEP, 2, 2, heads * unit)
    mem_own = lax.dynamic_index_in_dim(pieces, frame, 3, keepdims=False)
    mem_send = lax.dynamic_index_in_dim(pieces, 1 - frame, 3, keepdims=False)
    mem_own = mem_own.reshape(clips, -1, head_width)
    mem_peer = swap(mem_send.reshape(clips, -1, head_width), "frame")
    packed, normed = pl.pallas_call(
        project_local_kernel,
        in_specs=[vmem] * 6,
        out_specs=[vmem] * 2,
        out_shape=shapes,
        compiler_params=pltpu.CompilerParams(vmem_limit_bytes=VMEM_LIMIT),
        name="project_local",
    )(x, swap(x, "frame"), full, gain, shift, bias)
    rest = jnp.concatenate([proj, up, down], axis=1)
    column = lax.all_gather(rest, ("clip", "frame"), axis=0, tiled=False)
    column = column.reshape((outers, 4) + rest.shape)
    place = lax.axis_index("clip") % 2 * 2 + frame
    column = lax.dynamic_index_in_dim(column, place, 1, keepdims=False)
    return full, packed, normed, mem_own, mem_peer, column


def device_of(outer, inner, frame, head):
    return (outer * 2 + inner, frame, head)


def plane_peer(inner, frame, step):
    return (inner + step // 2) % 2, (frame + step % 2) % 2


def row_piece(value, row):
    return value[:, row * LANES : (row + 1) * LANES]


def tail_kernel(
    row_own, row_recv, x, middle_grad, grads, joined_sum, gain, taps, pool_gain, pool_shift,
    bias_grad, hot, space_hot, cached, mem_own, mem_recv, vectors, up_bias, rest,
    grad_in, out, rest_out, small_out,
    near, part, far, small, pair_in, plane_in, line_in, row_full, rest_in,
    cross_sems, near_sems, far_sems, pair_sems, plane_sems, line_sems, rest_sems,
    *, unit, plan, table_rows,
):
    chunks, outers, _, shard_rows, cols = part.shape
    clips, rows, model = x.shape
    half = model // 2
    clip = lax.axis_index("clip")
    frame = lax.axis_index("frame")
    head = lax.axis_index("head")
    outer, inner = clip // 2, clip % 2
    place = inner * 2 + frame
    barrier = pltpu.get_barrier_semaphore()
    partner = (clip, frame, 1 - head)

    def line_device(step):
        return device_of((outer + step) % outers, inner, frame, head)

    def plane_device(step):
        there_inner, there_frame = plane_peer(inner, frame, step)
        return device_of(outer, there_inner, there_frame, head)

    def plane_place(step):
        there_inner, there_frame = plane_peer(inner, frame, step)
        return there_inner * 2 + there_frame

    def greet(device):
        pl.semaphore_signal(barrier, inc=1, device_id=device, device_id_type=MESH_ID)

    each(1, outers, lambda step: greet(line_device(step)))
    for step in range(1, 4):
        greet(plane_device(step))
    greet(partner)

    def move(source, target, sems, device):
        return pltpu.make_async_remote_copy(
            src_ref=source, dst_ref=target, send_sem=sems[0], recv_sem=sems[1],
            device_id=device, device_id_type=MESH_ID,
        )

    def pair_sum():
        return move(
            small.at[1 - head], pair_in, (pair_sems.at[0, 0], pair_sems.at[1, 0]), partner
        )

    def plane_sum(step):
        sems = (plane_sems.at[0, 0, step - 1], plane_sems.at[1, 0, step - 1])
        source = small.at[head, plane_place(step)]
        return move(source, plane_in.at[step - 1], sems, plane_device(step))

    def line_sum(step):
        sems = (line_sems.at[0, 0, step], line_sems.at[1, 0, step])
        source = small.at[head, place, (outer + step) % outers]
        return move(source, line_in.at[step], sems, line_device(step))

    def line_share(step, at):
        sems = (line_sems.at[0, 1, step], line_sems.at[1, 1, step])
        block = small_out.at[head, place, at]
        return move(block, block, sems, line_device(step))

    def plane_share(step, at):
        sems = (plane_sems.at[0, 1, step - 1], plane_sems.at[1, 1, step - 1])
        block = small_out.at[head, at]
        return move(block, block, sems, plane_device(step))

    def pair_share(at):
        block = small_out.at[at]
        return move(block, block, (pair_sems.at[0, 1], pair_sems.at[1, 1]), partner)

    def near_copy(chunk, step):
        there_inner, there_frame = plane_peer(inner, frame, step)
        return pltpu.make_async_remote_copy(
            src_ref=grads.at[:, there_inner * 2 + there_frame, :, pl.ds(chunk * cols, cols)],
            dst_ref=near.at[chunk, step - 1],
            send_sem=near_sems.at[0, chunk, step - 1], recv_sem=near_sems.at[1, chunk, step - 1],
            device_id=device_of(outer, there_inner, there_frame, head), device_id_type=MESH_ID,
        )

    def far_copy(chunk, step):
        there = (outer + step) % outers
        return pltpu.make_async_remote_copy(
            src_ref=part.at[chunk, there], dst_ref=far.at[chunk, step],
            send_sem=far_sems.at[0, chunk, step], recv_sem=far_sems.at[1, chunk, step],
            device_id=device_of(there, inner, frame, head), device_id_type=MESH_ID,
        )

    def cross_copy(index, side):
        lanes = pl.ds(pl.multiple_of(side * half, LANES), half)
        return pltpu.make_async_remote_copy(
            src_ref=row_full.at[index, :, lanes], dst_ref=row_full.at[index, :, lanes],
            send_sem=cross_sems.at[0, index], recv_sem=cross_sems.at[1, index],
            device_id=(clip, frame, 1 - head), device_id_type=MESH_ID,
        )

    def rest_copy(step):
        there = (outer + step) % outers
        return pltpu.make_async_remote_copy(
            src_ref=rest.at[there], dst_ref=rest_in.at[step],
            send_sem=rest_sems.at[0, step], recv_sem=rest_sems.at[1, step],
            device_id=device_of(there, inner, frame, head), device_id_type=MESH_ID,
        )

    small[...] = jnp.zeros_like(small)
    pl.semaphore_wait(barrier, outers - 1 + 4)
    for chunk in range(chunks):
        for step in range(1, 4):
            near_copy(chunk, step).start()
    lanes_here = pl.ds(pl.multiple_of(head * half, LANES), half)

    def join(index):
        total = row_own[index].astype(F32) + row_recv[index].astype(F32)
        row_full[index, :, lanes_here] = total.astype(BF)
        cross_copy(index, head).start()

    each(0, clips, join)
    each(1, outers, lambda step: rest_copy(step).start())

    rows_small = small.shape[3]

    def put(row, value):
        count = value.shape[0]
        done = 0
        while done < count:
            block, offset = divmod(row + done, rows_small)
            size = min(count - done, rows_small - offset)
            at = (block // (4 * outers), block // outers % 4, block % outers)
            small[at[0], at[1], at[2], offset : offset + size, : value.shape[1]] = value[
                done : done + size
            ]
            done += size

    def put_wide(row, value):
        for index in range(value.shape[1] // LANES):
            put(row + index, row_piece(value, index))

    wide_rows_count = model // LANES

    joined_rows = joined_sum.shape[1] // LANES
    up_rows = up_bias.shape[1] // LANES
    for which in range(2):

        @pl.when(head == which)
        def _():
            for side in range(2):

                @pl.when(frame == side)
                def _():
                    put_wide(plan["joined"] + (2 * which + side) * joined_rows, joined_sum[...])

            put_wide(plan["up"] + which * up_rows, up_bias[...])

    heads = taps.shape[2] // (3 * LANES)
    tap_sum = jnp.sum(taps[...], axis=1)
    for member in range(3):
        totals = []
        for value in (tap_sum, pool_gain[...], pool_shift[...]):
            total = row_piece(value, member * heads)
            for index in range(1, heads):
                total = total + row_piece(value, member * heads + index)
            totals.append(total)
        put(plan["taps"] + member * 27, totals[0])
        put(plan["pool_gain"] + member, totals[1])
        put(plan["pool_shift"] + member, totals[2])
    heads_here = joined_sum.shape[1] // (3 * LANES)
    for side in range(2):

        @pl.when(frame == side)
        def _():
            for member in range(2):
                totals = [jnp.zeros((1, unit), F32) for _ in range(FRAMES // MEMF)]
                for index in range(clips):
                    for which, part in ((side, mem_own), (1 - side, mem_recv)):
                        for spot in range(heads_here):
                            at = (member * heads_here + spot) * LANES
                            value = part[index, :CELLS, at : at + unit].astype(F32)
                            at = ((2 * member + which) * heads_here + spot) * unit
                            for step in range(len(totals)):
                                rows_here = cached[
                                    index, step * CELLS : (step + 1) * CELLS, at : at + unit
                                ]
                                product = rows_here.astype(F32) * value
                                totals[step] = totals[step] + jnp.sum(
                                    product, axis=0, keepdims=True
                                )
                for step in range(len(totals)):
                    put(plan["squeeze"] + member * len(totals) + step, totals[step])

    time_sum = jnp.zeros((hot.shape[2], LANES), F32)
    bias_sum = jnp.zeros((BIAS_COLS, LANES), F32)
    for index in range(clips):
        value = bias_grad[index]
        bias_sum = bias_sum + value
        value = value[: hot.shape[1]]
        high = value.astype(BF)
        low = (value - high.astype(F32)).astype(BF)
        time_sum = time_sum + dot_f32(hot[index], high, ((0,), (0,)))
        time_sum = time_sum + dot_f32(hot[index], low, ((0,), (0,)))
    put(plan["time"], time_sum[:table_rows])
    high = bias_sum.astype(BF)
    low = (bias_sum - high.astype(F32)).astype(BF)
    space_sum = dot_f32(space_hot[...], high, ((1,), (0,)))
    space_sum = space_sum + dot_f32(space_hot[...], low, ((1,), (0,)))
    put(plan["space"], space_sum[: 2 * (2 * SIDE - 1)])

    gain_sum = jnp.zeros((1, model), F32)
    shift_sum = jnp.zeros((1, model), F32)
    for index in range(clips):
        cross_copy(index, 1 - head).wait_recv()
        incoming = row_full[index].astype(F32)
        centred, rate = row_stats(x[index].astype(F32))
        normal = centred * rate
        product = incoming * normal
        gain_sum = gain_sum + jnp.sum(product, axis=0, keepdims=True)
        shift_sum = shift_sum + jnp.sum(incoming, axis=0, keepdims=True)
        scaled = incoming * gain[0:1]
        mean_scaled = jnp.sum(scaled, axis=-1, keepdims=True) * (1.0 / model)
        mean_both = jnp.sum(scaled * normal, axis=-1, keepdims=True) * (1.0 / model)
        result = rate * (scaled - mean_scaled - normal * mean_both) + middle_grad[index]
        grad_in[index] = result.astype(BF)

    @pl.when(head == 0)
    def _():
        put_wide(plan["gain"], gain_sum)
        put_wide(plan["gain"] + wide_rows_count, vectors[0:1])
        put_wide(plan["shift"], shift_sum)
        put_wide(plan["shift"] + wide_rows_count, vectors[1:2])
        put_wide(plan["rows"], vectors[2:3])
        put_wide(plan["rows"] + wide_rows_count, vectors[3:4])

    def reduce_near(chunk):
        lanes = slice(chunk * cols, (chunk + 1) * cols)
        for step in range(1, 4):
            near_copy(chunk, step).wait_recv()

        def gathered(index):
            own = grads[index, place, :, lanes].astype(F32)
            own = own + near[chunk, 1, index].astype(F32)
            other = near[chunk, 0, index].astype(F32) + near[chunk, 2, index].astype(F32)
            return own, other

        def send(step):
            there = (outer + step) % outers
            own, other = gathered(there)
            part[chunk, there, 0] = own.astype(BF)
            part[chunk, there, 1] = other.astype(BF)
            far_copy(chunk, step).start()

        each(1, outers, send)
        own, other = gathered(outer)
        far[chunk, 0, 0] = own.astype(BF)
        far[chunk, 0, 1] = other.astype(BF)

    pair_sum().start()
    reduce_near(0)
    pair_sum().wait_recv()
    small[head] = small[head] + pair_in[...]
    for step in range(1, 4):
        plane_sum(step).start()
    for chunk in range(1, chunks):
        reduce_near(chunk)
    for step in range(1, 4):
        plane_sum(step).wait_recv()
    small[head, place] = small[head, place] + plane_in[0] + plane_in[1] + plane_in[2]
    each(1, outers, lambda step: line_sum(step).start())
    each(1, outers, lambda step: rest_copy(step).wait_recv())
    rest_out[...] = lax.fori_loop(
        1,
        outers,
        lambda step, sums: sums + rest_in[step].astype(F32),
        rest[outer].astype(F32),
    )
    each(1, outers, lambda step: line_sum(step).wait_recv())
    small_out[head, place, outer] = lax.fori_loop(
        1, outers, lambda step, sums: sums + line_in[step], small[head, place, outer]
    )
    each(1, outers, lambda step: line_share(step, outer).start())
    each(1, outers, lambda step: line_share(step, (outer + outers - step) % outers).wait_recv())
    for step in range(1, 4):
        plane_share(step, place).start()
    heads = cols // LANES
    group = heads * unit
    for chunk in range(chunks):
        each(1, outers, lambda step: far_copy(chunk, step).wait_recv())
        totals = []
        for side in range(2):
            totals.append(
                lax.fori_loop(
                    0,
                    outers,
                    lambda step, sums: sums + far[chunk, step, side].astype(F32),
                    jnp.zeros((shard_rows, cols), F32),
                )
            )

        def store(order):
            for spot, side in enumerate(order):
                for index in range(heads):
                    at = (2 * chunk + spot) * group + index * unit
                    value = totals[side][:, index * LANES : index * LANES + unit]
                    out[:, at : at + unit] = value

        @pl.when(frame == 0)
        def _():
            store((0, 1))

        @pl.when(frame == 1)
        def _():
            store((1, 0))

    for step in range(1, 4):
        plane_share(step, plane_place(step)).wait_recv()
    pair_share(head).start()
    pair_share(1 - head).wait_recv()
    pair_sum().wait_send()
    pair_share(head).wait_send()
    for step in range(1, 4):
        plane_sum(step).wait_send()
        plane_share(step, place).wait_send()
    each(1, outers, lambda step: line_sum(step).wait_send())
    each(1, outers, lambda step: line_share(step, outer).wait_send())
    each(1, outers, lambda step: rest_copy(step).wait_send())
    for index in range(clips):
        cross_copy(index, head).wait_send()
    for chunk in range(chunks):
        for step in range(1, 4):
            near_copy(chunk, step).wait_send()
        each(1, outers, lambda step: far_copy(chunk, step).wait_send())


def unpack_kernel(
    small, qkv, early, late, grad_in, block_out,
    grad_in_out, block_out_out, gain_out, shift_out, rows_out, joined_out, up_out, taps_out,
    pool_gain_out, pool_shift_out, squeeze_out, time_out, space_out, qkv_out, proj_out,
    up_grad_out, down_out, time_rows, *, plan, unit,
):
    for index in range(grad_in.shape[0]):
        grad_in_out[index] = grad_in[index]
        block_out_out[index] = block_out[index]
    head = lax.axis_index("head")
    rows_small = small.shape[1]

    def take(row, target):
        count = target.shape[0]
        done = 0
        while done < count:
            block, offset = divmod(row + done, rows_small)
            size = min(count - done, rows_small - offset)
            target[done : done + size] = small[block, offset : offset + size, : target.shape[1]]
            done += size

    def take_wide(row, target, at):
        for index in range(target.shape[1] // LANES):
            block, offset = divmod(row + index, rows_small)
            target[at : at + 1, index * LANES : (index + 1) * LANES] = small[
                block, offset : offset + 1
            ]

    per_row = gain_out.shape[1] // LANES
    for index in range(2):
        take_wide(plan["gain"] + index * per_row, gain_out, index)
        take_wide(plan["shift"] + index * per_row, shift_out, index)
        take_wide(plan["rows"] + index * per_row, rows_out, index)
    width = joined_out.shape[1]
    group = width // 2
    heads = group // unit
    joined_rows = 3 * heads
    up_rows = up_out.shape[0]
    for which in range(2):

        @pl.when(head == which)
        def _():
            for member in range(3):
                for side in range(2):
                    for index in range(heads):
                        row = plan["joined"] + (2 * which + side) * joined_rows
                        block, offset = divmod(row + member * heads + index, rows_small)
                        at = side * group + index * unit
                        joined_out[member : member + 1, at : at + unit] = small[
                            block, offset : offset + 1, :unit
                        ]
            take(plan["up"] + which * up_rows, up_out)

    for member in range(3):
        take(plan["taps"] + member * 27, taps_out.at[member])
        qkv_out[member] = qkv[:, member * width : (member + 1) * width]
    take(plan["pool_gain"], pool_gain_out)
    take(plan["pool_shift"], pool_shift_out)
    take(plan["time"], time_rows)
    time_out[...] = time_rows[...].T
    for index in range(2):
        count = squeeze_out.shape[1]
        take(plan["squeeze"] + index * count, squeeze_out.at[index])
        for spot in range(space_out.shape[0]):
            block, offset = divmod(
                plan["space"] + index * space_out.shape[0] + spot, rows_small
            )
            space_out[spot, index : index + 1] = small[block, offset : offset + 1, :unit]
    proj_width, up_width = proj_out.shape[1], up_grad_out.shape[1]
    proj_out[...] = early[:, :proj_width]
    up_grad_out[...] = early[:, proj_width : proj_width + up_width]
    at = proj_width + up_width
    first = early.shape[1] - at
    down_out[:, :first] = early[:, at:]
    down_out[:, first:] = late[...]


def unpack(small, qkv, early, late, grad_in, block_out, plan, unit, hidden_width, table_rows):
    shard_rows, width = qkv.shape
    model = grad_in.shape[2]
    rest_width = early.shape[1] + late.shape[1]
    out = jax.ShapeDtypeStruct
    vmem = pl.BlockSpec(memory_space=pltpu.VMEM)
    shapes = [
        out(grad_in.shape, BF),
        out(block_out.shape, BF),
        out((2, model), F32),
        out((2, model), F32),
        out((2, model), F32),
        out((3, width // 3), F32),
        out((hidden_width // LANES, LANES), F32),
        out((3, 27, unit), F32),
        out((3, unit), F32),
        out((3, unit), F32),
        out((2, FRAMES // MEMF, unit), F32),
        out((unit, table_rows), F32),
        out((2 * SIDE - 1, 2, unit), F32),
        out((3, shard_rows, width // 3), F32),
        out((shard_rows, rest_width - 2 * hidden_width), F32),
        out((shard_rows, hidden_width), F32),
        out((shard_rows, hidden_width), F32),
    ]
    return pl.pallas_call(
        partial(unpack_kernel, plan=plan, unit=unit),
        in_specs=[vmem] * 6,
        out_specs=[vmem] * len(shapes),
        out_shape=shapes,
        scratch_shapes=[pltpu.VMEM((table_rows, unit), F32)],
        compiler_params=pltpu.CompilerParams(vmem_limit_bytes=VMEM_LIMIT),
        name="unpack_results",
    )(small, qkv, early, late, grad_in, block_out)


def tail(
    row_own, row_recv, x, middle_grad, grads, joined_sum, gain, taps, pool_gain, pool_shift,
    bias_grad, hot, space_hot, cached, mem_own, mem_recv, vectors, up_bias, rest, clip_count, devices,
    unit, table_rows,
):
    clips, rows, model = x.shape
    wide = grads.shape[3]
    heads = wide // (3 * LANES)
    width = 3 * 2 * heads * unit
    outers = clip_count // 2
    shard_rows = model // (4 * outers)
    chunks = 3
    cols = wide // chunks
    plan = {}
    at = 0
    for name, count in (
        ("gain", 2 * model // LANES),
        ("shift", 2 * model // LANES),
        ("rows", 2 * model // LANES),
        ("joined", 4 * wide // LANES),
        ("up", 2 * up_bias.shape[1] // LANES),
        ("taps", 81),
        ("pool_gain", 3),
        ("pool_shift", 3),
        ("squeeze", 2 * FRAMES // MEMF),
        ("time", table_rows),
        ("space", 2 * (2 * SIDE - 1)),
    ):
        plan[name] = at
        at += count
    block = -(-at // (devices * 8)) * 8
    small_shape = (2, 4, outers, block, LANES)
    out = jax.ShapeDtypeStruct
    dma = pltpu.SemaphoreType.DMA
    vmem = pl.BlockSpec(memory_space=pltpu.VMEM)
    shapes = [
        out((clips, rows, model), BF),
        out((shard_rows, width), F32),
        out((shard_rows, rest.shape[2]), F32),
        out(small_shape, F32),
    ]
    results = pl.pallas_call(
        partial(tail_kernel, unit=unit, plan=plan, table_rows=table_rows),
        in_specs=[vmem] * 19,
        out_specs=[vmem] * len(shapes),
        out_shape=shapes,
        scratch_shapes=[
            pltpu.VMEM((chunks, 3, outers, shard_rows, cols), BF),
            pltpu.VMEM((chunks, outers, 2, shard_rows, cols), BF),
            pltpu.VMEM((chunks, outers, 2, shard_rows, cols), BF),
            pltpu.VMEM(small_shape, F32),
            pltpu.VMEM(small_shape[1:], F32),
            pltpu.VMEM((3,) + small_shape[2:], F32),
            pltpu.VMEM(small_shape[2:], F32),
            pltpu.VMEM((clips, rows, model), BF),
            pltpu.VMEM(rest.shape, BF),
            dma((2, clips)),
            dma((2, chunks, 3)),
            dma((2, chunks, outers)),
            dma((2, 2)),
            dma((2, 2, 3)),
            dma((2, 2, outers)),
            dma((2, outers)),
        ],
        compiler_params=pltpu.CompilerParams(
            collective_id=0, has_side_effects=True, vmem_limit_bytes=VMEM_LIMIT
        ),
        name="tail_gradients",
    )(
        row_own, row_recv, x, middle_grad, grads, joined_sum, gain, taps, pool_gain, pool_shift,
        bias_grad, hot, space_hot, cached, mem_own, mem_recv, vectors, up_bias, rest,
    )
    return results, plan


def feed_kernel(
    att_own, att_recv, x, cot, weights, gain, shift, out_shift, up_shift,
    block_out, middle_grad, grad_own, grad_send, grad_rest, vectors, up_bias,
    attended, normed, cots, active, hidden_low, branch, middle, send, recv, sems,
):
    clips, rows, model = x.shape
    span = attended.shape[0] // clips
    group = att_own.shape[2]
    head_width = 2 * group
    hidden_width = up_shift.shape[1]
    tiles = 4
    tile = hidden_width // tiles
    clip_at = lax.axis_index("clip")
    frame = lax.axis_index("frame")
    head = lax.axis_index("head")
    partner = (clip_at, frame, 1 - head)

    def cross(kind, index):
        return pltpu.make_async_remote_copy(
            src_ref=send.at[kind, index], dst_ref=recv.at[kind, index],
            send_sem=sems.at[0, kind, index], recv_sem=sems.at[1, kind, index],
            device_id=partner, device_id_type=MESH_ID,
        )

    barrier = pltpu.get_barrier_semaphore()
    pl.semaphore_signal(barrier, inc=1, device_id=partner, device_id_type=MESH_ID)
    for ref in (attended, normed, cots, branch):
        ref[...] = jnp.zeros_like(ref)

    def assemble(low, high):
        for index in range(clips):
            at = slice(index * span, index * span + rows)
            attended[at, :group] = low[index]
            attended[at, group:] = high[index]

    @pl.when(frame == 0)
    def _():
        assemble(att_own, att_recv)

    @pl.when(frame == 1)
    def _():
        assemble(att_recv, att_own)

    for index in range(clips):
        cots[index * span : index * span + rows] = cot[index]
    pl.semaphore_wait(barrier, 1)

    def block_rows(index):
        return pl.ds(pl.multiple_of(index * span, 16), span)

    def project(index):
        part = dot_f32(attended[block_rows(index)], weights[:, :head_width], ((1,), (1,)))
        send[0, index] = part[:rows].astype(BF)
        cross(0, index).start()

    each(0, clips, project)

    def feed(index, bias_sum):
        cross(0, index).wait_recv()
        branch_rows = send[0, index].astype(F32) + recv[0, index].astype(F32)
        value = x[index].astype(F32) + branch_rows + out_shift[0:1]
        middle[index] = value
        centred, rate = row_stats(value)
        low = (centred * rate * gain[1:2] + shift[1:2]).astype(BF)
        at = pl.multiple_of(index * span, 16)
        normed[pl.ds(at, rows)] = low
        low = normed[block_rows(index)]
        cot_rows = cots[block_rows(index)]
        out_part = jnp.zeros((span, model), F32)
        norm_part = jnp.zeros((span, model), F32)
        sums = []
        for step in range(tiles):
            lanes = slice(step * tile, (step + 1) * tile)
            up = weights[:, head_width + step * tile : head_width + (step + 1) * tile]
            at = head_width + hidden_width + step * tile
            down = weights[:, at : at + tile]
            hidden = dot_f32(low, up, ((1,), (0,))) + up_shift[:, lanes]
            incoming = dot_f32(cot_rows, down, ((1,), (0,)))
            normal = 0.5 * (1.0 + lax.erf(hidden * (0.5**0.5)))
            density = jnp.exp(hidden * hidden * -0.5) * ((2.0 * np.pi) ** -0.5)
            acted = (hidden * normal).astype(BF)
            back = (incoming * (normal + hidden * density)).astype(BF)
            active[block_rows(index), lanes] = acted
            hidden_low[block_rows(index), lanes] = back
            sums.append(jnp.sum(back.astype(F32), axis=0, keepdims=True))
            out_part = out_part + dot_f32(acted, down, ((1,), (1,)))
            norm_part = norm_part + dot_f32(back, up, ((1,), (1,)))
        send[1, index] = norm_part[:rows].astype(BF)
        cross(1, index).start()
        send[2, index] = out_part[:rows].astype(BF)
        cross(2, index).start()
        return bias_sum + jnp.concatenate(sums, axis=1)

    up_bias[...] = lax.fori_loop(0, clips, feed, jnp.zeros((1, hidden_width), F32))

    wide = hidden_width // 2
    for step in range(2):
        lanes = slice(step * wide, (step + 1) * wide)
        value = dot_f32(normed[...], hidden_low[:, lanes], ((0,), (0,)))
        at = head_width + step * wide
        grad_rest[:, at : at + wide] = value.astype(BF)
        value = dot_f32(cots[...], active[:, lanes], ((0,), (0,)))
        at = head_width + hidden_width + step * wide
        grad_rest[:, at : at + wide] = value.astype(BF)

    def back(index, sums):
        gain_sum, shift_sum, first_sum, second_sum = sums
        cross(1, index).wait_recv()
        incoming = send[1, index].astype(F32) + recv[1, index].astype(F32)
        centred, rate = row_stats(middle[index])
        normal = centred * rate
        scaled = incoming * gain[1:2]
        mean_scaled = jnp.sum(scaled, axis=-1, keepdims=True) * (1.0 / model)
        mean_both = jnp.sum(scaled * normal, axis=-1, keepdims=True) * (1.0 / model)
        cot_rows = cot[index].astype(F32)
        value = cot_rows + rate * (scaled - mean_scaled - normal * mean_both)
        middle_grad[index] = value
        at = pl.multiple_of(index * span, 16)
        branch[pl.ds(at, rows)] = value.astype(BF)
        part = dot_f32(branch[block_rows(index)], weights[:, :head_width], ((1,), (0,)))
        part = part[:rows].astype(BF)

        @pl.when(frame == 0)
        def _():
            grad_own[index] = part[:, :group]
            grad_send[index] = part[:, group:]

        @pl.when(frame == 1)
        def _():
            grad_send[index] = part[:, :group]
            grad_own[index] = part[:, group:]

        cross(2, index).wait_recv()
        out_rows = send[2, index].astype(F32) + recv[2, index].astype(F32)
        block_out[index] = (middle[index] + out_rows + out_shift[1:2]).astype(BF)

        def column(rows_here):
            return jnp.sum(rows_here, axis=0, keepdims=True)

        return (
            gain_sum + column(incoming * normal),
            shift_sum + column(incoming),
            first_sum + column(value),
            second_sum + column(cot_rows),
        )

    start = tuple(jnp.zeros((1, model), F32) for _ in range(4))
    sums = lax.fori_loop(0, clips, back, start)
    for row in range(4):
        vectors[row : row + 1] = sums[row]
    value = dot_f32(branch[...], attended[...], ((0,), (0,)))
    grad_rest[:, :head_width] = value.astype(BF)
    for kind in range(3):
        each(0, clips, lambda index: cross(kind, index).wait_send())


def feed(att_own, att_recv, x, cot, weights, gain, shift, out_shift, up_shift):
    clips, rows, model = x.shape
    group = att_own.shape[2]
    hidden_width = up_shift.shape[1]
    span = -(-rows // 16) * 16
    out = jax.ShapeDtypeStruct
    vmem = pl.BlockSpec(memory_space=pltpu.VMEM)
    shapes = [
        out((clips, rows, model), BF),
        out((clips, rows, model), F32),
        out((clips, rows, group), BF),
        out((clips, rows, group), BF),
        out(weights.shape, BF),
        out((4, model), F32),
        out((1, hidden_width), F32),
    ]
    return pl.pallas_call(
        feed_kernel,
        in_specs=[vmem] * 9,
        out_specs=[vmem] * len(shapes),
        out_shape=shapes,
        scratch_shapes=[
            pltpu.VMEM((clips * span, 2 * group), BF),
            pltpu.VMEM((clips * span, model), BF),
            pltpu.VMEM((clips * span, model), BF),
            pltpu.VMEM((clips * span, hidden_width), BF),
            pltpu.VMEM((clips * span, hidden_width), BF),
            pltpu.VMEM((clips * span, model), BF),
            pltpu.VMEM((clips, rows, model), F32),
            pltpu.VMEM((3, clips, rows, model), BF),
            pltpu.VMEM((3, clips, rows, model), BF),
            pltpu.SemaphoreType.DMA((2, 3, clips)),
        ],
        compiler_params=pltpu.CompilerParams(
            collective_id=4, has_side_effects=True, vmem_limit_bytes=VMEM_LIMIT
        ),
        name="feed_forward_both_ways",
    )(att_own, att_recv, x, cot, weights, gain, shift, out_shift, up_shift)


def precise(pattern, *operands):
    return jnp.einsum(pattern, *operands, precision=lax.Precision.HIGHEST)


def split_groups(value, which, axis):
    half = value.shape[axis] // 2
    low = lax.slice_in_dim(value, 0, half, axis=axis)
    high = lax.slice_in_dim(value, half, None, axis=axis)
    first = which == 0
    return jnp.where(first, low, high), jnp.where(first, high, low)


def join_groups(own, peer, which, axis):
    first = which == 0
    return jnp.concatenate([jnp.where(first, own, peer), jnp.where(first, peer, own)], axis=axis)


def time_choices(stride_group, memory_place, which, own, table_rows):
    local = jnp.arange(own, dtype=jnp.int32)
    times = jnp.concatenate([which * own + local, (1 - which) * own + local])
    stride = jnp.left_shift(jnp.int32(2), stride_group)[:, None, None]
    offset = 8 * (FRAMES - 1)
    current = stride * (times[None, :, None] - times[None, None, :]) + offset
    slots = [memory_place[:, index : index + 1] for index in range(4)]
    first = jnp.concatenate([slots[2], slots[0], slots[3], slots[1]], axis=1)
    second = jnp.concatenate([slots[3], slots[1], slots[2], slots[0]], axis=1)
    places = jnp.where(which == 0, first, second)
    memory = stride * times[None, :, None] + places[:, None, :] + offset
    chosen = jnp.concatenate([current, memory], axis=2)
    return (chosen[..., None] == jnp.arange(table_rows, dtype=jnp.int32)).astype(F32)


def space_choices():
    places = np.arange(SIDE)
    offsets = places[:, None] - places[None, :] + SIDE - 1
    hot = offsets.reshape(-1)[:, None] == np.arange(2 * SIDE - 1)[None, :]
    return jnp.asarray(hot.astype(np.float32))


def space_sums():
    spans = 2 * SIDE - 1
    hot = np.zeros((32, BIAS_COLS), np.float32)
    for axis in range(2):
        for query in range(SIDE):
            for key in range(SIDE):
                col = SPACE_AT + axis * CELLS + query * SIDE + key
                hot[axis * spans + query - key + SIDE - 1, col] = 1.0
    return hot


def wide_rows(rows, heads):
    count, members, unit = rows.shape
    padded = jnp.pad(rows, ((0, 0), (0, 0), (0, LANES - unit)))
    spread = jnp.broadcast_to(padded[:, :, None], (count, members, heads, LANES))
    return spread.reshape(count, members * heads * LANES)


def local(
    clips_in,
    cached_kv,
    old_memory,
    stride_group,
    memory_place,
    norm_gain,
    norm_shift,
    qkv_weight,
    qkv_shift,
    pool_kernel,
    pool_gain,
    pool_shift,
    squeeze_kernel,
    time_table,
    space_tables,
    proj_weight,
    out_shift,
    up_weight,
    up_shift,
    down_weight,
    cotangent,
):
    clip_count, rows_clip, model_width = clips_in.shape
    head_width = qkv_weight.shape[2]
    unit = pool_gain.shape[1]
    head_count = head_width // unit
    frame_count = lax.axis_size("frame")
    heads = head_count // frame_count
    own_frames = rows_clip // CELLS
    group_width = heads * unit
    group_span = FRAMES // MEMF
    scale = unit ** (-0.5)
    which = lax.axis_index("frame")
    into_np, outof_np = placement(frame_count)
    keys_np, mask_np, pad_np = bias_constants(frame_count)
    consts = (
        jnp.asarray(into_np, BF),
        jnp.asarray(outof_np, BF),
        jnp.asarray(keys_np, BF),
        jnp.asarray(mask_np),
        jnp.asarray(pad_np),
    )

    cached_flat = cached_kv.reshape(clip_count, rows_clip, 2 * head_width)
    time_hot = time_choices(stride_group, memory_place, which, own_frames, time_table.shape[0])
    time_rows = precise("ctkr,rd->ctkd", time_hot, time_table).reshape(clip_count, -1, unit)
    space_hot = space_choices()
    space_rows = precise("pr,xrd->xpd", space_hot, space_tables).reshape(2 * CELLS, unit)
    space_rows = jnp.broadcast_to(space_rows[None], (clip_count,) + space_rows.shape)
    bias = jnp.concatenate(
        [
            jnp.pad(time_rows, ((0, 0), (0, SPACE_AT - time_rows.shape[1]), (0, LANES - unit))),
            jnp.pad(
                space_rows,
                ((0, 0), (0, BIAS_COLS - SPACE_AT - 2 * CELLS), (0, LANES - unit)),
            ),
        ],
        axis=1,
    )
    bias = bias * (1.0 / scale)
    inputs = (
        clips_in, qkv_weight.transpose(1, 0, 2), norm_gain, norm_shift, qkv_shift, cached_flat,
        old_memory.reshape(clip_count, -1, 2 * head_width), squeeze_kernel, proj_weight.T, up_weight,
        down_weight.T,
    )
    clip_axis = lax.axis_size("clip")
    if qkv_weight.shape[0] % 16:
        attn_group, packed, normed, mem_own, mem_peer, column = project_plain(
            *inputs, clip_axis, unit
        )
        forward = attention_forward(
            packed, mem_own, mem_peer, column, consts, pool_kernel, pool_gain, pool_shift, bias,
            scale, unit, rows_clip,
        )
    else:
        attn_group, packed, normed, *forward = front(
            *inputs, consts, pool_kernel, pool_gain, pool_shift, bias, scale, clip_axis, unit
        )
    attended_own, attended_peer, rest_full = forward[:3]
    rest_full = rest_full.reshape(model_width, -1)
    saved = forward[3:]
    block_out, middle_grad, attended_grad_own, attended_grad_send, grad_rest, vectors, up_grads = (
        feed(
            attended_own, attended_peer, clips_in, cotangent, rest_full, norm_gain,
            norm_shift, out_shift, up_shift.reshape(1, -1),
        )
    )
    outers = lax.axis_size("clip") // 2
    grad_rest = grad_rest.reshape(outers, 4, -1, grad_rest.shape[1])
    backward = attention_backward(
        packed, normed, attn_group, attended_grad_own, attended_grad_send, grad_rest, consts,
        pool_kernel, pool_gain, bias, saved, scale, unit,
    )
    row_own, row_recv, mem_grad_own, mem_grad_peer = backward[:4]
    taps_grad, pool_gain_grad, pool_shift_grad, bias_grad = backward[4:8]
    attn_grad, joined_grad, rest_part, rest_early = backward[8:]

    time_count = time_rows.shape[1]
    hot = time_hot.reshape(clip_count, time_count, -1).astype(BF)
    hot = jnp.pad(hot, ((0, 0), (0, 0), (0, -hot.shape[2] % LANES)))
    devices = lax.axis_size("clip") * frame_count * lax.axis_size("head")
    (grad_in, qkv_shard, rest_late, small), plan = tail(
        row_own, row_recv, clips_in, middle_grad,
        attn_grad.reshape(outers, 4, -1, attn_grad.shape[1]), joined_grad, norm_gain, taps_grad,
        pool_gain_grad, pool_shift_grad, bias_grad, hot,
        jnp.asarray(space_sums(), BF), cached_flat, mem_grad_own, mem_grad_peer, vectors,
        up_grads, rest_part, lax.axis_size("clip"), devices, unit, time_table.shape[0],
    )
    (
        grad_in, block_out, gain_sums, shift_sums, out_sums, qkv_bias_sum, up_bias_sum, kernel_sum,
        pool_gain_sum, pool_shift_sum, squeeze_sum, time_sum, space_sum, qkv_shard, proj_shard,
        up_shard, down_shard,
    ) = unpack(
        small.reshape((devices,) + small.shape[3:]), qkv_shard, rest_early, rest_late, grad_in, block_out, plan, unit,
        up_weight.shape[1], time_table.shape[0],
    )
    return (
        block_out,
        grad_in,
        gain_sums,
        shift_sums,
        qkv_shard.transpose(1, 0, 2),
        qkv_bias_sum,
        kernel_sum,
        pool_gain_sum,
        pool_shift_sum,
        squeeze_sum,
        time_sum.T,
        space_sum.transpose(1, 0, 2),
        proj_shard.T,
        out_sums,
        up_shard,
        up_bias_sum.reshape(-1),
        down_shard.T,
    )


def solution(mesh):
    return jax.shard_map(
        local,
        mesh=mesh,
        in_specs=(
            P("clip", "frame", None),
            P("clip", "frame", None, "head"),
            P("clip", "frame", None, "head"),
            P("clip"),
            P("clip", None),
            P(),
            P(),
            P(("clip", "frame"), None, "head"),
            P(None, "head"),
            P(),
            P(),
            P(),
            P(),
            P(),
            P(),
            P("head", ("clip", "frame")),
            P(),
            P(("clip", "frame"), "head"),
            P("head"),
            P("head", ("clip", "frame")),
            P("clip", "frame", None),
        ),
        out_specs=(
            P("clip", "frame", None),
            P("clip", "frame", None),
            P(),
            P(),
            P(("clip", "frame"), None, "head"),
            P(None, "head"),
            P(),
            P(),
            P(),
            P(),
            P(),
            P(),
            P("head", ("clip", "frame")),
            P(),
            P(("clip", "frame"), "head"),
            P("head"),
            P("head", ("clip", "frame")),
        ),
        check_vma=False,
    )
```

```python
from functools import partial

import jax
import jax.numpy as jnp
import numpy as np
from jax import lax
from jax.experimental import pallas as pl
from jax.experimental.pallas import tpu as pltpu
from jax.sharding import PartitionSpec as P

FRAMES = 8
MEMF = 2
SIDE = 7
CELLS = SIDE * SIDE
LANES = 128
HALF = 208
QROWS = 2 * HALF
GRID_ROWS = FRAMES * SIDE * 8
MEM_AT = QROWS
MEM_PAD = 112
MEM_BACK = 64
MEM_STEP = 56
TURN_STEP = 3
TURN_PAIRS = 1
TURN_LAG = 5
KROWS = 640
BIAS_COLS = 256
SPACE_AT = 128
PAD_LANE = 127
BF = jnp.bfloat16
F32 = jnp.float32
VMEM_LIMIT = 60 * 1024 * 1024
MESH_ID = pl.DeviceIdType.MESH


def dot_f32(a, b, dims):
    return lax.dot_general(a, b, (dims, ((), ())), preferred_element_type=F32)


def frame_order(first, own):
    rest = [t for t in range(FRAMES) if not first * own <= t < (first + 1) * own]
    return list(range(first * own, (first + 1) * own)) + rest


def placement(frame_count):
    own = FRAMES // frame_count
    into = np.zeros((frame_count, GRID_ROWS, QROWS), np.float32)
    for first in range(frame_count):
        for slot, frame in enumerate(frame_order(first, own)):
            base = (slot // own) * HALF + (slot % own) * CELLS
            for high in range(SIDE):
                for wide in range(SIDE):
                    row = (frame * SIDE + high) * 8 + wide
                    into[first, row, base + high * SIDE + wide] = 1.0
    return into, np.ascontiguousarray(into.transpose(0, 2, 1))


def bias_constants(frame_count):
    own = FRAMES // frame_count
    frames_all = FRAMES + 2 * MEMF
    keys = np.zeros((BIAS_COLS, KROWS), np.float32)
    valid = np.zeros((KROWS,), bool)

    def mark(col, slot, high, wide):
        valid[col] = True
        for query in range(FRAMES):
            keys[query * frames_all + slot, col] = 1.0
        for place in range(SIDE):
            keys[SPACE_AT + place * SIDE + high, col] = 1.0
            keys[SPACE_AT + CELLS + place * SIDE + wide, col] = 1.0

    mask = np.zeros((QROWS, BIAS_COLS), np.float32)
    for slot in range(FRAMES):
        base = (slot // own) * HALF + (slot % own) * CELLS
        for high in range(SIDE):
            for wide in range(SIDE):
                row = base + high * SIDE + wide
                mark(row, slot, high, wide)
                mask[row, slot * frames_all : (slot + 1) * frames_all] = 1.0
                mask[row, SPACE_AT + high * SIDE : SPACE_AT + (high + 1) * SIDE] = 1.0
                low = SPACE_AT + CELLS + wide * SIDE
                mask[row, low : low + SIDE] = 1.0
    for group in range(2):
        for inner in range(MEMF):
            slot = FRAMES + group * MEMF + inner
            for high in range(SIDE):
                for wide in range(SIDE):
                    col = MEM_AT + group * MEM_PAD + inner * MEM_STEP + high * SIDE + wide
                    mark(col, slot, high, wide)
    keys[PAD_LANE, ~valid] = -1e9
    pad_row = np.zeros((1, BIAS_COLS), np.float32)
    pad_row[0, PAD_LANE] = 1.0
    return keys, mask, pad_row


def spread_heads(source, target, rows_at, units, unit, first=0):
    count = source.shape[0]
    for index in range(units):
        at = (first + index) * unit
        target[rows_at : rows_at + count, index * LANES : index * LANES + unit] = source[
            :, at : at + unit
        ]


def spread_tables(kernel_ref, taps, pairs, heads, unit):
    taps[...] = jnp.zeros_like(taps)
    for _, target in pairs:
        target[...] = jnp.zeros_like(target)
    for member in range(3):
        for index in range(heads):
            at = (member * heads + index) * LANES
            for tap in range(27):
                row = kernel_ref[member, tap : tap + 1]
                taps[tap, :, at : at + unit] = jnp.broadcast_to(row, (8, unit))
            for source, target in pairs:
                target[:, at : at + unit] = source[member : member + 1]


def load_shifted(field, shifted):
    grid = field.reshape(FRAMES, SIDE, 8, field.shape[-1])
    flat = field.reshape(FRAMES * SIDE, 8, field.shape[-1])
    shifted[1, 1 : FRAMES + 1, 1 : SIDE + 1] = grid
    shifted[0, 1 : FRAMES + 1, 1 : SIDE + 1] = pltpu.roll(flat, 1, 1).reshape(grid.shape)
    shifted[2, 1 : FRAMES + 1, 1 : SIDE + 1] = pltpu.roll(flat, 7, 1).reshape(grid.shape)


def convolve(shifted, taps, target, flip):
    tiles = target.shape[-1] // LANES

    def step(pair, carry):
        for sub in range(2):
            frame = pair * 2 + sub
            for tile in range(tiles):
                lanes = slice(tile * LANES, (tile + 1) * LANES)
                total = None
                for i in range(3):
                    for k in range(3):
                        rows = shifted[k, frame + i, :, :, lanes]
                        for j in range(3):
                            if flip:
                                tap = (2 - i) * 9 + (2 - j) * 3 + (2 - k)
                            else:
                                tap = i * 9 + j * 3 + k
                            value = rows[j : j + SIDE] * taps[tap, :, lanes][None]
                            total = value if total is None else total + value
                target[frame, :, :, lanes] = total
        return carry

    lax.fori_loop(0, FRAMES // 2, step, 0)


def tap_grads(shifted, grads, target):
    tiles = target.shape[-1] // LANES

    def step(index, carry):
        lanes = pl.ds(pl.multiple_of(index * LANES, LANES), LANES)

        def inner(frame, sums):
            centre = grads[frame + 1, 1 : SIDE + 1, :, lanes]
            new = []
            for i in range(3):
                for k in range(3):
                    rows = shifted[k, frame + i, :, :, lanes]
                    for j in range(3):
                        parts = [rows[j + high] * centre[high] for high in range(SIDE)]
                        parts.append(sums[len(new)])
                        while len(parts) > 1:
                            pairs = zip(parts[::2], parts[1::2])
                            parts = [left + right for left, right in pairs]
                        new.append(parts[0])
            return tuple(new)

        start = tuple(jnp.zeros((8, LANES), F32) for _ in range(27))
        sums = lax.fori_loop(0, FRAMES, inner, start, unroll=4)
        for i in range(3):
            for k in range(3):
                for j in range(3):
                    target[i * 9 + j * 3 + k, :, lanes] += sums[(i * 3 + k) * 3 + j]
        return carry

    lax.fori_loop(0, tiles, step, 0)


def head_stats(values, unit):
    average = jnp.sum(values, axis=-1, keepdims=True) * (1.0 / unit)
    lane = lax.broadcasted_iota(jnp.int32, values.shape, 1)
    centred = jnp.where(lane < unit, values - average, 0.0)
    variance = jnp.sum(centred * centred, axis=-1, keepdims=True) * (1.0 / unit)
    return centred, lax.rsqrt(variance + 1e-06)


def frame_partner():
    return (lax.axis_index("clip"), 1 - lax.axis_index("frame"), lax.axis_index("head"))


def partner_copy(source, target, send_sem, recv_sem):
    return pltpu.make_async_remote_copy(
        src_ref=source, dst_ref=target, send_sem=send_sem, recv_sem=recv_sem,
        device_id=frame_partner(), device_id_type=MESH_ID,
    )


def side_partner():
    clip = lax.axis_index("clip")
    across = (clip // 2) * 2 + 1 - clip % 2
    return (across, lax.axis_index("frame"), lax.axis_index("head"))


def side_copy(source, target, send_sem, recv_sem):
    return pltpu.make_async_remote_copy(
        src_ref=source, dst_ref=target, send_sem=send_sem, recv_sem=recv_sem,
        device_id=side_partner(), device_id_type=MESH_ID,
    )


def greet_partner():
    barrier = pltpu.get_barrier_semaphore()
    pl.semaphore_signal(barrier, inc=1, device_id=frame_partner(), device_id_type=MESH_ID)
    pl.semaphore_wait(barrier, 1)


def plane_stage(column_ref, rest_full, side_sems, pair_sems, turn_sems, own_sem):
    outers = column_ref.shape[0]
    split = min(TURN_PAIRS, outers)
    outer = lax.axis_index("clip") // 2
    inner = lax.axis_index("clip") % 2
    frame = lax.axis_index("frame")
    place = inner * 2 + frame
    side_place = (1 - inner) * 2 + frame
    pair_place = inner * 2 + 1 - frame
    turn_place = (1 - inner) * 2 + 1 - frame
    own_copy = pltpu.make_async_copy(column_ref, rest_full.at[:, place], own_sem)

    def side_move(at, source, target):
        return side_copy(source, target, side_sems.at[0, at], side_sems.at[1, at])

    def pair_move(at, source, target):
        return partner_copy(source, target, pair_sems.at[0, at], pair_sems.at[1, at])

    def to_side(at):
        return side_move(at, column_ref.at[at], rest_full.at[at, place])

    def to_pair(at):
        return pair_move(at, column_ref.at[at], rest_full.at[at, place])

    def turn_side(at):
        block = rest_full.at[at, pair_place]
        return side_copy(block, block, turn_sems.at[0, at], turn_sems.at[1, at])

    def turn_pair(at):
        block = rest_full.at[at, side_place]
        return partner_copy(block, block, turn_sems.at[0, at], turn_sems.at[1, at])

    def turned(at):
        block = rest_full.at[at, turn_place]
        return side_copy(block, block, turn_sems.at[0, at], turn_sems.at[1, at])

    def side_arrival(at):
        block = rest_full.at[at, side_place]
        return side_move(at, block, block)

    def pair_arrival(at):
        block = rest_full.at[at, pair_place]
        return pair_move(at, block, block)

    def send(at):
        to_side(at).start()
        to_pair(at).start()

    def spot(step):
        return (outer + step) % outers

    def turn(step):
        at = spot(step)
        if step < split:
            side_arrival(at).wait_recv()
            turn_pair(at).start()
        else:
            pair_arrival(at).wait_recv()
            turn_side(at).start()

    def finish():
        own_copy.wait()
        each(0, split, lambda step: pair_arrival(spot(step)).wait_recv())
        each(split, outers, lambda step: side_arrival(spot(step)).wait_recv())
        each(0, outers, lambda at: turned(at).wait_recv())
        each(0, split, lambda step: turn_pair(spot(step)).wait_send())
        each(split, outers, lambda step: turn_side(spot(step)).wait_send())
        each(0, outers, lambda at: to_side(at).wait_send())
        each(0, outers, lambda at: to_pair(at).wait_send())

    return own_copy, send, turn, finish


def attend_clip(
    packed, mem_own, mem_peer, frame, into_ref, outof_ref, gain_ref, shift_ref, bias_ref,
    keyhot_ref, mask_ref, pad_ref, out_own, out_peer, q_out, k_out, v_out, p_out, c_out, shifted,
    taps, heads, unit, scale, after_conv,
):
    units = 3 * heads
    own_rows = out_own.shape[0]
    load_shifted(dot_f32(into_ref[frame], packed[...], ((1,), (0,))), shifted)
    conv = c_out.at[0]
    convolve(shifted, taps, conv, False)
    after_conv()
    k_out[0, MEM_AT:, :] = jnp.zeros((KROWS - MEM_AT, heads * LANES), BF)
    v_out[0, MEM_AT:, :] = jnp.zeros((KROWS - MEM_AT, heads * LANES), BF)
    spread_heads(mem_own, k_out.at[0], MEM_AT, heads, unit, 0 * heads)
    spread_heads(mem_own, v_out.at[0], MEM_AT, heads, unit, 1 * heads)
    spread_heads(mem_peer, k_out.at[0], MEM_AT + MEM_PAD, heads, unit, 0 * heads)
    spread_heads(mem_peer, v_out.at[0], MEM_AT + MEM_PAD, heads, unit, 1 * heads)
    for index in range(units):
        lanes = slice(index * LANES, (index + 1) * LANES)
        block = conv[:, :, :, lanes].reshape(GRID_ROWS, LANES)
        centred, rate = head_stats(block, unit)
        normal = centred * rate * gain_ref[:, lanes] + shift_ref[:, lanes]
        parts = [normal.astype(BF)] if index % heads == 0 else parts + [normal.astype(BF)]
        if index % heads == heads - 1:
            whole = jnp.concatenate(parts, axis=1)
            rows = dot_f32(outof_ref[frame], whole, ((1,), (0,))).astype(BF)
            (q_out, k_out, v_out)[index // heads][0, 0:QROWS, :] = rows

    bias = bias_ref[0]
    bias_high = bias.astype(BF)
    bias_low = (bias - bias_high.astype(F32)).astype(BF)
    for head in range(heads):
        lanes = slice(head * LANES, (head + 1) * LANES)
        keys = k_out[0, :, lanes]
        values = v_out[0, :, lanes]
        for half in range(2):
            rows = slice(half * HALF, (half + 1) * HALF)
            query = q_out[0, rows, lanes]
            table = dot_f32(query, bias_high, ((1,), (1,))) + dot_f32(query, bias_low, ((1,), (1,)))
            table = table * mask_ref[rows, :] + pad_ref[...]
            table_high = table.astype(BF)
            table_low = (table - table_high.astype(F32)).astype(BF)
            scores = dot_f32(query, keys, ((1,), (1,)))
            scores = scores + dot_f32(table_high, keyhot_ref[...], ((1,), (0,)))
            scores = scores + dot_f32(table_low, keyhot_ref[...], ((1,), (0,)))
            top = jnp.max(scores, axis=-1, keepdims=True)
            weights = jnp.exp((scores - top) * scale)
            total = jnp.sum(weights, axis=-1, keepdims=True)
            probs = (weights * (1.0 / total)).astype(BF)
            p_out[0, head, rows, :] = probs
            mixed = dot_f32(probs, values, ((1,), (0,))) + query.astype(F32)
            target = (out_own, out_peer)[half]
            target[:, head * unit : (head + 1) * unit] = mixed[:own_rows, :unit].astype(BF)


def forward_kernel(
    packed_ref, mem_own_ref, mem_peer_ref, column_ref, into_ref, outof_ref, kernel_ref,
    pool_gain_ref, pool_shift_ref, bias_ref, keyhot_ref, mask_ref, pad_ref,
    out_own, out_recv, rest_full, q_out, k_out, v_out, p_out, c_out,
    shifted, taps, gain_ref, shift_ref, out_send, out_sems, side_sems, pair_sems, turn_sems,
    own_sem,
    *, heads, unit, scale,
):
    clip = pl.program_id(0)
    clips = out_send.shape[0]
    frame = lax.axis_index("frame")

    def out_copy(index):
        return partner_copy(
            out_send.at[index], out_recv.at[index], out_sems.at[0, index], out_sems.at[1, index]
        )

    own_copy, send, turn, finish = plane_stage(
        column_ref, rest_full, side_sems, pair_sems, turn_sems, own_sem
    )

    @pl.when(clip == 0)
    def _():
        barrier = pltpu.get_barrier_semaphore()
        for device in (frame_partner(), side_partner()):
            pl.semaphore_signal(barrier, inc=1, device_id=device, device_id_type=MESH_ID)
        pl.semaphore_wait(barrier, 2)
        each(0, column_ref.shape[0], send)
        own_copy.start()
        shifted[...] = jnp.zeros_like(shifted)
        pairs = ((pool_gain_ref, gain_ref), (pool_shift_ref, shift_ref))
        spread_tables(kernel_ref, taps, pairs, heads, unit)

    @pl.when(clip == jnp.minimum(TURN_STEP, clips - 1))
    def _():
        for step in range(column_ref.shape[0]):
            turn(step)

    attend_clip(
        packed_ref.at[0], mem_own_ref.at[0], mem_peer_ref.at[0], frame, into_ref, outof_ref,
        gain_ref, shift_ref, bias_ref, keyhot_ref, mask_ref, pad_ref, out_own.at[0],
        out_send.at[clip], q_out, k_out, v_out, p_out, c_out, shifted, taps, heads, unit, scale,
        lambda: None,
    )
    out_copy(clip).start()

    @pl.when(clip == clips - 1)
    def _():
        finish()
        for index in range(clips):
            out_copy(index).wait()


def backward_kernel(
    packed_ref, normed_ref, weight_ref, grad_own_ref, grad_send_ref, rest_ref, into_ref, outof_ref,
    kernel_ref, pool_gain_ref, bias_ref, keyhot_ref, mask_ref, q_ref, k_ref, v_ref, p_ref, c_ref,
    row_own, row_recv, mem_own, mem_recv, taps_out, gain_out, shift_out, bias_out, weight_out,
    joined_out, rest_part, rest_out,
    shifted, taps, gain_ref, grads, spread, pooled, peer, mem_send, rest_own, rest_side, rest_send,
    rest_peer, rest_sum, rest_far, weight_sum, keep, cross_send, cross_recv, row_send,
    grad_sems, mem_sems, own_sems, side_sems, rest_sems, far_sems, cross_sems, row_sems,
    *, heads, unit, scale,
):
    units = 3 * heads
    own_rows = grad_own_ref.shape[1]
    clip = pl.program_id(0)
    clips = peer.shape[0]
    clip_at = lax.axis_index("clip")
    frame = lax.axis_index("frame")
    head_at = lax.axis_index("head")

    def grad_copy(index):
        return partner_copy(
            grad_send_ref.at[index], peer.at[index], grad_sems.at[0, index], grad_sems.at[1, index]
        )

    def mem_copy(index):
        return partner_copy(
            mem_send.at[index], mem_recv.at[index], mem_sems.at[0, index], mem_sems.at[1, index]
        )

    def row_copy(index):
        return partner_copy(
            row_send.at[index], row_recv.at[index], row_sems.at[0, index], row_sems.at[1, index]
        )

    def cross_copy(index):
        return pltpu.make_async_remote_copy(
            src_ref=cross_send.at[index], dst_ref=cross_recv.at[index],
            send_sem=cross_sems.at[0, index], recv_sem=cross_sems.at[1, index],
            device_id=(clip_at, frame, 1 - head_at), device_id_type=MESH_ID,
        )

    def finish_rows(index):
        cross_copy(index).wait_recv()
        total = (keep[index].astype(F32) + cross_recv[index].astype(F32)).astype(BF)
        row_own[index] = total[:own_rows]
        row_send[index] = total[HALF : HALF + own_rows]
        row_copy(index).start()

    chunks, outers, _, _, cols = rest_own.shape
    side_at = clip_at % 2
    outer = clip_at // 2
    early = rest_far.shape[0]

    def rest_at(side, chunk):
        return rest_ref.at[:, pl.ds(side * 2, 2), :, pl.ds(chunk * cols, cols)]

    def own_copy(chunk):
        return pltpu.make_async_copy(
            rest_at(side_at, chunk), rest_own.at[chunk], own_sems.at[chunk]
        )

    def over_copy(chunk):
        return side_copy(
            rest_at(1 - side_at, chunk), rest_side.at[chunk], side_sems.at[0, chunk],
            side_sems.at[1, chunk],
        )

    def rest_copy(chunk):
        return partner_copy(
            rest_send.at[chunk], rest_peer.at[chunk], rest_sems.at[0, chunk],
            rest_sems.at[1, chunk],
        )

    def pass_on(chunk):
        own_copy(chunk).wait()
        over_copy(chunk).wait_recv()

        def add(index):
            def total(part):
                first = rest_own[chunk, index, part].astype(F32)
                return (first + rest_side[chunk, index, part].astype(F32)).astype(BF)

            rest_send[chunk, index] = total(1 - frame)
            rest_sum[chunk, index] = total(frame)

        each(0, outers, add)
        rest_copy(chunk).start()

    def far_device(step):
        return (((outer + step) % outers) * 2 + side_at, frame, head_at)

    def far_copy(chunk, step):
        there = (outer + step) % outers
        return pltpu.make_async_remote_copy(
            src_ref=rest_sum.at[chunk, there], dst_ref=rest_far.at[chunk, step],
            send_sem=far_sems.at[0, chunk, step], recv_sem=far_sems.at[1, chunk, step],
            device_id=far_device(step), device_id_type=MESH_ID,
        )

    def settle(chunk):
        rest_copy(chunk).wait_recv()

        def add(index):
            total = rest_sum[chunk, index].astype(F32) + rest_peer[chunk, index].astype(F32)
            if chunk < early:
                rest_sum[chunk, index] = total.astype(BF)
            else:
                rest_part[index] = total.astype(BF)

        each(0, outers, add)
        if chunk < early:
            each(1, outers, lambda step: far_copy(chunk, step).start())

    @pl.when(clip == 0)
    def _():
        barrier = pltpu.get_barrier_semaphore()

        def greet(device):
            pl.semaphore_signal(barrier, inc=1, device_id=device, device_id_type=MESH_ID)

        for device in (frame_partner(), side_partner(), (clip_at, frame, 1 - head_at)):
            greet(device)
        each(1, outers, lambda step: greet(far_device(step)))
        pl.semaphore_wait(barrier, 3 + outers - 1)
        for index in range(clips):
            grad_copy(index).start()
        over_copy(0).start()
        own_copy(0).start()
        shifted[...] = jnp.zeros_like(shifted)
        grads[...] = jnp.zeros_like(grads)
        spread[...] = jnp.zeros_like(spread)
        taps_out[...] = jnp.zeros_like(taps_out)
        gain_out[...] = jnp.zeros_like(gain_out)
        shift_out[...] = jnp.zeros_like(shift_out)
        weight_sum[...] = jnp.zeros_like(weight_sum)
        joined_out[...] = jnp.zeros_like(joined_out)
        spread_tables(kernel_ref, taps, ((pool_gain_ref, gain_ref),), heads, unit)

    def pump(odd):
        for chunk in range(chunks):
            point = min(chunk + 1, 2 * clips - 1)
            if point % 2 == odd:

                @pl.when(clip == point // 2)
                def _():
                    if chunk + 1 < chunks:
                        over_copy(chunk + 1).start()
                        own_copy(chunk + 1).start()
                    pass_on(chunk)
                    if chunk:
                        settle(chunk - 1)

    pump(0)
    load_shifted(dot_f32(into_ref[frame], packed_ref[0], ((1,), (0,))), shifted)
    spread_heads(grad_own_ref.at[0], spread, 0, heads, unit)
    grad_copy(clip).wait_recv()
    spread_heads(peer.at[clip], spread, HALF, heads, unit)
    bias_low = bias_ref[0].astype(BF)
    bias_sum = jnp.zeros((BIAS_COLS, LANES), F32)
    for head in range(heads):
        lanes = slice(head * LANES, (head + 1) * LANES)
        keys = k_ref[0, :, lanes]
        values = v_ref[0, :, lanes]
        keys_grad = jnp.zeros((KROWS, LANES), F32)
        values_grad = jnp.zeros((KROWS, LANES), F32)
        for half in range(2):
            rows = slice(half * HALF, (half + 1) * HALF)
            query = q_ref[0, rows, lanes]
            out_grad = spread[rows, lanes]
            probs = p_ref[0, head, rows, :]
            wide = probs.astype(F32)
            probs_grad = dot_f32(out_grad, values, ((1,), (1,)))
            weighted = wide * probs_grad
            shared = jnp.sum(weighted, axis=-1, keepdims=True)
            score_grad = (weighted - wide * shared).astype(BF)
            values_grad = values_grad + dot_f32(probs, out_grad, ((0,), (0,)))
            keys_grad = keys_grad + dot_f32(score_grad, query, ((0,), (0,)))
            table_grad = dot_f32(score_grad, keyhot_ref[...], ((1,), (1,))) * mask_ref[rows, :]
            table_low = table_grad.astype(BF)
            query_grad = dot_f32(score_grad, keys, ((1,), (0,)))
            query_grad = query_grad + dot_f32(table_low, bias_low, ((1,), (0,)))
            query_grad = query_grad * scale + out_grad.astype(F32)
            pooled[rows, lanes] = query_grad.astype(BF)
            bias_sum = bias_sum + dot_f32(table_low, query, ((0,), (0,)))
        keys_grad = (keys_grad * scale).astype(BF)
        values_grad = values_grad.astype(BF)
        for member, part in enumerate((keys_grad, values_grad)):
            at = ((member + 1) * heads + head) * LANES
            pooled[:, at : at + LANES] = part[:QROWS]
            at = (member * heads + head) * LANES
            low = MEM_AT + MEM_PAD
            mem_own[0, :, at : at + LANES] = part[MEM_AT : MEM_AT + MEM_BACK]
            mem_send[clip, :, at : at + LANES] = part[low : low + MEM_BACK]
    bias_out[0] = bias_sum
    mem_copy(clip).start()

    for index in range(units):
        lanes = slice(index * LANES, (index + 1) * LANES)
        if index % heads == 0:
            member = slice(index * LANES, (index + heads) * LANES)
            arrived = dot_f32(into_ref[frame], pooled[:, member], ((1,), (0,)))
        at = index % heads * LANES
        incoming = arrived[:, at : at + LANES]
        block = c_ref[0, :, :, :, lanes].reshape(GRID_ROWS, LANES)
        centred, rate = head_stats(block, unit)
        normal = centred * rate
        product = incoming * normal
        gain_out[:, lanes] += jnp.sum(product, axis=0, keepdims=True)
        shift_out[:, lanes] += jnp.sum(incoming, axis=0, keepdims=True)
        inner = incoming * gain_ref[:, lanes]
        mean_inner = jnp.sum(inner, axis=-1, keepdims=True) * (1.0 / unit)
        mean_both = jnp.sum(inner * normal, axis=-1, keepdims=True) * (1.0 / unit)
        lane = lax.broadcasted_iota(jnp.int32, block.shape, 1)
        result = rate * (inner - mean_inner - normal * mean_both)
        result = jnp.where(lane < unit, result, 0.0)
        flat = result.reshape(FRAMES * SIDE, 8, LANES)
        shape = (FRAMES, SIDE, 8, LANES)
        grads[1, 1 : FRAMES + 1, 1 : SIDE + 1, :, lanes] = flat.reshape(shape)
        grads[0, 1 : FRAMES + 1, 1 : SIDE + 1, :, lanes] = pltpu.roll(flat, 1, 1).reshape(shape)
        grads[2, 1 : FRAMES + 1, 1 : SIDE + 1, :, lanes] = pltpu.roll(flat, 7, 1).reshape(shape)

    @pl.when(clip > 0)
    def _():
        finish_rows(clip - 1)

    pump(1)
    tap_grads(shifted, grads.at[1], taps_out)
    conv = shifted.at[1, 1 : FRAMES + 1, 1 : SIDE + 1]
    convolve(grads, taps, conv, True)
    for member in range(3):
        lanes = slice(member * heads * LANES, (member + 1) * heads * LANES)
        block = shifted[1, 1 : FRAMES + 1, 1 : SIDE + 1, :, lanes].reshape(GRID_ROWS, -1)
        rows = dot_f32(outof_ref[frame], block.astype(BF), ((1,), (0,))).astype(BF)
        pooled[:, lanes] = rows
        joined_out[:, lanes] += jnp.sum(rows.astype(F32), axis=0, keepdims=True)
    weight_sum[...] += dot_f32(normed_ref[0], pooled[...], ((0,), (0,)))
    result = dot_f32(pooled[...], weight_ref[...], ((1,), (1,))).astype(BF)
    cut = result.shape[1] // 2

    @pl.when(head_at == 0)
    def _():
        keep[clip] = result[:, :cut]
        cross_send[clip] = result[:, cut:]

    @pl.when(head_at == 1)
    def _():
        keep[clip] = result[:, cut:]
        cross_send[clip] = result[:, :cut]

    cross_copy(clip).start()

    @pl.when(clip == clips - 1)
    def _():
        weight_out[...] = weight_sum[...].astype(BF)
        finish_rows(clip)
        settle(chunks - 1)
        for chunk in range(early):
            each(1, outers, lambda step: far_copy(chunk, step).wait_recv())
            rest_out[:, chunk * cols : (chunk + 1) * cols] = lax.fori_loop(
                1,
                outers,
                lambda step, sums: sums + rest_far[chunk, step].astype(F32),
                rest_sum[chunk, outer].astype(F32),
            )
        for index in range(clips):
            grad_copy(index).wait_send()
            cross_copy(index).wait_send()
            mem_copy(index).wait()
            row_copy(index).wait()
        for chunk in range(chunks):
            over_copy(chunk).wait_send()
            rest_copy(chunk).wait_send()
        for chunk in range(early):
            each(1, outers, lambda step: far_copy(chunk, step).wait_send())


def whole_spec(shape):
    return pl.BlockSpec(shape, lambda clip: (0,) * len(shape))


def clip_spec(shape):
    return pl.BlockSpec((1,) + shape, lambda clip: (clip,) + (0,) * len(shape))


def once_spec(shape):
    return pl.BlockSpec(
        shape, lambda clip: (0,) * len(shape), pipeline_mode=pl.Buffered(1)
    )


def any_spec():
    return pl.BlockSpec(memory_space=pl.ANY)


def attention_forward(
    packed, mem_own, mem_peer, column, consts, kernels, gains, shifts, bias, scale, unit, rows
):
    clips = packed.shape[0]
    heads = packed.shape[2] // (3 * LANES)
    into, outof, keyhot, mask, pad_row = consts
    wide = 3 * heads * LANES
    mem_shape = mem_own.shape[1:]
    outers = column.shape[0]
    dma = pltpu.SemaphoreType.DMA
    out = jax.ShapeDtypeStruct
    return pl.pallas_call(
        partial(forward_kernel, heads=heads, unit=unit, scale=scale),
        grid=(clips,),
        in_specs=[
            clip_spec((QROWS, wide)),
            clip_spec(mem_shape),
            clip_spec(mem_shape),
            once_spec(column.shape),
            once_spec(into.shape),
            once_spec(outof.shape),
            once_spec(kernels.shape),
            once_spec(gains.shape),
            once_spec(shifts.shape),
            clip_spec((BIAS_COLS, LANES)),
            once_spec((BIAS_COLS, KROWS)),
            once_spec((QROWS, BIAS_COLS)),
            once_spec((1, BIAS_COLS)),
        ],
        out_specs=[
            clip_spec((rows, heads * unit)),
            any_spec(),
            any_spec(),
            clip_spec((QROWS, heads * LANES)),
            clip_spec((KROWS, heads * LANES)),
            clip_spec((KROWS, heads * LANES)),
            clip_spec((heads, QROWS, KROWS)),
            clip_spec((FRAMES, SIDE, 8, wide)),
        ],
        scratch_shapes=[
            pltpu.VMEM((3, FRAMES + 2, SIDE + 2, 8, wide), F32),
            pltpu.VMEM((27, 8, wide), F32),
            pltpu.VMEM((1, wide), F32),
            pltpu.VMEM((1, wide), F32),
            pltpu.VMEM((clips, rows, heads * unit), BF),
            dma((2, clips)),
            dma((2, outers)),
            dma((2, outers)),
            dma((2, outers)),
            pltpu.SemaphoreType.DMA,
        ],
        out_shape=[
            out((clips, rows, heads * unit), BF),
            out((clips, rows, heads * unit), BF),
            out((outers, 4) + column.shape[1:], BF),
            out((clips, QROWS, heads * LANES), BF),
            out((clips, KROWS, heads * LANES), BF),
            out((clips, KROWS, heads * LANES), BF),
            out((clips, heads, QROWS, KROWS), BF),
            out((clips, FRAMES, SIDE, 8, wide), F32),
        ],
        compiler_params=pltpu.CompilerParams(
            collective_id=1, has_side_effects=True, vmem_limit_bytes=VMEM_LIMIT
        ),
        name="pooled_attention_forward",
    )(
        packed, mem_own, mem_peer, column, into, outof, kernels, gains, shifts, bias, keyhot, mask,
        pad_row,
    )


def attention_backward(
    packed, normed, weight, grad_own, grad_send, rest, consts, kernels, gains, bias, saved, scale,
    unit,
):
    clips, rows, width = grad_own.shape
    heads = width // unit
    model = weight.shape[0]
    half = model // 2
    into, outof, keyhot, mask, pad_row = consts
    wide = 3 * heads * LANES
    outers, _, shard_rows, rest_width = rest.shape
    chunks = 9
    early = 8
    cols = rest_width // chunks
    out = jax.ShapeDtypeStruct
    dma = pltpu.SemaphoreType.DMA
    return pl.pallas_call(
        partial(backward_kernel, heads=heads, unit=unit, scale=scale),
        grid=(clips,),
        in_specs=[
            clip_spec((QROWS, wide)),
            clip_spec((QROWS, model)),
            once_spec((model, wide)),
            clip_spec((rows, width)),
            any_spec(),
            any_spec(),
            once_spec(into.shape),
            once_spec(outof.shape),
            once_spec(kernels.shape),
            once_spec(gains.shape),
            clip_spec((BIAS_COLS, LANES)),
            once_spec((BIAS_COLS, KROWS)),
            once_spec((QROWS, BIAS_COLS)),
            clip_spec((QROWS, heads * LANES)),
            clip_spec((KROWS, heads * LANES)),
            clip_spec((KROWS, heads * LANES)),
            clip_spec((heads, QROWS, KROWS)),
            clip_spec((FRAMES, SIDE, 8, wide)),
        ],
        out_specs=[
            whole_spec((clips, rows, half)),
            any_spec(),
            clip_spec((MEM_BACK, 2 * heads * LANES)),
            any_spec(),
            whole_spec((27, 8, wide)),
            whole_spec((1, wide)),
            whole_spec((1, wide)),
            clip_spec((BIAS_COLS, LANES)),
            whole_spec((model, wide)),
            whole_spec((1, wide)),
            whole_spec((outers, shard_rows, cols)),
            whole_spec((shard_rows, early * cols)),
        ],
        scratch_shapes=[
            pltpu.VMEM((3, FRAMES + 2, SIDE + 2, 8, wide), F32),
            pltpu.VMEM((27, 8, wide), F32),
            pltpu.VMEM((1, wide), F32),
            pltpu.VMEM((3, FRAMES + 2, SIDE + 2, 8, wide), F32),
            pltpu.VMEM((QROWS, heads * LANES), BF),
            pltpu.VMEM((QROWS, wide), BF),
            pltpu.VMEM((clips, rows, width), BF),
            pltpu.VMEM((clips, MEM_BACK, 2 * heads * LANES), BF),
            pltpu.VMEM((chunks, outers, 2, shard_rows, cols), BF),
            pltpu.VMEM((chunks, outers, 2, shard_rows, cols), BF),
            pltpu.VMEM((chunks, outers, shard_rows, cols), BF),
            pltpu.VMEM((chunks, outers, shard_rows, cols), BF),
            pltpu.VMEM((chunks, outers, shard_rows, cols), BF),
            pltpu.VMEM((early, outers, shard_rows, cols), BF),
            pltpu.VMEM((model, wide), F32),
            pltpu.VMEM((clips, QROWS, half), BF),
            pltpu.VMEM((clips, QROWS, half), BF),
            pltpu.VMEM((clips, QROWS, half), BF),
            pltpu.VMEM((clips, rows, half), BF),
            dma((2, clips)),
            dma((2, clips)),
            dma((chunks,)),
            dma((2, chunks)),
            dma((2, chunks)),
            dma((2, early, outers)),
            dma((2, clips)),
            dma((2, clips)),
        ],
        out_shape=[
            out((clips, rows, half), BF),
            out((clips, rows, half), BF),
            out((clips, MEM_BACK, 2 * heads * LANES), BF),
            out((clips, MEM_BACK, 2 * heads * LANES), BF),
            out((27, 8, wide), F32),
            out((1, wide), F32),
            out((1, wide), F32),
            out((clips, BIAS_COLS, LANES), F32),
            out((model, wide), BF),
            out((1, wide), F32),
            out((outers, shard_rows, cols), BF),
            out((shard_rows, early * cols), F32),
        ],
        compiler_params=pltpu.CompilerParams(
            collective_id=2, has_side_effects=True, vmem_limit_bytes=VMEM_LIMIT
        ),
        name="pooled_attention_backward",
    )(
        packed, normed, weight, grad_own, grad_send, rest, into, outof, kernels, gains, bias, keyhot,
        mask, *saved,
    )


def row_stats(values):
    width = values.shape[-1]
    centred = values - jnp.sum(values, axis=-1, keepdims=True) * (1.0 / width)
    variance = jnp.sum(centred * centred, axis=-1, keepdims=True) * (1.0 / width)
    return centred, lax.rsqrt(variance + 1e-06)


def each(low, high, act):
    def body(step, carry):
        act(step)
        return carry

    lax.fori_loop(low, high, body, 0)


def norm_rows(source, index, gain, shift, target, at):
    rows = source.shape[1]
    centred, rate = row_stats(source[index].astype(F32))
    target[index, at : at + rows] = (centred * rate * gain[0:1] + shift[0:1]).astype(BF)


def project_rows(normed, weight, bias, packed):
    def step(index):
        packed[index] = (dot_f32(normed[index], weight, ((1,), (0,))) + bias[...]).astype(BF)

    each(0, packed.shape[0], step)


def project_moves(
    x, attn, gain, shift, attn_shift, cached, old, squeeze, proj, up, down, full, normed, mem_own,
    mem_peer, rest_column, shards, bias, rest, mem_send, squeeze_rows, x_peer, columns, far_sems,
    near_sems, x_sems, cross_sems, mem_sems, rest_sems,
):
    outers = full.shape[0]
    clips, rows, model = x.shape
    clip = lax.axis_index("clip")
    frame = lax.axis_index("frame")
    head = lax.axis_index("head")
    outer, inner = clip // 2, clip % 2
    place = inner * 2 + frame
    half = model // 2
    lanes = pl.ds(pl.multiple_of(head * half, LANES), half)
    barrier = pltpu.get_barrier_semaphore()

    def far_device(step):
        return device_of((outer + step) % outers, inner, frame, head)

    def near_device(step):
        there_inner, there_frame = plane_peer(inner, frame, step)
        return device_of(outer, there_inner, there_frame, head)

    def greet(device):
        pl.semaphore_signal(barrier, inc=1, device_id=device, device_id_type=MESH_ID)

    group = mem_own.shape[2] // 2
    heads = shards.shape[2] // (3 * LANES)
    unit = group // heads

    def squeeze_clip(index):
        total = jnp.zeros((CELLS, cached.shape[2]), F32)
        for step in range(squeeze_rows.shape[0]):
            rows_here = cached[index, step * CELLS : (step + 1) * CELLS].astype(F32)
            total = total + rows_here * squeeze_rows[step : step + 1]
        pieces = ((0, total.astype(BF)), (MEM_STEP, old[index]))
        for side in range(2):

            @pl.when(frame == side)
            def _():
                for at, value in pieces:
                    for member in range(2):
                        local = slice(member * group, (member + 1) * group)
                        low = (2 * member + side) * group
                        mem_own[index, at : at + CELLS, local] = value[:, low : low + group]
                        low = (2 * member + 1 - side) * group
                        mem_send[index, at : at + CELLS, local] = value[:, low : low + group]

    def far_copy(step, at):
        return pltpu.make_async_remote_copy(
            src_ref=shards, dst_ref=columns.at[at],
            send_sem=far_sems.at[0, step], recv_sem=far_sems.at[1, step],
            device_id=far_device(step), device_id_type=MESH_ID,
        )

    def near_copy(index, step, source, at):
        return pltpu.make_async_remote_copy(
            src_ref=source.at[(frame + step % 2) % 2], dst_ref=full.at[at, place],
            send_sem=near_sems.at[0, index, step - 1], recv_sem=near_sems.at[1, index, step - 1],
            device_id=near_device(step), device_id_type=MESH_ID,
        )

    def near_arrival(index, step, at):
        there_inner, there_frame = plane_peer(inner, frame, step)
        return pltpu.make_async_remote_copy(
            src_ref=shards.at[0], dst_ref=full.at[at, there_inner * 2 + there_frame],
            send_sem=near_sems.at[0, index, step - 1], recv_sem=near_sems.at[1, index, step - 1],
            device_id=near_device(step), device_id_type=MESH_ID,
        )

    def x_copy(index):
        return partner_copy(
            x.at[index, :, lanes], x_peer.at[index, :, lanes], x_sems.at[0, index],
            x_sems.at[1, index],
        )

    def cross_copy(index):
        return pltpu.make_async_remote_copy(
            src_ref=x_peer.at[index, :, lanes], dst_ref=x_peer.at[index, :, lanes],
            send_sem=cross_sems.at[0, index], recv_sem=cross_sems.at[1, index],
            device_id=(clip, frame, 1 - head), device_id_type=MESH_ID,
        )

    def cross_arrival(index):
        other = pl.ds(pl.multiple_of((1 - head) * half, LANES), half)
        return pltpu.make_async_remote_copy(
            src_ref=x_peer.at[index, :, other], dst_ref=x_peer.at[index, :, other],
            send_sem=cross_sems.at[0, index], recv_sem=cross_sems.at[1, index],
            device_id=(clip, frame, 1 - head), device_id_type=MESH_ID,
        )

    mem_copy = partner_copy(mem_send, mem_peer, mem_sems.at[0], mem_sems.at[1])

    def rest_copy(step, at):
        return pltpu.make_async_remote_copy(
            src_ref=rest, dst_ref=rest_column.at[at],
            send_sem=rest_sems.at[0, step], recv_sem=rest_sems.at[1, step],
            device_id=far_device(step), device_id_type=MESH_ID,
        )

    def origin(step):
        return (outer + outers - step) % outers

    def prologue():
        each(1, outers, lambda step: greet(far_device(step)))
        for step in range(1, 4):
            greet(near_device(step))
        greet((clip, frame, 1 - head))
        shards[...] = jnp.zeros_like(shards)
        bias[...] = jnp.zeros_like(bias)
        for member in range(3):
            for side in range(2):
                for index in range(heads):
                    target = (member * heads + index) * LANES
                    source = slice(side * group + index * unit, side * group + (index + 1) * unit)
                    shards[side, :, target : target + unit] = attn[member, :, source]
        at = 0
        for part in (proj, up, down):
            rest[:, at : at + part.shape[1]] = part[...]
            at += part.shape[1]
        for side in range(2):

            @pl.when(frame == side)
            def _():
                for member in range(3):
                    for index in range(heads):
                        target = (member * heads + index) * LANES
                        source = slice(side * group + index * unit, side * group + (index + 1) * unit)
                        bias[:, target : target + unit] = attn_shift[member : member + 1, source]

        for member in range(2):
            for index in range(2 * heads):
                at = (2 * member * heads + index) * unit
                squeeze_rows[:, at : at + unit] = squeeze[member]
        mem_own[...] = jnp.zeros_like(mem_own)
        mem_send[...] = jnp.zeros_like(mem_send)

        pl.semaphore_wait(barrier, outers - 1 + 4)
        each(1, outers, lambda step: far_copy(step, outer).start())
        for step in range(1, 4):
            near_copy(0, step, shards, outer).start()
        each(0, clips, lambda index: x_copy(index).start())
        each(0, clips, squeeze_clip)
        rest_column[outer] = rest[...]
        full[outer, place] = shards[frame]
        normed[...] = jnp.zeros_like(normed)
        each(0, clips, lambda index: norm_rows(x, index, gain, shift, normed, 0))

        def forward(index):
            at = origin(index)
            far_copy(index, at).wait_recv()
            for step in range(1, 4):
                near_copy(index, step, columns.at[at], at).start()
            full[at, place] = columns[at, frame]

        each(1, outers, forward)
        each(1, outers, lambda step: rest_copy(step, outer).start())

        def relay(index):
            x_copy(index).wait_recv()
            cross_copy(index).start()

        each(0, clips, relay)
        mem_copy.start()

        def receive(index):
            cross_arrival(index).wait_recv()
            norm_rows(x_peer, index, gain, shift, normed, HALF)

        each(0, clips, receive)

        def arrive(index):
            for step in range(1, 4):
                near_arrival(index, step, origin(index)).wait_recv()

        each(0, outers, arrive)
    def rest_arrive():
        each(1, outers, lambda step: rest_copy(step, origin(step)).wait_recv())

    def finish():
        each(1, outers, lambda step: rest_copy(step, outer).wait_send())
        each(1, outers, lambda step: far_copy(step, outer).wait_send())
        for step in range(1, 4):
            near_copy(0, step, shards, outer).wait_send()

        def sent(index):
            for step in range(1, 4):
                near_copy(index, step, columns.at[origin(index)], origin(index)).wait_send()

        each(1, outers, sent)

        def x_sent(index):
            x_copy(index).wait_send()
            cross_copy(index).wait_send()

        each(0, clips, x_sent)

    return outer, prologue, mem_copy, rest_arrive, finish


def front_kernel(
    x, attn, gain, shift, attn_shift, cached, old, squeeze, proj, up, down, into_ref, outof_ref,
    kernel_ref, pool_gain_ref, pool_shift_ref, bias_ref, keyhot_ref, mask_ref, pad_ref,
    full_out, packed_out, normed_out, out_own, out_recv, rest_full, q_out, k_out, v_out, p_out,
    c_out, full, shards, attn_bias, rest, mem_send, mem_own, mem_peer, squeeze_rows, x_peer, columns, normed,
    rest_column, shifted, taps, gain_ref, shift_ref, out_send, far_sems, near_sems, x_sems,
    cross_sems, mem_sems, rest_sems, out_sems, side_sems, pair_sems, turn_sems, own_sem,
    *, heads, unit, scale,
):
    clip = pl.program_id(0)
    clips = out_send.shape[0]
    outers = full.shape[0]
    frame = lax.axis_index("frame")
    outer, prologue, mem_copy, rest_arrive, project_finish = project_moves(
        x, attn, gain, shift, attn_shift, cached, old, squeeze, proj, up, down, full, normed,
        mem_own, mem_peer, rest_column, shards, attn_bias, rest, mem_send, squeeze_rows, x_peer,
        columns, far_sems, near_sems, x_sems, cross_sems, mem_sems, rest_sems,
    )
    own_copy, send, turn, plane_finish = plane_stage(
        rest_column, rest_full, side_sems, pair_sems, turn_sems, own_sem
    )

    def out_copy(index):
        return partner_copy(
            out_send.at[index], out_recv.at[index], out_sems.at[0, index], out_sems.at[1, index]
        )

    @pl.when(clip == 0)
    def _():
        prologue()
        send(outer)
        shifted[...] = jnp.zeros_like(shifted)
        pairs = ((pool_gain_ref, gain_ref), (pool_shift_ref, shift_ref))
        spread_tables(kernel_ref, taps, pairs, heads, unit)

    def points(odd):
        for step in range(outers):
            point = min(step + TURN_LAG, 2 * clips - 1)
            if step and step % 2 == odd:

                @pl.when(clip == step // 2)
                def _():
                    send((outer + step) % outers)

            if point % 2 == odd:

                @pl.when(clip == point // 2)
                def _():
                    turn(step)

    def after_conv():
        @pl.when(clip == 0)
        def _():
            mem_copy.wait_recv()
            rest_arrive()
            own_copy.start()

        points(1)

    points(0)
    @pl.when(clip == clips - 1)
    def _():
        full_out[...] = full[...]

    normed_out[0] = normed[clip]
    weight = full[...].reshape(x.shape[2], full.shape[3])
    rows = dot_f32(normed[clip], weight, ((1,), (0,))) + attn_bias[...]
    packed_out[0] = rows.astype(BF)
    attend_clip(
        packed_out.at[0], mem_own.at[clip], mem_peer.at[clip], frame, into_ref, outof_ref, gain_ref,
        shift_ref, bias_ref, keyhot_ref, mask_ref, pad_ref, out_own.at[0], out_send.at[clip], q_out,
        k_out, v_out, p_out, c_out, shifted, taps, heads, unit, scale, after_conv,
    )
    out_copy(clip).start()

    @pl.when(clip == clips - 1)
    def _():
        mem_copy.wait_send()
        project_finish()
        plane_finish()
        for index in range(clips):
            out_copy(index).wait()


def front(
    x, attn, gain, shift, attn_shift, cached, old, squeeze, proj, up, down, consts, kernels, gains,
    shifts, bias, scale, clip_count, unit,
):
    clips, rows, model = x.shape
    _, shard_rows, head_width = attn.shape
    heads = head_width // (2 * unit)
    wide = 3 * heads * LANES
    outers = clip_count // 2
    into, outof, keyhot, mask, pad_row = consts
    rest_shape = (shard_rows, proj.shape[1] + up.shape[1] + down.shape[1])
    mem_shape = (clips, MEM_PAD, head_width)
    out = jax.ShapeDtypeStruct
    dma = pltpu.SemaphoreType.DMA
    operands = (
        x, attn, gain, shift, attn_shift, cached, old, squeeze, proj, up, down, into, outof,
        kernels, gains, shifts, bias, keyhot, mask, pad_row,
    )
    specs = [once_spec(value.shape) for value in operands]
    specs[16] = clip_spec((BIAS_COLS, LANES))
    results = pl.pallas_call(
        partial(front_kernel, heads=heads, unit=unit, scale=scale),
        grid=(clips,),
        in_specs=specs,
        out_specs=[
            whole_spec((outers, 4, shard_rows, wide)),
            clip_spec((QROWS, wide)),
            clip_spec((QROWS, model)),
            clip_spec((rows, heads * unit)),
            any_spec(),
            any_spec(),
            clip_spec((QROWS, heads * LANES)),
            clip_spec((KROWS, heads * LANES)),
            clip_spec((KROWS, heads * LANES)),
            clip_spec((heads, QROWS, KROWS)),
            clip_spec((FRAMES, SIDE, 8, wide)),
        ],
        out_shape=[
            out((outers, 4, shard_rows, wide), BF),
            out((clips, QROWS, wide), BF),
            out((clips, QROWS, model), BF),
            out((clips, rows, heads * unit), BF),
            out((clips, rows, heads * unit), BF),
            out((outers, 4) + rest_shape, BF),
            out((clips, QROWS, heads * LANES), BF),
            out((clips, KROWS, heads * LANES), BF),
            out((clips, KROWS, heads * LANES), BF),
            out((clips, heads, QROWS, KROWS), BF),
            out((clips, FRAMES, SIDE, 8, wide), F32),
        ],
        scratch_shapes=[
            pltpu.VMEM((outers, 4, shard_rows, wide), BF),
            pltpu.VMEM((2, shard_rows, wide), BF),
            pltpu.VMEM((1, wide), F32),
            pltpu.VMEM(rest_shape, BF),
            pltpu.VMEM(mem_shape, BF),
            pltpu.VMEM(mem_shape, BF),
            pltpu.VMEM(mem_shape, BF),
            pltpu.VMEM((squeeze.shape[1], cached.shape[2]), F32),
            pltpu.VMEM((clips, rows, model), BF),
            pltpu.VMEM((outers, 2, shard_rows, wide), BF),
            pltpu.VMEM((clips, QROWS, model), BF),
            pltpu.VMEM((outers,) + rest_shape, BF),
            pltpu.VMEM((3, FRAMES + 2, SIDE + 2, 8, wide), F32),
            pltpu.VMEM((27, 8, wide), F32),
            pltpu.VMEM((1, wide), F32),
            pltpu.VMEM((1, wide), F32),
            pltpu.VMEM((clips, rows, heads * unit), BF),
            dma((2, outers)),
            dma((2, outers, 3)),
            dma((2, clips)),
            dma((2, clips)),
            dma((2,)),
            dma((2, outers)),
            dma((2, clips)),
            dma((2, outers)),
            dma((2, outers)),
            dma((2, outers)),
            pltpu.SemaphoreType.DMA,
        ],
        compiler_params=pltpu.CompilerParams(
            collective_id=1, has_side_effects=True, vmem_limit_bytes=VMEM_LIMIT
        ),
        name="project_and_attend",
    )(*operands)
    return (results[0].reshape(model, wide),) + tuple(results[1:])


def project_local_kernel(x, x_peer, weight, gain, shift, bias, packed, normed):
    normed[...] = jnp.zeros_like(normed)
    each(0, x.shape[0], lambda index: norm_rows(x, index, gain, shift, normed, 0))
    each(0, x.shape[0], lambda index: norm_rows(x_peer, index, gain, shift, normed, HALF))
    project_rows(normed, weight[...], bias, packed)


def swap(value, axis):
    return lax.ppermute(value, axis, [(0, 1), (1, 0)])


def padded_heads(value, unit):
    value = value.reshape(value.shape[0], 3, 2, -1, unit)
    value = jnp.pad(value, ((0, 0),) * 4 + ((0, LANES - unit),))
    return value.transpose(2, 0, 1, 3, 4).reshape(2, value.shape[0], -1)


def project_plain(
    x, attn, gain, shift, attn_shift, cached, old, squeeze, proj, up, down, clip_count, unit
):
    clips, rows, model = x.shape
    _, shard_rows, head_width = attn.shape
    heads = head_width // (2 * unit)
    width = 3 * heads * LANES
    outers = clip_count // 2
    rest_shape = (shard_rows, proj.shape[1] + up.shape[1] + down.shape[1])
    out = jax.ShapeDtypeStruct
    dma = pltpu.SemaphoreType.DMA
    vmem = pl.BlockSpec(memory_space=pltpu.VMEM)
    shapes = [out((clips, QROWS, width), BF), out((clips, QROWS, model), BF)]
    frame = lax.axis_index("frame")
    shards = padded_heads(attn.transpose(1, 0, 2), unit)
    full = lax.all_gather(shards, ("clip", "frame"), axis=1, tiled=True)
    full = lax.dynamic_index_in_dim(full, frame, 0, keepdims=False)
    bias = padded_heads(attn_shift[None], unit)
    bias = lax.dynamic_index_in_dim(bias, frame, 0, keepdims=False)
    steps = squeeze.shape[1]
    wide = cached.astype(F32).reshape(clips, steps, CELLS, 2, head_width)
    tiled = jnp.tile(squeeze, (1, 1, 2 * heads))
    mem = sum(wide[:, step] * tiled[:, step] for step in range(steps)).astype(BF)
    mem = jnp.stack([mem, old.reshape(mem.shape)], axis=1)
    mem = jnp.pad(mem, ((0, 0), (0, 0), (0, MEM_STEP - CELLS), (0, 0), (0, 0)))
    pieces = mem.reshape(clips, 2 * MEM_STEP, 2, 2, heads * unit)
    mem_own = lax.dynamic_index_in_dim(pieces, frame, 3, keepdims=False)
    mem_send = lax.dynamic_index_in_dim(pieces, 1 - frame, 3, keepdims=False)
    mem_own = mem_own.reshape(clips, -1, head_width)
    mem_peer = swap(mem_send.reshape(clips, -1, head_width), "frame")
    packed, normed = pl.pallas_call(
        project_local_kernel,
        in_specs=[vmem] * 6,
        out_specs=[vmem] * 2,
        out_shape=shapes,
        compiler_params=pltpu.CompilerParams(vmem_limit_bytes=VMEM_LIMIT),
        name="project_local",
    )(x, swap(x, "frame"), full, gain, shift, bias)
    rest = jnp.concatenate([proj, up, down], axis=1)
    column = lax.all_gather(rest, ("clip", "frame"), axis=0, tiled=False)
    column = column.reshape((outers, 4) + rest.shape)
    place = lax.axis_index("clip") % 2 * 2 + frame
    column = lax.dynamic_index_in_dim(column, place, 1, keepdims=False)
    return full, packed, normed, mem_own, mem_peer, column


def device_of(outer, inner, frame, head):
    return (outer * 2 + inner, frame, head)


def plane_peer(inner, frame, step):
    return (inner + step // 2) % 2, (frame + step % 2) % 2


def row_piece(value, row):
    return value[:, row * LANES : (row + 1) * LANES]


def tail_kernel(
    row_own, row_recv, x, middle_grad, grads, joined_sum, gain, taps, pool_gain, pool_shift,
    bias_grad, hot, space_hot, cached, mem_own, mem_recv, vectors, up_bias, rest,
    grad_in, out, rest_out, small_out,
    near, part, far, small, pair_in, plane_in, line_in, row_full, rest_in,
    cross_sems, near_sems, far_sems, pair_sems, plane_sems, line_sems, rest_sems,
    *, unit, plan, table_rows,
):
    chunks, outers, _, shard_rows, cols = part.shape
    clips, rows, model = x.shape
    half = model // 2
    clip = lax.axis_index("clip")
    frame = lax.axis_index("frame")
    head = lax.axis_index("head")
    outer, inner = clip // 2, clip % 2
    place = inner * 2 + frame
    barrier = pltpu.get_barrier_semaphore()
    partner = (clip, frame, 1 - head)

    def line_device(step):
        return device_of((outer + step) % outers, inner, frame, head)

    def plane_device(step):
        there_inner, there_frame = plane_peer(inner, frame, step)
        return device_of(outer, there_inner, there_frame, head)

    def plane_place(step):
        there_inner, there_frame = plane_peer(inner, frame, step)
        return there_inner * 2 + there_frame

    def greet(device):
        pl.semaphore_signal(barrier, inc=1, device_id=device, device_id_type=MESH_ID)

    each(1, outers, lambda step: greet(line_device(step)))
    for step in range(1, 4):
        greet(plane_device(step))
    greet(partner)

    def move(source, target, sems, device):
        return pltpu.make_async_remote_copy(
            src_ref=source, dst_ref=target, send_sem=sems[0], recv_sem=sems[1],
            device_id=device, device_id_type=MESH_ID,
        )

    def pair_sum():
        return move(
            small.at[1 - head], pair_in, (pair_sems.at[0, 0], pair_sems.at[1, 0]), partner
        )

    def plane_sum(step):
        sems = (plane_sems.at[0, 0, step - 1], plane_sems.at[1, 0, step - 1])
        source = small.at[head, plane_place(step)]
        return move(source, plane_in.at[step - 1], sems, plane_device(step))

    def line_sum(step):
        sems = (line_sems.at[0, 0, step], line_sems.at[1, 0, step])
        source = small.at[head, place, (outer + step) % outers]
        return move(source, line_in.at[step], sems, line_device(step))

    def line_share(step, at):
        sems = (line_sems.at[0, 1, step], line_sems.at[1, 1, step])
        block = small_out.at[head, place, at]
        return move(block, block, sems, line_device(step))

    def plane_share(step, at):
        sems = (plane_sems.at[0, 1, step - 1], plane_sems.at[1, 1, step - 1])
        block = small_out.at[head, at]
        return move(block, block, sems, plane_device(step))

    def pair_share(at):
        block = small_out.at[at]
        return move(block, block, (pair_sems.at[0, 1], pair_sems.at[1, 1]), partner)

    def near_copy(chunk, step):
        there_inner, there_frame = plane_peer(inner, frame, step)
        return pltpu.make_async_remote_copy(
            src_ref=grads.at[:, there_inner * 2 + there_frame, :, pl.ds(chunk * cols, cols)],
            dst_ref=near.at[chunk, step - 1],
            send_sem=near_sems.at[0, chunk, step - 1], recv_sem=near_sems.at[1, chunk, step - 1],
            device_id=device_of(outer, there_inner, there_frame, head), device_id_type=MESH_ID,
        )

    def far_copy(chunk, step):
        there = (outer + step) % outers
        return pltpu.make_async_remote_copy(
            src_ref=part.at[chunk, there], dst_ref=far.at[chunk, step],
            send_sem=far_sems.at[0, chunk, step], recv_sem=far_sems.at[1, chunk, step],
            device_id=device_of(there, inner, frame, head), device_id_type=MESH_ID,
        )

    def cross_copy(index, side):
        lanes = pl.ds(pl.multiple_of(side * half, LANES), half)
        return pltpu.make_async_remote_copy(
            src_ref=row_full.at[index, :, lanes], dst_ref=row_full.at[index, :, lanes],
            send_sem=cross_sems.at[0, index], recv_sem=cross_sems.at[1, index],
            device_id=(clip, frame, 1 - head), device_id_type=MESH_ID,
        )

    def rest_copy(step):
        there = (outer + step) % outers
        return pltpu.make_async_remote_copy(
            src_ref=rest.at[there], dst_ref=rest_in.at[step],
            send_sem=rest_sems.at[0, step], recv_sem=rest_sems.at[1, step],
            device_id=device_of(there, inner, frame, head), device_id_type=MESH_ID,
        )

    small[...] = jnp.zeros_like(small)
    pl.semaphore_wait(barrier, outers - 1 + 4)
    for chunk in range(chunks):
        for step in range(1, 4):
            near_copy(chunk, step).start()
    lanes_here = pl.ds(pl.multiple_of(head * half, LANES), half)

    def join(index):
        total = row_own[index].astype(F32) + row_recv[index].astype(F32)
        row_full[index, :, lanes_here] = total.astype(BF)
        cross_copy(index, head).start()

    each(0, clips, join)
    each(1, outers, lambda step: rest_copy(step).start())

    rows_small = small.shape[3]

    def put(row, value):
        count = value.shape[0]
        done = 0
        while done < count:
            block, offset = divmod(row + done, rows_small)
            size = min(count - done, rows_small - offset)
            at = (block // (4 * outers), block // outers % 4, block % outers)
            small[at[0], at[1], at[2], offset : offset + size, : value.shape[1]] = value[
                done : done + size
            ]
            done += size

    def put_wide(row, value):
        for index in range(value.shape[1] // LANES):
            put(row + index, row_piece(value, index))

    wide_rows_count = model // LANES

    joined_rows = joined_sum.shape[1] // LANES
    up_rows = up_bias.shape[1] // LANES
    for which in range(2):

        @pl.when(head == which)
        def _():
            for side in range(2):

                @pl.when(frame == side)
                def _():
                    put_wide(plan["joined"] + (2 * which + side) * joined_rows, joined_sum[...])

            put_wide(plan["up"] + which * up_rows, up_bias[...])

    heads = taps.shape[2] // (3 * LANES)
    tap_sum = jnp.sum(taps[...], axis=1)
    for member in range(3):
        totals = []
        for value in (tap_sum, pool_gain[...], pool_shift[...]):
            total = row_piece(value, member * heads)
            for index in range(1, heads):
                total = total + row_piece(value, member * heads + index)
            totals.append(total)
        put(plan["taps"] + member * 27, totals[0])
        put(plan["pool_gain"] + member, totals[1])
        put(plan["pool_shift"] + member, totals[2])
    heads_here = joined_sum.shape[1] // (3 * LANES)
    for side in range(2):

        @pl.when(frame == side)
        def _():
            for member in range(2):
                totals = [jnp.zeros((1, unit), F32) for _ in range(FRAMES // MEMF)]
                for index in range(clips):
                    for which, part in ((side, mem_own), (1 - side, mem_recv)):
                        for spot in range(heads_here):
                            at = (member * heads_here + spot) * LANES
                            value = part[index, :CELLS, at : at + unit].astype(F32)
                            at = ((2 * member + which) * heads_here + spot) * unit
                            for step in range(len(totals)):
                                rows_here = cached[
                                    index, step * CELLS : (step + 1) * CELLS, at : at + unit
                                ]
                                product = rows_here.astype(F32) * value
                                totals[step] = totals[step] + jnp.sum(
                                    product, axis=0, keepdims=True
                                )
                for step in range(len(totals)):
                    put(plan["squeeze"] + member * len(totals) + step, totals[step])

    time_sum = jnp.zeros((hot.shape[2], LANES), F32)
    bias_sum = jnp.zeros((BIAS_COLS, LANES), F32)
    for index in range(clips):
        value = bias_grad[index]
        bias_sum = bias_sum + value
        value = value[: hot.shape[1]]
        high = value.astype(BF)
        low = (value - high.astype(F32)).astype(BF)
        time_sum = time_sum + dot_f32(hot[index], high, ((0,), (0,)))
        time_sum = time_sum + dot_f32(hot[index], low, ((0,), (0,)))
    put(plan["time"], time_sum[:table_rows])
    high = bias_sum.astype(BF)
    low = (bias_sum - high.astype(F32)).astype(BF)
    space_sum = dot_f32(space_hot[...], high, ((1,), (0,)))
    space_sum = space_sum + dot_f32(space_hot[...], low, ((1,), (0,)))
    put(plan["space"], space_sum[: 2 * (2 * SIDE - 1)])

    gain_sum = jnp.zeros((1, model), F32)
    shift_sum = jnp.zeros((1, model), F32)
    for index in range(clips):
        cross_copy(index, 1 - head).wait_recv()
        incoming = row_full[index].astype(F32)
        centred, rate = row_stats(x[index].astype(F32))
        normal = centred * rate
        product = incoming * normal
        gain_sum = gain_sum + jnp.sum(product, axis=0, keepdims=True)
        shift_sum = shift_sum + jnp.sum(incoming, axis=0, keepdims=True)
        scaled = incoming * gain[0:1]
        mean_scaled = jnp.sum(scaled, axis=-1, keepdims=True) * (1.0 / model)
        mean_both = jnp.sum(scaled * normal, axis=-1, keepdims=True) * (1.0 / model)
        result = rate * (scaled - mean_scaled - normal * mean_both) + middle_grad[index]
        grad_in[index] = result.astype(BF)

    @pl.when(head == 0)
    def _():
        put_wide(plan["gain"], gain_sum)
        put_wide(plan["gain"] + wide_rows_count, vectors[0:1])
        put_wide(plan["shift"], shift_sum)
        put_wide(plan["shift"] + wide_rows_count, vectors[1:2])
        put_wide(plan["rows"], vectors[2:3])
        put_wide(plan["rows"] + wide_rows_count, vectors[3:4])

    def reduce_near(chunk):
        lanes = slice(chunk * cols, (chunk + 1) * cols)
        for step in range(1, 4):
            near_copy(chunk, step).wait_recv()

        def gathered(index):
            own = grads[index, place, :, lanes].astype(F32)
            own = own + near[chunk, 1, index].astype(F32)
            other = near[chunk, 0, index].astype(F32) + near[chunk, 2, index].astype(F32)
            return own, other

        def send(step):
            there = (outer + step) % outers
            own, other = gathered(there)
            part[chunk, there, 0] = own.astype(BF)
            part[chunk, there, 1] = other.astype(BF)
            far_copy(chunk, step).start()

        each(1, outers, send)
        own, other = gathered(outer)
        far[chunk, 0, 0] = own.astype(BF)
        far[chunk, 0, 1] = other.astype(BF)

    pair_sum().start()
    reduce_near(0)
    pair_sum().wait_recv()
    small[head] = small[head] + pair_in[...]
    for step in range(1, 4):
        plane_sum(step).start()
    for chunk in range(1, chunks):
        reduce_near(chunk)
    for step in range(1, 4):
        plane_sum(step).wait_recv()
    small[head, place] = small[head, place] + plane_in[0] + plane_in[1] + plane_in[2]
    each(1, outers, lambda step: line_sum(step).start())
    each(1, outers, lambda step: rest_copy(step).wait_recv())
    rest_out[...] = lax.fori_loop(
        1,
        outers,
        lambda step, sums: sums + rest_in[step].astype(F32),
        rest[outer].astype(F32),
    )
    each(1, outers, lambda step: line_sum(step).wait_recv())
    small_out[head, place, outer] = lax.fori_loop(
        1, outers, lambda step, sums: sums + line_in[step], small[head, place, outer]
    )
    each(1, outers, lambda step: line_share(step, outer).start())
    each(1, outers, lambda step: line_share(step, (outer + outers - step) % outers).wait_recv())
    for step in range(1, 4):
        plane_share(step, place).start()
    heads = cols // LANES
    group = heads * unit
    for chunk in range(chunks):
        each(1, outers, lambda step: far_copy(chunk, step).wait_recv())
        totals = []
        for side in range(2):
            totals.append(
                lax.fori_loop(
                    0,
                    outers,
                    lambda step, sums: sums + far[chunk, step, side].astype(F32),
                    jnp.zeros((shard_rows, cols), F32),
                )
            )

        def store(order):
            for spot, side in enumerate(order):
                for index in range(heads):
                    at = (2 * chunk + spot) * group + index * unit
                    value = totals[side][:, index * LANES : index * LANES + unit]
                    out[:, at : at + unit] = value

        @pl.when(frame == 0)
        def _():
            store((0, 1))

        @pl.when(frame == 1)
        def _():
            store((1, 0))

    for step in range(1, 4):
        plane_share(step, plane_place(step)).wait_recv()
    pair_share(head).start()
    pair_share(1 - head).wait_recv()
    pair_sum().wait_send()
    pair_share(head).wait_send()
    for step in range(1, 4):
        plane_sum(step).wait_send()
        plane_share(step, place).wait_send()
    each(1, outers, lambda step: line_sum(step).wait_send())
    each(1, outers, lambda step: line_share(step, outer).wait_send())
    each(1, outers, lambda step: rest_copy(step).wait_send())
    for index in range(clips):
        cross_copy(index, head).wait_send()
    for chunk in range(chunks):
        for step in range(1, 4):
            near_copy(chunk, step).wait_send()
        each(1, outers, lambda step: far_copy(chunk, step).wait_send())


def unpack_kernel(
    small, qkv, early, late, grad_in, block_out,
    grad_in_out, block_out_out, gain_out, shift_out, rows_out, joined_out, up_out, taps_out,
    pool_gain_out, pool_shift_out, squeeze_out, time_out, space_out, qkv_out, proj_out,
    up_grad_out, down_out, time_rows, *, plan, unit,
):
    for index in range(grad_in.shape[0]):
        grad_in_out[index] = grad_in[index]
        block_out_out[index] = block_out[index]
    head = lax.axis_index("head")
    rows_small = small.shape[1]

    def take(row, target):
        count = target.shape[0]
        done = 0
        while done < count:
            block, offset = divmod(row + done, rows_small)
            size = min(count - done, rows_small - offset)
            target[done : done + size] = small[block, offset : offset + size, : target.shape[1]]
            done += size

    def take_wide(row, target, at):
        for index in range(target.shape[1] // LANES):
            block, offset = divmod(row + index, rows_small)
            target[at : at + 1, index * LANES : (index + 1) * LANES] = small[
                block, offset : offset + 1
            ]

    per_row = gain_out.shape[1] // LANES
    for index in range(2):
        take_wide(plan["gain"] + index * per_row, gain_out, index)
        take_wide(plan["shift"] + index * per_row, shift_out, index)
        take_wide(plan["rows"] + index * per_row, rows_out, index)
    width = joined_out.shape[1]
    group = width // 2
    heads = group // unit
    joined_rows = 3 * heads
    up_rows = up_out.shape[0]
    for which in range(2):

        @pl.when(head == which)
        def _():
            for member in range(3):
                for side in range(2):
                    for index in range(heads):
                        row = plan["joined"] + (2 * which + side) * joined_rows
                        block, offset = divmod(row + member * heads + index, rows_small)
                        at = side * group + index * unit
                        joined_out[member : member + 1, at : at + unit] = small[
                            block, offset : offset + 1, :unit
                        ]
            take(plan["up"] + which * up_rows, up_out)

    for member in range(3):
        take(plan["taps"] + member * 27, taps_out.at[member])
        qkv_out[member] = qkv[:, member * width : (member + 1) * width]
    take(plan["pool_gain"], pool_gain_out)
    take(plan["pool_shift"], pool_shift_out)
    take(plan["time"], time_rows)
    time_out[...] = time_rows[...].T
    for index in range(2):
        count = squeeze_out.shape[1]
        take(plan["squeeze"] + index * count, squeeze_out.at[index])
        for spot in range(space_out.shape[0]):
            block, offset = divmod(
                plan["space"] + index * space_out.shape[0] + spot, rows_small
            )
            space_out[spot, index : index + 1] = small[block, offset : offset + 1, :unit]
    proj_width, up_width = proj_out.shape[1], up_grad_out.shape[1]
    proj_out[...] = early[:, :proj_width]
    up_grad_out[...] = early[:, proj_width : proj_width + up_width]
    at = proj_width + up_width
    first = early.shape[1] - at
    down_out[:, :first] = early[:, at:]
    down_out[:, first:] = late[...]


def unpack(small, qkv, early, late, grad_in, block_out, plan, unit, hidden_width, table_rows):
    shard_rows, width = qkv.shape
    model = grad_in.shape[2]
    rest_width = early.shape[1] + late.shape[1]
    out = jax.ShapeDtypeStruct
    vmem = pl.BlockSpec(memory_space=pltpu.VMEM)
    shapes = [
        out(grad_in.shape, BF),
        out(block_out.shape, BF),
        out((2, model), F32),
        out((2, model), F32),
        out((2, model), F32),
        out((3, width // 3), F32),
        out((hidden_width // LANES, LANES), F32),
        out((3, 27, unit), F32),
        out((3, unit), F32),
        out((3, unit), F32),
        out((2, FRAMES // MEMF, unit), F32),
        out((unit, table_rows), F32),
        out((2 * SIDE - 1, 2, unit), F32),
        out((3, shard_rows, width // 3), F32),
        out((shard_rows, rest_width - 2 * hidden_width), F32),
        out((shard_rows, hidden_width), F32),
        out((shard_rows, hidden_width), F32),
    ]
    return pl.pallas_call(
        partial(unpack_kernel, plan=plan, unit=unit),
        in_specs=[vmem] * 6,
        out_specs=[vmem] * len(shapes),
        out_shape=shapes,
        scratch_shapes=[pltpu.VMEM((table_rows, unit), F32)],
        compiler_params=pltpu.CompilerParams(vmem_limit_bytes=VMEM_LIMIT),
        name="unpack_results",
    )(small, qkv, early, late, grad_in, block_out)


def tail(
    row_own, row_recv, x, middle_grad, grads, joined_sum, gain, taps, pool_gain, pool_shift,
    bias_grad, hot, space_hot, cached, mem_own, mem_recv, vectors, up_bias, rest, clip_count, devices,
    unit, table_rows,
):
    clips, rows, model = x.shape
    wide = grads.shape[3]
    heads = wide // (3 * LANES)
    width = 3 * 2 * heads * unit
    outers = clip_count // 2
    shard_rows = model // (4 * outers)
    chunks = 3
    cols = wide // chunks
    plan = {}
    at = 0
    for name, count in (
        ("gain", 2 * model // LANES),
        ("shift", 2 * model // LANES),
        ("rows", 2 * model // LANES),
        ("joined", 4 * wide // LANES),
        ("up", 2 * up_bias.shape[1] // LANES),
        ("taps", 81),
        ("pool_gain", 3),
        ("pool_shift", 3),
        ("squeeze", 2 * FRAMES // MEMF),
        ("time", table_rows),
        ("space", 2 * (2 * SIDE - 1)),
    ):
        plan[name] = at
        at += count
    block = -(-at // (devices * 8)) * 8
    small_shape = (2, 4, outers, block, LANES)
    out = jax.ShapeDtypeStruct
    dma = pltpu.SemaphoreType.DMA
    vmem = pl.BlockSpec(memory_space=pltpu.VMEM)
    shapes = [
        out((clips, rows, model), BF),
        out((shard_rows, width), F32),
        out((shard_rows, rest.shape[2]), F32),
        out(small_shape, F32),
    ]
    results = pl.pallas_call(
        partial(tail_kernel, unit=unit, plan=plan, table_rows=table_rows),
        in_specs=[vmem] * 19,
        out_specs=[vmem] * len(shapes),
        out_shape=shapes,
        scratch_shapes=[
            pltpu.VMEM((chunks, 3, outers, shard_rows, cols), BF),
            pltpu.VMEM((chunks, outers, 2, shard_rows, cols), BF),
            pltpu.VMEM((chunks, outers, 2, shard_rows, cols), BF),
            pltpu.VMEM(small_shape, F32),
            pltpu.VMEM(small_shape[1:], F32),
            pltpu.VMEM((3,) + small_shape[2:], F32),
            pltpu.VMEM(small_shape[2:], F32),
            pltpu.VMEM((clips, rows, model), BF),
            pltpu.VMEM(rest.shape, BF),
            dma((2, clips)),
            dma((2, chunks, 3)),
            dma((2, chunks, outers)),
            dma((2, 2)),
            dma((2, 2, 3)),
            dma((2, 2, outers)),
            dma((2, outers)),
        ],
        compiler_params=pltpu.CompilerParams(
            collective_id=0, has_side_effects=True, vmem_limit_bytes=VMEM_LIMIT
        ),
        name="tail_gradients",
    )(
        row_own, row_recv, x, middle_grad, grads, joined_sum, gain, taps, pool_gain, pool_shift,
        bias_grad, hot, space_hot, cached, mem_own, mem_recv, vectors, up_bias, rest,
    )
    return results, plan


def feed_kernel(
    att_own, att_recv, x, cot, weights, gain, shift, out_shift, up_shift,
    block_out, middle_grad, grad_own, grad_send, grad_rest, vectors, up_bias,
    attended, normed, cots, active, hidden_low, branch, middle, send, recv, sems,
):
    clips, rows, model = x.shape
    span = attended.shape[0] // clips
    group = att_own.shape[2]
    head_width = 2 * group
    hidden_width = up_shift.shape[1]
    tiles = 4
    tile = hidden_width // tiles
    clip_at = lax.axis_index("clip")
    frame = lax.axis_index("frame")
    head = lax.axis_index("head")
    partner = (clip_at, frame, 1 - head)

    def cross(kind, index):
        return pltpu.make_async_remote_copy(
            src_ref=send.at[kind, index], dst_ref=recv.at[kind, index],
            send_sem=sems.at[0, kind, index], recv_sem=sems.at[1, kind, index],
            device_id=partner, device_id_type=MESH_ID,
        )

    barrier = pltpu.get_barrier_semaphore()
    pl.semaphore_signal(barrier, inc=1, device_id=partner, device_id_type=MESH_ID)
    for ref in (attended, normed, cots, branch):
        ref[...] = jnp.zeros_like(ref)

    def assemble(low, high):
        for index in range(clips):
            at = slice(index * span, index * span + rows)
            attended[at, :group] = low[index]
            attended[at, group:] = high[index]

    @pl.when(frame == 0)
    def _():
        assemble(att_own, att_recv)

    @pl.when(frame == 1)
    def _():
        assemble(att_recv, att_own)

    for index in range(clips):
        cots[index * span : index * span + rows] = cot[index]
    pl.semaphore_wait(barrier, 1)

    def block_rows(index):
        return pl.ds(pl.multiple_of(index * span, 16), span)

    def project(index):
        part = dot_f32(attended[block_rows(index)], weights[:, :head_width], ((1,), (1,)))
        send[0, index] = part[:rows].astype(BF)
        cross(0, index).start()

    each(0, clips, project)

    def feed(index, bias_sum):
        cross(0, index).wait_recv()
        branch_rows = send[0, index].astype(F32) + recv[0, index].astype(F32)
        value = x[index].astype(F32) + branch_rows + out_shift[0:1]
        middle[index] = value
        centred, rate = row_stats(value)
        low = (centred * rate * gain[1:2] + shift[1:2]).astype(BF)
        at = pl.multiple_of(index * span, 16)
        normed[pl.ds(at, rows)] = low
        low = normed[block_rows(index)]
        cot_rows = cots[block_rows(index)]
        out_part = jnp.zeros((span, model), F32)
        norm_part = jnp.zeros((span, model), F32)
        sums = []
        for step in range(tiles):
            lanes = slice(step * tile, (step + 1) * tile)
            up = weights[:, head_width + step * tile : head_width + (step + 1) * tile]
            at = head_width + hidden_width + step * tile
            down = weights[:, at : at + tile]
            hidden = dot_f32(low, up, ((1,), (0,))) + up_shift[:, lanes]
            incoming = dot_f32(cot_rows, down, ((1,), (0,)))
            normal = 0.5 * (1.0 + lax.erf(hidden * (0.5**0.5)))
            density = jnp.exp(hidden * hidden * -0.5) * ((2.0 * np.pi) ** -0.5)
            acted = (hidden * normal).astype(BF)
            back = (incoming * (normal + hidden * density)).astype(BF)
            active[block_rows(index), lanes] = acted
            hidden_low[block_rows(index), lanes] = back
            sums.append(jnp.sum(back.astype(F32), axis=0, keepdims=True))
            out_part = out_part + dot_f32(acted, down, ((1,), (1,)))
            norm_part = norm_part + dot_f32(back, up, ((1,), (1,)))
        send[1, index] = norm_part[:rows].astype(BF)
        cross(1, index).start()
        send[2, index] = out_part[:rows].astype(BF)
        cross(2, index).start()
        return bias_sum + jnp.concatenate(sums, axis=1)

    up_bias[...] = lax.fori_loop(0, clips, feed, jnp.zeros((1, hidden_width), F32))

    wide = hidden_width // 2
    for step in range(2):
        lanes = slice(step * wide, (step + 1) * wide)
        value = dot_f32(normed[...], hidden_low[:, lanes], ((0,), (0,)))
        at = head_width + step * wide
        grad_rest[:, at : at + wide] = value.astype(BF)
        value = dot_f32(cots[...], active[:, lanes], ((0,), (0,)))
        at = head_width + hidden_width + step * wide
        grad_rest[:, at : at + wide] = value.astype(BF)

    def back(index, sums):
        gain_sum, shift_sum, first_sum, second_sum = sums
        cross(1, index).wait_recv()
        incoming = send[1, index].astype(F32) + recv[1, index].astype(F32)
        centred, rate = row_stats(middle[index])
        normal = centred * rate
        scaled = incoming * gain[1:2]
        mean_scaled = jnp.sum(scaled, axis=-1, keepdims=True) * (1.0 / model)
        mean_both = jnp.sum(scaled * normal, axis=-1, keepdims=True) * (1.0 / model)
        cot_rows = cot[index].astype(F32)
        value = cot_rows + rate * (scaled - mean_scaled - normal * mean_both)
        middle_grad[index] = value
        at = pl.multiple_of(index * span, 16)
        branch[pl.ds(at, rows)] = value.astype(BF)
        part = dot_f32(branch[block_rows(index)], weights[:, :head_width], ((1,), (0,)))
        part = part[:rows].astype(BF)

        @pl.when(frame == 0)
        def _():
            grad_own[index] = part[:, :group]
            grad_send[index] = part[:, group:]

        @pl.when(frame == 1)
        def _():
            grad_send[index] = part[:, :group]
            grad_own[index] = part[:, group:]

        cross(2, index).wait_recv()
        out_rows = send[2, index].astype(F32) + recv[2, index].astype(F32)
        block_out[index] = (middle[index] + out_rows + out_shift[1:2]).astype(BF)

        def column(rows_here):
            return jnp.sum(rows_here, axis=0, keepdims=True)

        return (
            gain_sum + column(incoming * normal),
            shift_sum + column(incoming),
            first_sum + column(value),
            second_sum + column(cot_rows),
        )

    start = tuple(jnp.zeros((1, model), F32) for _ in range(4))
    sums = lax.fori_loop(0, clips, back, start)
    for row in range(4):
        vectors[row : row + 1] = sums[row]
    value = dot_f32(branch[...], attended[...], ((0,), (0,)))
    grad_rest[:, :head_width] = value.astype(BF)
    for kind in range(3):
        each(0, clips, lambda index: cross(kind, index).wait_send())


def feed(att_own, att_recv, x, cot, weights, gain, shift, out_shift, up_shift):
    clips, rows, model = x.shape
    group = att_own.shape[2]
    hidden_width = up_shift.shape[1]
    span = -(-rows // 16) * 16
    out = jax.ShapeDtypeStruct
    vmem = pl.BlockSpec(memory_space=pltpu.VMEM)
    shapes = [
        out((clips, rows, model), BF),
        out((clips, rows, model), F32),
        out((clips, rows, group), BF),
        out((clips, rows, group), BF),
        out(weights.shape, BF),
        out((4, model), F32),
        out((1, hidden_width), F32),
    ]
    return pl.pallas_call(
        feed_kernel,
        in_specs=[vmem] * 9,
        out_specs=[vmem] * len(shapes),
        out_shape=shapes,
        scratch_shapes=[
            pltpu.VMEM((clips * span, 2 * group), BF),
            pltpu.VMEM((clips * span, model), BF),
            pltpu.VMEM((clips * span, model), BF),
            pltpu.VMEM((clips * span, hidden_width), BF),
            pltpu.VMEM((clips * span, hidden_width), BF),
            pltpu.VMEM((clips * span, model), BF),
            pltpu.VMEM((clips, rows, model), F32),
            pltpu.VMEM((3, clips, rows, model), BF),
            pltpu.VMEM((3, clips, rows, model), BF),
            pltpu.SemaphoreType.DMA((2, 3, clips)),
        ],
        compiler_params=pltpu.CompilerParams(
            collective_id=4, has_side_effects=True, vmem_limit_bytes=VMEM_LIMIT
        ),
        name="feed_forward_both_ways",
    )(att_own, att_recv, x, cot, weights, gain, shift, out_shift, up_shift)


def precise(pattern, *operands):
    return jnp.einsum(pattern, *operands, precision=lax.Precision.HIGHEST)


def split_groups(value, which, axis):
    half = value.shape[axis] // 2
    low = lax.slice_in_dim(value, 0, half, axis=axis)
    high = lax.slice_in_dim(value, half, None, axis=axis)
    first = which == 0
    return jnp.where(first, low, high), jnp.where(first, high, low)


def join_groups(own, peer, which, axis):
    first = which == 0
    return jnp.concatenate([jnp.where(first, own, peer), jnp.where(first, peer, own)], axis=axis)


def time_choices(stride_group, memory_place, which, own, table_rows):
    local = jnp.arange(own, dtype=jnp.int32)
    times = jnp.concatenate([which * own + local, (1 - which) * own + local])
    stride = jnp.left_shift(jnp.int32(2), stride_group)[:, None, None]
    offset = 8 * (FRAMES - 1)
    current = stride * (times[None, :, None] - times[None, None, :]) + offset
    slots = [memory_place[:, index : index + 1] for index in range(4)]
    first = jnp.concatenate([slots[2], slots[0], slots[3], slots[1]], axis=1)
    second = jnp.concatenate([slots[3], slots[1], slots[2], slots[0]], axis=1)
    places = jnp.where(which == 0, first, second)
    memory = stride * times[None, :, None] + places[:, None, :] + offset
    chosen = jnp.concatenate([current, memory], axis=2)
    return (chosen[..., None] == jnp.arange(table_rows, dtype=jnp.int32)).astype(F32)


def space_choices():
    places = np.arange(SIDE)
    offsets = places[:, None] - places[None, :] + SIDE - 1
    hot = offsets.reshape(-1)[:, None] == np.arange(2 * SIDE - 1)[None, :]
    return jnp.asarray(hot.astype(np.float32))


def space_sums():
    spans = 2 * SIDE - 1
    hot = np.zeros((32, BIAS_COLS), np.float32)
    for axis in range(2):
        for query in range(SIDE):
            for key in range(SIDE):
                col = SPACE_AT + axis * CELLS + query * SIDE + key
                hot[axis * spans + query - key + SIDE - 1, col] = 1.0
    return hot


def wide_rows(rows, heads):
    count, members, unit = rows.shape
    padded = jnp.pad(rows, ((0, 0), (0, 0), (0, LANES - unit)))
    spread = jnp.broadcast_to(padded[:, :, None], (count, members, heads, LANES))
    return spread.reshape(count, members * heads * LANES)


def local(
    clips_in,
    cached_kv,
    old_memory,
    stride_group,
    memory_place,
    norm_gain,
    norm_shift,
    qkv_weight,
    qkv_shift,
    pool_kernel,
    pool_gain,
    pool_shift,
    squeeze_kernel,
    time_table,
    space_tables,
    proj_weight,
    out_shift,
    up_weight,
    up_shift,
    down_weight,
    cotangent,
):
    clip_count, rows_clip, model_width = clips_in.shape
    head_width = qkv_weight.shape[2]
    unit = pool_gain.shape[1]
    head_count = head_width // unit
    frame_count = lax.axis_size("frame")
    heads = head_count // frame_count
    own_frames = rows_clip // CELLS
    group_width = heads * unit
    group_span = FRAMES // MEMF
    scale = unit ** (-0.5)
    which = lax.axis_index("frame")
    into_np, outof_np = placement(frame_count)
    keys_np, mask_np, pad_np = bias_constants(frame_count)
    consts = (
        jnp.asarray(into_np, BF),
        jnp.asarray(outof_np, BF),
        jnp.asarray(keys_np, BF),
        jnp.asarray(mask_np),
        jnp.asarray(pad_np),
    )

    cached_flat = cached_kv.reshape(clip_count, rows_clip, 2 * head_width)
    time_hot = time_choices(stride_group, memory_place, which, own_frames, time_table.shape[0])
    time_rows = precise("ctkr,rd->ctkd", time_hot, time_table).reshape(clip_count, -1, unit)
    space_hot = space_choices()
    space_rows = precise("pr,xrd->xpd", space_hot, space_tables).reshape(2 * CELLS, unit)
    space_rows = jnp.broadcast_to(space_rows[None], (clip_count,) + space_rows.shape)
    bias = jnp.concatenate(
        [
            jnp.pad(time_rows, ((0, 0), (0, SPACE_AT - time_rows.shape[1]), (0, LANES - unit))),
            jnp.pad(
                space_rows,
                ((0, 0), (0, BIAS_COLS - SPACE_AT - 2 * CELLS), (0, LANES - unit)),
            ),
        ],
        axis=1,
    )
    bias = bias * (1.0 / scale)
    inputs = (
        clips_in, qkv_weight.transpose(1, 0, 2), norm_gain, norm_shift, qkv_shift, cached_flat,
        old_memory.reshape(clip_count, -1, 2 * head_width), squeeze_kernel, proj_weight.T, up_weight,
        down_weight.T,
    )
    clip_axis = lax.axis_size("clip")
    if qkv_weight.shape[0] % 16:
        attn_group, packed, normed, mem_own, mem_peer, column = project_plain(
            *inputs, clip_axis, unit
        )
        forward = attention_forward(
            packed, mem_own, mem_peer, column, consts, pool_kernel, pool_gain, pool_shift, bias,
            scale, unit, rows_clip,
        )
    else:
        attn_group, packed, normed, *forward = front(
            *inputs, consts, pool_kernel, pool_gain, pool_shift, bias, scale, clip_axis, unit
        )
    attended_own, attended_peer, rest_full = forward[:3]
    rest_full = rest_full.reshape(model_width, -1)
    saved = forward[3:]
    block_out, middle_grad, attended_grad_own, attended_grad_send, grad_rest, vectors, up_grads = (
        feed(
            attended_own, attended_peer, clips_in, cotangent, rest_full, norm_gain,
            norm_shift, out_shift, up_shift.reshape(1, -1),
        )
    )
    outers = lax.axis_size("clip") // 2
    grad_rest = grad_rest.reshape(outers, 4, -1, grad_rest.shape[1])
    backward = attention_backward(
        packed, normed, attn_group, attended_grad_own, attended_grad_send, grad_rest, consts,
        pool_kernel, pool_gain, bias, saved, scale, unit,
    )
    row_own, row_recv, mem_grad_own, mem_grad_peer = backward[:4]
    taps_grad, pool_gain_grad, pool_shift_grad, bias_grad = backward[4:8]
    attn_grad, joined_grad, rest_part, rest_early = backward[8:]

    time_count = time_rows.shape[1]
    hot = time_hot.reshape(clip_count, time_count, -1).astype(BF)
    hot = jnp.pad(hot, ((0, 0), (0, 0), (0, -hot.shape[2] % LANES)))
    devices = lax.axis_size("clip") * frame_count * lax.axis_size("head")
    (grad_in, qkv_shard, rest_late, small), plan = tail(
        row_own, row_recv, clips_in, middle_grad,
        attn_grad.reshape(outers, 4, -1, attn_grad.shape[1]), joined_grad, norm_gain, taps_grad,
        pool_gain_grad, pool_shift_grad, bias_grad, hot,
        jnp.asarray(space_sums(), BF), cached_flat, mem_grad_own, mem_grad_peer, vectors,
        up_grads, rest_part, lax.axis_size("clip"), devices, unit, time_table.shape[0],
    )
    (
        grad_in, block_out, gain_sums, shift_sums, out_sums, qkv_bias_sum, up_bias_sum, kernel_sum,
        pool_gain_sum, pool_shift_sum, squeeze_sum, time_sum, space_sum, qkv_shard, proj_shard,
        up_shard, down_shard,
    ) = unpack(
        small.reshape((devices,) + small.shape[3:]), qkv_shard, rest_early, rest_late, grad_in, block_out, plan, unit,
        up_weight.shape[1], time_table.shape[0],
    )
    return (
        block_out,
        grad_in,
        gain_sums,
        shift_sums,
        qkv_shard.transpose(1, 0, 2),
        qkv_bias_sum,
        kernel_sum,
        pool_gain_sum,
        pool_shift_sum,
        squeeze_sum,
        time_sum.T,
        space_sum.transpose(1, 0, 2),
        proj_shard.T,
        out_sums,
        up_shard,
        up_bias_sum.reshape(-1),
        down_shard.T,
    )


def solution(mesh):
    return jax.shard_map(
        local,
        mesh=mesh,
        in_specs=(
            P("clip", "frame", None),
            P("clip", "frame", None, "head"),
            P("clip", "frame", None, "head"),
            P("clip"),
            P("clip", None),
            P(),
            P(),
            P(("clip", "frame"), None, "head"),
            P(None, "head"),
            P(),
            P(),
            P(),
            P(),
            P(),
            P(),
            P("head", ("clip", "frame")),
            P(),
            P(("clip", "frame"), "head"),
            P("head"),
            P("head", ("clip", "frame")),
            P("clip", "frame", None),
        ),
        out_specs=(
            P("clip", "frame", None),
            P("clip", "frame", None),
            P(),
            P(),
            P(("clip", "frame"), None, "head"),
            P(None, "head"),
            P(),
            P(),
            P(),
            P(),
            P(),
            P(),
            P("head", ("clip", "frame")),
            P(),
            P(("clip", "frame"), "head"),
            P("head"),
            P("head", ("clip", "frame")),
        ),
        check_vma=False,
    )
```

```python
from functools import partial

import jax
import jax.numpy as jnp
import numpy as np
from jax import lax
from jax.experimental import pallas as pl
from jax.experimental.pallas import tpu as pltpu
from jax.sharding import PartitionSpec as P

FRAMES = 8
MEMF = 2
SIDE = 7
CELLS = SIDE * SIDE
LANES = 128
HALF = 208
QROWS = 2 * HALF
GRID_ROWS = FRAMES * SIDE * 8
MEM_AT = QROWS
MEM_PAD = 112
MEM_BACK = 64
MEM_STEP = 56
TURN_STEP = 3
TURN_PAIRS = 1
TURN_LAG = 4
KROWS = 640
BIAS_COLS = 256
SPACE_AT = 128
PAD_LANE = 127
BF = jnp.bfloat16
F32 = jnp.float32
VMEM_LIMIT = 60 * 1024 * 1024
MESH_ID = pl.DeviceIdType.MESH


def dot_f32(a, b, dims):
    return lax.dot_general(a, b, (dims, ((), ())), preferred_element_type=F32)


def frame_order(first, own):
    rest = [t for t in range(FRAMES) if not first * own <= t < (first + 1) * own]
    return list(range(first * own, (first + 1) * own)) + rest


def placement(frame_count):
    own = FRAMES // frame_count
    into = np.zeros((frame_count, GRID_ROWS, QROWS), np.float32)
    for first in range(frame_count):
        for slot, frame in enumerate(frame_order(first, own)):
            base = (slot // own) * HALF + (slot % own) * CELLS
            for high in range(SIDE):
                for wide in range(SIDE):
                    row = (frame * SIDE + high) * 8 + wide
                    into[first, row, base + high * SIDE + wide] = 1.0
    return into, np.ascontiguousarray(into.transpose(0, 2, 1))


def bias_constants(frame_count):
    own = FRAMES // frame_count
    frames_all = FRAMES + 2 * MEMF
    keys = np.zeros((BIAS_COLS, KROWS), np.float32)
    valid = np.zeros((KROWS,), bool)

    def mark(col, slot, high, wide):
        valid[col] = True
        for query in range(FRAMES):
            keys[query * frames_all + slot, col] = 1.0
        for place in range(SIDE):
            keys[SPACE_AT + place * SIDE + high, col] = 1.0
            keys[SPACE_AT + CELLS + place * SIDE + wide, col] = 1.0

    mask = np.zeros((QROWS, BIAS_COLS), np.float32)
    for slot in range(FRAMES):
        base = (slot // own) * HALF + (slot % own) * CELLS
        for high in range(SIDE):
            for wide in range(SIDE):
                row = base + high * SIDE + wide
                mark(row, slot, high, wide)
                mask[row, slot * frames_all : (slot + 1) * frames_all] = 1.0
                mask[row, SPACE_AT + high * SIDE : SPACE_AT + (high + 1) * SIDE] = 1.0
                low = SPACE_AT + CELLS + wide * SIDE
                mask[row, low : low + SIDE] = 1.0
    for group in range(2):
        for inner in range(MEMF):
            slot = FRAMES + group * MEMF + inner
            for high in range(SIDE):
                for wide in range(SIDE):
                    col = MEM_AT + group * MEM_PAD + inner * MEM_STEP + high * SIDE + wide
                    mark(col, slot, high, wide)
    keys[PAD_LANE, ~valid] = -1e9
    pad_row = np.zeros((1, BIAS_COLS), np.float32)
    pad_row[0, PAD_LANE] = 1.0
    return keys, mask, pad_row


def spread_heads(source, target, rows_at, units, unit, first=0):
    count = source.shape[0]
    for index in range(units):
        at = (first + index) * unit
        target[rows_at : rows_at + count, index * LANES : index * LANES + unit] = source[
            :, at : at + unit
        ]


def spread_tables(kernel_ref, taps, pairs, heads, unit):
    taps[...] = jnp.zeros_like(taps)
    for _, target in pairs:
        target[...] = jnp.zeros_like(target)
    for member in range(3):
        for index in range(heads):
            at = (member * heads + index) * LANES
            for tap in range(27):
                row = kernel_ref[member, tap : tap + 1]
                taps[tap, :, at : at + unit] = jnp.broadcast_to(row, (8, unit))
            for source, target in pairs:
                target[:, at : at + unit] = source[member : member + 1]


def load_shifted(field, shifted):
    grid = field.reshape(FRAMES, SIDE, 8, field.shape[-1])
    flat = field.reshape(FRAMES * SIDE, 8, field.shape[-1])
    shifted[1, 1 : FRAMES + 1, 1 : SIDE + 1] = grid
    shifted[0, 1 : FRAMES + 1, 1 : SIDE + 1] = pltpu.roll(flat, 1, 1).reshape(grid.shape)
    shifted[2, 1 : FRAMES + 1, 1 : SIDE + 1] = pltpu.roll(flat, 7, 1).reshape(grid.shape)


def convolve(shifted, taps, target, flip):
    tiles = target.shape[-1] // LANES

    def step(pair, carry):
        for sub in range(2):
            frame = pair * 2 + sub
            for tile in range(tiles):
                lanes = slice(tile * LANES, (tile + 1) * LANES)
                total = None
                for i in range(3):
                    for k in range(3):
                        rows = shifted[k, frame + i, :, :, lanes]
                        for j in range(3):
                            if flip:
                                tap = (2 - i) * 9 + (2 - j) * 3 + (2 - k)
                            else:
                                tap = i * 9 + j * 3 + k
                            value = rows[j : j + SIDE] * taps[tap, :, lanes][None]
                            total = value if total is None else total + value
                target[frame, :, :, lanes] = total
        return carry

    lax.fori_loop(0, FRAMES // 2, step, 0)


def tap_grads(shifted, grads, target):
    tiles = target.shape[-1] // LANES

    def step(index, carry):
        lanes = pl.ds(pl.multiple_of(index * LANES, LANES), LANES)

        def inner(frame, sums):
            centre = grads[frame + 1, 1 : SIDE + 1, :, lanes]
            new = []
            for i in range(3):
                for k in range(3):
                    rows = shifted[k, frame + i, :, :, lanes]
                    for j in range(3):
                        parts = [rows[j + high] * centre[high] for high in range(SIDE)]
                        parts.append(sums[len(new)])
                        while len(parts) > 1:
                            pairs = zip(parts[::2], parts[1::2])
                            parts = [left + right for left, right in pairs]
                        new.append(parts[0])
            return tuple(new)

        start = tuple(jnp.zeros((8, LANES), F32) for _ in range(27))
        sums = lax.fori_loop(0, FRAMES, inner, start, unroll=4)
        for i in range(3):
            for k in range(3):
                for j in range(3):
                    target[i * 9 + j * 3 + k, :, lanes] += sums[(i * 3 + k) * 3 + j]
        return carry

    lax.fori_loop(0, tiles, step, 0)


def head_stats(values, unit):
    average = jnp.sum(values, axis=-1, keepdims=True) * (1.0 / unit)
    lane = lax.broadcasted_iota(jnp.int32, values.shape, 1)
    centred = jnp.where(lane < unit, values - average, 0.0)
    variance = jnp.sum(centred * centred, axis=-1, keepdims=True) * (1.0 / unit)
    return centred, lax.rsqrt(variance + 1e-06)


def frame_partner():
    return (lax.axis_index("clip"), 1 - lax.axis_index("frame"), lax.axis_index("head"))


def partner_copy(source, target, send_sem, recv_sem):
    return pltpu.make_async_remote_copy(
        src_ref=source, dst_ref=target, send_sem=send_sem, recv_sem=recv_sem,
        device_id=frame_partner(), device_id_type=MESH_ID,
    )


def side_partner():
    clip = lax.axis_index("clip")
    across = (clip // 2) * 2 + 1 - clip % 2
    return (across, lax.axis_index("frame"), lax.axis_index("head"))


def side_copy(source, target, send_sem, recv_sem):
    return pltpu.make_async_remote_copy(
        src_ref=source, dst_ref=target, send_sem=send_sem, recv_sem=recv_sem,
        device_id=side_partner(), device_id_type=MESH_ID,
    )


def greet_partner():
    barrier = pltpu.get_barrier_semaphore()
    pl.semaphore_signal(barrier, inc=1, device_id=frame_partner(), device_id_type=MESH_ID)
    pl.semaphore_wait(barrier, 1)


def plane_stage(column_ref, rest_full, side_sems, pair_sems, turn_sems, own_sem):
    outers = column_ref.shape[0]
    split = min(TURN_PAIRS, outers)
    outer = lax.axis_index("clip") // 2
    inner = lax.axis_index("clip") % 2
    frame = lax.axis_index("frame")
    place = inner * 2 + frame
    side_place = (1 - inner) * 2 + frame
    pair_place = inner * 2 + 1 - frame
    turn_place = (1 - inner) * 2 + 1 - frame
    own_copy = pltpu.make_async_copy(column_ref, rest_full.at[:, place], own_sem)

    def side_move(at, source, target):
        return side_copy(source, target, side_sems.at[0, at], side_sems.at[1, at])

    def pair_move(at, source, target):
        return partner_copy(source, target, pair_sems.at[0, at], pair_sems.at[1, at])

    def to_side(at):
        return side_move(at, column_ref.at[at], rest_full.at[at, place])

    def to_pair(at):
        return pair_move(at, column_ref.at[at], rest_full.at[at, place])

    def turn_side(at):
        block = rest_full.at[at, pair_place]
        return side_copy(block, block, turn_sems.at[0, at], turn_sems.at[1, at])

    def turn_pair(at):
        block = rest_full.at[at, side_place]
        return partner_copy(block, block, turn_sems.at[0, at], turn_sems.at[1, at])

    def turned(at):
        block = rest_full.at[at, turn_place]
        return side_copy(block, block, turn_sems.at[0, at], turn_sems.at[1, at])

    def side_arrival(at):
        block = rest_full.at[at, side_place]
        return side_move(at, block, block)

    def pair_arrival(at):
        block = rest_full.at[at, pair_place]
        return pair_move(at, block, block)

    def send(at):
        to_side(at).start()
        to_pair(at).start()

    def spot(step):
        return (outer + step) % outers

    def turn(step):
        at = spot(step)
        if step < split:
            side_arrival(at).wait_recv()
            turn_pair(at).start()
        else:
            pair_arrival(at).wait_recv()
            turn_side(at).start()

    def finish():
        own_copy.wait()
        each(0, split, lambda step: pair_arrival(spot(step)).wait_recv())
        each(split, outers, lambda step: side_arrival(spot(step)).wait_recv())
        each(0, outers, lambda at: turned(at).wait_recv())
        each(0, split, lambda step: turn_pair(spot(step)).wait_send())
        each(split, outers, lambda step: turn_side(spot(step)).wait_send())
        each(0, outers, lambda at: to_side(at).wait_send())
        each(0, outers, lambda at: to_pair(at).wait_send())

    return own_copy, send, turn, finish


def attend_clip(
    packed, mem_own, mem_peer, frame, into_ref, outof_ref, gain_ref, shift_ref, bias_ref,
    keyhot_ref, mask_ref, pad_ref, out_own, out_peer, q_out, k_out, v_out, p_out, c_out, shifted,
    taps, heads, unit, scale, after_conv,
):
    units = 3 * heads
    own_rows = out_own.shape[0]
    load_shifted(dot_f32(into_ref[frame], packed[...], ((1,), (0,))), shifted)
    conv = c_out.at[0]
    convolve(shifted, taps, conv, False)
    after_conv()
    k_out[0, MEM_AT:, :] = jnp.zeros((KROWS - MEM_AT, heads * LANES), BF)
    v_out[0, MEM_AT:, :] = jnp.zeros((KROWS - MEM_AT, heads * LANES), BF)
    spread_heads(mem_own, k_out.at[0], MEM_AT, heads, unit, 0 * heads)
    spread_heads(mem_own, v_out.at[0], MEM_AT, heads, unit, 1 * heads)
    spread_heads(mem_peer, k_out.at[0], MEM_AT + MEM_PAD, heads, unit, 0 * heads)
    spread_heads(mem_peer, v_out.at[0], MEM_AT + MEM_PAD, heads, unit, 1 * heads)
    for index in range(units):
        lanes = slice(index * LANES, (index + 1) * LANES)
        block = conv[:, :, :, lanes].reshape(GRID_ROWS, LANES)
        centred, rate = head_stats(block, unit)
        normal = centred * rate * gain_ref[:, lanes] + shift_ref[:, lanes]
        parts = [normal.astype(BF)] if index % heads == 0 else parts + [normal.astype(BF)]
        if index % heads == heads - 1:
            whole = jnp.concatenate(parts, axis=1)
            rows = dot_f32(outof_ref[frame], whole, ((1,), (0,))).astype(BF)
            (q_out, k_out, v_out)[index // heads][0, 0:QROWS, :] = rows

    bias = bias_ref[0]
    bias_high = bias.astype(BF)
    bias_low = (bias - bias_high.astype(F32)).astype(BF)
    for head in range(heads):
        lanes = slice(head * LANES, (head + 1) * LANES)
        keys = k_out[0, :, lanes]
        values = v_out[0, :, lanes]
        for half in range(2):
            rows = slice(half * HALF, (half + 1) * HALF)
            query = q_out[0, rows, lanes]
            table = dot_f32(query, bias_high, ((1,), (1,))) + dot_f32(query, bias_low, ((1,), (1,)))
            table = table * mask_ref[rows, :] + pad_ref[...]
            table_high = table.astype(BF)
            table_low = (table - table_high.astype(F32)).astype(BF)
            scores = dot_f32(query, keys, ((1,), (1,)))
            scores = scores + dot_f32(table_high, keyhot_ref[...], ((1,), (0,)))
            scores = scores + dot_f32(table_low, keyhot_ref[...], ((1,), (0,)))
            top = jnp.max(scores, axis=-1, keepdims=True)
            weights = jnp.exp((scores - top) * scale)
            total = jnp.sum(weights, axis=-1, keepdims=True)
            probs = (weights * (1.0 / total)).astype(BF)
            p_out[0, head, rows, :] = probs
            mixed = dot_f32(probs, values, ((1,), (0,))) + query.astype(F32)
            target = (out_own, out_peer)[half]
            target[:, head * unit : (head + 1) * unit] = mixed[:own_rows, :unit].astype(BF)


def forward_kernel(
    packed_ref, mem_own_ref, mem_peer_ref, column_ref, into_ref, outof_ref, kernel_ref,
    pool_gain_ref, pool_shift_ref, bias_ref, keyhot_ref, mask_ref, pad_ref,
    out_own, out_recv, rest_full, q_out, k_out, v_out, p_out, c_out,
    shifted, taps, gain_ref, shift_ref, out_send, out_sems, side_sems, pair_sems, turn_sems,
    own_sem,
    *, heads, unit, scale,
):
    clip = pl.program_id(0)
    clips = out_send.shape[0]
    frame = lax.axis_index("frame")

    def out_copy(index):
        return partner_copy(
            out_send.at[index], out_recv.at[index], out_sems.at[0, index], out_sems.at[1, index]
        )

    own_copy, send, turn, finish = plane_stage(
        column_ref, rest_full, side_sems, pair_sems, turn_sems, own_sem
    )

    @pl.when(clip == 0)
    def _():
        barrier = pltpu.get_barrier_semaphore()
        for device in (frame_partner(), side_partner()):
            pl.semaphore_signal(barrier, inc=1, device_id=device, device_id_type=MESH_ID)
        pl.semaphore_wait(barrier, 2)
        each(0, column_ref.shape[0], send)
        own_copy.start()
        shifted[...] = jnp.zeros_like(shifted)
        pairs = ((pool_gain_ref, gain_ref), (pool_shift_ref, shift_ref))
        spread_tables(kernel_ref, taps, pairs, heads, unit)

    @pl.when(clip == jnp.minimum(TURN_STEP, clips - 1))
    def _():
        for step in range(column_ref.shape[0]):
            turn(step)

    attend_clip(
        packed_ref.at[0], mem_own_ref.at[0], mem_peer_ref.at[0], frame, into_ref, outof_ref,
        gain_ref, shift_ref, bias_ref, keyhot_ref, mask_ref, pad_ref, out_own.at[0],
        out_send.at[clip], q_out, k_out, v_out, p_out, c_out, shifted, taps, heads, unit, scale,
        lambda: None,
    )
    out_copy(clip).start()

    @pl.when(clip == clips - 1)
    def _():
        finish()
        for index in range(clips):
            out_copy(index).wait()


def backward_kernel(
    packed_ref, normed_ref, weight_ref, grad_own_ref, grad_send_ref, rest_ref, into_ref, outof_ref,
    kernel_ref, pool_gain_ref, bias_ref, keyhot_ref, mask_ref, q_ref, k_ref, v_ref, p_ref, c_ref,
    row_own, row_recv, mem_own, mem_recv, taps_out, gain_out, shift_out, bias_out, weight_out,
    joined_out, rest_part, rest_out,
    shifted, taps, gain_ref, grads, spread, pooled, peer, mem_send, rest_own, rest_side, rest_send,
    rest_peer, rest_sum, rest_far, weight_sum, keep, cross_send, cross_recv, row_send,
    grad_sems, mem_sems, own_sems, side_sems, rest_sems, far_sems, cross_sems, row_sems,
    *, heads, unit, scale,
):
    units = 3 * heads
    own_rows = grad_own_ref.shape[1]
    clip = pl.program_id(0)
    clips = peer.shape[0]
    clip_at = lax.axis_index("clip")
    frame = lax.axis_index("frame")
    head_at = lax.axis_index("head")

    def grad_copy(index):
        return partner_copy(
            grad_send_ref.at[index], peer.at[index], grad_sems.at[0, index], grad_sems.at[1, index]
        )

    def mem_copy(index):
        return partner_copy(
            mem_send.at[index], mem_recv.at[index], mem_sems.at[0, index], mem_sems.at[1, index]
        )

    def row_copy(index):
        return partner_copy(
            row_send.at[index], row_recv.at[index], row_sems.at[0, index], row_sems.at[1, index]
        )

    def cross_copy(index):
        return pltpu.make_async_remote_copy(
            src_ref=cross_send.at[index], dst_ref=cross_recv.at[index],
            send_sem=cross_sems.at[0, index], recv_sem=cross_sems.at[1, index],
            device_id=(clip_at, frame, 1 - head_at), device_id_type=MESH_ID,
        )

    def finish_rows(index):
        cross_copy(index).wait_recv()
        total = (keep[index].astype(F32) + cross_recv[index].astype(F32)).astype(BF)
        row_own[index] = total[:own_rows]
        row_send[index] = total[HALF : HALF + own_rows]
        row_copy(index).start()

    chunks, outers, _, _, cols = rest_own.shape
    side_at = clip_at % 2
    outer = clip_at // 2
    early = rest_far.shape[0]

    def rest_at(side, chunk):
        return rest_ref.at[:, pl.ds(side * 2, 2), :, pl.ds(chunk * cols, cols)]

    def own_copy(chunk):
        return pltpu.make_async_copy(
            rest_at(side_at, chunk), rest_own.at[chunk], own_sems.at[chunk]
        )

    def over_copy(chunk):
        return side_copy(
            rest_at(1 - side_at, chunk), rest_side.at[chunk], side_sems.at[0, chunk],
            side_sems.at[1, chunk],
        )

    def rest_copy(chunk):
        return partner_copy(
            rest_send.at[chunk], rest_peer.at[chunk], rest_sems.at[0, chunk],
            rest_sems.at[1, chunk],
        )

    def pass_on(chunk):
        own_copy(chunk).wait()
        over_copy(chunk).wait_recv()

        def add(index):
            def total(part):
                first = rest_own[chunk, index, part].astype(F32)
                return (first + rest_side[chunk, index, part].astype(F32)).astype(BF)

            rest_send[chunk, index] = total(1 - frame)
            rest_sum[chunk, index] = total(frame)

        each(0, outers, add)
        rest_copy(chunk).start()

    def far_device(step):
        return (((outer + step) % outers) * 2 + side_at, frame, head_at)

    def far_copy(chunk, step):
        there = (outer + step) % outers
        return pltpu.make_async_remote_copy(
            src_ref=rest_sum.at[chunk, there], dst_ref=rest_far.at[chunk, step],
            send_sem=far_sems.at[0, chunk, step], recv_sem=far_sems.at[1, chunk, step],
            device_id=far_device(step), device_id_type=MESH_ID,
        )

    def settle(chunk):
        rest_copy(chunk).wait_recv()

        def add(index):
            total = rest_sum[chunk, index].astype(F32) + rest_peer[chunk, index].astype(F32)
            if chunk < early:
                rest_sum[chunk, index] = total.astype(BF)
            else:
                rest_part[index] = total.astype(BF)

        each(0, outers, add)
        if chunk < early:
            each(1, outers, lambda step: far_copy(chunk, step).start())

    @pl.when(clip == 0)
    def _():
        barrier = pltpu.get_barrier_semaphore()

        def greet(device):
            pl.semaphore_signal(barrier, inc=1, device_id=device, device_id_type=MESH_ID)

        for device in (frame_partner(), side_partner(), (clip_at, frame, 1 - head_at)):
            greet(device)
        each(1, outers, lambda step: greet(far_device(step)))
        pl.semaphore_wait(barrier, 3 + outers - 1)
        for index in range(clips):
            grad_copy(index).start()
        over_copy(0).start()
        own_copy(0).start()
        shifted[...] = jnp.zeros_like(shifted)
        grads[...] = jnp.zeros_like(grads)
        spread[...] = jnp.zeros_like(spread)
        taps_out[...] = jnp.zeros_like(taps_out)
        gain_out[...] = jnp.zeros_like(gain_out)
        shift_out[...] = jnp.zeros_like(shift_out)
        weight_sum[...] = jnp.zeros_like(weight_sum)
        joined_out[...] = jnp.zeros_like(joined_out)
        spread_tables(kernel_ref, taps, ((pool_gain_ref, gain_ref),), heads, unit)

    def pump(odd):
        for chunk in range(chunks):
            point = min(chunk + 1, 2 * clips - 1)
            if point % 2 == odd:

                @pl.when(clip == point // 2)
                def _():
                    if chunk + 1 < chunks:
                        over_copy(chunk + 1).start()
                        own_copy(chunk + 1).start()
                    pass_on(chunk)
                    if chunk:
                        settle(chunk - 1)

    pump(0)
    load_shifted(dot_f32(into_ref[frame], packed_ref[0], ((1,), (0,))), shifted)
    spread_heads(grad_own_ref.at[0], spread, 0, heads, unit)
    grad_copy(clip).wait_recv()
    spread_heads(peer.at[clip], spread, HALF, heads, unit)
    bias_low = bias_ref[0].astype(BF)
    bias_sum = jnp.zeros((BIAS_COLS, LANES), F32)
    for head in range(heads):
        lanes = slice(head * LANES, (head + 1) * LANES)
        keys = k_ref[0, :, lanes]
        values = v_ref[0, :, lanes]
        keys_grad = jnp.zeros((KROWS, LANES), F32)
        values_grad = jnp.zeros((KROWS, LANES), F32)
        for half in range(2):
            rows = slice(half * HALF, (half + 1) * HALF)
            query = q_ref[0, rows, lanes]
            out_grad = spread[rows, lanes]
            probs = p_ref[0, head, rows, :]
            wide = probs.astype(F32)
            probs_grad = dot_f32(out_grad, values, ((1,), (1,)))
            weighted = wide * probs_grad
            shared = jnp.sum(weighted, axis=-1, keepdims=True)
            score_grad = (weighted - wide * shared).astype(BF)
            values_grad = values_grad + dot_f32(probs, out_grad, ((0,), (0,)))
            keys_grad = keys_grad + dot_f32(score_grad, query, ((0,), (0,)))
            table_grad = dot_f32(score_grad, keyhot_ref[...], ((1,), (1,))) * mask_ref[rows, :]
            table_low = table_grad.astype(BF)
            query_grad = dot_f32(score_grad, keys, ((1,), (0,)))
            query_grad = query_grad + dot_f32(table_low, bias_low, ((1,), (0,)))
            query_grad = query_grad * scale + out_grad.astype(F32)
            pooled[rows, lanes] = query_grad.astype(BF)
            bias_sum = bias_sum + dot_f32(table_low, query, ((0,), (0,)))
        keys_grad = (keys_grad * scale).astype(BF)
        values_grad = values_grad.astype(BF)
        for member, part in enumerate((keys_grad, values_grad)):
            at = ((member + 1) * heads + head) * LANES
            pooled[:, at : at + LANES] = part[:QROWS]
            at = (member * heads + head) * LANES
            low = MEM_AT + MEM_PAD
            mem_own[0, :, at : at + LANES] = part[MEM_AT : MEM_AT + MEM_BACK]
            mem_send[clip, :, at : at + LANES] = part[low : low + MEM_BACK]
    bias_out[0] = bias_sum
    mem_copy(clip).start()

    for index in range(units):
        lanes = slice(index * LANES, (index + 1) * LANES)
        if index % heads == 0:
            member = slice(index * LANES, (index + heads) * LANES)
            arrived = dot_f32(into_ref[frame], pooled[:, member], ((1,), (0,)))
        at = index % heads * LANES
        incoming = arrived[:, at : at + LANES]
        block = c_ref[0, :, :, :, lanes].reshape(GRID_ROWS, LANES)
        centred, rate = head_stats(block, unit)
        normal = centred * rate
        product = incoming * normal
        gain_out[:, lanes] += jnp.sum(product, axis=0, keepdims=True)
        shift_out[:, lanes] += jnp.sum(incoming, axis=0, keepdims=True)
        inner = incoming * gain_ref[:, lanes]
        mean_inner = jnp.sum(inner, axis=-1, keepdims=True) * (1.0 / unit)
        mean_both = jnp.sum(inner * normal, axis=-1, keepdims=True) * (1.0 / unit)
        lane = lax.broadcasted_iota(jnp.int32, block.shape, 1)
        result = rate * (inner - mean_inner - normal * mean_both)
        result = jnp.where(lane < unit, result, 0.0)
        flat = result.reshape(FRAMES * SIDE, 8, LANES)
        shape = (FRAMES, SIDE, 8, LANES)
        grads[1, 1 : FRAMES + 1, 1 : SIDE + 1, :, lanes] = flat.reshape(shape)
        grads[0, 1 : FRAMES + 1, 1 : SIDE + 1, :, lanes] = pltpu.roll(flat, 1, 1).reshape(shape)
        grads[2, 1 : FRAMES + 1, 1 : SIDE + 1, :, lanes] = pltpu.roll(flat, 7, 1).reshape(shape)

    @pl.when(clip > 0)
    def _():
        finish_rows(clip - 1)

    pump(1)
    tap_grads(shifted, grads.at[1], taps_out)
    conv = shifted.at[1, 1 : FRAMES + 1, 1 : SIDE + 1]
    convolve(grads, taps, conv, True)
    for member in range(3):
        lanes = slice(member * heads * LANES, (member + 1) * heads * LANES)
        block = shifted[1, 1 : FRAMES + 1, 1 : SIDE + 1, :, lanes].reshape(GRID_ROWS, -1)
        rows = dot_f32(outof_ref[frame], block.astype(BF), ((1,), (0,))).astype(BF)
        pooled[:, lanes] = rows
        joined_out[:, lanes] += jnp.sum(rows.astype(F32), axis=0, keepdims=True)
    weight_sum[...] += dot_f32(normed_ref[0], pooled[...], ((0,), (0,)))
    result = dot_f32(pooled[...], weight_ref[...], ((1,), (1,))).astype(BF)
    cut = result.shape[1] // 2

    @pl.when(head_at == 0)
    def _():
        keep[clip] = result[:, :cut]
        cross_send[clip] = result[:, cut:]

    @pl.when(head_at == 1)
    def _():
        keep[clip] = result[:, cut:]
        cross_send[clip] = result[:, :cut]

    cross_copy(clip).start()

    @pl.when(clip == clips - 1)
    def _():
        weight_out[...] = weight_sum[...].astype(BF)
        finish_rows(clip)
        settle(chunks - 1)
        for chunk in range(early):
            each(1, outers, lambda step: far_copy(chunk, step).wait_recv())
            rest_out[:, chunk * cols : (chunk + 1) * cols] = lax.fori_loop(
                1,
                outers,
                lambda step, sums: sums + rest_far[chunk, step].astype(F32),
                rest_sum[chunk, outer].astype(F32),
            )
        for index in range(clips):
            grad_copy(index).wait_send()
            cross_copy(index).wait_send()
            mem_copy(index).wait()
            row_copy(index).wait()
        for chunk in range(chunks):
            over_copy(chunk).wait_send()
            rest_copy(chunk).wait_send()
        for chunk in range(early):
            each(1, outers, lambda step: far_copy(chunk, step).wait_send())


def whole_spec(shape):
    return pl.BlockSpec(shape, lambda clip: (0,) * len(shape))


def clip_spec(shape):
    return pl.BlockSpec((1,) + shape, lambda clip: (clip,) + (0,) * len(shape))


def once_spec(shape):
    return pl.BlockSpec(
        shape, lambda clip: (0,) * len(shape), pipeline_mode=pl.Buffered(1)
    )


def any_spec():
    return pl.BlockSpec(memory_space=pl.ANY)


def attention_forward(
    packed, mem_own, mem_peer, column, consts, kernels, gains, shifts, bias, scale, unit, rows
):
    clips = packed.shape[0]
    heads = packed.shape[2] // (3 * LANES)
    into, outof, keyhot, mask, pad_row = consts
    wide = 3 * heads * LANES
    mem_shape = mem_own.shape[1:]
    outers = column.shape[0]
    dma = pltpu.SemaphoreType.DMA
    out = jax.ShapeDtypeStruct
    return pl.pallas_call(
        partial(forward_kernel, heads=heads, unit=unit, scale=scale),
        grid=(clips,),
        in_specs=[
            clip_spec((QROWS, wide)),
            clip_spec(mem_shape),
            clip_spec(mem_shape),
            once_spec(column.shape),
            once_spec(into.shape),
            once_spec(outof.shape),
            once_spec(kernels.shape),
            once_spec(gains.shape),
            once_spec(shifts.shape),
            clip_spec((BIAS_COLS, LANES)),
            once_spec((BIAS_COLS, KROWS)),
            once_spec((QROWS, BIAS_COLS)),
            once_spec((1, BIAS_COLS)),
        ],
        out_specs=[
            clip_spec((rows, heads * unit)),
            any_spec(),
            any_spec(),
            clip_spec((QROWS, heads * LANES)),
            clip_spec((KROWS, heads * LANES)),
            clip_spec((KROWS, heads * LANES)),
            clip_spec((heads, QROWS, KROWS)),
            clip_spec((FRAMES, SIDE, 8, wide)),
        ],
        scratch_shapes=[
            pltpu.VMEM((3, FRAMES + 2, SIDE + 2, 8, wide), F32),
            pltpu.VMEM((27, 8, wide), F32),
            pltpu.VMEM((1, wide), F32),
            pltpu.VMEM((1, wide), F32),
            pltpu.VMEM((clips, rows, heads * unit), BF),
            dma((2, clips)),
            dma((2, outers)),
            dma((2, outers)),
            dma((2, outers)),
            pltpu.SemaphoreType.DMA,
        ],
        out_shape=[
            out((clips, rows, heads * unit), BF),
            out((clips, rows, heads * unit), BF),
            out((outers, 4) + column.shape[1:], BF),
            out((clips, QROWS, heads * LANES), BF),
            out((clips, KROWS, heads * LANES), BF),
            out((clips, KROWS, heads * LANES), BF),
            out((clips, heads, QROWS, KROWS), BF),
            out((clips, FRAMES, SIDE, 8, wide), F32),
        ],
        compiler_params=pltpu.CompilerParams(
            collective_id=1, has_side_effects=True, vmem_limit_bytes=VMEM_LIMIT
        ),
        name="pooled_attention_forward",
    )(
        packed, mem_own, mem_peer, column, into, outof, kernels, gains, shifts, bias, keyhot, mask,
        pad_row,
    )


def attention_backward(
    packed, normed, weight, grad_own, grad_send, rest, consts, kernels, gains, bias, saved, scale,
    unit,
):
    clips, rows, width = grad_own.shape
    heads = width // unit
    model = weight.shape[0]
    half = model // 2
    into, outof, keyhot, mask, pad_row = consts
    wide = 3 * heads * LANES
    outers, _, shard_rows, rest_width = rest.shape
    chunks = 9
    early = 8
    cols = rest_width // chunks
    out = jax.ShapeDtypeStruct
    dma = pltpu.SemaphoreType.DMA
    return pl.pallas_call(
        partial(backward_kernel, heads=heads, unit=unit, scale=scale),
        grid=(clips,),
        in_specs=[
            clip_spec((QROWS, wide)),
            clip_spec((QROWS, model)),
            once_spec((model, wide)),
            clip_spec((rows, width)),
            any_spec(),
            any_spec(),
            once_spec(into.shape),
            once_spec(outof.shape),
            once_spec(kernels.shape),
            once_spec(gains.shape),
            clip_spec((BIAS_COLS, LANES)),
            once_spec((BIAS_COLS, KROWS)),
            once_spec((QROWS, BIAS_COLS)),
            clip_spec((QROWS, heads * LANES)),
            clip_spec((KROWS, heads * LANES)),
            clip_spec((KROWS, heads * LANES)),
            clip_spec((heads, QROWS, KROWS)),
            clip_spec((FRAMES, SIDE, 8, wide)),
        ],
        out_specs=[
            whole_spec((clips, rows, half)),
            any_spec(),
            clip_spec((MEM_BACK, 2 * heads * LANES)),
            any_spec(),
            whole_spec((27, 8, wide)),
            whole_spec((1, wide)),
            whole_spec((1, wide)),
            clip_spec((BIAS_COLS, LANES)),
            whole_spec((model, wide)),
            whole_spec((1, wide)),
            whole_spec((outers, shard_rows, cols)),
            whole_spec((shard_rows, early * cols)),
        ],
        scratch_shapes=[
            pltpu.VMEM((3, FRAMES + 2, SIDE + 2, 8, wide), F32),
            pltpu.VMEM((27, 8, wide), F32),
            pltpu.VMEM((1, wide), F32),
            pltpu.VMEM((3, FRAMES + 2, SIDE + 2, 8, wide), F32),
            pltpu.VMEM((QROWS, heads * LANES), BF),
            pltpu.VMEM((QROWS, wide), BF),
            pltpu.VMEM((clips, rows, width), BF),
            pltpu.VMEM((clips, MEM_BACK, 2 * heads * LANES), BF),
            pltpu.VMEM((chunks, outers, 2, shard_rows, cols), BF),
            pltpu.VMEM((chunks, outers, 2, shard_rows, cols), BF),
            pltpu.VMEM((chunks, outers, shard_rows, cols), BF),
            pltpu.VMEM((chunks, outers, shard_rows, cols), BF),
            pltpu.VMEM((chunks, outers, shard_rows, cols), BF),
            pltpu.VMEM((early, outers, shard_rows, cols), BF),
            pltpu.VMEM((model, wide), F32),
            pltpu.VMEM((clips, QROWS, half), BF),
            pltpu.VMEM((clips, QROWS, half), BF),
            pltpu.VMEM((clips, QROWS, half), BF),
            pltpu.VMEM((clips, rows, half), BF),
            dma((2, clips)),
            dma((2, clips)),
            dma((chunks,)),
            dma((2, chunks)),
            dma((2, chunks)),
            dma((2, early, outers)),
            dma((2, clips)),
            dma((2, clips)),
        ],
        out_shape=[
            out((clips, rows, half), BF),
            out((clips, rows, half), BF),
            out((clips, MEM_BACK, 2 * heads * LANES), BF),
            out((clips, MEM_BACK, 2 * heads * LANES), BF),
            out((27, 8, wide), F32),
            out((1, wide), F32),
            out((1, wide), F32),
            out((clips, BIAS_COLS, LANES), F32),
            out((model, wide), BF),
            out((1, wide), F32),
            out((outers, shard_rows, cols), BF),
            out((shard_rows, early * cols), F32),
        ],
        compiler_params=pltpu.CompilerParams(
            collective_id=2, has_side_effects=True, vmem_limit_bytes=VMEM_LIMIT
        ),
        name="pooled_attention_backward",
    )(
        packed, normed, weight, grad_own, grad_send, rest, into, outof, kernels, gains, bias, keyhot,
        mask, *saved,
    )


def row_stats(values):
    width = values.shape[-1]
    centred = values - jnp.sum(values, axis=-1, keepdims=True) * (1.0 / width)
    variance = jnp.sum(centred * centred, axis=-1, keepdims=True) * (1.0 / width)
    return centred, lax.rsqrt(variance + 1e-06)


def each(low, high, act):
    def body(step, carry):
        act(step)
        return carry

    lax.fori_loop(low, high, body, 0)


def norm_rows(source, index, gain, shift, target, at):
    rows = source.shape[1]
    centred, rate = row_stats(source[index].astype(F32))
    target[index, at : at + rows] = (centred * rate * gain[0:1] + shift[0:1]).astype(BF)


def project_rows(normed, weight, bias, packed):
    def step(index):
        packed[index] = (dot_f32(normed[index], weight, ((1,), (0,))) + bias[...]).astype(BF)

    each(0, packed.shape[0], step)


def project_moves(
    x, attn, gain, shift, attn_shift, cached, old, squeeze, proj, up, down, full, normed, mem_own,
    mem_peer, rest_column, shards, bias, rest, mem_send, squeeze_rows, x_peer, columns, far_sems,
    near_sems, x_sems, cross_sems, mem_sems, rest_sems,
):
    outers = full.shape[0]
    clips, rows, model = x.shape
    clip = lax.axis_index("clip")
    frame = lax.axis_index("frame")
    head = lax.axis_index("head")
    outer, inner = clip // 2, clip % 2
    place = inner * 2 + frame
    half = model // 2
    lanes = pl.ds(pl.multiple_of(head * half, LANES), half)
    barrier = pltpu.get_barrier_semaphore()

    def far_device(step):
        return device_of((outer + step) % outers, inner, frame, head)

    def near_device(step):
        there_inner, there_frame = plane_peer(inner, frame, step)
        return device_of(outer, there_inner, there_frame, head)

    def greet(device):
        pl.semaphore_signal(barrier, inc=1, device_id=device, device_id_type=MESH_ID)

    group = mem_own.shape[2] // 2
    heads = shards.shape[2] // (3 * LANES)
    unit = group // heads

    def squeeze_clip(index):
        total = jnp.zeros((CELLS, cached.shape[2]), F32)
        for step in range(squeeze_rows.shape[0]):
            rows_here = cached[index, step * CELLS : (step + 1) * CELLS].astype(F32)
            total = total + rows_here * squeeze_rows[step : step + 1]
        pieces = ((0, total.astype(BF)), (MEM_STEP, old[index]))
        for side in range(2):

            @pl.when(frame == side)
            def _():
                for at, value in pieces:
                    for member in range(2):
                        local = slice(member * group, (member + 1) * group)
                        low = (2 * member + side) * group
                        mem_own[index, at : at + CELLS, local] = value[:, low : low + group]
                        low = (2 * member + 1 - side) * group
                        mem_send[index, at : at + CELLS, local] = value[:, low : low + group]

    def far_copy(step, at):
        return pltpu.make_async_remote_copy(
            src_ref=shards, dst_ref=columns.at[at],
            send_sem=far_sems.at[0, step], recv_sem=far_sems.at[1, step],
            device_id=far_device(step), device_id_type=MESH_ID,
        )

    def near_copy(index, step, source, at):
        return pltpu.make_async_remote_copy(
            src_ref=source.at[(frame + step % 2) % 2], dst_ref=full.at[at, place],
            send_sem=near_sems.at[0, index, step - 1], recv_sem=near_sems.at[1, index, step - 1],
            device_id=near_device(step), device_id_type=MESH_ID,
        )

    def turn_copy(index):
        block = full.at[origin(index), inner * 2 + 1 - frame]
        return side_copy(block, block, near_sems.at[0, index, 2], near_sems.at[1, index, 2])

    def near_arrival(index, step, at):
        there_inner, there_frame = plane_peer(inner, frame, step)
        return pltpu.make_async_remote_copy(
            src_ref=shards.at[0], dst_ref=full.at[at, there_inner * 2 + there_frame],
            send_sem=near_sems.at[0, index, step - 1], recv_sem=near_sems.at[1, index, step - 1],
            device_id=near_device(step), device_id_type=MESH_ID,
        )

    def x_copy(index):
        return partner_copy(
            x.at[index, :, lanes], x_peer.at[index, :, lanes], x_sems.at[0, index],
            x_sems.at[1, index],
        )

    def cross_copy(index):
        return pltpu.make_async_remote_copy(
            src_ref=x_peer.at[index, :, lanes], dst_ref=x_peer.at[index, :, lanes],
            send_sem=cross_sems.at[0, index], recv_sem=cross_sems.at[1, index],
            device_id=(clip, frame, 1 - head), device_id_type=MESH_ID,
        )

    def cross_arrival(index):
        other = pl.ds(pl.multiple_of((1 - head) * half, LANES), half)
        return pltpu.make_async_remote_copy(
            src_ref=x_peer.at[index, :, other], dst_ref=x_peer.at[index, :, other],
            send_sem=cross_sems.at[0, index], recv_sem=cross_sems.at[1, index],
            device_id=(clip, frame, 1 - head), device_id_type=MESH_ID,
        )

    mem_copy = partner_copy(mem_send, mem_peer, mem_sems.at[0], mem_sems.at[1])

    def rest_copy(step, at):
        return pltpu.make_async_remote_copy(
            src_ref=rest, dst_ref=rest_column.at[at],
            send_sem=rest_sems.at[0, step], recv_sem=rest_sems.at[1, step],
            device_id=far_device(step), device_id_type=MESH_ID,
        )

    def origin(step):
        return (outer + outers - step) % outers

    def prologue():
        each(1, outers, lambda step: greet(far_device(step)))
        for step in range(1, 4):
            greet(near_device(step))
        greet((clip, frame, 1 - head))
        shards[...] = jnp.zeros_like(shards)
        bias[...] = jnp.zeros_like(bias)
        for member in range(3):
            for side in range(2):
                for index in range(heads):
                    target = (member * heads + index) * LANES
                    source = slice(side * group + index * unit, side * group + (index + 1) * unit)
                    shards[side, :, target : target + unit] = attn[member, :, source]
        at = 0
        for part in (proj, up, down):
            rest[:, at : at + part.shape[1]] = part[...]
            at += part.shape[1]
        for side in range(2):

            @pl.when(frame == side)
            def _():
                for member in range(3):
                    for index in range(heads):
                        target = (member * heads + index) * LANES
                        source = slice(side * group + index * unit, side * group + (index + 1) * unit)
                        bias[:, target : target + unit] = attn_shift[member : member + 1, source]

        for member in range(2):
            for index in range(2 * heads):
                at = (2 * member * heads + index) * unit
                squeeze_rows[:, at : at + unit] = squeeze[member]
        mem_own[...] = jnp.zeros_like(mem_own)
        mem_send[...] = jnp.zeros_like(mem_send)

        pl.semaphore_wait(barrier, outers - 1 + 4)
        each(1, outers, lambda step: far_copy(step, outer).start())
        for step in range(1, 3):
            near_copy(0, step, shards, outer).start()
        each(0, clips, lambda index: x_copy(index).start())
        each(0, clips, squeeze_clip)
        rest_column[outer] = rest[...]
        full[outer, place] = shards[frame]
        normed[...] = jnp.zeros_like(normed)
        each(0, clips, lambda index: norm_rows(x, index, gain, shift, normed, 0))

        def forward(index):
            at = origin(index)
            far_copy(index, at).wait_recv()
            for step in range(1, 3):
                near_copy(index, step, columns.at[at], at).start()
            full[at, place] = columns[at, frame]

        each(1, outers, forward)
        each(1, outers, lambda step: rest_copy(step, outer).start())

        def relay(index):
            x_copy(index).wait_recv()
            cross_copy(index).start()

        each(0, clips, relay)
        mem_copy.start()

        def receive(index):
            cross_arrival(index).wait_recv()
            norm_rows(x_peer, index, gain, shift, normed, HALF)

        each(0, clips, receive)

        def pass_side(index):
            near_arrival(index, 1, origin(index)).wait_recv()
            turn_copy(index).start()

        def arrive(index):
            for step in range(2, 4):
                near_arrival(index, step, origin(index)).wait_recv()

        each(0, outers, pass_side)

        each(0, outers, arrive)
    def rest_arrive():
        each(1, outers, lambda step: rest_copy(step, origin(step)).wait_recv())

    def finish():
        each(1, outers, lambda step: rest_copy(step, outer).wait_send())
        each(1, outers, lambda step: far_copy(step, outer).wait_send())
        each(0, outers, lambda index: turn_copy(index).wait_send())
        for step in range(1, 3):
            near_copy(0, step, shards, outer).wait_send()

        def sent(index):
            for step in range(1, 3):
                near_copy(index, step, columns.at[origin(index)], origin(index)).wait_send()

        each(1, outers, sent)

        def x_sent(index):
            x_copy(index).wait_send()
            cross_copy(index).wait_send()

        each(0, clips, x_sent)

    return outer, prologue, mem_copy, rest_arrive, finish


def front_kernel(
    x, attn, gain, shift, attn_shift, cached, old, squeeze, proj, up, down, into_ref, outof_ref,
    kernel_ref, pool_gain_ref, pool_shift_ref, bias_ref, keyhot_ref, mask_ref, pad_ref,
    full_out, packed_out, normed_out, out_own, out_recv, rest_full, q_out, k_out, v_out, p_out,
    c_out, full, shards, attn_bias, rest, mem_send, mem_own, mem_peer, squeeze_rows, x_peer, columns, normed,
    rest_column, shifted, taps, gain_ref, shift_ref, out_send, far_sems, near_sems, x_sems,
    cross_sems, mem_sems, rest_sems, out_sems, side_sems, pair_sems, turn_sems, own_sem,
    *, heads, unit, scale,
):
    clip = pl.program_id(0)
    clips = out_send.shape[0]
    outers = full.shape[0]
    frame = lax.axis_index("frame")
    outer, prologue, mem_copy, rest_arrive, project_finish = project_moves(
        x, attn, gain, shift, attn_shift, cached, old, squeeze, proj, up, down, full, normed,
        mem_own, mem_peer, rest_column, shards, attn_bias, rest, mem_send, squeeze_rows, x_peer,
        columns, far_sems, near_sems, x_sems, cross_sems, mem_sems, rest_sems,
    )
    own_copy, send, turn, plane_finish = plane_stage(
        rest_column, rest_full, side_sems, pair_sems, turn_sems, own_sem
    )

    def out_copy(index):
        return partner_copy(
            out_send.at[index], out_recv.at[index], out_sems.at[0, index], out_sems.at[1, index]
        )

    @pl.when(clip == 0)
    def _():
        prologue()
        send(outer)
        shifted[...] = jnp.zeros_like(shifted)
        pairs = ((pool_gain_ref, gain_ref), (pool_shift_ref, shift_ref))
        spread_tables(kernel_ref, taps, pairs, heads, unit)

    def points(odd):
        for step in range(outers):
            point = min(step + TURN_LAG, 2 * clips - 1)
            if step and step % 2 == odd:

                @pl.when(clip == step // 2)
                def _():
                    send((outer + step) % outers)

            if point % 2 == odd:

                @pl.when(clip == point // 2)
                def _():
                    turn(step)

    def after_conv():
        @pl.when(clip == 0)
        def _():
            mem_copy.wait_recv()
            rest_arrive()
            own_copy.start()

        points(1)

    points(0)
    @pl.when(clip == clips - 1)
    def _():
        full_out[...] = full[...]

    normed_out[0] = normed[clip]
    weight = full[...].reshape(x.shape[2], full.shape[3])
    rows = dot_f32(normed[clip], weight, ((1,), (0,))) + attn_bias[...]
    packed_out[0] = rows.astype(BF)
    attend_clip(
        packed_out.at[0], mem_own.at[clip], mem_peer.at[clip], frame, into_ref, outof_ref, gain_ref,
        shift_ref, bias_ref, keyhot_ref, mask_ref, pad_ref, out_own.at[0], out_send.at[clip], q_out,
        k_out, v_out, p_out, c_out, shifted, taps, heads, unit, scale, after_conv,
    )
    out_copy(clip).start()

    @pl.when(clip == clips - 1)
    def _():
        mem_copy.wait_send()
        project_finish()
        plane_finish()
        for index in range(clips):
            out_copy(index).wait()


def front(
    x, attn, gain, shift, attn_shift, cached, old, squeeze, proj, up, down, consts, kernels, gains,
    shifts, bias, scale, clip_count, unit,
):
    clips, rows, model = x.shape
    _, shard_rows, head_width = attn.shape
    heads = head_width // (2 * unit)
    wide = 3 * heads * LANES
    outers = clip_count // 2
    into, outof, keyhot, mask, pad_row = consts
    rest_shape = (shard_rows, proj.shape[1] + up.shape[1] + down.shape[1])
    mem_shape = (clips, MEM_PAD, head_width)
    out = jax.ShapeDtypeStruct
    dma = pltpu.SemaphoreType.DMA
    operands = (
        x, attn, gain, shift, attn_shift, cached, old, squeeze, proj, up, down, into, outof,
        kernels, gains, shifts, bias, keyhot, mask, pad_row,
    )
    specs = [once_spec(value.shape) for value in operands]
    specs[16] = clip_spec((BIAS_COLS, LANES))
    results = pl.pallas_call(
        partial(front_kernel, heads=heads, unit=unit, scale=scale),
        grid=(clips,),
        in_specs=specs,
        out_specs=[
            whole_spec((outers, 4, shard_rows, wide)),
            clip_spec((QROWS, wide)),
            clip_spec((QROWS, model)),
            clip_spec((rows, heads * unit)),
            any_spec(),
            any_spec(),
            clip_spec((QROWS, heads * LANES)),
            clip_spec((KROWS, heads * LANES)),
            clip_spec((KROWS, heads * LANES)),
            clip_spec((heads, QROWS, KROWS)),
            clip_spec((FRAMES, SIDE, 8, wide)),
        ],
        out_shape=[
            out((outers, 4, shard_rows, wide), BF),
            out((clips, QROWS, wide), BF),
            out((clips, QROWS, model), BF),
            out((clips, rows, heads * unit), BF),
            out((clips, rows, heads * unit), BF),
            out((outers, 4) + rest_shape, BF),
            out((clips, QROWS, heads * LANES), BF),
            out((clips, KROWS, heads * LANES), BF),
            out((clips, KROWS, heads * LANES), BF),
            out((clips, heads, QROWS, KROWS), BF),
            out((clips, FRAMES, SIDE, 8, wide), F32),
        ],
        scratch_shapes=[
            pltpu.VMEM((outers, 4, shard_rows, wide), BF),
            pltpu.VMEM((2, shard_rows, wide), BF),
            pltpu.VMEM((1, wide), F32),
            pltpu.VMEM(rest_shape, BF),
            pltpu.VMEM(mem_shape, BF),
            pltpu.VMEM(mem_shape, BF),
            pltpu.VMEM(mem_shape, BF),
            pltpu.VMEM((squeeze.shape[1], cached.shape[2]), F32),
            pltpu.VMEM((clips, rows, model), BF),
            pltpu.VMEM((outers, 2, shard_rows, wide), BF),
            pltpu.VMEM((clips, QROWS, model), BF),
            pltpu.VMEM((outers,) + rest_shape, BF),
            pltpu.VMEM((3, FRAMES + 2, SIDE + 2, 8, wide), F32),
            pltpu.VMEM((27, 8, wide), F32),
            pltpu.VMEM((1, wide), F32),
            pltpu.VMEM((1, wide), F32),
            pltpu.VMEM((clips, rows, heads * unit), BF),
            dma((2, outers)),
            dma((2, outers, 3)),
            dma((2, clips)),
            dma((2, clips)),
            dma((2,)),
            dma((2, outers)),
            dma((2, clips)),
            dma((2, outers)),
            dma((2, outers)),
            dma((2, outers)),
            pltpu.SemaphoreType.DMA,
        ],
        compiler_params=pltpu.CompilerParams(
            collective_id=1, has_side_effects=True, vmem_limit_bytes=VMEM_LIMIT
        ),
        name="project_and_attend",
    )(*operands)
    return (results[0].reshape(model, wide),) + tuple(results[1:])


def project_local_kernel(x, x_peer, weight, gain, shift, bias, packed, normed):
    normed[...] = jnp.zeros_like(normed)
    each(0, x.shape[0], lambda index: norm_rows(x, index, gain, shift, normed, 0))
    each(0, x.shape[0], lambda index: norm_rows(x_peer, index, gain, shift, normed, HALF))
    project_rows(normed, weight[...], bias, packed)


def swap(value, axis):
    return lax.ppermute(value, axis, [(0, 1), (1, 0)])


def padded_heads(value, unit):
    value = value.reshape(value.shape[0], 3, 2, -1, unit)
    value = jnp.pad(value, ((0, 0),) * 4 + ((0, LANES - unit),))
    return value.transpose(2, 0, 1, 3, 4).reshape(2, value.shape[0], -1)


def project_plain(
    x, attn, gain, shift, attn_shift, cached, old, squeeze, proj, up, down, clip_count, unit
):
    clips, rows, model = x.shape
    _, shard_rows, head_width = attn.shape
    heads = head_width // (2 * unit)
    width = 3 * heads * LANES
    outers = clip_count // 2
    rest_shape = (shard_rows, proj.shape[1] + up.shape[1] + down.shape[1])
    out = jax.ShapeDtypeStruct
    dma = pltpu.SemaphoreType.DMA
    vmem = pl.BlockSpec(memory_space=pltpu.VMEM)
    shapes = [out((clips, QROWS, width), BF), out((clips, QROWS, model), BF)]
    frame = lax.axis_index("frame")
    shards = padded_heads(attn.transpose(1, 0, 2), unit)
    full = lax.all_gather(shards, ("clip", "frame"), axis=1, tiled=True)
    full = lax.dynamic_index_in_dim(full, frame, 0, keepdims=False)
    bias = padded_heads(attn_shift[None], unit)
    bias = lax.dynamic_index_in_dim(bias, frame, 0, keepdims=False)
    steps = squeeze.shape[1]
    wide = cached.astype(F32).reshape(clips, steps, CELLS, 2, head_width)
    tiled = jnp.tile(squeeze, (1, 1, 2 * heads))
    mem = sum(wide[:, step] * tiled[:, step] for step in range(steps)).astype(BF)
    mem = jnp.stack([mem, old.reshape(mem.shape)], axis=1)
    mem = jnp.pad(mem, ((0, 0), (0, 0), (0, MEM_STEP - CELLS), (0, 0), (0, 0)))
    pieces = mem.reshape(clips, 2 * MEM_STEP, 2, 2, heads * unit)
    mem_own = lax.dynamic_index_in_dim(pieces, frame, 3, keepdims=False)
    mem_send = lax.dynamic_index_in_dim(pieces, 1 - frame, 3, keepdims=False)
    mem_own = mem_own.reshape(clips, -1, head_width)
    mem_peer = swap(mem_send.reshape(clips, -1, head_width), "frame")
    packed, normed = pl.pallas_call(
        project_local_kernel,
        in_specs=[vmem] * 6,
        out_specs=[vmem] * 2,
        out_shape=shapes,
        compiler_params=pltpu.CompilerParams(vmem_limit_bytes=VMEM_LIMIT),
        name="project_local",
    )(x, swap(x, "frame"), full, gain, shift, bias)
    rest = jnp.concatenate([proj, up, down], axis=1)
    column = lax.all_gather(rest, ("clip", "frame"), axis=0, tiled=False)
    column = column.reshape((outers, 4) + rest.shape)
    place = lax.axis_index("clip") % 2 * 2 + frame
    column = lax.dynamic_index_in_dim(column, place, 1, keepdims=False)
    return full, packed, normed, mem_own, mem_peer, column


def device_of(outer, inner, frame, head):
    return (outer * 2 + inner, frame, head)


def plane_peer(inner, frame, step):
    return (inner + step // 2) % 2, (frame + step % 2) % 2


def row_piece(value, row):
    return value[:, row * LANES : (row + 1) * LANES]


def tail_kernel(
    row_own, row_recv, x, middle_grad, grads, joined_sum, gain, taps, pool_gain, pool_shift,
    bias_grad, hot, space_hot, cached, mem_own, mem_recv, vectors, up_bias, rest,
    grad_in, out, rest_out, small_out,
    near, part, far, small, pair_in, plane_in, line_in, row_full, rest_in,
    cross_sems, near_sems, far_sems, pair_sems, plane_sems, line_sems, rest_sems,
    *, unit, plan, table_rows,
):
    chunks, outers, _, shard_rows, cols = part.shape
    clips, rows, model = x.shape
    half = model // 2
    clip = lax.axis_index("clip")
    frame = lax.axis_index("frame")
    head = lax.axis_index("head")
    outer, inner = clip // 2, clip % 2
    place = inner * 2 + frame
    barrier = pltpu.get_barrier_semaphore()
    partner = (clip, frame, 1 - head)

    def line_device(step):
        return device_of((outer + step) % outers, inner, frame, head)

    def plane_device(step):
        there_inner, there_frame = plane_peer(inner, frame, step)
        return device_of(outer, there_inner, there_frame, head)

    def plane_place(step):
        there_inner, there_frame = plane_peer(inner, frame, step)
        return there_inner * 2 + there_frame

    def greet(device):
        pl.semaphore_signal(barrier, inc=1, device_id=device, device_id_type=MESH_ID)

    each(1, outers, lambda step: greet(line_device(step)))
    for step in range(1, 4):
        greet(plane_device(step))
    greet(partner)

    def move(source, target, sems, device):
        return pltpu.make_async_remote_copy(
            src_ref=source, dst_ref=target, send_sem=sems[0], recv_sem=sems[1],
            device_id=device, device_id_type=MESH_ID,
        )

    def pair_sum():
        return move(
            small.at[1 - head], pair_in, (pair_sems.at[0, 0], pair_sems.at[1, 0]), partner
        )

    def plane_sum(step):
        sems = (plane_sems.at[0, 0, step - 1], plane_sems.at[1, 0, step - 1])
        source = small.at[head, plane_place(step)]
        return move(source, plane_in.at[step - 1], sems, plane_device(step))

    def line_sum(step):
        sems = (line_sems.at[0, 0, step], line_sems.at[1, 0, step])
        source = small.at[head, place, (outer + step) % outers]
        return move(source, line_in.at[step], sems, line_device(step))

    def line_share(step, at):
        sems = (line_sems.at[0, 1, step], line_sems.at[1, 1, step])
        block = small_out.at[head, place, at]
        return move(block, block, sems, line_device(step))

    def plane_share(step, at):
        sems = (plane_sems.at[0, 1, step - 1], plane_sems.at[1, 1, step - 1])
        block = small_out.at[head, at]
        return move(block, block, sems, plane_device(step))

    def pair_share(at):
        block = small_out.at[at]
        return move(block, block, (pair_sems.at[0, 1], pair_sems.at[1, 1]), partner)

    def near_copy(chunk, step):
        there_inner, there_frame = plane_peer(inner, frame, step)
        return pltpu.make_async_remote_copy(
            src_ref=grads.at[:, there_inner * 2 + there_frame, :, pl.ds(chunk * cols, cols)],
            dst_ref=near.at[chunk, step - 1],
            send_sem=near_sems.at[0, chunk, step - 1], recv_sem=near_sems.at[1, chunk, step - 1],
            device_id=device_of(outer, there_inner, there_frame, head), device_id_type=MESH_ID,
        )

    def far_copy(chunk, step):
        there = (outer + step) % outers
        return pltpu.make_async_remote_copy(
            src_ref=part.at[chunk, there], dst_ref=far.at[chunk, step],
            send_sem=far_sems.at[0, chunk, step], recv_sem=far_sems.at[1, chunk, step],
            device_id=device_of(there, inner, frame, head), device_id_type=MESH_ID,
        )

    def cross_copy(index, side):
        lanes = pl.ds(pl.multiple_of(side * half, LANES), half)
        return pltpu.make_async_remote_copy(
            src_ref=row_full.at[index, :, lanes], dst_ref=row_full.at[index, :, lanes],
            send_sem=cross_sems.at[0, index], recv_sem=cross_sems.at[1, index],
            device_id=(clip, frame, 1 - head), device_id_type=MESH_ID,
        )

    def rest_copy(step):
        there = (outer + step) % outers
        return pltpu.make_async_remote_copy(
            src_ref=rest.at[there], dst_ref=rest_in.at[step],
            send_sem=rest_sems.at[0, step], recv_sem=rest_sems.at[1, step],
            device_id=device_of(there, inner, frame, head), device_id_type=MESH_ID,
        )

    small[...] = jnp.zeros_like(small)
    pl.semaphore_wait(barrier, outers - 1 + 4)
    for chunk in range(chunks):
        for step in range(1, 4):
            near_copy(chunk, step).start()
    lanes_here = pl.ds(pl.multiple_of(head * half, LANES), half)

    def join(index):
        total = row_own[index].astype(F32) + row_recv[index].astype(F32)
        row_full[index, :, lanes_here] = total.astype(BF)
        cross_copy(index, head).start()

    each(0, clips, join)
    each(1, outers, lambda step: rest_copy(step).start())

    rows_small = small.shape[3]

    def put(row, value):
        count = value.shape[0]
        done = 0
        while done < count:
            block, offset = divmod(row + done, rows_small)
            size = min(count - done, rows_small - offset)
            at = (block // (4 * outers), block // outers % 4, block % outers)
            small[at[0], at[1], at[2], offset : offset + size, : value.shape[1]] = value[
                done : done + size
            ]
            done += size

    def put_wide(row, value):
        for index in range(value.shape[1] // LANES):
            put(row + index, row_piece(value, index))

    wide_rows_count = model // LANES

    joined_rows = joined_sum.shape[1] // LANES
    up_rows = up_bias.shape[1] // LANES
    for which in range(2):

        @pl.when(head == which)
        def _():
            for side in range(2):

                @pl.when(frame == side)
                def _():
                    put_wide(plan["joined"] + (2 * which + side) * joined_rows, joined_sum[...])

            put_wide(plan["up"] + which * up_rows, up_bias[...])

    heads = taps.shape[2] // (3 * LANES)
    tap_sum = jnp.sum(taps[...], axis=1)
    for member in range(3):
        totals = []
        for value in (tap_sum, pool_gain[...], pool_shift[...]):
            total = row_piece(value, member * heads)
            for index in range(1, heads):
                total = total + row_piece(value, member * heads + index)
            totals.append(total)
        put(plan["taps"] + member * 27, totals[0])
        put(plan["pool_gain"] + member, totals[1])
        put(plan["pool_shift"] + member, totals[2])
    heads_here = joined_sum.shape[1] // (3 * LANES)
    for side in range(2):

        @pl.when(frame == side)
        def _():
            for member in range(2):
                totals = [jnp.zeros((1, unit), F32) for _ in range(FRAMES // MEMF)]
                for index in range(clips):
                    for which, part in ((side, mem_own), (1 - side, mem_recv)):
                        for spot in range(heads_here):
                            at = (member * heads_here + spot) * LANES
                            value = part[index, :CELLS, at : at + unit].astype(F32)
                            at = ((2 * member + which) * heads_here + spot) * unit
                            for step in range(len(totals)):
                                rows_here = cached[
                                    index, step * CELLS : (step + 1) * CELLS, at : at + unit
                                ]
                                product = rows_here.astype(F32) * value
                                totals[step] = totals[step] + jnp.sum(
                                    product, axis=0, keepdims=True
                                )
                for step in range(len(totals)):
                    put(plan["squeeze"] + member * len(totals) + step, totals[step])

    time_sum = jnp.zeros((hot.shape[2], LANES), F32)
    bias_sum = jnp.zeros((BIAS_COLS, LANES), F32)
    for index in range(clips):
        value = bias_grad[index]
        bias_sum = bias_sum + value
        value = value[: hot.shape[1]]
        high = value.astype(BF)
        low = (value - high.astype(F32)).astype(BF)
        time_sum = time_sum + dot_f32(hot[index], high, ((0,), (0,)))
        time_sum = time_sum + dot_f32(hot[index], low, ((0,), (0,)))
    put(plan["time"], time_sum[:table_rows])
    high = bias_sum.astype(BF)
    low = (bias_sum - high.astype(F32)).astype(BF)
    space_sum = dot_f32(space_hot[...], high, ((1,), (0,)))
    space_sum = space_sum + dot_f32(space_hot[...], low, ((1,), (0,)))
    put(plan["space"], space_sum[: 2 * (2 * SIDE - 1)])

    gain_sum = jnp.zeros((1, model), F32)
    shift_sum = jnp.zeros((1, model), F32)
    for index in range(clips):
        cross_copy(index, 1 - head).wait_recv()
        incoming = row_full[index].astype(F32)
        centred, rate = row_stats(x[index].astype(F32))
        normal = centred * rate
        product = incoming * normal
        gain_sum = gain_sum + jnp.sum(product, axis=0, keepdims=True)
        shift_sum = shift_sum + jnp.sum(incoming, axis=0, keepdims=True)
        scaled = incoming * gain[0:1]
        mean_scaled = jnp.sum(scaled, axis=-1, keepdims=True) * (1.0 / model)
        mean_both = jnp.sum(scaled * normal, axis=-1, keepdims=True) * (1.0 / model)
        result = rate * (scaled - mean_scaled - normal * mean_both) + middle_grad[index]
        grad_in[index] = result.astype(BF)

    @pl.when(head == 0)
    def _():
        put_wide(plan["gain"], gain_sum)
        put_wide(plan["gain"] + wide_rows_count, vectors[0:1])
        put_wide(plan["shift"], shift_sum)
        put_wide(plan["shift"] + wide_rows_count, vectors[1:2])
        put_wide(plan["rows"], vectors[2:3])
        put_wide(plan["rows"] + wide_rows_count, vectors[3:4])

    def reduce_near(chunk):
        lanes = slice(chunk * cols, (chunk + 1) * cols)
        for step in range(1, 4):
            near_copy(chunk, step).wait_recv()

        def gathered(index):
            own = grads[index, place, :, lanes].astype(F32)
            own = own + near[chunk, 1, index].astype(F32)
            other = near[chunk, 0, index].astype(F32) + near[chunk, 2, index].astype(F32)
            return own, other

        def send(step):
            there = (outer + step) % outers
            own, other = gathered(there)
            part[chunk, there, 0] = own.astype(BF)
            part[chunk, there, 1] = other.astype(BF)
            far_copy(chunk, step).start()

        each(1, outers, send)
        own, other = gathered(outer)
        far[chunk, 0, 0] = own.astype(BF)
        far[chunk, 0, 1] = other.astype(BF)

    pair_sum().start()
    reduce_near(0)
    pair_sum().wait_recv()
    small[head] = small[head] + pair_in[...]
    for step in range(1, 4):
        plane_sum(step).start()
    for chunk in range(1, chunks):
        reduce_near(chunk)
    for step in range(1, 4):
        plane_sum(step).wait_recv()
    small[head, place] = small[head, place] + plane_in[0] + plane_in[1] + plane_in[2]
    each(1, outers, lambda step: line_sum(step).start())
    each(1, outers, lambda step: rest_copy(step).wait_recv())
    rest_out[...] = lax.fori_loop(
        1,
        outers,
        lambda step, sums: sums + rest_in[step].astype(F32),
        rest[outer].astype(F32),
    )
    each(1, outers, lambda step: line_sum(step).wait_recv())
    small_out[head, place, outer] = lax.fori_loop(
        1, outers, lambda step, sums: sums + line_in[step], small[head, place, outer]
    )
    each(1, outers, lambda step: line_share(step, outer).start())
    each(1, outers, lambda step: line_share(step, (outer + outers - step) % outers).wait_recv())
    for step in range(1, 4):
        plane_share(step, place).start()
    heads = cols // LANES
    group = heads * unit
    for chunk in range(chunks):
        each(1, outers, lambda step: far_copy(chunk, step).wait_recv())
        totals = []
        for side in range(2):
            totals.append(
                lax.fori_loop(
                    0,
                    outers,
                    lambda step, sums: sums + far[chunk, step, side].astype(F32),
                    jnp.zeros((shard_rows, cols), F32),
                )
            )

        def store(order):
            for spot, side in enumerate(order):
                for index in range(heads):
                    at = (2 * chunk + spot) * group + index * unit
                    value = totals[side][:, index * LANES : index * LANES + unit]
                    out[:, at : at + unit] = value

        @pl.when(frame == 0)
        def _():
            store((0, 1))

        @pl.when(frame == 1)
        def _():
            store((1, 0))

    for step in range(1, 4):
        plane_share(step, plane_place(step)).wait_recv()
    pair_share(head).start()
    pair_share(1 - head).wait_recv()
    pair_sum().wait_send()
    pair_share(head).wait_send()
    for step in range(1, 4):
        plane_sum(step).wait_send()
        plane_share(step, place).wait_send()
    each(1, outers, lambda step: line_sum(step).wait_send())
    each(1, outers, lambda step: line_share(step, outer).wait_send())
    each(1, outers, lambda step: rest_copy(step).wait_send())
    for index in range(clips):
        cross_copy(index, head).wait_send()
    for chunk in range(chunks):
        for step in range(1, 4):
            near_copy(chunk, step).wait_send()
        each(1, outers, lambda step: far_copy(chunk, step).wait_send())


def unpack_kernel(
    small, qkv, early, late, grad_in, block_out,
    grad_in_out, block_out_out, gain_out, shift_out, rows_out, joined_out, up_out, taps_out,
    pool_gain_out, pool_shift_out, squeeze_out, time_out, space_out, qkv_out, proj_out,
    up_grad_out, down_out, time_rows, *, plan, unit,
):
    for index in range(grad_in.shape[0]):
        grad_in_out[index] = grad_in[index]
        block_out_out[index] = block_out[index]
    head = lax.axis_index("head")
    rows_small = small.shape[1]

    def take(row, target):
        count = target.shape[0]
        done = 0
        while done < count:
            block, offset = divmod(row + done, rows_small)
            size = min(count - done, rows_small - offset)
            target[done : done + size] = small[block, offset : offset + size, : target.shape[1]]
            done += size

    def take_wide(row, target, at):
        for index in range(target.shape[1] // LANES):
            block, offset = divmod(row + index, rows_small)
            target[at : at + 1, index * LANES : (index + 1) * LANES] = small[
                block, offset : offset + 1
            ]

    per_row = gain_out.shape[1] // LANES
    for index in range(2):
        take_wide(plan["gain"] + index * per_row, gain_out, index)
        take_wide(plan["shift"] + index * per_row, shift_out, index)
        take_wide(plan["rows"] + index * per_row, rows_out, index)
    width = joined_out.shape[1]
    group = width // 2
    heads = group // unit
    joined_rows = 3 * heads
    up_rows = up_out.shape[0]
    for which in range(2):

        @pl.when(head == which)
        def _():
            for member in range(3):
                for side in range(2):
                    for index in range(heads):
                        row = plan["joined"] + (2 * which + side) * joined_rows
                        block, offset = divmod(row + member * heads + index, rows_small)
                        at = side * group + index * unit
                        joined_out[member : member + 1, at : at + unit] = small[
                            block, offset : offset + 1, :unit
                        ]
            take(plan["up"] + which * up_rows, up_out)

    for member in range(3):
        take(plan["taps"] + member * 27, taps_out.at[member])
        qkv_out[member] = qkv[:, member * width : (member + 1) * width]
    take(plan["pool_gain"], pool_gain_out)
    take(plan["pool_shift"], pool_shift_out)
    take(plan["time"], time_rows)
    time_out[...] = time_rows[...].T
    for index in range(2):
        count = squeeze_out.shape[1]
        take(plan["squeeze"] + index * count, squeeze_out.at[index])
        for spot in range(space_out.shape[0]):
            block, offset = divmod(
                plan["space"] + index * space_out.shape[0] + spot, rows_small
            )
            space_out[spot, index : index + 1] = small[block, offset : offset + 1, :unit]
    proj_width, up_width = proj_out.shape[1], up_grad_out.shape[1]
    proj_out[...] = early[:, :proj_width]
    up_grad_out[...] = early[:, proj_width : proj_width + up_width]
    at = proj_width + up_width
    first = early.shape[1] - at
    down_out[:, :first] = early[:, at:]
    down_out[:, first:] = late[...]


def unpack(small, qkv, early, late, grad_in, block_out, plan, unit, hidden_width, table_rows):
    shard_rows, width = qkv.shape
    model = grad_in.shape[2]
    rest_width = early.shape[1] + late.shape[1]
    out = jax.ShapeDtypeStruct
    vmem = pl.BlockSpec(memory_space=pltpu.VMEM)
    shapes = [
        out(grad_in.shape, BF),
        out(block_out.shape, BF),
        out((2, model), F32),
        out((2, model), F32),
        out((2, model), F32),
        out((3, width // 3), F32),
        out((hidden_width // LANES, LANES), F32),
        out((3, 27, unit), F32),
        out((3, unit), F32),
        out((3, unit), F32),
        out((2, FRAMES // MEMF, unit), F32),
        out((unit, table_rows), F32),
        out((2 * SIDE - 1, 2, unit), F32),
        out((3, shard_rows, width // 3), F32),
        out((shard_rows, rest_width - 2 * hidden_width), F32),
        out((shard_rows, hidden_width), F32),
        out((shard_rows, hidden_width), F32),
    ]
    return pl.pallas_call(
        partial(unpack_kernel, plan=plan, unit=unit),
        in_specs=[vmem] * 6,
        out_specs=[vmem] * len(shapes),
        out_shape=shapes,
        scratch_shapes=[pltpu.VMEM((table_rows, unit), F32)],
        compiler_params=pltpu.CompilerParams(vmem_limit_bytes=VMEM_LIMIT),
        name="unpack_results",
    )(small, qkv, early, late, grad_in, block_out)


def tail(
    row_own, row_recv, x, middle_grad, grads, joined_sum, gain, taps, pool_gain, pool_shift,
    bias_grad, hot, space_hot, cached, mem_own, mem_recv, vectors, up_bias, rest, clip_count, devices,
    unit, table_rows,
):
    clips, rows, model = x.shape
    wide = grads.shape[3]
    heads = wide // (3 * LANES)
    width = 3 * 2 * heads * unit
    outers = clip_count // 2
    shard_rows = model // (4 * outers)
    chunks = 3
    cols = wide // chunks
    plan = {}
    at = 0
    for name, count in (
        ("gain", 2 * model // LANES),
        ("shift", 2 * model // LANES),
        ("rows", 2 * model // LANES),
        ("joined", 4 * wide // LANES),
        ("up", 2 * up_bias.shape[1] // LANES),
        ("taps", 81),
        ("pool_gain", 3),
        ("pool_shift", 3),
        ("squeeze", 2 * FRAMES // MEMF),
        ("time", table_rows),
        ("space", 2 * (2 * SIDE - 1)),
    ):
        plan[name] = at
        at += count
    block = -(-at // (devices * 8)) * 8
    small_shape = (2, 4, outers, block, LANES)
    out = jax.ShapeDtypeStruct
    dma = pltpu.SemaphoreType.DMA
    vmem = pl.BlockSpec(memory_space=pltpu.VMEM)
    shapes = [
        out((clips, rows, model), BF),
        out((shard_rows, width), F32),
        out((shard_rows, rest.shape[2]), F32),
        out(small_shape, F32),
    ]
    results = pl.pallas_call(
        partial(tail_kernel, unit=unit, plan=plan, table_rows=table_rows),
        in_specs=[vmem] * 19,
        out_specs=[vmem] * len(shapes),
        out_shape=shapes,
        scratch_shapes=[
            pltpu.VMEM((chunks, 3, outers, shard_rows, cols), BF),
            pltpu.VMEM((chunks, outers, 2, shard_rows, cols), BF),
            pltpu.VMEM((chunks, outers, 2, shard_rows, cols), BF),
            pltpu.VMEM(small_shape, F32),
            pltpu.VMEM(small_shape[1:], F32),
            pltpu.VMEM((3,) + small_shape[2:], F32),
            pltpu.VMEM(small_shape[2:], F32),
            pltpu.VMEM((clips, rows, model), BF),
            pltpu.VMEM(rest.shape, BF),
            dma((2, clips)),
            dma((2, chunks, 3)),
            dma((2, chunks, outers)),
            dma((2, 2)),
            dma((2, 2, 3)),
            dma((2, 2, outers)),
            dma((2, outers)),
        ],
        compiler_params=pltpu.CompilerParams(
            collective_id=0, has_side_effects=True, vmem_limit_bytes=VMEM_LIMIT
        ),
        name="tail_gradients",
    )(
        row_own, row_recv, x, middle_grad, grads, joined_sum, gain, taps, pool_gain, pool_shift,
        bias_grad, hot, space_hot, cached, mem_own, mem_recv, vectors, up_bias, rest,
    )
    return results, plan


def feed_kernel(
    att_own, att_recv, x, cot, weights, gain, shift, out_shift, up_shift,
    block_out, middle_grad, grad_own, grad_send, grad_rest, vectors, up_bias,
    attended, normed, cots, active, hidden_low, branch, middle, send, recv, sems,
):
    clips, rows, model = x.shape
    span = attended.shape[0] // clips
    group = att_own.shape[2]
    head_width = 2 * group
    hidden_width = up_shift.shape[1]
    tiles = 4
    tile = hidden_width // tiles
    clip_at = lax.axis_index("clip")
    frame = lax.axis_index("frame")
    head = lax.axis_index("head")
    partner = (clip_at, frame, 1 - head)

    def cross(kind, index):
        return pltpu.make_async_remote_copy(
            src_ref=send.at[kind, index], dst_ref=recv.at[kind, index],
            send_sem=sems.at[0, kind, index], recv_sem=sems.at[1, kind, index],
            device_id=partner, device_id_type=MESH_ID,
        )

    barrier = pltpu.get_barrier_semaphore()
    pl.semaphore_signal(barrier, inc=1, device_id=partner, device_id_type=MESH_ID)
    for ref in (attended, normed, cots, branch):
        ref[...] = jnp.zeros_like(ref)

    def assemble(low, high):
        for index in range(clips):
            at = slice(index * span, index * span + rows)
            attended[at, :group] = low[index]
            attended[at, group:] = high[index]

    @pl.when(frame == 0)
    def _():
        assemble(att_own, att_recv)

    @pl.when(frame == 1)
    def _():
        assemble(att_recv, att_own)

    for index in range(clips):
        cots[index * span : index * span + rows] = cot[index]
    pl.semaphore_wait(barrier, 1)

    def block_rows(index):
        return pl.ds(pl.multiple_of(index * span, 16), span)

    def project(index):
        part = dot_f32(attended[block_rows(index)], weights[:, :head_width], ((1,), (1,)))
        send[0, index] = part[:rows].astype(BF)
        cross(0, index).start()

    each(0, clips, project)

    def feed(index, bias_sum):
        cross(0, index).wait_recv()
        branch_rows = send[0, index].astype(F32) + recv[0, index].astype(F32)
        value = x[index].astype(F32) + branch_rows + out_shift[0:1]
        middle[index] = value
        centred, rate = row_stats(value)
        low = (centred * rate * gain[1:2] + shift[1:2]).astype(BF)
        at = pl.multiple_of(index * span, 16)
        normed[pl.ds(at, rows)] = low
        low = normed[block_rows(index)]
        cot_rows = cots[block_rows(index)]
        out_part = jnp.zeros((span, model), F32)
        norm_part = jnp.zeros((span, model), F32)
        sums = []
        for step in range(tiles):
            lanes = slice(step * tile, (step + 1) * tile)
            up = weights[:, head_width + step * tile : head_width + (step + 1) * tile]
            at = head_width + hidden_width + step * tile
            down = weights[:, at : at + tile]
            hidden = dot_f32(low, up, ((1,), (0,))) + up_shift[:, lanes]
            incoming = dot_f32(cot_rows, down, ((1,), (0,)))
            normal = 0.5 * (1.0 + lax.erf(hidden * (0.5**0.5)))
            density = jnp.exp(hidden * hidden * -0.5) * ((2.0 * np.pi) ** -0.5)
            acted = (hidden * normal).astype(BF)
            back = (incoming * (normal + hidden * density)).astype(BF)
            active[block_rows(index), lanes] = acted
            hidden_low[block_rows(index), lanes] = back
            sums.append(jnp.sum(back.astype(F32), axis=0, keepdims=True))
            out_part = out_part + dot_f32(acted, down, ((1,), (1,)))
            norm_part = norm_part + dot_f32(back, up, ((1,), (1,)))
        send[1, index] = norm_part[:rows].astype(BF)
        cross(1, index).start()
        send[2, index] = out_part[:rows].astype(BF)
        cross(2, index).start()
        return bias_sum + jnp.concatenate(sums, axis=1)

    up_bias[...] = lax.fori_loop(0, clips, feed, jnp.zeros((1, hidden_width), F32))

    wide = hidden_width // 2
    for step in range(2):
        lanes = slice(step * wide, (step + 1) * wide)
        value = dot_f32(normed[...], hidden_low[:, lanes], ((0,), (0,)))
        at = head_width + step * wide
        grad_rest[:, at : at + wide] = value.astype(BF)
        value = dot_f32(cots[...], active[:, lanes], ((0,), (0,)))
        at = head_width + hidden_width + step * wide
        grad_rest[:, at : at + wide] = value.astype(BF)

    def back(index, sums):
        gain_sum, shift_sum, first_sum, second_sum = sums
        cross(1, index).wait_recv()
        incoming = send[1, index].astype(F32) + recv[1, index].astype(F32)
        centred, rate = row_stats(middle[index])
        normal = centred * rate
        scaled = incoming * gain[1:2]
        mean_scaled = jnp.sum(scaled, axis=-1, keepdims=True) * (1.0 / model)
        mean_both = jnp.sum(scaled * normal, axis=-1, keepdims=True) * (1.0 / model)
        cot_rows = cot[index].astype(F32)
        value = cot_rows + rate * (scaled - mean_scaled - normal * mean_both)
        middle_grad[index] = value
        at = pl.multiple_of(index * span, 16)
        branch[pl.ds(at, rows)] = value.astype(BF)
        part = dot_f32(branch[block_rows(index)], weights[:, :head_width], ((1,), (0,)))
        part = part[:rows].astype(BF)

        @pl.when(frame == 0)
        def _():
            grad_own[index] = part[:, :group]
            grad_send[index] = part[:, group:]

        @pl.when(frame == 1)
        def _():
            grad_send[index] = part[:, :group]
            grad_own[index] = part[:, group:]

        cross(2, index).wait_recv()
        out_rows = send[2, index].astype(F32) + recv[2, index].astype(F32)
        block_out[index] = (middle[index] + out_rows + out_shift[1:2]).astype(BF)

        def column(rows_here):
            return jnp.sum(rows_here, axis=0, keepdims=True)

        return (
            gain_sum + column(incoming * normal),
            shift_sum + column(incoming),
            first_sum + column(value),
            second_sum + column(cot_rows),
        )

    start = tuple(jnp.zeros((1, model), F32) for _ in range(4))
    sums = lax.fori_loop(0, clips, back, start)
    for row in range(4):
        vectors[row : row + 1] = sums[row]
    value = dot_f32(branch[...], attended[...], ((0,), (0,)))
    grad_rest[:, :head_width] = value.astype(BF)
    for kind in range(3):
        each(0, clips, lambda index: cross(kind, index).wait_send())


def feed(att_own, att_recv, x, cot, weights, gain, shift, out_shift, up_shift):
    clips, rows, model = x.shape
    group = att_own.shape[2]
    hidden_width = up_shift.shape[1]
    span = -(-rows // 16) * 16
    out = jax.ShapeDtypeStruct
    vmem = pl.BlockSpec(memory_space=pltpu.VMEM)
    shapes = [
        out((clips, rows, model), BF),
        out((clips, rows, model), F32),
        out((clips, rows, group), BF),
        out((clips, rows, group), BF),
        out(weights.shape, BF),
        out((4, model), F32),
        out((1, hidden_width), F32),
    ]
    return pl.pallas_call(
        feed_kernel,
        in_specs=[vmem] * 9,
        out_specs=[vmem] * len(shapes),
        out_shape=shapes,
        scratch_shapes=[
            pltpu.VMEM((clips * span, 2 * group), BF),
            pltpu.VMEM((clips * span, model), BF),
            pltpu.VMEM((clips * span, model), BF),
            pltpu.VMEM((clips * span, hidden_width), BF),
            pltpu.VMEM((clips * span, hidden_width), BF),
            pltpu.VMEM((clips * span, model), BF),
            pltpu.VMEM((clips, rows, model), F32),
            pltpu.VMEM((3, clips, rows, model), BF),
            pltpu.VMEM((3, clips, rows, model), BF),
            pltpu.SemaphoreType.DMA((2, 3, clips)),
        ],
        compiler_params=pltpu.CompilerParams(
            collective_id=4, has_side_effects=True, vmem_limit_bytes=VMEM_LIMIT
        ),
        name="feed_forward_both_ways",
    )(att_own, att_recv, x, cot, weights, gain, shift, out_shift, up_shift)


def precise(pattern, *operands):
    return jnp.einsum(pattern, *operands, precision=lax.Precision.HIGHEST)


def split_groups(value, which, axis):
    half = value.shape[axis] // 2
    low = lax.slice_in_dim(value, 0, half, axis=axis)
    high = lax.slice_in_dim(value, half, None, axis=axis)
    first = which == 0
    return jnp.where(first, low, high), jnp.where(first, high, low)


def join_groups(own, peer, which, axis):
    first = which == 0
    return jnp.concatenate([jnp.where(first, own, peer), jnp.where(first, peer, own)], axis=axis)


def time_choices(stride_group, memory_place, which, own, table_rows):
    local = jnp.arange(own, dtype=jnp.int32)
    times = jnp.concatenate([which * own + local, (1 - which) * own + local])
    stride = jnp.left_shift(jnp.int32(2), stride_group)[:, None, None]
    offset = 8 * (FRAMES - 1)
    current = stride * (times[None, :, None] - times[None, None, :]) + offset
    slots = [memory_place[:, index : index + 1] for index in range(4)]
    first = jnp.concatenate([slots[2], slots[0], slots[3], slots[1]], axis=1)
    second = jnp.concatenate([slots[3], slots[1], slots[2], slots[0]], axis=1)
    places = jnp.where(which == 0, first, second)
    memory = stride * times[None, :, None] + places[:, None, :] + offset
    chosen = jnp.concatenate([current, memory], axis=2)
    return (chosen[..., None] == jnp.arange(table_rows, dtype=jnp.int32)).astype(F32)


def space_choices():
    places = np.arange(SIDE)
    offsets = places[:, None] - places[None, :] + SIDE - 1
    hot = offsets.reshape(-1)[:, None] == np.arange(2 * SIDE - 1)[None, :]
    return jnp.asarray(hot.astype(np.float32))


def space_sums():
    spans = 2 * SIDE - 1
    hot = np.zeros((32, BIAS_COLS), np.float32)
    for axis in range(2):
        for query in range(SIDE):
            for key in range(SIDE):
                col = SPACE_AT + axis * CELLS + query * SIDE + key
                hot[axis * spans + query - key + SIDE - 1, col] = 1.0
    return hot


def wide_rows(rows, heads):
    count, members, unit = rows.shape
    padded = jnp.pad(rows, ((0, 0), (0, 0), (0, LANES - unit)))
    spread = jnp.broadcast_to(padded[:, :, None], (count, members, heads, LANES))
    return spread.reshape(count, members * heads * LANES)


def local(
    clips_in,
    cached_kv,
    old_memory,
    stride_group,
    memory_place,
    norm_gain,
    norm_shift,
    qkv_weight,
    qkv_shift,
    pool_kernel,
    pool_gain,
    pool_shift,
    squeeze_kernel,
    time_table,
    space_tables,
    proj_weight,
    out_shift,
    up_weight,
    up_shift,
    down_weight,
    cotangent,
):
    clip_count, rows_clip, model_width = clips_in.shape
    head_width = qkv_weight.shape[2]
    unit = pool_gain.shape[1]
    head_count = head_width // unit
    frame_count = lax.axis_size("frame")
    heads = head_count // frame_count
    own_frames = rows_clip // CELLS
    group_width = heads * unit
    group_span = FRAMES // MEMF
    scale = unit ** (-0.5)
    which = lax.axis_index("frame")
    into_np, outof_np = placement(frame_count)
    keys_np, mask_np, pad_np = bias_constants(frame_count)
    consts = (
        jnp.asarray(into_np, BF),
        jnp.asarray(outof_np, BF),
        jnp.asarray(keys_np, BF),
        jnp.asarray(mask_np),
        jnp.asarray(pad_np),
    )

    cached_flat = cached_kv.reshape(clip_count, rows_clip, 2 * head_width)
    time_hot = time_choices(stride_group, memory_place, which, own_frames, time_table.shape[0])
    time_rows = precise("ctkr,rd->ctkd", time_hot, time_table).reshape(clip_count, -1, unit)
    space_hot = space_choices()
    space_rows = precise("pr,xrd->xpd", space_hot, space_tables).reshape(2 * CELLS, unit)
    space_rows = jnp.broadcast_to(space_rows[None], (clip_count,) + space_rows.shape)
    bias = jnp.concatenate(
        [
            jnp.pad(time_rows, ((0, 0), (0, SPACE_AT - time_rows.shape[1]), (0, LANES - unit))),
            jnp.pad(
                space_rows,
                ((0, 0), (0, BIAS_COLS - SPACE_AT - 2 * CELLS), (0, LANES - unit)),
            ),
        ],
        axis=1,
    )
    bias = bias * (1.0 / scale)
    inputs = (
        clips_in, qkv_weight.transpose(1, 0, 2), norm_gain, norm_shift, qkv_shift, cached_flat,
        old_memory.reshape(clip_count, -1, 2 * head_width), squeeze_kernel, proj_weight.T, up_weight,
        down_weight.T,
    )
    clip_axis = lax.axis_size("clip")
    if qkv_weight.shape[0] % 16:
        attn_group, packed, normed, mem_own, mem_peer, column = project_plain(
            *inputs, clip_axis, unit
        )
        forward = attention_forward(
            packed, mem_own, mem_peer, column, consts, pool_kernel, pool_gain, pool_shift, bias,
            scale, unit, rows_clip,
        )
    else:
        attn_group, packed, normed, *forward = front(
            *inputs, consts, pool_kernel, pool_gain, pool_shift, bias, scale, clip_axis, unit
        )
    attended_own, attended_peer, rest_full = forward[:3]
    rest_full = rest_full.reshape(model_width, -1)
    saved = forward[3:]
    block_out, middle_grad, attended_grad_own, attended_grad_send, grad_rest, vectors, up_grads = (
        feed(
            attended_own, attended_peer, clips_in, cotangent, rest_full, norm_gain,
            norm_shift, out_shift, up_shift.reshape(1, -1),
        )
    )
    outers = lax.axis_size("clip") // 2
    grad_rest = grad_rest.reshape(outers, 4, -1, grad_rest.shape[1])
    backward = attention_backward(
        packed, normed, attn_group, attended_grad_own, attended_grad_send, grad_rest, consts,
        pool_kernel, pool_gain, bias, saved, scale, unit,
    )
    row_own, row_recv, mem_grad_own, mem_grad_peer = backward[:4]
    taps_grad, pool_gain_grad, pool_shift_grad, bias_grad = backward[4:8]
    attn_grad, joined_grad, rest_part, rest_early = backward[8:]

    time_count = time_rows.shape[1]
    hot = time_hot.reshape(clip_count, time_count, -1).astype(BF)
    hot = jnp.pad(hot, ((0, 0), (0, 0), (0, -hot.shape[2] % LANES)))
    devices = lax.axis_size("clip") * frame_count * lax.axis_size("head")
    (grad_in, qkv_shard, rest_late, small), plan = tail(
        row_own, row_recv, clips_in, middle_grad,
        attn_grad.reshape(outers, 4, -1, attn_grad.shape[1]), joined_grad, norm_gain, taps_grad,
        pool_gain_grad, pool_shift_grad, bias_grad, hot,
        jnp.asarray(space_sums(), BF), cached_flat, mem_grad_own, mem_grad_peer, vectors,
        up_grads, rest_part, lax.axis_size("clip"), devices, unit, time_table.shape[0],
    )
    (
        grad_in, block_out, gain_sums, shift_sums, out_sums, qkv_bias_sum, up_bias_sum, kernel_sum,
        pool_gain_sum, pool_shift_sum, squeeze_sum, time_sum, space_sum, qkv_shard, proj_shard,
        up_shard, down_shard,
    ) = unpack(
        small.reshape((devices,) + small.shape[3:]), qkv_shard, rest_early, rest_late, grad_in, block_out, plan, unit,
        up_weight.shape[1], time_table.shape[0],
    )
    return (
        block_out,
        grad_in,
        gain_sums,
        shift_sums,
        qkv_shard.transpose(1, 0, 2),
        qkv_bias_sum,
        kernel_sum,
        pool_gain_sum,
        pool_shift_sum,
        squeeze_sum,
        time_sum.T,
        space_sum.transpose(1, 0, 2),
        proj_shard.T,
        out_sums,
        up_shard,
        up_bias_sum.reshape(-1),
        down_shard.T,
    )


def solution(mesh):
    return jax.shard_map(
        local,
        mesh=mesh,
        in_specs=(
            P("clip", "frame", None),
            P("clip", "frame", None, "head"),
            P("clip", "frame", None, "head"),
            P("clip"),
            P("clip", None),
            P(),
            P(),
            P(("clip", "frame"), None, "head"),
            P(None, "head"),
            P(),
            P(),
            P(),
            P(),
            P(),
            P(),
            P("head", ("clip", "frame")),
            P(),
            P(("clip", "frame"), "head"),
            P("head"),
            P("head", ("clip", "frame")),
            P("clip", "frame", None),
        ),
        out_specs=(
            P("clip", "frame", None),
            P("clip", "frame", None),
            P(),
            P(),
            P(("clip", "frame"), None, "head"),
            P(None, "head"),
            P(),
            P(),
            P(),
            P(),
            P(),
            P(),
            P("head", ("clip", "frame")),
            P(),
            P(("clip", "frame"), "head"),
            P("head"),
            P("head", ("clip", "frame")),
        ),
        check_vma=False,
    )
```

```python
from functools import partial

import jax
import jax.numpy as jnp
import numpy as np
from jax import lax
from jax.experimental import pallas as pl
from jax.experimental.pallas import tpu as pltpu
from jax.sharding import PartitionSpec as P

FRAMES = 8
MEMF = 2
SIDE = 7
CELLS = SIDE * SIDE
LANES = 128
HALF = 208
QROWS = 2 * HALF
GRID_ROWS = FRAMES * SIDE * 8
MEM_AT = QROWS
MEM_PAD = 112
MEM_BACK = 64
MEM_STEP = 56
TURN_STEP = 3
TURN_PAIRS = 1
TURN_LAG = 4
KROWS = 640
BIAS_COLS = 256
SPACE_AT = 128
PAD_LANE = 127
BF = jnp.bfloat16
F32 = jnp.float32
VMEM_LIMIT = 60 * 1024 * 1024
MESH_ID = pl.DeviceIdType.MESH


def dot_f32(a, b, dims):
    return lax.dot_general(a, b, (dims, ((), ())), preferred_element_type=F32)


def frame_order(first, own):
    rest = [t for t in range(FRAMES) if not first * own <= t < (first + 1) * own]
    return list(range(first * own, (first + 1) * own)) + rest


def placement(frame_count):
    own = FRAMES // frame_count
    into = np.zeros((frame_count, GRID_ROWS, QROWS), np.float32)
    for first in range(frame_count):
        for slot, frame in enumerate(frame_order(first, own)):
            base = (slot // own) * HALF + (slot % own) * CELLS
            for high in range(SIDE):
                for wide in range(SIDE):
                    row = (frame * SIDE + high) * 8 + wide
                    into[first, row, base + high * SIDE + wide] = 1.0
    return into, np.ascontiguousarray(into.transpose(0, 2, 1))


def bias_constants(frame_count):
    own = FRAMES // frame_count
    frames_all = FRAMES + 2 * MEMF
    keys = np.zeros((BIAS_COLS, KROWS), np.float32)
    valid = np.zeros((KROWS,), bool)

    def mark(col, slot, high, wide):
        valid[col] = True
        for query in range(FRAMES):
            keys[query * frames_all + slot, col] = 1.0
        for place in range(SIDE):
            keys[SPACE_AT + place * SIDE + high, col] = 1.0
            keys[SPACE_AT + CELLS + place * SIDE + wide, col] = 1.0

    mask = np.zeros((QROWS, BIAS_COLS), np.float32)
    for slot in range(FRAMES):
        base = (slot // own) * HALF + (slot % own) * CELLS
        for high in range(SIDE):
            for wide in range(SIDE):
                row = base + high * SIDE + wide
                mark(row, slot, high, wide)
                mask[row, slot * frames_all : (slot + 1) * frames_all] = 1.0
                mask[row, SPACE_AT + high * SIDE : SPACE_AT + (high + 1) * SIDE] = 1.0
                low = SPACE_AT + CELLS + wide * SIDE
                mask[row, low : low + SIDE] = 1.0
    for group in range(2):
        for inner in range(MEMF):
            slot = FRAMES + group * MEMF + inner
            for high in range(SIDE):
                for wide in range(SIDE):
                    col = MEM_AT + group * MEM_PAD + inner * MEM_STEP + high * SIDE + wide
                    mark(col, slot, high, wide)
    keys[PAD_LANE, ~valid] = -1e9
    pad_row = np.zeros((1, BIAS_COLS), np.float32)
    pad_row[0, PAD_LANE] = 1.0
    return keys, mask, pad_row


def spread_heads(source, target, rows_at, units, unit, first=0):
    count = source.shape[0]
    for index in range(units):
        at = (first + index) * unit
        target[rows_at : rows_at + count, index * LANES : index * LANES + unit] = source[
            :, at : at + unit
        ]


def spread_tables(kernel_ref, taps, pairs, heads, unit):
    taps[...] = jnp.zeros_like(taps)
    for _, target in pairs:
        target[...] = jnp.zeros_like(target)
    for member in range(3):
        for index in range(heads):
            at = (member * heads + index) * LANES
            for tap in range(27):
                row = kernel_ref[member, tap : tap + 1]
                taps[tap, :, at : at + unit] = jnp.broadcast_to(row, (8, unit))
            for source, target in pairs:
                target[:, at : at + unit] = source[member : member + 1]


def load_shifted(field, shifted):
    grid = field.reshape(FRAMES, SIDE, 8, field.shape[-1])
    flat = field.reshape(FRAMES * SIDE, 8, field.shape[-1])
    shifted[1, 1 : FRAMES + 1, 1 : SIDE + 1] = grid
    shifted[0, 1 : FRAMES + 1, 1 : SIDE + 1] = pltpu.roll(flat, 1, 1).reshape(grid.shape)
    shifted[2, 1 : FRAMES + 1, 1 : SIDE + 1] = pltpu.roll(flat, 7, 1).reshape(grid.shape)


def convolve(shifted, taps, target, flip):
    tiles = target.shape[-1] // LANES

    def step(pair, carry):
        for sub in range(2):
            frame = pair * 2 + sub
            for tile in range(tiles):
                lanes = slice(tile * LANES, (tile + 1) * LANES)
                total = None
                for i in range(3):
                    for k in range(3):
                        rows = shifted[k, frame + i, :, :, lanes]
                        for j in range(3):
                            if flip:
                                tap = (2 - i) * 9 + (2 - j) * 3 + (2 - k)
                            else:
                                tap = i * 9 + j * 3 + k
                            value = rows[j : j + SIDE] * taps[tap, :, lanes][None]
                            total = value if total is None else total + value
                target[frame, :, :, lanes] = total
        return carry

    lax.fori_loop(0, FRAMES // 2, step, 0)


def tap_grads(shifted, grads, target):
    tiles = target.shape[-1] // LANES

    def step(index, carry):
        lanes = pl.ds(pl.multiple_of(index * LANES, LANES), LANES)

        def inner(frame, sums):
            centre = grads[frame + 1, 1 : SIDE + 1, :, lanes]
            new = []
            for i in range(3):
                for k in range(3):
                    rows = shifted[k, frame + i, :, :, lanes]
                    for j in range(3):
                        parts = [rows[j + high] * centre[high] for high in range(SIDE)]
                        parts.append(sums[len(new)])
                        while len(parts) > 1:
                            pairs = zip(parts[::2], parts[1::2])
                            parts = [left + right for left, right in pairs]
                        new.append(parts[0])
            return tuple(new)

        start = tuple(jnp.zeros((8, LANES), F32) for _ in range(27))
        sums = lax.fori_loop(0, FRAMES, inner, start, unroll=4)
        for i in range(3):
            for k in range(3):
                for j in range(3):
                    target[i * 9 + j * 3 + k, :, lanes] += sums[(i * 3 + k) * 3 + j]
        return carry

    lax.fori_loop(0, tiles, step, 0)


def head_stats(values, unit):
    average = jnp.sum(values, axis=-1, keepdims=True) * (1.0 / unit)
    lane = lax.broadcasted_iota(jnp.int32, values.shape, 1)
    centred = jnp.where(lane < unit, values - average, 0.0)
    variance = jnp.sum(centred * centred, axis=-1, keepdims=True) * (1.0 / unit)
    return centred, lax.rsqrt(variance + 1e-06)


def frame_partner():
    return (lax.axis_index("clip"), 1 - lax.axis_index("frame"), lax.axis_index("head"))


def partner_copy(source, target, send_sem, recv_sem):
    return pltpu.make_async_remote_copy(
        src_ref=source, dst_ref=target, send_sem=send_sem, recv_sem=recv_sem,
        device_id=frame_partner(), device_id_type=MESH_ID,
    )


def side_partner():
    clip = lax.axis_index("clip")
    across = (clip // 2) * 2 + 1 - clip % 2
    return (across, lax.axis_index("frame"), lax.axis_index("head"))


def side_copy(source, target, send_sem, recv_sem):
    return pltpu.make_async_remote_copy(
        src_ref=source, dst_ref=target, send_sem=send_sem, recv_sem=recv_sem,
        device_id=side_partner(), device_id_type=MESH_ID,
    )


def greet_partner():
    barrier = pltpu.get_barrier_semaphore()
    pl.semaphore_signal(barrier, inc=1, device_id=frame_partner(), device_id_type=MESH_ID)
    pl.semaphore_wait(barrier, 1)


def plane_stage(column_ref, rest_full, side_sems, pair_sems, turn_sems, own_sem):
    outers = column_ref.shape[0]
    split = min(TURN_PAIRS, outers)
    outer = lax.axis_index("clip") // 2
    inner = lax.axis_index("clip") % 2
    frame = lax.axis_index("frame")
    place = inner * 2 + frame
    side_place = (1 - inner) * 2 + frame
    pair_place = inner * 2 + 1 - frame
    turn_place = (1 - inner) * 2 + 1 - frame
    own_copy = pltpu.make_async_copy(column_ref, rest_full.at[:, place], own_sem)

    def side_move(at, source, target):
        return side_copy(source, target, side_sems.at[0, at], side_sems.at[1, at])

    def pair_move(at, source, target):
        return partner_copy(source, target, pair_sems.at[0, at], pair_sems.at[1, at])

    def to_side(at):
        return side_move(at, column_ref.at[at], rest_full.at[at, place])

    def to_pair(at):
        return pair_move(at, column_ref.at[at], rest_full.at[at, place])

    def turn_side(at):
        block = rest_full.at[at, pair_place]
        return side_copy(block, block, turn_sems.at[0, at], turn_sems.at[1, at])

    def turn_pair(at):
        block = rest_full.at[at, side_place]
        return partner_copy(block, block, turn_sems.at[0, at], turn_sems.at[1, at])

    def turned(at):
        block = rest_full.at[at, turn_place]
        return side_copy(block, block, turn_sems.at[0, at], turn_sems.at[1, at])

    def side_arrival(at):
        block = rest_full.at[at, side_place]
        return side_move(at, block, block)

    def pair_arrival(at):
        block = rest_full.at[at, pair_place]
        return pair_move(at, block, block)

    def send(at):
        to_side(at).start()
        to_pair(at).start()

    def spot(step):
        return (outer + step) % outers

    def turn(step):
        at = spot(step)
        if step < split:
            side_arrival(at).wait_recv()
            turn_pair(at).start()
        else:
            pair_arrival(at).wait_recv()
            turn_side(at).start()

    def finish():
        own_copy.wait()
        each(0, split, lambda step: pair_arrival(spot(step)).wait_recv())
        each(split, outers, lambda step: side_arrival(spot(step)).wait_recv())
        each(0, outers, lambda at: turned(at).wait_recv())
        each(0, split, lambda step: turn_pair(spot(step)).wait_send())
        each(split, outers, lambda step: turn_side(spot(step)).wait_send())
        each(0, outers, lambda at: to_side(at).wait_send())
        each(0, outers, lambda at: to_pair(at).wait_send())

    return own_copy, send, turn, finish


def attend_clip(
    packed, mem_own, mem_peer, frame, into_ref, outof_ref, gain_ref, shift_ref, bias_ref,
    keyhot_ref, mask_ref, pad_ref, out_own, out_peer, q_out, k_out, v_out, p_out, c_out, shifted,
    taps, heads, unit, scale, after_conv,
):
    units = 3 * heads
    own_rows = out_own.shape[0]
    load_shifted(dot_f32(into_ref[frame], packed[...], ((1,), (0,))), shifted)
    conv = c_out.at[0]
    convolve(shifted, taps, conv, False)
    after_conv()
    k_out[0, MEM_AT:, :] = jnp.zeros((KROWS - MEM_AT, heads * LANES), BF)
    v_out[0, MEM_AT:, :] = jnp.zeros((KROWS - MEM_AT, heads * LANES), BF)
    spread_heads(mem_own, k_out.at[0], MEM_AT, heads, unit, 0 * heads)
    spread_heads(mem_own, v_out.at[0], MEM_AT, heads, unit, 1 * heads)
    spread_heads(mem_peer, k_out.at[0], MEM_AT + MEM_PAD, heads, unit, 0 * heads)
    spread_heads(mem_peer, v_out.at[0], MEM_AT + MEM_PAD, heads, unit, 1 * heads)
    for index in range(units):
        lanes = slice(index * LANES, (index + 1) * LANES)
        block = conv[:, :, :, lanes].reshape(GRID_ROWS, LANES)
        centred, rate = head_stats(block, unit)
        normal = centred * rate * gain_ref[:, lanes] + shift_ref[:, lanes]
        parts = [normal.astype(BF)] if index % heads == 0 else parts + [normal.astype(BF)]
        if index % heads == heads - 1:
            whole = jnp.concatenate(parts, axis=1)
            rows = dot_f32(outof_ref[frame], whole, ((1,), (0,))).astype(BF)
            (q_out, k_out, v_out)[index // heads][0, 0:QROWS, :] = rows

    bias = bias_ref[0]
    bias_high = bias.astype(BF)
    bias_low = (bias - bias_high.astype(F32)).astype(BF)
    for head in range(heads):
        lanes = slice(head * LANES, (head + 1) * LANES)
        keys = k_out[0, :, lanes]
        values = v_out[0, :, lanes]
        for half in range(2):
            rows = slice(half * HALF, (half + 1) * HALF)
            query = q_out[0, rows, lanes]
            table = dot_f32(query, bias_high, ((1,), (1,))) + dot_f32(query, bias_low, ((1,), (1,)))
            table = table * mask_ref[rows, :] + pad_ref[...]
            table_high = table.astype(BF)
            table_low = (table - table_high.astype(F32)).astype(BF)
            scores = dot_f32(query, keys, ((1,), (1,)))
            scores = scores + dot_f32(table_high, keyhot_ref[...], ((1,), (0,)))
            scores = scores + dot_f32(table_low, keyhot_ref[...], ((1,), (0,)))
            top = jnp.max(scores, axis=-1, keepdims=True)
            weights = jnp.exp((scores - top) * scale)
            total = jnp.sum(weights, axis=-1, keepdims=True)
            probs = (weights * (1.0 / total)).astype(BF)
            p_out[0, head, rows, :] = probs
            mixed = dot_f32(probs, values, ((1,), (0,))) + query.astype(F32)
            target = (out_own, out_peer)[half]
            target[:, head * unit : (head + 1) * unit] = mixed[:own_rows, :unit].astype(BF)


def forward_kernel(
    packed_ref, mem_own_ref, mem_peer_ref, column_ref, into_ref, outof_ref, kernel_ref,
    pool_gain_ref, pool_shift_ref, bias_ref, keyhot_ref, mask_ref, pad_ref,
    out_own, out_recv, rest_full, q_out, k_out, v_out, p_out, c_out,
    shifted, taps, gain_ref, shift_ref, out_send, out_sems, side_sems, pair_sems, turn_sems,
    own_sem,
    *, heads, unit, scale,
):
    clip = pl.program_id(0)
    clips = out_send.shape[0]
    frame = lax.axis_index("frame")

    def out_copy(index):
        return partner_copy(
            out_send.at[index], out_recv.at[index], out_sems.at[0, index], out_sems.at[1, index]
        )

    own_copy, send, turn, finish = plane_stage(
        column_ref, rest_full, side_sems, pair_sems, turn_sems, own_sem
    )

    @pl.when(clip == 0)
    def _():
        barrier = pltpu.get_barrier_semaphore()
        for device in (frame_partner(), side_partner()):
            pl.semaphore_signal(barrier, inc=1, device_id=device, device_id_type=MESH_ID)
        pl.semaphore_wait(barrier, 2)
        each(0, column_ref.shape[0], send)
        own_copy.start()
        shifted[...] = jnp.zeros_like(shifted)
        pairs = ((pool_gain_ref, gain_ref), (pool_shift_ref, shift_ref))
        spread_tables(kernel_ref, taps, pairs, heads, unit)

    @pl.when(clip == jnp.minimum(TURN_STEP, clips - 1))
    def _():
        for step in range(column_ref.shape[0]):
            turn(step)

    attend_clip(
        packed_ref.at[0], mem_own_ref.at[0], mem_peer_ref.at[0], frame, into_ref, outof_ref,
        gain_ref, shift_ref, bias_ref, keyhot_ref, mask_ref, pad_ref, out_own.at[0],
        out_send.at[clip], q_out, k_out, v_out, p_out, c_out, shifted, taps, heads, unit, scale,
        lambda: None,
    )
    out_copy(clip).start()

    @pl.when(clip == clips - 1)
    def _():
        finish()
        for index in range(clips):
            out_copy(index).wait()


def backward_kernel(
    packed_ref, normed_ref, weight_ref, grad_own_ref, grad_send_ref, rest_ref, into_ref, outof_ref,
    kernel_ref, pool_gain_ref, bias_ref, keyhot_ref, mask_ref, q_ref, k_ref, v_ref, p_ref, c_ref,
    row_own, row_recv, mem_own, mem_recv, taps_out, gain_out, shift_out, bias_out, weight_out,
    joined_out, rest_part, rest_out,
    shifted, taps, gain_ref, grads, spread, pooled, peer, mem_send, rest_own, rest_side, rest_send,
    rest_peer, rest_sum, rest_far, weight_sum, keep, cross_send, cross_recv, row_send,
    grad_sems, mem_sems, own_sems, side_sems, rest_sems, far_sems, cross_sems, row_sems,
    *, heads, unit, scale,
):
    units = 3 * heads
    own_rows = grad_own_ref.shape[1]
    clip = pl.program_id(0)
    clips = peer.shape[0]
    clip_at = lax.axis_index("clip")
    frame = lax.axis_index("frame")
    head_at = lax.axis_index("head")

    def grad_copy(index):
        return partner_copy(
            grad_send_ref.at[index], peer.at[index], grad_sems.at[0, index], grad_sems.at[1, index]
        )

    def mem_copy(index):
        return partner_copy(
            mem_send.at[index], mem_recv.at[index], mem_sems.at[0, index], mem_sems.at[1, index]
        )

    def row_copy(index):
        return partner_copy(
            row_send.at[index], row_recv.at[index], row_sems.at[0, index], row_sems.at[1, index]
        )

    def cross_copy(index):
        return pltpu.make_async_remote_copy(
            src_ref=cross_send.at[index], dst_ref=cross_recv.at[index],
            send_sem=cross_sems.at[0, index], recv_sem=cross_sems.at[1, index],
            device_id=(clip_at, frame, 1 - head_at), device_id_type=MESH_ID,
        )

    def finish_rows(index):
        cross_copy(index).wait_recv()
        total = (keep[index].astype(F32) + cross_recv[index].astype(F32)).astype(BF)
        row_own[index] = total[:own_rows]
        row_send[index] = total[HALF : HALF + own_rows]
        row_copy(index).start()

    chunks, outers, _, _, cols = rest_own.shape
    side_at = clip_at % 2
    outer = clip_at // 2
    early = rest_far.shape[0]

    def rest_at(side, chunk):
        return rest_ref.at[:, pl.ds(side * 2, 2), :, pl.ds(chunk * cols, cols)]

    def own_copy(chunk):
        return pltpu.make_async_copy(
            rest_at(side_at, chunk), rest_own.at[chunk], own_sems.at[chunk]
        )

    def over_copy(chunk):
        return side_copy(
            rest_at(1 - side_at, chunk), rest_side.at[chunk], side_sems.at[0, chunk],
            side_sems.at[1, chunk],
        )

    def rest_copy(chunk):
        return partner_copy(
            rest_send.at[chunk], rest_peer.at[chunk], rest_sems.at[0, chunk],
            rest_sems.at[1, chunk],
        )

    def pass_on(chunk):
        own_copy(chunk).wait()
        over_copy(chunk).wait_recv()

        def add(index):
            def total(part):
                first = rest_own[chunk, index, part].astype(F32)
                return (first + rest_side[chunk, index, part].astype(F32)).astype(BF)

            rest_send[chunk, index] = total(1 - frame)
            rest_sum[chunk, index] = total(frame)

        each(0, outers, add)
        rest_copy(chunk).start()

    def far_device(step):
        return (((outer + step) % outers) * 2 + side_at, frame, head_at)

    def far_copy(chunk, step):
        there = (outer + step) % outers
        return pltpu.make_async_remote_copy(
            src_ref=rest_sum.at[chunk, there], dst_ref=rest_far.at[chunk, step],
            send_sem=far_sems.at[0, chunk, step], recv_sem=far_sems.at[1, chunk, step],
            device_id=far_device(step), device_id_type=MESH_ID,
        )

    def settle(chunk):
        rest_copy(chunk).wait_recv()

        def add(index):
            total = rest_sum[chunk, index].astype(F32) + rest_peer[chunk, index].astype(F32)
            if chunk < early:
                rest_sum[chunk, index] = total.astype(BF)
            else:
                rest_part[index] = total.astype(BF)

        each(0, outers, add)
        if chunk < early:
            each(1, outers, lambda step: far_copy(chunk, step).start())

    @pl.when(clip == 0)
    def _():
        barrier = pltpu.get_barrier_semaphore()

        def greet(device):
            pl.semaphore_signal(barrier, inc=1, device_id=device, device_id_type=MESH_ID)

        for device in (frame_partner(), side_partner(), (clip_at, frame, 1 - head_at)):
            greet(device)
        each(1, outers, lambda step: greet(far_device(step)))
        pl.semaphore_wait(barrier, 3 + outers - 1)
        for index in range(clips):
            grad_copy(index).start()
        over_copy(0).start()
        own_copy(0).start()
        shifted[...] = jnp.zeros_like(shifted)
        grads[...] = jnp.zeros_like(grads)
        spread[...] = jnp.zeros_like(spread)
        taps_out[...] = jnp.zeros_like(taps_out)
        gain_out[...] = jnp.zeros_like(gain_out)
        shift_out[...] = jnp.zeros_like(shift_out)
        weight_sum[...] = jnp.zeros_like(weight_sum)
        joined_out[...] = jnp.zeros_like(joined_out)
        spread_tables(kernel_ref, taps, ((pool_gain_ref, gain_ref),), heads, unit)

    def pump(odd):
        for chunk in range(chunks):
            point = min(chunk + 1, 2 * clips - 1)
            if point % 2 == odd:

                @pl.when(clip == point // 2)
                def _():
                    if chunk + 1 < chunks:
                        over_copy(chunk + 1).start()
                        own_copy(chunk + 1).start()
                    pass_on(chunk)
                    if chunk:
                        settle(chunk - 1)

    pump(0)
    load_shifted(dot_f32(into_ref[frame], packed_ref[0], ((1,), (0,))), shifted)
    spread_heads(grad_own_ref.at[0], spread, 0, heads, unit)
    grad_copy(clip).wait_recv()
    spread_heads(peer.at[clip], spread, HALF, heads, unit)
    bias_low = bias_ref[0].astype(BF)
    bias_sum = jnp.zeros((BIAS_COLS, LANES), F32)
    for head in range(heads):
        lanes = slice(head * LANES, (head + 1) * LANES)
        keys = k_ref[0, :, lanes]
        values = v_ref[0, :, lanes]
        keys_grad = jnp.zeros((KROWS, LANES), F32)
        values_grad = jnp.zeros((KROWS, LANES), F32)
        for half in range(2):
            rows = slice(half * HALF, (half + 1) * HALF)
            query = q_ref[0, rows, lanes]
            out_grad = spread[rows, lanes]
            probs = p_ref[0, head, rows, :]
            wide = probs.astype(F32)
            probs_grad = dot_f32(out_grad, values, ((1,), (1,)))
            weighted = wide * probs_grad
            shared = jnp.sum(weighted, axis=-1, keepdims=True)
            score_grad = (weighted - wide * shared).astype(BF)
            values_grad = values_grad + dot_f32(probs, out_grad, ((0,), (0,)))
            keys_grad = keys_grad + dot_f32(score_grad, query, ((0,), (0,)))
            table_grad = dot_f32(score_grad, keyhot_ref[...], ((1,), (1,))) * mask_ref[rows, :]
            table_low = table_grad.astype(BF)
            query_grad = dot_f32(score_grad, keys, ((1,), (0,)))
            query_grad = query_grad + dot_f32(table_low, bias_low, ((1,), (0,)))
            query_grad = query_grad * scale + out_grad.astype(F32)
            pooled[rows, lanes] = query_grad.astype(BF)
            bias_sum = bias_sum + dot_f32(table_low, query, ((0,), (0,)))
        keys_grad = (keys_grad * scale).astype(BF)
        values_grad = values_grad.astype(BF)
        for member, part in enumerate((keys_grad, values_grad)):
            at = ((member + 1) * heads + head) * LANES
            pooled[:, at : at + LANES] = part[:QROWS]
            at = (member * heads + head) * LANES
            low = MEM_AT + MEM_PAD
            mem_own[0, :, at : at + LANES] = part[MEM_AT : MEM_AT + MEM_BACK]
            mem_send[clip, :, at : at + LANES] = part[low : low + MEM_BACK]
    bias_out[0] = bias_sum
    mem_copy(clip).start()

    for index in range(units):
        lanes = slice(index * LANES, (index + 1) * LANES)
        if index % heads == 0:
            member = slice(index * LANES, (index + heads) * LANES)
            arrived = dot_f32(into_ref[frame], pooled[:, member], ((1,), (0,)))
        at = index % heads * LANES
        incoming = arrived[:, at : at + LANES]
        block = c_ref[0, :, :, :, lanes].reshape(GRID_ROWS, LANES)
        centred, rate = head_stats(block, unit)
        normal = centred * rate
        product = incoming * normal
        gain_out[:, lanes] += jnp.sum(product, axis=0, keepdims=True)
        shift_out[:, lanes] += jnp.sum(incoming, axis=0, keepdims=True)
        inner = incoming * gain_ref[:, lanes]
        mean_inner = jnp.sum(inner, axis=-1, keepdims=True) * (1.0 / unit)
        mean_both = jnp.sum(inner * normal, axis=-1, keepdims=True) * (1.0 / unit)
        lane = lax.broadcasted_iota(jnp.int32, block.shape, 1)
        result = rate * (inner - mean_inner - normal * mean_both)
        result = jnp.where(lane < unit, result, 0.0)
        flat = result.reshape(FRAMES * SIDE, 8, LANES)
        shape = (FRAMES, SIDE, 8, LANES)
        grads[1, 1 : FRAMES + 1, 1 : SIDE + 1, :, lanes] = flat.reshape(shape)
        grads[0, 1 : FRAMES + 1, 1 : SIDE + 1, :, lanes] = pltpu.roll(flat, 1, 1).reshape(shape)
        grads[2, 1 : FRAMES + 1, 1 : SIDE + 1, :, lanes] = pltpu.roll(flat, 7, 1).reshape(shape)

    @pl.when(clip > 0)
    def _():
        finish_rows(clip - 1)

    pump(1)
    tap_grads(shifted, grads.at[1], taps_out)
    conv = shifted.at[1, 1 : FRAMES + 1, 1 : SIDE + 1]
    convolve(grads, taps, conv, True)
    for member in range(3):
        lanes = slice(member * heads * LANES, (member + 1) * heads * LANES)
        block = shifted[1, 1 : FRAMES + 1, 1 : SIDE + 1, :, lanes].reshape(GRID_ROWS, -1)
        rows = dot_f32(outof_ref[frame], block.astype(BF), ((1,), (0,))).astype(BF)
        pooled[:, lanes] = rows
        joined_out[:, lanes] += jnp.sum(rows.astype(F32), axis=0, keepdims=True)
    weight_sum[...] += dot_f32(normed_ref[0], pooled[...], ((0,), (0,)))
    result = dot_f32(pooled[...], weight_ref[...], ((1,), (1,))).astype(BF)
    cut = result.shape[1] // 2

    @pl.when(head_at == 0)
    def _():
        keep[clip] = result[:, :cut]
        cross_send[clip] = result[:, cut:]

    @pl.when(head_at == 1)
    def _():
        keep[clip] = result[:, cut:]
        cross_send[clip] = result[:, :cut]

    cross_copy(clip).start()

    @pl.when(clip == clips - 1)
    def _():
        weight_out[...] = weight_sum[...].astype(BF)
        finish_rows(clip)
        settle(chunks - 1)
        for chunk in range(early):
            each(1, outers, lambda step: far_copy(chunk, step).wait_recv())
            rest_out[:, chunk * cols : (chunk + 1) * cols] = lax.fori_loop(
                1,
                outers,
                lambda step, sums: sums + rest_far[chunk, step].astype(F32),
                rest_sum[chunk, outer].astype(F32),
            )
        for index in range(clips):
            grad_copy(index).wait_send()
            cross_copy(index).wait_send()
            mem_copy(index).wait()
            row_copy(index).wait()
        for chunk in range(chunks):
            over_copy(chunk).wait_send()
            rest_copy(chunk).wait_send()
        for chunk in range(early):
            each(1, outers, lambda step: far_copy(chunk, step).wait_send())


def whole_spec(shape):
    return pl.BlockSpec(shape, lambda clip: (0,) * len(shape))


def clip_spec(shape):
    return pl.BlockSpec((1,) + shape, lambda clip: (clip,) + (0,) * len(shape))


def once_spec(shape):
    return pl.BlockSpec(
        shape, lambda clip: (0,) * len(shape), pipeline_mode=pl.Buffered(1)
    )


def any_spec():
    return pl.BlockSpec(memory_space=pl.ANY)


def attention_forward(
    packed, mem_own, mem_peer, column, consts, kernels, gains, shifts, bias, scale, unit, rows
):
    clips = packed.shape[0]
    heads = packed.shape[2] // (3 * LANES)
    into, outof, keyhot, mask, pad_row = consts
    wide = 3 * heads * LANES
    mem_shape = mem_own.shape[1:]
    outers = column.shape[0]
    dma = pltpu.SemaphoreType.DMA
    out = jax.ShapeDtypeStruct
    return pl.pallas_call(
        partial(forward_kernel, heads=heads, unit=unit, scale=scale),
        grid=(clips,),
        in_specs=[
            clip_spec((QROWS, wide)),
            clip_spec(mem_shape),
            clip_spec(mem_shape),
            once_spec(column.shape),
            once_spec(into.shape),
            once_spec(outof.shape),
            once_spec(kernels.shape),
            once_spec(gains.shape),
            once_spec(shifts.shape),
            clip_spec((BIAS_COLS, LANES)),
            once_spec((BIAS_COLS, KROWS)),
            once_spec((QROWS, BIAS_COLS)),
            once_spec((1, BIAS_COLS)),
        ],
        out_specs=[
            clip_spec((rows, heads * unit)),
            any_spec(),
            any_spec(),
            clip_spec((QROWS, heads * LANES)),
            clip_spec((KROWS, heads * LANES)),
            clip_spec((KROWS, heads * LANES)),
            clip_spec((heads, QROWS, KROWS)),
            clip_spec((FRAMES, SIDE, 8, wide)),
        ],
        scratch_shapes=[
            pltpu.VMEM((3, FRAMES + 2, SIDE + 2, 8, wide), F32),
            pltpu.VMEM((27, 8, wide), F32),
            pltpu.VMEM((1, wide), F32),
            pltpu.VMEM((1, wide), F32),
            pltpu.VMEM((clips, rows, heads * unit), BF),
            dma((2, clips)),
            dma((2, outers)),
            dma((2, outers)),
            dma((2, outers)),
            pltpu.SemaphoreType.DMA,
        ],
        out_shape=[
            out((clips, rows, heads * unit), BF),
            out((clips, rows, heads * unit), BF),
            out((outers, 4) + column.shape[1:], BF),
            out((clips, QROWS, heads * LANES), BF),
            out((clips, KROWS, heads * LANES), BF),
            out((clips, KROWS, heads * LANES), BF),
            out((clips, heads, QROWS, KROWS), BF),
            out((clips, FRAMES, SIDE, 8, wide), F32),
        ],
        compiler_params=pltpu.CompilerParams(
            collective_id=1, has_side_effects=True, vmem_limit_bytes=VMEM_LIMIT
        ),
        name="pooled_attention_forward",
    )(
        packed, mem_own, mem_peer, column, into, outof, kernels, gains, shifts, bias, keyhot, mask,
        pad_row,
    )


def attention_backward(
    packed, normed, weight, grad_own, grad_send, rest, consts, kernels, gains, bias, saved, scale,
    unit,
):
    clips, rows, width = grad_own.shape
    heads = width // unit
    model = weight.shape[0]
    half = model // 2
    into, outof, keyhot, mask, pad_row = consts
    wide = 3 * heads * LANES
    outers, _, shard_rows, rest_width = rest.shape
    chunks = 9
    early = 8
    cols = rest_width // chunks
    out = jax.ShapeDtypeStruct
    dma = pltpu.SemaphoreType.DMA
    return pl.pallas_call(
        partial(backward_kernel, heads=heads, unit=unit, scale=scale),
        grid=(clips,),
        in_specs=[
            clip_spec((QROWS, wide)),
            clip_spec((QROWS, model)),
            once_spec((model, wide)),
            clip_spec((rows, width)),
            any_spec(),
            any_spec(),
            once_spec(into.shape),
            once_spec(outof.shape),
            once_spec(kernels.shape),
            once_spec(gains.shape),
            clip_spec((BIAS_COLS, LANES)),
            once_spec((BIAS_COLS, KROWS)),
            once_spec((QROWS, BIAS_COLS)),
            clip_spec((QROWS, heads * LANES)),
            clip_spec((KROWS, heads * LANES)),
            clip_spec((KROWS, heads * LANES)),
            clip_spec((heads, QROWS, KROWS)),
            clip_spec((FRAMES, SIDE, 8, wide)),
        ],
        out_specs=[
            whole_spec((clips, rows, half)),
            any_spec(),
            clip_spec((MEM_BACK, 2 * heads * LANES)),
            any_spec(),
            whole_spec((27, 8, wide)),
            whole_spec((1, wide)),
            whole_spec((1, wide)),
            clip_spec((BIAS_COLS, LANES)),
            whole_spec((model, wide)),
            whole_spec((1, wide)),
            whole_spec((outers, shard_rows, cols)),
            whole_spec((shard_rows, early * cols)),
        ],
        scratch_shapes=[
            pltpu.VMEM((3, FRAMES + 2, SIDE + 2, 8, wide), F32),
            pltpu.VMEM((27, 8, wide), F32),
            pltpu.VMEM((1, wide), F32),
            pltpu.VMEM((3, FRAMES + 2, SIDE + 2, 8, wide), F32),
            pltpu.VMEM((QROWS, heads * LANES), BF),
            pltpu.VMEM((QROWS, wide), BF),
            pltpu.VMEM((clips, rows, width), BF),
            pltpu.VMEM((clips, MEM_BACK, 2 * heads * LANES), BF),
            pltpu.VMEM((chunks, outers, 2, shard_rows, cols), BF),
            pltpu.VMEM((chunks, outers, 2, shard_rows, cols), BF),
            pltpu.VMEM((chunks, outers, shard_rows, cols), BF),
            pltpu.VMEM((chunks, outers, shard_rows, cols), BF),
            pltpu.VMEM((chunks, outers, shard_rows, cols), BF),
            pltpu.VMEM((early, outers, shard_rows, cols), BF),
            pltpu.VMEM((model, wide), F32),
            pltpu.VMEM((clips, QROWS, half), BF),
            pltpu.VMEM((clips, QROWS, half), BF),
            pltpu.VMEM((clips, QROWS, half), BF),
            pltpu.VMEM((clips, rows, half), BF),
            dma((2, clips)),
            dma((2, clips)),
            dma((chunks,)),
            dma((2, chunks)),
            dma((2, chunks)),
            dma((2, early, outers)),
            dma((2, clips)),
            dma((2, clips)),
        ],
        out_shape=[
            out((clips, rows, half), BF),
            out((clips, rows, half), BF),
            out((clips, MEM_BACK, 2 * heads * LANES), BF),
            out((clips, MEM_BACK, 2 * heads * LANES), BF),
            out((27, 8, wide), F32),
            out((1, wide), F32),
            out((1, wide), F32),
            out((clips, BIAS_COLS, LANES), F32),
            out((model, wide), BF),
            out((1, wide), F32),
            out((outers, shard_rows, cols), BF),
            out((shard_rows, early * cols), F32),
        ],
        compiler_params=pltpu.CompilerParams(
            collective_id=2, has_side_effects=True, vmem_limit_bytes=VMEM_LIMIT
        ),
        name="pooled_attention_backward",
    )(
        packed, normed, weight, grad_own, grad_send, rest, into, outof, kernels, gains, bias, keyhot,
        mask, *saved,
    )


def row_stats(values):
    width = values.shape[-1]
    centred = values - jnp.sum(values, axis=-1, keepdims=True) * (1.0 / width)
    variance = jnp.sum(centred * centred, axis=-1, keepdims=True) * (1.0 / width)
    return centred, lax.rsqrt(variance + 1e-06)


def each(low, high, act):
    def body(step, carry):
        act(step)
        return carry

    lax.fori_loop(low, high, body, 0)


def norm_rows(source, index, gain, shift, target, at):
    rows = source.shape[1]
    centred, rate = row_stats(source[index].astype(F32))
    target[index, at : at + rows] = (centred * rate * gain[0:1] + shift[0:1]).astype(BF)


def project_rows(normed, weight, bias, packed):
    def step(index):
        packed[index] = (dot_f32(normed[index], weight, ((1,), (0,))) + bias[...]).astype(BF)

    each(0, packed.shape[0], step)


def project_moves(
    x, attn, gain, shift, attn_shift, cached, old, squeeze, proj, up, down, full, normed, mem_own,
    mem_peer, rest_column, shards, bias, rest, mem_send, squeeze_rows, x_peer, columns, far_sems,
    near_sems, x_sems, cross_sems, mem_sems, rest_sems,
):
    outers = full.shape[0]
    clips, rows, model = x.shape
    clip = lax.axis_index("clip")
    frame = lax.axis_index("frame")
    head = lax.axis_index("head")
    outer, inner = clip // 2, clip % 2
    place = inner * 2 + frame
    half = model // 2
    lanes = pl.ds(pl.multiple_of(head * half, LANES), half)
    barrier = pltpu.get_barrier_semaphore()

    def far_device(step):
        return device_of((outer + step) % outers, inner, frame, head)

    def near_device(step):
        there_inner, there_frame = plane_peer(inner, frame, step)
        return device_of(outer, there_inner, there_frame, head)

    def greet(device):
        pl.semaphore_signal(barrier, inc=1, device_id=device, device_id_type=MESH_ID)

    group = mem_own.shape[2] // 2
    heads = shards.shape[2] // (3 * LANES)
    unit = group // heads

    def squeeze_clip(index):
        total = jnp.zeros((CELLS, cached.shape[2]), F32)
        for step in range(squeeze_rows.shape[0]):
            rows_here = cached[index, step * CELLS : (step + 1) * CELLS].astype(F32)
            total = total + rows_here * squeeze_rows[step : step + 1]
        pieces = ((0, total.astype(BF)), (MEM_STEP, old[index]))
        for side in range(2):

            @pl.when(frame == side)
            def _():
                for at, value in pieces:
                    for member in range(2):
                        local = slice(member * group, (member + 1) * group)
                        low = (2 * member + side) * group
                        mem_own[index, at : at + CELLS, local] = value[:, low : low + group]
                        low = (2 * member + 1 - side) * group
                        mem_send[index, at : at + CELLS, local] = value[:, low : low + group]

    def far_copy(step, at):
        return pltpu.make_async_remote_copy(
            src_ref=shards, dst_ref=columns.at[at],
            send_sem=far_sems.at[0, step], recv_sem=far_sems.at[1, step],
            device_id=far_device(step), device_id_type=MESH_ID,
        )

    def near_copy(index, step, source, at):
        return pltpu.make_async_remote_copy(
            src_ref=source.at[(frame + step % 2) % 2], dst_ref=full.at[at, place],
            send_sem=near_sems.at[0, index, step - 1], recv_sem=near_sems.at[1, index, step - 1],
            device_id=near_device(step), device_id_type=MESH_ID,
        )

    def turn_copy(index):
        block = full.at[origin(index), inner * 2 + 1 - frame]
        return side_copy(block, block, near_sems.at[0, index, 2], near_sems.at[1, index, 2])

    def near_arrival(index, step, at):
        there_inner, there_frame = plane_peer(inner, frame, step)
        return pltpu.make_async_remote_copy(
            src_ref=shards.at[0], dst_ref=full.at[at, there_inner * 2 + there_frame],
            send_sem=near_sems.at[0, index, step - 1], recv_sem=near_sems.at[1, index, step - 1],
            device_id=near_device(step), device_id_type=MESH_ID,
        )

    def x_copy(index):
        return partner_copy(
            x.at[index, :, lanes], x_peer.at[index, :, lanes], x_sems.at[0, index],
            x_sems.at[1, index],
        )

    def cross_copy(index):
        return pltpu.make_async_remote_copy(
            src_ref=x_peer.at[index, :, lanes], dst_ref=x_peer.at[index, :, lanes],
            send_sem=cross_sems.at[0, index], recv_sem=cross_sems.at[1, index],
            device_id=(clip, frame, 1 - head), device_id_type=MESH_ID,
        )

    def cross_arrival(index):
        other = pl.ds(pl.multiple_of((1 - head) * half, LANES), half)
        return pltpu.make_async_remote_copy(
            src_ref=x_peer.at[index, :, other], dst_ref=x_peer.at[index, :, other],
            send_sem=cross_sems.at[0, index], recv_sem=cross_sems.at[1, index],
            device_id=(clip, frame, 1 - head), device_id_type=MESH_ID,
        )

    mem_copy = partner_copy(mem_send, mem_peer, mem_sems.at[0], mem_sems.at[1])

    def rest_copy(step, at):
        return pltpu.make_async_remote_copy(
            src_ref=rest, dst_ref=rest_column.at[at],
            send_sem=rest_sems.at[0, step], recv_sem=rest_sems.at[1, step],
            device_id=far_device(step), device_id_type=MESH_ID,
        )

    def origin(step):
        return (outer + outers - step) % outers

    def prologue():
        each(1, outers, lambda step: greet(far_device(step)))
        for step in range(1, 4):
            greet(near_device(step))
        greet((clip, frame, 1 - head))
        shards[...] = jnp.zeros_like(shards)
        bias[...] = jnp.zeros_like(bias)
        for member in range(3):
            for side in range(2):
                for index in range(heads):
                    target = (member * heads + index) * LANES
                    source = slice(side * group + index * unit, side * group + (index + 1) * unit)
                    shards[side, :, target : target + unit] = attn[member, :, source]
        at = 0
        for part in (proj, up, down):
            rest[:, at : at + part.shape[1]] = part[...]
            at += part.shape[1]
        for side in range(2):

            @pl.when(frame == side)
            def _():
                for member in range(3):
                    for index in range(heads):
                        target = (member * heads + index) * LANES
                        source = slice(side * group + index * unit, side * group + (index + 1) * unit)
                        bias[:, target : target + unit] = attn_shift[member : member + 1, source]

        for member in range(2):
            for index in range(2 * heads):
                at = (2 * member * heads + index) * unit
                squeeze_rows[:, at : at + unit] = squeeze[member]
        mem_own[...] = jnp.zeros_like(mem_own)
        mem_send[...] = jnp.zeros_like(mem_send)

        pl.semaphore_wait(barrier, outers - 1 + 4)
        each(1, outers, lambda step: far_copy(step, outer).start())
        for step in range(1, 3):
            near_copy(0, step, shards, outer).start()
        each(0, clips, lambda index: x_copy(index).start())
        each(0, clips, squeeze_clip)
        rest_column[outer] = rest[...]
        full[outer, place] = shards[frame]
        normed[...] = jnp.zeros_like(normed)
        each(0, clips, lambda index: norm_rows(x, index, gain, shift, normed, 0))

        def forward(index):
            at = origin(index)
            far_copy(index, at).wait_recv()
            for step in range(1, 3):
                near_copy(index, step, columns.at[at], at).start()
            full[at, place] = columns[at, frame]

        each(1, outers, forward)
        each(1, outers, lambda step: rest_copy(step, outer).start())

        def relay(index):
            x_copy(index).wait_recv()
            cross_copy(index).start()

        each(0, clips, relay)
        mem_copy.start()

        def receive(index):
            cross_arrival(index).wait_recv()
            norm_rows(x_peer, index, gain, shift, normed, HALF)

        each(0, clips, receive)

        def pass_side(index):
            near_arrival(index, 1, origin(index)).wait_recv()
            turn_copy(index).start()

        def arrive(index):
            for step in range(2, 4):
                near_arrival(index, step, origin(index)).wait_recv()

        each(0, outers, pass_side)

        each(0, outers, arrive)
    def rest_arrive():
        each(1, outers, lambda step: rest_copy(step, origin(step)).wait_recv())

    def finish():
        each(1, outers, lambda step: rest_copy(step, outer).wait_send())
        each(1, outers, lambda step: far_copy(step, outer).wait_send())
        each(0, outers, lambda index: turn_copy(index).wait_send())
        for step in range(1, 3):
            near_copy(0, step, shards, outer).wait_send()

        def sent(index):
            for step in range(1, 3):
                near_copy(index, step, columns.at[origin(index)], origin(index)).wait_send()

        each(1, outers, sent)

        def x_sent(index):
            x_copy(index).wait_send()
            cross_copy(index).wait_send()

        each(0, clips, x_sent)

    return outer, prologue, mem_copy, rest_arrive, finish


def front_kernel(
    x, attn, gain, shift, attn_shift, cached, old, squeeze, proj, up, down, into_ref, outof_ref,
    kernel_ref, pool_gain_ref, pool_shift_ref, bias_ref, keyhot_ref, mask_ref, pad_ref,
    full_out, packed_out, normed_out, out_own, out_recv, rest_full, q_out, k_out, v_out, p_out,
    c_out, full, shards, attn_bias, rest, mem_send, mem_own, mem_peer, squeeze_rows, x_peer, columns, normed,
    rest_column, shifted, taps, gain_ref, shift_ref, out_send, far_sems, near_sems, x_sems,
    cross_sems, mem_sems, rest_sems, out_sems, side_sems, pair_sems, turn_sems, own_sem,
    *, heads, unit, scale,
):
    clip = pl.program_id(0)
    clips = out_send.shape[0]
    outers = full.shape[0]
    frame = lax.axis_index("frame")
    outer, prologue, mem_copy, rest_arrive, project_finish = project_moves(
        x, attn, gain, shift, attn_shift, cached, old, squeeze, proj, up, down, full, normed,
        mem_own, mem_peer, rest_column, shards, attn_bias, rest, mem_send, squeeze_rows, x_peer,
        columns, far_sems, near_sems, x_sems, cross_sems, mem_sems, rest_sems,
    )
    own_copy, send, turn, plane_finish = plane_stage(
        rest_column, rest_full, side_sems, pair_sems, turn_sems, own_sem
    )

    def out_copy(index):
        return partner_copy(
            out_send.at[index], out_recv.at[index], out_sems.at[0, index], out_sems.at[1, index]
        )

    @pl.when(clip == 0)
    def _():
        prologue()
        send(outer)
        shifted[...] = jnp.zeros_like(shifted)
        pairs = ((pool_gain_ref, gain_ref), (pool_shift_ref, shift_ref))
        spread_tables(kernel_ref, taps, pairs, heads, unit)

    def points(odd):
        for step in range(outers):
            point = min(step + TURN_LAG, 2 * clips - 1)
            if step and step % 2 == odd:

                @pl.when(clip == step // 2)
                def _():
                    send((outer + step) % outers)

            if point % 2 == odd:

                @pl.when(clip == point // 2)
                def _():
                    turn(step)

    def after_conv():
        @pl.when(clip == 0)
        def _():
            mem_copy.wait_recv()
            rest_arrive()
            own_copy.start()

        points(1)

    points(0)
    @pl.when(clip == clips - 1)
    def _():
        full_out[...] = full[...]

    normed_out[0] = normed[clip]
    weight = full[...].reshape(x.shape[2], full.shape[3])
    rows = dot_f32(normed[clip], weight, ((1,), (0,))) + attn_bias[...]
    packed_out[0] = rows.astype(BF)
    attend_clip(
        packed_out.at[0], mem_own.at[clip], mem_peer.at[clip], frame, into_ref, outof_ref, gain_ref,
        shift_ref, bias_ref, keyhot_ref, mask_ref, pad_ref, out_own.at[0], out_send.at[clip], q_out,
        k_out, v_out, p_out, c_out, shifted, taps, heads, unit, scale, after_conv,
    )
    out_copy(clip).start()

    @pl.when(clip == clips - 1)
    def _():
        mem_copy.wait_send()
        project_finish()
        plane_finish()
        for index in range(clips):
            out_copy(index).wait()


def front(
    x, attn, gain, shift, attn_shift, cached, old, squeeze, proj, up, down, consts, kernels, gains,
    shifts, bias, scale, clip_count, unit,
):
    clips, rows, model = x.shape
    _, shard_rows, head_width = attn.shape
    heads = head_width // (2 * unit)
    wide = 3 * heads * LANES
    outers = clip_count // 2
    into, outof, keyhot, mask, pad_row = consts
    rest_shape = (shard_rows, proj.shape[1] + up.shape[1] + down.shape[1])
    mem_shape = (clips, MEM_PAD, head_width)
    out = jax.ShapeDtypeStruct
    dma = pltpu.SemaphoreType.DMA
    operands = (
        x, attn, gain, shift, attn_shift, cached, old, squeeze, proj, up, down, into, outof,
        kernels, gains, shifts, bias, keyhot, mask, pad_row,
    )
    specs = [once_spec(value.shape) for value in operands]
    specs[16] = clip_spec((BIAS_COLS, LANES))
    results = pl.pallas_call(
        partial(front_kernel, heads=heads, unit=unit, scale=scale),
        grid=(clips,),
        in_specs=specs,
        out_specs=[
            whole_spec((outers, 4, shard_rows, wide)),
            clip_spec((QROWS, wide)),
            clip_spec((QROWS, model)),
            clip_spec((rows, heads * unit)),
            any_spec(),
            any_spec(),
            clip_spec((QROWS, heads * LANES)),
            clip_spec((KROWS, heads * LANES)),
            clip_spec((KROWS, heads * LANES)),
            clip_spec((heads, QROWS, KROWS)),
            clip_spec((FRAMES, SIDE, 8, wide)),
        ],
        out_shape=[
            out((outers, 4, shard_rows, wide), BF),
            out((clips, QROWS, wide), BF),
            out((clips, QROWS, model), BF),
            out((clips, rows, heads * unit), BF),
            out((clips, rows, heads * unit), BF),
            out((outers, 4) + rest_shape, BF),
            out((clips, QROWS, heads * LANES), BF),
            out((clips, KROWS, heads * LANES), BF),
            out((clips, KROWS, heads * LANES), BF),
            out((clips, heads, QROWS, KROWS), BF),
            out((clips, FRAMES, SIDE, 8, wide), F32),
        ],
        scratch_shapes=[
            pltpu.VMEM((outers, 4, shard_rows, wide), BF),
            pltpu.VMEM((2, shard_rows, wide), BF),
            pltpu.VMEM((1, wide), F32),
            pltpu.VMEM(rest_shape, BF),
            pltpu.VMEM(mem_shape, BF),
            pltpu.VMEM(mem_shape, BF),
            pltpu.VMEM(mem_shape, BF),
            pltpu.VMEM((squeeze.shape[1], cached.shape[2]), F32),
            pltpu.VMEM((clips, rows, model), BF),
            pltpu.VMEM((outers, 2, shard_rows, wide), BF),
            pltpu.VMEM((clips, QROWS, model), BF),
            pltpu.VMEM((outers,) + rest_shape, BF),
            pltpu.VMEM((3, FRAMES + 2, SIDE + 2, 8, wide), F32),
            pltpu.VMEM((27, 8, wide), F32),
            pltpu.VMEM((1, wide), F32),
            pltpu.VMEM((1, wide), F32),
            pltpu.VMEM((clips, rows, heads * unit), BF),
            dma((2, outers)),
            dma((2, outers, 3)),
            dma((2, clips)),
            dma((2, clips)),
            dma((2,)),
            dma((2, outers)),
            dma((2, clips)),
            dma((2, outers)),
            dma((2, outers)),
            dma((2, outers)),
            pltpu.SemaphoreType.DMA,
        ],
        compiler_params=pltpu.CompilerParams(
            collective_id=1, has_side_effects=True, vmem_limit_bytes=VMEM_LIMIT
        ),
        name="project_and_attend",
    )(*operands)
    return (results[0].reshape(model, wide),) + tuple(results[1:])


def project_local_kernel(x, x_peer, weight, gain, shift, bias, packed, normed):
    normed[...] = jnp.zeros_like(normed)
    each(0, x.shape[0], lambda index: norm_rows(x, index, gain, shift, normed, 0))
    each(0, x.shape[0], lambda index: norm_rows(x_peer, index, gain, shift, normed, HALF))
    project_rows(normed, weight[...], bias, packed)


def swap(value, axis):
    return lax.ppermute(value, axis, [(0, 1), (1, 0)])


def padded_heads(value, unit):
    value = value.reshape(value.shape[0], 3, 2, -1, unit)
    value = jnp.pad(value, ((0, 0),) * 4 + ((0, LANES - unit),))
    return value.transpose(2, 0, 1, 3, 4).reshape(2, value.shape[0], -1)


def project_plain(
    x, attn, gain, shift, attn_shift, cached, old, squeeze, proj, up, down, clip_count, unit
):
    clips, rows, model = x.shape
    _, shard_rows, head_width = attn.shape
    heads = head_width // (2 * unit)
    width = 3 * heads * LANES
    outers = clip_count // 2
    rest_shape = (shard_rows, proj.shape[1] + up.shape[1] + down.shape[1])
    out = jax.ShapeDtypeStruct
    dma = pltpu.SemaphoreType.DMA
    vmem = pl.BlockSpec(memory_space=pltpu.VMEM)
    shapes = [out((clips, QROWS, width), BF), out((clips, QROWS, model), BF)]
    frame = lax.axis_index("frame")
    shards = padded_heads(attn.transpose(1, 0, 2), unit)
    full = lax.all_gather(shards, ("clip", "frame"), axis=1, tiled=True)
    full = lax.dynamic_index_in_dim(full, frame, 0, keepdims=False)
    bias = padded_heads(attn_shift[None], unit)
    bias = lax.dynamic_index_in_dim(bias, frame, 0, keepdims=False)
    steps = squeeze.shape[1]
    wide = cached.astype(F32).reshape(clips, steps, CELLS, 2, head_width)
    tiled = jnp.tile(squeeze, (1, 1, 2 * heads))
    mem = sum(wide[:, step] * tiled[:, step] for step in range(steps)).astype(BF)
    mem = jnp.stack([mem, old.reshape(mem.shape)], axis=1)
    mem = jnp.pad(mem, ((0, 0), (0, 0), (0, MEM_STEP - CELLS), (0, 0), (0, 0)))
    pieces = mem.reshape(clips, 2 * MEM_STEP, 2, 2, heads * unit)
    mem_own = lax.dynamic_index_in_dim(pieces, frame, 3, keepdims=False)
    mem_send = lax.dynamic_index_in_dim(pieces, 1 - frame, 3, keepdims=False)
    mem_own = mem_own.reshape(clips, -1, head_width)
    mem_peer = swap(mem_send.reshape(clips, -1, head_width), "frame")
    packed, normed = pl.pallas_call(
        project_local_kernel,
        in_specs=[vmem] * 6,
        out_specs=[vmem] * 2,
        out_shape=shapes,
        compiler_params=pltpu.CompilerParams(vmem_limit_bytes=VMEM_LIMIT),
        name="project_local",
    )(x, swap(x, "frame"), full, gain, shift, bias)
    rest = jnp.concatenate([proj, up, down], axis=1)
    column = lax.all_gather(rest, ("clip", "frame"), axis=0, tiled=False)
    column = column.reshape((outers, 4) + rest.shape)
    place = lax.axis_index("clip") % 2 * 2 + frame
    column = lax.dynamic_index_in_dim(column, place, 1, keepdims=False)
    return full, packed, normed, mem_own, mem_peer, column


def device_of(outer, inner, frame, head):
    return (outer * 2 + inner, frame, head)


def plane_peer(inner, frame, step):
    return (inner + step // 2) % 2, (frame + step % 2) % 2


def row_piece(value, row):
    return value[:, row * LANES : (row + 1) * LANES]


def tail_kernel(
    row_own, row_recv, x, middle_grad, grads, joined_sum, gain, taps, pool_gain, pool_shift,
    bias_grad, hot, space_hot, cached, mem_own, mem_recv, vectors, up_bias, rest,
    grad_in, out, rest_out, small_out,
    near, part, far, small, pair_in, plane_in, line_in, row_full, rest_in,
    cross_sems, near_sems, far_sems, pair_sems, plane_sems, line_sems, rest_sems,
    *, unit, plan, table_rows,
):
    chunks, outers, _, shard_rows, cols = part.shape
    clips, rows, model = x.shape
    half = model // 2
    clip = lax.axis_index("clip")
    frame = lax.axis_index("frame")
    head = lax.axis_index("head")
    outer, inner = clip // 2, clip % 2
    place = inner * 2 + frame
    barrier = pltpu.get_barrier_semaphore()
    partner = (clip, frame, 1 - head)

    def line_device(step):
        return device_of((outer + step) % outers, inner, frame, head)

    def plane_device(step):
        there_inner, there_frame = plane_peer(inner, frame, step)
        return device_of(outer, there_inner, there_frame, head)

    def plane_place(step):
        there_inner, there_frame = plane_peer(inner, frame, step)
        return there_inner * 2 + there_frame

    def greet(device):
        pl.semaphore_signal(barrier, inc=1, device_id=device, device_id_type=MESH_ID)

    each(1, outers, lambda step: greet(line_device(step)))
    for step in range(1, 4):
        greet(plane_device(step))
    greet(partner)

    def move(source, target, sems, device):
        return pltpu.make_async_remote_copy(
            src_ref=source, dst_ref=target, send_sem=sems[0], recv_sem=sems[1],
            device_id=device, device_id_type=MESH_ID,
        )

    def pair_sum():
        return move(
            small.at[1 - head], pair_in, (pair_sems.at[0, 0], pair_sems.at[1, 0]), partner
        )

    def plane_sum(step):
        sems = (plane_sems.at[0, 0, step - 1], plane_sems.at[1, 0, step - 1])
        source = small.at[head, plane_place(step)]
        return move(source, plane_in.at[step - 1], sems, plane_device(step))

    def line_sum(step):
        sems = (line_sems.at[0, 0, step], line_sems.at[1, 0, step])
        source = small.at[head, place, (outer + step) % outers]
        return move(source, line_in.at[step], sems, line_device(step))

    def line_share(step, at):
        sems = (line_sems.at[0, 1, step], line_sems.at[1, 1, step])
        block = small_out.at[head, place, at]
        return move(block, block, sems, line_device(step))

    def plane_share(step, at):
        sems = (plane_sems.at[0, 1, step - 1], plane_sems.at[1, 1, step - 1])
        block = small_out.at[head, at]
        return move(block, block, sems, plane_device(step))

    def pair_share(at):
        block = small_out.at[at]
        return move(block, block, (pair_sems.at[0, 1], pair_sems.at[1, 1]), partner)

    def near_copy(chunk, step):
        there_inner, there_frame = plane_peer(inner, frame, step)
        return pltpu.make_async_remote_copy(
            src_ref=grads.at[:, there_inner * 2 + there_frame, :, pl.ds(chunk * cols, cols)],
            dst_ref=near.at[chunk, step - 1],
            send_sem=near_sems.at[0, chunk, step - 1], recv_sem=near_sems.at[1, chunk, step - 1],
            device_id=device_of(outer, there_inner, there_frame, head), device_id_type=MESH_ID,
        )

    def far_copy(chunk, step):
        there = (outer + step) % outers
        return pltpu.make_async_remote_copy(
            src_ref=part.at[chunk, there], dst_ref=far.at[chunk, step],
            send_sem=far_sems.at[0, chunk, step], recv_sem=far_sems.at[1, chunk, step],
            device_id=device_of(there, inner, frame, head), device_id_type=MESH_ID,
        )

    def cross_copy(index, side):
        lanes = pl.ds(pl.multiple_of(side * half, LANES), half)
        return pltpu.make_async_remote_copy(
            src_ref=row_full.at[index, :, lanes], dst_ref=row_full.at[index, :, lanes],
            send_sem=cross_sems.at[0, index], recv_sem=cross_sems.at[1, index],
            device_id=(clip, frame, 1 - head), device_id_type=MESH_ID,
        )

    def rest_copy(step):
        there = (outer + step) % outers
        return pltpu.make_async_remote_copy(
            src_ref=rest.at[there], dst_ref=rest_in.at[step],
            send_sem=rest_sems.at[0, step], recv_sem=rest_sems.at[1, step],
            device_id=device_of(there, inner, frame, head), device_id_type=MESH_ID,
        )

    small[...] = jnp.zeros_like(small)
    pl.semaphore_wait(barrier, outers - 1 + 4)
    for chunk in range(chunks):
        for step in range(1, 4):
            near_copy(chunk, step).start()
    lanes_here = pl.ds(pl.multiple_of(head * half, LANES), half)

    def join(index):
        total = row_own[index].astype(F32) + row_recv[index].astype(F32)
        row_full[index, :, lanes_here] = total.astype(BF)
        cross_copy(index, head).start()

    each(0, clips, join)
    each(1, outers, lambda step: rest_copy(step).start())

    rows_small = small.shape[3]

    def put(row, value):
        count = value.shape[0]
        done = 0
        while done < count:
            block, offset = divmod(row + done, rows_small)
            size = min(count - done, rows_small - offset)
            at = (block // (4 * outers), block // outers % 4, block % outers)
            small[at[0], at[1], at[2], offset : offset + size, : value.shape[1]] = value[
                done : done + size
            ]
            done += size

    def put_wide(row, value):
        for index in range(value.shape[1] // LANES):
            put(row + index, row_piece(value, index))

    wide_rows_count = model // LANES

    joined_rows = joined_sum.shape[1] // LANES
    up_rows = up_bias.shape[1] // LANES
    for which in range(2):

        @pl.when(head == which)
        def _():
            for side in range(2):

                @pl.when(frame == side)
                def _():
                    put_wide(plan["joined"] + (2 * which + side) * joined_rows, joined_sum[...])

            put_wide(plan["up"] + which * up_rows, up_bias[...])

    heads = taps.shape[2] // (3 * LANES)
    tap_sum = jnp.sum(taps[...], axis=1)
    for member in range(3):
        totals = []
        for value in (tap_sum, pool_gain[...], pool_shift[...]):
            total = row_piece(value, member * heads)
            for index in range(1, heads):
                total = total + row_piece(value, member * heads + index)
            totals.append(total)
        put(plan["taps"] + member * 27, totals[0])
        put(plan["pool_gain"] + member, totals[1])
        put(plan["pool_shift"] + member, totals[2])
    heads_here = joined_sum.shape[1] // (3 * LANES)
    for side in range(2):

        @pl.when(frame == side)
        def _():
            for member in range(2):
                totals = [jnp.zeros((1, unit), F32) for _ in range(FRAMES // MEMF)]
                for index in range(clips):
                    for which, part in ((side, mem_own), (1 - side, mem_recv)):
                        for spot in range(heads_here):
                            at = (member * heads_here + spot) * LANES
                            value = part[index, :CELLS, at : at + unit].astype(F32)
                            at = ((2 * member + which) * heads_here + spot) * unit
                            for step in range(len(totals)):
                                rows_here = cached[
                                    index, step * CELLS : (step + 1) * CELLS, at : at + unit
                                ]
                                product = rows_here.astype(F32) * value
                                totals[step] = totals[step] + jnp.sum(
                                    product, axis=0, keepdims=True
                                )
                for step in range(len(totals)):
                    put(plan["squeeze"] + member * len(totals) + step, totals[step])

    time_sum = jnp.zeros((hot.shape[2], LANES), F32)
    bias_sum = jnp.zeros((BIAS_COLS, LANES), F32)
    for index in range(clips):
        value = bias_grad[index]
        bias_sum = bias_sum + value
        value = value[: hot.shape[1]]
        high = value.astype(BF)
        low = (value - high.astype(F32)).astype(BF)
        time_sum = time_sum + dot_f32(hot[index], high, ((0,), (0,)))
        time_sum = time_sum + dot_f32(hot[index], low, ((0,), (0,)))
    put(plan["time"], time_sum[:table_rows])
    high = bias_sum.astype(BF)
    low = (bias_sum - high.astype(F32)).astype(BF)
    space_sum = dot_f32(space_hot[...], high, ((1,), (0,)))
    space_sum = space_sum + dot_f32(space_hot[...], low, ((1,), (0,)))
    put(plan["space"], space_sum[: 2 * (2 * SIDE - 1)])

    gain_sum = jnp.zeros((1, model), F32)
    shift_sum = jnp.zeros((1, model), F32)
    for index in range(clips):
        cross_copy(index, 1 - head).wait_recv()
        incoming = row_full[index].astype(F32)
        centred, rate = row_stats(x[index].astype(F32))
        normal = centred * rate
        product = incoming * normal
        gain_sum = gain_sum + jnp.sum(product, axis=0, keepdims=True)
        shift_sum = shift_sum + jnp.sum(incoming, axis=0, keepdims=True)
        scaled = incoming * gain[0:1]
        mean_scaled = jnp.sum(scaled, axis=-1, keepdims=True) * (1.0 / model)
        mean_both = jnp.sum(scaled * normal, axis=-1, keepdims=True) * (1.0 / model)
        result = rate * (scaled - mean_scaled - normal * mean_both) + middle_grad[index]
        grad_in[index] = result.astype(BF)

    @pl.when(head == 0)
    def _():
        put_wide(plan["gain"], gain_sum)
        put_wide(plan["gain"] + wide_rows_count, vectors[0:1])
        put_wide(plan["shift"], shift_sum)
        put_wide(plan["shift"] + wide_rows_count, vectors[1:2])
        put_wide(plan["rows"], vectors[2:3])
        put_wide(plan["rows"] + wide_rows_count, vectors[3:4])

    def reduce_near(chunk):
        lanes = slice(chunk * cols, (chunk + 1) * cols)
        for step in range(1, 4):
            near_copy(chunk, step).wait_recv()

        def gathered(index):
            own = grads[index, place, :, lanes].astype(F32)
            own = own + near[chunk, 1, index].astype(F32)
            other = near[chunk, 0, index].astype(F32) + near[chunk, 2, index].astype(F32)
            return own, other

        def send(step):
            there = (outer + step) % outers
            own, other = gathered(there)
            part[chunk, there, 0] = own.astype(BF)
            part[chunk, there, 1] = other.astype(BF)
            far_copy(chunk, step).start()

        each(1, outers, send)
        own, other = gathered(outer)
        far[chunk, 0, 0] = own.astype(BF)
        far[chunk, 0, 1] = other.astype(BF)

    pair_sum().start()
    reduce_near(0)
    pair_sum().wait_recv()
    small[head] = small[head] + pair_in[...]
    for step in range(1, 4):
        plane_sum(step).start()
    for chunk in range(1, chunks):
        reduce_near(chunk)
    for step in range(1, 4):
        plane_sum(step).wait_recv()
    small[head, place] = small[head, place] + plane_in[0] + plane_in[1] + plane_in[2]
    each(1, outers, lambda step: line_sum(step).start())
    each(1, outers, lambda step: rest_copy(step).wait_recv())
    rest_out[...] = lax.fori_loop(
        1,
        outers,
        lambda step, sums: sums + rest_in[step].astype(F32),
        rest[outer].astype(F32),
    )
    each(1, outers, lambda step: line_sum(step).wait_recv())
    small_out[head, place, outer] = lax.fori_loop(
        1, outers, lambda step, sums: sums + line_in[step], small[head, place, outer]
    )
    each(1, outers, lambda step: line_share(step, outer).start())
    each(1, outers, lambda step: line_share(step, (outer + outers - step) % outers).wait_recv())
    for step in range(1, 4):
        plane_share(step, place).start()
    heads = cols // LANES
    group = heads * unit
    for chunk in range(chunks):
        each(1, outers, lambda step: far_copy(chunk, step).wait_recv())
        totals = []
        for side in range(2):
            totals.append(
                lax.fori_loop(
                    0,
                    outers,
                    lambda step, sums: sums + far[chunk, step, side].astype(F32),
                    jnp.zeros((shard_rows, cols), F32),
                )
            )

        def store(order):
            for spot, side in enumerate(order):
                for index in range(heads):
                    at = (2 * chunk + spot) * group + index * unit
                    value = totals[side][:, index * LANES : index * LANES + unit]
                    out[:, at : at + unit] = value

        @pl.when(frame == 0)
        def _():
            store((0, 1))

        @pl.when(frame == 1)
        def _():
            store((1, 0))

    for step in range(1, 4):
        plane_share(step, plane_place(step)).wait_recv()
    pair_share(head).start()
    pair_share(1 - head).wait_recv()
    pair_sum().wait_send()
    pair_share(head).wait_send()
    for step in range(1, 4):
        plane_sum(step).wait_send()
        plane_share(step, place).wait_send()
    each(1, outers, lambda step: line_sum(step).wait_send())
    each(1, outers, lambda step: line_share(step, outer).wait_send())
    each(1, outers, lambda step: rest_copy(step).wait_send())
    for index in range(clips):
        cross_copy(index, head).wait_send()
    for chunk in range(chunks):
        for step in range(1, 4):
            near_copy(chunk, step).wait_send()
        each(1, outers, lambda step: far_copy(chunk, step).wait_send())


def unpack_kernel(
    small, qkv, early, late, grad_in, block_out,
    grad_in_out, block_out_out, gain_out, shift_out, rows_out, joined_out, up_out, taps_out,
    pool_gain_out, pool_shift_out, squeeze_out, time_out, space_out, qkv_out, proj_out,
    up_grad_out, down_out, time_rows, *, plan, unit,
):
    for index in range(grad_in.shape[0]):
        grad_in_out[index] = grad_in[index]
        block_out_out[index] = block_out[index]
    head = lax.axis_index("head")
    rows_small = small.shape[1]

    def take(row, target):
        count = target.shape[0]
        done = 0
        while done < count:
            block, offset = divmod(row + done, rows_small)
            size = min(count - done, rows_small - offset)
            target[done : done + size] = small[block, offset : offset + size, : target.shape[1]]
            done += size

    def take_wide(row, target, at):
        for index in range(target.shape[1] // LANES):
            block, offset = divmod(row + index, rows_small)
            target[at : at + 1, index * LANES : (index + 1) * LANES] = small[
                block, offset : offset + 1
            ]

    per_row = gain_out.shape[1] // LANES
    for index in range(2):
        take_wide(plan["gain"] + index * per_row, gain_out, index)
        take_wide(plan["shift"] + index * per_row, shift_out, index)
        take_wide(plan["rows"] + index * per_row, rows_out, index)
    width = joined_out.shape[1]
    group = width // 2
    heads = group // unit
    joined_rows = 3 * heads
    up_rows = up_out.shape[0]
    for which in range(2):

        @pl.when(head == which)
        def _():
            for member in range(3):
                for side in range(2):
                    for index in range(heads):
                        row = plan["joined"] + (2 * which + side) * joined_rows
                        block, offset = divmod(row + member * heads + index, rows_small)
                        at = side * group + index * unit
                        joined_out[member : member + 1, at : at + unit] = small[
                            block, offset : offset + 1, :unit
                        ]
            take(plan["up"] + which * up_rows, up_out)

    for member in range(3):
        take(plan["taps"] + member * 27, taps_out.at[member])
        qkv_out[member] = qkv[:, member * width : (member + 1) * width]
    take(plan["pool_gain"], pool_gain_out)
    take(plan["pool_shift"], pool_shift_out)
    take(plan["time"], time_rows)
    time_out[...] = time_rows[...].T
    for index in range(2):
        count = squeeze_out.shape[1]
        take(plan["squeeze"] + index * count, squeeze_out.at[index])
        for spot in range(space_out.shape[0]):
            block, offset = divmod(
                plan["space"] + index * space_out.shape[0] + spot, rows_small
            )
            space_out[spot, index : index + 1] = small[block, offset : offset + 1, :unit]
    proj_width, up_width = proj_out.shape[1], up_grad_out.shape[1]
    proj_out[...] = early[:, :proj_width]
    up_grad_out[...] = early[:, proj_width : proj_width + up_width]
    at = proj_width + up_width
    first = early.shape[1] - at
    down_out[:, :first] = early[:, at:]
    down_out[:, first:] = late[...]


def unpack(small, qkv, early, late, grad_in, block_out, plan, unit, hidden_width, table_rows):
    shard_rows, width = qkv.shape
    model = grad_in.shape[2]
    rest_width = early.shape[1] + late.shape[1]
    out = jax.ShapeDtypeStruct
    vmem = pl.BlockSpec(memory_space=pltpu.VMEM)
    shapes = [
        out(grad_in.shape, BF),
        out(block_out.shape, BF),
        out((2, model), F32),
        out((2, model), F32),
        out((2, model), F32),
        out((3, width // 3), F32),
        out((hidden_width // LANES, LANES), F32),
        out((3, 27, unit), F32),
        out((3, unit), F32),
        out((3, unit), F32),
        out((2, FRAMES // MEMF, unit), F32),
        out((unit, table_rows), F32),
        out((2 * SIDE - 1, 2, unit), F32),
        out((3, shard_rows, width // 3), F32),
        out((shard_rows, rest_width - 2 * hidden_width), F32),
        out((shard_rows, hidden_width), F32),
        out((shard_rows, hidden_width), F32),
    ]
    return pl.pallas_call(
        partial(unpack_kernel, plan=plan, unit=unit),
        in_specs=[vmem] * 6,
        out_specs=[vmem] * len(shapes),
        out_shape=shapes,
        scratch_shapes=[pltpu.VMEM((table_rows, unit), F32)],
        compiler_params=pltpu.CompilerParams(vmem_limit_bytes=VMEM_LIMIT),
        name="unpack_results",
    )(small, qkv, early, late, grad_in, block_out)


def tail(
    row_own, row_recv, x, middle_grad, grads, joined_sum, gain, taps, pool_gain, pool_shift,
    bias_grad, hot, space_hot, cached, mem_own, mem_recv, vectors, up_bias, rest, clip_count, devices,
    unit, table_rows,
):
    clips, rows, model = x.shape
    wide = grads.shape[3]
    heads = wide // (3 * LANES)
    width = 3 * 2 * heads * unit
    outers = clip_count // 2
    shard_rows = model // (4 * outers)
    chunks = 3
    cols = wide // chunks
    plan = {}
    at = 0
    for name, count in (
        ("gain", 2 * model // LANES),
        ("shift", 2 * model // LANES),
        ("rows", 2 * model // LANES),
        ("joined", 4 * wide // LANES),
        ("up", 2 * up_bias.shape[1] // LANES),
        ("taps", 81),
        ("pool_gain", 3),
        ("pool_shift", 3),
        ("squeeze", 2 * FRAMES // MEMF),
        ("time", table_rows),
        ("space", 2 * (2 * SIDE - 1)),
    ):
        plan[name] = at
        at += count
    block = -(-at // (devices * 8)) * 8
    small_shape = (2, 4, outers, block, LANES)
    out = jax.ShapeDtypeStruct
    dma = pltpu.SemaphoreType.DMA
    vmem = pl.BlockSpec(memory_space=pltpu.VMEM)
    shapes = [
        out((clips, rows, model), BF),
        out((shard_rows, width), F32),
        out((shard_rows, rest.shape[2]), F32),
        out(small_shape, F32),
    ]
    results = pl.pallas_call(
        partial(tail_kernel, unit=unit, plan=plan, table_rows=table_rows),
        in_specs=[vmem] * 19,
        out_specs=[vmem] * len(shapes),
        out_shape=shapes,
        scratch_shapes=[
            pltpu.VMEM((chunks, 3, outers, shard_rows, cols), BF),
            pltpu.VMEM((chunks, outers, 2, shard_rows, cols), BF),
            pltpu.VMEM((chunks, outers, 2, shard_rows, cols), BF),
            pltpu.VMEM(small_shape, F32),
            pltpu.VMEM(small_shape[1:], F32),
            pltpu.VMEM((3,) + small_shape[2:], F32),
            pltpu.VMEM(small_shape[2:], F32),
            pltpu.VMEM((clips, rows, model), BF),
            pltpu.VMEM(rest.shape, BF),
            dma((2, clips)),
            dma((2, chunks, 3)),
            dma((2, chunks, outers)),
            dma((2, 2)),
            dma((2, 2, 3)),
            dma((2, 2, outers)),
            dma((2, outers)),
        ],
        compiler_params=pltpu.CompilerParams(
            collective_id=0, has_side_effects=True, vmem_limit_bytes=VMEM_LIMIT
        ),
        name="tail_gradients",
    )(
        row_own, row_recv, x, middle_grad, grads, joined_sum, gain, taps, pool_gain, pool_shift,
        bias_grad, hot, space_hot, cached, mem_own, mem_recv, vectors, up_bias, rest,
    )
    return results, plan


def feed_kernel(
    att_own, att_recv, x, cot, weights, gain, shift, out_shift, up_shift,
    block_out, middle_grad, grad_own, grad_send, grad_rest, vectors, up_bias,
    attended, normed, cots, active, hidden_low, branch, middle, send, recv, sems,
):
    clips, rows, model = x.shape
    span = attended.shape[0] // clips
    group = att_own.shape[2]
    head_width = 2 * group
    hidden_width = up_shift.shape[0] * LANES
    tiles = 4
    tile = hidden_width // tiles
    clip_at = lax.axis_index("clip")
    frame = lax.axis_index("frame")
    head = lax.axis_index("head")
    partner = (clip_at, frame, 1 - head)

    def cross(kind, index):
        return pltpu.make_async_remote_copy(
            src_ref=send.at[kind, index], dst_ref=recv.at[kind, index],
            send_sem=sems.at[0, kind, index], recv_sem=sems.at[1, kind, index],
            device_id=partner, device_id_type=MESH_ID,
        )

    barrier = pltpu.get_barrier_semaphore()
    pl.semaphore_signal(barrier, inc=1, device_id=partner, device_id_type=MESH_ID)
    for ref in (attended, normed, cots, branch):
        ref[...] = jnp.zeros_like(ref)

    def assemble(low, high):
        for index in range(clips):
            at = slice(index * span, index * span + rows)
            attended[at, :group] = low[index]
            attended[at, group:] = high[index]

    @pl.when(frame == 0)
    def _():
        assemble(att_own, att_recv)

    @pl.when(frame == 1)
    def _():
        assemble(att_recv, att_own)

    for index in range(clips):
        cots[index * span : index * span + rows] = cot[index]
    pl.semaphore_wait(barrier, 1)

    def block_rows(index):
        return pl.ds(pl.multiple_of(index * span, 16), span)

    def project(index):
        part = dot_f32(attended[block_rows(index)], weights[:, :head_width], ((1,), (1,)))
        send[0, index] = part[:rows].astype(BF)
        cross(0, index).start()

    each(0, clips, project)

    def feed(index, bias_sum):
        cross(0, index).wait_recv()
        branch_rows = send[0, index].astype(F32) + recv[0, index].astype(F32)
        value = x[index].astype(F32) + branch_rows + out_shift[0:1]
        middle[index] = value
        centred, rate = row_stats(value)
        low = (centred * rate * gain[1:2] + shift[1:2]).astype(BF)
        at = pl.multiple_of(index * span, 16)
        normed[pl.ds(at, rows)] = low
        low = normed[block_rows(index)]
        cot_rows = cots[block_rows(index)]
        out_part = jnp.zeros((span, model), F32)
        norm_part = jnp.zeros((span, model), F32)
        sums = []
        for step in range(tiles):
            lanes = slice(step * tile, (step + 1) * tile)
            up = weights[:, head_width + step * tile : head_width + (step + 1) * tile]
            at = head_width + hidden_width + step * tile
            down = weights[:, at : at + tile]
            first = step * tile // LANES
            pieces = [up_shift[first + row : first + row + 1] for row in range(tile // LANES)]
            hidden = dot_f32(low, up, ((1,), (0,))) + jnp.concatenate(pieces, axis=1)
            incoming = dot_f32(cot_rows, down, ((1,), (0,)))
            normal = 0.5 * (1.0 + lax.erf(hidden * (0.5**0.5)))
            density = jnp.exp(hidden * hidden * -0.5) * ((2.0 * np.pi) ** -0.5)
            acted = (hidden * normal).astype(BF)
            back = (incoming * (normal + hidden * density)).astype(BF)
            active[block_rows(index), lanes] = acted
            hidden_low[block_rows(index), lanes] = back
            sums.append(jnp.sum(back.astype(F32), axis=0, keepdims=True))
            out_part = out_part + dot_f32(acted, down, ((1,), (1,)))
            norm_part = norm_part + dot_f32(back, up, ((1,), (1,)))
        send[1, index] = norm_part[:rows].astype(BF)
        cross(1, index).start()
        send[2, index] = out_part[:rows].astype(BF)
        cross(2, index).start()
        return bias_sum + jnp.concatenate(sums, axis=1)

    up_bias[...] = lax.fori_loop(0, clips, feed, jnp.zeros((1, hidden_width), F32))

    wide = hidden_width // 2
    for step in range(2):
        lanes = slice(step * wide, (step + 1) * wide)
        value = dot_f32(normed[...], hidden_low[:, lanes], ((0,), (0,)))
        at = head_width + step * wide
        grad_rest[:, at : at + wide] = value.astype(BF)
        value = dot_f32(cots[...], active[:, lanes], ((0,), (0,)))
        at = head_width + hidden_width + step * wide
        grad_rest[:, at : at + wide] = value.astype(BF)

    def back(index, sums):
        gain_sum, shift_sum, first_sum, second_sum = sums
        cross(1, index).wait_recv()
        incoming = send[1, index].astype(F32) + recv[1, index].astype(F32)
        centred, rate = row_stats(middle[index])
        normal = centred * rate
        scaled = incoming * gain[1:2]
        mean_scaled = jnp.sum(scaled, axis=-1, keepdims=True) * (1.0 / model)
        mean_both = jnp.sum(scaled * normal, axis=-1, keepdims=True) * (1.0 / model)
        cot_rows = cot[index].astype(F32)
        value = cot_rows + rate * (scaled - mean_scaled - normal * mean_both)
        middle_grad[index] = value
        at = pl.multiple_of(index * span, 16)
        branch[pl.ds(at, rows)] = value.astype(BF)
        part = dot_f32(branch[block_rows(index)], weights[:, :head_width], ((1,), (0,)))
        part = part[:rows].astype(BF)

        @pl.when(frame == 0)
        def _():
            grad_own[index] = part[:, :group]
            grad_send[index] = part[:, group:]

        @pl.when(frame == 1)
        def _():
            grad_send[index] = part[:, :group]
            grad_own[index] = part[:, group:]

        cross(2, index).wait_recv()
        out_rows = send[2, index].astype(F32) + recv[2, index].astype(F32)
        block_out[index] = (middle[index] + out_rows + out_shift[1:2]).astype(BF)

        def column(rows_here):
            return jnp.sum(rows_here, axis=0, keepdims=True)

        return (
            gain_sum + column(incoming * normal),
            shift_sum + column(incoming),
            first_sum + column(value),
            second_sum + column(cot_rows),
        )

    start = tuple(jnp.zeros((1, model), F32) for _ in range(4))
    sums = lax.fori_loop(0, clips, back, start)
    for row in range(4):
        vectors[row : row + 1] = sums[row]
    value = dot_f32(branch[...], attended[...], ((0,), (0,)))
    grad_rest[:, :head_width] = value.astype(BF)
    for kind in range(3):
        each(0, clips, lambda index: cross(kind, index).wait_send())


def feed(att_own, att_recv, x, cot, weights, gain, shift, out_shift, up_shift):
    clips, rows, model = x.shape
    group = att_own.shape[2]
    hidden_width = up_shift.shape[0] * LANES
    span = -(-rows // 16) * 16
    out = jax.ShapeDtypeStruct
    vmem = pl.BlockSpec(memory_space=pltpu.VMEM)
    shapes = [
        out((clips, rows, model), BF),
        out((clips, rows, model), F32),
        out((clips, rows, group), BF),
        out((clips, rows, group), BF),
        out(weights.shape, BF),
        out((4, model), F32),
        out((1, hidden_width), F32),
    ]
    return pl.pallas_call(
        feed_kernel,
        in_specs=[vmem] * 9,
        out_specs=[vmem] * len(shapes),
        out_shape=shapes,
        scratch_shapes=[
            pltpu.VMEM((clips * span, 2 * group), BF),
            pltpu.VMEM((clips * span, model), BF),
            pltpu.VMEM((clips * span, model), BF),
            pltpu.VMEM((clips * span, hidden_width), BF),
            pltpu.VMEM((clips * span, hidden_width), BF),
            pltpu.VMEM((clips * span, model), BF),
            pltpu.VMEM((clips, rows, model), F32),
            pltpu.VMEM((3, clips, rows, model), BF),
            pltpu.VMEM((3, clips, rows, model), BF),
            pltpu.SemaphoreType.DMA((2, 3, clips)),
        ],
        compiler_params=pltpu.CompilerParams(
            collective_id=4, has_side_effects=True, vmem_limit_bytes=VMEM_LIMIT
        ),
        name="feed_forward_both_ways",
    )(att_own, att_recv, x, cot, weights, gain, shift, out_shift, up_shift)


def precise(pattern, *operands):
    return jnp.einsum(pattern, *operands, precision=lax.Precision.HIGHEST)


def split_groups(value, which, axis):
    half = value.shape[axis] // 2
    low = lax.slice_in_dim(value, 0, half, axis=axis)
    high = lax.slice_in_dim(value, half, None, axis=axis)
    first = which == 0
    return jnp.where(first, low, high), jnp.where(first, high, low)


def join_groups(own, peer, which, axis):
    first = which == 0
    return jnp.concatenate([jnp.where(first, own, peer), jnp.where(first, peer, own)], axis=axis)


def time_choices(stride_group, memory_place, which, own, table_rows):
    local = jnp.arange(own, dtype=jnp.int32)
    times = jnp.concatenate([which * own + local, (1 - which) * own + local])
    stride = jnp.left_shift(jnp.int32(2), stride_group)[:, None, None]
    offset = 8 * (FRAMES - 1)
    current = stride * (times[None, :, None] - times[None, None, :]) + offset
    slots = [memory_place[:, index : index + 1] for index in range(4)]
    first = jnp.concatenate([slots[2], slots[0], slots[3], slots[1]], axis=1)
    second = jnp.concatenate([slots[3], slots[1], slots[2], slots[0]], axis=1)
    places = jnp.where(which == 0, first, second)
    memory = stride * times[None, :, None] + places[:, None, :] + offset
    chosen = jnp.concatenate([current, memory], axis=2)
    return (chosen[..., None] == jnp.arange(table_rows, dtype=jnp.int32)).astype(F32)


def space_choices():
    places = np.arange(SIDE)
    offsets = places[:, None] - places[None, :] + SIDE - 1
    hot = offsets.reshape(-1)[:, None] == np.arange(2 * SIDE - 1)[None, :]
    return jnp.asarray(hot.astype(np.float32))


def space_sums():
    spans = 2 * SIDE - 1
    hot = np.zeros((32, BIAS_COLS), np.float32)
    for axis in range(2):
        for query in range(SIDE):
            for key in range(SIDE):
                col = SPACE_AT + axis * CELLS + query * SIDE + key
                hot[axis * spans + query - key + SIDE - 1, col] = 1.0
    return hot


def wide_rows(rows, heads):
    count, members, unit = rows.shape
    padded = jnp.pad(rows, ((0, 0), (0, 0), (0, LANES - unit)))
    spread = jnp.broadcast_to(padded[:, :, None], (count, members, heads, LANES))
    return spread.reshape(count, members * heads * LANES)


def local(
    clips_in,
    cached_kv,
    old_memory,
    stride_group,
    memory_place,
    norm_gain,
    norm_shift,
    qkv_weight,
    qkv_shift,
    pool_kernel,
    pool_gain,
    pool_shift,
    squeeze_kernel,
    time_table,
    space_tables,
    proj_weight,
    out_shift,
    up_weight,
    up_shift,
    down_weight,
    cotangent,
):
    clip_count, rows_clip, model_width = clips_in.shape
    head_width = qkv_weight.shape[2]
    unit = pool_gain.shape[1]
    head_count = head_width // unit
    frame_count = lax.axis_size("frame")
    heads = head_count // frame_count
    own_frames = rows_clip // CELLS
    group_width = heads * unit
    group_span = FRAMES // MEMF
    scale = unit ** (-0.5)
    which = lax.axis_index("frame")
    into_np, outof_np = placement(frame_count)
    keys_np, mask_np, pad_np = bias_constants(frame_count)
    consts = (
        jnp.asarray(into_np, BF),
        jnp.asarray(outof_np, BF),
        jnp.asarray(keys_np, BF),
        jnp.asarray(mask_np),
        jnp.asarray(pad_np),
    )

    cached_flat = cached_kv.reshape(clip_count, rows_clip, 2 * head_width)
    time_hot = time_choices(stride_group, memory_place, which, own_frames, time_table.shape[0])
    time_rows = precise("ctkr,rd->ctkd", time_hot, time_table).reshape(clip_count, -1, unit)
    flipped = space_tables[:, ::-1]
    shifted_rows = [flipped[:, SIDE - 1 - q : 2 * SIDE - 1 - q] for q in range(SIDE)]
    space_rows = jnp.concatenate(shifted_rows, axis=1).reshape(2 * CELLS, unit)
    space_rows = jnp.broadcast_to(space_rows[None], (clip_count,) + space_rows.shape)
    bias = jnp.concatenate(
        [
            jnp.pad(time_rows, ((0, 0), (0, SPACE_AT - time_rows.shape[1]), (0, LANES - unit))),
            jnp.pad(
                space_rows,
                ((0, 0), (0, BIAS_COLS - SPACE_AT - 2 * CELLS), (0, LANES - unit)),
            ),
        ],
        axis=1,
    )
    bias = bias * (1.0 / scale)
    inputs = (
        clips_in, qkv_weight.transpose(1, 0, 2), norm_gain, norm_shift, qkv_shift, cached_flat,
        old_memory.reshape(clip_count, -1, 2 * head_width), squeeze_kernel, proj_weight.T, up_weight,
        down_weight.T,
    )
    clip_axis = lax.axis_size("clip")
    if qkv_weight.shape[0] % 16:
        attn_group, packed, normed, mem_own, mem_peer, column = project_plain(
            *inputs, clip_axis, unit
        )
        forward = attention_forward(
            packed, mem_own, mem_peer, column, consts, pool_kernel, pool_gain, pool_shift, bias,
            scale, unit, rows_clip,
        )
    else:
        attn_group, packed, normed, *forward = front(
            *inputs, consts, pool_kernel, pool_gain, pool_shift, bias, scale, clip_axis, unit
        )
    attended_own, attended_peer, rest_full = forward[:3]
    rest_full = rest_full.reshape(model_width, -1)
    saved = forward[3:]
    block_out, middle_grad, attended_grad_own, attended_grad_send, grad_rest, vectors, up_grads = (
        feed(
            attended_own, attended_peer, clips_in, cotangent, rest_full, norm_gain,
            norm_shift, out_shift, up_shift.reshape(-1, LANES),
        )
    )
    outers = lax.axis_size("clip") // 2
    grad_rest = grad_rest.reshape(outers, 4, -1, grad_rest.shape[1])
    backward = attention_backward(
        packed, normed, attn_group, attended_grad_own, attended_grad_send, grad_rest, consts,
        pool_kernel, pool_gain, bias, saved, scale, unit,
    )
    row_own, row_recv, mem_grad_own, mem_grad_peer = backward[:4]
    taps_grad, pool_gain_grad, pool_shift_grad, bias_grad = backward[4:8]
    attn_grad, joined_grad, rest_part, rest_early = backward[8:]

    time_count = time_rows.shape[1]
    hot = time_choices(
        stride_group, memory_place, which, own_frames, -(-time_table.shape[0] // LANES) * LANES
    )
    hot = hot.astype(BF).reshape(clip_count, time_count, -1)
    devices = lax.axis_size("clip") * frame_count * lax.axis_size("head")
    (grad_in, qkv_shard, rest_late, small), plan = tail(
        row_own, row_recv, clips_in, middle_grad,
        attn_grad.reshape(outers, 4, -1, attn_grad.shape[1]), joined_grad, norm_gain, taps_grad,
        pool_gain_grad, pool_shift_grad, bias_grad, hot,
        jnp.asarray(space_sums(), BF), cached_flat, mem_grad_own, mem_grad_peer, vectors,
        up_grads, rest_part, lax.axis_size("clip"), devices, unit, time_table.shape[0],
    )
    (
        grad_in, block_out, gain_sums, shift_sums, out_sums, qkv_bias_sum, up_bias_sum, kernel_sum,
        pool_gain_sum, pool_shift_sum, squeeze_sum, time_sum, space_sum, qkv_shard, proj_shard,
        up_shard, down_shard,
    ) = unpack(
        small.reshape((devices,) + small.shape[3:]), qkv_shard, rest_early, rest_late, grad_in, block_out, plan, unit,
        up_weight.shape[1], time_table.shape[0],
    )
    return (
        block_out,
        grad_in,
        gain_sums,
        shift_sums,
        qkv_shard.transpose(1, 0, 2),
        qkv_bias_sum,
        kernel_sum,
        pool_gain_sum,
        pool_shift_sum,
        squeeze_sum,
        time_sum.T,
        space_sum.transpose(1, 0, 2),
        proj_shard.T,
        out_sums,
        up_shard,
        up_bias_sum.reshape(-1),
        down_shard.T,
    )


def solution(mesh):
    return jax.shard_map(
        local,
        mesh=mesh,
        in_specs=(
            P("clip", "frame", None),
            P("clip", "frame", None, "head"),
            P("clip", "frame", None, "head"),
            P("clip"),
            P("clip", None),
            P(),
            P(),
            P(("clip", "frame"), None, "head"),
            P(None, "head"),
            P(),
            P(),
            P(),
            P(),
            P(),
            P(),
            P("head", ("clip", "frame")),
            P(),
            P(("clip", "frame"), "head"),
            P("head"),
            P("head", ("clip", "frame")),
            P("clip", "frame", None),
        ),
        out_specs=(
            P("clip", "frame", None),
            P("clip", "frame", None),
            P(),
            P(),
            P(("clip", "frame"), None, "head"),
            P(None, "head"),
            P(),
            P(),
            P(),
            P(),
            P(),
            P(),
            P("head", ("clip", "frame")),
            P(),
            P(("clip", "frame"), "head"),
            P("head"),
            P("head", ("clip", "frame")),
        ),
        check_vma=False,
    )
```
